32 devices in a mesh: path: 2 (over x), rows: 16 (over z, y, core).
Axes of the slice: x: 2, y: 2, z: 4, core: 2. Of those that a mesh axis runs over, the one named last changes fastest.
Arguments:
- x_slow: bfloat16 [8, 1, 16, 8, 16, 1024], P('path', None, 'rows')
- x_fast: bfloat16 [32, 1, 16, 8, 16, 128], P('path', None, 'rows')
- w_lateral: bfloat16 [2, 5, 128, 256], replicated, may hold values from -0.25 to 0.25
- w_slow_time: bfloat16 [2, 3, 1280, 256], replicated, may hold values from -0.09375 to 0.09375
- w_slow_space: bfloat16 [2, 3, 3, 256, 256], replicated, may hold values from -0.125 to 0.125
- w_slow_point: bfloat16 [2, 256, 1024], replicated, may hold values from -0.375 to 0.375
- w_fast_time: bfloat16 [2, 3, 128, 32], replicated, may hold values from -0.3125 to 0.3125
- w_fast_space: bfloat16 [2, 3, 3, 32, 32], replicated, may hold values from -0.375 to 0.375
- w_fast_point: bfloat16 [2, 32, 128], replicated, may hold values from -1 to 1
- gain_slow: float32 [2, 1792], replicated, may hold values from 0.4 to 1.6
- bias_slow: float32 [2, 1792], replicated, may hold values from -1.75 to 1.75
- gain_fast: float32 [2, 192], replicated, may hold values from 0.4 to 1.6
- bias_fast: float32 [2, 192], replicated, may hold values from -1.75 to 1.75
- clip_size: int32 [1, 8], replicated, may hold values from 10 to 16, as said below
- cot_slow: bfloat16 [8, 1, 16, 8, 16, 1024], P('path', None, 'rows')
- cot_fast: bfloat16 [32, 1, 16, 8, 16, 128], P('path', None, 'rows')
Outputs:
- out_slow: float32 [8, 1, 16, 8, 16, 1024], P('path', None, 'rows')
- out_fast: float32 [32, 1, 16, 8, 16, 128], P('path', None, 'rows')
- grad_x_slow: float32 [8, 1, 16, 8, 16, 1024], P('path', None, 'rows')
- grad_x_fast: float32 [32, 1, 16, 8, 16, 128], P('path', None, 'rows')
- grad_lateral: float32 [2, 5, 128, 256], replicated
- grad_slow_time: float32 [2, 3, 1280, 256], replicated
- grad_slow_space: float32 [2, 3, 3, 256, 256], replicated
- grad_slow_point: float32 [2, 256, 1024], replicated
- grad_fast_time: float32 [2, 3, 128, 32], replicated
- grad_fast_space: float32 [2, 3, 3, 32, 32], replicated
- grad_fast_point: float32 [2, 32, 128], replicated
- grad_gain_slow: float32 [2, 1792], replicated
- grad_bias_slow: float32 [2, 1792], replicated
- grad_gain_fast: float32 [2, 192], replicated
- grad_bias_fast: float32 [2, 192], replicated
The draws below stay inside these ranges and needn't reach their ends.
Inputs may be any that keep to these rules, and one draw needn't show every extreme that they name: `clip_size`: each clip's side is 10, 14 or 16; some clip has the smallest side and some the largest.
All inputs are finite; a program needn't handle non-finite values.
Results may differ from the reference program's by a relative error of at most 0.01.
Values may be sent and summed in bfloat16 or wider, within the bound.
No kernel may reach another device: no remote copies, remote signals or barrier semaphores. Data moves between devices by JAX's collectives and lax.ppermute only.
A program may use at most 192 MiB of HBM per device.

```python
import jax
import jax.numpy as jnp
from jax import lax

CS = 1024
LAT = 256
BS = 256
CF = 128
BF = 32
TS = 8
HP = 16
BLOCKS = 2
K = 1
TF = 32
RB = 8
BANDS = 16
PAIRS = 8
CLIPS = 8


def frame_band_ramp(frames):
    along = jnp.arange(frames, dtype=jnp.float32) / max(frames - 1, 1)
    across = jnp.arange(BANDS, dtype=jnp.float32) / max(BANDS - 1, 1)
    return 0.5 * (along[:, None, None, None, None, None] + across[None, None, :, None, None, None])


def draw_x_slow(key, part):
    shape = (TS, K, BANDS, RB, HP, CS)
    ramp = frame_band_ramp(TS)
    scale = 1.0 + 2.0 * ramp
    base = jax.random.normal(key, shape, jnp.float32)
    return (base * scale).astype(jnp.bfloat16)


def draw_x_fast(key, part):
    shape = (TF, K, BANDS, RB, HP, CF)
    ramp = frame_band_ramp(TF)
    scale = 1.0 + 2.0 * ramp
    base = jax.random.normal(key, shape, jnp.float32)
    return (base * scale).astype(jnp.bfloat16)


def draw_cot_slow(key, part):
    shape = (TS, K, BANDS, RB, HP, CS)
    ramp = frame_band_ramp(TS)
    common = jax.random.normal(jax.random.fold_in(key, 7), (CS,), jnp.float32)
    base = jax.random.normal(key, shape, jnp.float32)
    value = base + common * (0.5 + ramp)
    return value.astype(jnp.bfloat16)


def draw_cot_fast(key, part):
    shape = (TF, K, BANDS, RB, HP, CF)
    ramp = frame_band_ramp(TF)
    common = jax.random.normal(jax.random.fold_in(key, 7), (CF,), jnp.float32)
    base = jax.random.normal(key, shape, jnp.float32)
    value = base + common * (0.5 + ramp)
    return value.astype(jnp.bfloat16)


def draw_clip_size(key, part):
    total_clips = K * PAIRS
    picked = jax.random.randint(jax.random.fold_in(key, 11), (total_clips,), 0, 3)
    table = jnp.array([HP * 5 // 8, HP * 7 // 8, HP], dtype=jnp.int32)
    sides = jnp.take(table, picked)
    order = jax.random.permutation(jax.random.fold_in(key, 12), total_clips)
    sides = sides.at[order[0]].set(HP).at[order[1]].set(HP * 5 // 8)
    return sides.reshape(K, PAIRS).astype(jnp.int32)


def bell_draw(key, extent, scale, most, held_as=jnp.bfloat16):
    result = jax.random.normal(key, extent, jnp.float32) * scale
    return jnp.minimum(jnp.maximum(result, -most), most).astype(held_as)


def setup_inputs(seed: int = 0) -> dict:
    seeds = jax.random.split(jax.random.key(seed), 17)
    x_slow = draw_x_slow(jax.random.fold_in(seeds[16], 71), 0)
    x_fast = draw_x_fast(jax.random.fold_in(seeds[16], 71), 0)
    w_lateral = bell_draw(seeds[2], (BLOCKS, 5, CF, LAT), (5 * CF) ** -0.5, 0.25)
    w_slow_time = bell_draw(seeds[3], (BLOCKS, 3, CS + LAT, BS), (3 * (CS + LAT)) ** -0.5, 0.09375)
    w_slow_space = bell_draw(seeds[4], (BLOCKS, 3, 3, BS, BS), (9 * BS) ** -0.5, 0.125)
    w_slow_point = bell_draw(seeds[5], (BLOCKS, BS, CS), BS ** -0.5, 0.375)
    w_fast_time = bell_draw(seeds[6], (BLOCKS, 3, CF, BF), (3 * CF) ** -0.5, 0.3125)
    w_fast_space = bell_draw(seeds[7], (BLOCKS, 3, 3, BF, BF), (9 * BF) ** -0.5, 0.375)
    w_fast_point = bell_draw(seeds[8], (BLOCKS, BF, CF), BF ** -0.5, 1.0)
    gain_slow = jnp.clip(1.0 + 0.12 * jax.random.normal(seeds[9], (BLOCKS, LAT + 2 * BS + CS), jnp.float32), 0.4, 1.6)
    bias_slow = bell_draw(seeds[10], (BLOCKS, LAT + 2 * BS + CS), 0.3, 1.75, jnp.float32)
    gain_fast = jnp.clip(1.0 + 0.12 * jax.random.normal(seeds[11], (BLOCKS, 2 * BF + CF), jnp.float32), 0.4, 1.6)
    bias_fast = bell_draw(seeds[12], (BLOCKS, 2 * BF + CF), 0.3, 1.75, jnp.float32)
    clip_size = draw_clip_size(jax.random.fold_in(seeds[16], 71), 0)
    cot_slow = draw_cot_slow(jax.random.fold_in(seeds[16], 71), 0)
    cot_fast = draw_cot_fast(jax.random.fold_in(seeds[16], 71), 0)
    return dict(x_slow=x_slow, x_fast=x_fast, w_lateral=w_lateral, w_slow_time=w_slow_time, w_slow_space=w_slow_space, w_slow_point=w_slow_point, w_fast_time=w_fast_time, w_fast_space=w_fast_space, w_fast_point=w_fast_point, gain_slow=gain_slow, bias_slow=bias_slow, gain_fast=gain_fast, bias_fast=bias_fast, clip_size=clip_size, cot_slow=cot_slow, cot_fast=cot_fast)


epsilon = 1e-05
highest = lax.Precision.HIGHEST

@jax.custom_vjp
def low(v):
    return lax.optimization_barrier(v.astype(jnp.bfloat16)).astype(jnp.float32)

@jax.custom_vjp
def low_back(v):
    return v

def low_keep(v):
    return (low(v), None)

def low_pass(kept, grad):
    return (grad,)

def back_keep(v):
    return (v, None)

def back_low(kept, grad):
    return (low(grad),)
low.defvjp(low_keep, low_pass)
low_back.defvjp(back_keep, back_low)

def product(value, weight):
    return jnp.einsum('...c,cd->...d', value, weight, precision=highest)

def time_conv(value, weight):
    frames = value.shape[0]
    padded = jnp.pad(value, ((1, 1), (0, 0), (0, 0), (0, 0), (0, 0)))
    total = product(padded[0:frames], weight[0])
    for tap in range(1, 3):
        total = total + product(padded[tap:tap + frames], weight[tap])
    return total

def space_conv(value, weight):
    height = value.shape[2]
    breadth = value.shape[3]
    padded = jnp.pad(value, ((0, 0), (0, 0), (1, 1), (1, 1), (0, 0)))
    total = product(padded[:, :, 0:height, 0:breadth], weight[0, 0])
    for row_tap in range(3):
        for col_tap in range(3):
            if row_tap + col_tap > 0:
                total = total + product(padded[:, :, row_tap:row_tap + height, col_tap:col_tap + breadth], weight[row_tap, col_tap])
    return total

def lateral_conv(value, weight):
    frames = value.shape[0] // 4
    padded = jnp.pad(value, ((2, 2), (0, 0), (0, 0), (0, 0), (0, 0)))
    total = product(padded[0:4 * frames - 3:4], weight[0])
    for tap in range(1, 5):
        total = total + product(padded[tap:tap + 4 * frames - 3:4], weight[tap])
    return total

def batch_norm(value, gain, bias, mask, count):
    first = lax.optimization_barrier(jnp.sum(value * mask, axis=(0, 1, 2, 3)))
    second = lax.optimization_barrier(jnp.sum(value * value * mask, axis=(0, 1, 2, 3)))
    mean = first / count
    spread = second / count - mean * mean
    return (value - mean) * lax.rsqrt(spread + epsilon) * gain + bias

def forward(slow_in, fast_in, w_lateral, w_slow_time, w_slow_space, w_slow_point, w_fast_time, w_fast_space, w_fast_point, gain_slow, bias_slow, gain_fast, bias_fast, mask, count_slow, count_fast):
    slow = slow_in * mask
    fast = fast_in * mask
    lat_end = LAT
    first_end = LAT + BS
    second_end = LAT + 2 * BS
    for block in range(BLOCKS):
        fast_low = low(fast)
        lateral = low_back(lateral_conv(fast_low, w_lateral[block]))
        lat_act = jax.nn.silu(batch_norm(lateral, gain_slow[block, :lat_end], bias_slow[block, :lat_end], mask, count_slow)) * mask
        joined = low(jnp.concatenate([slow, lat_act], axis=-1))
        first = low_back(time_conv(joined, w_slow_time[block]))
        act1 = low(jax.nn.silu(batch_norm(first, gain_slow[block, lat_end:first_end], bias_slow[block, lat_end:first_end], mask, count_slow)) * mask)
        second = low_back(space_conv(act1, w_slow_space[block]))
        act2 = low(jax.nn.silu(batch_norm(second, gain_slow[block, first_end:second_end], bias_slow[block, first_end:second_end], mask, count_slow)) * mask)
        third = low_back(product(act2, w_slow_point[block]))
        fast_first = low_back(time_conv(fast_low, w_fast_time[block]))
        fast_act1 = low(jax.nn.silu(batch_norm(fast_first, gain_fast[block, :BF], bias_fast[block, :BF], mask, count_fast)) * mask)
        fast_second = low_back(space_conv(fast_act1, w_fast_space[block]))
        fast_act2 = low(jax.nn.silu(batch_norm(fast_second, gain_fast[block, BF:2 * BF], bias_fast[block, BF:2 * BF], mask, count_fast)) * mask)
        fast_third = low_back(product(fast_act2, w_fast_point[block]))
        new_slow = jax.nn.silu(slow + batch_norm(third, gain_slow[block, second_end:], bias_slow[block, second_end:], mask, count_slow)) * mask
        new_fast = jax.nn.silu(fast + batch_norm(fast_third, gain_fast[block, 2 * BF:], bias_fast[block, 2 * BF:], mask, count_fast)) * mask
        slow = new_slow
        fast = new_fast
    return (slow, fast)

def reference(x_slow, x_fast, w_lateral, w_slow_time, w_slow_space, w_slow_point, w_fast_time, w_fast_space, w_fast_point, gain_slow, bias_slow, gain_fast, bias_fast, clip_size, cot_slow, cot_fast):

    def to_clips(value):
        return value.astype(jnp.float32).reshape(value.shape[0], CLIPS, HP, HP, value.shape[-1])
    sides = clip_size.reshape(CLIPS)
    spots = jnp.arange(HP, dtype=jnp.int32)
    inside = (spots[None, :] < sides[:, None]).astype(jnp.float32)
    mask = (inside[:, :, None] * inside[:, None, :])[None, :, :, :, None]
    area = jnp.sum(sides * sides).astype(jnp.float32)
    count_slow = TS * area
    count_fast = TF * area
    params = (w_lateral, w_slow_time, w_slow_space, w_slow_point, w_fast_time, w_fast_space, w_fast_point, gain_slow, bias_slow, gain_fast, bias_fast)
    primals = (to_clips(x_slow), to_clips(x_fast)) + tuple((value.astype(jnp.float32) for value in params))

    def run(*values):
        return forward(*values, mask, count_slow, count_fast)
    outs, pull = jax.vjp(run, *primals)
    grads = pull((to_clips(cot_slow), to_clips(cot_fast)))
    out_slow = outs[0].reshape(x_slow.shape)
    out_fast = outs[1].reshape(x_fast.shape)
    grad_x_slow = grads[0].reshape(x_slow.shape)
    grad_x_fast = grads[1].reshape(x_fast.shape)
    return (out_slow, out_fast, grad_x_slow, grad_x_fast, grads[2], grads[3], grads[4], grads[5], grads[6], grads[7], grads[8], grads[9], grads[10], grads[11], grads[12])
```

```python
import jax
import jax.numpy as jnp
from jax import lax
from jax.sharding import PartitionSpec as P

TS = 8
BLOCKS = 2
TF = 32


epsilon = 1e-05


def partner(value, axis, stride):
    mask = 2**stride
    pairs = [(source, source ^ mask) for source in range(lax.axis_size(axis))]
    return lax.ppermute(value, axis, pairs)


def with_halo(value, sides, width):
    for axis, dim in sides:
        size, length = (lax.axis_size(axis), value.shape[dim])
        up = [(i, (i + 1) % size) for i in range(size - 1)]
        down = [(j, i) for i, j in up]
        last = lax.slice_in_dim(value, length - width, length, axis=dim)
        leading = lax.slice_in_dim(value, 0, width, axis=dim)
        before = lax.ppermute(last, axis, up)
        after = lax.ppermute(leading, axis, down)
        value = jnp.concatenate([before, value, after], axis=dim)
    return value


def shifted(value, axis, steps):
    count = lax.axis_size(axis)
    leading, last = (max(0, -steps), min(count, count - steps))
    return lax.ppermute(value, axis, [(source, source + steps) for source in range(leading, last)])


def product(value, weight):
    return jnp.einsum("...c,cd->...d", value, weight, preferred_element_type=jnp.float32)


def product_back(grad, weight):
    return jnp.einsum("...d,cd->...c", grad, weight, preferred_element_type=jnp.float32)


def outer_sum(value, grad):
    return jnp.einsum("tkrwc,tkrwd->cd", value, grad, preferred_element_type=jnp.float32)


def silu_slope(value):
    sigma = jax.nn.sigmoid(value)
    return sigma * (1.0 + value * (1.0 - sigma))


def time_conv_wide(wide, weight, frames):
    total = product(wide[0:frames], weight[0])
    for tap in range(1, 3):
        total = total + product(wide[tap : tap + frames], weight[tap])
    return total


def lateral_local(wide, weight, frames):
    total = product(wide[0 : 4 * frames - 3 : 4], weight[0])
    for tap in range(1, 5):
        total = total + product(wide[tap : tap + 4 * frames - 3 : 4], weight[tap])
    return total


def space_conv_wide(wide, weight, rows, cols):
    total = product(wide[:, :, 0:rows, 0:cols], weight[0, 0])
    for row_tap in range(3):
        for col_tap in range(3):
            if row_tap + col_tap > 0:
                total = total + product(
                    wide[:, :, row_tap : row_tap + rows, col_tap : col_tap + cols],
                    weight[row_tap, col_tap],
                )
    return total


def moments(value, mask):
    return (
        jnp.sum(value * mask, axis=(0, 1, 2, 3)),
        jnp.sum(value * value * mask, axis=(0, 1, 2, 3)),
    )


def global_sum(value):
    total = lax.axis_size("path") * lax.axis_size("rows")
    spread = jnp.broadcast_to(value[None], (total,) + value.shape)
    got = lax.all_to_all(spread, ("path", "rows"), 0, 0, tiled=True)
    return jnp.sum(got, axis=0)


def global_moments(first, second):
    size = first.shape[0]
    both = global_sum(jnp.concatenate([first, second]))
    return (both[:size], both[size:])


def global_grads(first, second):
    return global_moments(first, second)


def exchange_steps():
    steps = [("rows", 1), ("path", 1)]
    stride = 2
    while stride < lax.axis_size("rows"):
        steps.append(("rows", stride))
        stride *= 2
    return steps


def swap(value, axis, stride):
    pairs = [(source, source ^ stride) for source in range(lax.axis_size(axis))]
    return lax.ppermute(value, axis, pairs)


def reduce_rows(value):
    steps = exchange_steps()
    for axis, stride in steps:
        size = value.shape[0] // 2
        upper = (lax.axis_index(axis) // stride) % 2
        keep = lax.dynamic_slice_in_dim(value, upper * size, size, 0)
        give = lax.dynamic_slice_in_dim(value, (1 - upper) * size, size, 0)
        value = keep + swap(give.astype(jnp.bfloat16), axis, stride).astype(jnp.float32)
    value = value.astype(jnp.bfloat16)
    for axis, stride in reversed(steps):
        upper = (lax.axis_index(axis) // stride) % 2
        got = swap(value, axis, stride)
        value = jnp.concatenate(
            [jnp.where(upper == 0, value, got), jnp.where(upper == 0, got, value)], axis=0
        )
    return value.astype(jnp.float32)


def pack_rows(values):
    pieces = []
    for value in values:
        last = value.shape[-1]
        flat = value.reshape(-1, last)
        if last > 256:
            pieces.extend(flat[:, at : at + 256] for at in range(0, last, 256))
        elif last == 256:
            pieces.append(flat)
        else:
            pieces.append(flat.reshape(-1, 256))
    total = lax.axis_size("path") * lax.axis_size("rows") * 16
    count = sum(piece.shape[0] for piece in pieces)
    short = (-count) % total
    if short:
        pieces.append(jnp.zeros((short, 256), jnp.float32))
    return jnp.concatenate(pieces, axis=0)


def unpack_rows(flat, likes):
    outs = []
    at = 0
    for like in likes:
        last = like.shape[-1]
        if last > 256:
            rows = like.size // last
            parts = []
            for _ in range(0, last, 256):
                parts.append(flat[at : at + rows])
                at += rows
            outs.append(jnp.concatenate(parts, axis=1).reshape(like.shape))
        else:
            rows = like.size // 256
            outs.append(flat[at : at + rows].reshape(like.shape))
            at += rows
    return outs


def reduce_weights(grads):
    return unpack_rows(reduce_rows(pack_rows(grads)), grads)


def standardize(value, total_first, total_second, count):
    mean = total_first / count
    rstd = lax.rsqrt(total_second / count - mean * mean + epsilon)
    return ((value - mean) * rstd, rstd)


def norm_back(grad_out, hat, rstd, gain, sum_out, sum_hat, count, mask):
    return (gain * rstd * (grad_out - mask * (sum_out + hat * sum_hat) / count)).astype(
        jnp.bfloat16
    )


def grad_sums(grad_out, hat):
    return (jnp.sum(grad_out, axis=(0, 1, 2, 3)), jnp.sum(grad_out * hat, axis=(0, 1, 2, 3)))


def edge_rows(value, half):
    return jnp.where(half == 0, value[:, :, -1], value[:, :, 0])


def widen_rows(value, got, half):
    empty = jnp.zeros_like(got)
    upper = jnp.where(half == 1, got, empty)
    lower = jnp.where(half == 0, got, empty)
    joined = jnp.concatenate([upper[:, :, None], value, lower[:, :, None]], axis=2)
    return jnp.pad(joined, ((0, 0), (0, 0), (0, 0), (1, 1), (0, 0)))


def split_pair(got, first_edge, second_edge):
    first_size = first_edge.size
    return (got[:first_size].reshape(first_edge.shape), got[first_size:].reshape(second_edge.shape))


def rows_forward(slow_part, fast_part, half):
    slow_edge = edge_rows(slow_part, half)
    fast_edge = edge_rows(fast_part, half)
    got = partner(jnp.concatenate([slow_edge.reshape(-1), fast_edge.reshape(-1)]), "rows", 0)
    got_slow, got_fast = split_pair(got, slow_edge, fast_edge)
    return (widen_rows(slow_part, got_slow, half), widen_rows(fast_part, got_fast, half))


def rows_backward(slow_part, fast_part, half):
    slow_edge = edge_rows(slow_part, half)
    fast_edge = edge_rows(fast_part, half)
    got = partner(jnp.concatenate([slow_edge.reshape(-1), fast_edge.reshape(-1)]), "rows", 0)
    got_slow, got_fast = split_pair(got, slow_edge, fast_edge)
    return (widen_rows(slow_part, got_slow, half), widen_rows(fast_part, got_fast, half))


def gain_parts(gain_slow, bias_slow, gain_fast, bias_fast, lat_end, inner_slow, inner_fast):
    cuts = (0, lat_end, lat_end + inner_slow, lat_end + 2 * inner_slow, gain_slow.shape[0])
    fast_cuts = (0, inner_fast, 2 * inner_fast, gain_fast.shape[0])
    slow_pieces = [
        (gain_slow[cuts[index] : cuts[index + 1]], bias_slow[cuts[index] : cuts[index + 1]])
        for index in range(4)
    ]
    fast_pieces = [
        (
            gain_fast[fast_cuts[index] : fast_cuts[index + 1]],
            bias_fast[fast_cuts[index] : fast_cuts[index + 1]],
        )
        for index in range(3)
    ]
    return (slow_pieces, fast_pieces)


def slow_first_conv(joined, w_slow_time, frames_slow):
    joined_wide = with_halo(joined, (("path", 0),), 1)
    first = time_conv_wide(joined_wide, w_slow_time, frames_slow)
    return first


def forward_block(slow, fast, weights, mask, half, count_slow, count_fast):
    (
        w_lateral,
        w_slow_time,
        w_slow_space,
        w_slow_point,
        w_fast_time,
        w_fast_space,
        w_fast_point,
        gain_slow,
        bias_slow,
        gain_fast,
        bias_fast,
    ) = weights
    frames_slow = slow.shape[0]
    frames_fast = fast.shape[0]
    rows = slow.shape[2]
    cols = slow.shape[3]
    lat_end = w_lateral.shape[2]
    inner_slow = w_slow_space.shape[3]
    inner_fast = w_fast_space.shape[3]
    slow_pieces, fast_pieces = gain_parts(
        gain_slow, bias_slow, gain_fast, bias_fast, lat_end, inner_slow, inner_fast
    )
    fast_wide = with_halo(fast.astype(jnp.bfloat16), (("path", 0),), 2)
    lateral = lateral_local(fast_wide, w_lateral, frames_slow)
    fast_first = time_conv_wide(fast_wide[1:-1], w_fast_time, frames_fast)
    lat_one, lat_two = moments(lateral, mask)
    ff_one, ff_two = moments(fast_first, mask)
    tot_one, tot_two = global_moments(
        jnp.concatenate([lat_one, ff_one]), jnp.concatenate([lat_two, ff_two])
    )
    lat_hat, lat_rstd = standardize(lateral, tot_one[:lat_end], tot_two[:lat_end], count_slow)
    lat_act = jax.nn.silu(lat_hat * slow_pieces[0][0] + slow_pieces[0][1]) * mask
    joined = jnp.concatenate([slow, lat_act], axis=-1).astype(jnp.bfloat16)
    first = slow_first_conv(joined, w_slow_time, frames_slow)
    ff_hat, ff_rstd = standardize(fast_first, tot_one[lat_end:], tot_two[lat_end:], count_fast)
    fast_act1 = (jax.nn.silu(ff_hat * fast_pieces[0][0] + fast_pieces[0][1]) * mask).astype(
        jnp.bfloat16
    )
    first_one, first_two = moments(first, mask)
    sum_one, sum_two = global_moments(first_one, first_two)
    first_hat, first_rstd = standardize(first, sum_one, sum_two, count_slow)
    slow_act1 = (jax.nn.silu(first_hat * slow_pieces[1][0] + slow_pieces[1][1]) * mask).astype(
        jnp.bfloat16
    )
    slow_wide1, fast_wide1 = rows_forward(slow_act1, fast_act1, half)
    second = space_conv_wide(slow_wide1, w_slow_space, rows, cols)
    fast_second = space_conv_wide(fast_wide1, w_fast_space, rows, cols)
    sec_one, sec_two = moments(second, mask)
    fs_one, fs_two = moments(fast_second, mask)
    two_one, two_two = global_moments(
        jnp.concatenate([sec_one, fs_one]), jnp.concatenate([sec_two, fs_two])
    )
    second_hat, second_rstd = standardize(
        second, two_one[:inner_slow], two_two[:inner_slow], count_slow
    )
    fs_hat, fs_rstd = standardize(
        fast_second, two_one[inner_slow:], two_two[inner_slow:], count_fast
    )
    slow_act2 = (jax.nn.silu(second_hat * slow_pieces[2][0] + slow_pieces[2][1]) * mask).astype(
        jnp.bfloat16
    )
    fast_act2 = (jax.nn.silu(fs_hat * fast_pieces[1][0] + fast_pieces[1][1]) * mask).astype(
        jnp.bfloat16
    )
    third = product(slow_act2, w_slow_point)
    fast_third = product(fast_act2, w_fast_point)
    thr_one, thr_two = moments(third, mask)
    ft_one, ft_two = moments(fast_third, mask)
    last_one, last_two = global_moments(
        jnp.concatenate([thr_one, ft_one]), jnp.concatenate([thr_two, ft_two])
    )
    width_slow = slow.shape[-1]
    third_hat, third_rstd = standardize(
        third, last_one[:width_slow], last_two[:width_slow], count_slow
    )
    ft_hat, ft_rstd = standardize(
        fast_third, last_one[width_slow:], last_two[width_slow:], count_fast
    )
    slow_out = jax.nn.silu(slow + third_hat * slow_pieces[3][0] + slow_pieces[3][1]) * mask
    fast_out = jax.nn.silu(fast + ft_hat * fast_pieces[2][0] + fast_pieces[2][1]) * mask
    kept = {
        "slow": slow,
        "fast": fast,
        "fast_wide": fast_wide,
        "lat_hat": lat_hat,
        "lat_rstd": lat_rstd,
        "joined": joined,
        "first_hat": first_hat,
        "first_rstd": first_rstd,
        "ff_hat": ff_hat,
        "ff_rstd": ff_rstd,
        "slow_wide1": slow_wide1,
        "fast_wide1": fast_wide1,
        "second_hat": second_hat,
        "second_rstd": second_rstd,
        "fs_hat": fs_hat,
        "fs_rstd": fs_rstd,
        "slow_act2": slow_act2,
        "fast_act2": fast_act2,
        "third_hat": third_hat,
        "third_rstd": third_rstd,
        "ft_hat": ft_hat,
        "ft_rstd": ft_rstd,
    }
    return (slow_out, fast_out, kept)


def backward_block(d_slow, d_fast, kept, weights, mask, half, count_slow, count_fast):
    (
        w_lateral,
        w_slow_time,
        w_slow_space,
        w_slow_point,
        w_fast_time,
        w_fast_space,
        w_fast_point,
        gain_slow,
        bias_slow,
        gain_fast,
        bias_fast,
    ) = weights
    frames_slow = d_slow.shape[0]
    frames_fast = d_fast.shape[0]
    rows = d_slow.shape[2]
    cols = d_slow.shape[3]
    width_slow = d_slow.shape[-1]
    lat_end = w_lateral.shape[2]
    inner_slow = w_slow_space.shape[3]
    inner_fast = w_fast_space.shape[3]
    slow_pieces, fast_pieces = gain_parts(
        gain_slow, bias_slow, gain_fast, bias_fast, lat_end, inner_slow, inner_fast
    )
    pre_slow = kept["slow"] + kept["third_hat"] * slow_pieces[3][0] + slow_pieces[3][1]
    pre_fast = kept["fast"] + kept["ft_hat"] * fast_pieces[2][0] + fast_pieces[2][1]
    grad_pre = d_slow * mask * silu_slope(pre_slow)
    grad_pre_fast = d_fast * mask * silu_slope(pre_fast)
    out_s, hat_s = grad_sums(grad_pre, kept["third_hat"])
    out_f, hat_f = grad_sums(grad_pre_fast, kept["ft_hat"])
    tot_out3, tot_hat3 = global_grads(
        jnp.concatenate([out_s, out_f]), jnp.concatenate([hat_s, hat_f])
    )
    d_third = norm_back(
        grad_pre,
        kept["third_hat"],
        kept["third_rstd"],
        slow_pieces[3][0],
        tot_out3[:width_slow],
        tot_hat3[:width_slow],
        count_slow,
        mask,
    )
    d_fthird = norm_back(
        grad_pre_fast,
        kept["ft_hat"],
        kept["ft_rstd"],
        fast_pieces[2][0],
        tot_out3[width_slow:],
        tot_hat3[width_slow:],
        count_fast,
        mask,
    )
    grad_point = outer_sum(kept["slow_act2"], d_third)
    grad_fpoint = outer_sum(kept["fast_act2"], d_fthird)
    e_two = (
        product_back(d_third, w_slow_point)
        * mask
        * silu_slope(kept["second_hat"] * slow_pieces[2][0] + slow_pieces[2][1])
    )
    e_ftwo = (
        product_back(d_fthird, w_fast_point)
        * mask
        * silu_slope(kept["fs_hat"] * fast_pieces[1][0] + fast_pieces[1][1])
    )
    out_s, hat_s = grad_sums(e_two, kept["second_hat"])
    out_f, hat_f = grad_sums(e_ftwo, kept["fs_hat"])
    tot_out2, tot_hat2 = global_grads(
        jnp.concatenate([out_s, out_f]), jnp.concatenate([hat_s, hat_f])
    )
    d_second = norm_back(
        e_two,
        kept["second_hat"],
        kept["second_rstd"],
        slow_pieces[2][0],
        tot_out2[:inner_slow],
        tot_hat2[:inner_slow],
        count_slow,
        mask,
    )
    d_fsecond = norm_back(
        e_ftwo,
        kept["fs_hat"],
        kept["fs_rstd"],
        fast_pieces[1][0],
        tot_out2[inner_slow:],
        tot_hat2[inner_slow:],
        count_fast,
        mask,
    )
    wide_second, wide_fsecond = rows_backward(d_second, d_fsecond, half)
    space_terms = []
    fspace_terms = []
    e_one = jnp.zeros(d_second.shape[:4] + (inner_slow,), jnp.float32)
    e_fone = jnp.zeros(d_fsecond.shape[:4] + (inner_fast,), jnp.float32)
    for row_tap in range(3):
        for col_tap in range(3):
            space_terms.append(
                outer_sum(
                    kept["slow_wide1"][:, :, row_tap : row_tap + rows, col_tap : col_tap + cols],
                    d_second,
                )
            )
            fspace_terms.append(
                outer_sum(
                    kept["fast_wide1"][:, :, row_tap : row_tap + rows, col_tap : col_tap + cols],
                    d_fsecond,
                )
            )
            e_one = e_one + product_back(
                wide_second[
                    :, :, 2 - row_tap : 2 - row_tap + rows, 2 - col_tap : 2 - col_tap + cols
                ],
                w_slow_space[row_tap, col_tap],
            )
            e_fone = e_fone + product_back(
                wide_fsecond[
                    :, :, 2 - row_tap : 2 - row_tap + rows, 2 - col_tap : 2 - col_tap + cols
                ],
                w_fast_space[row_tap, col_tap],
            )
    grad_space = jnp.stack(space_terms).reshape((3, 3) + space_terms[0].shape)
    grad_fspace = jnp.stack(fspace_terms).reshape((3, 3) + fspace_terms[0].shape)
    e_one = e_one * mask * silu_slope(kept["first_hat"] * slow_pieces[1][0] + slow_pieces[1][1])
    e_fone = e_fone * mask * silu_slope(kept["ff_hat"] * fast_pieces[0][0] + fast_pieces[0][1])
    out_s, hat_s = grad_sums(e_one, kept["first_hat"])
    out_f, hat_f = grad_sums(e_fone, kept["ff_hat"])
    tot_out1, tot_hat1 = global_grads(
        jnp.concatenate([out_s, out_f]), jnp.concatenate([hat_s, hat_f])
    )
    d_first = norm_back(
        e_one,
        kept["first_hat"],
        kept["first_rstd"],
        slow_pieces[1][0],
        tot_out1[:inner_slow],
        tot_hat1[:inner_slow],
        count_slow,
        mask,
    )
    d_ffirst = norm_back(
        e_fone,
        kept["ff_hat"],
        kept["ff_rstd"],
        fast_pieces[0][0],
        tot_out1[inner_slow:],
        tot_hat1[inner_slow:],
        count_fast,
        mask,
    )
    first_grad_wide = with_halo(d_first, (("path", 0),), 1)
    grad_time = jnp.stack(
        [
            outer_sum(kept["joined"], first_grad_wide[2 - tap : 2 - tap + frames_slow])
            for tap in range(3)
        ]
    )
    d_joined = product_back(first_grad_wide[2 : 2 + frames_slow], w_slow_time[0])
    for tap in range(1, 3):
        d_joined = d_joined + product_back(
            first_grad_wide[2 - tap : 2 - tap + frames_slow], w_slow_time[tap]
        )
    d_slow_in = grad_pre + d_joined[..., :width_slow]
    e_lat = (
        d_joined[..., width_slow:]
        * mask
        * silu_slope(kept["lat_hat"] * slow_pieces[0][0] + slow_pieces[0][1])
    )
    out_l, hat_l = grad_sums(e_lat, kept["lat_hat"])
    tot_outl, tot_hatl = global_grads(out_l, hat_l)
    d_lateral = norm_back(
        e_lat,
        kept["lat_hat"],
        kept["lat_rstd"],
        slow_pieces[0][0],
        tot_outl,
        tot_hatl,
        count_slow,
        mask,
    )
    fast_wide = kept["fast_wide"]
    grad_lat = jnp.stack(
        [outer_sum(fast_wide[tap : tap + 4 * frames_slow - 3 : 4], d_lateral) for tap in range(5)]
    )
    pieces = [product_back(d_lateral, w_lateral[tap]) for tap in range(5)]
    tail = pieces[0].shape[1:]
    spread = jnp.stack(pieces[:4], axis=1).reshape((4 * frames_slow,) + tail)
    empty = jnp.zeros_like(pieces[4])
    carry = jnp.stack([pieces[4], empty, empty, empty], axis=1).reshape((4 * frames_slow,) + tail)
    buffer = jnp.pad(spread, ((0, 4), (0, 0), (0, 0), (0, 0), (0, 0))) + jnp.pad(
        carry, ((4, 0), (0, 0), (0, 0), (0, 0), (0, 0))
    )
    lat_fast = buffer[2 : 2 + frames_fast]
    got = shifted(d_lateral[0], "path", -1)
    extra = jnp.stack([product_back(got, w_lateral[0]), product_back(got, w_lateral[1])])
    extra = jnp.pad(extra, ((frames_fast - 2, 0), (0, 0), (0, 0), (0, 0), (0, 0)))
    ffirst_grad_wide = with_halo(d_ffirst, (("path", 0),), 1)
    grad_ftime = jnp.stack(
        [outer_sum(fast_wide[1 + tap : 1 + tap + frames_fast], d_ffirst) for tap in range(3)]
    )
    d_fast_conv = product_back(ffirst_grad_wide[2 : 2 + frames_fast], w_fast_time[0])
    for tap in range(1, 3):
        d_fast_conv = d_fast_conv + product_back(
            ffirst_grad_wide[2 - tap : 2 - tap + frames_fast], w_fast_time[tap]
        )
    d_fast_in = grad_pre_fast + d_fast_conv + lat_fast + extra
    gain_grad_slow = jnp.concatenate(
        [tot_hatl, tot_hat1[:inner_slow], tot_hat2[:inner_slow], tot_hat3[:width_slow]]
    )
    bias_grad_slow = jnp.concatenate(
        [tot_outl, tot_out1[:inner_slow], tot_out2[:inner_slow], tot_out3[:width_slow]]
    )
    gain_grad_fast = jnp.concatenate(
        [tot_hat1[inner_slow:], tot_hat2[inner_slow:], tot_hat3[width_slow:]]
    )
    bias_grad_fast = jnp.concatenate(
        [tot_out1[inner_slow:], tot_out2[inner_slow:], tot_out3[width_slow:]]
    )
    grads = (
        grad_lat,
        grad_time,
        grad_space,
        grad_point,
        grad_ftime,
        grad_fspace,
        grad_fpoint,
        gain_grad_slow,
        bias_grad_slow,
        gain_grad_fast,
        bias_grad_fast,
    )
    return (d_slow_in, d_fast_in, grads)


def on_device(
    x_slow,
    x_fast,
    w_lateral,
    w_slow_time,
    w_slow_space,
    w_slow_point,
    w_fast_time,
    w_fast_space,
    w_fast_point,
    gain_slow,
    bias_slow,
    gain_fast,
    bias_fast,
    clip_size,
    cot_slow,
    cot_fast,
):
    place = lax.axis_index("rows")
    half = place % 2
    couple = place // 2
    sides = lax.dynamic_slice_in_dim(clip_size, couple, 1, 1)[:, 0]
    rows = x_slow.shape[3]
    cols = x_slow.shape[4]
    lines = half * rows + jnp.arange(rows, dtype=jnp.int32)
    spots = jnp.arange(cols, dtype=jnp.int32)
    mask = (
        (lines[None, :, None] < sides[:, None, None])
        & (spots[None, None, :] < sides[:, None, None])
    ).astype(jnp.float32)[None, :, :, :, None]
    area = jnp.sum(clip_size * clip_size).astype(jnp.float32)
    count_slow = TS * area
    count_fast = TF * area
    params = (
        w_lateral,
        w_slow_time,
        w_slow_space,
        w_slow_point,
        w_fast_time,
        w_fast_space,
        w_fast_point,
        gain_slow,
        bias_slow,
        gain_fast,
        bias_fast,
    )
    slow = x_slow[:, :, 0].astype(jnp.float32) * mask
    fast = x_fast[:, :, 0].astype(jnp.float32) * mask
    kept_all = []
    for block in range(BLOCKS):
        weights = tuple((value[block] for value in params))
        slow, fast, kept = forward_block(slow, fast, weights, mask, half, count_slow, count_fast)
        kept_all.append(kept)
    out_slow = slow[:, :, None]
    out_fast = fast[:, :, None]
    d_slow = cot_slow[:, :, 0].astype(jnp.float32)
    d_fast = cot_fast[:, :, 0].astype(jnp.float32)
    grads_all = [None] * BLOCKS
    for block in reversed(range(BLOCKS)):
        weights = tuple((value[block] for value in params))
        d_slow, d_fast, grads = backward_block(
            d_slow, d_fast, kept_all[block], weights, mask, half, count_slow, count_fast
        )
        grads_all[block] = tuple(reduce_weights(grads[:7])) + grads[7:]
    stacked = [
        jnp.stack([grads_all[block][index] for block in range(BLOCKS)]) for index in range(11)
    ]
    weight_tot = stacked[:7]
    grad_x_slow = (d_slow * mask)[:, :, None]
    grad_x_fast = (d_fast * mask)[:, :, None]
    return (
        out_slow,
        out_fast,
        grad_x_slow,
        grad_x_fast,
        weight_tot[0],
        weight_tot[1],
        weight_tot[2],
        weight_tot[3],
        weight_tot[4],
        weight_tot[5],
        weight_tot[6],
        stacked[7],
        stacked[8],
        stacked[9],
        stacked[10],
    )


def solution(mesh):
    in_specs = (
        P("path", None, "rows", None, None, None),
        P("path", None, "rows", None, None, None),
        P(),
        P(),
        P(),
        P(),
        P(),
        P(),
        P(),
        P(),
        P(),
        P(),
        P(),
        P(),
        P("path", None, "rows", None, None, None),
        P("path", None, "rows", None, None, None),
    )
    out_specs = (
        P("path", None, "rows", None, None, None),
        P("path", None, "rows", None, None, None),
        P("path", None, "rows", None, None, None),
        P("path", None, "rows", None, None, None),
        P(),
        P(),
        P(),
        P(),
        P(),
        P(),
        P(),
        P(),
        P(),
        P(),
        P(),
    )
    return jax.shard_map(
        on_device, mesh=mesh, in_specs=in_specs, out_specs=out_specs, check_vma=False
    )
```

```python
import functools

import jax
import jax.numpy as jnp
from jax import lax
from jax.experimental import pallas as pl
from jax.experimental.pallas import tpu as pltpu
from jax.sharding import PartitionSpec as P

TS = 8
TF = 32
F32 = jnp.float32
BF16 = jnp.bfloat16
EPSILON = 1e-05
LANES = 128
AXES = ("path", "rows")


def swap(value, axis, stride):
    pairs = [(source, source ^ stride) for source in range(lax.axis_size(axis))]
    return lax.ppermute(value, axis, pairs)


def from_before(value):
    size = lax.axis_size("path")
    return lax.ppermute(value, "path", [(i, i + 1) for i in range(size - 1)])


def from_after(value):
    size = lax.axis_size("path")
    return lax.ppermute(value, "path", [(i + 1, i) for i in range(size - 1)])


def gather_sums(parts):
    row = jnp.concatenate(parts, axis=1)
    total = lax.axis_size("path") * lax.axis_size("rows")
    spread = jnp.broadcast_to(row[None], (total,) + row.shape)
    return lax.all_to_all(spread, AXES, 0, 0, tiled=True)


def exchange_steps():
    steps = [("rows", 1), ("path", 1)]
    stride = 2
    while stride < lax.axis_size("rows"):
        steps.append(("rows", stride))
        stride *= 2
    return steps


def reduce_rows(value):
    steps = exchange_steps()
    for axis, stride in steps:
        size = value.shape[0] // 2
        upper = (lax.axis_index(axis) // stride) % 2
        keep = lax.dynamic_slice_in_dim(value, upper * size, size, 0)
        give = lax.dynamic_slice_in_dim(value, (1 - upper) * size, size, 0)
        value = keep + swap(give.astype(BF16), axis, stride).astype(F32)
    value = value.astype(BF16)
    for axis, stride in reversed(steps):
        upper = (lax.axis_index(axis) // stride) % 2
        got = swap(value, axis, stride)
        value = jnp.concatenate(
            [jnp.where(upper == 0, value, got), jnp.where(upper == 0, got, value)], axis=0
        )
    return value


def run(body, outs, args, scratch=(), flops=0, name=None):
    moved = sum(a.size * a.dtype.itemsize for a in args)
    moved += sum(o.size * o.dtype.itemsize for o in outs)
    return pl.pallas_call(
        body,
        out_shape=tuple(outs),
        in_specs=[pl.BlockSpec(memory_space=pltpu.VMEM) for _ in args],
        out_specs=tuple(pl.BlockSpec(memory_space=pltpu.VMEM) for _ in outs),
        scratch_shapes=list(scratch),
        compiler_params=pltpu.CompilerParams(vmem_limit_bytes=32 * 2**20),
        cost_estimate=pl.CostEstimate(flops=flops, bytes_accessed=moved, transcendentals=0),
        name=name,
    )(*args)


def shape(dims, dtype=F32):
    return jax.ShapeDtypeStruct(tuple(dims), dtype)


class Masks:
    def __init__(self, spots, cols):
        self.main = (0, spots)
        self.ext = (spots, 2 * spots + 2 * cols)
        self.prev = (2 * spots + 2 * cols, 3 * spots + 2 * cols)
        self.next = (3 * spots + 2 * cols, 4 * spots + 2 * cols)
        self.slow = (4 * spots + 2 * cols, 4 * spots + 2 * cols + 8)
        self.fast = (4 * spots + 2 * cols + 8, 4 * spots + 2 * cols + 16)


def widen(rows, width):
    return jnp.concatenate([rows] * (width // LANES), axis=1)


def sublane_sums(value):
    return jnp.sum(value.reshape(value.shape[0] // 8, 8, value.shape[1]), axis=0)


def row_sum(value):
    return jnp.sum(value, axis=0, keepdims=True)


def fold_packed(row):
    full = jnp.broadcast_to(row, (8, LANES))
    full = full + pltpu.roll(full, 64, 1)
    full = full + pltpu.roll(full, 32, 1)
    return full[0:1]


def totals(st, lo, width, packed=False):
    first = jnp.sum(st[:, :, lo : lo + width], axis=0)
    second = jnp.sum(st[:, :, lo + width : lo + 2 * width], axis=0)
    if packed:
        return fold_packed(first), fold_packed(second)
    return first, second


def norm_rows(st, lo, width, count, packed=False):
    first, second = totals(st, lo, width, packed)
    mean = first / count
    return mean, lax.rsqrt(second / count - mean * mean + EPSILON)


def sigmoid(value):
    return 0.5 * jnp.tanh(0.5 * value) + 0.5


def silu(value):
    return value * sigmoid(value)


def silu_slope(value):
    sigma = sigmoid(value)
    return sigma * (1.0 + value * (1.0 - sigma))


def dot(a, b):
    return jnp.dot(a, b, preferred_element_type=F32)


def dot_nt(a, b):
    return lax.dot_general(a, b, (((1,), (1,)), ((), ())), preferred_element_type=F32)


def dot_tn(a, b):
    return lax.dot_general(a, b, (((0,), (0,)), ((), ())), preferred_element_type=F32)


def flat(value):
    return value.reshape(value.shape[0] * value.shape[1], value.shape[2])


def store_shifts(dst, t, value, cols):
    rows, width = value.shape
    spot = lax.broadcasted_iota(jnp.int32, (rows, width), 0) & (cols - 1)
    left = jnp.where(spot == 0, 0.0, pltpu.roll(value, 1, 0))
    right = jnp.where(spot == cols - 1, 0.0, pltpu.roll(value, rows - 1, 0))
    dst[t, :, 0:width] = left.astype(BF16)
    dst[t, :, width : 2 * width] = value.astype(BF16)
    dst[t, :, 2 * width : 3 * width] = right.astype(BF16)


def taps_of(frames_ref, frames, group):
    return jnp.concatenate(
        [
            jnp.concatenate([frames_ref[group * t + f] for f in range(7)], axis=1)
            for t in range(frames)
        ],
        axis=0,
    )


def entry_sums(y, lat, frames, spots):
    width = y.shape[1]
    one = jnp.zeros((8, width), F32)
    two = jnp.zeros((8, width), F32)
    for t in range(frames):
        part = y[t * spots : (t + 1) * spots]
        one = one + sublane_sums(part)
        two = two + sublane_sums(part * part)
    one = row_sum(one)
    two = row_sum(two)
    return jnp.concatenate([one[:, :lat], two[:, :lat], one[:, lat:], two[:, lat:]], axis=1)


def fast_entry(m, frames, group, x, before, after, mk, w7, fw, y, s):
    spots = x.shape[1]
    count = x.shape[0]

    def put(at, value, span):
        fw[at] = (value.astype(F32) * mk[span[0] : span[1], :]).astype(BF16)

    for k in range(2):
        put(k, before[k], m.prev)
        put(2 + count + k, after[k], m.next)
    for k in range(count):
        put(2 + k, x[k], m.main)
    out = dot(taps_of(fw, frames, group), w7[...])
    for t in range(frames):
        y[t] = out[t * spots : (t + 1) * spots]
    s[...] = entry_sums(out, w7.shape[1] - LANES, frames, spots)


def slow_partial(m, frames, x, before, after, mk, wt, xm, fpart):
    spots, wide = x.shape[1], x.shape[2]
    sources = [(before, m.prev)] + [(x.at[t], m.main) for t in range(frames)] + [(after, m.next)]
    for k, (src, span) in enumerate(sources):
        for lo in range(0, wide, 256):
            mask = widen(mk[span[0] : span[1], :], 256)
            xm[k, :, lo : lo + 256] = (src[:, lo : lo + 256].astype(F32) * mask).astype(BF16)
    out = dot(flat(xm[0:frames]), wt[0, :wide, :])
    for j in range(1, 3):
        out = out + dot(flat(xm[j : j + frames]), wt[j, :wide, :])
    for t in range(frames):
        fpart[t] = out[t * spots : (t + 1) * spots]


def lat_join(m, n, frames, lat, st, y, before, after, fpart, wt, gs, bs, mk, jl, first, s, nl, jw):
    spots = y.shape[1]
    wide = wt.shape[1] - lat
    count = widen(mk[m.slow[0] : m.slow[0] + 1, :], lat)
    mean, rstd = norm_rows(st, 0, lat, count)
    nl[0:1, :] = mean
    nl[1:2, :] = rstd
    scale = rstd * gs[n : n + 1, 0:lat]
    bias = bs[n : n + 1, 0:lat]
    sources = (
        [(before[:, 0:lat], m.prev)]
        + [(y[t, :, 0:lat], m.main) for t in range(frames)]
        + [(after[:, 0:lat], m.next)]
    )
    for k, (value, span) in enumerate(sources):
        mask = widen(mk[span[0] : span[1], :], lat)
        act = (silu((value - mean) * scale + bias) * mask).astype(BF16)
        jw[k] = act
        if 1 <= k <= frames:
            jl[k - 1] = act
    out = flat(fpart[...])
    for j in range(3):
        out = out + dot(flat(jw[j : j + frames]), wt[j, wide:, :])
    one = jnp.zeros((8, out.shape[1]), F32)
    two = jnp.zeros((8, out.shape[1]), F32)
    for t in range(frames):
        part = out[t * spots : (t + 1) * spots]
        first[t] = part
        one = one + sublane_sums(part)
        two = two + sublane_sums(part * part)
    s[...] = jnp.concatenate([row_sum(one), row_sum(two)], axis=1)


def space_forward(
    m, n, frames, cols, lo, at, width, col0, packed, span, st, z, row, w, g, b, mk, aw, out, s, nz, vw
):
    spots = z.shape[1]
    count = widen(mk[span[0] : span[0] + 1, :], width)
    mean, rstd = norm_rows(st, at, width, count, packed)
    nz[0:1, :] = mean
    nz[1:2, :] = rstd
    scale = rstd * g[n : n + 1, lo : lo + width]
    bias = b[n : n + 1, lo : lo + width]
    mask = widen(mk[m.ext[0] : m.ext[1], :], width)
    for t in range(frames):
        value = jnp.concatenate([row[t], z[t, :, col0 : col0 + width], row[t]], axis=0)
        act = silu((value - mean) * scale + bias) * mask
        aw[t] = act.astype(BF16)
        store_shifts(vw, t, act, cols)
    total = dot(flat(vw[:, 0:spots, :]), w[0])
    for i in range(1, 3):
        total = total + dot(flat(vw[:, i * cols : i * cols + spots, :]), w[i])
    mask = widen(mk[m.main[0] : m.main[1], :], width)
    one = jnp.zeros((8, width), F32)
    two = jnp.zeros((8, width), F32)
    for t in range(frames):
        part = total[t * spots : (t + 1) * spots]
        out[t] = part
        part = part * mask
        one = one + sublane_sums(part)
        two = two + sublane_sums(part * part)
    s[...] = jnp.concatenate([row_sum(one), row_sum(two)], axis=1)


def slow_third(m, n, frames, lo, halo, st, z, *rest):
    if halo:
        before, after, wp, g, b, mk, a2, third, s, nz, aw = rest
    else:
        wp, g, b, mk, a2, third, s, nz, aw = rest
    spots, width = z.shape[1], z.shape[2]
    wide = wp.shape[1]
    count = widen(mk[m.slow[0] : m.slow[0] + 1, :], width)
    mean, rstd = norm_rows(st, 0, width, count)
    nz[0:1, :] = mean
    nz[1:2, :] = rstd
    scale = rstd * g[n : n + 1, lo : lo + width]
    bias = b[n : n + 1, lo : lo + width]
    sources = [(z[t], m.main, t + halo) for t in range(frames)]
    if halo:
        sources += [(before[...], m.prev, 0), (after[...], m.next, frames + 1)]
    for value, span, at in sources:
        mask = widen(mk[span[0] : span[1], :], width)
        act = (silu((value - mean) * scale + bias) * mask).astype(BF16)
        aw[at] = act
        if halo <= at < frames + halo:
            a2[at - halo] = act
    acts = flat(aw[...])
    ones, twos = [], []
    for at in range(0, wide, 256):
        out = dot(acts, wp[:, at : at + 256])
        one = jnp.zeros((8, 256), F32)
        two = jnp.zeros((8, 256), F32)
        for t in range(frames + 2 * halo):
            part = out[t * spots : (t + 1) * spots]
            third[t, :, at : at + 256] = part
            if halo <= t < frames + halo:
                one = one + sublane_sums(part)
                two = two + sublane_sums(part * part)
        ones.append(row_sum(one))
        twos.append(row_sum(two))
    s[...] = jnp.concatenate(ones + twos, axis=1)


def fast_third(m, n, frames, lo, at, st, z, wp, g, b, mk, a2, ft, s, nz):
    spots = z.shape[1]
    count = mk[m.fast[0] : m.fast[0] + 1, :]
    mean, rstd = norm_rows(st, at, LANES, count, True)
    nz[0:1, :] = mean
    nz[1:2, :] = rstd
    scale = rstd * g[n : n + 1, lo : lo + LANES]
    bias = b[n : n + 1, lo : lo + LANES]
    mask = mk[m.main[0] : m.main[1], :]
    for t in range(frames):
        a2[t] = (silu((z[t] - mean) * scale + bias) * mask).astype(BF16)
    acts = flat(a2[...])
    one = jnp.zeros((8, LANES), F32)
    two = jnp.zeros((8, LANES), F32)
    out = dot(acts, wp[...])
    for t in range(frames):
        for lane in range(0, wp.shape[1], LANES):
            part = out[t * spots : (t + 1) * spots, lane : lane + LANES]
            ft[t, :, lane : lane + LANES] = part
            one = one + sublane_sums(part)
            two = two + sublane_sums(part * part)
    s[...] = jnp.concatenate([row_sum(one), row_sum(two)], axis=1)


def fast_next(m, n, frames, group, lo, at, st, ft, before, after, fw0, w7, g, b, mk, f1, fw1, y, s, nz):
    spots = ft.shape[1]
    count = mk[m.fast[0] : m.fast[0] + 1, :]
    mean, rstd = norm_rows(st, at, LANES, count)
    nz[0:1, :] = mean
    nz[1:2, :] = rstd
    scale = rstd * g[n : n + 1, lo : lo + LANES]
    bias = b[n : n + 1, lo : lo + LANES]
    total = frames * group

    def out_of(k, value, span):
        z = fw0[k].astype(F32) + ((value - mean) * scale + bias)
        return silu(z) * mk[span[0] : span[1], :]

    for k in range(2):
        lane = k * LANES
        fw1[k] = out_of(k, before[:, lane : lane + LANES], m.prev).astype(BF16)
        fw1[2 + total + k] = out_of(2 + total + k, after[:, lane : lane + LANES], m.next).astype(BF16)
    for t in range(frames):
        for f in range(group):
            k = t * group + f
            value = out_of(2 + k, ft[t, :, f * LANES : (f + 1) * LANES], m.main)
            f1[k] = value
            fw1[2 + k] = value.astype(BF16)
    out = dot(taps_of(fw1, frames, group), w7[...])
    for t in range(frames):
        y[t] = out[t * spots : (t + 1) * spots]
    s[...] = entry_sums(out, w7.shape[1] - LANES, frames, spots)


def fast_last(m, n, frames, group, lo, at, st, ft, f1, cot, g, b, mk, out, pre, s, nz):
    count = mk[m.fast[0] : m.fast[0] + 1, :]
    mean, rstd = norm_rows(st, at, LANES, count)
    nz[0:1, :] = mean
    nz[1:2, :] = rstd
    gain = g[n : n + 1, lo : lo + LANES]
    bias = b[n : n + 1, lo : lo + LANES]
    mask = mk[m.main[0] : m.main[1], :]
    one = jnp.zeros((8, LANES), F32)
    two = jnp.zeros((8, LANES), F32)
    for t in range(frames):
        for f in range(group):
            k = t * group + f
            hat = (ft[t, :, f * LANES : (f + 1) * LANES] - mean) * rstd
            z = f1[k] + hat * gain + bias
            sigma = sigmoid(z)
            out[k] = z * sigma * mask
            grad = cot[k].astype(F32) * mask * (sigma * (1.0 + z * (1.0 - sigma)))
            pre[k] = grad
            one = one + sublane_sums(grad)
            two = two + sublane_sums(grad * hat)
    s[...] = jnp.concatenate([row_sum(one), row_sum(two)], axis=1)


def chunked(total, step, body, init):
    def turn(i, carry):
        return body(pl.multiple_of(i * step, step), carry)

    return lax.fori_loop(0, total // step, turn, init)


def slow_next(m, n, frames, lo, at0, st, third, xm, wt, g, b, mk, slow1, sw, fpart, nz):
    spots, wide = third.shape[1], third.shape[2]
    count = widen(mk[m.slow[0] : m.slow[0] + 1, :], wide)
    mean, rstd = norm_rows(st, at0, wide, count)
    nz[0:1, :] = mean
    nz[1:2, :] = rstd
    scale = rstd * g[n : n + 1, lo : lo + wide]
    bias = b[n : n + 1, lo : lo + wide]
    spans = [m.prev] + [m.main] * frames + [m.next]
    for k, span in enumerate(spans):

        def turn(at, carry, k=k, span=span):
            mask = widen(mk[pl.ds(span[0] + at, 16), :], 512)
            for c in range(0, wide, 512):
                z = third[k, pl.ds(at, 16), c : c + 512]
                z = (z - mean[:, c : c + 512]) * scale[:, c : c + 512] + bias[:, c : c + 512]
                z = xm[k, pl.ds(at, 16), c : c + 512].astype(F32) + z
                value = silu(z) * mask
                sw[k, pl.ds(at, 16), c : c + 512] = value.astype(BF16)
                if 1 <= k <= frames:
                    slow1[k - 1, pl.ds(at, 16), c : c + 512] = value
            return carry

        chunked(spots, 16, turn, 0)
    out = dot(flat(sw[0:frames]), wt[0, :wide, :])
    for j in range(1, 3):
        out = out + dot(flat(sw[j : j + frames]), wt[j, :wide, :])
    for t in range(frames):
        fpart[t] = out[t * spots : (t + 1) * spots]


def slow_last(m, n, frames, lo, st, third, slow1, cot, g, b, mk, out, pre, s, nz):
    spots, wide = third.shape[1], third.shape[2]
    count = widen(mk[m.slow[0] : m.slow[0] + 1, :], wide)
    mean, rstd = norm_rows(st, 0, wide, count)
    nz[0:1, :] = mean
    nz[1:2, :] = rstd
    gain = g[n : n + 1, lo : lo + wide]
    bias = b[n : n + 1, lo : lo + wide]
    carry = (jnp.zeros((8, wide), F32), jnp.zeros((8, wide), F32))
    for t in range(frames):

        def turn(at, sums, t=t):
            one, two = sums
            ones, twos = [], []
            mask = widen(mk[pl.ds(m.main[0] + at, 16), :], 512)
            for c in range(0, wide, 512):
                hat = (third[t, pl.ds(at, 16), c : c + 512] - mean[:, c : c + 512]) * rstd[:, c : c + 512]
                z = slow1[t, pl.ds(at, 16), c : c + 512] + hat * gain[:, c : c + 512] + bias[:, c : c + 512]
                sigma = sigmoid(z)
                out[t, pl.ds(at, 16), c : c + 512] = z * sigma * mask
                grad = cot[t, pl.ds(at, 16), c : c + 512].astype(F32) * mask
                grad = grad * (sigma * (1.0 + z * (1.0 - sigma)))
                pre[t, pl.ds(at, 16), c : c + 512] = grad
                ones.append(sublane_sums(grad))
                twos.append(sublane_sums(grad * hat))
            return one + jnp.concatenate(ones, axis=1), two + jnp.concatenate(twos, axis=1)

        carry = chunked(spots, 16, turn, carry)
    s[...] = jnp.concatenate([row_sum(carry[0]), row_sum(carry[1])], axis=1)


def slow_third_back(m, n, frames, lo3, lo2, at, halo, st, pre, third, n3, z, n2, wp, g, b, mk, d3, e2, s, gb):
    spots, wide = pre.shape[1], pre.shape[2]
    width = z.shape[2]
    count = widen(mk[m.slow[0] : m.slow[0] + 1, :], wide)
    one, two = totals(st, at, wide)
    gb[0:1, :] = one
    gb[1:2, :] = two
    mean, rstd = n3[0:1, :], n3[1:2, :]
    scale = g[n : n + 1, lo3 : lo3 + wide] * rstd
    one = one / count
    two = two / count * rstd
    for t in range(frames):

        def turn(i, carry, t=t):
            mask = widen(mk[pl.ds(m.main[0] + i, 16), :], 512)
            for c in range(0, wide, 512):
                hat = (third[t + halo, pl.ds(i, 16), c : c + 512] - mean[:, c : c + 512]) * two[:, c : c + 512]
                grad = pre[t, pl.ds(i, 16), c : c + 512] - mask * (one[:, c : c + 512] + hat)
                d3[t, pl.ds(i, 16), c : c + 512] = (scale[:, c : c + 512] * grad).astype(BF16)
            return carry

        chunked(spots, 16, turn, 0)
    out = dot_nt(flat(d3[...]), wp[...])
    mean, rstd = n2[0:1, :], n2[1:2, :]
    gain = g[n : n + 1, lo2 : lo2 + width]
    bias = b[n : n + 1, lo2 : lo2 + width]
    back_act(m, frames, spots, out, z, 0, mean, rstd, gain, bias, mk, e2, s)


def back_act(m, frames, spots, out, z, col0, mean, rstd, gain, bias, mk, e, s):
    width = out.shape[1]
    mask = widen(mk[m.main[0] : m.main[1], :], width)
    one = jnp.zeros((8, width), F32)
    two = jnp.zeros((8, width), F32)
    for t in range(frames):
        hat = (z[t, :, col0 : col0 + width] - mean) * rstd
        grad = out[t * spots : (t + 1) * spots] * mask * silu_slope(hat * gain + bias)
        e[t] = grad
        one = one + sublane_sums(grad)
        two = two + sublane_sums(grad * hat)
    s[...] = jnp.concatenate([row_sum(one), row_sum(two)], axis=1)


def fast_third_back(m, n, frames, group, lo3, lo2, at, st, pre, ft, n3, z, n2, wp, g, b, mk, d3, e2, s, gb):
    spots = z.shape[1]
    count = mk[m.fast[0] : m.fast[0] + 1, :]
    one, two = totals(st, at, LANES)
    gb[0:1, :] = one
    gb[1:2, :] = two
    mean, rstd = n3[0:1, :], n3[1:2, :]
    scale = g[n : n + 1, lo3 : lo3 + LANES] * rstd
    one = one / count
    two = two / count * rstd
    mask = mk[m.main[0] : m.main[1], :]
    for t in range(frames):
        for f in range(group):
            hat = (ft[t, :, f * LANES : (f + 1) * LANES] - mean) * two
            grad = pre[t * group + f] - mask * (one + hat)
            d3[t, :, f * LANES : (f + 1) * LANES] = (scale * grad).astype(BF16)
    out = dot_nt(flat(d3[...]), wp[...])
    mean, rstd = n2[0:1, :], n2[1:2, :]
    gain = g[n : n + 1, lo2 : lo2 + LANES]
    bias = b[n : n + 1, lo2 : lo2 + LANES]
    back_act(m, frames, spots, out, z, 0, mean, rstd, gain, bias, mk, e2, s)


def space_back(
    m, n, frames, cols, lo2, lo1, at, width, col0, packed, span,
    st, e, erow, z, zrow, nz, z1, n1, w, g, b, mk, d2, e1, s, gb, vw,
):
    spots = z.shape[1]
    count = widen(mk[span[0] : span[0] + 1, :], width)
    one, two = totals(st, at, width, packed)
    gb[0:1, :] = one
    gb[1:2, :] = two
    mean, rstd = nz[0:1, :], nz[1:2, :]
    scale = g[n : n + 1, lo2 : lo2 + width] * rstd
    one = one / count
    two = two / count * rstd
    mask = widen(mk[m.ext[0] : m.ext[1], :], width)
    for t in range(frames):
        grad = jnp.concatenate([erow[t], e[t], erow[t]], axis=0)
        value = jnp.concatenate([zrow[t], z[t], zrow[t]], axis=0)
        grad = scale * mask * (grad - (one + (value - mean) * two))
        d2[t] = grad[cols : cols + spots].astype(BF16)
        store_shifts(vw, t, grad.astype(BF16).astype(F32), cols)
    total = None
    for i in range(3):
        rows = (2 - i) * cols
        for j in range(3):
            lane = (2 - j) * width
            part = dot_nt(flat(vw[:, rows : rows + spots, lane : lane + width]), w[i, j * width : (j + 1) * width, :])
            total = part if total is None else total + part
    mean, rstd = n1[0:1, :], n1[1:2, :]
    gain = g[n : n + 1, lo1 : lo1 + width]
    bias = b[n : n + 1, lo1 : lo1 + width]
    back_act(m, frames, spots, total, z1, col0, mean, rstd, gain, bias, mk, e1, s)


def slow_first_back(m, n, frames, lo1, lo3, at, halo, last, st, *rest):
    if last:
        e, ep, en, z, zp, zn, n1, wt, y, nl, pre, g, b, mk, dw, el, s, gx, gb = rest
    else:
        e, ep, en, z, zp, zn, n1, wt, y, nl, pre, xm, third, n3, g, b, mk, dw, el, s, pre0, s3, gb = rest
    spots, width = z.shape[1], z.shape[2]
    lat = nl.shape[1]
    wide = wt.shape[1] - lat
    count = widen(mk[m.slow[0] : m.slow[0] + 1, :], width)
    one, two = totals(st, at, width)
    gb[0:1, :] = one
    gb[1:2, :] = two
    mean, rstd = n1[0:1, :], n1[1:2, :]
    scale = g[n : n + 1, lo1 : lo1 + width] * rstd
    one = one / count
    two = two / count * rstd
    sources = (
        [(ep, zp, m.prev)] + [(e.at[t], z.at[t], m.main) for t in range(frames)] + [(en, zn, m.next)]
    )
    for k, (grad, value, span) in enumerate(sources):
        mask = widen(mk[span[0] : span[1], :], width)
        dw[k] = (scale * mask * (grad[...] - (one + (value[...] - mean) * two))).astype(BF16)
    taps = [flat(dw[2 - j : 2 - j + frames]) for j in range(3)]

    def back(lo, size):
        out = dot_nt(taps[0], wt[0, lo : lo + size, :])
        for j in range(1, 3):
            out = out + dot_nt(taps[j], wt[j, lo : lo + size, :])
        return out

    out = back(wide, lat)
    back_act(
        m, frames, spots, out, y, 0, nl[0:1, :], nl[1:2, :], g[n : n + 1, 0:lat], b[n : n + 1, 0:lat], mk, el, s
    )
    mask = widen(mk[m.main[0] : m.main[1], :], 256)
    ones, twos = [], []
    for c in range(0, wide, 256):
        out = back(c, 256)
        if not last:
            mean, rstd = n3[0:1, c : c + 256], n3[1:2, c : c + 256]
            gain = g[n - 1 : n, lo3 + c : lo3 + c + 256]
            bias = b[n - 1 : n, lo3 + c : lo3 + c + 256]
            one = jnp.zeros((8, 256), F32)
            two = jnp.zeros((8, 256), F32)
        for t in range(frames):
            grad = (out[t * spots : (t + 1) * spots] + pre[t, :, c : c + 256]) * mask
            if last:
                gx[t, :, c : c + 256] = grad
            else:
                hat = (third[t + halo, :, c : c + 256] - mean) * rstd
                z0 = xm[t + 1, :, c : c + 256].astype(F32) + hat * gain + bias
                grad = grad * silu_slope(z0)
                pre0[t, :, c : c + 256] = grad
                one = one + sublane_sums(grad)
                two = two + sublane_sums(grad * hat)
        if not last:
            ones.append(row_sum(one))
            twos.append(row_sum(two))
    if not last:
        s3[...] = jnp.concatenate(ones + twos, axis=1)


def fast_first_back(m, n, frames, group, lo1, lo3, at1, atl, last, st1, stl, *rest):
    if last:
        el, eln, ef, efp, efn, y, yp, yn, nl, n1, w7, pre, gs, g, b, mk, dl, dfw, gx, gbl, gb1, buf = rest
    else:
        (el, eln, ef, efp, efn, y, yp, yn, nl, n1, w7, pre, fw0, ft, n3, gs, g, b, mk,
         dl, dfw, pre0, s, gbl, gb1, buf) = rest
    spots = y.shape[1]
    lat = nl.shape[1]
    count = widen(mk[m.slow[0] : m.slow[0] + 1, :], lat)
    one, two = totals(stl, atl, lat)
    gbl[0:1, :] = one
    gbl[1:2, :] = two
    mean, rstd = nl[0:1, :], nl[1:2, :]
    scale = gs[n : n + 1, 0:lat] * rstd
    one = one / count
    two = two / count * rstd

    def lat_grad(grad, value, span):
        mask = widen(mk[span[0] : span[1], :], lat)
        return (scale * mask * (grad - (one + (value - mean) * two))).astype(BF16)

    for t in range(frames):
        dl[t] = lat_grad(el[t], y[t, :, 0:lat], m.main)
    dl_next = lat_grad(eln[...], yn[:, 0:lat], m.next)
    fcount = mk[m.fast[0] : m.fast[0] + 1, :]
    fone, ftwo = totals(st1, at1, LANES, True)
    gb1[0:1, :] = fone
    gb1[1:2, :] = ftwo
    fmean, frstd = n1[0:1, :], n1[1:2, :]
    fscale = g[n : n + 1, lo1 : lo1 + LANES] * frstd
    fone = fone / fcount
    ftwo = ftwo / fcount * frstd

    def first_grad(grad, value, span):
        mask = mk[span[0] : span[1], :]
        return (fscale * mask * (grad - (fone + (value - fmean) * ftwo))).astype(BF16)

    for t in range(frames):
        dfw[t] = first_grad(ef[t], y[t, :, lat:], m.main)
    df_prev = first_grad(efp[...], yp[:, lat:], m.prev)
    df_next = first_grad(efn[...], yn[:, lat:], m.next)
    both = jnp.concatenate([flat(dl[...]), flat(dfw[...])], axis=1)
    buf[...] = jnp.zeros(buf.shape, F32)
    out = dot_nt(both, w7[...])
    for t in range(frames):
        for f in range(7):
            k = group * t + f
            buf[k] = buf[k] + out[t * spots : (t + 1) * spots, f * LANES : (f + 1) * LANES]
    buf[2] = buf[2] + dot_nt(df_prev, w7[6 * LANES : 7 * LANES, lat:])
    after = dot_nt(jnp.concatenate([dl_next, df_next], axis=1), w7[0 : 2 * LANES, :])
    total = frames * group
    for f in range(2):
        buf[total + f] = buf[total + f] + after[:, f * LANES : (f + 1) * LANES]
    mask = mk[m.main[0] : m.main[1], :]
    if last:
        for k in range(total):
            gx[k] = (pre[k] + buf[2 + k]) * mask
        return
    mean, rstd = n3[0:1, :], n3[1:2, :]
    gain = g[n - 1 : n, lo3 : lo3 + LANES]
    bias = b[n - 1 : n, lo3 : lo3 + LANES]
    one = jnp.zeros((8, LANES), F32)
    two = jnp.zeros((8, LANES), F32)
    for k in range(total):
        t, f = k // group, k % group
        hat = (ft[t, :, f * LANES : (f + 1) * LANES] - mean) * rstd
        z0 = fw0[2 + k].astype(F32) + hat * gain + bias
        grad = (pre[k] + buf[2 + k]) * mask * silu_slope(z0)
        pre0[k] = grad
        one = one + sublane_sums(grad)
        two = two + sublane_sums(grad * hat)
    s[...] = jnp.concatenate([row_sum(one), row_sum(two)], axis=1)


def point_weights(a2, d3, out):
    acts = flat(a2[...])
    for k in range(out.shape[0]):
        out[k] = dot_tn(acts, flat(d3[:, :, k * 256 : (k + 1) * 256]))


def space_weights(cols, aw, d2, out, vw):
    frames, spots, width = d2.shape
    for t in range(frames):
        store_shifts(vw, t, aw[t].astype(F32), cols)
    grads = flat(d2[...])
    for i in range(3):
        out[i] = dot_tn(flat(vw[:, i * cols : i * cols + spots, :]), grads)


def time_weights(skip, slow, jl, dw, out):
    frames, spots, width = jl.shape
    wide = slow.shape[2]
    grads = jnp.concatenate([flat(dw[2 - j : 2 - j + frames]) for j in range(3)], axis=1)
    for c in range(0, wide + jl.shape[2], 256):
        if c < wide:
            acts = flat(slow[skip : skip + frames, :, c : c + 256])
        else:
            acts = flat(jl[:, :, c - wide : c - wide + 256])
        got = dot_tn(acts, grads)
        for j in range(3):
            out[j, c : c + 256, :] = got[:, j * width : (j + 1) * width]


def group_blocks(value, group):
    size = LANES // group
    rows = lax.broadcasted_iota(jnp.int32, (LANES, LANES), 0) >> (size.bit_length() - 1)
    lanes = lax.broadcasted_iota(jnp.int32, (LANES, LANES), 1) >> (size.bit_length() - 1)
    kept = jnp.where(rows == lanes, value, 0.0)
    kept = kept + pltpu.roll(kept, 64, 1)
    kept = kept + pltpu.roll(kept, 32, 1)
    total = kept[0:size]
    for k in range(1, group):
        total = total + kept[k * size : (k + 1) * size]
    return total


def at_lanes(blocks):
    lanes = lax.broadcasted_iota(jnp.int32, blocks[0].shape, 1) >> 5
    out = jnp.zeros(blocks[0].shape, F32)
    for k, block in enumerate(blocks):
        out = jnp.where(lanes == k, block, out)
    return out


def fast_weights(group, cols, lat, fw, dl, df, fa1, d2, fa2, d3, glat, gfast, vw):
    frames, spots, _ = dl.shape
    size = LANES // group
    both = jnp.concatenate([flat(dl[...]), flat(df[...])], axis=1)
    taps = [[None] * group for _ in range(3)]
    for f in range(7):
        acts = jnp.concatenate([fw[group * t + f] for t in range(frames)], axis=0)
        got = dot_tn(acts, both)
        if f < 5:
            glat[f * LANES : (f + 1) * LANES, :] = got[:, :lat]
        for k in range(group):
            if 0 <= f - k - 1 < 3:
                taps[f - k - 1][k] = got[:, lat:]
    lanes = lax.broadcasted_iota(jnp.int32, (LANES, LANES), 1) >> (size.bit_length() - 1)
    tap_sums = []
    for j in range(3):
        kept = jnp.zeros((LANES, LANES), F32)
        for k in range(group):
            kept = jnp.where(lanes == k, taps[j][k], kept)
        kept = kept + pltpu.roll(kept, 64, 1)
        tap_sums.append(kept + pltpu.roll(kept, 32, 1))
    gfast[0:LANES, :] = at_lanes(tap_sums)
    for t in range(frames):
        store_shifts(vw, t, fa1[t].astype(F32), cols)
    grads = flat(d2[...])
    for i in range(3):
        got = dot_tn(flat(vw[:, i * cols : i * cols + spots, :]), grads)
        blocks = [group_blocks(got[j * LANES : (j + 1) * LANES], group) for j in range(3)]
        gfast[LANES + size * i : LANES + size * (i + 1), :] = at_lanes(blocks)
    acts = flat(fa2[...])
    total = jnp.zeros((size, LANES), F32)
    for k in range(group):
        got = dot_tn(acts, flat(d3[:, :, k * LANES : (k + 1) * LANES]))
        total = total + got[k * size : (k + 1) * size]
    gfast[LANES + 3 * size : LANES + 4 * size, :] = total


def on_device(
    x_slow,
    x_fast,
    w_lateral,
    w_slow_time,
    w_slow_space,
    w_slow_point,
    w_fast_time,
    w_fast_space,
    w_fast_point,
    gain_slow,
    bias_slow,
    gain_fast,
    bias_fast,
    clip_size,
    cot_slow,
    cot_fast,
):
    frames, fast_frames = x_slow.shape[0], x_fast.shape[0]
    group = fast_frames // frames
    rows, cols = x_slow.shape[3], x_slow.shape[4]
    spots = rows * cols
    wide, fwide = x_slow.shape[5], x_fast.shape[5]
    lat = w_lateral.shape[3]
    width = w_slow_space.shape[3]
    inner = w_fast_space.shape[3]
    m = Masks(spots, cols)

    place = lax.axis_index("rows")
    half = place % 2
    side = lax.dynamic_slice_in_dim(clip_size, place // 2, 1, 1)[0, 0]
    area = jnp.sum(clip_size * clip_size).astype(F32)
    path = lax.axis_index("path")

    def mask_rows(first, count, valid):
        line = half * rows + first + jnp.arange(count * cols, dtype=jnp.int32) // cols
        spot = jnp.arange(count * cols, dtype=jnp.int32) % cols
        inside = (line >= 0) & (line < 2 * rows) & (line < side) & (spot < side) & valid
        return jnp.broadcast_to(inside.astype(F32)[:, None], (count * cols, LANES))

    mk = jnp.concatenate(
        [
            mask_rows(0, rows, True),
            mask_rows(-1, rows + 2, True),
            mask_rows(0, rows, path > 0),
            mask_rows(0, rows, path < lax.axis_size("path") - 1),
            jnp.full((8, LANES), TS * area),
            jnp.full((8, LANES), TF * area),
        ],
        axis=0,
    )

    w7 = jnp.concatenate(
        [jnp.pad(w_lateral.reshape(2, 5 * fwide, lat), ((0, 0), (0, 2 * fwide), (0, 0)))]
        + [
            jnp.pad(
                w_fast_time.reshape(2, 3 * fwide, inner),
                ((0, 0), (fwide * (k + 1), fwide * (3 - k)), (0, 0)),
            )
            for k in range(group)
        ],
        axis=2,
    )
    same = jnp.arange(LANES)[:, None] // inner == jnp.arange(LANES)[None, :] // inner
    wfs = jnp.where(same, jnp.tile(w_fast_space, (1, 1, 1, group, group)), 0).reshape(2, 3, 3 * LANES, LANES)
    same = jnp.arange(LANES)[:, None] // inner == jnp.arange(group * fwide)[None, :] // fwide
    wfp = jnp.where(same, jnp.tile(w_fast_point, (1, group, group)), 0)
    wsp = w_slow_space.reshape(2, 3, 3 * width, width)

    def packed(value):
        return jnp.concatenate(
            [
                jnp.tile(value[:, 0:inner], (1, group)),
                jnp.tile(value[:, inner : 2 * inner], (1, group)),
                value[:, 2 * inner :],
            ],
            axis=1,
        )

    gf, bf = packed(gain_fast), packed(bias_fast)
    lo1, lo2, lo3 = lat, lat + width, lat + 2 * width

    def own_row(value):
        return jnp.where(half == 0, value[:, spots - cols :], value[:, :cols])

    def other_row(value):
        return swap(own_row(value), "rows", 1)

    xs = x_slow.reshape(frames, spots, wide)
    xf = x_fast.reshape(fast_frames, spots, fwide)
    cs = cot_slow.reshape(frames, spots, wide)
    cf = cot_fast.reshape(fast_frames, spots, fwide)

    xf_prev, xf_next = from_before(xf[-2:]), from_after(xf[:2])
    xs_prev, xs_next = from_before(xs[-1]), from_after(xs[0])

    def part(fn, *static):
        return functools.partial(fn, *static)

    fw, y, sy = run(
        part(fast_entry, m, frames, group),
        [
            shape((fast_frames + 4, spots, fwide), BF16),
            shape((frames, spots, lat + LANES)),
            shape((1, 2 * lat + 2 * LANES)),
        ],
        [xf, xf_prev, xf_next, mk, w7[0]],
        flops=2 * frames * spots * 7 * fwide * (lat + LANES),
        name="fast_entry",
    )
    st = gather_sums([sy])
    sw, fpart = run(
        part(slow_partial, m, frames),
        [shape((frames + 2, spots, wide), BF16), shape((frames, spots, width))],
        [xs, xs_prev, xs_next, mk, w_slow_time[0]],
        flops=2 * frames * spots * 3 * wide * width,
        name="slow_partial",
    )

    saved = []
    slow1 = fast1 = None
    fast_lo = 2 * lat
    for n in range(2):
        keep = {"y": y, "fw": fw, "sw": sw}
        yp, yn = from_before(y[-1]), from_after(y[0])
        ff_row = other_row(y[:, :, lat:])
        jl, first, s_first, nl = run(
            part(lat_join, m, n, frames, lat),
            [
                shape((frames, spots, lat), BF16),
                shape((frames, spots, width)),
                shape((1, 2 * width)),
                shape((2, lat)),
            ],
            [st, y, yp, yn, fpart, w_slow_time[n], gain_slow, bias_slow, mk],
            [pltpu.VMEM((frames + 2, spots, lat), BF16)],
            flops=2 * frames * spots * 3 * lat * width,
            name="lat_join",
        )
        fa1, fs, s_fs, nf1 = run(
            part(space_forward, m, n, frames, cols, 0, fast_lo, LANES, lat, True, m.fast),
            [
                shape((frames, spots + 2 * cols, LANES), BF16),
                shape((frames, spots, LANES)),
                shape((1, 2 * LANES)),
                shape((2, LANES)),
            ],
            [st, y, ff_row, wfs[n], gf, bf, mk],
            [pltpu.VMEM((frames, spots + 2 * cols, 3 * LANES), BF16)],
            flops=2 * frames * spots * 9 * LANES * LANES,
            name="fast_space",
        )
        st = gather_sums([s_first, s_fs])
        first_row = other_row(first)
        fs_row = other_row(fs)
        firstp, firstn = from_before(first[-1]), from_after(first[0])
        a1, second, s_second, n1 = run(
            part(space_forward, m, n, frames, cols, lo1, 0, width, 0, False, m.slow),
            [
                shape((frames, spots + 2 * cols, width), BF16),
                shape((frames, spots, width)),
                shape((1, 2 * width)),
                shape((2, width)),
            ],
            [st, first, first_row, wsp[n], gain_slow, bias_slow, mk],
            [pltpu.VMEM((frames, spots + 2 * cols, 3 * width), BF16)],
            flops=2 * frames * spots * 9 * width * width,
            name="slow_space",
        )
        fa2, ft, s_ft, nf2 = run(
            part(fast_third, m, n, frames, LANES, 2 * width),
            [
                shape((frames, spots, LANES), BF16),
                shape((frames, spots, group * fwide)),
                shape((1, 2 * LANES)),
                shape((2, LANES)),
            ],
            [st, fs, wfp[n], gf, bf, mk],
            flops=2 * frames * spots * LANES * group * fwide,
            name="fast_third",
        )
        st = gather_sums([s_second, s_ft])
        second_row = other_row(second)
        halo = 1 - n
        extra = []
        if halo:
            extra = [from_before(second[-1]), from_after(second[0])]
            ftp = from_before(ft[-1, :, (group - 2) * fwide :])
            ftn = from_after(ft[0, :, : 2 * fwide])
        a2, third, s_third, n2 = run(
            part(slow_third, m, n, frames, lo2, halo),
            [
                shape((frames, spots, width), BF16),
                shape((frames + 2 * halo, spots, wide)),
                shape((1, 2 * wide)),
                shape((2, width)),
            ],
            [st, second] + extra + [w_slow_point[n], gain_slow, bias_slow, mk],
            [pltpu.VMEM((frames + 2 * halo, spots, width), BF16)],
            flops=2 * frames * spots * width * wide,
            name="slow_third",
        )
        keep.update(
            yp=yp, yn=yn, jl=jl, first=first, firstp=firstp, firstn=firstn, nl=nl, fa1=fa1, fs=fs, fs_row=fs_row,
            nf1=nf1, a1=a1, second=second, second_row=second_row, n1=n1, fa2=fa2, ft=ft, nf2=nf2, a2=a2,
            third=third, n2=n2,
        )
        if n == 0:
            fast1, fw, y, sy, nf3 = run(
                part(fast_next, m, n, frames, group, 2 * LANES, 2 * width),
                [
                    shape((fast_frames, spots, fwide)),
                    shape((fast_frames + 4, spots, fwide), BF16),
                    shape((frames, spots, lat + LANES)),
                    shape((1, 2 * lat + 2 * LANES)),
                    shape((2, LANES)),
                ],
                [st, ft, ftp, ftn, fw, w7[1], gf, bf, mk],
                flops=2 * frames * spots * 7 * fwide * (lat + LANES),
                name="fast_next",
            )
            st3 = gather_sums([sy, s_third])
            slow1, sw, fpart, n3 = run(
                part(slow_next, m, n, frames, lo3, 2 * lat + 2 * LANES),
                [
                    shape((frames, spots, wide)),
                    shape((frames + 2, spots, wide), BF16),
                    shape((frames, spots, width)),
                    shape((2, wide)),
                ],
                [st3, third, sw, w_slow_time[1], gain_slow, bias_slow, mk],
                flops=2 * frames * spots * 3 * wide * width,
                name="slow_next",
            )
            st = st3
        else:
            out_fast, pre_f, s_pf, nf3 = run(
                part(fast_last, m, n, frames, group, 2 * LANES, 2 * width),
                [
                    shape((fast_frames, spots, fwide)),
                    shape((fast_frames, spots, fwide)),
                    shape((1, 2 * LANES)),
                    shape((2, LANES)),
                ],
                [st, ft, fast1, cf, gf, bf, mk],
                name="fast_last",
            )
            st = gather_sums([s_third, s_pf])
            out_slow, pre, s_pre, n3 = run(
                part(slow_last, m, n, frames, lo3),
                [
                    shape((frames, spots, wide)),
                    shape((frames, spots, wide)),
                    shape((1, 2 * wide)),
                    shape((2, wide)),
                ],
                [st, third, slow1, cs, gain_slow, bias_slow, mk],
                name="slow_last",
            )
        keep.update(n3=n3, nf3=nf3)
        saved.append(keep)

    def third_back(n, st, at, pre):
        k = saved[n]
        return run(
            part(slow_third_back, m, n, frames, lo3, lo2, at, 1 - n),
            [
                shape((frames, spots, wide), BF16),
                shape((frames, spots, width)),
                shape((1, 2 * width)),
                shape((2, wide)),
            ],
            [st, pre, k["third"], k["n3"], k["second"], k["n2"], w_slow_point[n], gain_slow, bias_slow, mk],
            flops=2 * frames * spots * width * wide,
            name="slow_third_back",
        )

    def fast_back3(n, st, at, pre):
        k = saved[n]
        return run(
            part(fast_third_back, m, n, frames, group, 2 * LANES, LANES, at),
            [
                shape((frames, spots, group * fwide), BF16),
                shape((frames, spots, LANES)),
                shape((1, 2 * LANES)),
                shape((2, LANES)),
            ],
            [st, pre, k["ft"], k["nf3"], k["fs"], k["nf2"], wfp[n], gf, bf, mk],
            flops=2 * frames * spots * LANES * group * fwide,
            name="fast_third_back",
        )

    def second_back(n, st, at, e2, e2_row):
        k = saved[n]
        return run(
            part(space_back, m, n, frames, cols, lo2, lo1, at, width, 0, False, m.slow),
            [
                shape((frames, spots, width), BF16),
                shape((frames, spots, width)),
                shape((1, 2 * width)),
                shape((2, width)),
            ],
            [st, e2, e2_row, k["second"], k["second_row"], k["n2"], k["first"], k["n1"], wsp[n],
             gain_slow, bias_slow, mk],
            [pltpu.VMEM((frames, spots + 2 * cols, 3 * width), BF16)],
            flops=2 * frames * spots * 9 * width * width,
            name="slow_space_back",
        )

    def fast_back2(n, st, at, ef2, ef2_row):
        k = saved[n]
        return run(
            part(space_back, m, n, frames, cols, LANES, 0, at, LANES, lat, True, m.fast),
            [
                shape((frames, spots, LANES), BF16),
                shape((frames, spots, LANES)),
                shape((1, 2 * LANES)),
                shape((2, LANES)),
            ],
            [st, ef2, ef2_row, k["fs"], k["fs_row"], k["nf2"], k["y"], k["nf1"], wfs[n], gf, bf, mk],
            [pltpu.VMEM((frames, spots + 2 * cols, 3 * LANES), BF16)],
            flops=2 * frames * spots * 9 * LANES * LANES,
            name="fast_space_back",
        )

    def first_back(n, st, e1, e1p, e1n, pre):
        k = saved[n]
        last = n == 0
        args = [st, e1, e1p, e1n, k["first"], k["firstp"], k["firstn"], k["n1"], w_slow_time[n], k["y"], k["nl"], pre]
        outs = [
            shape((frames + 2, spots, width), BF16),
            shape((frames, spots, lat)),
            shape((1, 2 * lat)),
            shape((frames, spots, wide)),
        ]
        if not last:
            args += [saved[0]["sw"], saved[0]["third"], saved[0]["n3"]]
            outs += [shape((1, 2 * wide))]
        outs += [shape((2, width))]
        return run(
            part(slow_first_back, m, n, frames, lo1, lo3, 0, 1, last),
            outs,
            args + [gain_slow, bias_slow, mk],
            flops=2 * frames * spots * 3 * (wide + lat) * width,
            name="slow_first_back",
        )

    def fast_back1(n, st1, at1, stl, atl, el, el_next, ef1, ef1p, ef1n, pre):
        k = saved[n]
        last = n == 0
        args = [st1, stl, el, el_next, ef1, ef1p, ef1n, k["y"], k["yp"], k["yn"], k["nl"], k["nf1"], w7[n], pre]
        outs = [
            shape((frames, spots, lat), BF16),
            shape((frames, spots, LANES), BF16),
            shape((fast_frames, spots, fwide)),
        ]
        if not last:
            args += [saved[0]["fw"], saved[0]["ft"], saved[0]["nf3"]]
            outs += [shape((1, 2 * LANES))]
        outs += [shape((2, lat)), shape((2, LANES))]
        return run(
            part(fast_first_back, m, n, frames, group, 0, 2 * LANES, at1, atl, last),
            outs,
            args + [gain_slow, gf, bf, mk],
            [pltpu.VMEM((fast_frames + 4, spots, fwide), F32)],
            flops=2 * frames * spots * 7 * fwide * (lat + LANES),
            name="fast_first_back",
        )

    def weights_point(n, d3):
        (out,) = run(
            point_weights,
            [shape((wide // 256, width, 256))],
            [saved[n]["a2"], d3],
            flops=2 * frames * spots * width * wide,
            name="point_weights",
        )
        return out.reshape(-1, 256)

    def weights_space(n, d2):
        (out,) = run(
            part(space_weights, cols),
            [shape((3, 3 * width, width))],
            [saved[n]["a1"], d2],
            [pltpu.VMEM((frames, spots + 2 * cols, 3 * width), BF16)],
            flops=2 * frames * spots * 9 * width * width,
            name="space_weights",
        )
        return out.reshape(-1, 256)

    def weights_time(n, dw):
        (out,) = run(
            part(time_weights, 1),
            [shape((3, wide + lat, width))],
            [saved[n]["sw"], saved[n]["jl"], dw],
            flops=2 * frames * spots * 3 * (wide + lat) * width,
            name="time_weights",
        )
        return out.reshape(-1, 256)

    def weights_fast(n, dl, df, d2, d3):
        k = saved[n]
        glat, gfast = run(
            part(fast_weights, group, cols, lat),
            [shape((5 * fwide, lat)), shape((2 * LANES, LANES))],
            [k["fw"], dl, df, k["fa1"], d2, k["fa2"], d3],
            [pltpu.VMEM((frames, spots + 2 * cols, 3 * LANES), BF16)],
            flops=2 * frames * spots * 7 * fwide * (lat + LANES),
            name="fast_weights",
        )
        gfast = jnp.concatenate([gfast[:LANES], gfast[LANES:]], axis=1)
        return jnp.concatenate([glat, gfast], axis=0)

    d3f1, ef2, s_ef2, gbf3_1 = fast_back3(1, st, 2 * wide, pre_f)
    st = gather_sums([s_pre, s_ef2])
    ef2_row = other_row(ef2)
    d3, e2, s_e2, gb3_1 = third_back(1, st, 0, pre)
    d2f1, ef1, s_ef1, gbf2_1 = fast_back2(1, st, 2 * wide, ef2, ef2_row)
    st = st_ef1 = gather_sums([s_e2, s_ef1])
    e2_row = other_row(e2)
    ef1p, ef1n = from_before(ef1[-1]), from_after(ef1[0])
    point1 = weights_point(1, d3)
    d2, e1, s_e1, gb2_1 = second_back(1, st, 0, e2, e2_row)
    st = gather_sums([s_e1])
    e1p, e1n = from_before(e1[-1]), from_after(e1[0])
    space1 = weights_space(1, d2)
    dw, el, s_el, pre, s_pre, gb1_1 = first_back(1, st, e1, e1p, e1n, pre)
    st = gather_sums([s_el, s_pre])
    el_next = from_after(el[0])
    time1 = weights_time(1, dw)
    d3, e2, s_e2, gb3_0 = third_back(0, st, 2 * lat, pre)
    dl1, df1, pre_f, s_pf, gbl_1, gbf1_1 = fast_back1(
        1, st_ef1, 2 * width, st, 0, el, el_next, ef1, ef1p, ef1n, pre_f
    )
    st = gather_sums([s_e2, s_pf])
    e2_row = other_row(e2)
    point0 = weights_point(0, d3)
    fast_1 = weights_fast(1, dl1, df1, d2f1, d3f1)
    d2, e1, s_e1, gb2_0 = second_back(0, st, 0, e2, e2_row)
    d3f0, ef2, s_ef2, gbf3_0 = fast_back3(0, st, 2 * width, pre_f)
    st = gather_sums([s_e1, s_ef2])
    e1p, e1n = from_before(e1[-1]), from_after(e1[0])
    ef2_row = other_row(ef2)
    space0 = weights_space(0, d2)
    dw, el, s_el, gx_slow, gb1_0 = first_back(0, st, e1, e1p, e1n, pre)
    d2f0, ef1, s_ef1, gbf2_0 = fast_back2(0, st, 2 * width, ef2, ef2_row)
    st = gather_sums([s_el, s_ef1])
    el_next = from_after(el[0])
    ef1p, ef1n = from_before(ef1[-1]), from_after(ef1[0])
    time0 = weights_time(0, dw)
    dl0, df0, gx_fast, gbl_0, gbf1_0 = fast_back1(0, st, 2 * lat, st, 0, el, el_next, ef1, ef1p, ef1n, pre_f)
    fast_0 = weights_fast(0, dl0, df0, d2f0, d3f0)

    def reduced(*pieces):
        sizes = [piece.shape[0] for piece in pieces]
        got = reduce_rows(jnp.concatenate(pieces, axis=0))
        outs, at = [], 0
        for size in sizes:
            outs.append(got[at : at + size])
            at += size
        return outs

    point1, space1, time1, fast_1 = reduced(point1, space1, time1, fast_1)
    point0, space0 = reduced(point0, space0)
    time0, fast_0 = reduced(time0, fast_0)

    def stack(zero, one):
        return jnp.stack([zero.astype(F32), one.astype(F32)])

    def from_fast(value):
        tail = value[5 * fwide :]
        tail = jnp.concatenate([tail[:, :LANES], tail[:, LANES:]], axis=0)
        time = tail[:LANES, : 3 * inner].reshape(fwide, 3, inner).transpose(1, 0, 2)
        space = tail[LANES : LANES + 3 * inner, : 3 * inner].reshape(3, inner, 3, inner).transpose(0, 2, 1, 3)
        return value[: 5 * fwide].reshape(5, fwide, lat), time, space, tail[LANES + 3 * inner :]

    lat0, ftime0, fspace0, fpoint0 = from_fast(fast_0)
    lat1, ftime1, fspace1, fpoint1 = from_fast(fast_1)

    def from_point(value):
        return jnp.concatenate(
            [value[k * width : (k + 1) * width] for k in range(wide // 256)], axis=1
        )

    def slow_rows(gbl, gb1, gb2, gb3, row):
        return jnp.concatenate([gbl[row], gb1[row], gb2[row], gb3[row]])

    def fast_rows(gb1, gb2, gb3, row):
        return jnp.concatenate([gb1[row, :inner], gb2[row, :inner], gb3[row]])

    slow_sums = [(gbl_0, gb1_0, gb2_0, gb3_0), (gbl_1, gb1_1, gb2_1, gb3_1)]
    fast_sums = [(gbf1_0, gbf2_0, gbf3_0), (gbf1_1, gbf2_1, gbf3_1)]
    return (
        out_slow.reshape(x_slow.shape),
        out_fast.reshape(x_fast.shape),
        gx_slow.reshape(x_slow.shape),
        gx_fast.reshape(x_fast.shape),
        stack(lat0, lat1),
        stack(time0, time1).reshape(w_slow_time.shape),
        stack(space0, space1).reshape(w_slow_space.shape),
        stack(from_point(point0), from_point(point1)),
        stack(ftime0, ftime1),
        stack(fspace0, fspace1),
        stack(fpoint0, fpoint1),
        jnp.stack([slow_rows(*sums, 1) for sums in slow_sums]),
        jnp.stack([slow_rows(*sums, 0) for sums in slow_sums]),
        jnp.stack([fast_rows(*sums, 1) for sums in fast_sums]),
        jnp.stack([fast_rows(*sums, 0) for sums in fast_sums]),
    )


def solution(mesh):
    spread = P("path", None, "rows", None, None, None)
    return jax.shard_map(
        on_device,
        mesh=mesh,
        in_specs=(spread, spread) + (P(),) * 12 + (spread, spread),
        out_specs=(spread,) * 4 + (P(),) * 11,
        check_vma=False,
    )
```

```python
import functools

import jax
import jax.numpy as jnp
import numpy as np
from jax import lax
from jax.experimental import pallas as pl
from jax.experimental.pallas import tpu as pltpu
from jax.sharding import PartitionSpec as P

TS = 8
TF = 32
F32 = jnp.float32
BF16 = jnp.bfloat16
EPSILON = 1e-05
LANES = 128
AXES = ("path", "rows")
VMEM_LIMIT = 56 * 2**20


def swap(value, axis, stride):
    pairs = [(source, source ^ stride) for source in range(lax.axis_size(axis))]
    return lax.ppermute(value, axis, pairs)


def gather_sums(spread):
    return lax.all_to_all(spread, AXES, 0, 0, tiled=True)


def swap_path(value):
    assert lax.axis_size("path") == 2
    return lax.ppermute(value, "path", [(0, 1), (1, 0)])


def exchange_steps():
    steps = [("rows", 1), ("path", 1)]
    stride = 2
    while stride < lax.axis_size("rows"):
        steps.append(("rows", stride))
        stride *= 2
    return steps


def reduce_rows(value):
    steps = exchange_steps()
    for axis, stride in steps:
        size = value.shape[0] // 2
        upper = (lax.axis_index(axis) // stride) % 2
        keep = lax.dynamic_slice_in_dim(value, upper * size, size, 0)
        give = lax.dynamic_slice_in_dim(value, (1 - upper) * size, size, 0)
        value = keep + swap(give.astype(BF16), axis, stride).astype(F32)
    value = value.astype(BF16)
    for axis, stride in reversed(steps):
        upper = (lax.axis_index(axis) // stride) % 2
        got = swap(value, axis, stride)
        value = jnp.concatenate(
            [jnp.where(upper == 0, value, got), jnp.where(upper == 0, got, value)], axis=0
        )
    return value


class Stage:
    def __init__(self, name):
        self.name = name
        self.arrays, self.views, self.scalars = [], [], []
        self.outs, self.temps, self.steps = [], [], []
        self.flops = 0

    def take(self, array, *view):
        for at, known in enumerate(self.arrays):
            if known is array:
                break
        else:
            at = len(self.arrays)
            self.arrays.append(array)
        for k, (other, seen) in enumerate(self.views):
            if other == at and seen == view:
                return ("in", k)
        self.views.append((at, view))
        return ("in", len(self.views) - 1)

    def scalar(self, array):
        self.scalars.append(array)
        return ("scalar", len(self.scalars) - 1)

    def give(self, dims, dtype=F32):
        self.outs.append(jax.ShapeDtypeStruct(tuple(dims), dtype))
        return ("out", len(self.outs) - 1)

    def temp(self, dims, dtype=F32):
        self.temps.append(pltpu.VMEM(tuple(dims), dtype))
        return ("temp", len(self.temps) - 1)

    def step(self, fn, *handles, flops=0):
        self.flops += flops
        self.steps.append((fn, handles))

    def view_shape(self, view):
        at, index = view
        return np.broadcast_to(np.zeros((), np.int8), self.arrays[at].shape)[index].shape

    def run(self):
        arrays, views, outs, steps = self.arrays, self.views, self.outs, self.steps
        order = []
        for _, handles in steps:
            for handle in handles:
                if handle[0] == "in" and handle[1] not in order:
                    order.append(handle[1])

        def body(*refs):
            refs = list(refs)

            def cut(count):
                taken = refs[:count]
                del refs[:count]
                return taken

            scalars, hbm_in, hbm_out = cut(len(self.scalars)), cut(len(arrays)), cut(len(outs))
            held, made, temps = cut(len(views)), cut(len(outs)), cut(len(self.temps))
            (sems,) = refs
            copies = {}
            for k in order:
                at, index = views[k]
                src = hbm_in[at].at[index] if index else hbm_in[at]
                copies[k] = pltpu.make_async_copy(src, held[k], sems.at[k])
                copies[k].start()
            waited, sent = set(), {}
            for fn, handles in steps:
                given = []
                for kind, k in handles:
                    if kind == "in" and k not in waited:
                        copies[k].wait()
                        waited.add(k)
                    given.append({"in": held, "out": made, "temp": temps, "scalar": scalars}[kind][k])
                fn(*given)
                for kind, k in handles:
                    if kind == "out" and k not in sent:
                        sent[k] = pltpu.make_async_copy(made[k], hbm_out[k], sems.at[len(views) + k])
                        sent[k].start()
            for copy in sent.values():
                copy.wait()

        moved = sum(a.size * a.dtype.itemsize for a in outs)
        for view in views:
            moved += int(np.prod(self.view_shape(view))) * arrays[view[0]].dtype.itemsize
        scratch = [pltpu.VMEM(self.view_shape(view), arrays[view[0]].dtype) for view in views]
        scratch += [pltpu.VMEM(o.shape, o.dtype) for o in outs]
        scratch += self.temps + [pltpu.SemaphoreType.DMA((len(views) + len(outs),))]
        return pl.pallas_call(
            body,
            out_shape=tuple(outs),
            in_specs=[pl.BlockSpec(memory_space=pltpu.SMEM) for _ in self.scalars]
            + [pl.BlockSpec(memory_space=pl.ANY) for _ in arrays],
            out_specs=tuple(pl.BlockSpec(memory_space=pl.ANY) for _ in outs),
            scratch_shapes=scratch,
            compiler_params=pltpu.CompilerParams(vmem_limit_bytes=VMEM_LIMIT),
            cost_estimate=pl.CostEstimate(flops=self.flops, bytes_accessed=moved, transcendentals=0),
            name=self.name,
        )(*self.scalars, *arrays)


class Masks:
    def __init__(self, spots, cols):
        self.main = (0, spots)
        self.ext = (spots, 2 * spots + 2 * cols)
        self.prev = (2 * spots + 2 * cols, 3 * spots + 2 * cols)
        self.next = (3 * spots + 2 * cols, 4 * spots + 2 * cols)
        self.slow = (4 * spots + 2 * cols, 4 * spots + 2 * cols + 8)
        self.fast = (4 * spots + 2 * cols + 8, 4 * spots + 2 * cols + 16)
        self.half = (4 * spots + 2 * cols + 16, 4 * spots + 2 * cols + 24)
        self.path = (4 * spots + 2 * cols + 24, 4 * spots + 2 * cols + 32)
        self.rows = 4 * spots + 2 * cols + 32


def make_masks(m, rows, cols, last, place, clips, mk):
    half = place[0] % 2
    path = place[1]
    side = clips[0, place[0] // 2]
    area = 0
    for k in range(clips.shape[1]):
        area = area + clips[0, k] * clips[0, k]
    shift = cols.bit_length() - 1

    def inside(first, count):
        at = lax.broadcasted_iota(jnp.int32, (count * cols, LANES), 0)
        line = half * rows + first + (at >> shift)
        spot = at & (cols - 1)
        good = (line >= 0) & (line < 2 * rows) & (line < side) & (spot < side)
        return jnp.where(good, 1.0, 0.0)

    main = inside(0, rows)
    mk[m.main[0] : m.main[1], :] = main
    mk[m.ext[0] : m.ext[1], :] = inside(-1, rows + 2)
    mk[m.prev[0] : m.prev[1], :] = main * jnp.where(path > 0, 1.0, 0.0)
    mk[m.next[0] : m.next[1], :] = main * jnp.where(path < last, 1.0, 0.0)

    def fill(span, value):
        mk[span[0] : span[1], :] = jnp.full((8, LANES), value, F32)

    fill(m.slow, TS * area.astype(F32))
    fill(m.fast, TF * area.astype(F32))
    fill(m.half, half.astype(F32))
    fill(m.path, path.astype(F32))


def own_row(m, spots, cols, col0, width, z, mk, row):
    for t in range(z.shape[0]):
        lower = mk[m.half[0] : m.half[0] + 1, :] > 0.5
        for lane in range(0, width, LANES):
            at = col0 + lane
            row[t, :, lane : lane + LANES] = jnp.where(
                lower, z[t, 0:cols, at : at + LANES], z[t, spots - cols : spots, at : at + LANES]
            )


def own_edge(m, lead, tail, z, mk, edge):
    frames = z.shape[0]
    second = mk[m.path[0] : m.path[0] + 1, :] > 0.5
    for lane in range(0, edge.shape[1], LANES):
        edge[:, lane : lane + LANES] = jnp.where(
            second,
            z[0, :, lead + lane : lead + lane + LANES],
            z[frames - 1, :, tail + lane : tail + lane + LANES],
        )


def spread_sums(*refs):
    parts, out = refs[:-1], refs[-1]
    row = jnp.concatenate([part[...] for part in parts], axis=1)
    out[...] = jnp.broadcast_to(row[None], out.shape)


def make_w7(lat, group, wl, wf, w7):
    inner = wf.shape[1]
    w7[...] = jnp.zeros(w7.shape, BF16)
    for j in range(wl.shape[0]):
        w7[j * LANES : (j + 1) * LANES, 0:lat] = wl[j]
    at = lax.broadcasted_iota(jnp.int32, (inner, LANES), 0)
    lane = lax.broadcasted_iota(jnp.int32, (inner, LANES), 1)
    places = [jnp.where(lane == at + inner * k, 1.0, 0.0).astype(BF16) for k in range(group)]
    for f in range(1, group + 3):
        used = [k for k in range(group) if 0 <= f - 1 - k < 3]
        got = None
        for k in used:
            more = dot_tn(wf[f - 1 - k], places[k])
            got = more if got is None else got + more
        w7[f * LANES : (f + 1) * LANES, lat : lat + LANES] = got.astype(BF16)


def make_blocks(group, ws, wp, wfs, wfp):
    inner = wp.shape[0]
    at = lax.broadcasted_iota(jnp.int32, (inner, LANES), 0)
    lane = lax.broadcasted_iota(jnp.int32, (inner, LANES), 1)
    tile = jnp.where((lane & (inner - 1)) == at, 1.0, 0.0).astype(BF16)
    shift = inner.bit_length() - 1
    for tap in range(ws.shape[0]):
        got = dot(ws[tap], tile)
        for k in range(group):
            kept = jnp.where((lane >> shift) == k, got, 0.0).astype(BF16)
            row = (tap % 3) * LANES + k * inner
            wfs[tap // 3, row : row + inner, :] = kept
    wfp[...] = jnp.zeros(wfp.shape, BF16)
    for k in range(group):
        wfp[k * inner : (k + 1) * inner, k * LANES : (k + 1) * LANES] = wp[...]


def widen(rows, width):
    return jnp.concatenate([rows] * (width // LANES), axis=1)


def sublane_sums(value):
    return jnp.sum(value.reshape(value.shape[0] // 8, 8, value.shape[1]), axis=0)


def row_sum(value):
    return jnp.sum(value, axis=0, keepdims=True)


def fold_packed(row):
    full = jnp.broadcast_to(row, (8, LANES))
    full = full + pltpu.roll(full, 64, 1)
    full = full + pltpu.roll(full, 32, 1)
    return full[0:1]


def totals(st, lo, width, packed=False):
    first = jnp.sum(st[:, :, lo : lo + width], axis=0)
    second = jnp.sum(st[:, :, lo + width : lo + 2 * width], axis=0)
    if packed:
        return fold_packed(first), fold_packed(second)
    return first, second


def norm_rows(st, lo, width, count, packed=False):
    first, second = totals(st, lo, width, packed)
    mean = first / count
    return mean, lax.rsqrt(second / count - mean * mean + EPSILON)


def sigmoid(value):
    return 0.5 * jnp.tanh(0.5 * value) + 0.5


def silu(value):
    return value * sigmoid(value)


def silu_slope(value):
    sigma = sigmoid(value)
    return sigma * (1.0 + value * (1.0 - sigma))


def dot(a, b):
    return jnp.dot(a, b, preferred_element_type=F32)


def dot_nt(a, b):
    return lax.dot_general(a, b, (((1,), (1,)), ((), ())), preferred_element_type=F32)


def dot_tn(a, b):
    return lax.dot_general(a, b, (((0,), (0,)), ((), ())), preferred_element_type=F32)


def flat(value):
    return value.reshape(value.shape[0] * value.shape[1], value.shape[2])


def store_shifts(dst, t, value, cols):
    rows, width = value.shape
    spot = lax.broadcasted_iota(jnp.int32, (rows, width), 0) & (cols - 1)
    left = jnp.where(spot == 0, 0.0, pltpu.roll(value, 1, 0))
    right = jnp.where(spot == cols - 1, 0.0, pltpu.roll(value, rows - 1, 0))
    dst[t, :, 0:width] = left.astype(BF16)
    dst[t, :, width : 2 * width] = value.astype(BF16)
    dst[t, :, 2 * width : 3 * width] = right.astype(BF16)


def taps_of(frames_ref, frames, group):
    return jnp.concatenate(
        [
            jnp.concatenate([frames_ref[group * t + f] for f in range(7)], axis=1)
            for t in range(frames)
        ],
        axis=0,
    )


def entry_sums(y, lat, frames, spots):
    width = y.shape[1]
    one = jnp.zeros((8, width), F32)
    two = jnp.zeros((8, width), F32)
    for t in range(frames):
        part = y[t * spots : (t + 1) * spots]
        one = one + sublane_sums(part)
        two = two + sublane_sums(part * part)
    one = row_sum(one)
    two = row_sum(two)
    return jnp.concatenate([one[:, :lat], two[:, :lat], one[:, lat:], two[:, lat:]], axis=1)


def fast_entry(m, frames, group, x, before, after, mk, w7, fw, y, s):
    spots = x.shape[1]
    count = x.shape[0]

    def put(at, value, span):
        fw[at] = (value.astype(F32) * mk[span[0] : span[1], :]).astype(BF16)

    for k in range(2):
        put(k, before[k], m.prev)
        put(2 + count + k, after[k], m.next)
    for k in range(count):
        put(2 + k, x[k], m.main)
    out = dot(taps_of(fw, frames, group), w7[...])
    for t in range(frames):
        y[t] = out[t * spots : (t + 1) * spots]
    s[...] = entry_sums(out, w7.shape[1] - LANES, frames, spots)


def slow_partial(m, frames, x, before, after, mk, wt, xm, fpart):
    spots, wide = x.shape[1], x.shape[2]
    sources = [(before, m.prev)] + [(x.at[t], m.main) for t in range(frames)] + [(after, m.next)]
    for k, (src, span) in enumerate(sources):
        for lo in range(0, wide, 256):
            mask = widen(mk[span[0] : span[1], :], 256)
            xm[k, :, lo : lo + 256] = (src[:, lo : lo + 256].astype(F32) * mask).astype(BF16)
    out = dot(flat(xm[0:frames]), wt[0, :wide, :])
    for j in range(1, 3):
        out = out + dot(flat(xm[j : j + frames]), wt[j, :wide, :])
    for t in range(frames):
        fpart[t] = out[t * spots : (t + 1) * spots]


def lat_join(m, n, frames, lat, st, y, before, after, fpart, wt, gs, bs, mk, jl, first, s, nl, jw):
    spots = y.shape[1]
    wide = wt.shape[1] - lat
    count = widen(mk[m.slow[0] : m.slow[0] + 1, :], lat)
    mean, rstd = norm_rows(st, 0, lat, count)
    nl[0:1, :] = mean
    nl[1:2, :] = rstd
    scale = rstd * gs[n : n + 1, 0:lat]
    bias = bs[n : n + 1, 0:lat]
    sources = (
        [(before[:, 0:lat], m.prev)]
        + [(y[t, :, 0:lat], m.main) for t in range(frames)]
        + [(after[:, 0:lat], m.next)]
    )
    for k, (value, span) in enumerate(sources):
        mask = widen(mk[span[0] : span[1], :], lat)
        act = (silu((value - mean) * scale + bias) * mask).astype(BF16)
        jw[k] = act
        if 1 <= k <= frames:
            jl[k - 1] = act
    out = flat(fpart[...])
    for j in range(3):
        out = out + dot(flat(jw[j : j + frames]), wt[j, wide:, :])
    one = jnp.zeros((8, out.shape[1]), F32)
    two = jnp.zeros((8, out.shape[1]), F32)
    for t in range(frames):
        part = out[t * spots : (t + 1) * spots]
        first[t] = part
        one = one + sublane_sums(part)
        two = two + sublane_sums(part * part)
    s[...] = jnp.concatenate([row_sum(one), row_sum(two)], axis=1)


def space_forward(
    m, n, frames, cols, lo, at, width, col0, packed, span, st, z, row, w, g, b, mk, aw, out, s, nz, vw
):
    spots = z.shape[1]
    count = widen(mk[span[0] : span[0] + 1, :], width)
    mean, rstd = norm_rows(st, at, width, count, packed)
    nz[0:1, :] = mean
    nz[1:2, :] = rstd
    scale = rstd * g[n : n + 1, lo : lo + width]
    bias = b[n : n + 1, lo : lo + width]
    mask = widen(mk[m.ext[0] : m.ext[1], :], width)
    for t in range(frames):
        value = jnp.concatenate([row[t], z[t, :, col0 : col0 + width], row[t]], axis=0)
        act = silu((value - mean) * scale + bias) * mask
        aw[t] = act.astype(BF16)
        store_shifts(vw, t, act, cols)
    total = dot(flat(vw[:, 0:spots, :]), w[0])
    for i in range(1, 3):
        total = total + dot(flat(vw[:, i * cols : i * cols + spots, :]), w[i])
    mask = widen(mk[m.main[0] : m.main[1], :], width)
    one = jnp.zeros((8, width), F32)
    two = jnp.zeros((8, width), F32)
    for t in range(frames):
        part = total[t * spots : (t + 1) * spots]
        out[t] = part
        part = part * mask
        one = one + sublane_sums(part)
        two = two + sublane_sums(part * part)
    s[...] = jnp.concatenate([row_sum(one), row_sum(two)], axis=1)


def slow_third(m, n, frames, lo, halo, st, z, *rest):
    if halo:
        before, after, wp, g, b, mk, a2, third, s, nz, aw = rest
    else:
        wp, g, b, mk, a2, third, s, nz, aw = rest
    spots, width = z.shape[1], z.shape[2]
    wide = wp.shape[1]
    count = widen(mk[m.slow[0] : m.slow[0] + 1, :], width)
    mean, rstd = norm_rows(st, 0, width, count)
    nz[0:1, :] = mean
    nz[1:2, :] = rstd
    scale = rstd * g[n : n + 1, lo : lo + width]
    bias = b[n : n + 1, lo : lo + width]
    sources = [(z[t], m.main, t + halo) for t in range(frames)]
    if halo:
        sources += [(before[...], m.prev, 0), (after[...], m.next, frames + 1)]
    for value, span, at in sources:
        mask = widen(mk[span[0] : span[1], :], width)
        act = (silu((value - mean) * scale + bias) * mask).astype(BF16)
        aw[at] = act
        if halo <= at < frames + halo:
            a2[at - halo] = act
    acts = flat(aw[...])
    ones, twos = [], []
    for at in range(0, wide, 256):
        out = dot(acts, wp[:, at : at + 256])
        one = jnp.zeros((8, 256), F32)
        two = jnp.zeros((8, 256), F32)
        for t in range(frames + 2 * halo):
            part = out[t * spots : (t + 1) * spots]
            third[t, :, at : at + 256] = part
            if halo <= t < frames + halo:
                one = one + sublane_sums(part)
                two = two + sublane_sums(part * part)
        ones.append(row_sum(one))
        twos.append(row_sum(two))
    s[...] = jnp.concatenate(ones + twos, axis=1)


def fast_third(m, n, frames, lo, at, st, z, wp, g, b, mk, a2, ft, s, nz):
    spots = z.shape[1]
    count = mk[m.fast[0] : m.fast[0] + 1, :]
    mean, rstd = norm_rows(st, at, LANES, count, True)
    nz[0:1, :] = mean
    nz[1:2, :] = rstd
    scale = rstd * g[n : n + 1, lo : lo + LANES]
    bias = b[n : n + 1, lo : lo + LANES]
    mask = mk[m.main[0] : m.main[1], :]
    for t in range(frames):
        a2[t] = (silu((z[t] - mean) * scale + bias) * mask).astype(BF16)
    acts = flat(a2[...])
    one = jnp.zeros((8, LANES), F32)
    two = jnp.zeros((8, LANES), F32)
    out = dot(acts, wp[...])
    for t in range(frames):
        for lane in range(0, wp.shape[1], LANES):
            part = out[t * spots : (t + 1) * spots, lane : lane + LANES]
            ft[t, :, lane : lane + LANES] = part
            one = one + sublane_sums(part)
            two = two + sublane_sums(part * part)
    s[...] = jnp.concatenate([row_sum(one), row_sum(two)], axis=1)


def fast_next(m, n, frames, group, lo, at, st, ft, before, after, fw0, w7, g, b, mk, f1, fw1, y, s, nz):
    spots = ft.shape[1]
    count = mk[m.fast[0] : m.fast[0] + 1, :]
    mean, rstd = norm_rows(st, at, LANES, count)
    nz[0:1, :] = mean
    nz[1:2, :] = rstd
    scale = rstd * g[n : n + 1, lo : lo + LANES]
    bias = b[n : n + 1, lo : lo + LANES]
    total = frames * group

    def out_of(k, value, span):
        z = fw0[k].astype(F32) + ((value - mean) * scale + bias)
        return silu(z) * mk[span[0] : span[1], :]

    for k in range(2):
        lane = k * LANES
        fw1[k] = out_of(k, before[:, lane : lane + LANES], m.prev).astype(BF16)
        fw1[2 + total + k] = out_of(2 + total + k, after[:, lane : lane + LANES], m.next).astype(BF16)
    for t in range(frames):
        for f in range(group):
            k = t * group + f
            value = out_of(2 + k, ft[t, :, f * LANES : (f + 1) * LANES], m.main)
            f1[k] = value
            fw1[2 + k] = value.astype(BF16)
    out = dot(taps_of(fw1, frames, group), w7[...])
    for t in range(frames):
        y[t] = out[t * spots : (t + 1) * spots]
    s[...] = entry_sums(out, w7.shape[1] - LANES, frames, spots)


def fast_last(m, n, frames, group, lo, at, st, ft, f1, cot, g, b, mk, out, pre, s, nz):
    count = mk[m.fast[0] : m.fast[0] + 1, :]
    mean, rstd = norm_rows(st, at, LANES, count)
    nz[0:1, :] = mean
    nz[1:2, :] = rstd
    gain = g[n : n + 1, lo : lo + LANES]
    bias = b[n : n + 1, lo : lo + LANES]
    mask = mk[m.main[0] : m.main[1], :]
    one = jnp.zeros((8, LANES), F32)
    two = jnp.zeros((8, LANES), F32)
    for t in range(frames):
        for f in range(group):
            k = t * group + f
            hat = (ft[t, :, f * LANES : (f + 1) * LANES] - mean) * rstd
            z = f1[k] + hat * gain + bias
            sigma = sigmoid(z)
            out[k] = z * sigma * mask
            grad = cot[k].astype(F32) * mask * (sigma * (1.0 + z * (1.0 - sigma)))
            pre[k] = grad
            one = one + sublane_sums(grad)
            two = two + sublane_sums(grad * hat)
    s[...] = jnp.concatenate([row_sum(one), row_sum(two)], axis=1)


def chunked(total, step, body, init):
    def turn(i, carry):
        return body(pl.multiple_of(i * step, step), carry)

    return lax.fori_loop(0, total // step, turn, init)


def slow_next(m, n, frames, lo, at0, st, third, xm, wt, g, b, mk, slow1, sw, fpart, nz):
    spots, wide = third.shape[1], third.shape[2]
    count = widen(mk[m.slow[0] : m.slow[0] + 1, :], wide)
    mean, rstd = norm_rows(st, at0, wide, count)
    nz[0:1, :] = mean
    nz[1:2, :] = rstd
    scale = rstd * g[n : n + 1, lo : lo + wide]
    bias = b[n : n + 1, lo : lo + wide]
    spans = [m.prev] + [m.main] * frames + [m.next]
    for k, span in enumerate(spans):

        def turn(at, carry, k=k, span=span):
            mask = widen(mk[pl.ds(span[0] + at, 16), :], 512)
            for c in range(0, wide, 512):
                z = third[k, pl.ds(at, 16), c : c + 512]
                z = (z - mean[:, c : c + 512]) * scale[:, c : c + 512] + bias[:, c : c + 512]
                z = xm[k, pl.ds(at, 16), c : c + 512].astype(F32) + z
                value = silu(z) * mask
                sw[k, pl.ds(at, 16), c : c + 512] = value.astype(BF16)
                if 1 <= k <= frames:
                    slow1[k - 1, pl.ds(at, 16), c : c + 512] = value
            return carry

        chunked(spots, 16, turn, 0)
    out = dot(flat(sw[0:frames]), wt[0, :wide, :])
    for j in range(1, 3):
        out = out + dot(flat(sw[j : j + frames]), wt[j, :wide, :])
    for t in range(frames):
        fpart[t] = out[t * spots : (t + 1) * spots]


def slow_last(m, n, frames, lo, st, third, slow1, cot, g, b, mk, out, pre, s, nz):
    spots, wide = third.shape[1], third.shape[2]
    count = widen(mk[m.slow[0] : m.slow[0] + 1, :], wide)
    mean, rstd = norm_rows(st, 0, wide, count)
    nz[0:1, :] = mean
    nz[1:2, :] = rstd
    gain = g[n : n + 1, lo : lo + wide]
    bias = b[n : n + 1, lo : lo + wide]
    carry = (jnp.zeros((8, wide), F32), jnp.zeros((8, wide), F32))
    for t in range(frames):

        def turn(at, sums, t=t):
            one, two = sums
            ones, twos = [], []
            mask = widen(mk[pl.ds(m.main[0] + at, 16), :], 512)
            for c in range(0, wide, 512):
                hat = (third[t, pl.ds(at, 16), c : c + 512] - mean[:, c : c + 512]) * rstd[:, c : c + 512]
                z = slow1[t, pl.ds(at, 16), c : c + 512] + hat * gain[:, c : c + 512] + bias[:, c : c + 512]
                sigma = sigmoid(z)
                out[t, pl.ds(at, 16), c : c + 512] = z * sigma * mask
                grad = cot[t, pl.ds(at, 16), c : c + 512].astype(F32) * mask
                grad = grad * (sigma * (1.0 + z * (1.0 - sigma)))
                pre[t, pl.ds(at, 16), c : c + 512] = grad
                ones.append(sublane_sums(grad))
                twos.append(sublane_sums(grad * hat))
            return one + jnp.concatenate(ones, axis=1), two + jnp.concatenate(twos, axis=1)

        carry = chunked(spots, 16, turn, carry)
    s[...] = jnp.concatenate([row_sum(carry[0]), row_sum(carry[1])], axis=1)


def slow_third_back(m, n, frames, lo3, lo2, at, halo, st, pre, third, n3, z, n2, wp, g, b, mk, d3, e2, s, gb):
    spots, wide = pre.shape[1], pre.shape[2]
    width = z.shape[2]
    count = widen(mk[m.slow[0] : m.slow[0] + 1, :], wide)
    one, two = totals(st, at, wide)
    gb[0:1, :] = one
    gb[1:2, :] = two
    mean, rstd = n3[0:1, :], n3[1:2, :]
    scale = g[n : n + 1, lo3 : lo3 + wide] * rstd
    one = one / count
    two = two / count * rstd
    for t in range(frames):

        def turn(i, carry, t=t):
            mask = widen(mk[pl.ds(m.main[0] + i, 16), :], 512)
            for c in range(0, wide, 512):
                hat = (third[t + halo, pl.ds(i, 16), c : c + 512] - mean[:, c : c + 512]) * two[:, c : c + 512]
                grad = pre[t, pl.ds(i, 16), c : c + 512] - mask * (one[:, c : c + 512] + hat)
                d3[t, pl.ds(i, 16), c : c + 512] = (scale[:, c : c + 512] * grad).astype(BF16)
            return carry

        chunked(spots, 16, turn, 0)
    out = dot_nt(flat(d3[...]), wp[...])
    mean, rstd = n2[0:1, :], n2[1:2, :]
    gain = g[n : n + 1, lo2 : lo2 + width]
    bias = b[n : n + 1, lo2 : lo2 + width]
    back_act(m, frames, spots, out, z, 0, mean, rstd, gain, bias, mk, e2, s)


def back_act(m, frames, spots, out, z, col0, mean, rstd, gain, bias, mk, e, s):
    width = out.shape[1]
    mask = widen(mk[m.main[0] : m.main[1], :], width)
    one = jnp.zeros((8, width), F32)
    two = jnp.zeros((8, width), F32)
    for t in range(frames):
        hat = (z[t, :, col0 : col0 + width] - mean) * rstd
        grad = out[t * spots : (t + 1) * spots] * mask * silu_slope(hat * gain + bias)
        e[t] = grad
        one = one + sublane_sums(grad)
        two = two + sublane_sums(grad * hat)
    s[...] = jnp.concatenate([row_sum(one), row_sum(two)], axis=1)


def fast_third_back(m, n, frames, group, lo3, lo2, at, st, pre, ft, n3, z, n2, wp, g, b, mk, d3, e2, s, gb):
    spots = z.shape[1]
    count = mk[m.fast[0] : m.fast[0] + 1, :]
    one, two = totals(st, at, LANES)
    gb[0:1, :] = one
    gb[1:2, :] = two
    mean, rstd = n3[0:1, :], n3[1:2, :]
    scale = g[n : n + 1, lo3 : lo3 + LANES] * rstd
    one = one / count
    two = two / count * rstd
    mask = mk[m.main[0] : m.main[1], :]
    for t in range(frames):
        for f in range(group):
            hat = (ft[t, :, f * LANES : (f + 1) * LANES] - mean) * two
            grad = pre[t * group + f] - mask * (one + hat)
            d3[t, :, f * LANES : (f + 1) * LANES] = (scale * grad).astype(BF16)
    out = dot_nt(flat(d3[...]), wp[...])
    mean, rstd = n2[0:1, :], n2[1:2, :]
    gain = g[n : n + 1, lo2 : lo2 + LANES]
    bias = b[n : n + 1, lo2 : lo2 + LANES]
    back_act(m, frames, spots, out, z, 0, mean, rstd, gain, bias, mk, e2, s)


def space_back(
    m, n, frames, cols, lo2, lo1, at, width, col0, packed, span,
    st, e, erow, z, zrow, nz, z1, n1, w, g, b, mk, d2, e1, s, gb, vw,
):
    spots = z.shape[1]
    count = widen(mk[span[0] : span[0] + 1, :], width)
    one, two = totals(st, at, width, packed)
    gb[0:1, :] = one
    gb[1:2, :] = two
    mean, rstd = nz[0:1, :], nz[1:2, :]
    scale = g[n : n + 1, lo2 : lo2 + width] * rstd
    one = one / count
    two = two / count * rstd
    mask = widen(mk[m.ext[0] : m.ext[1], :], width)
    for t in range(frames):
        grad = jnp.concatenate([erow[t], e[t], erow[t]], axis=0)
        value = jnp.concatenate([zrow[t], z[t], zrow[t]], axis=0)
        grad = scale * mask * (grad - (one + (value - mean) * two))
        d2[t] = grad[cols : cols + spots].astype(BF16)
        store_shifts(vw, t, grad.astype(BF16).astype(F32), cols)
    total = None
    for i in range(3):
        rows = (2 - i) * cols
        for j in range(3):
            lane = (2 - j) * width
            part = dot_nt(flat(vw[:, rows : rows + spots, lane : lane + width]), w[i, j * width : (j + 1) * width, :])
            total = part if total is None else total + part
    mean, rstd = n1[0:1, :], n1[1:2, :]
    gain = g[n : n + 1, lo1 : lo1 + width]
    bias = b[n : n + 1, lo1 : lo1 + width]
    back_act(m, frames, spots, total, z1, col0, mean, rstd, gain, bias, mk, e1, s)


def slow_first_back(m, n, frames, lo1, lo3, at, halo, last, st, *rest):
    if last:
        e, ep, en, z, zp, zn, n1, wt, y, nl, pre, g, b, mk, dw, el, s, gx, gb = rest
    else:
        e, ep, en, z, zp, zn, n1, wt, y, nl, pre, xm, third, n3, g, b, mk, dw, el, s, pre0, s3, gb = rest
    spots, width = z.shape[1], z.shape[2]
    lat = nl.shape[1]
    wide = wt.shape[1] - lat
    count = widen(mk[m.slow[0] : m.slow[0] + 1, :], width)
    one, two = totals(st, at, width)
    gb[0:1, :] = one
    gb[1:2, :] = two
    mean, rstd = n1[0:1, :], n1[1:2, :]
    scale = g[n : n + 1, lo1 : lo1 + width] * rstd
    one = one / count
    two = two / count * rstd
    sources = (
        [(ep, zp, m.prev)] + [(e.at[t], z.at[t], m.main) for t in range(frames)] + [(en, zn, m.next)]
    )
    for k, (grad, value, span) in enumerate(sources):
        mask = widen(mk[span[0] : span[1], :], width)
        dw[k] = (scale * mask * (grad[...] - (one + (value[...] - mean) * two))).astype(BF16)
    taps = [flat(dw[2 - j : 2 - j + frames]) for j in range(3)]

    def back(lo, size):
        out = dot_nt(taps[0], wt[0, lo : lo + size, :])
        for j in range(1, 3):
            out = out + dot_nt(taps[j], wt[j, lo : lo + size, :])
        return out

    out = back(wide, lat)
    back_act(
        m, frames, spots, out, y, 0, nl[0:1, :], nl[1:2, :], g[n : n + 1, 0:lat], b[n : n + 1, 0:lat], mk, el, s
    )
    mask = widen(mk[m.main[0] : m.main[1], :], 256)
    ones, twos = [], []
    for c in range(0, wide, 256):
        out = back(c, 256)
        if not last:
            mean, rstd = n3[0:1, c : c + 256], n3[1:2, c : c + 256]
            gain = g[n - 1 : n, lo3 + c : lo3 + c + 256]
            bias = b[n - 1 : n, lo3 + c : lo3 + c + 256]
            one = jnp.zeros((8, 256), F32)
            two = jnp.zeros((8, 256), F32)
        for t in range(frames):
            grad = (out[t * spots : (t + 1) * spots] + pre[t, :, c : c + 256]) * mask
            if last:
                gx[t, :, c : c + 256] = grad
            else:
                hat = (third[t + halo, :, c : c + 256] - mean) * rstd
                z0 = xm[t + 1, :, c : c + 256].astype(F32) + hat * gain + bias
                grad = grad * silu_slope(z0)
                pre0[t, :, c : c + 256] = grad
                one = one + sublane_sums(grad)
                two = two + sublane_sums(grad * hat)
        if not last:
            ones.append(row_sum(one))
            twos.append(row_sum(two))
    if not last:
        s3[...] = jnp.concatenate(ones + twos, axis=1)


def fast_first_back(m, n, frames, group, lo1, lo3, at1, atl, last, st1, stl, *rest):
    if last:
        el, eln, ef, efp, efn, y, yp, yn, nl, n1, w7, pre, gs, g, b, mk, dl, dfw, gx, gbl, gb1, buf = rest
    else:
        (el, eln, ef, efp, efn, y, yp, yn, nl, n1, w7, pre, fw0, ft, n3, gs, g, b, mk,
         dl, dfw, pre0, s, gbl, gb1, buf) = rest
    spots = y.shape[1]
    lat = nl.shape[1]
    count = widen(mk[m.slow[0] : m.slow[0] + 1, :], lat)
    one, two = totals(stl, atl, lat)
    gbl[0:1, :] = one
    gbl[1:2, :] = two
    mean, rstd = nl[0:1, :], nl[1:2, :]
    scale = gs[n : n + 1, 0:lat] * rstd
    one = one / count
    two = two / count * rstd

    def lat_grad(grad, value, span):
        mask = widen(mk[span[0] : span[1], :], lat)
        return (scale * mask * (grad - (one + (value - mean) * two))).astype(BF16)

    for t in range(frames):
        dl[t] = lat_grad(el[t], y[t, :, 0:lat], m.main)
    dl_next = lat_grad(eln[...], yn[:, 0:lat], m.next)
    fcount = mk[m.fast[0] : m.fast[0] + 1, :]
    fone, ftwo = totals(st1, at1, LANES, True)
    gb1[0:1, :] = fone
    gb1[1:2, :] = ftwo
    fmean, frstd = n1[0:1, :], n1[1:2, :]
    fscale = g[n : n + 1, lo1 : lo1 + LANES] * frstd
    fone = fone / fcount
    ftwo = ftwo / fcount * frstd

    def first_grad(grad, value, span):
        mask = mk[span[0] : span[1], :]
        return (fscale * mask * (grad - (fone + (value - fmean) * ftwo))).astype(BF16)

    for t in range(frames):
        dfw[t] = first_grad(ef[t], y[t, :, lat:], m.main)
    df_prev = first_grad(efp[...], yp[:, lat:], m.prev)
    df_next = first_grad(efn[...], yn[:, lat:], m.next)
    both = jnp.concatenate([flat(dl[...]), flat(dfw[...])], axis=1)
    buf[...] = jnp.zeros(buf.shape, F32)
    out = dot_nt(both, w7[...])
    for t in range(frames):
        for f in range(7):
            k = group * t + f
            buf[k] = buf[k] + out[t * spots : (t + 1) * spots, f * LANES : (f + 1) * LANES]
    buf[2] = buf[2] + dot_nt(df_prev, w7[6 * LANES : 7 * LANES, lat:])
    after = dot_nt(jnp.concatenate([dl_next, df_next], axis=1), w7[0 : 2 * LANES, :])
    total = frames * group
    for f in range(2):
        buf[total + f] = buf[total + f] + after[:, f * LANES : (f + 1) * LANES]
    mask = mk[m.main[0] : m.main[1], :]
    if last:
        for k in range(total):
            gx[k] = (pre[k] + buf[2 + k]) * mask
        return
    mean, rstd = n3[0:1, :], n3[1:2, :]
    gain = g[n - 1 : n, lo3 : lo3 + LANES]
    bias = b[n - 1 : n, lo3 : lo3 + LANES]
    one = jnp.zeros((8, LANES), F32)
    two = jnp.zeros((8, LANES), F32)
    for k in range(total):
        t, f = k // group, k % group
        hat = (ft[t, :, f * LANES : (f + 1) * LANES] - mean) * rstd
        z0 = fw0[2 + k].astype(F32) + hat * gain + bias
        grad = (pre[k] + buf[2 + k]) * mask * silu_slope(z0)
        pre0[k] = grad
        one = one + sublane_sums(grad)
        two = two + sublane_sums(grad * hat)
    s[...] = jnp.concatenate([row_sum(one), row_sum(two)], axis=1)


def point_weights(a2, d3, out):
    acts = flat(a2[...])
    for k in range(out.shape[0]):
        out[k] = dot_tn(acts, flat(d3[:, :, k * 256 : (k + 1) * 256]))


def space_weights(cols, aw, d2, out, vw):
    frames, spots, width = d2.shape
    for t in range(frames):
        store_shifts(vw, t, aw[t].astype(F32), cols)
    grads = flat(d2[...])
    for i in range(3):
        out[i] = dot_tn(flat(vw[:, i * cols : i * cols + spots, :]), grads)


def time_weights(skip, slow, jl, dw, out):
    frames, spots, width = jl.shape
    wide = slow.shape[2]
    grads = jnp.concatenate([flat(dw[2 - j : 2 - j + frames]) for j in range(3)], axis=1)
    for c in range(0, wide + jl.shape[2], 256):
        if c < wide:
            acts = flat(slow[skip : skip + frames, :, c : c + 256])
        else:
            acts = flat(jl[:, :, c - wide : c - wide + 256])
        got = dot_tn(acts, grads)
        for j in range(3):
            out[j, c : c + 256, :] = got[:, j * width : (j + 1) * width]


def group_blocks(value, group):
    size = LANES // group
    rows = lax.broadcasted_iota(jnp.int32, (LANES, LANES), 0) >> (size.bit_length() - 1)
    lanes = lax.broadcasted_iota(jnp.int32, (LANES, LANES), 1) >> (size.bit_length() - 1)
    kept = jnp.where(rows == lanes, value, 0.0)
    kept = kept + pltpu.roll(kept, 64, 1)
    kept = kept + pltpu.roll(kept, 32, 1)
    total = kept[0:size]
    for k in range(1, group):
        total = total + kept[k * size : (k + 1) * size]
    return total


def at_lanes(blocks):
    lanes = lax.broadcasted_iota(jnp.int32, blocks[0].shape, 1) >> 5
    out = jnp.zeros(blocks[0].shape, F32)
    for k, block in enumerate(blocks):
        out = jnp.where(lanes == k, block, out)
    return out


def fast_weights(group, cols, lat, fw, dl, df, fa1, d2, fa2, d3, glat, gfast, vw):
    frames, spots, _ = dl.shape
    size = LANES // group
    both = jnp.concatenate([flat(dl[...]), flat(df[...])], axis=1)
    taps = [[None] * group for _ in range(3)]
    for f in range(7):
        acts = jnp.concatenate([fw[group * t + f] for t in range(frames)], axis=0)
        got = dot_tn(acts, both)
        if f < 5:
            glat[f * LANES : (f + 1) * LANES, :] = got[:, :lat]
        for k in range(group):
            if 0 <= f - k - 1 < 3:
                taps[f - k - 1][k] = got[:, lat:]
    lanes = lax.broadcasted_iota(jnp.int32, (LANES, LANES), 1) >> (size.bit_length() - 1)
    tap_sums = []
    for j in range(3):
        kept = jnp.zeros((LANES, LANES), F32)
        for k in range(group):
            kept = jnp.where(lanes == k, taps[j][k], kept)
        kept = kept + pltpu.roll(kept, 64, 1)
        tap_sums.append(kept + pltpu.roll(kept, 32, 1))
    gfast[0:LANES, :] = at_lanes(tap_sums)
    for t in range(frames):
        store_shifts(vw, t, fa1[t].astype(F32), cols)
    grads = flat(d2[...])
    for i in range(3):
        got = dot_tn(flat(vw[:, i * cols : i * cols + spots, :]), grads)
        blocks = [group_blocks(got[j * LANES : (j + 1) * LANES], group) for j in range(3)]
        gfast[LANES + size * i : LANES + size * (i + 1), :] = at_lanes(blocks)
    acts = flat(fa2[...])
    total = jnp.zeros((size, LANES), F32)
    for k in range(group):
        got = dot_tn(acts, flat(d3[:, :, k * LANES : (k + 1) * LANES]))
        total = total + got[k * size : (k + 1) * size]
    gfast[LANES + 3 * size : LANES + 4 * size, :] = total


def on_device(
    x_slow,
    x_fast,
    w_lateral,
    w_slow_time,
    w_slow_space,
    w_slow_point,
    w_fast_time,
    w_fast_space,
    w_fast_point,
    gain_slow,
    bias_slow,
    gain_fast,
    bias_fast,
    clip_size,
    cot_slow,
    cot_fast,
):
    frames, fast_frames = x_slow.shape[0], x_fast.shape[0]
    group = fast_frames // frames
    rows, cols = x_slow.shape[3], x_slow.shape[4]
    spots = rows * cols
    wide, fwide = x_slow.shape[5], x_fast.shape[5]
    lat = w_lateral.shape[3]
    width = w_slow_space.shape[3]
    inner = w_fast_space.shape[3]
    packs = group * fwide
    both = lat + LANES
    m = Masks(spots, cols)
    devices = lax.axis_size("path") * lax.axis_size("rows")
    path = lax.axis_index("path")
    ext = spots + 2 * cols
    lo1, lo2, lo3 = lat, lat + width, lat + 2 * width
    every = slice(None)

    def part(fn, *static):
        return functools.partial(fn, *static)

    xs = x_slow.reshape(frames, spots, wide)
    xf = x_fast.reshape(fast_frames, spots, fwide)
    cs = cot_slow.reshape(frames, spots, wide)
    cf = cot_fast.reshape(fast_frames, spots, fwide)
    wft = jnp.swapaxes(w_fast_time, 2, 3)
    wfs_raw = w_fast_space.reshape(2, 9, inner, inner)
    wsp = w_slow_space.reshape(2, 3, 3 * width, width)

    def packed(value):
        return jnp.concatenate(
            [value[:, 0:inner]] * group + [value[:, inner : 2 * inner]] * group + [value[:, 2 * inner :]],
            axis=1,
        )

    gf, bf = packed(gain_fast), packed(bias_fast)

    xf_edge = swap_path(jnp.where(path > 0, xf[:2], xf[-2:]))
    xs_edge = swap_path(jnp.where(path > 0, xs[0], xs[-1]))

    def payload(k, *sums):
        size = sum(k.temps[s[1]].shape[1] for s in sums)
        out = k.give((devices, 1, size))
        k.step(spread_sums, *sums, out)
        return out

    def row_out(k, z, mk, col0, size):
        out = k.give((frames, cols, size))
        k.step(part(own_row, m, spots, cols, col0, size), z, mk, out)
        return out

    def edge_out(k, z, mk, size, tail=0):
        out = k.give((spots, size))
        k.step(part(own_edge, m, 0, tail), z, mk, out)
        return out

    def finish(k, **handles):
        got = k.run()
        return {name: got[handle[1]] for name, handle in handles.items()}

    def other_row(value):
        return swap(value, "rows", 1)

    first_flops = 2 * frames * spots * 7 * fwide * both
    k = Stage("entry")
    mk_out = k.give((m.rows, LANES))
    place = jnp.stack([lax.axis_index("rows"), path]).astype(jnp.int32)
    k.step(
        part(make_masks, m, rows, cols, lax.axis_size("path") - 1), k.scalar(place), k.scalar(clip_size), mk_out
    )
    w7_out = k.give((7 * fwide, both), BF16)
    k.step(part(make_w7, lat, group), k.take(w_lateral, 0), k.take(wft, 0), w7_out)
    fw = k.give((fast_frames + 4, spots, fwide), BF16)
    y = k.give((frames, spots, both))
    sy = k.temp((1, 2 * both))
    edge = k.take(xf_edge)
    k.step(
        part(fast_entry, m, frames, group), k.take(xf), edge, edge, mk_out, w7_out, fw, y, sy, flops=first_flops
    )
    pay = payload(k, sy)
    got = finish(
        k, mk=mk_out, w7=w7_out, fw=fw, y=y, pay=pay, ff_row=row_out(k, y, mk_out, lat, LANES),
        edge=edge_out(k, y, mk_out, both),
    )
    mk = got["mk"]
    saved = [{"fw": got["fw"], "y": got["y"], "w7": got["w7"]}, {}]
    st = gather_sums(got["pay"])
    saved[0]["ff_row"] = other_row(got["ff_row"])
    saved[0]["y_edge"] = swap_path(got["edge"])
    k = Stage("prepare")
    w7_out = k.give((7 * fwide, both), BF16)
    k.step(part(make_w7, lat, group), k.take(w_lateral, 1), k.take(wft, 1), w7_out)
    blocks = []
    for n in range(2):
        blocks += [k.give((3, 3 * LANES, LANES), BF16), k.give((LANES, packs), BF16)]
        k.step(part(make_blocks, group), k.take(wfs_raw, n), k.take(w_fast_point, n), *blocks[-2:])
    got = finish(k, w7=w7_out, wfs0=blocks[0], wfp0=blocks[1], wfs1=blocks[2], wfp1=blocks[3])
    saved[1]["w7"] = got["w7"]
    wfs, wfp = [got["wfs0"], got["wfs1"]], [got["wfp0"], got["wfp1"]]
    k = Stage("slow_partial")
    xm = k.give((frames + 2, spots, wide), BF16)
    fpart = k.give((frames, spots, width))
    edge = k.take(xs_edge)
    k.step(
        part(slow_partial, m, frames),
        k.take(xs), edge, edge, k.take(mk), k.take(w_slow_time, 0, every, slice(0, wide)), xm, fpart,
        flops=2 * frames * spots * 3 * wide * width,
    )
    got = finish(k, sw=xm, fpart=fpart)
    saved[0]["sw"] = got["sw"]
    fpart_in = got["fpart"]

    for n in range(2):
        v = saved[n]
        k = Stage("join")
        mk_in, gs, bs = k.take(mk), k.take(gain_slow), k.take(bias_slow)
        st_in = k.take(st)
        names = {}
        if n == 0:
            fpart = k.take(fpart_in)
        else:
            fpart = k.temp((frames, spots, width))
            names.update(
                slow1=k.give((frames, spots, wide)),
                sw=k.give((frames + 2, spots, wide), BF16),
            )
            n3 = k.give((2, wide))
            k.step(
                part(slow_next, m, 0, frames, lo3, 2 * both),
                st_in, k.take(saved[0]["third"]), k.take(saved[0]["sw"]),
                k.take(w_slow_time, 1, every, slice(0, wide)), gs, bs, mk_in,
                names["slow1"], names["sw"], fpart, n3,
                flops=2 * frames * spots * 3 * wide * width,
            )
            names["n3"] = n3
        y_in, edge = k.take(v["y"]), k.take(v["y_edge"])
        jl = k.give((frames, spots, lat), BF16)
        first = k.give((frames, spots, width))
        nl = k.give((2, lat))
        s_first, s_fs = k.temp((1, 2 * width)), k.temp((1, 2 * LANES))
        k.step(
            part(lat_join, m, n, frames, lat),
            st_in, y_in, edge, edge, fpart, k.take(w_slow_time, n, every, slice(wide, wide + lat)), gs, bs, mk_in,
            jl, first, s_first, nl, k.temp((frames + 2, spots, lat), BF16),
            flops=2 * frames * spots * 3 * lat * width,
        )
        fa1 = k.give((frames, ext, LANES), BF16)
        fs = k.give((frames, spots, LANES))
        nf1 = k.give((2, LANES))
        k.step(
            part(space_forward, m, n, frames, cols, 0, 2 * lat, LANES, lat, True, m.fast),
            st_in, y_in, k.take(v["ff_row"]), k.take(wfs[n]), k.take(gf), k.take(bf), mk_in,
            fa1, fs, s_fs, nf1, k.temp((frames, ext, 3 * LANES), BF16),
            flops=2 * frames * spots * 9 * LANES * LANES,
        )
        pay = payload(k, s_first, s_fs)
        got = finish(
            k, jl=jl, first=first, nl=nl, fa1=fa1, fs=fs, nf1=nf1, pay=pay,
            first_row=row_out(k, first, mk_in, 0, width), fs_row=row_out(k, fs, mk_in, 0, LANES),
            first_edge=edge_out(k, first, mk_in, width), **names,
        )
        st = gather_sums(got["pay"])
        for name in ("jl", "first", "nl", "fa1", "fs", "nf1"):
            v[name] = got[name]
        if n == 1:
            slow1, saved[1]["sw"], saved[0]["n3"] = got["slow1"], got["sw"], got["n3"]
        first_row = other_row(got["first_row"])
        v["fs_row"] = other_row(got["fs_row"])
        v["first_edge"] = swap_path(got["first_edge"])
        k = Stage("space")
        mk_in, st_in = k.take(mk), k.take(st)
        a1 = k.give((frames, ext, width), BF16)
        second = k.give((frames, spots, width))
        n1 = k.give((2, width))
        s_second, s_ft = k.temp((1, 2 * width)), k.temp((1, 2 * LANES))
        k.step(
            part(space_forward, m, n, frames, cols, lo1, 0, width, 0, False, m.slow),
            st_in, k.take(v["first"]), k.take(first_row), k.take(wsp, n), k.take(gain_slow), k.take(bias_slow), mk_in,
            a1, second, s_second, n1, k.temp((frames, ext, 3 * width), BF16),
            flops=2 * frames * spots * 9 * width * width,
        )
        fa2 = k.give((frames, spots, LANES), BF16)
        ft = k.give((frames, spots, packs))
        nf2 = k.give((2, LANES))
        k.step(
            part(fast_third, m, n, frames, LANES, 2 * width),
            st_in, k.take(v["fs"]), k.take(wfp[n]), k.take(gf), k.take(bf), mk_in, fa2, ft, s_ft, nf2,
            flops=2 * frames * spots * LANES * packs,
        )
        pay = payload(k, s_second, s_ft)
        names = {"second_row": row_out(k, second, mk_in, 0, width)}
        if n == 0:
            names["second_edge"] = edge_out(k, second, mk_in, width)
            names["ft_edge"] = edge_out(k, ft, mk_in, 2 * fwide, (group - 2) * fwide)
        got = finish(k, a1=a1, second=second, n1=n1, fa2=fa2, ft=ft, nf2=nf2, pay=pay, **names)
        st = gather_sums(got["pay"])
        for name in ("a1", "second", "n1", "fa2", "ft", "nf2"):
            v[name] = got[name]
        v["second_row"] = other_row(got["second_row"])
        halo = 1 - n
        edges = []
        k = Stage("third")
        if n == 0:
            ft_edge = k.take(swap_path(got["ft_edge"]))
            edges = [k.take(swap_path(got["second_edge"]))] * 2
        mk_in, st_in = k.take(mk), k.take(st)
        a2 = k.give((frames, spots, width), BF16)
        third = k.give((frames + 2 * halo, spots, wide))
        n2 = k.give((2, width))
        nf3 = k.give((2, LANES))
        s_third = k.temp((1, 2 * wide))
        names = {}
        if n == 0:
            names.update(
                f1=k.give((fast_frames, spots, fwide)),
                fw=k.give((fast_frames + 4, spots, fwide), BF16),
                y=k.give((frames, spots, both)),
            )
            s_fast = k.temp((1, 2 * both))
            k.step(
                part(fast_next, m, n, frames, group, 2 * LANES, 2 * width),
                st_in, k.take(v["ft"]), ft_edge, ft_edge, k.take(v["fw"]), k.take(saved[1]["w7"]),
                k.take(gf), k.take(bf), mk_in, names["f1"], names["fw"], names["y"], s_fast, nf3,
                flops=first_flops,
            )
        else:
            names.update(out_fast=k.give((fast_frames, spots, fwide)), pre_f=k.give((fast_frames, spots, fwide)))
            s_fast = k.temp((1, 2 * LANES))
            k.step(
                part(fast_last, m, n, frames, group, 2 * LANES, 2 * width),
                st_in, k.take(v["ft"]), k.take(fast1), k.take(cf), k.take(gf), k.take(bf), mk_in,
                names["out_fast"], names["pre_f"], s_fast, nf3,
            )
        k.step(
            part(slow_third, m, n, frames, lo2, halo),
            st_in, k.take(v["second"]), *edges, k.take(w_slow_point, n), k.take(gain_slow), k.take(bias_slow), mk_in,
            a2, third, s_third, n2, k.temp((frames + 2 * halo, spots, width), BF16),
            flops=2 * frames * spots * width * wide,
        )
        if n == 0:
            pay = payload(k, s_fast, s_third)
            names["ff_row"] = row_out(k, names["y"], mk_in, lat, LANES)
            names["y_edge"] = edge_out(k, names["y"], mk_in, both)
        else:
            pay = payload(k, s_third, s_fast)
        got = finish(k, a2=a2, third=third, n2=n2, nf3=nf3, pay=pay, **names)
        st = gather_sums(got["pay"])
        for name in ("a2", "third", "n2", "nf3"):
            v[name] = got[name]
        if n == 0:
            fast1 = got["f1"]
            saved[1].update(
                fw=got["fw"], y=got["y"], ff_row=other_row(got["ff_row"]), y_edge=swap_path(got["y_edge"])
            )
        else:
            out_fast, pre_f = got["out_fast"], got["pre_f"]

    def third_back(k, n, at, st_in, mk_in, pre):
        v = saved[n]
        d3, e2 = k.give((frames, spots, wide), BF16), k.give((frames, spots, width))
        s, gb = k.temp((1, 2 * width)), k.give((2, wide))
        k.step(
            part(slow_third_back, m, n, frames, lo3, lo2, at, 1 - n),
            st_in, k.take(pre), k.take(v["third"]), k.take(v["n3"]), k.take(v["second"]), k.take(v["n2"]),
            k.take(w_slow_point, n), k.take(gain_slow), k.take(bias_slow), mk_in, d3, e2, s, gb,
            flops=2 * frames * spots * width * wide,
        )
        return dict(d3=d3, e2=e2, gb3=gb), s

    def fast_back3(k, n, at, st_in, mk_in, pre):
        v = saved[n]
        d3, e2 = k.give((frames, spots, packs), BF16), k.give((frames, spots, LANES))
        s, gb = k.temp((1, 2 * LANES)), k.give((2, LANES))
        k.step(
            part(fast_third_back, m, n, frames, group, 2 * LANES, LANES, at),
            st_in, k.take(pre), k.take(v["ft"]), k.take(v["nf3"]), k.take(v["fs"]), k.take(v["nf2"]),
            k.take(wfp[n]), k.take(gf), k.take(bf), mk_in, d3, e2, s, gb,
            flops=2 * frames * spots * LANES * packs,
        )
        return dict(d3f=d3, ef2=e2, gbf3=gb), s

    def second_back(k, n, at, st_in, mk_in, e2, e2_row):
        v = saved[n]
        d2, e1 = k.give((frames, spots, width), BF16), k.give((frames, spots, width))
        s, gb = k.temp((1, 2 * width)), k.give((2, width))
        k.step(
            part(space_back, m, n, frames, cols, lo2, lo1, at, width, 0, False, m.slow),
            st_in, k.take(e2), k.take(e2_row), k.take(v["second"]), k.take(v["second_row"]), k.take(v["n2"]),
            k.take(v["first"]), k.take(v["n1"]), k.take(wsp, n), k.take(gain_slow), k.take(bias_slow), mk_in,
            d2, e1, s, gb, k.temp((frames, ext, 3 * width), BF16),
            flops=2 * frames * spots * 9 * width * width,
        )
        return dict(d2=d2, e1=e1, gb2=gb), s

    def fast_back2(k, n, at, st_in, mk_in, ef2, ef2_row):
        v = saved[n]
        d2, e1 = k.give((frames, spots, LANES), BF16), k.give((frames, spots, LANES))
        s, gb = k.temp((1, 2 * LANES)), k.give((2, LANES))
        k.step(
            part(space_back, m, n, frames, cols, LANES, 0, at, LANES, lat, True, m.fast),
            st_in, k.take(ef2), k.take(ef2_row), k.take(v["fs"]), k.take(v["fs_row"]), k.take(v["nf2"]),
            k.take(v["y"]), k.take(v["nf1"]), k.take(wfs[n]), k.take(gf), k.take(bf), mk_in,
            d2, e1, s, gb, k.temp((frames, ext, 3 * LANES), BF16),
            flops=2 * frames * spots * 9 * LANES * LANES,
        )
        return dict(d2f=d2, ef1=e1, gbf2=gb), s

    def first_back(k, n, st_in, mk_in, e1, e1_edge, pre):
        v = saved[n]
        last = n == 0
        dw, el = k.give((frames + 2, spots, width), BF16), k.give((frames, spots, lat))
        s, gb = k.temp((1, 2 * lat)), k.give((2, width))
        down = k.give((frames, spots, wide))
        edge, zedge = k.take(e1_edge), k.take(v["first_edge"])
        args = [
            st_in, k.take(e1), edge, edge, k.take(v["first"]), zedge, zedge, k.take(v["n1"]),
            k.take(w_slow_time, n), k.take(v["y"]), k.take(v["nl"]), k.take(pre),
        ]
        outs = [dw, el, s, down]
        sums = [s]
        if not last:
            args += [k.take(saved[0]["sw"]), k.take(saved[0]["third"]), k.take(saved[0]["n3"])]
            sums.append(k.temp((1, 2 * wide)))
            outs.append(sums[1])
        k.step(
            part(slow_first_back, m, n, frames, lo1, lo3, 0, 1, last),
            *args, k.take(gain_slow), k.take(bias_slow), mk_in, *outs, gb,
            flops=2 * frames * spots * 3 * (wide + lat) * width,
        )
        return dict(dw=dw, el=el, down=down, gb1=gb), sums

    def fast_back1(k, n, st1, at1, stl, atl, mk_in, el, el_edge, ef1, ef1_edge, pre):
        v = saved[n]
        last = n == 0
        dl, df = k.give((frames, spots, lat), BF16), k.give((frames, spots, LANES), BF16)
        down = k.give((fast_frames, spots, fwide))
        gbl, gb1 = k.give((2, lat)), k.give((2, LANES))
        edge, yedge = k.take(ef1_edge), k.take(v["y_edge"])
        args = [
            st1, stl, k.take(el), k.take(el_edge), k.take(ef1), edge, edge, k.take(v["y"]), yedge, yedge,
            k.take(v["nl"]), k.take(v["nf1"]), k.take(v["w7"]), k.take(pre),
        ]
        outs = [dl, df, down]
        s = None
        if not last:
            args += [k.take(saved[0]["fw"]), k.take(saved[0]["ft"]), k.take(saved[0]["nf3"])]
            s = k.temp((1, 2 * LANES))
            outs.append(s)
        k.step(
            part(fast_first_back, m, n, frames, group, 0, 2 * LANES, at1, atl, last),
            *args, k.take(gain_slow), k.take(gf), k.take(bf), mk_in, *outs, gbl, gb1,
            k.temp((fast_frames + 4, spots, fwide)),
            flops=first_flops,
        )
        return dict(dl=dl, df=df, downf=down, gbl=gbl, gbf1=gb1), s

    def weights_point(n, d3):
        k = Stage("point_weights")
        out = k.give((wide // 256, width, 256))
        k.step(point_weights, k.take(saved[n]["a2"]), k.take(d3), out, flops=2 * frames * spots * width * wide)
        return k.run()[0].reshape(-1, 256)

    def weights_space(n, d2):
        k = Stage("space_weights")
        out = k.give((3, 3 * width, width))
        k.step(
            part(space_weights, cols), k.take(saved[n]["a1"]), k.take(d2), out,
            k.temp((frames, ext, 3 * width), BF16), flops=2 * frames * spots * 9 * width * width,
        )
        return k.run()[0].reshape(-1, 256)

    def weights_time(n, dw):
        k = Stage("time_weights")
        out = k.give((3, wide + lat, width))
        k.step(
            part(time_weights, 1), k.take(saved[n]["sw"]), k.take(saved[n]["jl"]), k.take(dw), out,
            flops=2 * frames * spots * 3 * (wide + lat) * width,
        )
        return k.run()[0].reshape(-1, 256)

    def weights_fast(n, dl, df, d2, d3):
        v = saved[n]
        k = Stage("fast_weights")
        glat, gfast = k.give((5 * fwide, lat)), k.give((2 * LANES, LANES))
        k.step(
            part(fast_weights, group, cols, lat),
            k.take(v["fw"]), k.take(dl), k.take(df), k.take(v["fa1"]), k.take(d2), k.take(v["fa2"]), k.take(d3),
            glat, gfast, k.temp((frames, ext, 3 * LANES), BF16), flops=first_flops,
        )
        glat, gfast = k.run()
        gfast = jnp.concatenate([gfast[:LANES], gfast[LANES:]], axis=1)
        return jnp.concatenate([glat, gfast], axis=0)

    b1, b0 = {}, {}
    k = Stage("last")
    mk_in, st_in = k.take(mk), k.take(st)
    out_slow, pre = k.give((frames, spots, wide)), k.give((frames, spots, wide))
    n3 = k.give((2, wide))
    s_pre = k.temp((1, 2 * wide))
    k.step(
        part(slow_last, m, 1, frames, lo3),
        st_in, k.take(saved[1]["third"]), k.take(slow1), k.take(cs), k.take(gain_slow), k.take(bias_slow), mk_in,
        out_slow, pre, s_pre, n3,
    )
    names, s_ef2 = fast_back3(k, 1, 2 * wide, st_in, mk_in, pre_f)
    pay = payload(k, s_pre, s_ef2)
    ef2_row = row_out(k, names["ef2"], mk_in, 0, LANES)
    b1 = finish(k, out_slow=out_slow, pre=pre, n3=n3, pay=pay, ef2_row=ef2_row, **names)
    saved[1]["n3"] = b1["n3"]
    out_slow = b1["out_slow"]
    st = gather_sums(b1["pay"])

    k = Stage("back_third")
    ef2_row = k.take(other_row(b1["ef2_row"]))
    mk_in, st_in = k.take(mk), k.take(st)
    names, s_e2 = third_back(k, 1, 0, st_in, mk_in, b1["pre"])
    more, s_ef1 = fast_back2(k, 1, 2 * wide, st_in, mk_in, b1["ef2"], k.arrays[k.views[ef2_row[1]][0]])
    pay = payload(k, s_e2, s_ef1)
    e2_row, ef1_edge = row_out(k, names["e2"], mk_in, 0, width), edge_out(k, more["ef1"], mk_in, LANES)
    b1.update(finish(k, pay=pay, e2_row=e2_row, ef1_edge=ef1_edge, **names, **more))
    st = st_ef1 = gather_sums(b1["pay"])
    e2_row, ef1_edge = other_row(b1["e2_row"]), swap_path(b1["ef1_edge"])
    point1 = weights_point(1, b1["d3"])

    k = Stage("back_space")
    mk_in, st_in = k.take(mk), k.take(st)
    names, s_e1 = second_back(k, 1, 0, st_in, mk_in, b1["e2"], e2_row)
    pay = payload(k, s_e1)
    e1_edge = edge_out(k, names["e1"], mk_in, width)
    b1.update(finish(k, pay=pay, e1_edge=e1_edge, **names))
    st = gather_sums(b1["pay"])
    e1_edge = swap_path(b1["e1_edge"])
    space1 = weights_space(1, b1["d2"])

    k = Stage("back_first")
    mk_in, st_in = k.take(mk), k.take(st)
    names, sums = first_back(k, 1, st_in, mk_in, b1["e1"], e1_edge, b1["pre"])
    pay = payload(k, *sums)
    el_edge = edge_out(k, names["el"], mk_in, lat)
    b1.update(finish(k, pay=pay, el_edge=el_edge, **names))
    st = gather_sums(b1["pay"])
    el_edge = swap_path(b1["el_edge"])
    time1 = weights_time(1, b1["dw"])

    k = Stage("back_third")
    mk_in, st_in = k.take(mk), k.take(st)
    names, s_e2 = third_back(k, 0, 2 * lat, st_in, mk_in, b1["down"])
    more, s_pf = fast_back1(
        k, 1, k.take(st_ef1), 2 * width, st_in, 0, mk_in, b1["el"], el_edge, b1["ef1"], ef1_edge, pre_f
    )
    pay = payload(k, s_e2, s_pf)
    e2_row = row_out(k, names["e2"], mk_in, 0, width)
    got = finish(k, pay=pay, e2_row=e2_row, **names, **more)
    for name in more:
        b1[name] = got[name]
    b0.update({name: got[name] for name in names})
    st = gather_sums(got["pay"])
    e2_row = other_row(got["e2_row"])
    point0 = weights_point(0, b0["d3"])
    fast_1 = weights_fast(1, b1["dl"], b1["df"], b1["d2f"], b1["d3f"])

    k = Stage("back_space")
    mk_in, st_in = k.take(mk), k.take(st)
    names, s_e1 = second_back(k, 0, 0, st_in, mk_in, b0["e2"], e2_row)
    more, s_ef2 = fast_back3(k, 0, 2 * width, st_in, mk_in, b1["downf"])
    pay = payload(k, s_e1, s_ef2)
    e1_edge, ef2_row = edge_out(k, names["e1"], mk_in, width), row_out(k, more["ef2"], mk_in, 0, LANES)
    b0.update(finish(k, pay=pay, e1_edge=e1_edge, ef2_row=ef2_row, **names, **more))
    st = gather_sums(b0["pay"])
    e1_edge, ef2_row = swap_path(b0["e1_edge"]), other_row(b0["ef2_row"])
    space0 = weights_space(0, b0["d2"])

    k = Stage("back_first")
    mk_in, st_in = k.take(mk), k.take(st)
    names, sums = first_back(k, 0, st_in, mk_in, b0["e1"], e1_edge, b1["down"])
    more, s_ef1 = fast_back2(k, 0, 2 * width, st_in, mk_in, b0["ef2"], ef2_row)
    pay = payload(k, *sums, s_ef1)
    el_edge, ef1_edge = edge_out(k, names["el"], mk_in, lat), edge_out(k, more["ef1"], mk_in, LANES)
    b0.update(finish(k, pay=pay, el_edge=el_edge, ef1_edge=ef1_edge, **names, **more))
    st = gather_sums(b0["pay"])
    el_edge, ef1_edge = swap_path(b0["el_edge"]), swap_path(b0["ef1_edge"])
    time0 = weights_time(0, b0["dw"])

    k = Stage("back_fast")
    mk_in, st_in = k.take(mk), k.take(st)
    more, _ = fast_back1(
        k, 0, st_in, 2 * lat, st_in, 0, mk_in, b0["el"], el_edge, b0["ef1"], ef1_edge, b1["downf"]
    )
    b0.update(finish(k, **more))
    fast_0 = weights_fast(0, b0["dl"], b0["df"], b0["d2f"], b0["d3f"])

    def reduced(*pieces):
        sizes = [piece.shape[0] for piece in pieces]
        got = reduce_rows(jnp.concatenate(pieces, axis=0))
        outs, at = [], 0
        for size in sizes:
            outs.append(got[at : at + size])
            at += size
        return outs

    point1, space1, time1, fast_1 = reduced(point1, space1, time1, fast_1)
    point0, space0 = reduced(point0, space0)
    time0, fast_0 = reduced(time0, fast_0)

    def stack(zero, one):
        return jnp.stack([zero.astype(F32), one.astype(F32)])

    def from_fast(value):
        tail = value[5 * fwide :]
        tail = jnp.concatenate([tail[:, :LANES], tail[:, LANES:]], axis=0)
        time = tail[:LANES, : 3 * inner].reshape(fwide, 3, inner).transpose(1, 0, 2)
        space = tail[LANES : LANES + 3 * inner, : 3 * inner].reshape(3, inner, 3, inner).transpose(0, 2, 1, 3)
        return value[: 5 * fwide].reshape(5, fwide, lat), time, space, tail[LANES + 3 * inner :]

    lat0, ftime0, fspace0, fpoint0 = from_fast(fast_0)
    lat1, ftime1, fspace1, fpoint1 = from_fast(fast_1)

    def from_point(value):
        return jnp.concatenate([value[k * width : (k + 1) * width] for k in range(wide // 256)], axis=1)

    def slow_rows(b, row):
        return jnp.concatenate([b[name][row] for name in ("gbl", "gb1", "gb2", "gb3")])

    def fast_rows(b, row):
        return jnp.concatenate([b["gbf1"][row, :inner], b["gbf2"][row, :inner], b["gbf3"][row]])

    return (
        out_slow.reshape(x_slow.shape),
        out_fast.reshape(x_fast.shape),
        b0["down"].reshape(x_slow.shape),
        b0["downf"].reshape(x_fast.shape),
        stack(lat0, lat1),
        stack(time0, time1).reshape(w_slow_time.shape),
        stack(space0, space1).reshape(w_slow_space.shape),
        stack(from_point(point0), from_point(point1)),
        stack(ftime0, ftime1),
        stack(fspace0, fspace1),
        stack(fpoint0, fpoint1),
        jnp.stack([slow_rows(b0, 1), slow_rows(b1, 1)]),
        jnp.stack([slow_rows(b0, 0), slow_rows(b1, 0)]),
        jnp.stack([fast_rows(b0, 1), fast_rows(b1, 1)]),
        jnp.stack([fast_rows(b0, 0), fast_rows(b1, 0)]),
    )


def solution(mesh):
    spread = P("path", None, "rows", None, None, None)
    return jax.shard_map(
        on_device,
        mesh=mesh,
        in_specs=(spread, spread) + (P(),) * 12 + (spread, spread),
        out_specs=(spread,) * 4 + (P(),) * 11,
        check_vma=False,
    )
```

```python
import functools

import jax
import jax.numpy as jnp
import numpy as np
from jax import lax
from jax.experimental import pallas as pl
from jax.experimental.pallas import tpu as pltpu
from jax.sharding import PartitionSpec as P

TS = 8
TF = 32
F32 = jnp.float32
BF16 = jnp.bfloat16
EPSILON = 1e-05
LANES = 128
AXES = ("path", "rows")
VMEM_LIMIT = 56 * 2**20


def swap(value, axis, stride):
    pairs = [(source, source ^ stride) for source in range(lax.axis_size(axis))]
    return lax.ppermute(value, axis, pairs)


def gather_sums(spread):
    return lax.all_to_all(spread, AXES, 0, 0, tiled=True)


def swap_path(value):
    assert lax.axis_size("path") == 2
    return lax.ppermute(value, "path", [(0, 1), (1, 0)])


def exchange_steps():
    steps = [("rows", 1), ("path", 1)]
    stride = 2
    while stride < lax.axis_size("rows"):
        steps.append(("rows", stride))
        stride *= 2
    return steps


def halve(value, axis, stride):
    size = value.shape[0] // 2
    upper = (lax.axis_index(axis) // stride) % 2
    keep = lax.dynamic_slice_in_dim(value, upper * size, size, 0)
    give = lax.dynamic_slice_in_dim(value, (1 - upper) * size, size, 0)
    return keep.astype(F32) + swap(give.astype(BF16), axis, stride).astype(F32)


def double(value, axis, stride):
    upper = (lax.axis_index(axis) // stride) % 2
    got = swap(value, axis, stride)
    return jnp.concatenate(
        [jnp.where(upper == 0, value, got), jnp.where(upper == 0, got, value)], axis=0
    )


class Stage:
    def __init__(self, name):
        self.name = name
        self.arrays, self.views, self.scalars, self.nears = [], [], [], []
        self.outs, self.temps, self.steps = [], [], []
        self.flops = 0

    def take(self, array, *view):
        for at, known in enumerate(self.arrays):
            if known is array:
                break
        else:
            at = len(self.arrays)
            self.arrays.append(array)
        for k, (other, seen) in enumerate(self.views):
            if other == at and seen == view:
                return ("in", k)
        self.views.append((at, view))
        return ("in", len(self.views) - 1)

    def near(self, array):
        for at, known in enumerate(self.nears):
            if known is array:
                return ("near", at)
        self.nears.append(array)
        return ("near", len(self.nears) - 1)

    def scalar(self, array):
        self.scalars.append(array)
        return ("scalar", len(self.scalars) - 1)

    def give(self, dims, dtype=F32):
        self.outs.append(jax.ShapeDtypeStruct(tuple(dims), dtype))
        return ("out", len(self.outs) - 1)

    def temp(self, dims, dtype=F32):
        self.temps.append(pltpu.VMEM(tuple(dims), dtype))
        return ("temp", len(self.temps) - 1)

    def step(self, fn, *handles, flops=0):
        self.flops += flops
        self.steps.append((fn, handles))

    def view_shape(self, view):
        at, index = view
        return np.broadcast_to(np.zeros((), np.int8), self.arrays[at].shape)[index].shape

    def run(self):
        arrays, views, outs, steps = self.arrays, self.views, self.outs, self.steps
        order = []
        for _, handles in steps:
            for handle in handles:
                if handle[0] == "in" and handle[1] not in order:
                    order.append(handle[1])

        def body(*refs):
            refs = list(refs)

            def cut(count):
                taken = refs[:count]
                del refs[:count]
                return taken

            scalars, nears = cut(len(self.scalars)), cut(len(self.nears))
            hbm_in, hbm_out = cut(len(arrays)), cut(len(outs))
            held, made, temps = cut(len(views)), cut(len(outs)), cut(len(self.temps))
            (sems,) = refs
            copies = {}
            for k in order:
                at, index = views[k]
                src = hbm_in[at].at[index] if index else hbm_in[at]
                copies[k] = pltpu.make_async_copy(src, held[k], sems.at[k])
                copies[k].start()
            waited, sent = set(), {}
            for fn, handles in steps:
                given = []
                for kind, k in handles:
                    if kind == "in" and k not in waited:
                        copies[k].wait()
                        waited.add(k)
                    given.append({"in": held, "out": made, "temp": temps, "scalar": scalars, "near": nears}[kind][k])
                fn(*given)
                for kind, k in handles:
                    if kind == "out" and k not in sent:
                        sent[k] = pltpu.make_async_copy(made[k], hbm_out[k], sems.at[len(views) + k])
                        sent[k].start()
            for copy in sent.values():
                copy.wait()

        moved = sum(a.size * a.dtype.itemsize for a in outs)
        for view in views:
            moved += int(np.prod(self.view_shape(view))) * arrays[view[0]].dtype.itemsize
        scratch = [pltpu.VMEM(self.view_shape(view), arrays[view[0]].dtype) for view in views]
        scratch += [pltpu.VMEM(o.shape, o.dtype) for o in outs]
        scratch += self.temps + [pltpu.SemaphoreType.DMA((len(views) + len(outs),))]
        return pl.pallas_call(
            body,
            out_shape=tuple(outs),
            in_specs=[pl.BlockSpec(memory_space=pltpu.SMEM) for _ in self.scalars]
            + [pl.BlockSpec(memory_space=pltpu.VMEM) for _ in self.nears]
            + [pl.BlockSpec(memory_space=pl.ANY) for _ in arrays],
            out_specs=tuple(pl.BlockSpec(memory_space=pl.ANY) for _ in outs),
            scratch_shapes=scratch,
            compiler_params=pltpu.CompilerParams(vmem_limit_bytes=VMEM_LIMIT),
            cost_estimate=pl.CostEstimate(flops=self.flops, bytes_accessed=moved, transcendentals=0),
            name=self.name,
        )(*self.scalars, *self.nears, *arrays)


class Masks:
    def __init__(self, spots, cols):
        self.main = (0, spots)
        self.ext = (spots, 2 * spots + 2 * cols)
        self.prev = (2 * spots + 2 * cols, 3 * spots + 2 * cols)
        self.next = (3 * spots + 2 * cols, 4 * spots + 2 * cols)
        self.slow = (4 * spots + 2 * cols, 4 * spots + 2 * cols + 8)
        self.fast = (4 * spots + 2 * cols + 8, 4 * spots + 2 * cols + 16)
        self.half = (4 * spots + 2 * cols + 16, 4 * spots + 2 * cols + 24)
        self.path = (4 * spots + 2 * cols + 24, 4 * spots + 2 * cols + 32)
        self.rows = 4 * spots + 2 * cols + 32


def make_masks(m, rows, cols, last, place, clips, mk):
    half = place[0] % 2
    path = place[1]
    side = clips[0, place[0] // 2]
    area = 0
    for k in range(clips.shape[1]):
        area = area + clips[0, k] * clips[0, k]
    shift = cols.bit_length() - 1

    def inside(first, count):
        at = lax.broadcasted_iota(jnp.int32, (count * cols, LANES), 0)
        line = half * rows + first + (at >> shift)
        spot = at & (cols - 1)
        good = (line >= 0) & (line < 2 * rows) & (line < side) & (spot < side)
        return jnp.where(good, 1.0, 0.0)

    main = inside(0, rows)
    mk[m.main[0] : m.main[1], :] = main
    mk[m.ext[0] : m.ext[1], :] = inside(-1, rows + 2)
    mk[m.prev[0] : m.prev[1], :] = main * jnp.where(path > 0, 1.0, 0.0)
    mk[m.next[0] : m.next[1], :] = main * jnp.where(path < last, 1.0, 0.0)

    def fill(span, value):
        mk[span[0] : span[1], :] = jnp.full((8, LANES), value, F32)

    fill(m.slow, TS * area.astype(F32))
    fill(m.fast, TF * area.astype(F32))
    fill(m.half, half.astype(F32))
    fill(m.path, path.astype(F32))


def own_row(m, spots, cols, col0, width, z, mk, row):
    for t in range(z.shape[0]):
        lower = mk[m.half[0] : m.half[0] + 1, :] > 0.5
        for lane in range(0, width, LANES):
            at = col0 + lane
            row[t, :, lane : lane + LANES] = jnp.where(
                lower, z[t, 0:cols, at : at + LANES], z[t, spots - cols : spots, at : at + LANES]
            )


def own_edge(m, lead, tail, z, mk, edge):
    frames = z.shape[0]
    second = mk[m.path[0] : m.path[0] + 1, :] > 0.5
    for lane in range(0, edge.shape[1], LANES):
        edge[:, lane : lane + LANES] = jnp.where(
            second,
            z[0, :, lead + lane : lead + lane + LANES],
            z[frames - 1, :, tail + lane : tail + lane + LANES],
        )


def spread_sums(*refs):
    parts, out = refs[:-1], refs[-1]
    row = jnp.concatenate([part[...] for part in parts], axis=1)
    out[...] = jnp.broadcast_to(row[None], out.shape)


def make_w7(lat, group, wl, wf, w7):
    inner = wf.shape[1]
    w7[...] = jnp.zeros(w7.shape, BF16)
    for j in range(wl.shape[0]):
        w7[j * LANES : (j + 1) * LANES, 0:lat] = wl[j]
    at = lax.broadcasted_iota(jnp.int32, (inner, LANES), 0)
    lane = lax.broadcasted_iota(jnp.int32, (inner, LANES), 1)
    places = [jnp.where(lane == at + inner * k, 1.0, 0.0).astype(BF16) for k in range(group)]
    for f in range(1, group + 3):
        used = [k for k in range(group) if 0 <= f - 1 - k < 3]
        got = None
        for k in used:
            more = dot_tn(wf[f - 1 - k], places[k])
            got = more if got is None else got + more
        w7[f * LANES : (f + 1) * LANES, lat : lat + LANES] = got.astype(BF16)


def make_blocks(group, ws, wp, wfs, wfp):
    inner = wp.shape[0]
    at = lax.broadcasted_iota(jnp.int32, (inner, LANES), 0)
    lane = lax.broadcasted_iota(jnp.int32, (inner, LANES), 1)
    tile = jnp.where((lane & (inner - 1)) == at, 1.0, 0.0).astype(BF16)
    shift = inner.bit_length() - 1
    for tap in range(ws.shape[0]):
        got = dot(ws[tap], tile)
        for k in range(group):
            kept = jnp.where((lane >> shift) == k, got, 0.0).astype(BF16)
            row = (tap % 3) * LANES + k * inner
            wfs[tap // 3, row : row + inner, :] = kept
    wfp[...] = jnp.zeros(wfp.shape, BF16)
    for k in range(group):
        wfp[k * inner : (k + 1) * inner, k * LANES : (k + 1) * LANES] = wp[...]


def widen(rows, width):
    return jnp.concatenate([rows] * (width // LANES), axis=1)


def sublane_sums(value):
    return jnp.sum(value.reshape(value.shape[0] // 8, 8, value.shape[1]), axis=0)


def row_sum(value):
    return jnp.sum(value, axis=0, keepdims=True)


def fold_packed(row):
    full = jnp.broadcast_to(row, (8, LANES))
    full = full + pltpu.roll(full, 64, 1)
    full = full + pltpu.roll(full, 32, 1)
    return full[0:1]


def totals(st, lo, width, packed=False):
    first = jnp.sum(st[:, :, lo : lo + width], axis=0)
    second = jnp.sum(st[:, :, lo + width : lo + 2 * width], axis=0)
    if packed:
        return fold_packed(first), fold_packed(second)
    return first, second


def norm_rows(st, lo, width, count, packed=False):
    first, second = totals(st, lo, width, packed)
    mean = first / count
    return mean, lax.rsqrt(second / count - mean * mean + EPSILON)


def sigmoid(value):
    return 0.5 * jnp.tanh(0.5 * value) + 0.5


def silu(value):
    return value * sigmoid(value)


def silu_slope(value):
    sigma = sigmoid(value)
    return sigma * (1.0 + value * (1.0 - sigma))


def dot(a, b):
    return jnp.dot(a, b, preferred_element_type=F32)


def dot_nt(a, b):
    return lax.dot_general(a, b, (((1,), (1,)), ((), ())), preferred_element_type=F32)


def dot_tn(a, b):
    return lax.dot_general(a, b, (((0,), (0,)), ((), ())), preferred_element_type=F32)


def flat(value):
    return value.reshape(value.shape[0] * value.shape[1], value.shape[2])


def store_shifts(dst, t, value, cols):
    rows, width = value.shape
    spot = lax.broadcasted_iota(jnp.int32, (rows, width), 0) & (cols - 1)
    left = jnp.where(spot == 0, 0.0, pltpu.roll(value, 1, 0))
    right = jnp.where(spot == cols - 1, 0.0, pltpu.roll(value, rows - 1, 0))
    dst[t, :, 0:width] = left.astype(BF16)
    dst[t, :, width : 2 * width] = value.astype(BF16)
    dst[t, :, 2 * width : 3 * width] = right.astype(BF16)


def taps_of(frames_ref, frames, group):
    return jnp.concatenate(
        [
            jnp.concatenate([frames_ref[group * t + f] for f in range(7)], axis=1)
            for t in range(frames)
        ],
        axis=0,
    )


def entry_sums(y, lat, frames, spots):
    width = y.shape[1]
    one = jnp.zeros((8, width), F32)
    two = jnp.zeros((8, width), F32)
    for t in range(frames):
        part = y[t * spots : (t + 1) * spots]
        one = one + sublane_sums(part)
        two = two + sublane_sums(part * part)
    one = row_sum(one)
    two = row_sum(two)
    return jnp.concatenate([one[:, :lat], two[:, :lat], one[:, lat:], two[:, lat:]], axis=1)


def fast_entry(m, frames, group, x, before, after, mk, w7, fw, y, s):
    spots = x.shape[1]
    count = x.shape[0]

    def put(at, value, span):
        fw[at] = (value.astype(F32) * mk[span[0] : span[1], :]).astype(BF16)

    for k in range(2):
        put(k, before[k], m.prev)
        put(2 + count + k, after[k], m.next)
    for k in range(count):
        put(2 + k, x[k], m.main)
    out = dot(taps_of(fw, frames, group), w7[...])
    for t in range(frames):
        y[t] = out[t * spots : (t + 1) * spots]
    s[...] = entry_sums(out, w7.shape[1] - LANES, frames, spots)


def slow_partial(m, frames, x, before, after, mk, wt, xm, fpart):
    spots, wide = x.shape[1], x.shape[2]
    sources = [(before, m.prev)] + [(x.at[t], m.main) for t in range(frames)] + [(after, m.next)]
    for k, (src, span) in enumerate(sources):
        for lo in range(0, wide, 256):
            mask = widen(mk[span[0] : span[1], :], 256)
            xm[k, :, lo : lo + 256] = (src[:, lo : lo + 256].astype(F32) * mask).astype(BF16)
    out = dot(flat(xm[0:frames]), wt[0, :wide, :])
    for j in range(1, 3):
        out = out + dot(flat(xm[j : j + frames]), wt[j, :wide, :])
    for t in range(frames):
        fpart[t] = out[t * spots : (t + 1) * spots]


def lat_join(m, n, frames, lat, st, y, before, after, fpart, wt, gs, bs, mk, jl, first, s, nl, jw):
    spots = y.shape[1]
    wide = wt.shape[1] - lat
    count = widen(mk[m.slow[0] : m.slow[0] + 1, :], lat)
    mean, rstd = norm_rows(st, 0, lat, count)
    nl[0:1, :] = mean
    nl[1:2, :] = rstd
    scale = rstd * gs[n : n + 1, 0:lat]
    bias = bs[n : n + 1, 0:lat]
    sources = (
        [(before[:, 0:lat], m.prev)]
        + [(y[t, :, 0:lat], m.main) for t in range(frames)]
        + [(after[:, 0:lat], m.next)]
    )
    for k, (value, span) in enumerate(sources):
        mask = widen(mk[span[0] : span[1], :], lat)
        act = (silu((value - mean) * scale + bias) * mask).astype(BF16)
        jw[k] = act
        if 1 <= k <= frames:
            jl[k - 1] = act
    out = flat(fpart[...])
    for j in range(3):
        out = out + dot(flat(jw[j : j + frames]), wt[j, wide:, :])
    one = jnp.zeros((8, out.shape[1]), F32)
    two = jnp.zeros((8, out.shape[1]), F32)
    for t in range(frames):
        part = out[t * spots : (t + 1) * spots]
        first[t] = part
        one = one + sublane_sums(part)
        two = two + sublane_sums(part * part)
    s[...] = jnp.concatenate([row_sum(one), row_sum(two)], axis=1)


def space_forward(
    m, n, frames, cols, lo, at, width, col0, packed, span, st, z, row, w, g, b, mk, aw, out, s, nz, vw
):
    spots = z.shape[1]
    count = widen(mk[span[0] : span[0] + 1, :], width)
    mean, rstd = norm_rows(st, at, width, count, packed)
    nz[0:1, :] = mean
    nz[1:2, :] = rstd
    scale = rstd * g[n : n + 1, lo : lo + width]
    bias = b[n : n + 1, lo : lo + width]
    mask = widen(mk[m.ext[0] : m.ext[1], :], width)
    for t in range(frames):
        value = jnp.concatenate([row[t], z[t, :, col0 : col0 + width], row[t]], axis=0)
        act = silu((value - mean) * scale + bias) * mask
        aw[t] = act.astype(BF16)
        store_shifts(vw, t, act, cols)
    total = dot(flat(vw[:, 0:spots, :]), w[0])
    for i in range(1, 3):
        total = total + dot(flat(vw[:, i * cols : i * cols + spots, :]), w[i])
    mask = widen(mk[m.main[0] : m.main[1], :], width)
    one = jnp.zeros((8, width), F32)
    two = jnp.zeros((8, width), F32)
    for t in range(frames):
        part = total[t * spots : (t + 1) * spots]
        out[t] = part
        part = part * mask
        one = one + sublane_sums(part)
        two = two + sublane_sums(part * part)
    s[...] = jnp.concatenate([row_sum(one), row_sum(two)], axis=1)


def slow_third(m, n, frames, lo, halo, st, z, *rest):
    if halo:
        before, after, wp, g, b, mk, a2, third, s, nz, aw = rest
    else:
        wp, g, b, mk, a2, third, s, nz, aw = rest
    spots, width = z.shape[1], z.shape[2]
    wide = wp.shape[1]
    count = widen(mk[m.slow[0] : m.slow[0] + 1, :], width)
    mean, rstd = norm_rows(st, 0, width, count)
    nz[0:1, :] = mean
    nz[1:2, :] = rstd
    scale = rstd * g[n : n + 1, lo : lo + width]
    bias = b[n : n + 1, lo : lo + width]
    sources = [(z[t], m.main, t + halo) for t in range(frames)]
    if halo:
        sources += [(before[...], m.prev, 0), (after[...], m.next, frames + 1)]
    for value, span, at in sources:
        mask = widen(mk[span[0] : span[1], :], width)
        act = (silu((value - mean) * scale + bias) * mask).astype(BF16)
        aw[at] = act
        if halo <= at < frames + halo:
            a2[at - halo] = act
    acts = flat(aw[...])
    ones, twos = [], []
    for at in range(0, wide, 256):
        out = dot(acts, wp[:, at : at + 256])
        one = jnp.zeros((8, 256), F32)
        two = jnp.zeros((8, 256), F32)
        for t in range(frames + 2 * halo):
            part = out[t * spots : (t + 1) * spots]
            third[t, :, at : at + 256] = part
            if halo <= t < frames + halo:
                one = one + sublane_sums(part)
                two = two + sublane_sums(part * part)
        ones.append(row_sum(one))
        twos.append(row_sum(two))
    s[...] = jnp.concatenate(ones + twos, axis=1)


def fast_third(m, n, frames, lo, at, st, z, wp, g, b, mk, a2, ft, s, nz):
    spots = z.shape[1]
    count = mk[m.fast[0] : m.fast[0] + 1, :]
    mean, rstd = norm_rows(st, at, LANES, count, True)
    nz[0:1, :] = mean
    nz[1:2, :] = rstd
    scale = rstd * g[n : n + 1, lo : lo + LANES]
    bias = b[n : n + 1, lo : lo + LANES]
    mask = mk[m.main[0] : m.main[1], :]
    for t in range(frames):
        a2[t] = (silu((z[t] - mean) * scale + bias) * mask).astype(BF16)
    acts = flat(a2[...])
    one = jnp.zeros((8, LANES), F32)
    two = jnp.zeros((8, LANES), F32)
    out = dot(acts, wp[...])
    for t in range(frames):
        for lane in range(0, wp.shape[1], LANES):
            part = out[t * spots : (t + 1) * spots, lane : lane + LANES]
            ft[t, :, lane : lane + LANES] = part
            one = one + sublane_sums(part)
            two = two + sublane_sums(part * part)
    s[...] = jnp.concatenate([row_sum(one), row_sum(two)], axis=1)


def fast_next(m, n, frames, group, lo, at, st, ft, before, after, fw0, w7, g, b, mk, f1, fw1, y, s, nz):
    spots = ft.shape[1]
    count = mk[m.fast[0] : m.fast[0] + 1, :]
    mean, rstd = norm_rows(st, at, LANES, count)
    nz[0:1, :] = mean
    nz[1:2, :] = rstd
    scale = rstd * g[n : n + 1, lo : lo + LANES]
    bias = b[n : n + 1, lo : lo + LANES]
    total = frames * group

    def out_of(k, value, span):
        z = fw0[k].astype(F32) + ((value - mean) * scale + bias)
        return silu(z) * mk[span[0] : span[1], :]

    for k in range(2):
        lane = k * LANES
        fw1[k] = out_of(k, before[:, lane : lane + LANES], m.prev).astype(BF16)
        fw1[2 + total + k] = out_of(2 + total + k, after[:, lane : lane + LANES], m.next).astype(BF16)
    for t in range(frames):
        for f in range(group):
            k = t * group + f
            value = out_of(2 + k, ft[t, :, f * LANES : (f + 1) * LANES], m.main)
            f1[k] = value
            fw1[2 + k] = value.astype(BF16)
    out = dot(taps_of(fw1, frames, group), w7[...])
    for t in range(frames):
        y[t] = out[t * spots : (t + 1) * spots]
    s[...] = entry_sums(out, w7.shape[1] - LANES, frames, spots)


def fast_last(m, n, frames, group, lo, at, st, ft, f1, cot, g, b, mk, out, pre, s, nz):
    count = mk[m.fast[0] : m.fast[0] + 1, :]
    mean, rstd = norm_rows(st, at, LANES, count)
    nz[0:1, :] = mean
    nz[1:2, :] = rstd
    gain = g[n : n + 1, lo : lo + LANES]
    bias = b[n : n + 1, lo : lo + LANES]
    mask = mk[m.main[0] : m.main[1], :]
    one = jnp.zeros((8, LANES), F32)
    two = jnp.zeros((8, LANES), F32)
    for t in range(frames):
        for f in range(group):
            k = t * group + f
            hat = (ft[t, :, f * LANES : (f + 1) * LANES] - mean) * rstd
            z = f1[k] + hat * gain + bias
            sigma = sigmoid(z)
            out[k] = z * sigma * mask
            grad = cot[k].astype(F32) * mask * (sigma * (1.0 + z * (1.0 - sigma)))
            pre[k] = grad
            one = one + sublane_sums(grad)
            two = two + sublane_sums(grad * hat)
    s[...] = jnp.concatenate([row_sum(one), row_sum(two)], axis=1)


def chunked(total, step, body, init):
    def turn(i, carry):
        return body(pl.multiple_of(i * step, step), carry)

    return lax.fori_loop(0, total // step, turn, init)


def slow_next(m, n, frames, lo, at0, st, third, xm, wt, g, b, mk, slow1, sw, fpart, nz):
    spots, wide = third.shape[1], third.shape[2]
    count = widen(mk[m.slow[0] : m.slow[0] + 1, :], wide)
    mean, rstd = norm_rows(st, at0, wide, count)
    nz[0:1, :] = mean
    nz[1:2, :] = rstd
    scale = rstd * g[n : n + 1, lo : lo + wide]
    bias = b[n : n + 1, lo : lo + wide]
    spans = [m.prev] + [m.main] * frames + [m.next]
    for k, span in enumerate(spans):

        def turn(at, carry, k=k, span=span):
            mask = widen(mk[pl.ds(span[0] + at, 16), :], 512)
            for c in range(0, wide, 512):
                z = third[k, pl.ds(at, 16), c : c + 512]
                z = (z - mean[:, c : c + 512]) * scale[:, c : c + 512] + bias[:, c : c + 512]
                z = xm[k, pl.ds(at, 16), c : c + 512].astype(F32) + z
                value = silu(z) * mask
                sw[k, pl.ds(at, 16), c : c + 512] = value.astype(BF16)
                if 1 <= k <= frames:
                    slow1[k - 1, pl.ds(at, 16), c : c + 512] = value
            return carry

        chunked(spots, 16, turn, 0)
    out = dot(flat(sw[0:frames]), wt[0, :wide, :])
    for j in range(1, 3):
        out = out + dot(flat(sw[j : j + frames]), wt[j, :wide, :])
    for t in range(frames):
        fpart[t] = out[t * spots : (t + 1) * spots]


def slow_last(m, n, frames, lo, st, third, slow1, cot, g, b, mk, out, pre, s, nz):
    spots, wide = third.shape[1], third.shape[2]
    count = widen(mk[m.slow[0] : m.slow[0] + 1, :], wide)
    mean, rstd = norm_rows(st, 0, wide, count)
    nz[0:1, :] = mean
    nz[1:2, :] = rstd
    gain = g[n : n + 1, lo : lo + wide]
    bias = b[n : n + 1, lo : lo + wide]
    carry = (jnp.zeros((8, wide), F32), jnp.zeros((8, wide), F32))
    for t in range(frames):

        def turn(at, sums, t=t):
            one, two = sums
            ones, twos = [], []
            mask = widen(mk[pl.ds(m.main[0] + at, 16), :], 512)
            for c in range(0, wide, 512):
                hat = (third[t, pl.ds(at, 16), c : c + 512] - mean[:, c : c + 512]) * rstd[:, c : c + 512]
                z = slow1[t, pl.ds(at, 16), c : c + 512] + hat * gain[:, c : c + 512] + bias[:, c : c + 512]
                sigma = sigmoid(z)
                out[t, pl.ds(at, 16), c : c + 512] = z * sigma * mask
                grad = cot[t, pl.ds(at, 16), c : c + 512].astype(F32) * mask
                grad = grad * (sigma * (1.0 + z * (1.0 - sigma)))
                pre[t, pl.ds(at, 16), c : c + 512] = grad
                ones.append(sublane_sums(grad))
                twos.append(sublane_sums(grad * hat))
            return one + jnp.concatenate(ones, axis=1), two + jnp.concatenate(twos, axis=1)

        carry = chunked(spots, 16, turn, carry)
    s[...] = jnp.concatenate([row_sum(carry[0]), row_sum(carry[1])], axis=1)


def slow_third_back(m, n, frames, lo3, lo2, at, halo, st, pre, third, n3, z, n2, wp, g, b, mk, d3, e2, s, gb):
    spots, wide = pre.shape[1], pre.shape[2]
    width = z.shape[2]
    count = widen(mk[m.slow[0] : m.slow[0] + 1, :], wide)
    one, two = totals(st, at, wide)
    gb[0:1, :] = one
    gb[1:2, :] = two
    mean, rstd = n3[0:1, :], n3[1:2, :]
    scale = g[n : n + 1, lo3 : lo3 + wide] * rstd
    one = one / count
    two = two / count * rstd
    for t in range(frames):

        def turn(i, carry, t=t):
            mask = widen(mk[pl.ds(m.main[0] + i, 16), :], 512)
            for c in range(0, wide, 512):
                hat = (third[t + halo, pl.ds(i, 16), c : c + 512] - mean[:, c : c + 512]) * two[:, c : c + 512]
                grad = pre[t, pl.ds(i, 16), c : c + 512] - mask * (one[:, c : c + 512] + hat)
                d3[t, pl.ds(i, 16), c : c + 512] = (scale[:, c : c + 512] * grad).astype(BF16)
            return carry

        chunked(spots, 16, turn, 0)
    out = dot_nt(flat(d3[...]), wp[...])
    mean, rstd = n2[0:1, :], n2[1:2, :]
    gain = g[n : n + 1, lo2 : lo2 + width]
    bias = b[n : n + 1, lo2 : lo2 + width]
    back_act(m, frames, spots, out, z, 0, mean, rstd, gain, bias, mk, e2, s)


def back_act(m, frames, spots, out, z, col0, mean, rstd, gain, bias, mk, e, s):
    width = out.shape[1]
    mask = widen(mk[m.main[0] : m.main[1], :], width)
    one = jnp.zeros((8, width), F32)
    two = jnp.zeros((8, width), F32)
    for t in range(frames):
        hat = (z[t, :, col0 : col0 + width] - mean) * rstd
        grad = out[t * spots : (t + 1) * spots] * mask * silu_slope(hat * gain + bias)
        e[t] = grad
        one = one + sublane_sums(grad)
        two = two + sublane_sums(grad * hat)
    s[...] = jnp.concatenate([row_sum(one), row_sum(two)], axis=1)


def fast_third_back(m, n, frames, group, lo3, lo2, at, st, pre, ft, n3, z, n2, wp, g, b, mk, d3, e2, s, gb):
    spots = z.shape[1]
    count = mk[m.fast[0] : m.fast[0] + 1, :]
    one, two = totals(st, at, LANES)
    gb[0:1, :] = one
    gb[1:2, :] = two
    mean, rstd = n3[0:1, :], n3[1:2, :]
    scale = g[n : n + 1, lo3 : lo3 + LANES] * rstd
    one = one / count
    two = two / count * rstd
    mask = mk[m.main[0] : m.main[1], :]
    for t in range(frames):
        for f in range(group):
            hat = (ft[t, :, f * LANES : (f + 1) * LANES] - mean) * two
            grad = pre[t * group + f] - mask * (one + hat)
            d3[t, :, f * LANES : (f + 1) * LANES] = (scale * grad).astype(BF16)
    out = dot_nt(flat(d3[...]), wp[...])
    mean, rstd = n2[0:1, :], n2[1:2, :]
    gain = g[n : n + 1, lo2 : lo2 + LANES]
    bias = b[n : n + 1, lo2 : lo2 + LANES]
    back_act(m, frames, spots, out, z, 0, mean, rstd, gain, bias, mk, e2, s)


def space_back(
    m, n, frames, cols, lo2, lo1, at, width, col0, packed, span,
    st, e, erow, z, zrow, nz, z1, n1, w, g, b, mk, d2, e1, s, gb, vw,
):
    spots = z.shape[1]
    count = widen(mk[span[0] : span[0] + 1, :], width)
    one, two = totals(st, at, width, packed)
    gb[0:1, :] = one
    gb[1:2, :] = two
    mean, rstd = nz[0:1, :], nz[1:2, :]
    scale = g[n : n + 1, lo2 : lo2 + width] * rstd
    one = one / count
    two = two / count * rstd
    mask = widen(mk[m.ext[0] : m.ext[1], :], width)
    for t in range(frames):
        grad = jnp.concatenate([erow[t], e[t], erow[t]], axis=0)
        value = jnp.concatenate([zrow[t], z[t], zrow[t]], axis=0)
        grad = scale * mask * (grad - (one + (value - mean) * two))
        d2[t] = grad[cols : cols + spots].astype(BF16)
        store_shifts(vw, t, grad.astype(BF16).astype(F32), cols)
    total = None
    for i in range(3):
        rows = (2 - i) * cols
        for j in range(3):
            lane = (2 - j) * width
            part = dot_nt(flat(vw[:, rows : rows + spots, lane : lane + width]), w[i, j * width : (j + 1) * width, :])
            total = part if total is None else total + part
    mean, rstd = n1[0:1, :], n1[1:2, :]
    gain = g[n : n + 1, lo1 : lo1 + width]
    bias = b[n : n + 1, lo1 : lo1 + width]
    back_act(m, frames, spots, total, z1, col0, mean, rstd, gain, bias, mk, e1, s)


def slow_first_back(m, n, frames, lo1, lo3, at, halo, last, st, *rest):
    if last:
        e, ep, en, z, zp, zn, n1, wt, y, nl, pre, g, b, mk, dw, el, s, gx, gb = rest
    else:
        e, ep, en, z, zp, zn, n1, wt, y, nl, pre, xm, third, n3, g, b, mk, dw, el, s, pre0, s3, gb = rest
    spots, width = z.shape[1], z.shape[2]
    lat = nl.shape[1]
    wide = wt.shape[1] - lat
    count = widen(mk[m.slow[0] : m.slow[0] + 1, :], width)
    one, two = totals(st, at, width)
    gb[0:1, :] = one
    gb[1:2, :] = two
    mean, rstd = n1[0:1, :], n1[1:2, :]
    scale = g[n : n + 1, lo1 : lo1 + width] * rstd
    one = one / count
    two = two / count * rstd
    sources = (
        [(ep, zp, m.prev)] + [(e.at[t], z.at[t], m.main) for t in range(frames)] + [(en, zn, m.next)]
    )
    for k, (grad, value, span) in enumerate(sources):
        mask = widen(mk[span[0] : span[1], :], width)
        dw[k] = (scale * mask * (grad[...] - (one + (value[...] - mean) * two))).astype(BF16)
    taps = [flat(dw[2 - j : 2 - j + frames]) for j in range(3)]

    def back(lo, size):
        out = dot_nt(taps[0], wt[0, lo : lo + size, :])
        for j in range(1, 3):
            out = out + dot_nt(taps[j], wt[j, lo : lo + size, :])
        return out

    out = back(wide, lat)
    back_act(
        m, frames, spots, out, y, 0, nl[0:1, :], nl[1:2, :], g[n : n + 1, 0:lat], b[n : n + 1, 0:lat], mk, el, s
    )
    mask = widen(mk[m.main[0] : m.main[1], :], 256)
    ones, twos = [], []
    for c in range(0, wide, 256):
        out = back(c, 256)
        if not last:
            mean, rstd = n3[0:1, c : c + 256], n3[1:2, c : c + 256]
            gain = g[n - 1 : n, lo3 + c : lo3 + c + 256]
            bias = b[n - 1 : n, lo3 + c : lo3 + c + 256]
            one = jnp.zeros((8, 256), F32)
            two = jnp.zeros((8, 256), F32)
        for t in range(frames):
            grad = (out[t * spots : (t + 1) * spots] + pre[t, :, c : c + 256]) * mask
            if last:
                gx[t, :, c : c + 256] = grad
            else:
                hat = (third[t + halo, :, c : c + 256] - mean) * rstd
                z0 = xm[t + 1, :, c : c + 256].astype(F32) + hat * gain + bias
                grad = grad * silu_slope(z0)
                pre0[t, :, c : c + 256] = grad
                one = one + sublane_sums(grad)
                two = two + sublane_sums(grad * hat)
        if not last:
            ones.append(row_sum(one))
            twos.append(row_sum(two))
    if not last:
        s3[...] = jnp.concatenate(ones + twos, axis=1)


def fast_first_back(m, n, frames, group, lo1, lo3, at1, atl, last, st1, stl, *rest):
    if last:
        el, eln, ef, efp, efn, y, yp, yn, nl, n1, w7, pre, gs, g, b, mk, dl, dfw, gx, gbl, gb1, buf = rest
    else:
        (el, eln, ef, efp, efn, y, yp, yn, nl, n1, w7, pre, fw0, ft, n3, gs, g, b, mk,
         dl, dfw, pre0, s, gbl, gb1, buf) = rest
    spots = y.shape[1]
    lat = nl.shape[1]
    count = widen(mk[m.slow[0] : m.slow[0] + 1, :], lat)
    one, two = totals(stl, atl, lat)
    gbl[0:1, :] = one
    gbl[1:2, :] = two
    mean, rstd = nl[0:1, :], nl[1:2, :]
    scale = gs[n : n + 1, 0:lat] * rstd
    one = one / count
    two = two / count * rstd

    def lat_grad(grad, value, span):
        mask = widen(mk[span[0] : span[1], :], lat)
        return (scale * mask * (grad - (one + (value - mean) * two))).astype(BF16)

    for t in range(frames):
        dl[t] = lat_grad(el[t], y[t, :, 0:lat], m.main)
    dl_next = lat_grad(eln[...], yn[:, 0:lat], m.next)
    fcount = mk[m.fast[0] : m.fast[0] + 1, :]
    fone, ftwo = totals(st1, at1, LANES, True)
    gb1[0:1, :] = fone
    gb1[1:2, :] = ftwo
    fmean, frstd = n1[0:1, :], n1[1:2, :]
    fscale = g[n : n + 1, lo1 : lo1 + LANES] * frstd
    fone = fone / fcount
    ftwo = ftwo / fcount * frstd

    def first_grad(grad, value, span):
        mask = mk[span[0] : span[1], :]
        return (fscale * mask * (grad - (fone + (value - fmean) * ftwo))).astype(BF16)

    for t in range(frames):
        dfw[t] = first_grad(ef[t], y[t, :, lat:], m.main)
    df_prev = first_grad(efp[...], yp[:, lat:], m.prev)
    df_next = first_grad(efn[...], yn[:, lat:], m.next)
    both = jnp.concatenate([flat(dl[...]), flat(dfw[...])], axis=1)
    buf[...] = jnp.zeros(buf.shape, F32)
    out = dot_nt(both, w7[...])
    for t in range(frames):
        for f in range(7):
            k = group * t + f
            buf[k] = buf[k] + out[t * spots : (t + 1) * spots, f * LANES : (f + 1) * LANES]
    buf[2] = buf[2] + dot_nt(df_prev, w7[6 * LANES : 7 * LANES, lat:])
    after = dot_nt(jnp.concatenate([dl_next, df_next], axis=1), w7[0 : 2 * LANES, :])
    total = frames * group
    for f in range(2):
        buf[total + f] = buf[total + f] + after[:, f * LANES : (f + 1) * LANES]
    mask = mk[m.main[0] : m.main[1], :]
    if last:
        for k in range(total):
            gx[k] = (pre[k] + buf[2 + k]) * mask
        return
    mean, rstd = n3[0:1, :], n3[1:2, :]
    gain = g[n - 1 : n, lo3 : lo3 + LANES]
    bias = b[n - 1 : n, lo3 : lo3 + LANES]
    one = jnp.zeros((8, LANES), F32)
    two = jnp.zeros((8, LANES), F32)
    for k in range(total):
        t, f = k // group, k % group
        hat = (ft[t, :, f * LANES : (f + 1) * LANES] - mean) * rstd
        z0 = fw0[2 + k].astype(F32) + hat * gain + bias
        grad = (pre[k] + buf[2 + k]) * mask * silu_slope(z0)
        pre0[k] = grad
        one = one + sublane_sums(grad)
        two = two + sublane_sums(grad * hat)
    s[...] = jnp.concatenate([row_sum(one), row_sum(two)], axis=1)


def point_weights(a2, d3, out):
    acts = flat(a2[...])
    for k in range(out.shape[0]):
        out[k] = dot_tn(acts, flat(d3[:, :, k * 256 : (k + 1) * 256])).astype(BF16)


def space_weights(cols, aw, d2, out, vw):
    frames, spots, width = d2.shape
    for t in range(frames):
        store_shifts(vw, t, aw[t].astype(F32), cols)
    grads = flat(d2[...])
    for i in range(3):
        out[i] = dot_tn(flat(vw[:, i * cols : i * cols + spots, :]), grads).astype(BF16)


def time_weights(skip, slow, jl, dw, out):
    frames, spots, width = jl.shape
    wide = slow.shape[2]
    grads = jnp.concatenate([flat(dw[2 - j : 2 - j + frames]) for j in range(3)], axis=1)
    for c in range(0, wide + jl.shape[2], 256):
        if c < wide:
            acts = flat(slow[skip : skip + frames, :, c : c + 256])
        else:
            acts = flat(jl[:, :, c - wide : c - wide + 256])
        got = dot_tn(acts, grads)
        for j in range(3):
            out[j, c : c + 256, :] = got[:, j * width : (j + 1) * width].astype(BF16)


def group_blocks(value, group):
    size = LANES // group
    rows = lax.broadcasted_iota(jnp.int32, (LANES, LANES), 0) >> (size.bit_length() - 1)
    lanes = lax.broadcasted_iota(jnp.int32, (LANES, LANES), 1) >> (size.bit_length() - 1)
    kept = jnp.where(rows == lanes, value, 0.0)
    kept = kept + pltpu.roll(kept, 64, 1)
    kept = kept + pltpu.roll(kept, 32, 1)
    total = kept[0:size]
    for k in range(1, group):
        total = total + kept[k * size : (k + 1) * size]
    return total


def at_lanes(blocks):
    lanes = lax.broadcasted_iota(jnp.int32, blocks[0].shape, 1) >> 5
    out = jnp.zeros(blocks[0].shape, F32)
    for k, block in enumerate(blocks):
        out = jnp.where(lanes == k, block, out)
    return out


def fast_weights(group, cols, lat, fw, dl, df, fa1, d2, fa2, d3, out, vw):
    frames, spots, _ = dl.shape
    size = LANES // group
    both = jnp.concatenate([flat(dl[...]), flat(df[...])], axis=1)
    taps = [[None] * group for _ in range(3)]
    for f in range(7):
        acts = jnp.concatenate([fw[group * t + f] for t in range(frames)], axis=0)
        got = dot_tn(acts, both)
        if f < 5:
            out[f * LANES : (f + 1) * LANES, :] = got[:, :lat].astype(BF16)
        for k in range(group):
            if 0 <= f - k - 1 < 3:
                taps[f - k - 1][k] = got[:, lat:]
    lanes = lax.broadcasted_iota(jnp.int32, (LANES, LANES), 1) >> (size.bit_length() - 1)
    tap_sums = []
    for j in range(3):
        kept = jnp.zeros((LANES, LANES), F32)
        for k in range(group):
            kept = jnp.where(lanes == k, taps[j][k], kept)
        kept = kept + pltpu.roll(kept, 64, 1)
        tap_sums.append(kept + pltpu.roll(kept, 32, 1))
    low = 5 * LANES
    out[low : low + LANES, 0:LANES] = at_lanes(tap_sums).T.astype(BF16)
    for t in range(frames):
        store_shifts(vw, t, fa1[t].astype(F32), cols)
    grads = flat(d2[...])
    for i in range(3):
        got = dot_tn(flat(vw[:, i * cols : i * cols + spots, :]), grads)
        blocks = [group_blocks(got[j * LANES : (j + 1) * LANES], group) for j in range(3)]
        out[low + size * i : low + size * (i + 1), LANES : 2 * LANES] = at_lanes(blocks).astype(BF16)
    acts = flat(fa2[...])
    total = jnp.zeros((size, LANES), F32)
    for k in range(group):
        got = dot_tn(acts, flat(d3[:, :, k * LANES : (k + 1) * LANES]))
        total = total + got[k * size : (k + 1) * size]
    out[low + 3 * size : low + 4 * size, LANES : 2 * LANES] = total.astype(BF16)


def unpack_fast(n, inner, load, outs):
    glat, gft, gfs, gfp = outs
    low = glat.shape[1]
    for at in range(0, low, inner):
        glat[n, at : at + inner, :] = load(at, inner)
    for i in range(4):
        got = load(low + inner * i, inner)
        if i < 3:
            gft[n, i] = got[:, 0:LANES]
            for j in range(3):
                moved = got[:, LANES:] if j == 0 else pltpu.roll(got[:, LANES:], LANES - inner * j, 1)
                gfs[n, 3 * i + j] = moved[:, 0:inner]
        else:
            gfp[n] = got[:, LANES:]


def rows_of(ref):
    def load(at, count):
        block, row = at // ref.shape[1], at % ref.shape[1]
        assert row + count <= ref.shape[1]
        return ref[block, row : row + count, :].astype(F32)

    return load


def assemble_time(step, one, zero, out):
    load = rows_of(zero)
    for at in range(0, out.shape[1], step):
        out[0, at : at + step, :] = load(at, step)
        out[1, at : at + step, :] = one[at : at + step, :].astype(F32)


def assemble_space(start, space1, zero, out):
    load = rows_of(zero)
    for at in range(0, out.shape[1], 256):
        out[0, at : at + 256, :] = load(start + at, 256)
        out[1, at : at + 256, :] = space1[at : at + 256, :].astype(F32)


def assemble_point(start, point1, zero, out):
    load = rows_of(zero)
    for at in range(0, out.shape[2], 256):
        out[0, :, at : at + 256] = load(start + at, 256)
        out[1, :, at : at + 256] = point1[at : at + 256, :].astype(F32)


def assemble_fast(inner, one, zero, *outs):
    unpack_fast(1, inner, rows_of(one), outs)
    unpack_fast(0, inner, rows_of(zero), outs)


def assemble_norms(inner, *refs):
    sums, (gs, bs, gf, bf) = refs[:-4], refs[-4:]
    lanes = lax.broadcasted_iota(jnp.int32, (8, LANES), 1) >> (inner.bit_length() - 1)
    for n in range(2):
        slow, fast = sums[7 * n : 7 * n + 4], sums[7 * n + 4 : 7 * n + 7]
        for row, gslow, gfast in ((1, gs, gf), (0, bs, bf)):
            at = 0
            for part in slow:
                gslow[n : n + 1, at : at + part.shape[1]] = part[row : row + 1, :]
                at += part.shape[1]
            one, two, three = [jnp.broadcast_to(part[row : row + 1, :], (8, LANES)) for part in fast]
            three = pltpu.roll(three, 2 * inner, 1)
            head = jnp.where(lanes == 0, one, jnp.where(lanes == 1, two, three))
            gfast[n : n + 1, 0:LANES] = head[0:1]
            gfast[n : n + 1, LANES : LANES + 2 * inner] = three[0:1, 0 : 2 * inner]


def on_device(
    x_slow,
    x_fast,
    w_lateral,
    w_slow_time,
    w_slow_space,
    w_slow_point,
    w_fast_time,
    w_fast_space,
    w_fast_point,
    gain_slow,
    bias_slow,
    gain_fast,
    bias_fast,
    clip_size,
    cot_slow,
    cot_fast,
):
    frames, fast_frames = x_slow.shape[0], x_fast.shape[0]
    group = fast_frames // frames
    rows, cols = x_slow.shape[3], x_slow.shape[4]
    spots = rows * cols
    wide, fwide = x_slow.shape[5], x_fast.shape[5]
    lat = w_lateral.shape[3]
    width = w_slow_space.shape[3]
    inner = w_fast_space.shape[3]
    packs = group * fwide
    both = lat + LANES
    m = Masks(spots, cols)
    devices = lax.axis_size("path") * lax.axis_size("rows")
    path = lax.axis_index("path")
    ext = spots + 2 * cols
    lo1, lo2, lo3 = lat, lat + width, lat + 2 * width
    every = slice(None)

    def part(fn, *static):
        return functools.partial(fn, *static)

    xs = x_slow.reshape(frames, spots, wide)
    xf = x_fast.reshape(fast_frames, spots, fwide)
    cs = cot_slow.reshape(frames, spots, wide)
    cf = cot_fast.reshape(fast_frames, spots, fwide)
    wft = jnp.swapaxes(w_fast_time, 2, 3)
    wfs_raw = w_fast_space.reshape(2, 9, inner, inner)
    wsp = w_slow_space.reshape(2, 3, 3 * width, width)

    def packed(value):
        return jnp.concatenate(
            [value[:, 0:inner]] * group + [value[:, inner : 2 * inner]] * group + [value[:, 2 * inner :]],
            axis=1,
        )

    gf, bf = packed(gain_fast), packed(bias_fast)

    xf_edge = swap_path(jnp.where(path > 0, xf[:2], xf[-2:]))
    xs_edge = swap_path(jnp.where(path > 0, xs[0], xs[-1]))

    def payload(k, *sums):
        size = sum(k.temps[s[1]].shape[1] for s in sums)
        out = k.give((devices, 1, size))
        k.step(spread_sums, *sums, out)
        return out

    def row_out(k, z, mk, col0, size):
        out = k.give((frames, cols, size))
        k.step(part(own_row, m, spots, cols, col0, size), z, mk, out)
        return out

    def edge_out(k, z, mk, size, tail=0):
        out = k.give((spots, size))
        k.step(part(own_edge, m, 0, tail), z, mk, out)
        return out

    def finish(k, **handles):
        got = k.run()
        return {name: got[handle[1]] for name, handle in handles.items()}

    def other_row(value):
        return swap(value, "rows", 1)

    first_flops = 2 * frames * spots * 7 * fwide * both
    k = Stage("entry")
    mk_out = k.give((m.rows, LANES))
    place = jnp.stack([lax.axis_index("rows"), path]).astype(jnp.int32)
    k.step(
        part(make_masks, m, rows, cols, lax.axis_size("path") - 1), k.scalar(place), k.scalar(clip_size), mk_out
    )
    w7_out = k.give((7 * fwide, both), BF16)
    k.step(part(make_w7, lat, group), k.take(w_lateral, 0), k.take(wft, 0), w7_out)
    fw = k.give((fast_frames + 4, spots, fwide), BF16)
    y = k.give((frames, spots, both))
    sy = k.temp((1, 2 * both))
    edge = k.near(xf_edge)
    k.step(
        part(fast_entry, m, frames, group), k.take(xf), edge, edge, mk_out, w7_out, fw, y, sy, flops=first_flops
    )
    pay = payload(k, sy)
    got = finish(
        k, mk=mk_out, w7=w7_out, fw=fw, y=y, pay=pay, ff_row=row_out(k, y, mk_out, lat, LANES),
        edge=edge_out(k, y, mk_out, both),
    )
    mk = got["mk"]
    saved = [{"fw": got["fw"], "y": got["y"], "w7": got["w7"]}, {}]
    st = gather_sums(got["pay"])
    saved[0]["ff_row"] = other_row(got["ff_row"])
    saved[0]["y_edge"] = swap_path(got["edge"])
    k = Stage("prepare")
    w7_out = k.give((7 * fwide, both), BF16)
    k.step(part(make_w7, lat, group), k.take(w_lateral, 1), k.take(wft, 1), w7_out)
    blocks = []
    for n in range(2):
        blocks += [k.give((3, 3 * LANES, LANES), BF16), k.give((LANES, packs), BF16)]
        k.step(part(make_blocks, group), k.take(wfs_raw, n), k.take(w_fast_point, n), *blocks[-2:])
    got = finish(k, w7=w7_out, wfs0=blocks[0], wfp0=blocks[1], wfs1=blocks[2], wfp1=blocks[3])
    saved[1]["w7"] = got["w7"]
    wfs, wfp = [got["wfs0"], got["wfs1"]], [got["wfp0"], got["wfp1"]]
    k = Stage("slow_partial")
    xm = k.give((frames + 2, spots, wide), BF16)
    fpart = k.give((frames, spots, width))
    edge = k.near(xs_edge)
    k.step(
        part(slow_partial, m, frames),
        k.take(xs), edge, edge, k.take(mk), k.take(w_slow_time, 0, every, slice(0, wide)), xm, fpart,
        flops=2 * frames * spots * 3 * wide * width,
    )
    got = finish(k, sw=xm, fpart=fpart)
    saved[0]["sw"] = got["sw"]
    fpart_in = got["fpart"]

    for n in range(2):
        v = saved[n]
        k = Stage("join")
        mk_in, gs, bs = k.take(mk), k.take(gain_slow), k.take(bias_slow)
        st_in = k.near(st)
        names = {}
        if n == 0:
            fpart = k.take(fpart_in)
        else:
            fpart = k.temp((frames, spots, width))
            names.update(
                slow1=k.give((frames, spots, wide)),
                sw=k.give((frames + 2, spots, wide), BF16),
            )
            n3 = k.give((2, wide))
            k.step(
                part(slow_next, m, 0, frames, lo3, 2 * both),
                st_in, k.take(saved[0]["third"]), k.take(saved[0]["sw"]),
                k.take(w_slow_time, 1, every, slice(0, wide)), gs, bs, mk_in,
                names["slow1"], names["sw"], fpart, n3,
                flops=2 * frames * spots * 3 * wide * width,
            )
            names["n3"] = n3
        y_in, edge = k.take(v["y"]), k.near(v["y_edge"])
        jl = k.give((frames, spots, lat), BF16)
        first = k.give((frames, spots, width))
        nl = k.give((2, lat))
        s_first, s_fs = k.temp((1, 2 * width)), k.temp((1, 2 * LANES))
        k.step(
            part(lat_join, m, n, frames, lat),
            st_in, y_in, edge, edge, fpart, k.take(w_slow_time, n, every, slice(wide, wide + lat)), gs, bs, mk_in,
            jl, first, s_first, nl, k.temp((frames + 2, spots, lat), BF16),
            flops=2 * frames * spots * 3 * lat * width,
        )
        fa1 = k.give((frames, ext, LANES), BF16)
        fs = k.give((frames, spots, LANES))
        nf1 = k.give((2, LANES))
        k.step(
            part(space_forward, m, n, frames, cols, 0, 2 * lat, LANES, lat, True, m.fast),
            st_in, y_in, k.near(v["ff_row"]), k.take(wfs[n]), k.take(gf), k.take(bf), mk_in,
            fa1, fs, s_fs, nf1, k.temp((frames, ext, 3 * LANES), BF16),
            flops=2 * frames * spots * 9 * LANES * LANES,
        )
        pay = payload(k, s_first, s_fs)
        got = finish(
            k, jl=jl, first=first, nl=nl, fa1=fa1, fs=fs, nf1=nf1, pay=pay,
            first_row=row_out(k, first, mk_in, 0, width), fs_row=row_out(k, fs, mk_in, 0, LANES),
            first_edge=edge_out(k, first, mk_in, width), **names,
        )
        st = gather_sums(got["pay"])
        for name in ("jl", "first", "nl", "fa1", "fs", "nf1"):
            v[name] = got[name]
        if n == 1:
            slow1, saved[1]["sw"], saved[0]["n3"] = got["slow1"], got["sw"], got["n3"]
        first_row = other_row(got["first_row"])
        v["fs_row"] = other_row(got["fs_row"])
        v["first_edge"] = swap_path(got["first_edge"])
        k = Stage("space")
        mk_in, st_in = k.take(mk), k.near(st)
        a1 = k.give((frames, ext, width), BF16)
        second = k.give((frames, spots, width))
        n1 = k.give((2, width))
        s_second, s_ft = k.temp((1, 2 * width)), k.temp((1, 2 * LANES))
        k.step(
            part(space_forward, m, n, frames, cols, lo1, 0, width, 0, False, m.slow),
            st_in, k.take(v["first"]), k.near(first_row), k.take(wsp, n), k.take(gain_slow), k.take(bias_slow), mk_in,
            a1, second, s_second, n1, k.temp((frames, ext, 3 * width), BF16),
            flops=2 * frames * spots * 9 * width * width,
        )
        fa2 = k.give((frames, spots, LANES), BF16)
        ft = k.give((frames, spots, packs))
        nf2 = k.give((2, LANES))
        k.step(
            part(fast_third, m, n, frames, LANES, 2 * width),
            st_in, k.take(v["fs"]), k.take(wfp[n]), k.take(gf), k.take(bf), mk_in, fa2, ft, s_ft, nf2,
            flops=2 * frames * spots * LANES * packs,
        )
        pay = payload(k, s_second, s_ft)
        names = {"second_row": row_out(k, second, mk_in, 0, width)}
        if n == 0:
            names["second_edge"] = edge_out(k, second, mk_in, width)
            names["ft_edge"] = edge_out(k, ft, mk_in, 2 * fwide, (group - 2) * fwide)
        got = finish(k, a1=a1, second=second, n1=n1, fa2=fa2, ft=ft, nf2=nf2, pay=pay, **names)
        st = gather_sums(got["pay"])
        for name in ("a1", "second", "n1", "fa2", "ft", "nf2"):
            v[name] = got[name]
        v["second_row"] = other_row(got["second_row"])
        halo = 1 - n
        edges = []
        k = Stage("third")
        if n == 0:
            ft_edge = k.near(swap_path(got["ft_edge"]))
            edges = [k.near(swap_path(got["second_edge"]))] * 2
        mk_in, st_in = k.take(mk), k.near(st)
        a2 = k.give((frames, spots, width), BF16)
        third = k.give((frames + 2 * halo, spots, wide))
        n2 = k.give((2, width))
        nf3 = k.give((2, LANES))
        s_third = k.temp((1, 2 * wide))
        names = {}
        if n == 0:
            names.update(
                f1=k.give((fast_frames, spots, fwide)),
                fw=k.give((fast_frames + 4, spots, fwide), BF16),
                y=k.give((frames, spots, both)),
            )
            s_fast = k.temp((1, 2 * both))
            k.step(
                part(fast_next, m, n, frames, group, 2 * LANES, 2 * width),
                st_in, k.take(v["ft"]), ft_edge, ft_edge, k.take(v["fw"]), k.take(saved[1]["w7"]),
                k.take(gf), k.take(bf), mk_in, names["f1"], names["fw"], names["y"], s_fast, nf3,
                flops=first_flops,
            )
        else:
            names.update(out_fast=k.give((fast_frames, spots, fwide)), pre_f=k.give((fast_frames, spots, fwide)))
            s_fast = k.temp((1, 2 * LANES))
            k.step(
                part(fast_last, m, n, frames, group, 2 * LANES, 2 * width),
                st_in, k.take(v["ft"]), k.take(fast1), k.take(cf), k.take(gf), k.take(bf), mk_in,
                names["out_fast"], names["pre_f"], s_fast, nf3,
            )
        k.step(
            part(slow_third, m, n, frames, lo2, halo),
            st_in, k.take(v["second"]), *edges, k.take(w_slow_point, n), k.take(gain_slow), k.take(bias_slow), mk_in,
            a2, third, s_third, n2, k.temp((frames + 2 * halo, spots, width), BF16),
            flops=2 * frames * spots * width * wide,
        )
        if n == 0:
            pay = payload(k, s_fast, s_third)
            names["ff_row"] = row_out(k, names["y"], mk_in, lat, LANES)
            names["y_edge"] = edge_out(k, names["y"], mk_in, both)
        else:
            pay = payload(k, s_third, s_fast)
        got = finish(k, a2=a2, third=third, n2=n2, nf3=nf3, pay=pay, **names)
        st = gather_sums(got["pay"])
        for name in ("a2", "third", "n2", "nf3"):
            v[name] = got[name]
        if n == 0:
            fast1 = got["f1"]
            saved[1].update(
                fw=got["fw"], y=got["y"], ff_row=other_row(got["ff_row"]), y_edge=swap_path(got["y_edge"])
            )
        else:
            out_fast, pre_f = got["out_fast"], got["pre_f"]

    def third_back(k, n, at, st_in, mk_in, pre):
        v = saved[n]
        d3, e2 = k.give((frames, spots, wide), BF16), k.give((frames, spots, width))
        s, gb = k.temp((1, 2 * width)), k.give((2, wide))
        k.step(
            part(slow_third_back, m, n, frames, lo3, lo2, at, 1 - n),
            st_in, k.take(pre), k.take(v["third"]), k.take(v["n3"]), k.take(v["second"]), k.take(v["n2"]),
            k.take(w_slow_point, n), k.take(gain_slow), k.take(bias_slow), mk_in, d3, e2, s, gb,
            flops=2 * frames * spots * width * wide,
        )
        return dict(d3=d3, e2=e2, gb3=gb), s

    def fast_back3(k, n, at, st_in, mk_in, pre):
        v = saved[n]
        d3, e2 = k.give((frames, spots, packs), BF16), k.give((frames, spots, LANES))
        s, gb = k.temp((1, 2 * LANES)), k.give((2, LANES))
        k.step(
            part(fast_third_back, m, n, frames, group, 2 * LANES, LANES, at),
            st_in, k.take(pre), k.take(v["ft"]), k.take(v["nf3"]), k.take(v["fs"]), k.take(v["nf2"]),
            k.take(wfp[n]), k.take(gf), k.take(bf), mk_in, d3, e2, s, gb,
            flops=2 * frames * spots * LANES * packs,
        )
        return dict(d3f=d3, ef2=e2, gbf3=gb), s

    def second_back(k, n, at, st_in, mk_in, e2, e2_row):
        v = saved[n]
        d2, e1 = k.give((frames, spots, width), BF16), k.give((frames, spots, width))
        s, gb = k.temp((1, 2 * width)), k.give((2, width))
        k.step(
            part(space_back, m, n, frames, cols, lo2, lo1, at, width, 0, False, m.slow),
            st_in, k.take(e2), k.near(e2_row), k.take(v["second"]), k.take(v["second_row"]), k.take(v["n2"]),
            k.take(v["first"]), k.take(v["n1"]), k.take(wsp, n), k.take(gain_slow), k.take(bias_slow), mk_in,
            d2, e1, s, gb, k.temp((frames, ext, 3 * width), BF16),
            flops=2 * frames * spots * 9 * width * width,
        )
        return dict(d2=d2, e1=e1, gb2=gb), s

    def fast_back2(k, n, at, st_in, mk_in, ef2, ef2_row):
        v = saved[n]
        d2, e1 = k.give((frames, spots, LANES), BF16), k.give((frames, spots, LANES))
        s, gb = k.temp((1, 2 * LANES)), k.give((2, LANES))
        k.step(
            part(space_back, m, n, frames, cols, LANES, 0, at, LANES, lat, True, m.fast),
            st_in, k.take(ef2), k.near(ef2_row), k.take(v["fs"]), k.take(v["fs_row"]), k.take(v["nf2"]),
            k.take(v["y"]), k.take(v["nf1"]), k.take(wfs[n]), k.take(gf), k.take(bf), mk_in,
            d2, e1, s, gb, k.temp((frames, ext, 3 * LANES), BF16),
            flops=2 * frames * spots * 9 * LANES * LANES,
        )
        return dict(d2f=d2, ef1=e1, gbf2=gb), s

    def first_back(k, n, st_in, mk_in, e1, e1_edge, pre):
        v = saved[n]
        last = n == 0
        dw, el = k.give((frames + 2, spots, width), BF16), k.give((frames, spots, lat))
        s, gb = k.temp((1, 2 * lat)), k.give((2, width))
        down = k.give((frames, spots, wide))
        edge, zedge = k.near(e1_edge), k.take(v["first_edge"])
        args = [
            st_in, k.take(e1), edge, edge, k.take(v["first"]), zedge, zedge, k.take(v["n1"]),
            k.take(w_slow_time, n), k.take(v["y"]), k.take(v["nl"]), k.take(pre),
        ]
        outs = [dw, el, s, down]
        sums = [s]
        if not last:
            args += [k.take(saved[0]["sw"]), k.take(saved[0]["third"]), k.take(saved[0]["n3"])]
            sums.append(k.temp((1, 2 * wide)))
            outs.append(sums[1])
        k.step(
            part(slow_first_back, m, n, frames, lo1, lo3, 0, 1, last),
            *args, k.take(gain_slow), k.take(bias_slow), mk_in, *outs, gb,
            flops=2 * frames * spots * 3 * (wide + lat) * width,
        )
        return dict(dw=dw, el=el, down=down, gb1=gb), sums

    def fast_back1(k, n, st1, at1, stl, atl, mk_in, el, el_edge, ef1, ef1_edge, pre):
        v = saved[n]
        last = n == 0
        dl, df = k.give((frames, spots, lat), BF16), k.give((frames, spots, LANES), BF16)
        down = k.give((fast_frames, spots, fwide))
        gbl, gb1 = k.give((2, lat)), k.give((2, LANES))
        edge, yedge = k.take(ef1_edge), k.take(v["y_edge"])
        args = [
            st1, stl, k.take(el), k.near(el_edge), k.take(ef1), edge, edge, k.take(v["y"]), yedge, yedge,
            k.take(v["nl"]), k.take(v["nf1"]), k.take(v["w7"]), k.take(pre),
        ]
        outs = [dl, df, down]
        s = None
        if not last:
            args += [k.take(saved[0]["fw"]), k.take(saved[0]["ft"]), k.take(saved[0]["nf3"])]
            s = k.temp((1, 2 * LANES))
            outs.append(s)
        k.step(
            part(fast_first_back, m, n, frames, group, 0, 2 * LANES, at1, atl, last),
            *args, k.take(gain_slow), k.take(gf), k.take(bf), mk_in, *outs, gbl, gb1,
            k.temp((fast_frames + 4, spots, fwide)),
            flops=first_flops,
        )
        return dict(dl=dl, df=df, downf=down, gbl=gbl, gbf1=gb1), s

    def weights_point(n, d3):
        k = Stage("point_weights")
        out = k.give((wide // 256, width, 256), BF16)
        k.step(point_weights, k.take(saved[n]["a2"]), k.take(d3), out, flops=2 * frames * spots * width * wide)
        return k.run()[0].reshape(-1, 256)

    def weights_space(n, d2):
        k = Stage("space_weights")
        out = k.give((3, 3 * width, width), BF16)
        k.step(
            part(space_weights, cols), k.take(saved[n]["a1"]), k.take(d2), out,
            k.temp((frames, ext, 3 * width), BF16), flops=2 * frames * spots * 9 * width * width,
        )
        return k.run()[0].reshape(-1, 256)

    def weights_time(n, dw):
        k = Stage("time_weights")
        out = k.give((3, wide + lat, width), BF16)
        k.step(
            part(time_weights, 1), k.take(saved[n]["sw"]), k.take(saved[n]["jl"]), k.take(dw), out,
            flops=2 * frames * spots * 3 * (wide + lat) * width,
        )
        return k.run()[0].reshape(-1, 256)

    def weights_fast(n, dl, df, d2, d3):
        v = saved[n]
        k = Stage("fast_weights")
        out = k.give((7 * LANES - LANES, 2 * LANES), BF16)
        k.step(
            part(fast_weights, group, cols, lat),
            k.take(v["fw"]), k.take(dl), k.take(df), k.take(v["fa1"]), k.take(d2), k.take(v["fa2"]), k.take(d3),
            out, k.temp((frames, ext, 3 * LANES), BF16), flops=first_flops,
        )
        return k.run()[0]

    b1, b0 = {}, {}
    k = Stage("last")
    mk_in, st_in = k.take(mk), k.near(st)
    out_slow, pre = k.give((frames, spots, wide)), k.give((frames, spots, wide))
    n3 = k.give((2, wide))
    s_pre = k.temp((1, 2 * wide))
    k.step(
        part(slow_last, m, 1, frames, lo3),
        st_in, k.take(saved[1]["third"]), k.take(slow1), k.take(cs), k.take(gain_slow), k.take(bias_slow), mk_in,
        out_slow, pre, s_pre, n3,
    )
    names, s_ef2 = fast_back3(k, 1, 2 * wide, st_in, mk_in, pre_f)
    pay = payload(k, s_pre, s_ef2)
    ef2_row = row_out(k, names["ef2"], mk_in, 0, LANES)
    b1 = finish(k, out_slow=out_slow, pre=pre, n3=n3, pay=pay, ef2_row=ef2_row, **names)
    saved[1]["n3"] = b1["n3"]
    out_slow = b1["out_slow"]
    st = gather_sums(b1["pay"])

    k = Stage("back_third")
    ef2_row = other_row(b1["ef2_row"])
    mk_in, st_in = k.take(mk), k.near(st)
    names, s_e2 = third_back(k, 1, 0, st_in, mk_in, b1["pre"])
    more, s_ef1 = fast_back2(k, 1, 2 * wide, st_in, mk_in, b1["ef2"], ef2_row)
    pay = payload(k, s_e2, s_ef1)
    e2_row, ef1_edge = row_out(k, names["e2"], mk_in, 0, width), edge_out(k, more["ef1"], mk_in, LANES)
    b1.update(finish(k, pay=pay, e2_row=e2_row, ef1_edge=ef1_edge, **names, **more))
    st = st_ef1 = gather_sums(b1["pay"])
    e2_row, ef1_edge = other_row(b1["e2_row"]), swap_path(b1["ef1_edge"])
    point1 = weights_point(1, b1["d3"])

    k = Stage("back_space")
    mk_in, st_in = k.take(mk), k.near(st)
    names, s_e1 = second_back(k, 1, 0, st_in, mk_in, b1["e2"], e2_row)
    pay = payload(k, s_e1)
    e1_edge = edge_out(k, names["e1"], mk_in, width)
    b1.update(finish(k, pay=pay, e1_edge=e1_edge, **names))
    st = gather_sums(b1["pay"])
    e1_edge = swap_path(b1["e1_edge"])
    space1 = weights_space(1, b1["d2"])

    k = Stage("back_first")
    mk_in, st_in = k.take(mk), k.near(st)
    names, sums = first_back(k, 1, st_in, mk_in, b1["e1"], e1_edge, b1["pre"])
    pay = payload(k, *sums)
    el_edge = edge_out(k, names["el"], mk_in, lat)
    b1.update(finish(k, pay=pay, el_edge=el_edge, **names))
    st = gather_sums(b1["pay"])
    el_edge = swap_path(b1["el_edge"])
    time1 = weights_time(1, b1["dw"])
    point1, space1, time1 = lax.psum((point1, space1, time1), AXES)

    k = Stage("back_third")
    mk_in, st_in = k.take(mk), k.near(st)
    names, s_e2 = third_back(k, 0, 2 * lat, st_in, mk_in, b1["down"])
    more, s_pf = fast_back1(
        k, 1, k.take(st_ef1), 2 * width, st_in, 0, mk_in, b1["el"], el_edge, b1["ef1"], ef1_edge, pre_f
    )
    pay = payload(k, s_e2, s_pf)
    e2_row = row_out(k, names["e2"], mk_in, 0, width)
    got = finish(k, pay=pay, e2_row=e2_row, **names, **more)
    for name in more:
        b1[name] = got[name]
    b0.update({name: got[name] for name in names})
    st = gather_sums(got["pay"])
    e2_row = other_row(got["e2_row"])
    point0 = weights_point(0, b0["d3"])
    fast_1 = weights_fast(1, b1["dl"], b1["df"], b1["d2f"], b1["d3f"])

    k = Stage("back_space")
    mk_in, st_in = k.take(mk), k.near(st)
    names, s_e1 = second_back(k, 0, 0, st_in, mk_in, b0["e2"], e2_row)
    more, s_ef2 = fast_back3(k, 0, 2 * width, st_in, mk_in, b1["downf"])
    pay = payload(k, s_e1, s_ef2)
    e1_edge, ef2_row = edge_out(k, names["e1"], mk_in, width), row_out(k, more["ef2"], mk_in, 0, LANES)
    b0.update(finish(k, pay=pay, e1_edge=e1_edge, ef2_row=ef2_row, **names, **more))
    st = gather_sums(b0["pay"])
    e1_edge, ef2_row = swap_path(b0["e1_edge"]), other_row(b0["ef2_row"])
    space0 = weights_space(0, b0["d2"])
    steps = exchange_steps()
    mid = jnp.concatenate([fast_1, point0, space0], axis=0)
    mid = halve(mid, *steps[0])

    k = Stage("back_first")
    mk_in, st_in = k.take(mk), k.near(st)
    names, sums = first_back(k, 0, st_in, mk_in, b0["e1"], e1_edge, b1["down"])
    more, s_ef1 = fast_back2(k, 0, 2 * width, st_in, mk_in, b0["ef2"], ef2_row)
    pay = payload(k, *sums, s_ef1)
    el_edge, ef1_edge = edge_out(k, names["el"], mk_in, lat), edge_out(k, more["ef1"], mk_in, LANES)
    b0.update(finish(k, pay=pay, el_edge=el_edge, ef1_edge=ef1_edge, **names, **more))
    pay, mid = lax.optimization_barrier((b0["pay"], mid))
    st = gather_sums(pay)
    el_edge, ef1_edge = swap_path(b0["el_edge"]), swap_path(b0["ef1_edge"])
    mid = halve(mid, *steps[1])
    time0 = weights_time(0, b0["dw"])
    late = halve(time0, *steps[0])
    st, mid = lax.optimization_barrier((st, mid))
    mid = halve(mid, *steps[2])

    k = Stage("back_fast")
    mk_in, st_in = k.take(mk), k.near(st)
    more, _ = fast_back1(
        k, 0, st_in, 2 * lat, st_in, 0, mk_in, b0["el"], el_edge, b0["ef1"], ef1_edge, b1["downf"]
    )
    b0.update(finish(k, **more))
    dl0, mid, late = lax.optimization_barrier((b0["dl"], mid, late))
    late = halve(late, *steps[1])
    rest = weights_fast(0, dl0, b0["df"], b0["d2f"], b0["d3f"])
    for step in steps[:3]:
        rest = halve(rest, *step)
    late = halve(late, *steps[2])
    parts = [mid.shape[0], late.shape[0], rest.shape[0]]
    value = jnp.concatenate([mid, late, rest], axis=0)
    for step in steps[3:]:
        value = halve(value, *step)
    value = value.astype(BF16)
    for step in reversed(steps):
        value = double(value, *step)
    value = value.reshape(8, sum(parts), 256)

    k = Stage("assemble")
    cut = [0, parts[0], parts[0] + parts[1], sum(parts)]
    mid, late, rest = [k.take(value, every, slice(lo, hi)) for lo, hi in zip(cut[:-1], cut[1:])]
    gtime = k.give((2, 3 * (wide + lat), width))
    k.step(part(assemble_time, 160), k.take(time1), late, gtime)
    start = fast_1.shape[0]
    gpoint = k.give((2, width, wide))
    k.step(part(assemble_point, start), k.take(point1), mid, gpoint)
    gspace = k.give((2, 9 * width, width))
    k.step(part(assemble_space, start + point0.shape[0]), k.take(space1), mid, gspace)
    fast_outs = [
        k.give((2, 5 * fwide, lat)), k.give((2, 3, inner, fwide)), k.give((2, 9, inner, inner)),
        k.give((2, inner, fwide)),
    ]
    k.step(part(assemble_fast, inner), mid, rest, *fast_outs)
    sums = [k.take(b[name]) for b in (b0, b1) for name in ("gbl", "gb1", "gb2", "gb3", "gbf1", "gbf2", "gbf3")]
    norm_outs = [k.give(like.shape) for like in (gain_slow, bias_slow, gain_fast, bias_fast)]
    k.step(part(assemble_norms, inner), *sums, *norm_outs)
    got = k.run()
    glat, gft, gfs, gfp = [got[h[1]] for h in fast_outs]

    return (
        out_slow.reshape(x_slow.shape),
        out_fast.reshape(x_fast.shape),
        b0["down"].reshape(x_slow.shape),
        b0["downf"].reshape(x_fast.shape),
        glat.reshape(w_lateral.shape),
        got[gtime[1]].reshape(w_slow_time.shape),
        got[gspace[1]].reshape(w_slow_space.shape),
        got[gpoint[1]],
        jnp.swapaxes(gft, 2, 3),
        gfs.reshape(w_fast_space.shape),
        gfp,
        *[got[h[1]] for h in norm_outs],
    )


def solution(mesh):
    spread = P("path", None, "rows", None, None, None)
    return jax.shard_map(
        on_device,
        mesh=mesh,
        in_specs=(spread, spread) + (P(),) * 12 + (spread, spread),
        out_specs=(spread,) * 4 + (P(),) * 11,
        check_vma=False,
    )
```

```python
import functools

import jax
import jax.numpy as jnp
import numpy as np
from jax import lax
from jax.experimental import pallas as pl
from jax.experimental.pallas import tpu as pltpu
from jax.sharding import PartitionSpec as P

TS = 8
TF = 32
F32 = jnp.float32
BF16 = jnp.bfloat16
EPSILON = 1e-05
LANES = 128
AXES = ("path", "rows")
VMEM_LIMIT = 56 * 2**20


def swap(value, axis, stride):
    pairs = [(source, source ^ stride) for source in range(lax.axis_size(axis))]
    return lax.ppermute(value, axis, pairs)


def gather_sums(spread):
    return lax.all_to_all(spread, AXES, 0, 0, tiled=True)


def swap_path(value):
    assert lax.axis_size("path") == 2
    return lax.ppermute(value, "path", [(0, 1), (1, 0)])


def exchange_steps():
    steps = [("rows", 1), ("path", 1)]
    stride = 2
    while stride < lax.axis_size("rows"):
        steps.append(("rows", stride))
        stride *= 2
    return steps


def halve(value, axis, stride):
    size = value.shape[0] // 2
    upper = (lax.axis_index(axis) // stride) % 2
    keep = lax.dynamic_slice_in_dim(value, upper * size, size, 0)
    give = lax.dynamic_slice_in_dim(value, (1 - upper) * size, size, 0)
    return keep.astype(F32) + swap(give.astype(BF16), axis, stride).astype(F32)


def double(value, axis, stride):
    upper = (lax.axis_index(axis) // stride) % 2
    got = swap(value, axis, stride)
    return jnp.concatenate(
        [jnp.where(upper == 0, value, got), jnp.where(upper == 0, got, value)], axis=0
    )


def halve_both(one, two, first, second):
    return halve(one, *first), halve(two, *second)


def parted(value):
    size = value.shape[0] // 2
    return value[:size], value[size:]


class Stage:
    def __init__(self, name):
        self.name = name
        self.arrays, self.views, self.scalars, self.pairs = [], [], [], []
        self.outs, self.temps, self.steps = [], [], []
        self.flops = 0

    def take(self, array, *view):
        for at, known in enumerate(self.arrays):
            if known is array:
                break
        else:
            at = len(self.arrays)
            self.arrays.append(array)
        for k, (other, seen) in enumerate(self.views):
            if other == at and seen == view:
                return ("in", k)
        self.views.append((at, view))
        return ("in", len(self.views) - 1)

    def take_blocks(self, value, got, flip, rows):
        self.pairs.append((self.take(value, slice(None), rows), self.take(got, slice(None), rows), flip))
        return ("pair", len(self.pairs) - 1)

    def scalar(self, array):
        self.scalars.append(array)
        return ("scalar", len(self.scalars) - 1)

    def give(self, dims, dtype=F32):
        self.outs.append(jax.ShapeDtypeStruct(tuple(dims), dtype))
        return ("out", len(self.outs) - 1)

    def temp(self, dims, dtype=F32):
        self.temps.append(pltpu.VMEM(tuple(dims), dtype))
        return ("temp", len(self.temps) - 1)

    def step(self, fn, *handles, flops=0):
        self.flops += flops
        self.steps.append((fn, handles))

    def sem(self, view, block):
        return 8 * view + block

    def view_shape(self, view):
        at, index = view
        return np.broadcast_to(np.zeros((), np.int8), self.arrays[at].shape)[index].shape

    def run(self):
        arrays, views, outs, steps, pairs = self.arrays, self.views, self.outs, self.steps, self.pairs
        order, home = [], {}
        for k, (one, two, flip) in enumerate(pairs):
            home[one[1]], home[two[1]] = (k, 0, flip), (k, 1, flip)

        def need(handle):
            if handle[0] == "in":
                return [handle[1]]
            return [part[1] for part in pairs[handle[1]][:2]] if handle[0] == "pair" else []

        for _, handles in steps:
            for handle in handles:
                for k in need(handle):
                    if k not in order:
                        order.append(k)

        def body(*refs):
            refs = list(refs)

            def cut(count):
                taken = refs[:count]
                del refs[:count]
                return taken

            scalars, hbm_in, hbm_out = cut(len(self.scalars)), cut(len(arrays)), cut(len(outs))
            alone = [k for k in range(len(views)) if k not in home]
            held = dict(zip(alone, cut(len(alone))))
            joint, made, temps, (sems,) = cut(len(pairs)), cut(len(outs)), cut(len(self.temps)), refs
            copies = {}
            for k in order:
                at, index = views[k]
                src = hbm_in[at].at[index] if index else hbm_in[at]
                if k in home:
                    pair, second, flip = home[k]
                    count = self.view_shape(views[k])[0]
                    copies[k] = []
                    for block in range(count):
                        to = (second * count + block) ^ scalars[flip[1]][0]
                        copies[k].append(
                            pltpu.make_async_copy(src.at[block], joint[pair].at[to], sems.at[self.sem(k, block)])
                        )
                else:
                    copies[k] = [pltpu.make_async_copy(src, held[k], sems.at[self.sem(k, 0)])]
                for copy in copies[k]:
                    copy.start()
            waited, sent = set(), {}
            for fn, handles in steps:
                given = []
                for handle in handles:
                    for k in need(handle):
                        if k not in waited:
                            for copy in copies[k]:
                                copy.wait()
                            waited.add(k)
                    place = {"in": held, "pair": joint, "out": made, "temp": temps, "scalar": scalars}
                    given.append(place[handle[0]][handle[1]])
                fn(*given)
                for kind, k in handles:
                    if kind == "out" and k not in sent:
                        sent[k] = pltpu.make_async_copy(made[k], hbm_out[k], sems.at[8 * len(views) + k])
                        sent[k].start()
            for copy in sent.values():
                copy.wait()

        moved = sum(a.size * a.dtype.itemsize for a in outs)
        for view in views:
            moved += int(np.prod(self.view_shape(view))) * arrays[view[0]].dtype.itemsize
        scratch = [
            pltpu.VMEM(self.view_shape(view), arrays[view[0]].dtype) for k, view in enumerate(views) if k not in home
        ]
        for one, _, _ in pairs:
            size = self.view_shape(views[one[1]])
            scratch.append(pltpu.VMEM((2 * size[0],) + size[1:], arrays[views[one[1]][0]].dtype))
        scratch += [pltpu.VMEM(o.shape, o.dtype) for o in outs]
        scratch += self.temps + [pltpu.SemaphoreType.DMA((8 * len(views) + len(outs),))]
        return pl.pallas_call(
            body,
            out_shape=tuple(outs),
            in_specs=[pl.BlockSpec(memory_space=pltpu.SMEM) for _ in self.scalars]
            + [pl.BlockSpec(memory_space=pl.ANY) for _ in arrays],
            out_specs=tuple(pl.BlockSpec(memory_space=pl.ANY) for _ in outs),
            scratch_shapes=scratch,
            compiler_params=pltpu.CompilerParams(vmem_limit_bytes=VMEM_LIMIT),
            cost_estimate=pl.CostEstimate(flops=self.flops, bytes_accessed=moved, transcendentals=0),
            name=self.name,
        )(*self.scalars, *arrays)


class Masks:
    def __init__(self, spots, cols):
        self.main = (0, spots)
        self.ext = (spots, 2 * spots + 2 * cols)
        self.prev = (2 * spots + 2 * cols, 3 * spots + 2 * cols)
        self.next = (3 * spots + 2 * cols, 4 * spots + 2 * cols)
        self.slow = (4 * spots + 2 * cols, 4 * spots + 2 * cols + 8)
        self.fast = (4 * spots + 2 * cols + 8, 4 * spots + 2 * cols + 16)
        self.half = (4 * spots + 2 * cols + 16, 4 * spots + 2 * cols + 24)
        self.path = (4 * spots + 2 * cols + 24, 4 * spots + 2 * cols + 32)
        self.rows = 4 * spots + 2 * cols + 32


def make_masks(m, rows, cols, last, place, clips, mk):
    half = place[0] % 2
    path = place[1]
    side = clips[0, place[0] // 2]
    area = 0
    for k in range(clips.shape[1]):
        area = area + clips[0, k] * clips[0, k]
    shift = cols.bit_length() - 1

    def inside(first, count):
        at = lax.broadcasted_iota(jnp.int32, (count * cols, LANES), 0)
        line = half * rows + first + (at >> shift)
        spot = at & (cols - 1)
        good = (line >= 0) & (line < 2 * rows) & (line < side) & (spot < side)
        return jnp.where(good, 1.0, 0.0)

    main = inside(0, rows)
    mk[m.main[0] : m.main[1], :] = main
    mk[m.ext[0] : m.ext[1], :] = inside(-1, rows + 2)
    mk[m.prev[0] : m.prev[1], :] = main * jnp.where(path > 0, 1.0, 0.0)
    mk[m.next[0] : m.next[1], :] = main * jnp.where(path < last, 1.0, 0.0)

    def fill(span, value):
        mk[span[0] : span[1], :] = jnp.full((8, LANES), value, F32)

    fill(m.slow, TS * area.astype(F32))
    fill(m.fast, TF * area.astype(F32))
    fill(m.half, half.astype(F32))
    fill(m.path, path.astype(F32))


def own_row(m, spots, cols, col0, width, z, mk, row):
    for t in range(z.shape[0]):
        lower = mk[m.half[0] : m.half[0] + 1, :] > 0.5
        for lane in range(0, width, LANES):
            at = col0 + lane
            row[t, :, lane : lane + LANES] = jnp.where(
                lower, z[t, 0:cols, at : at + LANES], z[t, spots - cols : spots, at : at + LANES]
            )


def own_edge(m, lead, tail, z, mk, edge):
    frames = z.shape[0]
    second = mk[m.path[0] : m.path[0] + 1, :] > 0.5
    for lane in range(0, edge.shape[1], LANES):
        edge[:, lane : lane + LANES] = jnp.where(
            second,
            z[0, :, lead + lane : lead + lane + LANES],
            z[frames - 1, :, tail + lane : tail + lane + LANES],
        ).astype(edge.dtype)


def spread_sums(*refs):
    parts, out = refs[:-1], refs[-1]
    row = jnp.concatenate([part[...] for part in parts], axis=1)
    out[...] = jnp.broadcast_to(row[None], out.shape)


def make_w7(lat, group, wl, wf, w7):
    inner = wf.shape[1]
    w7[...] = jnp.zeros(w7.shape, BF16)
    for j in range(wl.shape[0]):
        w7[j * LANES : (j + 1) * LANES, 0:lat] = wl[j]
    at = lax.broadcasted_iota(jnp.int32, (inner, LANES), 0)
    lane = lax.broadcasted_iota(jnp.int32, (inner, LANES), 1)
    places = [jnp.where(lane == at + inner * k, 1.0, 0.0).astype(BF16) for k in range(group)]
    for f in range(1, group + 3):
        used = [k for k in range(group) if 0 <= f - 1 - k < 3]
        got = None
        for k in used:
            more = dot_tn(wf[f - 1 - k], places[k])
            got = more if got is None else got + more
        w7[f * LANES : (f + 1) * LANES, lat : lat + LANES] = got.astype(BF16)


def make_blocks(group, ws, wp, wfs, wfp):
    inner = wp.shape[0]
    at = lax.broadcasted_iota(jnp.int32, (inner, LANES), 0)
    lane = lax.broadcasted_iota(jnp.int32, (inner, LANES), 1)
    tile = jnp.where((lane & (inner - 1)) == at, 1.0, 0.0).astype(BF16)
    shift = inner.bit_length() - 1
    for tap in range(ws.shape[0]):
        got = dot(ws[tap], tile)
        for k in range(group):
            kept = jnp.where((lane >> shift) == k, got, 0.0).astype(BF16)
            row = (tap % 3) * LANES + k * inner
            wfs[tap // 3, row : row + inner, :] = kept
    wfp[...] = jnp.zeros(wfp.shape, BF16)
    for k in range(group):
        wfp[k * inner : (k + 1) * inner, k * LANES : (k + 1) * LANES] = wp[...]


def widen(rows, width):
    return jnp.concatenate([rows] * (width // LANES), axis=1)


def sublane_sums(value):
    return jnp.sum(value.reshape(value.shape[0] // 8, 8, value.shape[1]), axis=0)


def row_sum(value):
    return jnp.sum(value, axis=0, keepdims=True)


def fold_packed(row):
    full = jnp.broadcast_to(row, (8, LANES))
    full = full + pltpu.roll(full, 64, 1)
    full = full + pltpu.roll(full, 32, 1)
    return full[0:1]


def totals(st, lo, width, packed=False):
    first = jnp.sum(st[:, :, lo : lo + width], axis=0)
    second = jnp.sum(st[:, :, lo + width : lo + 2 * width], axis=0)
    if packed:
        return fold_packed(first), fold_packed(second)
    return first, second


def norm_rows(st, lo, width, count, packed=False):
    first, second = totals(st, lo, width, packed)
    mean = first / count
    return mean, lax.rsqrt(second / count - mean * mean + EPSILON)


def sigmoid(value):
    return 0.5 * jnp.tanh(0.5 * value) + 0.5


def silu(value):
    return value * sigmoid(value)


def silu_slope(value):
    sigma = sigmoid(value)
    return sigma * (1.0 + value * (1.0 - sigma))


def dot(a, b):
    return jnp.dot(a, b, preferred_element_type=F32)


def dot_nt(a, b):
    return lax.dot_general(a, b, (((1,), (1,)), ((), ())), preferred_element_type=F32)


def dot_tn(a, b):
    return lax.dot_general(a, b, (((0,), (0,)), ((), ())), preferred_element_type=F32)


def flat(value):
    return value.reshape(value.shape[0] * value.shape[1], value.shape[2])


def store_shifts(dst, t, value, cols):
    rows, width = value.shape
    spot = lax.broadcasted_iota(jnp.int32, (rows, width), 0) & (cols - 1)
    left = jnp.where(spot == 0, 0.0, pltpu.roll(value, 1, 0))
    right = jnp.where(spot == cols - 1, 0.0, pltpu.roll(value, rows - 1, 0))
    dst[t, :, 0:width] = left.astype(BF16)
    dst[t, :, width : 2 * width] = value.astype(BF16)
    dst[t, :, 2 * width : 3 * width] = right.astype(BF16)


def taps_of(frames_ref, frames, group):
    return jnp.concatenate(
        [
            jnp.concatenate([frames_ref[group * t + f] for f in range(7)], axis=1)
            for t in range(frames)
        ],
        axis=0,
    )


def entry_sums(y, lat, frames, spots):
    width = y.shape[1]
    one = jnp.zeros((8, width), F32)
    two = jnp.zeros((8, width), F32)
    for t in range(frames):
        part = y[t * spots : (t + 1) * spots]
        one = one + sublane_sums(part)
        two = two + sublane_sums(part * part)
    one = row_sum(one)
    two = row_sum(two)
    return jnp.concatenate([one[:, :lat], two[:, :lat], one[:, lat:], two[:, lat:]], axis=1)


def fast_entry(m, frames, group, x, before, after, mk, w7, fw, y, s):
    spots = x.shape[1]
    count = x.shape[0]

    def put(at, value, span):
        fw[at] = (value.astype(F32) * mk[span[0] : span[1], :]).astype(BF16)

    for k in range(2):
        put(k, before[k], m.prev)
        put(2 + count + k, after[k], m.next)
    for k in range(count):
        put(2 + k, x[k], m.main)
    out = dot(taps_of(fw, frames, group), w7[...])
    for t in range(frames):
        y[t] = out[t * spots : (t + 1) * spots]
    s[...] = entry_sums(out, w7.shape[1] - LANES, frames, spots)


def slow_partial(m, frames, x, before, after, mk, wt, xm, fpart):
    spots, wide = x.shape[1], x.shape[2]
    sources = [(before, m.prev)] + [(x.at[t], m.main) for t in range(frames)] + [(after, m.next)]
    for k, (src, span) in enumerate(sources):
        for lo in range(0, wide, 256):
            mask = widen(mk[span[0] : span[1], :], 256)
            xm[k, :, lo : lo + 256] = (src[:, lo : lo + 256].astype(F32) * mask).astype(BF16)
    out = dot(flat(xm[0:frames]), wt[0, :wide, :])
    for j in range(1, 3):
        out = out + dot(flat(xm[j : j + frames]), wt[j, :wide, :])
    for t in range(frames):
        fpart[t] = out[t * spots : (t + 1) * spots]


def lat_join(m, n, frames, lat, st, y, before, after, fpart, wt, gs, bs, mk, jl, first, s, nl, jw):
    spots = y.shape[1]
    wide = wt.shape[1] - lat
    count = widen(mk[m.slow[0] : m.slow[0] + 1, :], lat)
    mean, rstd = norm_rows(st, 0, lat, count)
    nl[0:1, :] = mean
    nl[1:2, :] = rstd
    scale = rstd * gs[n : n + 1, 0:lat]
    bias = bs[n : n + 1, 0:lat]
    sources = (
        [(before[:, 0:lat], m.prev)]
        + [(y[t, :, 0:lat], m.main) for t in range(frames)]
        + [(after[:, 0:lat], m.next)]
    )
    for k, (value, span) in enumerate(sources):
        mask = widen(mk[span[0] : span[1], :], lat)
        act = (silu((value - mean) * scale + bias) * mask).astype(BF16)
        jw[k] = act
        if 1 <= k <= frames:
            jl[k - 1] = act
    out = flat(fpart[...])
    for j in range(3):
        out = out + dot(flat(jw[j : j + frames]), wt[j, wide:, :])
    one = jnp.zeros((8, out.shape[1]), F32)
    two = jnp.zeros((8, out.shape[1]), F32)
    for t in range(frames):
        part = out[t * spots : (t + 1) * spots]
        first[t] = part
        one = one + sublane_sums(part)
        two = two + sublane_sums(part * part)
    s[...] = jnp.concatenate([row_sum(one), row_sum(two)], axis=1)


def space_forward(
    m, n, frames, cols, lo, at, width, col0, packed, span, st, z, row, w, g, b, mk, aw, out, s, nz, vw
):
    spots = z.shape[1]
    count = widen(mk[span[0] : span[0] + 1, :], width)
    mean, rstd = norm_rows(st, at, width, count, packed)
    nz[0:1, :] = mean
    nz[1:2, :] = rstd
    scale = rstd * g[n : n + 1, lo : lo + width]
    bias = b[n : n + 1, lo : lo + width]
    mask = widen(mk[m.ext[0] : m.ext[1], :], width)
    for t in range(frames):
        value = jnp.concatenate([row[t], z[t, :, col0 : col0 + width], row[t]], axis=0)
        act = silu((value - mean) * scale + bias) * mask
        aw[t] = act.astype(BF16)
        store_shifts(vw, t, act, cols)
    total = dot(flat(vw[:, 0:spots, :]), w[0])
    for i in range(1, 3):
        total = total + dot(flat(vw[:, i * cols : i * cols + spots, :]), w[i])
    mask = widen(mk[m.main[0] : m.main[1], :], width)
    one = jnp.zeros((8, width), F32)
    two = jnp.zeros((8, width), F32)
    for t in range(frames):
        part = total[t * spots : (t + 1) * spots]
        out[t] = part
        part = part * mask
        one = one + sublane_sums(part)
        two = two + sublane_sums(part * part)
    s[...] = jnp.concatenate([row_sum(one), row_sum(two)], axis=1)


def slow_third(m, n, frames, lo, halo, st, z, *rest):
    if halo:
        before, after, wp, g, b, mk, a2, third, s, nz, aw = rest
    else:
        wp, g, b, mk, a2, third, s, nz, aw = rest
    spots, width = z.shape[1], z.shape[2]
    wide = wp.shape[1]
    count = widen(mk[m.slow[0] : m.slow[0] + 1, :], width)
    mean, rstd = norm_rows(st, 0, width, count)
    nz[0:1, :] = mean
    nz[1:2, :] = rstd
    scale = rstd * g[n : n + 1, lo : lo + width]
    bias = b[n : n + 1, lo : lo + width]
    sources = [(z[t], m.main, t + halo) for t in range(frames)]
    if halo:
        sources += [(before[...], m.prev, 0), (after[...], m.next, frames + 1)]
    for value, span, at in sources:
        mask = widen(mk[span[0] : span[1], :], width)
        act = (silu((value - mean) * scale + bias) * mask).astype(BF16)
        aw[at] = act
        if halo <= at < frames + halo:
            a2[at - halo] = act
    acts = flat(aw[...])
    ones, twos = [], []
    for at in range(0, wide, 256):
        out = dot(acts, wp[:, at : at + 256])
        one = jnp.zeros((8, 256), F32)
        two = jnp.zeros((8, 256), F32)
        for t in range(frames + 2 * halo):
            part = out[t * spots : (t + 1) * spots]
            third[t, :, at : at + 256] = part
            if halo <= t < frames + halo:
                one = one + sublane_sums(part)
                two = two + sublane_sums(part * part)
        ones.append(row_sum(one))
        twos.append(row_sum(two))
    s[...] = jnp.concatenate(ones + twos, axis=1)


def fast_third(m, n, frames, lo, at, st, z, wp, g, b, mk, a2, ft, s, nz):
    spots = z.shape[1]
    count = mk[m.fast[0] : m.fast[0] + 1, :]
    mean, rstd = norm_rows(st, at, LANES, count, True)
    nz[0:1, :] = mean
    nz[1:2, :] = rstd
    scale = rstd * g[n : n + 1, lo : lo + LANES]
    bias = b[n : n + 1, lo : lo + LANES]
    mask = mk[m.main[0] : m.main[1], :]
    for t in range(frames):
        a2[t] = (silu((z[t] - mean) * scale + bias) * mask).astype(BF16)
    acts = flat(a2[...])
    one = jnp.zeros((8, LANES), F32)
    two = jnp.zeros((8, LANES), F32)
    out = dot(acts, wp[...])
    for t in range(frames):
        for lane in range(0, wp.shape[1], LANES):
            part = out[t * spots : (t + 1) * spots, lane : lane + LANES]
            ft[t, :, lane : lane + LANES] = part
            one = one + sublane_sums(part)
            two = two + sublane_sums(part * part)
    s[...] = jnp.concatenate([row_sum(one), row_sum(two)], axis=1)


def fast_next(m, n, frames, group, lo, at, st, ft, before, after, fw0, w7, g, b, mk, f1, fw1, y, s, nz):
    spots = ft.shape[1]
    count = mk[m.fast[0] : m.fast[0] + 1, :]
    mean, rstd = norm_rows(st, at, LANES, count)
    nz[0:1, :] = mean
    nz[1:2, :] = rstd
    scale = rstd * g[n : n + 1, lo : lo + LANES]
    bias = b[n : n + 1, lo : lo + LANES]
    total = frames * group

    def out_of(k, value, span):
        z = fw0[k].astype(F32) + ((value - mean) * scale + bias)
        return silu(z) * mk[span[0] : span[1], :]

    for k in range(2):
        lane = k * LANES
        fw1[k] = out_of(k, before[:, lane : lane + LANES], m.prev).astype(BF16)
        fw1[2 + total + k] = out_of(2 + total + k, after[:, lane : lane + LANES], m.next).astype(BF16)
    for t in range(frames):
        for f in range(group):
            k = t * group + f
            value = out_of(2 + k, ft[t, :, f * LANES : (f + 1) * LANES], m.main)
            f1[k] = value
            fw1[2 + k] = value.astype(BF16)
    out = dot(taps_of(fw1, frames, group), w7[...])
    for t in range(frames):
        y[t] = out[t * spots : (t + 1) * spots]
    s[...] = entry_sums(out, w7.shape[1] - LANES, frames, spots)


def fast_last(m, n, frames, group, lo, at, st, ft, f1, cot, g, b, mk, out, pre, s, nz):
    count = mk[m.fast[0] : m.fast[0] + 1, :]
    mean, rstd = norm_rows(st, at, LANES, count)
    nz[0:1, :] = mean
    nz[1:2, :] = rstd
    gain = g[n : n + 1, lo : lo + LANES]
    bias = b[n : n + 1, lo : lo + LANES]
    mask = mk[m.main[0] : m.main[1], :]
    one = jnp.zeros((8, LANES), F32)
    two = jnp.zeros((8, LANES), F32)
    for t in range(frames):
        for f in range(group):
            k = t * group + f
            hat = (ft[t, :, f * LANES : (f + 1) * LANES] - mean) * rstd
            z = f1[k] + hat * gain + bias
            sigma = sigmoid(z)
            out[k] = z * sigma * mask
            grad = cot[k].astype(F32) * mask * (sigma * (1.0 + z * (1.0 - sigma)))
            pre[k] = grad
            one = one + sublane_sums(grad)
            two = two + sublane_sums(grad * hat)
    s[...] = jnp.concatenate([row_sum(one), row_sum(two)], axis=1)


def chunked(total, step, body, init):
    def turn(i, carry):
        return body(pl.multiple_of(i * step, step), carry)

    return lax.fori_loop(0, total // step, turn, init)


def slow_next(m, n, frames, lo, at0, st, third, xm, wt, g, b, mk, slow1, sw, fpart, nz):
    spots, wide = third.shape[1], third.shape[2]
    count = widen(mk[m.slow[0] : m.slow[0] + 1, :], wide)
    mean, rstd = norm_rows(st, at0, wide, count)
    nz[0:1, :] = mean
    nz[1:2, :] = rstd
    scale = rstd * g[n : n + 1, lo : lo + wide]
    bias = b[n : n + 1, lo : lo + wide]
    spans = [m.prev] + [m.main] * frames + [m.next]
    for k, span in enumerate(spans):

        def turn(at, carry, k=k, span=span):
            mask = widen(mk[pl.ds(span[0] + at, 16), :], 512)
            for c in range(0, wide, 512):
                z = third[k, pl.ds(at, 16), c : c + 512]
                z = (z - mean[:, c : c + 512]) * scale[:, c : c + 512] + bias[:, c : c + 512]
                z = xm[k, pl.ds(at, 16), c : c + 512].astype(F32) + z
                value = silu(z) * mask
                sw[k, pl.ds(at, 16), c : c + 512] = value.astype(BF16)
                if 1 <= k <= frames:
                    slow1[k - 1, pl.ds(at, 16), c : c + 512] = value
            return carry

        chunked(spots, 16, turn, 0)
    out = dot(flat(sw[0:frames]), wt[0, :wide, :])
    for j in range(1, 3):
        out = out + dot(flat(sw[j : j + frames]), wt[j, :wide, :])
    for t in range(frames):
        fpart[t] = out[t * spots : (t + 1) * spots]


def slow_last(m, n, frames, lo, st, third, slow1, cot, g, b, mk, out, pre, s, nz):
    spots, wide = third.shape[1], third.shape[2]
    count = widen(mk[m.slow[0] : m.slow[0] + 1, :], wide)
    mean, rstd = norm_rows(st, 0, wide, count)
    nz[0:1, :] = mean
    nz[1:2, :] = rstd
    gain = g[n : n + 1, lo : lo + wide]
    bias = b[n : n + 1, lo : lo + wide]
    carry = (jnp.zeros((8, wide), F32), jnp.zeros((8, wide), F32))
    for t in range(frames):

        def turn(at, sums, t=t):
            one, two = sums
            ones, twos = [], []
            mask = widen(mk[pl.ds(m.main[0] + at, 16), :], 512)
            for c in range(0, wide, 512):
                hat = (third[t, pl.ds(at, 16), c : c + 512] - mean[:, c : c + 512]) * rstd[:, c : c + 512]
                z = slow1[t, pl.ds(at, 16), c : c + 512] + hat * gain[:, c : c + 512] + bias[:, c : c + 512]
                sigma = sigmoid(z)
                out[t, pl.ds(at, 16), c : c + 512] = z * sigma * mask
                grad = cot[t, pl.ds(at, 16), c : c + 512].astype(F32) * mask
                grad = grad * (sigma * (1.0 + z * (1.0 - sigma)))
                pre[t, pl.ds(at, 16), c : c + 512] = grad
                ones.append(sublane_sums(grad))
                twos.append(sublane_sums(grad * hat))
            return one + jnp.concatenate(ones, axis=1), two + jnp.concatenate(twos, axis=1)

        carry = chunked(spots, 16, turn, carry)
    s[...] = jnp.concatenate([row_sum(carry[0]), row_sum(carry[1])], axis=1)


def slow_third_back(m, n, frames, lo3, lo2, at, halo, st, pre, third, n3, z, n2, wp, g, b, mk, d3, e2, s, gb):
    spots, wide = pre.shape[1], pre.shape[2]
    width = z.shape[2]
    count = widen(mk[m.slow[0] : m.slow[0] + 1, :], wide)
    one, two = totals(st, at, wide)
    gb[0:1, :] = one
    gb[1:2, :] = two
    mean, rstd = n3[0:1, :], n3[1:2, :]
    scale = g[n : n + 1, lo3 : lo3 + wide] * rstd
    one = one / count
    two = two / count * rstd
    for t in range(frames):

        def turn(i, carry, t=t):
            mask = widen(mk[pl.ds(m.main[0] + i, 16), :], 512)
            for c in range(0, wide, 512):
                hat = (third[t + halo, pl.ds(i, 16), c : c + 512] - mean[:, c : c + 512]) * two[:, c : c + 512]
                grad = pre[t, pl.ds(i, 16), c : c + 512] - mask * (one[:, c : c + 512] + hat)
                d3[t, pl.ds(i, 16), c : c + 512] = (scale[:, c : c + 512] * grad).astype(BF16)
            return carry

        chunked(spots, 16, turn, 0)
    out = dot_nt(flat(d3[...]), wp[...])
    mean, rstd = n2[0:1, :], n2[1:2, :]
    gain = g[n : n + 1, lo2 : lo2 + width]
    bias = b[n : n + 1, lo2 : lo2 + width]
    back_act(m, frames, spots, out, z, 0, mean, rstd, gain, bias, mk, e2, s)


def back_act(m, frames, spots, out, z, col0, mean, rstd, gain, bias, mk, e, s):
    width = out.shape[1]
    mask = widen(mk[m.main[0] : m.main[1], :], width)
    one = jnp.zeros((8, width), F32)
    two = jnp.zeros((8, width), F32)
    for t in range(frames):
        hat = (z[t, :, col0 : col0 + width] - mean) * rstd
        grad = out[t * spots : (t + 1) * spots] * mask * silu_slope(hat * gain + bias)
        e[t] = grad
        one = one + sublane_sums(grad)
        two = two + sublane_sums(grad * hat)
    s[...] = jnp.concatenate([row_sum(one), row_sum(two)], axis=1)


def fast_third_back(m, n, frames, group, lo3, lo2, at, st, pre, ft, n3, z, n2, wp, g, b, mk, d3, e2, s, gb):
    spots = z.shape[1]
    count = mk[m.fast[0] : m.fast[0] + 1, :]
    one, two = totals(st, at, LANES)
    gb[0:1, :] = one
    gb[1:2, :] = two
    mean, rstd = n3[0:1, :], n3[1:2, :]
    scale = g[n : n + 1, lo3 : lo3 + LANES] * rstd
    one = one / count
    two = two / count * rstd
    mask = mk[m.main[0] : m.main[1], :]
    for t in range(frames):
        for f in range(group):
            hat = (ft[t, :, f * LANES : (f + 1) * LANES] - mean) * two
            grad = pre[t * group + f] - mask * (one + hat)
            d3[t, :, f * LANES : (f + 1) * LANES] = (scale * grad).astype(BF16)
    out = dot_nt(flat(d3[...]), wp[...])
    mean, rstd = n2[0:1, :], n2[1:2, :]
    gain = g[n : n + 1, lo2 : lo2 + LANES]
    bias = b[n : n + 1, lo2 : lo2 + LANES]
    back_act(m, frames, spots, out, z, 0, mean, rstd, gain, bias, mk, e2, s)


def space_back(
    m, n, frames, cols, lo2, lo1, at, width, col0, packed, span,
    st, e, erow, z, zrow, nz, z1, n1, w, g, b, mk, d2, e1, s, gb, vw,
):
    spots = z.shape[1]
    count = widen(mk[span[0] : span[0] + 1, :], width)
    one, two = totals(st, at, width, packed)
    gb[0:1, :] = one
    gb[1:2, :] = two
    mean, rstd = nz[0:1, :], nz[1:2, :]
    scale = g[n : n + 1, lo2 : lo2 + width] * rstd
    one = one / count
    two = two / count * rstd
    mask = widen(mk[m.ext[0] : m.ext[1], :], width)
    for t in range(frames):
        grad = jnp.concatenate([erow[t], e[t], erow[t]], axis=0)
        value = jnp.concatenate([zrow[t], z[t], zrow[t]], axis=0)
        grad = scale * mask * (grad - (one + (value - mean) * two))
        d2[t] = grad[cols : cols + spots].astype(BF16)
        store_shifts(vw, t, grad.astype(BF16).astype(F32), cols)
    total = None
    for i in range(3):
        rows = (2 - i) * cols
        for j in range(3):
            lane = (2 - j) * width
            part = dot_nt(flat(vw[:, rows : rows + spots, lane : lane + width]), w[i, j * width : (j + 1) * width, :])
            total = part if total is None else total + part
    mean, rstd = n1[0:1, :], n1[1:2, :]
    gain = g[n : n + 1, lo1 : lo1 + width]
    bias = b[n : n + 1, lo1 : lo1 + width]
    back_act(m, frames, spots, total, z1, col0, mean, rstd, gain, bias, mk, e1, s)


def slow_first_back(m, n, frames, lo1, lo3, at, halo, last, st, *rest):
    if last:
        e, ep, en, z, zp, zn, n1, wt, y, nl, pre, g, b, mk, dw, el, s, gx, gb = rest
    else:
        e, ep, en, z, zp, zn, n1, wt, y, nl, pre, xm, third, n3, g, b, mk, dw, el, s, pre0, s3, gb = rest
    spots, width = z.shape[1], z.shape[2]
    lat = nl.shape[1]
    wide = wt.shape[1] - lat
    count = widen(mk[m.slow[0] : m.slow[0] + 1, :], width)
    one, two = totals(st, at, width)
    gb[0:1, :] = one
    gb[1:2, :] = two
    mean, rstd = n1[0:1, :], n1[1:2, :]
    scale = g[n : n + 1, lo1 : lo1 + width] * rstd
    one = one / count
    two = two / count * rstd
    sources = (
        [(ep, zp, m.prev)] + [(e.at[t], z.at[t], m.main) for t in range(frames)] + [(en, zn, m.next)]
    )
    for k, (grad, value, span) in enumerate(sources):
        mask = widen(mk[span[0] : span[1], :], width)
        dw[k] = (scale * mask * (grad[...] - (one + (value[...] - mean) * two))).astype(BF16)
    taps = [flat(dw[2 - j : 2 - j + frames]) for j in range(3)]

    def back(lo, size):
        out = dot_nt(taps[0], wt[0, lo : lo + size, :])
        for j in range(1, 3):
            out = out + dot_nt(taps[j], wt[j, lo : lo + size, :])
        return out

    out = back(wide, lat)
    back_act(
        m, frames, spots, out, y, 0, nl[0:1, :], nl[1:2, :], g[n : n + 1, 0:lat], b[n : n + 1, 0:lat], mk, el, s
    )
    mask = widen(mk[m.main[0] : m.main[1], :], 256)
    ones, twos = [], []
    for c in range(0, wide, 256):
        out = back(c, 256)
        if not last:
            mean, rstd = n3[0:1, c : c + 256], n3[1:2, c : c + 256]
            gain = g[n - 1 : n, lo3 + c : lo3 + c + 256]
            bias = b[n - 1 : n, lo3 + c : lo3 + c + 256]
            one = jnp.zeros((8, 256), F32)
            two = jnp.zeros((8, 256), F32)
        for t in range(frames):
            grad = (out[t * spots : (t + 1) * spots] + pre[t, :, c : c + 256]) * mask
            if last:
                gx[t, :, c : c + 256] = grad
            else:
                hat = (third[t + halo, :, c : c + 256] - mean) * rstd
                z0 = xm[t + 1, :, c : c + 256].astype(F32) + hat * gain + bias
                grad = grad * silu_slope(z0)
                pre0[t, :, c : c + 256] = grad
                one = one + sublane_sums(grad)
                two = two + sublane_sums(grad * hat)
        if not last:
            ones.append(row_sum(one))
            twos.append(row_sum(two))
    if not last:
        s3[...] = jnp.concatenate(ones + twos, axis=1)


def fast_first_back(m, n, frames, group, lo1, lo3, at1, atl, last, st1, stl, *rest):
    if last:
        el, eln, ef, efp, efn, y, yp, yn, nl, n1, w7, pre, gs, g, b, mk, dl, dfw, gx, gbl, gb1, buf = rest
    else:
        (el, eln, ef, efp, efn, y, yp, yn, nl, n1, w7, pre, fw0, ft, n3, gs, g, b, mk,
         dl, dfw, pre0, s, gbl, gb1, buf) = rest
    spots = y.shape[1]
    lat = nl.shape[1]
    count = widen(mk[m.slow[0] : m.slow[0] + 1, :], lat)
    one, two = totals(stl, atl, lat)
    gbl[0:1, :] = one
    gbl[1:2, :] = two
    mean, rstd = nl[0:1, :], nl[1:2, :]
    scale = gs[n : n + 1, 0:lat] * rstd
    one = one / count
    two = two / count * rstd

    def lat_grad(grad, value, span):
        mask = widen(mk[span[0] : span[1], :], lat)
        return (scale * mask * (grad - (one + (value - mean) * two))).astype(BF16)

    for t in range(frames):
        dl[t] = lat_grad(el[t], y[t, :, 0:lat], m.main)
    dl_next = lat_grad(eln[...], yn[:, 0:lat], m.next)
    fcount = mk[m.fast[0] : m.fast[0] + 1, :]
    fone, ftwo = totals(st1, at1, LANES, True)
    gb1[0:1, :] = fone
    gb1[1:2, :] = ftwo
    fmean, frstd = n1[0:1, :], n1[1:2, :]
    fscale = g[n : n + 1, lo1 : lo1 + LANES] * frstd
    fone = fone / fcount
    ftwo = ftwo / fcount * frstd

    def first_grad(grad, value, span):
        mask = mk[span[0] : span[1], :]
        return (fscale * mask * (grad - (fone + (value - fmean) * ftwo))).astype(BF16)

    for t in range(frames):
        dfw[t] = first_grad(ef[t], y[t, :, lat:], m.main)
    df_prev = first_grad(efp[...], yp[:, lat:], m.prev)
    df_next = first_grad(efn[...], yn[:, lat:], m.next)
    both = jnp.concatenate([flat(dl[...]), flat(dfw[...])], axis=1)
    buf[...] = jnp.zeros(buf.shape, F32)
    out = dot_nt(both, w7[...])
    for t in range(frames):
        for f in range(7):
            k = group * t + f
            buf[k] = buf[k] + out[t * spots : (t + 1) * spots, f * LANES : (f + 1) * LANES]
    buf[2] = buf[2] + dot_nt(df_prev, w7[6 * LANES : 7 * LANES, lat:])
    after = dot_nt(jnp.concatenate([dl_next, df_next], axis=1), w7[0 : 2 * LANES, :])
    total = frames * group
    for f in range(2):
        buf[total + f] = buf[total + f] + after[:, f * LANES : (f + 1) * LANES]
    mask = mk[m.main[0] : m.main[1], :]
    if last:
        for k in range(total):
            gx[k] = (pre[k] + buf[2 + k]) * mask
        return
    mean, rstd = n3[0:1, :], n3[1:2, :]
    gain = g[n - 1 : n, lo3 : lo3 + LANES]
    bias = b[n - 1 : n, lo3 : lo3 + LANES]
    one = jnp.zeros((8, LANES), F32)
    two = jnp.zeros((8, LANES), F32)
    for k in range(total):
        t, f = k // group, k % group
        hat = (ft[t, :, f * LANES : (f + 1) * LANES] - mean) * rstd
        z0 = fw0[2 + k].astype(F32) + hat * gain + bias
        grad = (pre[k] + buf[2 + k]) * mask * silu_slope(z0)
        pre0[k] = grad
        one = one + sublane_sums(grad)
        two = two + sublane_sums(grad * hat)
    s[...] = jnp.concatenate([row_sum(one), row_sum(two)], axis=1)


def point_weights(a2, d3, out):
    acts = flat(a2[...])
    for k in range(out.shape[0]):
        out[k] = dot_tn(acts, flat(d3[:, :, k * 256 : (k + 1) * 256])).astype(BF16)


def space_weights(cols, aw, d2, out, vw):
    frames, spots, width = d2.shape
    for t in range(frames):
        store_shifts(vw, t, aw[t].astype(F32), cols)
    grads = flat(d2[...])
    for i in range(3):
        out[i] = dot_tn(flat(vw[:, i * cols : i * cols + spots, :]), grads).astype(BF16)


def time_weights(skip, slow, jl, dw, out):
    frames, spots, width = jl.shape
    wide = slow.shape[2]
    grads = jnp.concatenate([flat(dw[2 - j : 2 - j + frames]) for j in range(3)], axis=1)
    for c in range(0, wide + jl.shape[2], 256):
        if c < wide:
            acts = flat(slow[skip : skip + frames, :, c : c + 256])
        else:
            acts = flat(jl[:, :, c - wide : c - wide + 256])
        got = dot_tn(acts, grads)
        for j in range(3):
            out[j, c : c + 256, :] = got[:, j * width : (j + 1) * width].astype(BF16)


def group_blocks(value, group):
    size = LANES // group
    rows = lax.broadcasted_iota(jnp.int32, (LANES, LANES), 0) >> (size.bit_length() - 1)
    lanes = lax.broadcasted_iota(jnp.int32, (LANES, LANES), 1) >> (size.bit_length() - 1)
    kept = jnp.where(rows == lanes, value, 0.0)
    kept = kept + pltpu.roll(kept, 64, 1)
    kept = kept + pltpu.roll(kept, 32, 1)
    total = kept[0:size]
    for k in range(1, group):
        total = total + kept[k * size : (k + 1) * size]
    return total


def at_lanes(blocks):
    lanes = lax.broadcasted_iota(jnp.int32, blocks[0].shape, 1) >> 5
    out = jnp.zeros(blocks[0].shape, F32)
    for k, block in enumerate(blocks):
        out = jnp.where(lanes == k, block, out)
    return out


def fast_weights(group, cols, lat, fw, dl, df, fa1, d2, fa2, d3, out, vw):
    frames, spots, _ = dl.shape
    size = LANES // group
    both = jnp.concatenate([flat(dl[...]), flat(df[...])], axis=1)
    taps = [[None] * group for _ in range(3)]
    for f in range(7):
        acts = jnp.concatenate([fw[group * t + f] for t in range(frames)], axis=0)
        got = dot_tn(acts, both)
        if f < 5:
            out[f * LANES : (f + 1) * LANES, :] = got[:, :lat].astype(BF16)
        for k in range(group):
            if 0 <= f - k - 1 < 3:
                taps[f - k - 1][k] = got[:, lat:]
    lanes = lax.broadcasted_iota(jnp.int32, (LANES, LANES), 1) >> (size.bit_length() - 1)
    tap_sums = []
    for j in range(3):
        kept = jnp.zeros((LANES, LANES), F32)
        for k in range(group):
            kept = jnp.where(lanes == k, taps[j][k], kept)
        kept = kept + pltpu.roll(kept, 64, 1)
        tap_sums.append(kept + pltpu.roll(kept, 32, 1))
    low = 5 * LANES
    out[low : low + LANES, 0:LANES] = at_lanes(tap_sums).T.astype(BF16)
    for t in range(frames):
        store_shifts(vw, t, fa1[t].astype(F32), cols)
    grads = flat(d2[...])
    for i in range(3):
        got = dot_tn(flat(vw[:, i * cols : i * cols + spots, :]), grads)
        blocks = [group_blocks(got[j * LANES : (j + 1) * LANES], group) for j in range(3)]
        out[low + size * i : low + size * (i + 1), LANES : 2 * LANES] = at_lanes(blocks).astype(BF16)
    acts = flat(fa2[...])
    total = jnp.zeros((size, LANES), F32)
    for k in range(group):
        got = dot_tn(acts, flat(d3[:, :, k * LANES : (k + 1) * LANES]))
        total = total + got[k * size : (k + 1) * size]
    out[low + 3 * size : low + 4 * size, LANES : 2 * LANES] = total.astype(BF16)


def unpack_fast(n, inner, load, outs):
    glat, gft, gfs, gfp = outs
    low = glat.shape[1]
    for at in range(0, low, inner):
        glat[n, at : at + inner, :] = load(at, inner)
    for i in range(4):
        got = load(low + inner * i, inner)
        if i < 3:
            gft[n, i] = got[:, 0:LANES]
            for j in range(3):
                moved = got[:, LANES:] if j == 0 else pltpu.roll(got[:, LANES:], LANES - inner * j, 1)
                gfs[n, 3 * i + j] = moved[:, 0:inner]
        else:
            gfp[n] = got[:, LANES:]


def rows_of(one, two=None):
    def load(at, count):
        ref = one
        size = one.shape[1]
        if two is not None:
            core, rest = at // (8 * size), at % (8 * size)
            if rest >= 4 * size:
                ref, rest = two, rest - 4 * size
            at = core * 4 * size + rest
        block, row = at // size, at % size
        assert row + count <= size
        return ref[block, row : row + count, :].astype(F32)

    return load


def assemble_time(step, start, one, zero_one, zero_two, out):
    load = rows_of(zero_one, zero_two)
    for at in range(0, out.shape[1], step):
        out[0, at : at + step, :] = load(at, step)
        out[1, at : at + step, :] = one[start + at : start + at + step, :].astype(F32)


def assemble_space(start0, start1, one, zero_one, zero_two, out):
    load = rows_of(zero_one, zero_two)
    for at in range(0, out.shape[1], 256):
        out[0, at : at + 256, :] = load(start0 + at, 256)
        out[1, at : at + 256, :] = one[start1 + at : start1 + at + 256, :].astype(F32)


def assemble_point(start0, start1, one, zero_one, zero_two, out):
    load = rows_of(zero_one, zero_two)
    for at in range(0, out.shape[2], 256):
        out[0, :, at : at + 256] = load(start0 + at, 256)
        out[1, :, at : at + 256] = one[start1 + at : start1 + at + 256, :].astype(F32)


def assemble_fast(inner, one_one, one_two, zero, *outs):
    unpack_fast(1, inner, rows_of(one_one, one_two), outs)
    unpack_fast(0, inner, rows_of(zero), outs)


def join_pair(value, got, out):
    size = value.shape[0]
    out[0:size, :] = value[...]
    out[size : 2 * size, :] = got[...]


def assemble_norms(inner, *refs):
    sums, (gs, bs, gf, bf) = refs[:-4], refs[-4:]
    lanes = lax.broadcasted_iota(jnp.int32, (8, LANES), 1) >> (inner.bit_length() - 1)
    for n in range(2):
        slow, fast = sums[7 * n : 7 * n + 4], sums[7 * n + 4 : 7 * n + 7]
        for row, gslow, gfast in ((1, gs, gf), (0, bs, bf)):
            at = 0
            for part in slow:
                gslow[n : n + 1, at : at + part.shape[1]] = part[row : row + 1, :]
                at += part.shape[1]
            one, two, three = [jnp.broadcast_to(part[row : row + 1, :], (8, LANES)) for part in fast]
            three = pltpu.roll(three, 2 * inner, 1)
            head = jnp.where(lanes == 0, one, jnp.where(lanes == 1, two, three))
            gfast[n : n + 1, 0:LANES] = head[0:1]
            gfast[n : n + 1, LANES : LANES + 2 * inner] = three[0:1, 0 : 2 * inner]


def on_device(
    x_slow,
    x_fast,
    w_lateral,
    w_slow_time,
    w_slow_space,
    w_slow_point,
    w_fast_time,
    w_fast_space,
    w_fast_point,
    gain_slow,
    bias_slow,
    gain_fast,
    bias_fast,
    clip_size,
    cot_slow,
    cot_fast,
):
    frames, fast_frames = x_slow.shape[0], x_fast.shape[0]
    group = fast_frames // frames
    rows, cols = x_slow.shape[3], x_slow.shape[4]
    spots = rows * cols
    wide, fwide = x_slow.shape[5], x_fast.shape[5]
    lat = w_lateral.shape[3]
    width = w_slow_space.shape[3]
    inner = w_fast_space.shape[3]
    packs = group * fwide
    both = lat + LANES
    m = Masks(spots, cols)
    devices = lax.axis_size("path") * lax.axis_size("rows")
    path = lax.axis_index("path")
    ext = spots + 2 * cols
    lo1, lo2, lo3 = lat, lat + width, lat + 2 * width
    every = slice(None)

    def part(fn, *static):
        return functools.partial(fn, *static)

    xs = x_slow.reshape(frames, spots, wide)
    xf = x_fast.reshape(fast_frames, spots, fwide)
    cs = cot_slow.reshape(frames, spots, wide)
    cf = cot_fast.reshape(fast_frames, spots, fwide)
    wft = jnp.swapaxes(w_fast_time, 2, 3)
    wfs_raw = w_fast_space.reshape(2, 9, inner, inner)
    wsp = w_slow_space.reshape(2, 3, 3 * width, width)

    def packed(value):
        return jnp.concatenate(
            [value[:, 0:inner]] * group + [value[:, inner : 2 * inner]] * group + [value[:, 2 * inner :]],
            axis=1,
        )

    xf_edge = swap_path(jnp.where(path > 0, xf[:2], xf[-2:]))
    xs_edge = swap_path(jnp.where(path > 0, xs[0], xs[-1]))

    def payload(k, *sums):
        size = sum(k.temps[s[1]].shape[1] for s in sums)
        out = k.give((devices, 1, size))
        k.step(spread_sums, *sums, out)
        return out

    def row_out(k, z, mk, col0, size):
        out = k.give((frames, cols, size))
        k.step(part(own_row, m, spots, cols, col0, size), z, mk, out)
        return out

    def edge_out(k, z, mk, size, tail=0):
        out = k.give((spots, size), BF16)
        k.step(part(own_edge, m, 0, tail), z, mk, out)
        return out

    def finish(k, **handles):
        got = k.run()
        return {name: got[handle[1]] for name, handle in handles.items()}

    def other_row(value):
        return swap(value, "rows", 1)

    first_flops = 2 * frames * spots * 7 * fwide * both
    k = Stage("entry")
    mk_out = k.give((m.rows, LANES))
    place = jnp.stack([lax.axis_index("rows"), path]).astype(jnp.int32)
    k.step(
        part(make_masks, m, rows, cols, lax.axis_size("path") - 1), k.scalar(place), k.scalar(clip_size), mk_out
    )
    w7_out = k.give((7 * fwide, both), BF16)
    k.step(part(make_w7, lat, group), k.take(w_lateral, 0), k.take(wft, 0), w7_out)
    fw = k.give((fast_frames + 4, spots, fwide), BF16)
    y = k.give((frames, spots, both))
    sy = k.temp((1, 2 * both))
    edge = k.take(xf_edge)
    k.step(
        part(fast_entry, m, frames, group), k.take(xf), edge, edge, mk_out, w7_out, fw, y, sy, flops=first_flops
    )
    pay = payload(k, sy)
    got = finish(
        k, mk=mk_out, w7=w7_out, fw=fw, y=y, pay=pay, ff_row=row_out(k, y, mk_out, lat, LANES),
        edge=edge_out(k, y, mk_out, both),
    )
    mk = got["mk"]
    saved = [{"fw": got["fw"], "y": got["y"], "w7": got["w7"]}, {}]
    st = gather_sums(got["pay"])
    saved[0]["ff_row"] = other_row(got["ff_row"])
    saved[0]["y_edge"] = swap_path(got["edge"])
    mk, wft, gain_fast, bias_fast = lax.optimization_barrier((mk, wft, gain_fast, bias_fast))
    gf, bf = packed(gain_fast), packed(bias_fast)
    k = Stage("prepare")
    w7_out = k.give((7 * fwide, both), BF16)
    k.step(part(make_w7, lat, group), k.take(w_lateral, 1), k.take(wft, 1), w7_out)
    blocks = []
    for n in range(2):
        blocks += [k.give((3, 3 * LANES, LANES), BF16), k.give((LANES, packs), BF16)]
        k.step(part(make_blocks, group), k.take(wfs_raw, n), k.take(w_fast_point, n), *blocks[-2:])
    got = finish(k, w7=w7_out, wfs0=blocks[0], wfp0=blocks[1], wfs1=blocks[2], wfp1=blocks[3])
    saved[1]["w7"] = got["w7"]
    wfs, wfp = [got["wfs0"], got["wfs1"]], [got["wfp0"], got["wfp1"]]
    k = Stage("slow_partial")
    xm = k.give((frames + 2, spots, wide), BF16)
    fpart = k.give((frames, spots, width))
    edge = k.take(xs_edge)
    k.step(
        part(slow_partial, m, frames),
        k.take(xs), edge, edge, k.take(mk), k.take(w_slow_time, 0, every, slice(0, wide)), xm, fpart,
        flops=2 * frames * spots * 3 * wide * width,
    )
    got = finish(k, sw=xm, fpart=fpart)
    saved[0]["sw"] = got["sw"]
    fpart_in = got["fpart"]

    for n in range(2):
        v = saved[n]
        k = Stage("join")
        mk_in, gs, bs = k.take(mk), k.take(gain_slow), k.take(bias_slow)
        st_in = k.take(st)
        names = {}
        if n == 0:
            fpart = k.take(fpart_in)
        else:
            fpart = k.temp((frames, spots, width))
            names.update(
                slow1=k.give((frames, spots, wide)),
                sw=k.give((frames + 2, spots, wide), BF16),
            )
            n3 = k.give((2, wide))
            k.step(
                part(slow_next, m, 0, frames, lo3, 2 * both),
                st_in, k.take(saved[0]["third"]), k.take(saved[0]["sw"]),
                k.take(w_slow_time, 1, every, slice(0, wide)), gs, bs, mk_in,
                names["slow1"], names["sw"], fpart, n3,
                flops=2 * frames * spots * 3 * wide * width,
            )
            names["n3"] = n3
        y_in, edge = k.take(v["y"]), k.take(v["y_edge"])
        jl = k.give((frames, spots, lat), BF16)
        first = k.give((frames, spots, width))
        nl = k.give((2, lat))
        s_first, s_fs = k.temp((1, 2 * width)), k.temp((1, 2 * LANES))
        k.step(
            part(lat_join, m, n, frames, lat),
            st_in, y_in, edge, edge, fpart, k.take(w_slow_time, n, every, slice(wide, wide + lat)), gs, bs, mk_in,
            jl, first, s_first, nl, k.temp((frames + 2, spots, lat), BF16),
            flops=2 * frames * spots * 3 * lat * width,
        )
        fa1 = k.give((frames, ext, LANES), BF16)
        fs = k.give((frames, spots, LANES))
        nf1 = k.give((2, LANES))
        k.step(
            part(space_forward, m, n, frames, cols, 0, 2 * lat, LANES, lat, True, m.fast),
            st_in, y_in, k.take(v["ff_row"]), k.take(wfs[n]), k.take(gf), k.take(bf), mk_in,
            fa1, fs, s_fs, nf1, k.temp((frames, ext, 3 * LANES), BF16),
            flops=2 * frames * spots * 9 * LANES * LANES,
        )
        pay = payload(k, s_first, s_fs)
        got = finish(
            k, jl=jl, first=first, nl=nl, fa1=fa1, fs=fs, nf1=nf1, pay=pay,
            first_row=row_out(k, first, mk_in, 0, width), fs_row=row_out(k, fs, mk_in, 0, LANES),
            first_edge=edge_out(k, first, mk_in, width), **names,
        )
        st = gather_sums(got["pay"])
        for name in ("jl", "first", "nl", "fa1", "fs", "nf1"):
            v[name] = got[name]
        if n == 1:
            slow1, saved[1]["sw"], saved[0]["n3"] = got["slow1"], got["sw"], got["n3"]
        first_row = other_row(got["first_row"])
        v["fs_row"] = other_row(got["fs_row"])
        v["first_edge"] = swap_path(got["first_edge"])
        k = Stage("space")
        mk_in, st_in = k.take(mk), k.take(st)
        a1 = k.give((frames, ext, width), BF16)
        second = k.give((frames, spots, width))
        n1 = k.give((2, width))
        s_second, s_ft = k.temp((1, 2 * width)), k.temp((1, 2 * LANES))
        k.step(
            part(space_forward, m, n, frames, cols, lo1, 0, width, 0, False, m.slow),
            st_in, k.take(v["first"]), k.take(first_row), k.take(wsp, n), k.take(gain_slow), k.take(bias_slow), mk_in,
            a1, second, s_second, n1, k.temp((frames, ext, 3 * width), BF16),
            flops=2 * frames * spots * 9 * width * width,
        )
        fa2 = k.give((frames, spots, LANES), BF16)
        ft = k.give((frames, spots, packs))
        nf2 = k.give((2, LANES))
        k.step(
            part(fast_third, m, n, frames, LANES, 2 * width),
            st_in, k.take(v["fs"]), k.take(wfp[n]), k.take(gf), k.take(bf), mk_in, fa2, ft, s_ft, nf2,
            flops=2 * frames * spots * LANES * packs,
        )
        pay = payload(k, s_second, s_ft)
        names = {"second_row": row_out(k, second, mk_in, 0, width)}
        if n == 0:
            names["second_edge"] = edge_out(k, second, mk_in, width)
            names["ft_edge"] = edge_out(k, ft, mk_in, 2 * fwide, (group - 2) * fwide)
        got = finish(k, a1=a1, second=second, n1=n1, fa2=fa2, ft=ft, nf2=nf2, pay=pay, **names)
        st = gather_sums(got["pay"])
        for name in ("a1", "second", "n1", "fa2", "ft", "nf2"):
            v[name] = got[name]
        v["second_row"] = other_row(got["second_row"])
        halo = 1 - n
        edges = []
        k = Stage("third")
        if n == 0:
            ft_edge = k.take(swap_path(got["ft_edge"]))
            edges = [k.take(swap_path(got["second_edge"]))] * 2
        mk_in, st_in = k.take(mk), k.take(st)
        a2 = k.give((frames, spots, width), BF16)
        third = k.give((frames + 2 * halo, spots, wide))
        n2 = k.give((2, width))
        nf3 = k.give((2, LANES))
        s_third = k.temp((1, 2 * wide))
        names = {}
        if n == 0:
            names.update(
                f1=k.give((fast_frames, spots, fwide)),
                fw=k.give((fast_frames + 4, spots, fwide), BF16),
                y=k.give((frames, spots, both)),
            )
            s_fast = k.temp((1, 2 * both))
            k.step(
                part(fast_next, m, n, frames, group, 2 * LANES, 2 * width),
                st_in, k.take(v["ft"]), ft_edge, ft_edge, k.take(v["fw"]), k.take(saved[1]["w7"]),
                k.take(gf), k.take(bf), mk_in, names["f1"], names["fw"], names["y"], s_fast, nf3,
                flops=first_flops,
            )
        else:
            names.update(out_fast=k.give((fast_frames, spots, fwide)), pre_f=k.give((fast_frames, spots, fwide)))
            s_fast = k.temp((1, 2 * LANES))
            k.step(
                part(fast_last, m, n, frames, group, 2 * LANES, 2 * width),
                st_in, k.take(v["ft"]), k.take(fast1), k.take(cf), k.take(gf), k.take(bf), mk_in,
                names["out_fast"], names["pre_f"], s_fast, nf3,
            )
        k.step(
            part(slow_third, m, n, frames, lo2, halo),
            st_in, k.take(v["second"]), *edges, k.take(w_slow_point, n), k.take(gain_slow), k.take(bias_slow), mk_in,
            a2, third, s_third, n2, k.temp((frames + 2 * halo, spots, width), BF16),
            flops=2 * frames * spots * width * wide,
        )
        if n == 0:
            pay = payload(k, s_fast, s_third)
            names["ff_row"] = row_out(k, names["y"], mk_in, lat, LANES)
            names["y_edge"] = edge_out(k, names["y"], mk_in, both)
        else:
            pay = payload(k, s_third, s_fast)
        got = finish(k, a2=a2, third=third, n2=n2, nf3=nf3, pay=pay, **names)
        st = gather_sums(got["pay"])
        for name in ("a2", "third", "n2", "nf3"):
            v[name] = got[name]
        if n == 0:
            fast1 = got["f1"]
            saved[1].update(
                fw=got["fw"], y=got["y"], ff_row=other_row(got["ff_row"]), y_edge=swap_path(got["y_edge"])
            )
        else:
            out_fast, pre_f = got["out_fast"], got["pre_f"]

    def third_back(k, n, at, st_in, mk_in, pre):
        v = saved[n]
        d3, e2 = k.give((frames, spots, wide), BF16), k.give((frames, spots, width))
        s, gb = k.temp((1, 2 * width)), k.give((2, wide))
        k.step(
            part(slow_third_back, m, n, frames, lo3, lo2, at, 1 - n),
            st_in, k.take(pre), k.take(v["third"]), k.take(v["n3"]), k.take(v["second"]), k.take(v["n2"]),
            k.take(w_slow_point, n), k.take(gain_slow), k.take(bias_slow), mk_in, d3, e2, s, gb,
            flops=2 * frames * spots * width * wide,
        )
        return dict(d3=d3, e2=e2, gb3=gb), s

    def fast_back3(k, n, at, st_in, mk_in, pre):
        v = saved[n]
        d3, e2 = k.give((frames, spots, packs), BF16), k.give((frames, spots, LANES))
        s, gb = k.temp((1, 2 * LANES)), k.give((2, LANES))
        k.step(
            part(fast_third_back, m, n, frames, group, 2 * LANES, LANES, at),
            st_in, k.take(pre), k.take(v["ft"]), k.take(v["nf3"]), k.take(v["fs"]), k.take(v["nf2"]),
            k.take(wfp[n]), k.take(gf), k.take(bf), mk_in, d3, e2, s, gb,
            flops=2 * frames * spots * LANES * packs,
        )
        return dict(d3f=d3, ef2=e2, gbf3=gb), s

    def second_back(k, n, at, st_in, mk_in, e2, e2_row):
        v = saved[n]
        d2, e1 = k.give((frames, spots, width), BF16), k.give((frames, spots, width))
        s, gb = k.temp((1, 2 * width)), k.give((2, width))
        k.step(
            part(space_back, m, n, frames, cols, lo2, lo1, at, width, 0, False, m.slow),
            st_in, k.take(e2), k.take(e2_row), k.take(v["second"]), k.take(v["second_row"]), k.take(v["n2"]),
            k.take(v["first"]), k.take(v["n1"]), k.take(wsp, n), k.take(gain_slow), k.take(bias_slow), mk_in,
            d2, e1, s, gb, k.temp((frames, ext, 3 * width), BF16),
            flops=2 * frames * spots * 9 * width * width,
        )
        return dict(d2=d2, e1=e1, gb2=gb), s

    def fast_back2(k, n, at, st_in, mk_in, ef2, ef2_row):
        v = saved[n]
        d2, e1 = k.give((frames, spots, LANES), BF16), k.give((frames, spots, LANES))
        s, gb = k.temp((1, 2 * LANES)), k.give((2, LANES))
        k.step(
            part(space_back, m, n, frames, cols, LANES, 0, at, LANES, lat, True, m.fast),
            st_in, k.take(ef2), k.take(ef2_row), k.take(v["fs"]), k.take(v["fs_row"]), k.take(v["nf2"]),
            k.take(v["y"]), k.take(v["nf1"]), k.take(wfs[n]), k.take(gf), k.take(bf), mk_in,
            d2, e1, s, gb, k.temp((frames, ext, 3 * LANES), BF16),
            flops=2 * frames * spots * 9 * LANES * LANES,
        )
        return dict(d2f=d2, ef1=e1, gbf2=gb), s

    def first_back(k, n, st_in, mk_in, e1, e1_edge, pre):
        v = saved[n]
        last = n == 0
        dw, el = k.give((frames + 2, spots, width), BF16), k.give((frames, spots, lat))
        s, gb = k.temp((1, 2 * lat)), k.give((2, width))
        down = k.give((frames, spots, wide))
        edge, zedge = k.take(e1_edge), k.take(v["first_edge"])
        args = [
            st_in, k.take(e1), edge, edge, k.take(v["first"]), zedge, zedge, k.take(v["n1"]),
            k.take(w_slow_time, n), k.take(v["y"]), k.take(v["nl"]), k.take(pre),
        ]
        outs = [dw, el, s, down]
        sums = [s]
        if not last:
            args += [k.take(saved[0]["sw"]), k.take(saved[0]["third"]), k.take(saved[0]["n3"])]
            sums.append(k.temp((1, 2 * wide)))
            outs.append(sums[1])
        k.step(
            part(slow_first_back, m, n, frames, lo1, lo3, 0, 1, last),
            *args, k.take(gain_slow), k.take(bias_slow), mk_in, *outs, gb,
            flops=2 * frames * spots * 3 * (wide + lat) * width,
        )
        return dict(dw=dw, el=el, down=down, gb1=gb), sums

    def fast_back1(k, n, st1, at1, stl, atl, mk_in, el, el_edge, ef1, ef1_edge, pre):
        v = saved[n]
        last = n == 0
        dl, df = k.give((frames, spots, lat), BF16), k.give((frames, spots, LANES), BF16)
        down = k.give((fast_frames, spots, fwide))
        gbl, gb1 = k.give((2, lat)), k.give((2, LANES))
        edge, yedge = k.take(ef1_edge), k.take(v["y_edge"])
        args = [
            st1, stl, k.take(el), k.take(el_edge), k.take(ef1), edge, edge, k.take(v["y"]), yedge, yedge,
            k.take(v["nl"]), k.take(v["nf1"]), k.take(v["w7"]), k.take(pre),
        ]
        outs = [dl, df, down]
        s = None
        if not last:
            args += [k.take(saved[0]["fw"]), k.take(saved[0]["ft"]), k.take(saved[0]["nf3"])]
            s = k.temp((1, 2 * LANES))
            outs.append(s)
        k.step(
            part(fast_first_back, m, n, frames, group, 0, 2 * LANES, at1, atl, last),
            *args, k.take(gain_slow), k.take(gf), k.take(bf), mk_in, *outs, gbl, gb1,
            k.temp((fast_frames + 4, spots, fwide)),
            flops=first_flops,
        )
        return dict(dl=dl, df=df, downf=down, gbl=gbl, gbf1=gb1), s

    def weights_point(n, d3):
        k = Stage("point_weights")
        out = k.give((wide // 256, width, 256), BF16)
        k.step(point_weights, k.take(saved[n]["a2"]), k.take(d3), out, flops=2 * frames * spots * width * wide)
        return k.run()[0].reshape(-1, 256)

    def weights_space(n, d2):
        k = Stage("space_weights")
        out = k.give((3, 3 * width, width), BF16)
        k.step(
            part(space_weights, cols), k.take(saved[n]["a1"]), k.take(d2), out,
            k.temp((frames, ext, 3 * width), BF16), flops=2 * frames * spots * 9 * width * width,
        )
        return k.run()[0].reshape(-1, 256)

    def weights_time(n, dw):
        k = Stage("time_weights")
        out = k.give((3, wide + lat, width), BF16)
        k.step(
            part(time_weights, 1), k.take(saved[n]["sw"]), k.take(saved[n]["jl"]), k.take(dw), out,
            flops=2 * frames * spots * 3 * (wide + lat) * width,
        )
        return k.run()[0].reshape(-1, 256)

    def weights_fast(n, dl, df, d2, d3):
        v = saved[n]
        k = Stage("fast_weights")
        out = k.give((7 * LANES - LANES, 2 * LANES), BF16)
        k.step(
            part(fast_weights, group, cols, lat),
            k.take(v["fw"]), k.take(dl), k.take(df), k.take(v["fa1"]), k.take(d2), k.take(v["fa2"]), k.take(d3),
            out, k.temp((frames, ext, 3 * LANES), BF16), flops=first_flops,
        )
        return k.run()[0]

    b1, b0 = {}, {}
    k = Stage("last")
    mk_in, st_in = k.take(mk), k.take(st)
    out_slow, pre = k.give((frames, spots, wide)), k.give((frames, spots, wide))
    n3 = k.give((2, wide))
    s_pre = k.temp((1, 2 * wide))
    k.step(
        part(slow_last, m, 1, frames, lo3),
        st_in, k.take(saved[1]["third"]), k.take(slow1), k.take(cs), k.take(gain_slow), k.take(bias_slow), mk_in,
        out_slow, pre, s_pre, n3,
    )
    names, s_ef2 = fast_back3(k, 1, 2 * wide, st_in, mk_in, pre_f)
    pay = payload(k, s_pre, s_ef2)
    ef2_row = row_out(k, names["ef2"], mk_in, 0, LANES)
    b1 = finish(k, out_slow=out_slow, pre=pre, n3=n3, pay=pay, ef2_row=ef2_row, **names)
    saved[1]["n3"] = b1["n3"]
    out_slow = b1["out_slow"]
    st = gather_sums(b1["pay"])

    k = Stage("back_third")
    ef2_row = other_row(b1["ef2_row"])
    mk_in, st_in = k.take(mk), k.take(st)
    names, s_e2 = third_back(k, 1, 0, st_in, mk_in, b1["pre"])
    more, s_ef1 = fast_back2(k, 1, 2 * wide, st_in, mk_in, b1["ef2"], ef2_row)
    pay = payload(k, s_e2, s_ef1)
    e2_row, ef1_edge = row_out(k, names["e2"], mk_in, 0, width), edge_out(k, more["ef1"], mk_in, LANES)
    b1.update(finish(k, pay=pay, e2_row=e2_row, ef1_edge=ef1_edge, **names, **more))
    st = st_ef1 = gather_sums(b1["pay"])
    e2_row, ef1_edge = other_row(b1["e2_row"]), swap_path(b1["ef1_edge"])
    point1 = weights_point(1, b1["d3"])

    k = Stage("back_space")
    mk_in, st_in = k.take(mk), k.take(st)
    names, s_e1 = second_back(k, 1, 0, st_in, mk_in, b1["e2"], e2_row)
    pay = payload(k, s_e1)
    e1_edge = edge_out(k, names["e1"], mk_in, width)
    b1.update(finish(k, pay=pay, e1_edge=e1_edge, **names))
    st = gather_sums(b1["pay"])
    e1_edge = swap_path(b1["e1_edge"])
    space1 = weights_space(1, b1["d2"])

    k = Stage("back_first")
    mk_in, st_in = k.take(mk), k.take(st)
    names, sums = first_back(k, 1, st_in, mk_in, b1["e1"], e1_edge, b1["pre"])
    pay = payload(k, *sums)
    el_edge = edge_out(k, names["el"], mk_in, lat)
    b1.update(finish(k, pay=pay, el_edge=el_edge, **names))
    st = gather_sums(b1["pay"])
    el_edge = swap_path(b1["el_edge"])
    time1 = weights_time(1, b1["dw"])
    sizes1 = [point1.shape[0], space1.shape[0], time1.shape[0]]
    ones = jnp.concatenate([point1, space1, time1], axis=0)
    ones = lax.psum(ones, AXES)

    SUMS = ("gbl", "gb1", "gb2", "gb3", "gbf1", "gbf2", "gbf3")
    steps = exchange_steps()
    core, across, down = steps[:3]
    seen = {}

    def block_zero(st=st, el_edge=el_edge, ef1_edge=ef1_edge, b1=b1, b0=b0):
        b1, b0 = dict(b1), dict(b0)
        k = Stage("back_third")
        mk_in, st_in = k.take(mk), k.take(st)
        names, s_e2 = third_back(k, 0, 2 * lat, st_in, mk_in, b1["down"])
        more, s_pf = fast_back1(
            k, 1, k.take(st_ef1), 2 * width, st_in, 0, mk_in, b1["el"], el_edge, b1["ef1"], ef1_edge, pre_f
        )
        pay = payload(k, s_e2, s_pf)
        e2_row = row_out(k, names["e2"], mk_in, 0, width)
        got = finish(k, pay=pay, e2_row=e2_row, **names, **more)
        for name in more:
            b1[name] = got[name]
        b0.update({name: got[name] for name in names})
        st = gather_sums(got["pay"])
        e2_row = other_row(got["e2_row"])
        point0 = weights_point(0, b0["d3"])
        fast_1 = weights_fast(1, b1["dl"], b1["df"], b1["d2f"], b1["d3f"])

        k = Stage("back_space")
        mk_in, st_in = k.take(mk), k.take(st)
        names, s_e1 = second_back(k, 0, 0, st_in, mk_in, b0["e2"], e2_row)
        more, s_ef2 = fast_back3(k, 0, 2 * width, st_in, mk_in, b1["downf"])
        pay = payload(k, s_e1, s_ef2)
        e1_edge, ef2_row = edge_out(k, names["e1"], mk_in, width), row_out(k, more["ef2"], mk_in, 0, LANES)
        b0.update(finish(k, pay=pay, e1_edge=e1_edge, ef2_row=ef2_row, **names, **more))
        st = gather_sums(b0["pay"])
        e1_edge, ef2_row = swap_path(b0["e1_edge"]), other_row(b0["ef2_row"])
        space0 = weights_space(0, b0["d2"])
        mid = halve(jnp.concatenate([fast_1, point0, space0], axis=0), *core)

        k = Stage("back_first")
        mk_in, st_in = k.take(mk), k.take(st)
        names, sums = first_back(k, 0, st_in, mk_in, b0["e1"], e1_edge, b1["down"])
        more, s_ef1 = fast_back2(k, 0, 2 * width, st_in, mk_in, b0["ef2"], ef2_row)
        pay = payload(k, *sums, s_ef1)
        el_edge, ef1_edge = edge_out(k, names["el"], mk_in, lat), edge_out(k, more["ef1"], mk_in, LANES)
        b0.update(finish(k, pay=pay, el_edge=el_edge, ef1_edge=ef1_edge, **names, **more))
        pay, mid = lax.optimization_barrier((b0["pay"], mid))
        st = gather_sums(pay)
        el_edge, ef1_edge = swap_path(b0["el_edge"]), swap_path(b0["ef1_edge"])
        mid = halve_both(*parted(mid), across, down)
        time0 = weights_time(0, b0["dw"])
        late = halve(time0, *core)
        st, mid = lax.optimization_barrier((st, mid))
        mid = halve_both(*mid, down, across)

        k = Stage("back_fast")
        mk_in, st_in = k.take(mk), k.take(st)
        more, _ = fast_back1(
            k, 0, st_in, 2 * lat, st_in, 0, mk_in, b0["el"], el_edge, b0["ef1"], ef1_edge, b1["downf"]
        )
        b0.update(finish(k, **more))
        dl0, mid, late = lax.optimization_barrier((b0["dl"], mid, late))
        late = halve_both(*parted(late), across, down)
        rest = weights_fast(0, dl0, b0["df"], b0["d2f"], b0["d3f"])
        rest = halve(rest, *core)
        late, rest = lax.optimization_barrier((late, rest))
        late = halve_both(*late, down, across)
        rest = halve(halve(rest, *across), *down)
        seen["parts"] = parts = [mid[0].shape[0], late[0].shape[0], rest.shape[0], mid[1].shape[0], late[1].shape[0]]
        value = jnp.concatenate([mid[0], late[0], rest, mid[1], late[1]], axis=0)
        for step in steps[3:]:
            value = halve(value, *step)
        value = value.astype(BF16)
        for step in reversed(steps[3:]):
            value = double(value, *step)
        cut = sum(parts[:3])
        one, two = value[:cut], value[cut:]
        one, two = [one, swap(one, *down)], [two, swap(two, *across)]
        one, two = [jnp.concatenate(pair, axis=0) for pair in (one, two)]
        one, two = [one, swap(one, *across)], [two, swap(two, *down)]
        joined = []
        for pair in (one, two):
            k = Stage("join_rows")
            out = k.give((2 * pair[0].shape[0], 256), BF16)
            k.step(join_pair, *[k.take(half) for half in pair], out)
            joined.append(k.run()[0])
        seen["fast"], seen["point"] = fast_1.shape[0], point0.shape[0]
        halves = [half for half in joined] + [swap(half, *core) for half in joined]
        sums = [b0[name] for name in SUMS] + [b1[name] for name in ("gbl", "gbf1")]
        return tuple(halves) + (b0["down"], b0["downf"]) + tuple(sums)

    like = jax.eval_shape(block_zero)
    got = lax.cond(
        clip_size[0, 0] > 0, block_zero, lambda: tuple(jnp.zeros(o.shape, o.dtype) for o in like)
    )
    one, two = (got[0], got[2]), (got[1], got[3])
    gx_slow, gx_fast = got[4:6]
    parts = seen["parts"]
    cut = sum(parts[:3])
    b0 = dict(zip(SUMS, got[6:13]))
    b1["gbl"], b1["gbf1"] = got[13:15]
    core_bit = lax.axis_index("rows") % 2
    down_bit = (lax.axis_index("rows") // 2) % 2

    k = Stage("assemble")
    flip_one = k.scalar((core_bit * 4 + path * 2 + down_bit).astype(jnp.int32).reshape(1))
    flip_two = k.scalar((core_bit * 4 + down_bit * 2 + path).astype(jnp.int32).reshape(1))
    one = [half.reshape(4, -1, 256) for half in one]
    two = [half.reshape(4, -1, 256) for half in two]
    ends = [0, parts[0], parts[0] + parts[1], cut]
    late_one = k.take_blocks(*one, flip_one, slice(ends[1], ends[2]))
    late_two = k.take_blocks(*two, flip_two, slice(parts[3], parts[3] + parts[4]))
    mid_one = k.take_blocks(*one, flip_one, slice(ends[0], ends[1]))
    mid_two = k.take_blocks(*two, flip_two, slice(0, parts[3]))
    rest = k.take_blocks(*one, flip_one, slice(ends[2], ends[3]))
    ones_in = k.take(ones)
    gtime = k.give((2, 3 * (wide + lat), width))
    k.step(part(assemble_time, 80, sizes1[0] + sizes1[1]), ones_in, late_one, late_two, gtime)
    start = seen["fast"]
    gpoint = k.give((2, width, wide))
    k.step(part(assemble_point, start, 0), ones_in, mid_one, mid_two, gpoint)
    gspace = k.give((2, 9 * width, width))
    k.step(part(assemble_space, start + seen["point"], sizes1[0]), ones_in, mid_one, mid_two, gspace)
    fast_outs = [
        k.give((2, 5 * fwide, lat)), k.give((2, 3, inner, fwide)), k.give((2, 9, inner, inner)),
        k.give((2, inner, fwide)),
    ]
    k.step(part(assemble_fast, inner), mid_one, mid_two, rest, *fast_outs)
    sums = [k.take(b[name]) for b in (b0, b1) for name in ("gbl", "gb1", "gb2", "gb3", "gbf1", "gbf2", "gbf3")]
    norm_outs = [k.give(like.shape) for like in (gain_slow, bias_slow, gain_fast, bias_fast)]
    k.step(part(assemble_norms, inner), *sums, *norm_outs)
    got = k.run()
    glat, gft, gfs, gfp = [got[h[1]] for h in fast_outs]

    return (
        out_slow.reshape(x_slow.shape),
        out_fast.reshape(x_fast.shape),
        gx_slow.reshape(x_slow.shape),
        gx_fast.reshape(x_fast.shape),
        glat.reshape(w_lateral.shape),
        got[gtime[1]].reshape(w_slow_time.shape),
        got[gspace[1]].reshape(w_slow_space.shape),
        got[gpoint[1]],
        jnp.swapaxes(gft, 2, 3),
        gfs.reshape(w_fast_space.shape),
        gfp,
        *[got[h[1]] for h in norm_outs],
    )


def solution(mesh):
    spread = P("path", None, "rows", None, None, None)
    return jax.shard_map(
        on_device,
        mesh=mesh,
        in_specs=(spread, spread) + (P(),) * 12 + (spread, spread),
        out_specs=(spread,) * 4 + (P(),) * 11,
        check_vma=False,
    )
```

```python
import functools

import jax
import jax.numpy as jnp
import numpy as np
from jax import lax
from jax.experimental import pallas as pl
from jax.experimental.pallas import tpu as pltpu
from jax.sharding import PartitionSpec as P

TS = 8
TF = 32
F32 = jnp.float32
BF16 = jnp.bfloat16
EPSILON = 1e-05
LANES = 128
AXES = ("path", "rows")
VMEM_LIMIT = 56 * 2**20


def swap(value, axis, stride):
    pairs = [(source, source ^ stride) for source in range(lax.axis_size(axis))]
    return lax.ppermute(value, axis, pairs)


def gather_sums(spread):
    return lax.all_to_all(spread, AXES, 0, 0, tiled=True)


def swap_path(value):
    assert lax.axis_size("path") == 2
    return lax.ppermute(value, "path", [(0, 1), (1, 0)])


def exchange_steps():
    steps = [("rows", 1), ("path", 1)]
    stride = 2
    while stride < lax.axis_size("rows"):
        steps.append(("rows", stride))
        stride *= 2
    return steps


def halve(value, axis, stride):
    size = value.shape[0] // 2
    upper = (lax.axis_index(axis) // stride) % 2
    keep = lax.dynamic_slice_in_dim(value, upper * size, size, 0)
    give = lax.dynamic_slice_in_dim(value, (1 - upper) * size, size, 0)
    return keep.astype(F32) + swap(give.astype(BF16), axis, stride).astype(F32)


def double(value, axis, stride):
    upper = (lax.axis_index(axis) // stride) % 2
    got = swap(value, axis, stride)
    return jnp.concatenate(
        [jnp.where(upper == 0, value, got), jnp.where(upper == 0, got, value)], axis=0
    )


def halve_both(one, two, first, second):
    return halve(one, *first), halve(two, *second)


def parted(value):
    size = value.shape[0] // 2
    return value[:size], value[size:]


class Stage:
    def __init__(self, name):
        self.name = name
        self.arrays, self.views, self.scalars, self.pairs = [], [], [], []
        self.outs, self.temps, self.steps = [], [], []
        self.entries, self.ontos = [], []
        self.flops = 0

    def take(self, array, *view):
        for at, known in enumerate(self.arrays):
            if known is array:
                break
        else:
            at = len(self.arrays)
            self.arrays.append(array)
        for k, (other, seen) in enumerate(self.views):
            if other == at and seen == view:
                return ("in", k)
        self.views.append((at, view))
        return ("in", len(self.views) - 1)

    def take_blocks(self, values, flip, rows):
        self.pairs.append(([self.take(value, slice(None), rows) for value in values], flip))
        return ("pair", len(self.pairs) - 1)

    def scalar(self, array):
        self.scalars.append(array)
        return ("scalar", len(self.scalars) - 1)

    def give(self, dims, dtype=F32, at=None, onto=None):
        self.outs.append(jax.ShapeDtypeStruct(tuple(dims), dtype))
        self.entries.append(at)
        self.ontos.append(onto)
        return ("out", len(self.outs) - 1)

    def temp(self, dims, dtype=F32):
        self.temps.append(pltpu.VMEM(tuple(dims), dtype))
        return ("temp", len(self.temps) - 1)

    def step(self, fn, *handles, flops=0):
        self.flops += flops
        self.steps.append((fn, handles))

    def sem(self, view, block):
        return 8 * view + block

    def view_shape(self, view):
        at, index = view
        return np.broadcast_to(np.zeros((), np.int8), self.arrays[at].shape)[index].shape

    def run(self):
        arrays, views, outs, steps, pairs = self.arrays, self.views, self.outs, self.steps, self.pairs
        order, home = [], {}
        for k, (members, flip) in enumerate(pairs):
            for j, member in enumerate(members):
                home[member[1]] = (k, j, flip)
        under = [onto for onto in self.ontos if onto is not None]

        def need(handle):
            if handle[0] == "in":
                return [handle[1]]
            return [part[1] for part in pairs[handle[1]][0]] if handle[0] == "pair" else []

        for _, handles in steps:
            for handle in handles:
                for k in need(handle):
                    if k not in order:
                        order.append(k)

        def body(*refs):
            refs = list(refs)

            def cut(count):
                taken = refs[:count]
                del refs[:count]
                return taken

            scalars, hbm_in = cut(len(self.scalars)), cut(len(arrays))
            cut(len(under))
            hbm_out = cut(len(outs))
            alone = [k for k in range(len(views)) if k not in home]
            held = dict(zip(alone, cut(len(alone))))
            joint, made, temps, (sems,) = cut(len(pairs)), cut(len(outs)), cut(len(self.temps)), refs
            copies = {}
            for k in order:
                at, index = views[k]
                src = hbm_in[at].at[index] if index else hbm_in[at]
                if k in home:
                    pair, second, flip = home[k]
                    count = self.view_shape(views[k])[0]
                    copies[k] = []
                    for block in range(count):
                        to = (second * count + block) ^ scalars[flip[1]][0]
                        copies[k].append(
                            pltpu.make_async_copy(src.at[block], joint[pair].at[to], sems.at[self.sem(k, block)])
                        )
                else:
                    copies[k] = [pltpu.make_async_copy(src, held[k], sems.at[self.sem(k, 0)])]
                for copy in copies[k]:
                    copy.start()
            waited, sent = set(), {}
            for fn, handles in steps:
                given = []
                for handle in handles:
                    for k in need(handle):
                        if k not in waited:
                            for copy in copies[k]:
                                copy.wait()
                            waited.add(k)
                    place = {"in": held, "pair": joint, "out": made, "temp": temps, "scalar": scalars}
                    given.append(place[handle[0]][handle[1]])
                fn(*given)
                for kind, k in handles:
                    if kind == "out" and k not in sent:
                        to = hbm_out[k] if self.entries[k] is None else hbm_out[k].at[self.entries[k]]
                        sent[k] = pltpu.make_async_copy(made[k], to, sems.at[8 * len(views) + k])
                        sent[k].start()
            for copy in sent.values():
                copy.wait()

        moved = sum(a.size * a.dtype.itemsize for a in outs)
        for view in views:
            moved += int(np.prod(self.view_shape(view))) * arrays[view[0]].dtype.itemsize
        scratch = [
            pltpu.VMEM(self.view_shape(view), arrays[view[0]].dtype) for k, view in enumerate(views) if k not in home
        ]
        for members, _ in pairs:
            size = self.view_shape(views[members[0][1]])
            scratch.append(
                pltpu.VMEM((len(members) * size[0],) + size[1:], arrays[views[members[0][1]][0]].dtype)
            )
        scratch += [
            pltpu.VMEM(o.shape if at is None else o.shape[1:], o.dtype) for o, at in zip(outs, self.entries)
        ]
        aliases = {}
        for k, onto in enumerate(self.ontos):
            if onto is not None:
                aliases[len(self.scalars) + len(arrays) + len(aliases)] = k
        scratch += self.temps + [pltpu.SemaphoreType.DMA((8 * len(views) + len(outs),))]
        return pl.pallas_call(
            body,
            out_shape=tuple(outs),
            in_specs=[pl.BlockSpec(memory_space=pltpu.SMEM) for _ in self.scalars]
            + [pl.BlockSpec(memory_space=pl.ANY) for _ in arrays + under],
            out_specs=tuple(pl.BlockSpec(memory_space=pl.ANY) for _ in outs),
            scratch_shapes=scratch,
            input_output_aliases=aliases,
            compiler_params=pltpu.CompilerParams(vmem_limit_bytes=VMEM_LIMIT),
            cost_estimate=pl.CostEstimate(flops=self.flops, bytes_accessed=moved, transcendentals=0),
            name=self.name,
        )(*self.scalars, *arrays, *under)


class Masks:
    def __init__(self, spots, cols):
        self.main = (0, spots)
        self.ext = (spots, 2 * spots + 2 * cols)
        self.prev = (2 * spots + 2 * cols, 3 * spots + 2 * cols)
        self.next = (3 * spots + 2 * cols, 4 * spots + 2 * cols)
        self.slow = (4 * spots + 2 * cols, 4 * spots + 2 * cols + 8)
        self.fast = (4 * spots + 2 * cols + 8, 4 * spots + 2 * cols + 16)
        self.half = (4 * spots + 2 * cols + 16, 4 * spots + 2 * cols + 24)
        self.path = (4 * spots + 2 * cols + 24, 4 * spots + 2 * cols + 32)
        self.rows = 4 * spots + 2 * cols + 32


def make_masks(m, rows, cols, last, place, clips, mk):
    half = place[0] % 2
    path = place[1]
    side = clips[0, place[0] // 2]
    area = 0
    for k in range(clips.shape[1]):
        area = area + clips[0, k] * clips[0, k]
    shift = cols.bit_length() - 1

    def inside(first, count):
        at = lax.broadcasted_iota(jnp.int32, (count * cols, LANES), 0)
        line = half * rows + first + (at >> shift)
        spot = at & (cols - 1)
        good = (line >= 0) & (line < 2 * rows) & (line < side) & (spot < side)
        return jnp.where(good, 1.0, 0.0)

    main = inside(0, rows)
    mk[m.main[0] : m.main[1], :] = main
    mk[m.ext[0] : m.ext[1], :] = inside(-1, rows + 2)
    mk[m.prev[0] : m.prev[1], :] = main * jnp.where(path > 0, 1.0, 0.0)
    mk[m.next[0] : m.next[1], :] = main * jnp.where(path < last, 1.0, 0.0)

    def fill(span, value):
        mk[span[0] : span[1], :] = jnp.full((8, LANES), value, F32)

    fill(m.slow, TS * area.astype(F32))
    fill(m.fast, TF * area.astype(F32))
    fill(m.half, half.astype(F32))
    fill(m.path, path.astype(F32))


def own_row(m, spots, cols, col0, width, z, mk, row):
    for t in range(z.shape[0]):
        lower = mk[m.half[0] : m.half[0] + 1, :] > 0.5
        for lane in range(0, width, LANES):
            at = col0 + lane
            row[t, :, lane : lane + LANES] = jnp.where(
                lower, z[t, 0:cols, at : at + LANES], z[t, spots - cols : spots, at : at + LANES]
            )


def own_edge(m, lead, tail, z, mk, edge):
    frames = z.shape[0]
    second = mk[m.path[0] : m.path[0] + 1, :] > 0.5
    for lane in range(0, edge.shape[1], LANES):
        edge[:, lane : lane + LANES] = jnp.where(
            second,
            z[0, :, lead + lane : lead + lane + LANES],
            z[frames - 1, :, tail + lane : tail + lane + LANES],
        ).astype(edge.dtype)


def spread_sums(*refs):
    parts, out = refs[:-1], refs[-1]
    row = jnp.concatenate([part[...] for part in parts], axis=1)
    out[...] = jnp.broadcast_to(row[None], out.shape)


def make_w7(lat, group, wl, wf, w7):
    inner = wf.shape[1]
    w7[...] = jnp.zeros(w7.shape, BF16)
    for j in range(wl.shape[0]):
        w7[j * LANES : (j + 1) * LANES, 0:lat] = wl[j]
    at = lax.broadcasted_iota(jnp.int32, (inner, LANES), 0)
    lane = lax.broadcasted_iota(jnp.int32, (inner, LANES), 1)
    places = [jnp.where(lane == at + inner * k, 1.0, 0.0).astype(BF16) for k in range(group)]
    for f in range(1, group + 3):
        used = [k for k in range(group) if 0 <= f - 1 - k < 3]
        got = None
        for k in used:
            more = dot_tn(wf[f - 1 - k], places[k])
            got = more if got is None else got + more
        w7[f * LANES : (f + 1) * LANES, lat : lat + LANES] = got.astype(BF16)


def make_blocks(group, ws, wp, wfs, wfp):
    inner = wp.shape[0]
    at = lax.broadcasted_iota(jnp.int32, (inner, LANES), 0)
    lane = lax.broadcasted_iota(jnp.int32, (inner, LANES), 1)
    tile = jnp.where((lane & (inner - 1)) == at, 1.0, 0.0).astype(BF16)
    shift = inner.bit_length() - 1
    for tap in range(ws.shape[0]):
        got = dot(ws[tap], tile)
        for k in range(group):
            kept = jnp.where((lane >> shift) == k, got, 0.0).astype(BF16)
            row = (tap % 3) * LANES + k * inner
            wfs[tap // 3, row : row + inner, :] = kept
    wfp[...] = jnp.zeros(wfp.shape, BF16)
    for k in range(group):
        wfp[k * inner : (k + 1) * inner, k * LANES : (k + 1) * LANES] = wp[...]


def widen(rows, width):
    return jnp.concatenate([rows] * (width // LANES), axis=1)


def sublane_sums(value):
    return jnp.sum(value.reshape(value.shape[0] // 8, 8, value.shape[1]), axis=0)


def row_sum(value):
    return jnp.sum(value, axis=0, keepdims=True)


def fold_packed(row):
    full = jnp.broadcast_to(row, (8, LANES))
    full = full + pltpu.roll(full, 64, 1)
    full = full + pltpu.roll(full, 32, 1)
    return full[0:1]


def totals(st, lo, width, packed=False):
    first = jnp.sum(st[:, :, lo : lo + width], axis=0)
    second = jnp.sum(st[:, :, lo + width : lo + 2 * width], axis=0)
    if packed:
        return fold_packed(first), fold_packed(second)
    return first, second


def norm_rows(st, lo, width, count, packed=False):
    first, second = totals(st, lo, width, packed)
    mean = first / count
    return mean, lax.rsqrt(second / count - mean * mean + EPSILON)


def sigmoid(value):
    return 0.5 * jnp.tanh(0.5 * value) + 0.5


def silu(value):
    return value * sigmoid(value)


def silu_slope(value):
    sigma = sigmoid(value)
    return sigma * (1.0 + value * (1.0 - sigma))


def dot(a, b):
    return jnp.dot(a, b, preferred_element_type=F32)


def dot_nt(a, b):
    return lax.dot_general(a, b, (((1,), (1,)), ((), ())), preferred_element_type=F32)


def dot_tn(a, b):
    return lax.dot_general(a, b, (((0,), (0,)), ((), ())), preferred_element_type=F32)


def flat(value):
    return value.reshape(value.shape[0] * value.shape[1], value.shape[2])


def store_shifts(dst, t, value, cols):
    rows, width = value.shape
    spot = lax.broadcasted_iota(jnp.int32, (rows, width), 0) & (cols - 1)
    left = jnp.where(spot == 0, 0.0, pltpu.roll(value, 1, 0))
    right = jnp.where(spot == cols - 1, 0.0, pltpu.roll(value, rows - 1, 0))
    dst[t, :, 0:width] = left.astype(BF16)
    dst[t, :, width : 2 * width] = value.astype(BF16)
    dst[t, :, 2 * width : 3 * width] = right.astype(BF16)


def taps_of(frames_ref, frames, group):
    return jnp.concatenate(
        [
            jnp.concatenate([frames_ref[group * t + f] for f in range(7)], axis=1)
            for t in range(frames)
        ],
        axis=0,
    )


def entry_sums(y, lat, frames, spots):
    width = y.shape[1]
    one = jnp.zeros((8, width), F32)
    two = jnp.zeros((8, width), F32)
    for t in range(frames):
        part = y[t * spots : (t + 1) * spots]
        one = one + sublane_sums(part)
        two = two + sublane_sums(part * part)
    one = row_sum(one)
    two = row_sum(two)
    return jnp.concatenate([one[:, :lat], two[:, :lat], one[:, lat:], two[:, lat:]], axis=1)


def fast_entry(m, frames, group, x, before, after, mk, w7, fw, y, s):
    spots = x.shape[1]
    count = x.shape[0]

    def put(at, value, span):
        fw[at] = (value.astype(F32) * mk[span[0] : span[1], :]).astype(BF16)

    for k in range(2):
        put(k, before[k], m.prev)
        put(2 + count + k, after[k], m.next)
    for k in range(count):
        put(2 + k, x[k], m.main)
    out = dot(taps_of(fw, frames, group), w7[...])
    for t in range(frames):
        y[t] = out[t * spots : (t + 1) * spots]
    s[...] = entry_sums(out, w7.shape[1] - LANES, frames, spots)


def slow_partial(m, frames, x, before, after, mk, wt, xm, fpart):
    spots, wide = x.shape[1], x.shape[2]
    sources = [(before, m.prev)] + [(x.at[t], m.main) for t in range(frames)] + [(after, m.next)]
    for k, (src, span) in enumerate(sources):
        for lo in range(0, wide, 256):
            mask = widen(mk[span[0] : span[1], :], 256)
            xm[k, :, lo : lo + 256] = (src[:, lo : lo + 256].astype(F32) * mask).astype(BF16)
    out = dot(flat(xm[0:frames]), wt[0, :wide, :])
    for j in range(1, 3):
        out = out + dot(flat(xm[j : j + frames]), wt[j, :wide, :])
    for t in range(frames):
        fpart[t] = out[t * spots : (t + 1) * spots]


def lat_join(m, n, frames, lat, st, y, before, after, fpart, wt, gs, bs, mk, jl, first, s, nl, jw):
    spots = y.shape[1]
    wide = wt.shape[1] - lat
    count = widen(mk[m.slow[0] : m.slow[0] + 1, :], lat)
    mean, rstd = norm_rows(st, 0, lat, count)
    nl[0:1, :] = mean
    nl[1:2, :] = rstd
    scale = rstd * gs[n : n + 1, 0:lat]
    bias = bs[n : n + 1, 0:lat]
    sources = (
        [(before[:, 0:lat], m.prev)]
        + [(y[t, :, 0:lat], m.main) for t in range(frames)]
        + [(after[:, 0:lat], m.next)]
    )
    for k, (value, span) in enumerate(sources):
        mask = widen(mk[span[0] : span[1], :], lat)
        act = (silu((value - mean) * scale + bias) * mask).astype(BF16)
        jw[k] = act
        if 1 <= k <= frames:
            jl[k - 1] = act
    out = flat(fpart[...])
    for j in range(3):
        out = out + dot(flat(jw[j : j + frames]), wt[j, wide:, :])
    one = jnp.zeros((8, out.shape[1]), F32)
    two = jnp.zeros((8, out.shape[1]), F32)
    for t in range(frames):
        part = out[t * spots : (t + 1) * spots]
        first[t] = part
        one = one + sublane_sums(part)
        two = two + sublane_sums(part * part)
    s[...] = jnp.concatenate([row_sum(one), row_sum(two)], axis=1)


def space_forward(
    m, n, frames, cols, lo, at, width, col0, packed, span, st, z, row, w, g, b, mk, aw, out, s, nz, vw
):
    spots = z.shape[1]
    count = widen(mk[span[0] : span[0] + 1, :], width)
    mean, rstd = norm_rows(st, at, width, count, packed)
    nz[0:1, :] = mean
    nz[1:2, :] = rstd
    scale = rstd * g[n : n + 1, lo : lo + width]
    bias = b[n : n + 1, lo : lo + width]
    mask = widen(mk[m.ext[0] : m.ext[1], :], width)
    for t in range(frames):
        value = jnp.concatenate([row[t], z[t, :, col0 : col0 + width], row[t]], axis=0)
        act = silu((value - mean) * scale + bias) * mask
        aw[t] = act.astype(BF16)
        store_shifts(vw, t, act, cols)
    total = dot(flat(vw[:, 0:spots, :]), w[0])
    for i in range(1, 3):
        total = total + dot(flat(vw[:, i * cols : i * cols + spots, :]), w[i])
    mask = widen(mk[m.main[0] : m.main[1], :], width)
    one = jnp.zeros((8, width), F32)
    two = jnp.zeros((8, width), F32)
    for t in range(frames):
        part = total[t * spots : (t + 1) * spots]
        out[t] = part
        part = part * mask
        one = one + sublane_sums(part)
        two = two + sublane_sums(part * part)
    s[...] = jnp.concatenate([row_sum(one), row_sum(two)], axis=1)


def slow_third(m, n, frames, lo, halo, st, z, *rest):
    if halo:
        before, after, wp, g, b, mk, a2, third, s, nz, aw = rest
    else:
        wp, g, b, mk, a2, third, s, nz, aw = rest
    spots, width = z.shape[1], z.shape[2]
    wide = wp.shape[1]
    count = widen(mk[m.slow[0] : m.slow[0] + 1, :], width)
    mean, rstd = norm_rows(st, 0, width, count)
    nz[0:1, :] = mean
    nz[1:2, :] = rstd
    scale = rstd * g[n : n + 1, lo : lo + width]
    bias = b[n : n + 1, lo : lo + width]
    sources = [(z[t], m.main, t + halo) for t in range(frames)]
    if halo:
        sources += [(before[...], m.prev, 0), (after[...], m.next, frames + 1)]
    for value, span, at in sources:
        mask = widen(mk[span[0] : span[1], :], width)
        act = (silu((value - mean) * scale + bias) * mask).astype(BF16)
        aw[at] = act
        if halo <= at < frames + halo:
            a2[at - halo] = act
    acts = flat(aw[...])
    ones, twos = [], []
    for at in range(0, wide, 256):
        out = dot(acts, wp[:, at : at + 256])
        one = jnp.zeros((8, 256), F32)
        two = jnp.zeros((8, 256), F32)
        for t in range(frames + 2 * halo):
            part = out[t * spots : (t + 1) * spots]
            third[t, :, at : at + 256] = part
            if halo <= t < frames + halo:
                one = one + sublane_sums(part)
                two = two + sublane_sums(part * part)
        ones.append(row_sum(one))
        twos.append(row_sum(two))
    s[...] = jnp.concatenate(ones + twos, axis=1)


def fast_third(m, n, frames, lo, at, st, z, wp, g, b, mk, a2, ft, s, nz):
    spots = z.shape[1]
    count = mk[m.fast[0] : m.fast[0] + 1, :]
    mean, rstd = norm_rows(st, at, LANES, count, True)
    nz[0:1, :] = mean
    nz[1:2, :] = rstd
    scale = rstd * g[n : n + 1, lo : lo + LANES]
    bias = b[n : n + 1, lo : lo + LANES]
    mask = mk[m.main[0] : m.main[1], :]
    for t in range(frames):
        a2[t] = (silu((z[t] - mean) * scale + bias) * mask).astype(BF16)
    acts = flat(a2[...])
    one = jnp.zeros((8, LANES), F32)
    two = jnp.zeros((8, LANES), F32)
    out = dot(acts, wp[...])
    for t in range(frames):
        for lane in range(0, wp.shape[1], LANES):
            part = out[t * spots : (t + 1) * spots, lane : lane + LANES]
            ft[t, :, lane : lane + LANES] = part
            one = one + sublane_sums(part)
            two = two + sublane_sums(part * part)
    s[...] = jnp.concatenate([row_sum(one), row_sum(two)], axis=1)


def fast_next(m, n, frames, group, lo, at, st, ft, before, after, fw0, w7, g, b, mk, f1, fw1, y, s, nz):
    spots = ft.shape[1]
    count = mk[m.fast[0] : m.fast[0] + 1, :]
    mean, rstd = norm_rows(st, at, LANES, count)
    nz[0:1, :] = mean
    nz[1:2, :] = rstd
    scale = rstd * g[n : n + 1, lo : lo + LANES]
    bias = b[n : n + 1, lo : lo + LANES]
    total = frames * group

    def out_of(k, value, span):
        z = fw0[k].astype(F32) + ((value - mean) * scale + bias)
        return silu(z) * mk[span[0] : span[1], :]

    for k in range(2):
        lane = k * LANES
        fw1[k] = out_of(k, before[:, lane : lane + LANES], m.prev).astype(BF16)
        fw1[2 + total + k] = out_of(2 + total + k, after[:, lane : lane + LANES], m.next).astype(BF16)
    for t in range(frames):
        for f in range(group):
            k = t * group + f
            value = out_of(2 + k, ft[t, :, f * LANES : (f + 1) * LANES], m.main)
            f1[k] = value
            fw1[2 + k] = value.astype(BF16)
    out = dot(taps_of(fw1, frames, group), w7[...])
    for t in range(frames):
        y[t] = out[t * spots : (t + 1) * spots]
    s[...] = entry_sums(out, w7.shape[1] - LANES, frames, spots)


def fast_last(m, n, frames, group, lo, at, st, ft, f1, cot, g, b, mk, out, pre, s, nz):
    count = mk[m.fast[0] : m.fast[0] + 1, :]
    mean, rstd = norm_rows(st, at, LANES, count)
    nz[0:1, :] = mean
    nz[1:2, :] = rstd
    gain = g[n : n + 1, lo : lo + LANES]
    bias = b[n : n + 1, lo : lo + LANES]
    mask = mk[m.main[0] : m.main[1], :]
    one = jnp.zeros((8, LANES), F32)
    two = jnp.zeros((8, LANES), F32)
    for t in range(frames):
        for f in range(group):
            k = t * group + f
            hat = (ft[t, :, f * LANES : (f + 1) * LANES] - mean) * rstd
            z = f1[k] + hat * gain + bias
            sigma = sigmoid(z)
            out[k] = z * sigma * mask
            grad = cot[k].astype(F32) * mask * (sigma * (1.0 + z * (1.0 - sigma)))
            pre[k] = grad
            one = one + sublane_sums(grad)
            two = two + sublane_sums(grad * hat)
    s[...] = jnp.concatenate([row_sum(one), row_sum(two)], axis=1)


def chunked(total, step, body, init):
    def turn(i, carry):
        return body(pl.multiple_of(i * step, step), carry)

    return lax.fori_loop(0, total // step, turn, init)


def slow_next(m, n, frames, lo, at0, st, third, xm, wt, g, b, mk, slow1, sw, fpart, nz):
    spots, wide = third.shape[1], third.shape[2]
    count = widen(mk[m.slow[0] : m.slow[0] + 1, :], wide)
    mean, rstd = norm_rows(st, at0, wide, count)
    nz[0:1, :] = mean
    nz[1:2, :] = rstd
    scale = rstd * g[n : n + 1, lo : lo + wide]
    bias = b[n : n + 1, lo : lo + wide]
    spans = [m.prev] + [m.main] * frames + [m.next]
    for k, span in enumerate(spans):

        def turn(at, carry, k=k, span=span):
            mask = widen(mk[pl.ds(span[0] + at, 16), :], 512)
            for c in range(0, wide, 512):
                z = third[k, pl.ds(at, 16), c : c + 512]
                z = (z - mean[:, c : c + 512]) * scale[:, c : c + 512] + bias[:, c : c + 512]
                z = xm[k, pl.ds(at, 16), c : c + 512].astype(F32) + z
                value = silu(z) * mask
                sw[k, pl.ds(at, 16), c : c + 512] = value.astype(BF16)
                if 1 <= k <= frames:
                    slow1[k - 1, pl.ds(at, 16), c : c + 512] = value
            return carry

        chunked(spots, 16, turn, 0)
    out = dot(flat(sw[0:frames]), wt[0, :wide, :])
    for j in range(1, 3):
        out = out + dot(flat(sw[j : j + frames]), wt[j, :wide, :])
    for t in range(frames):
        fpart[t] = out[t * spots : (t + 1) * spots]


def slow_last(m, n, frames, lo, st, third, slow1, cot, g, b, mk, out, pre, s, nz):
    spots, wide = third.shape[1], third.shape[2]
    count = widen(mk[m.slow[0] : m.slow[0] + 1, :], wide)
    mean, rstd = norm_rows(st, 0, wide, count)
    nz[0:1, :] = mean
    nz[1:2, :] = rstd
    gain = g[n : n + 1, lo : lo + wide]
    bias = b[n : n + 1, lo : lo + wide]
    carry = (jnp.zeros((8, wide), F32), jnp.zeros((8, wide), F32))
    for t in range(frames):

        def turn(at, sums, t=t):
            one, two = sums
            ones, twos = [], []
            mask = widen(mk[pl.ds(m.main[0] + at, 16), :], 512)
            for c in range(0, wide, 512):
                hat = (third[t, pl.ds(at, 16), c : c + 512] - mean[:, c : c + 512]) * rstd[:, c : c + 512]
                z = slow1[t, pl.ds(at, 16), c : c + 512] + hat * gain[:, c : c + 512] + bias[:, c : c + 512]
                sigma = sigmoid(z)
                out[t, pl.ds(at, 16), c : c + 512] = z * sigma * mask
                grad = cot[t, pl.ds(at, 16), c : c + 512].astype(F32) * mask
                grad = grad * (sigma * (1.0 + z * (1.0 - sigma)))
                pre[t, pl.ds(at, 16), c : c + 512] = grad
                ones.append(sublane_sums(grad))
                twos.append(sublane_sums(grad * hat))
            return one + jnp.concatenate(ones, axis=1), two + jnp.concatenate(twos, axis=1)

        carry = chunked(spots, 16, turn, carry)
    s[...] = jnp.concatenate([row_sum(carry[0]), row_sum(carry[1])], axis=1)


def slow_third_back(m, n, frames, lo3, lo2, at, halo, st, pre, third, n3, z, n2, wp, g, b, mk, d3, e2, s, gb):
    spots, wide = pre.shape[1], pre.shape[2]
    width = z.shape[2]
    count = widen(mk[m.slow[0] : m.slow[0] + 1, :], wide)
    one, two = totals(st, at, wide)
    gb[0:1, :] = one
    gb[1:2, :] = two
    mean, rstd = n3[0:1, :], n3[1:2, :]
    scale = g[n : n + 1, lo3 : lo3 + wide] * rstd
    one = one / count
    two = two / count * rstd
    for t in range(frames):

        def turn(i, carry, t=t):
            mask = widen(mk[pl.ds(m.main[0] + i, 16), :], 512)
            for c in range(0, wide, 512):
                hat = (third[t + halo, pl.ds(i, 16), c : c + 512] - mean[:, c : c + 512]) * two[:, c : c + 512]
                grad = pre[t, pl.ds(i, 16), c : c + 512] - mask * (one[:, c : c + 512] + hat)
                d3[t, pl.ds(i, 16), c : c + 512] = (scale[:, c : c + 512] * grad).astype(BF16)
            return carry

        chunked(spots, 16, turn, 0)
    out = dot_nt(flat(d3[...]), wp[...])
    mean, rstd = n2[0:1, :], n2[1:2, :]
    gain = g[n : n + 1, lo2 : lo2 + width]
    bias = b[n : n + 1, lo2 : lo2 + width]
    back_act(m, frames, spots, out, z, 0, mean, rstd, gain, bias, mk, e2, s)


def back_act(m, frames, spots, out, z, col0, mean, rstd, gain, bias, mk, e, s):
    width = out.shape[1]
    mask = widen(mk[m.main[0] : m.main[1], :], width)
    one = jnp.zeros((8, width), F32)
    two = jnp.zeros((8, width), F32)
    for t in range(frames):
        hat = (z[t, :, col0 : col0 + width] - mean) * rstd
        grad = out[t * spots : (t + 1) * spots] * mask * silu_slope(hat * gain + bias)
        e[t] = grad
        one = one + sublane_sums(grad)
        two = two + sublane_sums(grad * hat)
    s[...] = jnp.concatenate([row_sum(one), row_sum(two)], axis=1)


def fast_third_back(m, n, frames, group, lo3, lo2, at, st, pre, ft, n3, z, n2, wp, g, b, mk, d3, e2, s, gb):
    spots = z.shape[1]
    count = mk[m.fast[0] : m.fast[0] + 1, :]
    one, two = totals(st, at, LANES)
    gb[0:1, :] = one
    gb[1:2, :] = two
    mean, rstd = n3[0:1, :], n3[1:2, :]
    scale = g[n : n + 1, lo3 : lo3 + LANES] * rstd
    one = one / count
    two = two / count * rstd
    mask = mk[m.main[0] : m.main[1], :]
    for t in range(frames):
        for f in range(group):
            hat = (ft[t, :, f * LANES : (f + 1) * LANES] - mean) * two
            grad = pre[t * group + f] - mask * (one + hat)
            d3[t, :, f * LANES : (f + 1) * LANES] = (scale * grad).astype(BF16)
    out = dot_nt(flat(d3[...]), wp[...])
    mean, rstd = n2[0:1, :], n2[1:2, :]
    gain = g[n : n + 1, lo2 : lo2 + LANES]
    bias = b[n : n + 1, lo2 : lo2 + LANES]
    back_act(m, frames, spots, out, z, 0, mean, rstd, gain, bias, mk, e2, s)


def space_back(
    m, n, frames, cols, lo2, lo1, at, width, col0, packed, span,
    st, e, erow, z, zrow, nz, z1, n1, w, g, b, mk, d2, e1, s, gb, vw,
):
    spots = z.shape[1]
    count = widen(mk[span[0] : span[0] + 1, :], width)
    one, two = totals(st, at, width, packed)
    gb[0:1, :] = one
    gb[1:2, :] = two
    mean, rstd = nz[0:1, :], nz[1:2, :]
    scale = g[n : n + 1, lo2 : lo2 + width] * rstd
    one = one / count
    two = two / count * rstd
    mask = widen(mk[m.ext[0] : m.ext[1], :], width)
    for t in range(frames):
        grad = jnp.concatenate([erow[t], e[t], erow[t]], axis=0)
        value = jnp.concatenate([zrow[t], z[t], zrow[t]], axis=0)
        grad = scale * mask * (grad - (one + (value - mean) * two))
        d2[t] = grad[cols : cols + spots].astype(BF16)
        store_shifts(vw, t, grad.astype(BF16).astype(F32), cols)
    total = None
    for i in range(3):
        rows = (2 - i) * cols
        for j in range(3):
            lane = (2 - j) * width
            part = dot_nt(flat(vw[:, rows : rows + spots, lane : lane + width]), w[i, j * width : (j + 1) * width, :])
            total = part if total is None else total + part
    mean, rstd = n1[0:1, :], n1[1:2, :]
    gain = g[n : n + 1, lo1 : lo1 + width]
    bias = b[n : n + 1, lo1 : lo1 + width]
    back_act(m, frames, spots, total, z1, col0, mean, rstd, gain, bias, mk, e1, s)


def slow_first_back(m, n, frames, lo1, lo3, at, halo, last, st, *rest):
    if last:
        e, ep, en, z, zp, zn, n1, wt, y, nl, pre, g, b, mk, dw, el, s, gx, gb = rest
    else:
        e, ep, en, z, zp, zn, n1, wt, y, nl, pre, xm, third, n3, g, b, mk, dw, el, s, pre0, s3, gb = rest
    spots, width = z.shape[1], z.shape[2]
    lat = nl.shape[1]
    wide = wt.shape[1] - lat
    count = widen(mk[m.slow[0] : m.slow[0] + 1, :], width)
    one, two = totals(st, at, width)
    gb[0:1, :] = one
    gb[1:2, :] = two
    mean, rstd = n1[0:1, :], n1[1:2, :]
    scale = g[n : n + 1, lo1 : lo1 + width] * rstd
    one = one / count
    two = two / count * rstd
    sources = (
        [(ep, zp, m.prev)] + [(e.at[t], z.at[t], m.main) for t in range(frames)] + [(en, zn, m.next)]
    )
    for k, (grad, value, span) in enumerate(sources):
        mask = widen(mk[span[0] : span[1], :], width)
        dw[k] = (scale * mask * (grad[...] - (one + (value[...] - mean) * two))).astype(BF16)
    taps = [flat(dw[2 - j : 2 - j + frames]) for j in range(3)]

    def back(lo, size):
        out = dot_nt(taps[0], wt[0, lo : lo + size, :])
        for j in range(1, 3):
            out = out + dot_nt(taps[j], wt[j, lo : lo + size, :])
        return out

    out = back(wide, lat)
    back_act(
        m, frames, spots, out, y, 0, nl[0:1, :], nl[1:2, :], g[n : n + 1, 0:lat], b[n : n + 1, 0:lat], mk, el, s
    )
    mask = widen(mk[m.main[0] : m.main[1], :], 256)
    ones, twos = [], []
    for c in range(0, wide, 256):
        out = back(c, 256)
        if not last:
            mean, rstd = n3[0:1, c : c + 256], n3[1:2, c : c + 256]
            gain = g[n - 1 : n, lo3 + c : lo3 + c + 256]
            bias = b[n - 1 : n, lo3 + c : lo3 + c + 256]
            one = jnp.zeros((8, 256), F32)
            two = jnp.zeros((8, 256), F32)
        for t in range(frames):
            grad = (out[t * spots : (t + 1) * spots] + pre[t, :, c : c + 256]) * mask
            if last:
                gx[t, :, c : c + 256] = grad
            else:
                hat = (third[t + halo, :, c : c + 256] - mean) * rstd
                z0 = xm[t + 1, :, c : c + 256].astype(F32) + hat * gain + bias
                grad = grad * silu_slope(z0)
                pre0[t, :, c : c + 256] = grad
                one = one + sublane_sums(grad)
                two = two + sublane_sums(grad * hat)
        if not last:
            ones.append(row_sum(one))
            twos.append(row_sum(two))
    if not last:
        s3[...] = jnp.concatenate(ones + twos, axis=1)


def fast_first_back(m, n, frames, group, lo1, lo3, at1, atl, last, st1, stl, *rest):
    if last:
        el, eln, ef, efp, efn, y, yp, yn, nl, n1, w7, pre, gs, g, b, mk, dl, dfw, gx, gbl, gb1, buf = rest
    else:
        (el, eln, ef, efp, efn, y, yp, yn, nl, n1, w7, pre, fw0, ft, n3, gs, g, b, mk,
         dl, dfw, pre0, s, gbl, gb1, buf) = rest
    spots = y.shape[1]
    lat = nl.shape[1]
    count = widen(mk[m.slow[0] : m.slow[0] + 1, :], lat)
    one, two = totals(stl, atl, lat)
    gbl[0:1, :] = one
    gbl[1:2, :] = two
    mean, rstd = nl[0:1, :], nl[1:2, :]
    scale = gs[n : n + 1, 0:lat] * rstd
    one = one / count
    two = two / count * rstd

    def lat_grad(grad, value, span):
        mask = widen(mk[span[0] : span[1], :], lat)
        return (scale * mask * (grad - (one + (value - mean) * two))).astype(BF16)

    for t in range(frames):
        dl[t] = lat_grad(el[t], y[t, :, 0:lat], m.main)
    dl_next = lat_grad(eln[...], yn[:, 0:lat], m.next)
    fcount = mk[m.fast[0] : m.fast[0] + 1, :]
    fone, ftwo = totals(st1, at1, LANES, True)
    gb1[0:1, :] = fone
    gb1[1:2, :] = ftwo
    fmean, frstd = n1[0:1, :], n1[1:2, :]
    fscale = g[n : n + 1, lo1 : lo1 + LANES] * frstd
    fone = fone / fcount
    ftwo = ftwo / fcount * frstd

    def first_grad(grad, value, span):
        mask = mk[span[0] : span[1], :]
        return (fscale * mask * (grad - (fone + (value - fmean) * ftwo))).astype(BF16)

    for t in range(frames):
        dfw[t] = first_grad(ef[t], y[t, :, lat:], m.main)
    df_prev = first_grad(efp[...], yp[:, lat:], m.prev)
    df_next = first_grad(efn[...], yn[:, lat:], m.next)
    both = jnp.concatenate([flat(dl[...]), flat(dfw[...])], axis=1)
    buf[...] = jnp.zeros(buf.shape, F32)
    out = dot_nt(both, w7[...])
    for t in range(frames):
        for f in range(7):
            k = group * t + f
            buf[k] = buf[k] + out[t * spots : (t + 1) * spots, f * LANES : (f + 1) * LANES]
    buf[2] = buf[2] + dot_nt(df_prev, w7[6 * LANES : 7 * LANES, lat:])
    after = dot_nt(jnp.concatenate([dl_next, df_next], axis=1), w7[0 : 2 * LANES, :])
    total = frames * group
    for f in range(2):
        buf[total + f] = buf[total + f] + after[:, f * LANES : (f + 1) * LANES]
    mask = mk[m.main[0] : m.main[1], :]
    if last:
        for k in range(total):
            gx[k] = (pre[k] + buf[2 + k]) * mask
        return
    mean, rstd = n3[0:1, :], n3[1:2, :]
    gain = g[n - 1 : n, lo3 : lo3 + LANES]
    bias = b[n - 1 : n, lo3 : lo3 + LANES]
    one = jnp.zeros((8, LANES), F32)
    two = jnp.zeros((8, LANES), F32)
    for k in range(total):
        t, f = k // group, k % group
        hat = (ft[t, :, f * LANES : (f + 1) * LANES] - mean) * rstd
        z0 = fw0[2 + k].astype(F32) + hat * gain + bias
        grad = (pre[k] + buf[2 + k]) * mask * silu_slope(z0)
        pre0[k] = grad
        one = one + sublane_sums(grad)
        two = two + sublane_sums(grad * hat)
    s[...] = jnp.concatenate([row_sum(one), row_sum(two)], axis=1)


def point_weights(a2, d3, out):
    acts = flat(a2[...])
    for k in range(out.shape[0]):
        out[k] = dot_tn(acts, flat(d3[:, :, k * 256 : (k + 1) * 256])).astype(BF16)


def space_weights(cols, aw, d2, out, vw):
    frames, spots, width = d2.shape
    for t in range(frames):
        store_shifts(vw, t, aw[t].astype(F32), cols)
    grads = flat(d2[...])
    for i in range(3):
        out[i] = dot_tn(flat(vw[:, i * cols : i * cols + spots, :]), grads).astype(BF16)


def time_weights(skip, slow, jl, dw, out):
    frames, spots, width = jl.shape
    wide = slow.shape[2]
    grads = jnp.concatenate([flat(dw[2 - j : 2 - j + frames]) for j in range(3)], axis=1)
    for c in range(0, wide + jl.shape[2], 256):
        if c < wide:
            acts = flat(slow[skip : skip + frames, :, c : c + 256])
        else:
            acts = flat(jl[:, :, c - wide : c - wide + 256])
        got = dot_tn(acts, grads)
        for j in range(3):
            out[j, c : c + 256, :] = got[:, j * width : (j + 1) * width].astype(BF16)


def group_blocks(value, group):
    size = LANES // group
    rows = lax.broadcasted_iota(jnp.int32, (LANES, LANES), 0) >> (size.bit_length() - 1)
    lanes = lax.broadcasted_iota(jnp.int32, (LANES, LANES), 1) >> (size.bit_length() - 1)
    kept = jnp.where(rows == lanes, value, 0.0)
    kept = kept + pltpu.roll(kept, 64, 1)
    kept = kept + pltpu.roll(kept, 32, 1)
    total = kept[0:size]
    for k in range(1, group):
        total = total + kept[k * size : (k + 1) * size]
    return total


def at_lanes(blocks):
    lanes = lax.broadcasted_iota(jnp.int32, blocks[0].shape, 1) >> 5
    out = jnp.zeros(blocks[0].shape, F32)
    for k, block in enumerate(blocks):
        out = jnp.where(lanes == k, block, out)
    return out


def fast_weights(group, cols, lat, fw, dl, df, fa1, d2, fa2, d3, out, vw):
    frames, spots, _ = dl.shape
    size = LANES // group
    both = jnp.concatenate([flat(dl[...]), flat(df[...])], axis=1)
    taps = [[None] * group for _ in range(3)]
    for f in range(7):
        acts = jnp.concatenate([fw[group * t + f] for t in range(frames)], axis=0)
        got = dot_tn(acts, both)
        if f < 5:
            out[f * LANES : (f + 1) * LANES, :] = got[:, :lat].astype(BF16)
        for k in range(group):
            if 0 <= f - k - 1 < 3:
                taps[f - k - 1][k] = got[:, lat:]
    lanes = lax.broadcasted_iota(jnp.int32, (LANES, LANES), 1) >> (size.bit_length() - 1)
    tap_sums = []
    for j in range(3):
        kept = jnp.zeros((LANES, LANES), F32)
        for k in range(group):
            kept = jnp.where(lanes == k, taps[j][k], kept)
        kept = kept + pltpu.roll(kept, 64, 1)
        tap_sums.append(kept + pltpu.roll(kept, 32, 1))
    low = 5 * LANES
    out[low : low + LANES, 0:LANES] = at_lanes(tap_sums).T.astype(BF16)
    for t in range(frames):
        store_shifts(vw, t, fa1[t].astype(F32), cols)
    grads = flat(d2[...])
    for i in range(3):
        got = dot_tn(flat(vw[:, i * cols : i * cols + spots, :]), grads)
        blocks = [group_blocks(got[j * LANES : (j + 1) * LANES], group) for j in range(3)]
        out[low + size * i : low + size * (i + 1), LANES : 2 * LANES] = at_lanes(blocks).astype(BF16)
    acts = flat(fa2[...])
    total = jnp.zeros((size, LANES), F32)
    for k in range(group):
        got = dot_tn(acts, flat(d3[:, :, k * LANES : (k + 1) * LANES]))
        total = total + got[k * size : (k + 1) * size]
    out[low + 3 * size : low + 4 * size, LANES : 2 * LANES] = total.astype(BF16)


def unpack_fast(n, inner, load, outs):
    glat, gft, gfs, gfp = outs
    low = glat.shape[1]
    for at in range(0, low, inner):
        glat[n, at : at + inner, :] = load(at, inner)
    for i in range(4):
        got = load(low + inner * i, inner)
        if i < 3:
            gft[n, i] = got[:, 0:LANES]
            for j in range(3):
                moved = got[:, LANES:] if j == 0 else pltpu.roll(got[:, LANES:], LANES - inner * j, 1)
                gfs[n, 3 * i + j] = moved[:, 0:inner]
        else:
            gfp[n] = got[:, LANES:]


def rows_of(one, two=None):
    def load(at, count):
        ref = one
        size = one.shape[1]
        if two is not None:
            core, rest = at // (8 * size), at % (8 * size)
            if rest >= 4 * size:
                ref, rest = two, rest - 4 * size
            at = core * 4 * size + rest
        block, row = at // size, at % size
        assert row + count <= size
        return ref[block, row : row + count, :].astype(F32)

    return load


def copy_rows(start, one, out):
    for at in range(0, out.shape[0], 256):
        out[at : at + 256, :] = one[start + at : start + at + 256, :].astype(F32)


def copy_columns(start, one, out):
    for at in range(0, out.shape[1], 256):
        out[:, at : at + 256] = one[start + at : start + at + 256, :].astype(F32)


def place_rows(start, step, one, two, out):
    load = rows_of(one, two)
    for at in range(0, out.shape[0], step):
        out[at : at + step, :] = load(start + at, step)


def place_columns(start, one, two, out):
    load = rows_of(one, two)
    for at in range(0, out.shape[1], 256):
        out[:, at : at + 256] = load(start + at, 256)


def place_fast(inner, one_one, one_two, zero, *outs):
    unpack_fast(1, inner, rows_of(one_one, one_two), outs)
    unpack_fast(0, inner, rows_of(zero), outs)


def assemble_norms(inner, *refs):
    sums, (gs, bs, gf, bf) = refs[:-4], refs[-4:]
    lanes = lax.broadcasted_iota(jnp.int32, (8, LANES), 1) >> (inner.bit_length() - 1)
    for n in range(2):
        slow, fast = sums[7 * n : 7 * n + 4], sums[7 * n + 4 : 7 * n + 7]
        for row, gslow, gfast in ((1, gs, gf), (0, bs, bf)):
            at = 0
            for part in slow:
                gslow[n : n + 1, at : at + part.shape[1]] = part[row : row + 1, :]
                at += part.shape[1]
            one, two, three = [jnp.broadcast_to(part[row : row + 1, :], (8, LANES)) for part in fast]
            three = pltpu.roll(three, 2 * inner, 1)
            head = jnp.where(lanes == 0, one, jnp.where(lanes == 1, two, three))
            gfast[n : n + 1, 0:LANES] = head[0:1]
            gfast[n : n + 1, LANES : LANES + 2 * inner] = three[0:1, 0 : 2 * inner]


def on_device(
    x_slow,
    x_fast,
    w_lateral,
    w_slow_time,
    w_slow_space,
    w_slow_point,
    w_fast_time,
    w_fast_space,
    w_fast_point,
    gain_slow,
    bias_slow,
    gain_fast,
    bias_fast,
    clip_size,
    cot_slow,
    cot_fast,
):
    frames, fast_frames = x_slow.shape[0], x_fast.shape[0]
    group = fast_frames // frames
    rows, cols = x_slow.shape[3], x_slow.shape[4]
    spots = rows * cols
    wide, fwide = x_slow.shape[5], x_fast.shape[5]
    lat = w_lateral.shape[3]
    width = w_slow_space.shape[3]
    inner = w_fast_space.shape[3]
    packs = group * fwide
    both = lat + LANES
    m = Masks(spots, cols)
    devices = lax.axis_size("path") * lax.axis_size("rows")
    path = lax.axis_index("path")
    ext = spots + 2 * cols
    lo1, lo2, lo3 = lat, lat + width, lat + 2 * width
    every = slice(None)

    def part(fn, *static):
        return functools.partial(fn, *static)

    xs = x_slow.reshape(frames, spots, wide)
    xf = x_fast.reshape(fast_frames, spots, fwide)
    cs = cot_slow.reshape(frames, spots, wide)
    cf = cot_fast.reshape(fast_frames, spots, fwide)
    wft = jnp.swapaxes(w_fast_time, 2, 3)
    wfs_raw = w_fast_space.reshape(2, 9, inner, inner)
    wsp = w_slow_space.reshape(2, 3, 3 * width, width)

    def packed(value):
        return jnp.concatenate(
            [value[:, 0:inner]] * group + [value[:, inner : 2 * inner]] * group + [value[:, 2 * inner :]],
            axis=1,
        )

    xf_edge = swap_path(jnp.where(path > 0, xf[:2], xf[-2:]))
    xs_edge = swap_path(jnp.where(path > 0, xs[0], xs[-1]))

    def payload(k, *sums):
        size = sum(k.temps[s[1]].shape[1] for s in sums)
        out = k.give((devices, 1, size))
        k.step(spread_sums, *sums, out)
        return out

    def row_out(k, z, mk, col0, size):
        out = k.give((frames, cols, size))
        k.step(part(own_row, m, spots, cols, col0, size), z, mk, out)
        return out

    def edge_out(k, z, mk, size, tail=0):
        out = k.give((spots, size), BF16)
        k.step(part(own_edge, m, 0, tail), z, mk, out)
        return out

    def finish(k, **handles):
        got = k.run()
        return {name: got[handle[1]] for name, handle in handles.items()}

    def other_row(value):
        return swap(value, "rows", 1)

    first_flops = 2 * frames * spots * 7 * fwide * both
    k = Stage("entry")
    mk_out = k.give((m.rows, LANES))
    place = jnp.stack([lax.axis_index("rows"), path]).astype(jnp.int32)
    k.step(
        part(make_masks, m, rows, cols, lax.axis_size("path") - 1), k.scalar(place), k.scalar(clip_size), mk_out
    )
    w7_out = k.give((7 * fwide, both), BF16)
    k.step(part(make_w7, lat, group), k.take(w_lateral, 0), k.take(wft, 0), w7_out)
    fw = k.give((fast_frames + 4, spots, fwide), BF16)
    y = k.give((frames, spots, both))
    sy = k.temp((1, 2 * both))
    edge = k.take(xf_edge)
    k.step(
        part(fast_entry, m, frames, group), k.take(xf), edge, edge, mk_out, w7_out, fw, y, sy, flops=first_flops
    )
    pay = payload(k, sy)
    got = finish(
        k, mk=mk_out, w7=w7_out, fw=fw, y=y, pay=pay, ff_row=row_out(k, y, mk_out, lat, LANES),
        edge=edge_out(k, y, mk_out, both),
    )
    mk = got["mk"]
    saved = [{"fw": got["fw"], "y": got["y"], "w7": got["w7"]}, {}]
    st = gather_sums(got["pay"])
    saved[0]["ff_row"] = other_row(got["ff_row"])
    saved[0]["y_edge"] = swap_path(got["edge"])
    mk, wft, gain_fast, bias_fast = lax.optimization_barrier((mk, wft, gain_fast, bias_fast))
    gf, bf = packed(gain_fast), packed(bias_fast)
    k = Stage("prepare")
    w7_out = k.give((7 * fwide, both), BF16)
    k.step(part(make_w7, lat, group), k.take(w_lateral, 1), k.take(wft, 1), w7_out)
    blocks = []
    for n in range(2):
        blocks += [k.give((3, 3 * LANES, LANES), BF16), k.give((LANES, packs), BF16)]
        k.step(part(make_blocks, group), k.take(wfs_raw, n), k.take(w_fast_point, n), *blocks[-2:])
    got = finish(k, w7=w7_out, wfs0=blocks[0], wfp0=blocks[1], wfs1=blocks[2], wfp1=blocks[3])
    saved[1]["w7"] = got["w7"]
    wfs, wfp = [got["wfs0"], got["wfs1"]], [got["wfp0"], got["wfp1"]]
    k = Stage("slow_partial")
    xm = k.give((frames + 2, spots, wide), BF16)
    fpart = k.give((frames, spots, width))
    edge = k.take(xs_edge)
    k.step(
        part(slow_partial, m, frames),
        k.take(xs), edge, edge, k.take(mk), k.take(w_slow_time, 0, every, slice(0, wide)), xm, fpart,
        flops=2 * frames * spots * 3 * wide * width,
    )
    got = finish(k, sw=xm, fpart=fpart)
    saved[0]["sw"] = got["sw"]
    fpart_in = got["fpart"]

    for n in range(2):
        v = saved[n]
        k = Stage("join")
        mk_in, gs, bs = k.take(mk), k.take(gain_slow), k.take(bias_slow)
        st_in = k.take(st)
        names = {}
        if n == 0:
            fpart = k.take(fpart_in)
        else:
            fpart = k.temp((frames, spots, width))
            names.update(
                slow1=k.give((frames, spots, wide)),
                sw=k.give((frames + 2, spots, wide), BF16),
            )
            n3 = k.give((2, wide))
            k.step(
                part(slow_next, m, 0, frames, lo3, 2 * both),
                st_in, k.take(saved[0]["third"]), k.take(saved[0]["sw"]),
                k.take(w_slow_time, 1, every, slice(0, wide)), gs, bs, mk_in,
                names["slow1"], names["sw"], fpart, n3,
                flops=2 * frames * spots * 3 * wide * width,
            )
            names["n3"] = n3
        y_in, edge = k.take(v["y"]), k.take(v["y_edge"])
        jl = k.give((frames, spots, lat), BF16)
        first = k.give((frames, spots, width))
        nl = k.give((2, lat))
        s_first, s_fs = k.temp((1, 2 * width)), k.temp((1, 2 * LANES))
        k.step(
            part(lat_join, m, n, frames, lat),
            st_in, y_in, edge, edge, fpart, k.take(w_slow_time, n, every, slice(wide, wide + lat)), gs, bs, mk_in,
            jl, first, s_first, nl, k.temp((frames + 2, spots, lat), BF16),
            flops=2 * frames * spots * 3 * lat * width,
        )
        fa1 = k.give((frames, ext, LANES), BF16)
        fs = k.give((frames, spots, LANES))
        nf1 = k.give((2, LANES))
        k.step(
            part(space_forward, m, n, frames, cols, 0, 2 * lat, LANES, lat, True, m.fast),
            st_in, y_in, k.take(v["ff_row"]), k.take(wfs[n]), k.take(gf), k.take(bf), mk_in,
            fa1, fs, s_fs, nf1, k.temp((frames, ext, 3 * LANES), BF16),
            flops=2 * frames * spots * 9 * LANES * LANES,
        )
        pay = payload(k, s_first, s_fs)
        got = finish(
            k, jl=jl, first=first, nl=nl, fa1=fa1, fs=fs, nf1=nf1, pay=pay,
            first_row=row_out(k, first, mk_in, 0, width), fs_row=row_out(k, fs, mk_in, 0, LANES),
            first_edge=edge_out(k, first, mk_in, width), **names,
        )
        st = gather_sums(got["pay"])
        for name in ("jl", "first", "nl", "fa1", "fs", "nf1"):
            v[name] = got[name]
        if n == 1:
            slow1, saved[1]["sw"], saved[0]["n3"] = got["slow1"], got["sw"], got["n3"]
        first_row = other_row(got["first_row"])
        v["fs_row"] = other_row(got["fs_row"])
        v["first_edge"] = swap_path(got["first_edge"])
        k = Stage("space")
        mk_in, st_in = k.take(mk), k.take(st)
        a1 = k.give((frames, ext, width), BF16)
        second = k.give((frames, spots, width))
        n1 = k.give((2, width))
        s_second, s_ft = k.temp((1, 2 * width)), k.temp((1, 2 * LANES))
        k.step(
            part(space_forward, m, n, frames, cols, lo1, 0, width, 0, False, m.slow),
            st_in, k.take(v["first"]), k.take(first_row), k.take(wsp, n), k.take(gain_slow), k.take(bias_slow), mk_in,
            a1, second, s_second, n1, k.temp((frames, ext, 3 * width), BF16),
            flops=2 * frames * spots * 9 * width * width,
        )
        fa2 = k.give((frames, spots, LANES), BF16)
        ft = k.give((frames, spots, packs))
        nf2 = k.give((2, LANES))
        k.step(
            part(fast_third, m, n, frames, LANES, 2 * width),
            st_in, k.take(v["fs"]), k.take(wfp[n]), k.take(gf), k.take(bf), mk_in, fa2, ft, s_ft, nf2,
            flops=2 * frames * spots * LANES * packs,
        )
        pay = payload(k, s_second, s_ft)
        names = {"second_row": row_out(k, second, mk_in, 0, width)}
        if n == 0:
            names["second_edge"] = edge_out(k, second, mk_in, width)
            names["ft_edge"] = edge_out(k, ft, mk_in, 2 * fwide, (group - 2) * fwide)
        got = finish(k, a1=a1, second=second, n1=n1, fa2=fa2, ft=ft, nf2=nf2, pay=pay, **names)
        st = gather_sums(got["pay"])
        for name in ("a1", "second", "n1", "fa2", "ft", "nf2"):
            v[name] = got[name]
        v["second_row"] = other_row(got["second_row"])
        halo = 1 - n
        edges = []
        k = Stage("third")
        if n == 0:
            ft_edge = k.take(swap_path(got["ft_edge"]))
            edges = [k.take(swap_path(got["second_edge"]))] * 2
        mk_in, st_in = k.take(mk), k.take(st)
        a2 = k.give((frames, spots, width), BF16)
        third = k.give((frames + 2 * halo, spots, wide))
        n2 = k.give((2, width))
        nf3 = k.give((2, LANES))
        s_third = k.temp((1, 2 * wide))
        names = {}
        if n == 0:
            names.update(
                f1=k.give((fast_frames, spots, fwide)),
                fw=k.give((fast_frames + 4, spots, fwide), BF16),
                y=k.give((frames, spots, both)),
            )
            s_fast = k.temp((1, 2 * both))
            k.step(
                part(fast_next, m, n, frames, group, 2 * LANES, 2 * width),
                st_in, k.take(v["ft"]), ft_edge, ft_edge, k.take(v["fw"]), k.take(saved[1]["w7"]),
                k.take(gf), k.take(bf), mk_in, names["f1"], names["fw"], names["y"], s_fast, nf3,
                flops=first_flops,
            )
        else:
            names.update(out_fast=k.give((fast_frames, spots, fwide)), pre_f=k.give((fast_frames, spots, fwide)))
            s_fast = k.temp((1, 2 * LANES))
            k.step(
                part(fast_last, m, n, frames, group, 2 * LANES, 2 * width),
                st_in, k.take(v["ft"]), k.take(fast1), k.take(cf), k.take(gf), k.take(bf), mk_in,
                names["out_fast"], names["pre_f"], s_fast, nf3,
            )
        k.step(
            part(slow_third, m, n, frames, lo2, halo),
            st_in, k.take(v["second"]), *edges, k.take(w_slow_point, n), k.take(gain_slow), k.take(bias_slow), mk_in,
            a2, third, s_third, n2, k.temp((frames + 2 * halo, spots, width), BF16),
            flops=2 * frames * spots * width * wide,
        )
        if n == 0:
            pay = payload(k, s_fast, s_third)
            names["ff_row"] = row_out(k, names["y"], mk_in, lat, LANES)
            names["y_edge"] = edge_out(k, names["y"], mk_in, both)
        else:
            pay = payload(k, s_third, s_fast)
        got = finish(k, a2=a2, third=third, n2=n2, nf3=nf3, pay=pay, **names)
        st = gather_sums(got["pay"])
        for name in ("a2", "third", "n2", "nf3"):
            v[name] = got[name]
        if n == 0:
            fast1 = got["f1"]
            saved[1].update(
                fw=got["fw"], y=got["y"], ff_row=other_row(got["ff_row"]), y_edge=swap_path(got["y_edge"])
            )
        else:
            out_fast, pre_f = got["out_fast"], got["pre_f"]

    def third_back(k, n, at, st_in, mk_in, pre):
        v = saved[n]
        d3, e2 = k.give((frames, spots, wide), BF16), k.give((frames, spots, width))
        s, gb = k.temp((1, 2 * width)), k.give((2, wide))
        k.step(
            part(slow_third_back, m, n, frames, lo3, lo2, at, 1 - n),
            st_in, k.take(pre), k.take(v["third"]), k.take(v["n3"]), k.take(v["second"]), k.take(v["n2"]),
            k.take(w_slow_point, n), k.take(gain_slow), k.take(bias_slow), mk_in, d3, e2, s, gb,
            flops=2 * frames * spots * width * wide,
        )
        return dict(d3=d3, e2=e2, gb3=gb), s

    def fast_back3(k, n, at, st_in, mk_in, pre):
        v = saved[n]
        d3, e2 = k.give((frames, spots, packs), BF16), k.give((frames, spots, LANES))
        s, gb = k.temp((1, 2 * LANES)), k.give((2, LANES))
        k.step(
            part(fast_third_back, m, n, frames, group, 2 * LANES, LANES, at),
            st_in, k.take(pre), k.take(v["ft"]), k.take(v["nf3"]), k.take(v["fs"]), k.take(v["nf2"]),
            k.take(wfp[n]), k.take(gf), k.take(bf), mk_in, d3, e2, s, gb,
            flops=2 * frames * spots * LANES * packs,
        )
        return dict(d3f=d3, ef2=e2, gbf3=gb), s

    def second_back(k, n, at, st_in, mk_in, e2, e2_row):
        v = saved[n]
        d2, e1 = k.give((frames, spots, width), BF16), k.give((frames, spots, width))
        s, gb = k.temp((1, 2 * width)), k.give((2, width))
        k.step(
            part(space_back, m, n, frames, cols, lo2, lo1, at, width, 0, False, m.slow),
            st_in, k.take(e2), k.take(e2_row), k.take(v["second"]), k.take(v["second_row"]), k.take(v["n2"]),
            k.take(v["first"]), k.take(v["n1"]), k.take(wsp, n), k.take(gain_slow), k.take(bias_slow), mk_in,
            d2, e1, s, gb, k.temp((frames, ext, 3 * width), BF16),
            flops=2 * frames * spots * 9 * width * width,
        )
        return dict(d2=d2, e1=e1, gb2=gb), s

    def fast_back2(k, n, at, st_in, mk_in, ef2, ef2_row):
        v = saved[n]
        d2, e1 = k.give((frames, spots, LANES), BF16), k.give((frames, spots, LANES))
        s, gb = k.temp((1, 2 * LANES)), k.give((2, LANES))
        k.step(
            part(space_back, m, n, frames, cols, LANES, 0, at, LANES, lat, True, m.fast),
            st_in, k.take(ef2), k.take(ef2_row), k.take(v["fs"]), k.take(v["fs_row"]), k.take(v["nf2"]),
            k.take(v["y"]), k.take(v["nf1"]), k.take(wfs[n]), k.take(gf), k.take(bf), mk_in,
            d2, e1, s, gb, k.temp((frames, ext, 3 * LANES), BF16),
            flops=2 * frames * spots * 9 * LANES * LANES,
        )
        return dict(d2f=d2, ef1=e1, gbf2=gb), s

    def first_back(k, n, st_in, mk_in, e1, e1_edge, pre):
        v = saved[n]
        last = n == 0
        dw, el = k.give((frames + 2, spots, width), BF16), k.give((frames, spots, lat))
        s, gb = k.temp((1, 2 * lat)), k.give((2, width))
        down = k.give((frames, spots, wide))
        edge, zedge = k.take(e1_edge), k.take(v["first_edge"])
        args = [
            st_in, k.take(e1), edge, edge, k.take(v["first"]), zedge, zedge, k.take(v["n1"]),
            k.take(w_slow_time, n), k.take(v["y"]), k.take(v["nl"]), k.take(pre),
        ]
        outs = [dw, el, s, down]
        sums = [s]
        if not last:
            args += [k.take(saved[0]["sw"]), k.take(saved[0]["third"]), k.take(saved[0]["n3"])]
            sums.append(k.temp((1, 2 * wide)))
            outs.append(sums[1])
        k.step(
            part(slow_first_back, m, n, frames, lo1, lo3, 0, 1, last),
            *args, k.take(gain_slow), k.take(bias_slow), mk_in, *outs, gb,
            flops=2 * frames * spots * 3 * (wide + lat) * width,
        )
        return dict(dw=dw, el=el, down=down, gb1=gb), sums

    def fast_back1(k, n, st1, at1, stl, atl, mk_in, el, el_edge, ef1, ef1_edge, pre):
        v = saved[n]
        last = n == 0
        dl, df = k.give((frames, spots, lat), BF16), k.give((frames, spots, LANES), BF16)
        down = k.give((fast_frames, spots, fwide))
        gbl, gb1 = k.give((2, lat)), k.give((2, LANES))
        edge, yedge = k.take(ef1_edge), k.take(v["y_edge"])
        args = [
            st1, stl, k.take(el), k.take(el_edge), k.take(ef1), edge, edge, k.take(v["y"]), yedge, yedge,
            k.take(v["nl"]), k.take(v["nf1"]), k.take(v["w7"]), k.take(pre),
        ]
        outs = [dl, df, down]
        s = None
        if not last:
            args += [k.take(saved[0]["fw"]), k.take(saved[0]["ft"]), k.take(saved[0]["nf3"])]
            s = k.temp((1, 2 * LANES))
            outs.append(s)
        k.step(
            part(fast_first_back, m, n, frames, group, 0, 2 * LANES, at1, atl, last),
            *args, k.take(gain_slow), k.take(gf), k.take(bf), mk_in, *outs, gbl, gb1,
            k.temp((fast_frames + 4, spots, fwide)),
            flops=first_flops,
        )
        return dict(dl=dl, df=df, downf=down, gbl=gbl, gbf1=gb1), s

    def weights_point(n, d3):
        k = Stage("point_weights")
        out = k.give((wide // 256, width, 256), BF16)
        k.step(point_weights, k.take(saved[n]["a2"]), k.take(d3), out, flops=2 * frames * spots * width * wide)
        return k.run()[0].reshape(-1, 256)

    def weights_space(n, d2):
        k = Stage("space_weights")
        out = k.give((3, 3 * width, width), BF16)
        k.step(
            part(space_weights, cols), k.take(saved[n]["a1"]), k.take(d2), out,
            k.temp((frames, ext, 3 * width), BF16), flops=2 * frames * spots * 9 * width * width,
        )
        return k.run()[0].reshape(-1, 256)

    def weights_time(n, dw):
        k = Stage("time_weights")
        out = k.give((3, wide + lat, width), BF16)
        k.step(
            part(time_weights, 1), k.take(saved[n]["sw"]), k.take(saved[n]["jl"]), k.take(dw), out,
            flops=2 * frames * spots * 3 * (wide + lat) * width,
        )
        return k.run()[0].reshape(-1, 256)

    def weights_fast(n, dl, df, d2, d3):
        v = saved[n]
        k = Stage("fast_weights")
        out = k.give((7 * LANES - LANES, 2 * LANES), BF16)
        k.step(
            part(fast_weights, group, cols, lat),
            k.take(v["fw"]), k.take(dl), k.take(df), k.take(v["fa1"]), k.take(d2), k.take(v["fa2"]), k.take(d3),
            out, k.temp((frames, ext, 3 * LANES), BF16), flops=first_flops,
        )
        return k.run()[0]

    b1, b0 = {}, {}
    k = Stage("last")
    mk_in, st_in = k.take(mk), k.take(st)
    out_slow, pre = k.give((frames, spots, wide)), k.give((frames, spots, wide))
    n3 = k.give((2, wide))
    s_pre = k.temp((1, 2 * wide))
    k.step(
        part(slow_last, m, 1, frames, lo3),
        st_in, k.take(saved[1]["third"]), k.take(slow1), k.take(cs), k.take(gain_slow), k.take(bias_slow), mk_in,
        out_slow, pre, s_pre, n3,
    )
    names, s_ef2 = fast_back3(k, 1, 2 * wide, st_in, mk_in, pre_f)
    pay = payload(k, s_pre, s_ef2)
    ef2_row = row_out(k, names["ef2"], mk_in, 0, LANES)
    b1 = finish(k, out_slow=out_slow, pre=pre, n3=n3, pay=pay, ef2_row=ef2_row, **names)
    saved[1]["n3"] = b1["n3"]
    out_slow = b1["out_slow"]
    st = gather_sums(b1["pay"])

    k = Stage("back_third")
    ef2_row = other_row(b1["ef2_row"])
    mk_in, st_in = k.take(mk), k.take(st)
    names, s_e2 = third_back(k, 1, 0, st_in, mk_in, b1["pre"])
    more, s_ef1 = fast_back2(k, 1, 2 * wide, st_in, mk_in, b1["ef2"], ef2_row)
    pay = payload(k, s_e2, s_ef1)
    e2_row, ef1_edge = row_out(k, names["e2"], mk_in, 0, width), edge_out(k, more["ef1"], mk_in, LANES)
    b1.update(finish(k, pay=pay, e2_row=e2_row, ef1_edge=ef1_edge, **names, **more))
    st = st_ef1 = gather_sums(b1["pay"])
    e2_row, ef1_edge = other_row(b1["e2_row"]), swap_path(b1["ef1_edge"])
    point1 = weights_point(1, b1["d3"])

    k = Stage("back_space")
    mk_in, st_in = k.take(mk), k.take(st)
    names, s_e1 = second_back(k, 1, 0, st_in, mk_in, b1["e2"], e2_row)
    pay = payload(k, s_e1)
    e1_edge = edge_out(k, names["e1"], mk_in, width)
    b1.update(finish(k, pay=pay, e1_edge=e1_edge, **names))
    st = gather_sums(b1["pay"])
    e1_edge = swap_path(b1["e1_edge"])
    space1 = weights_space(1, b1["d2"])

    k = Stage("back_first")
    mk_in, st_in = k.take(mk), k.take(st)
    names, sums = first_back(k, 1, st_in, mk_in, b1["e1"], e1_edge, b1["pre"])
    pay = payload(k, *sums)
    el_edge = edge_out(k, names["el"], mk_in, lat)
    b1.update(finish(k, pay=pay, el_edge=el_edge, **names))
    st = gather_sums(b1["pay"])
    el_edge = swap_path(b1["el_edge"])
    time1 = weights_time(1, b1["dw"])
    sizes1 = [point1.shape[0], space1.shape[0], time1.shape[0]]
    ones = jnp.concatenate([point1, space1, time1], axis=0)
    ones = lax.psum(ones, AXES)

    SUMS = ("gbl", "gb1", "gb2", "gb3", "gbf1", "gbf2", "gbf3")
    steps = exchange_steps()
    core, across, down = steps[:3]
    seen = {}

    def block_zero(st=st, el_edge=el_edge, ef1_edge=ef1_edge, b1=b1, b0=b0):
        b1, b0 = dict(b1), dict(b0)
        k = Stage("back_third")
        mk_in, st_in = k.take(mk), k.take(st)
        names, s_e2 = third_back(k, 0, 2 * lat, st_in, mk_in, b1["down"])
        more, s_pf = fast_back1(
            k, 1, k.take(st_ef1), 2 * width, st_in, 0, mk_in, b1["el"], el_edge, b1["ef1"], ef1_edge, pre_f
        )
        pay = payload(k, s_e2, s_pf)
        e2_row = row_out(k, names["e2"], mk_in, 0, width)
        got = finish(k, pay=pay, e2_row=e2_row, **names, **more)
        for name in more:
            b1[name] = got[name]
        b0.update({name: got[name] for name in names})
        st = gather_sums(got["pay"])
        e2_row = other_row(got["e2_row"])
        point0 = weights_point(0, b0["d3"])
        fast_1 = weights_fast(1, b1["dl"], b1["df"], b1["d2f"], b1["d3f"])

        k = Stage("back_space")
        mk_in, st_in = k.take(mk), k.take(st)
        names, s_e1 = second_back(k, 0, 0, st_in, mk_in, b0["e2"], e2_row)
        more, s_ef2 = fast_back3(k, 0, 2 * width, st_in, mk_in, b1["downf"])
        pay = payload(k, s_e1, s_ef2)
        e1_edge, ef2_row = edge_out(k, names["e1"], mk_in, width), row_out(k, more["ef2"], mk_in, 0, LANES)
        b0.update(finish(k, pay=pay, e1_edge=e1_edge, ef2_row=ef2_row, **names, **more))
        st = gather_sums(b0["pay"])
        e1_edge, ef2_row = swap_path(b0["e1_edge"]), other_row(b0["ef2_row"])
        space0 = weights_space(0, b0["d2"])
        mid = halve(jnp.concatenate([fast_1, point0, space0], axis=0), *core)

        k = Stage("back_first")
        mk_in, st_in = k.take(mk), k.take(st)
        names, sums = first_back(k, 0, st_in, mk_in, b0["e1"], e1_edge, b1["down"])
        more, s_ef1 = fast_back2(k, 0, 2 * width, st_in, mk_in, b0["ef2"], ef2_row)
        pay = payload(k, *sums, s_ef1)
        el_edge, ef1_edge = edge_out(k, names["el"], mk_in, lat), edge_out(k, more["ef1"], mk_in, LANES)
        b0.update(finish(k, pay=pay, el_edge=el_edge, ef1_edge=ef1_edge, **names, **more))
        pay, mid = lax.optimization_barrier((b0["pay"], mid))
        st = gather_sums(pay)
        el_edge, ef1_edge = swap_path(b0["el_edge"]), swap_path(b0["ef1_edge"])
        mid = halve_both(*parted(mid), across, down)
        time0 = weights_time(0, b0["dw"])
        late = halve(time0, *core)
        st, mid = lax.optimization_barrier((st, mid))
        mid = jnp.concatenate(halve_both(*mid, down, across), axis=0)
        for step in steps[3:4]:
            mid = halve(mid, *step)

        k = Stage("back_fast")
        mk_in, st_in = k.take(mk), k.take(st)
        more, _ = fast_back1(
            k, 0, st_in, 2 * lat, st_in, 0, mk_in, b0["el"], el_edge, b0["ef1"], ef1_edge, b1["downf"]
        )
        b0.update(finish(k, **more))
        dl0, mid, late = lax.optimization_barrier((b0["dl"], mid, late))
        late = halve_both(*parted(late), across, down)
        rest = weights_fast(0, dl0, b0["df"], b0["d2f"], b0["d3f"])
        rest = halve(rest, *core)
        for step in steps[4:]:
            mid = halve(mid, *step)
        seen["fast"], seen["point"] = fast_1.shape[0], point0.shape[0]
        sums = [b0[name] for name in SUMS] + [b1[name] for name in ("gbl", "gbf1")]
        return (mid.astype(BF16), *late, rest, b0["down"], b0["downf"], *sums)

    like = jax.eval_shape(block_zero)
    got = lax.cond(
        clip_size[0, 0] > 0, block_zero, lambda: tuple(jnp.zeros(o.shape, o.dtype) for o in like)
    )
    mid, late, rest = got[0], got[1:3], got[3]
    gx_slow, gx_fast = got[4:6]
    b0 = dict(zip(SUMS, got[6:13]))
    b1["gbl"], b1["gbf1"] = got[13:15]

    def spread_both(one, two):
        one, two = [one, swap(one, *down)], [two, swap(two, *across)]
        one, two = [jnp.stack(pair) for pair in (one, two)]
        one, two = [one, swap(one, *across)], [two, swap(two, *down)]
        return [pair + [swap(half, *core) for half in pair] for pair in (one, two)]

    for step in reversed(steps[3:]):
        mid = double(mid, *step)
    mid_one, mid_two = spread_both(*parted(mid))
    late = halve_both(*late, down, across)
    rest = halve(halve(rest, *across), *down)
    parts = [late[0].shape[0], rest.shape[0], late[1].shape[0]]
    value = jnp.concatenate([late[0], rest, late[1]], axis=0)
    for step in steps[3:]:
        value = halve(value, *step)
    value = value.astype(BF16)
    for step in reversed(steps[3:]):
        value = double(value, *step)
    cut = parts[0] + parts[1]
    one, two = spread_both(value[:cut], value[cut:])

    time_rows, space_rows = 3 * (wide + lat), 9 * width
    k = Stage("assemble_one")
    ones_in = k.take(ones)
    gtime, gspace = k.give((2, time_rows, width), F32, 1), k.give((2, space_rows, width), F32, 1)
    gpoint = k.give((2, width, wide), F32, 1)
    k.step(part(copy_rows, sizes1[0] + sizes1[1]), ones_in, gtime)
    k.step(part(copy_rows, sizes1[0]), ones_in, gspace)
    k.step(part(copy_columns, 0), ones_in, gpoint)
    half_done = k.run()
    core_bit = lax.axis_index("rows") % 2
    down_bit = (lax.axis_index("rows") // 2) % 2

    k = Stage("assemble")
    flip_one = k.scalar((core_bit * 4 + path * 2 + down_bit).astype(jnp.int32).reshape(1))
    flip_two = k.scalar((core_bit * 4 + down_bit * 2 + path).astype(jnp.int32).reshape(1))
    mid_one, mid_two = k.take_blocks(mid_one, flip_one, every), k.take_blocks(mid_two, flip_two, every)
    start = seen["fast"]
    gspace = k.give((2, space_rows, width), F32, 0, half_done[1])
    k.step(part(place_rows, start + seen["point"], 256), mid_one, mid_two, gspace)
    gpoint = k.give((2, width, wide), F32, 0, half_done[2])
    k.step(part(place_columns, start), mid_one, mid_two, gpoint)
    late_one = k.take_blocks(one, flip_one, slice(0, parts[0]))
    late_two = k.take_blocks(two, flip_two, every)
    gtime = k.give((2, time_rows, width), F32, 0, half_done[0])
    k.step(part(place_rows, 0, 80), late_one, late_two, gtime)
    rest = k.take_blocks(one, flip_one, slice(parts[0], cut))
    fast_outs = [
        k.give((2, 5 * fwide, lat)), k.give((2, 3, inner, fwide)), k.give((2, 9, inner, inner)),
        k.give((2, inner, fwide)),
    ]
    k.step(part(place_fast, inner), mid_one, mid_two, rest, *fast_outs)
    sums = [k.take(b[name]) for b in (b0, b1) for name in ("gbl", "gb1", "gb2", "gb3", "gbf1", "gbf2", "gbf3")]
    norm_outs = [k.give(like.shape) for like in (gain_slow, bias_slow, gain_fast, bias_fast)]
    k.step(part(assemble_norms, inner), *sums, *norm_outs)
    got = k.run()
    glat, gft, gfs, gfp = [got[h[1]] for h in fast_outs]

    return (
        out_slow.reshape(x_slow.shape),
        out_fast.reshape(x_fast.shape),
        gx_slow.reshape(x_slow.shape),
        gx_fast.reshape(x_fast.shape),
        glat.reshape(w_lateral.shape),
        got[gtime[1]].reshape(w_slow_time.shape),
        got[gspace[1]].reshape(w_slow_space.shape),
        got[gpoint[1]],
        jnp.swapaxes(gft, 2, 3),
        gfs.reshape(w_fast_space.shape),
        gfp,
        *[got[h[1]] for h in norm_outs],
    )


def solution(mesh):
    spread = P("path", None, "rows", None, None, None)
    return jax.shard_map(
        on_device,
        mesh=mesh,
        in_specs=(spread, spread) + (P(),) * 12 + (spread, spread),
        out_specs=(spread,) * 4 + (P(),) * 11,
        check_vma=False,
    )
```

```python
import functools

import jax
import jax.numpy as jnp
import numpy as np
from jax import lax
from jax.experimental import pallas as pl
from jax.experimental.pallas import tpu as pltpu
from jax.sharding import PartitionSpec as P

TS = 8
TF = 32
F32 = jnp.float32
BF16 = jnp.bfloat16
EPSILON = 1e-05
LANES = 128
AXES = ("path", "rows")
VMEM_LIMIT = 56 * 2**20


def swap(value, axis, stride):
    pairs = [(source, source ^ stride) for source in range(lax.axis_size(axis))]
    return lax.ppermute(value, axis, pairs)


def gather_sums(spread):
    return lax.all_to_all(spread, AXES, 0, 0, tiled=True)


def swap_path(value):
    assert lax.axis_size("path") == 2
    return lax.ppermute(value, "path", [(0, 1), (1, 0)])


def exchange_steps():
    steps = [("rows", 1), ("path", 1)]
    stride = 2
    while stride < lax.axis_size("rows"):
        steps.append(("rows", stride))
        stride *= 2
    return steps


def halve(value, axis, stride):
    size = value.shape[0] // 2
    upper = (lax.axis_index(axis) // stride) % 2
    keep = lax.dynamic_slice_in_dim(value, upper * size, size, 0)
    give = lax.dynamic_slice_in_dim(value, (1 - upper) * size, size, 0)
    return keep.astype(F32) + swap(give.astype(BF16), axis, stride).astype(F32)


def double(value, axis, stride):
    upper = (lax.axis_index(axis) // stride) % 2
    got = swap(value, axis, stride)
    return jnp.concatenate(
        [jnp.where(upper == 0, value, got), jnp.where(upper == 0, got, value)], axis=0
    )


def halve_both(one, two, first, second):
    return halve(one, *first), halve(two, *second)


def parted(value):
    size = value.shape[0] // 2
    return value[:size], value[size:]


class Stage:
    def __init__(self, name):
        self.name = name
        self.arrays, self.views, self.scalars, self.pairs = [], [], [], []
        self.outs, self.temps, self.steps = [], [], []
        self.entries, self.ontos = [], []
        self.flops = 0

    def take(self, array, *view):
        for at, known in enumerate(self.arrays):
            if known is array:
                break
        else:
            at = len(self.arrays)
            self.arrays.append(array)
        for k, (other, seen) in enumerate(self.views):
            if other == at and seen == view:
                return ("in", k)
        self.views.append((at, view))
        return ("in", len(self.views) - 1)

    def take_blocks(self, values, flip, rows):
        self.pairs.append(([self.take(value, slice(None), rows) for value in values], flip))
        return ("pair", len(self.pairs) - 1)

    def scalar(self, array):
        self.scalars.append(array)
        return ("scalar", len(self.scalars) - 1)

    def give(self, dims, dtype=F32, at=None, onto=None):
        self.outs.append(jax.ShapeDtypeStruct(tuple(dims), dtype))
        self.entries.append(at)
        self.ontos.append(onto)
        return ("out", len(self.outs) - 1)

    def temp(self, dims, dtype=F32):
        self.temps.append(pltpu.VMEM(tuple(dims), dtype))
        return ("temp", len(self.temps) - 1)

    def step(self, fn, *handles, flops=0):
        self.flops += flops
        self.steps.append((fn, handles))

    def sem(self, view, block):
        return 8 * view + block

    def view_shape(self, view):
        at, index = view
        return np.broadcast_to(np.zeros((), np.int8), self.arrays[at].shape)[index].shape

    def run(self):
        arrays, views, outs, steps, pairs = self.arrays, self.views, self.outs, self.steps, self.pairs
        order, home = [], {}
        for k, (members, flip) in enumerate(pairs):
            for j, member in enumerate(members):
                home[member[1]] = (k, j, flip)
        under = [onto for onto in self.ontos if onto is not None]

        def need(handle):
            if handle[0] == "in":
                return [handle[1]]
            return [part[1] for part in pairs[handle[1]][0]] if handle[0] == "pair" else []

        for _, handles in steps:
            for handle in handles:
                for k in need(handle):
                    if k not in order:
                        order.append(k)

        def body(*refs):
            refs = list(refs)

            def cut(count):
                taken = refs[:count]
                del refs[:count]
                return taken

            scalars, hbm_in = cut(len(self.scalars)), cut(len(arrays))
            cut(len(under))
            hbm_out = cut(len(outs))
            alone = [k for k in range(len(views)) if k not in home]
            held = dict(zip(alone, cut(len(alone))))
            joint, made, temps, (sems,) = cut(len(pairs)), cut(len(outs)), cut(len(self.temps)), refs
            copies = {}
            for k in order:
                at, index = views[k]
                src = hbm_in[at].at[index] if index else hbm_in[at]
                if k in home:
                    pair, second, flip = home[k]
                    count = self.view_shape(views[k])[0]
                    copies[k] = []
                    for block in range(count):
                        to = (second * count + block) ^ scalars[flip[1]][0]
                        copies[k].append(
                            pltpu.make_async_copy(src.at[block], joint[pair].at[to], sems.at[self.sem(k, block)])
                        )
                else:
                    copies[k] = [pltpu.make_async_copy(src, held[k], sems.at[self.sem(k, 0)])]
                for copy in copies[k]:
                    copy.start()
            waited, sent = set(), {}
            for fn, handles in steps:
                given = []
                for handle in handles:
                    for k in need(handle):
                        if k not in waited:
                            for copy in copies[k]:
                                copy.wait()
                            waited.add(k)
                    place = {"in": held, "pair": joint, "out": made, "temp": temps, "scalar": scalars}
                    given.append(place[handle[0]][handle[1]])
                fn(*given)
                for kind, k in handles:
                    if kind == "out" and k not in sent:
                        to = hbm_out[k] if self.entries[k] is None else hbm_out[k].at[self.entries[k]]
                        sent[k] = pltpu.make_async_copy(made[k], to, sems.at[8 * len(views) + k])
                        sent[k].start()
            for copy in sent.values():
                copy.wait()

        moved = sum(a.size * a.dtype.itemsize for a in outs)
        for view in views:
            moved += int(np.prod(self.view_shape(view))) * arrays[view[0]].dtype.itemsize
        scratch = [
            pltpu.VMEM(self.view_shape(view), arrays[view[0]].dtype) for k, view in enumerate(views) if k not in home
        ]
        for members, _ in pairs:
            size = self.view_shape(views[members[0][1]])
            scratch.append(
                pltpu.VMEM((len(members) * size[0],) + size[1:], arrays[views[members[0][1]][0]].dtype)
            )
        scratch += [
            pltpu.VMEM(o.shape if at is None else o.shape[1:], o.dtype) for o, at in zip(outs, self.entries)
        ]
        aliases = {}
        for k, onto in enumerate(self.ontos):
            if onto is not None:
                aliases[len(self.scalars) + len(arrays) + len(aliases)] = k
        scratch += self.temps + [pltpu.SemaphoreType.DMA((8 * len(views) + len(outs),))]
        return pl.pallas_call(
            body,
            out_shape=tuple(outs),
            in_specs=[pl.BlockSpec(memory_space=pltpu.SMEM) for _ in self.scalars]
            + [pl.BlockSpec(memory_space=pl.ANY) for _ in arrays + under],
            out_specs=tuple(pl.BlockSpec(memory_space=pl.ANY) for _ in outs),
            scratch_shapes=scratch,
            input_output_aliases=aliases,
            compiler_params=pltpu.CompilerParams(vmem_limit_bytes=VMEM_LIMIT),
            cost_estimate=pl.CostEstimate(flops=self.flops, bytes_accessed=moved, transcendentals=0),
            name=self.name,
        )(*self.scalars, *arrays, *under)


class Masks:
    def __init__(self, spots, cols):
        self.main = (0, spots)
        self.ext = (spots, 2 * spots + 2 * cols)
        self.prev = (2 * spots + 2 * cols, 3 * spots + 2 * cols)
        self.next = (3 * spots + 2 * cols, 4 * spots + 2 * cols)
        self.slow = (4 * spots + 2 * cols, 4 * spots + 2 * cols + 8)
        self.fast = (4 * spots + 2 * cols + 8, 4 * spots + 2 * cols + 16)
        self.half = (4 * spots + 2 * cols + 16, 4 * spots + 2 * cols + 24)
        self.path = (4 * spots + 2 * cols + 24, 4 * spots + 2 * cols + 32)
        self.rows = 4 * spots + 2 * cols + 32


def make_masks(m, rows, cols, last, place, clips, mk):
    half = place[0] % 2
    path = place[1]
    side = clips[0, place[0] // 2]
    area = 0
    for k in range(clips.shape[1]):
        area = area + clips[0, k] * clips[0, k]
    shift = cols.bit_length() - 1

    def inside(first, count):
        at = lax.broadcasted_iota(jnp.int32, (count * cols, LANES), 0)
        line = half * rows + first + (at >> shift)
        spot = at & (cols - 1)
        good = (line >= 0) & (line < 2 * rows) & (line < side) & (spot < side)
        return jnp.where(good, 1.0, 0.0)

    main = inside(0, rows)
    mk[m.main[0] : m.main[1], :] = main
    mk[m.ext[0] : m.ext[1], :] = inside(-1, rows + 2)
    mk[m.prev[0] : m.prev[1], :] = main * jnp.where(path > 0, 1.0, 0.0)
    mk[m.next[0] : m.next[1], :] = main * jnp.where(path < last, 1.0, 0.0)

    def fill(span, value):
        mk[span[0] : span[1], :] = jnp.full((8, LANES), value, F32)

    fill(m.slow, TS * area.astype(F32))
    fill(m.fast, TF * area.astype(F32))
    fill(m.half, half.astype(F32))
    fill(m.path, path.astype(F32))


def own_row(m, spots, cols, col0, width, z, mk, row):
    for t in range(z.shape[0]):
        lower = mk[m.half[0] : m.half[0] + 1, :] > 0.5
        for lane in range(0, width, LANES):
            at = col0 + lane
            row[t, :, lane : lane + LANES] = jnp.where(
                lower, z[t, 0:cols, at : at + LANES], z[t, spots - cols : spots, at : at + LANES]
            )


def own_edge(m, lead, tail, z, mk, edge):
    frames = z.shape[0]
    second = mk[m.path[0] : m.path[0] + 1, :] > 0.5
    for lane in range(0, edge.shape[1], LANES):
        edge[:, lane : lane + LANES] = jnp.where(
            second,
            z[0, :, lead + lane : lead + lane + LANES],
            z[frames - 1, :, tail + lane : tail + lane + LANES],
        ).astype(edge.dtype)


def spread_sums(*refs):
    parts, out = refs[:-1], refs[-1]
    row = jnp.concatenate([part[...] for part in parts], axis=1)
    out[...] = jnp.broadcast_to(row[None], out.shape)


def make_w7(lat, group, wl, wf, w7):
    inner = wf.shape[1]
    w7[...] = jnp.zeros(w7.shape, BF16)
    for j in range(wl.shape[0]):
        w7[j * LANES : (j + 1) * LANES, 0:lat] = wl[j]
    at = lax.broadcasted_iota(jnp.int32, (inner, LANES), 0)
    lane = lax.broadcasted_iota(jnp.int32, (inner, LANES), 1)
    places = [jnp.where(lane == at + inner * k, 1.0, 0.0).astype(BF16) for k in range(group)]
    for f in range(1, group + 3):
        used = [k for k in range(group) if 0 <= f - 1 - k < 3]
        got = None
        for k in used:
            more = dot_tn(wf[f - 1 - k], places[k])
            got = more if got is None else got + more
        w7[f * LANES : (f + 1) * LANES, lat : lat + LANES] = got.astype(BF16)


def make_blocks(group, ws, wp, wfs, wfp):
    inner = wp.shape[0]
    at = lax.broadcasted_iota(jnp.int32, (inner, LANES), 0)
    lane = lax.broadcasted_iota(jnp.int32, (inner, LANES), 1)
    tile = jnp.where((lane & (inner - 1)) == at, 1.0, 0.0).astype(BF16)
    shift = inner.bit_length() - 1
    for tap in range(ws.shape[0]):
        got = dot(ws[tap], tile)
        for k in range(group):
            kept = jnp.where((lane >> shift) == k, got, 0.0).astype(BF16)
            row = (tap % 3) * LANES + k * inner
            wfs[tap // 3, row : row + inner, :] = kept
    wfp[...] = jnp.zeros(wfp.shape, BF16)
    for k in range(group):
        wfp[k * inner : (k + 1) * inner, k * LANES : (k + 1) * LANES] = wp[...]


def widen(rows, width):
    return jnp.concatenate([rows] * (width // LANES), axis=1)


def sublane_sums(value):
    return jnp.sum(value.reshape(value.shape[0] // 8, 8, value.shape[1]), axis=0)


def row_sum(value):
    return jnp.sum(value, axis=0, keepdims=True)


def fold_packed(row):
    full = jnp.broadcast_to(row, (8, LANES))
    full = full + pltpu.roll(full, 64, 1)
    full = full + pltpu.roll(full, 32, 1)
    return full[0:1]


def totals(st, lo, width, packed=False):
    first = jnp.sum(st[:, :, lo : lo + width], axis=0)
    second = jnp.sum(st[:, :, lo + width : lo + 2 * width], axis=0)
    if packed:
        return fold_packed(first), fold_packed(second)
    return first, second


def norm_rows(st, lo, width, count, packed=False):
    first, second = totals(st, lo, width, packed)
    mean = first / count
    return mean, lax.rsqrt(second / count - mean * mean + EPSILON)


def sigmoid(value):
    return 0.5 * jnp.tanh(0.5 * value) + 0.5


def silu(value):
    return value * sigmoid(value)


def silu_slope(value):
    sigma = sigmoid(value)
    return sigma * (1.0 + value * (1.0 - sigma))


def dot(a, b):
    return jnp.dot(a, b, preferred_element_type=F32)


def dot_nt(a, b):
    return lax.dot_general(a, b, (((1,), (1,)), ((), ())), preferred_element_type=F32)


def dot_tn(a, b):
    return lax.dot_general(a, b, (((0,), (0,)), ((), ())), preferred_element_type=F32)


def flat(value):
    return value.reshape(value.shape[0] * value.shape[1], value.shape[2])


def store_shifts(dst, t, value, cols):
    rows, width = value.shape
    spot = lax.broadcasted_iota(jnp.int32, (rows, width), 0) & (cols - 1)
    left = jnp.where(spot == 0, 0.0, pltpu.roll(value, 1, 0))
    right = jnp.where(spot == cols - 1, 0.0, pltpu.roll(value, rows - 1, 0))
    dst[t, :, 0:width] = left.astype(BF16)
    dst[t, :, width : 2 * width] = value.astype(BF16)
    dst[t, :, 2 * width : 3 * width] = right.astype(BF16)


def taps_of(frames_ref, frames, group):
    return jnp.concatenate(
        [
            jnp.concatenate([frames_ref[group * t + f] for f in range(7)], axis=1)
            for t in range(frames)
        ],
        axis=0,
    )


def entry_sums(y, lat, frames, spots):
    width = y.shape[1]
    one = jnp.zeros((8, width), F32)
    two = jnp.zeros((8, width), F32)
    for t in range(frames):
        part = y[t * spots : (t + 1) * spots]
        one = one + sublane_sums(part)
        two = two + sublane_sums(part * part)
    one = row_sum(one)
    two = row_sum(two)
    return jnp.concatenate([one[:, :lat], two[:, :lat], one[:, lat:], two[:, lat:]], axis=1)


def fast_entry(m, frames, group, x, before, after, mk, w7, fw, y, s):
    spots = x.shape[1]
    count = x.shape[0]

    def put(at, value, span):
        fw[at] = (value.astype(F32) * mk[span[0] : span[1], :]).astype(BF16)

    for k in range(2):
        put(k, before[k], m.prev)
        put(2 + count + k, after[k], m.next)
    for k in range(count):
        put(2 + k, x[k], m.main)
    out = dot(taps_of(fw, frames, group), w7[...])
    for t in range(frames):
        y[t] = out[t * spots : (t + 1) * spots]
    s[...] = entry_sums(out, w7.shape[1] - LANES, frames, spots)


def slow_partial(m, frames, x, before, after, mk, wt, xm, fpart):
    spots, wide = x.shape[1], x.shape[2]
    sources = [(before, m.prev)] + [(x.at[t], m.main) for t in range(frames)] + [(after, m.next)]
    for k, (src, span) in enumerate(sources):
        for lo in range(0, wide, 256):
            mask = widen(mk[span[0] : span[1], :], 256)
            xm[k, :, lo : lo + 256] = (src[:, lo : lo + 256].astype(F32) * mask).astype(BF16)
    out = dot(flat(xm[0:frames]), wt[0, :wide, :])
    for j in range(1, 3):
        out = out + dot(flat(xm[j : j + frames]), wt[j, :wide, :])
    for t in range(frames):
        fpart[t] = out[t * spots : (t + 1) * spots]


def lat_join(m, n, frames, lat, st, y, before, after, fpart, wt, gs, bs, mk, jl, first, s, nl, jw):
    spots = y.shape[1]
    wide = wt.shape[1] - lat
    count = widen(mk[m.slow[0] : m.slow[0] + 1, :], lat)
    mean, rstd = norm_rows(st, 0, lat, count)
    nl[0:1, :] = mean
    nl[1:2, :] = rstd
    scale = rstd * gs[n : n + 1, 0:lat]
    bias = bs[n : n + 1, 0:lat]
    sources = (
        [(before[:, 0:lat], m.prev)]
        + [(y[t, :, 0:lat], m.main) for t in range(frames)]
        + [(after[:, 0:lat], m.next)]
    )
    for k, (value, span) in enumerate(sources):
        mask = widen(mk[span[0] : span[1], :], lat)
        act = (silu((value - mean) * scale + bias) * mask).astype(BF16)
        jw[k] = act
        if 1 <= k <= frames:
            jl[k - 1] = act
    out = flat(fpart[...])
    for j in range(3):
        out = out + dot(flat(jw[j : j + frames]), wt[j, wide:, :])
    one = jnp.zeros((8, out.shape[1]), F32)
    two = jnp.zeros((8, out.shape[1]), F32)
    for t in range(frames):
        part = out[t * spots : (t + 1) * spots]
        first[t] = part
        one = one + sublane_sums(part)
        two = two + sublane_sums(part * part)
    s[...] = jnp.concatenate([row_sum(one), row_sum(two)], axis=1)


def space_forward(
    m, n, frames, cols, lo, at, width, col0, packed, span, st, z, row, w, g, b, mk, aw, out, s, nz, vw
):
    spots = z.shape[1]
    count = widen(mk[span[0] : span[0] + 1, :], width)
    mean, rstd = norm_rows(st, at, width, count, packed)
    nz[0:1, :] = mean
    nz[1:2, :] = rstd
    scale = rstd * g[n : n + 1, lo : lo + width]
    bias = b[n : n + 1, lo : lo + width]
    mask = widen(mk[m.ext[0] : m.ext[1], :], width)
    for t in range(frames):
        value = jnp.concatenate([row[t], z[t, :, col0 : col0 + width], row[t]], axis=0)
        act = silu((value - mean) * scale + bias) * mask
        aw[t] = act.astype(BF16)
        store_shifts(vw, t, act, cols)
    total = dot(flat(vw[:, 0:spots, :]), w[0])
    for i in range(1, 3):
        total = total + dot(flat(vw[:, i * cols : i * cols + spots, :]), w[i])
    mask = widen(mk[m.main[0] : m.main[1], :], width)
    one = jnp.zeros((8, width), F32)
    two = jnp.zeros((8, width), F32)
    for t in range(frames):
        part = total[t * spots : (t + 1) * spots]
        out[t] = part
        part = part * mask
        one = one + sublane_sums(part)
        two = two + sublane_sums(part * part)
    s[...] = jnp.concatenate([row_sum(one), row_sum(two)], axis=1)


def slow_third(m, n, frames, lo, halo, st, z, *rest):
    if halo:
        before, after, wp, g, b, mk, a2, third, s, nz, aw = rest
    else:
        wp, g, b, mk, a2, third, s, nz, aw = rest
    spots, width = z.shape[1], z.shape[2]
    wide = wp.shape[1]
    count = widen(mk[m.slow[0] : m.slow[0] + 1, :], width)
    mean, rstd = norm_rows(st, 0, width, count)
    nz[0:1, :] = mean
    nz[1:2, :] = rstd
    scale = rstd * g[n : n + 1, lo : lo + width]
    bias = b[n : n + 1, lo : lo + width]
    sources = [(z[t], m.main, t + halo) for t in range(frames)]
    if halo:
        sources += [(before[...], m.prev, 0), (after[...], m.next, frames + 1)]
    for value, span, at in sources:
        mask = widen(mk[span[0] : span[1], :], width)
        act = (silu((value - mean) * scale + bias) * mask).astype(BF16)
        aw[at] = act
        if halo <= at < frames + halo:
            a2[at - halo] = act
    acts = flat(aw[...])
    ones, twos = [], []
    for at in range(0, wide, 256):
        out = dot(acts, wp[:, at : at + 256])
        one = jnp.zeros((8, 256), F32)
        two = jnp.zeros((8, 256), F32)
        for t in range(frames + 2 * halo):
            part = out[t * spots : (t + 1) * spots]
            third[t, :, at : at + 256] = part
            if halo <= t < frames + halo:
                one = one + sublane_sums(part)
                two = two + sublane_sums(part * part)
        ones.append(row_sum(one))
        twos.append(row_sum(two))
    s[...] = jnp.concatenate(ones + twos, axis=1)


def fast_third(m, n, frames, lo, at, st, z, wp, g, b, mk, a2, ft, s, nz):
    spots = z.shape[1]
    count = mk[m.fast[0] : m.fast[0] + 1, :]
    mean, rstd = norm_rows(st, at, LANES, count, True)
    nz[0:1, :] = mean
    nz[1:2, :] = rstd
    scale = rstd * g[n : n + 1, lo : lo + LANES]
    bias = b[n : n + 1, lo : lo + LANES]
    mask = mk[m.main[0] : m.main[1], :]
    for t in range(frames):
        a2[t] = (silu((z[t] - mean) * scale + bias) * mask).astype(BF16)
    acts = flat(a2[...])
    one = jnp.zeros((8, LANES), F32)
    two = jnp.zeros((8, LANES), F32)
    out = dot(acts, wp[...])
    for t in range(frames):
        for lane in range(0, wp.shape[1], LANES):
            part = out[t * spots : (t + 1) * spots, lane : lane + LANES]
            ft[t, :, lane : lane + LANES] = part
            one = one + sublane_sums(part)
            two = two + sublane_sums(part * part)
    s[...] = jnp.concatenate([row_sum(one), row_sum(two)], axis=1)


def fast_next(m, n, frames, group, lo, at, st, ft, before, after, fw0, w7, g, b, mk, f1, fw1, y, s, nz):
    spots = ft.shape[1]
    count = mk[m.fast[0] : m.fast[0] + 1, :]
    mean, rstd = norm_rows(st, at, LANES, count)
    nz[0:1, :] = mean
    nz[1:2, :] = rstd
    scale = rstd * g[n : n + 1, lo : lo + LANES]
    bias = b[n : n + 1, lo : lo + LANES]
    total = frames * group

    def out_of(k, value, span):
        z = fw0[k].astype(F32) + ((value - mean) * scale + bias)
        return silu(z) * mk[span[0] : span[1], :]

    for k in range(2):
        lane = k * LANES
        fw1[k] = out_of(k, before[:, lane : lane + LANES], m.prev).astype(BF16)
        fw1[2 + total + k] = out_of(2 + total + k, after[:, lane : lane + LANES], m.next).astype(BF16)
    for t in range(frames):
        for f in range(group):
            k = t * group + f
            value = out_of(2 + k, ft[t, :, f * LANES : (f + 1) * LANES], m.main)
            f1[k] = value
            fw1[2 + k] = value.astype(BF16)
    out = dot(taps_of(fw1, frames, group), w7[...])
    for t in range(frames):
        y[t] = out[t * spots : (t + 1) * spots]
    s[...] = entry_sums(out, w7.shape[1] - LANES, frames, spots)


def fast_last(m, n, frames, group, lo, at, st, ft, f1, cot, g, b, mk, out, pre, s, nz):
    count = mk[m.fast[0] : m.fast[0] + 1, :]
    mean, rstd = norm_rows(st, at, LANES, count)
    nz[0:1, :] = mean
    nz[1:2, :] = rstd
    gain = g[n : n + 1, lo : lo + LANES]
    bias = b[n : n + 1, lo : lo + LANES]
    mask = mk[m.main[0] : m.main[1], :]
    one = jnp.zeros((8, LANES), F32)
    two = jnp.zeros((8, LANES), F32)
    for t in range(frames):
        for f in range(group):
            k = t * group + f
            hat = (ft[t, :, f * LANES : (f + 1) * LANES] - mean) * rstd
            z = f1[k] + hat * gain + bias
            sigma = sigmoid(z)
            out[k] = z * sigma * mask
            grad = cot[k].astype(F32) * mask * (sigma * (1.0 + z * (1.0 - sigma)))
            pre[k] = grad
            one = one + sublane_sums(grad)
            two = two + sublane_sums(grad * hat)
    s[...] = jnp.concatenate([row_sum(one), row_sum(two)], axis=1)


def chunked(total, step, body, init):
    def turn(i, carry):
        return body(pl.multiple_of(i * step, step), carry)

    return lax.fori_loop(0, total // step, turn, init)


def slow_next(m, n, frames, lo, at0, st, third, xm, wt, g, b, mk, slow1, sw, fpart, nz):
    spots, wide = third.shape[1], third.shape[2]
    count = widen(mk[m.slow[0] : m.slow[0] + 1, :], wide)
    mean, rstd = norm_rows(st, at0, wide, count)
    nz[0:1, :] = mean
    nz[1:2, :] = rstd
    scale = rstd * g[n : n + 1, lo : lo + wide]
    bias = b[n : n + 1, lo : lo + wide]
    spans = [m.prev] + [m.main] * frames + [m.next]
    for k, span in enumerate(spans):

        def turn(at, carry, k=k, span=span):
            mask = widen(mk[pl.ds(span[0] + at, 16), :], 512)
            for c in range(0, wide, 512):
                z = third[k, pl.ds(at, 16), c : c + 512]
                z = (z - mean[:, c : c + 512]) * scale[:, c : c + 512] + bias[:, c : c + 512]
                z = xm[k, pl.ds(at, 16), c : c + 512].astype(F32) + z
                value = silu(z) * mask
                sw[k, pl.ds(at, 16), c : c + 512] = value.astype(BF16)
                if 1 <= k <= frames:
                    slow1[k - 1, pl.ds(at, 16), c : c + 512] = value
            return carry

        chunked(spots, 16, turn, 0)
    out = dot(flat(sw[0:frames]), wt[0, :wide, :])
    for j in range(1, 3):
        out = out + dot(flat(sw[j : j + frames]), wt[j, :wide, :])
    for t in range(frames):
        fpart[t] = out[t * spots : (t + 1) * spots]


def slow_last(m, n, frames, lo, st, third, slow1, cot, g, b, mk, out, pre, s, nz):
    spots, wide = third.shape[1], third.shape[2]
    count = widen(mk[m.slow[0] : m.slow[0] + 1, :], wide)
    mean, rstd = norm_rows(st, 0, wide, count)
    nz[0:1, :] = mean
    nz[1:2, :] = rstd
    gain = g[n : n + 1, lo : lo + wide]
    bias = b[n : n + 1, lo : lo + wide]
    carry = (jnp.zeros((8, wide), F32), jnp.zeros((8, wide), F32))
    for t in range(frames):

        def turn(at, sums, t=t):
            one, two = sums
            ones, twos = [], []
            mask = widen(mk[pl.ds(m.main[0] + at, 16), :], 512)
            for c in range(0, wide, 512):
                hat = (third[t, pl.ds(at, 16), c : c + 512] - mean[:, c : c + 512]) * rstd[:, c : c + 512]
                z = slow1[t, pl.ds(at, 16), c : c + 512] + hat * gain[:, c : c + 512] + bias[:, c : c + 512]
                sigma = sigmoid(z)
                out[t, pl.ds(at, 16), c : c + 512] = z * sigma * mask
                grad = cot[t, pl.ds(at, 16), c : c + 512].astype(F32) * mask
                grad = grad * (sigma * (1.0 + z * (1.0 - sigma)))
                pre[t, pl.ds(at, 16), c : c + 512] = grad
                ones.append(sublane_sums(grad))
                twos.append(sublane_sums(grad * hat))
            return one + jnp.concatenate(ones, axis=1), two + jnp.concatenate(twos, axis=1)

        carry = chunked(spots, 16, turn, carry)
    s[...] = jnp.concatenate([row_sum(carry[0]), row_sum(carry[1])], axis=1)


def slow_third_back(m, n, frames, lo3, lo2, at, halo, st, pre, third, n3, z, n2, wp, g, b, mk, d3, e2, s, gb):
    spots, wide = pre.shape[1], pre.shape[2]
    width = z.shape[2]
    count = widen(mk[m.slow[0] : m.slow[0] + 1, :], wide)
    one, two = totals(st, at, wide)
    gb[0:1, :] = one
    gb[1:2, :] = two
    mean, rstd = n3[0:1, :], n3[1:2, :]
    scale = g[n : n + 1, lo3 : lo3 + wide] * rstd
    one = one / count
    two = two / count * rstd
    for t in range(frames):

        def turn(i, carry, t=t):
            mask = widen(mk[pl.ds(m.main[0] + i, 16), :], 512)
            for c in range(0, wide, 512):
                hat = (third[t + halo, pl.ds(i, 16), c : c + 512] - mean[:, c : c + 512]) * two[:, c : c + 512]
                grad = pre[t, pl.ds(i, 16), c : c + 512] - mask * (one[:, c : c + 512] + hat)
                d3[t, pl.ds(i, 16), c : c + 512] = (scale[:, c : c + 512] * grad).astype(BF16)
            return carry

        chunked(spots, 16, turn, 0)
    out = dot_nt(flat(d3[...]), wp[...])
    mean, rstd = n2[0:1, :], n2[1:2, :]
    gain = g[n : n + 1, lo2 : lo2 + width]
    bias = b[n : n + 1, lo2 : lo2 + width]
    back_act(m, frames, spots, out, z, 0, mean, rstd, gain, bias, mk, e2, s)


def back_act(m, frames, spots, out, z, col0, mean, rstd, gain, bias, mk, e, s):
    width = out.shape[1]
    mask = widen(mk[m.main[0] : m.main[1], :], width)
    one = jnp.zeros((8, width), F32)
    two = jnp.zeros((8, width), F32)
    for t in range(frames):
        hat = (z[t, :, col0 : col0 + width] - mean) * rstd
        grad = out[t * spots : (t + 1) * spots] * mask * silu_slope(hat * gain + bias)
        e[t] = grad
        one = one + sublane_sums(grad)
        two = two + sublane_sums(grad * hat)
    s[...] = jnp.concatenate([row_sum(one), row_sum(two)], axis=1)


def fast_third_back(m, n, frames, group, lo3, lo2, at, st, pre, ft, n3, z, n2, wp, g, b, mk, d3, e2, s, gb):
    spots = z.shape[1]
    count = mk[m.fast[0] : m.fast[0] + 1, :]
    one, two = totals(st, at, LANES)
    gb[0:1, :] = one
    gb[1:2, :] = two
    mean, rstd = n3[0:1, :], n3[1:2, :]
    scale = g[n : n + 1, lo3 : lo3 + LANES] * rstd
    one = one / count
    two = two / count * rstd
    mask = mk[m.main[0] : m.main[1], :]
    for t in range(frames):
        for f in range(group):
            hat = (ft[t, :, f * LANES : (f + 1) * LANES] - mean) * two
            grad = pre[t * group + f] - mask * (one + hat)
            d3[t, :, f * LANES : (f + 1) * LANES] = (scale * grad).astype(BF16)
    out = dot_nt(flat(d3[...]), wp[...])
    mean, rstd = n2[0:1, :], n2[1:2, :]
    gain = g[n : n + 1, lo2 : lo2 + LANES]
    bias = b[n : n + 1, lo2 : lo2 + LANES]
    back_act(m, frames, spots, out, z, 0, mean, rstd, gain, bias, mk, e2, s)


def space_back(
    m, n, frames, cols, lo2, lo1, at, width, col0, packed, span,
    st, e, erow, z, zrow, nz, z1, n1, w, g, b, mk, d2, e1, s, gb, vw,
):
    spots = z.shape[1]
    count = widen(mk[span[0] : span[0] + 1, :], width)
    one, two = totals(st, at, width, packed)
    gb[0:1, :] = one
    gb[1:2, :] = two
    mean, rstd = nz[0:1, :], nz[1:2, :]
    scale = g[n : n + 1, lo2 : lo2 + width] * rstd
    one = one / count
    two = two / count * rstd
    mask = widen(mk[m.ext[0] : m.ext[1], :], width)
    for t in range(frames):
        grad = jnp.concatenate([erow[t], e[t], erow[t]], axis=0)
        value = jnp.concatenate([zrow[t], z[t], zrow[t]], axis=0)
        grad = scale * mask * (grad - (one + (value - mean) * two))
        d2[t] = grad[cols : cols + spots].astype(BF16)
        store_shifts(vw, t, grad.astype(BF16).astype(F32), cols)
    total = None
    for i in range(3):
        rows = (2 - i) * cols
        for j in range(3):
            lane = (2 - j) * width
            part = dot_nt(flat(vw[:, rows : rows + spots, lane : lane + width]), w[i, j * width : (j + 1) * width, :])
            total = part if total is None else total + part
    mean, rstd = n1[0:1, :], n1[1:2, :]
    gain = g[n : n + 1, lo1 : lo1 + width]
    bias = b[n : n + 1, lo1 : lo1 + width]
    back_act(m, frames, spots, total, z1, col0, mean, rstd, gain, bias, mk, e1, s)


def first_taps(frames, dw):
    return [flat(dw[2 - j : 2 - j + frames]) for j in range(3)]


def time_back(taps, wt, lo, size):
    out = dot_nt(taps[0], wt[0, lo : lo + size, :])
    for j in range(1, 3):
        out = out + dot_nt(taps[j], wt[j, lo : lo + size, :])
    return out


def slow_first_back(m, n, frames, lo1, at, st, e, ep, en, z, zp, zn, n1, wt, y, nl, g, b, mk, dw, el, s, gb):
    spots, width = z.shape[1], z.shape[2]
    lat = nl.shape[1]
    wide = wt.shape[1] - lat
    count = widen(mk[m.slow[0] : m.slow[0] + 1, :], width)
    one, two = totals(st, at, width)
    gb[0:1, :] = one
    gb[1:2, :] = two
    mean, rstd = n1[0:1, :], n1[1:2, :]
    scale = g[n : n + 1, lo1 : lo1 + width] * rstd
    one = one / count
    two = two / count * rstd
    sources = (
        [(ep, zp, m.prev)] + [(e.at[t], z.at[t], m.main) for t in range(frames)] + [(en, zn, m.next)]
    )
    for k, (grad, value, span) in enumerate(sources):
        mask = widen(mk[span[0] : span[1], :], width)
        dw[k] = (scale * mask * (grad[...] - (one + (value[...] - mean) * two))).astype(BF16)
    out = time_back(first_taps(frames, dw), wt, wide, lat)
    back_act(
        m, frames, spots, out, y, 0, nl[0:1, :], nl[1:2, :], g[n : n + 1, 0:lat], b[n : n + 1, 0:lat], mk, el, s
    )


def slow_input_last(m, frames, dw, wt, pre, mk, gx):
    spots, wide = pre.shape[1], pre.shape[2]
    taps = first_taps(frames, dw)
    mask = widen(mk[m.main[0] : m.main[1], :], 256)
    for c in range(0, wide, 256):
        out = time_back(taps, wt, c, 256)
        for t in range(frames):
            gx[t, :, c : c + 256] = (out[t * spots : (t + 1) * spots] + pre[t, :, c : c + 256]) * mask


def slow_input_back(m, n, frames, lo3, halo, dw, wt, pre, xm, third, n3, g, b, mk, pre0, s3):
    spots, wide = pre.shape[1], pre.shape[2]
    taps = first_taps(frames, dw)
    mask = widen(mk[m.main[0] : m.main[1], :], 256)
    ones, twos = [], []
    for c in range(0, wide, 256):
        out = time_back(taps, wt, c, 256)
        mean, rstd = n3[0:1, c : c + 256], n3[1:2, c : c + 256]
        gain = g[n - 1 : n, lo3 + c : lo3 + c + 256]
        bias = b[n - 1 : n, lo3 + c : lo3 + c + 256]
        one = jnp.zeros((8, 256), F32)
        two = jnp.zeros((8, 256), F32)
        for t in range(frames):
            grad = (out[t * spots : (t + 1) * spots] + pre[t, :, c : c + 256]) * mask
            hat = (third[t + halo, :, c : c + 256] - mean) * rstd
            z0 = xm[t + 1, :, c : c + 256].astype(F32) + hat * gain + bias
            grad = grad * silu_slope(z0)
            pre0[t, :, c : c + 256] = grad
            one = one + sublane_sums(grad)
            two = two + sublane_sums(grad * hat)
        ones.append(row_sum(one))
        twos.append(row_sum(two))
    s3[...] = jnp.concatenate(ones + twos, axis=1)


def fast_first_back(
    m, n, frames, lo1, at1, atl, st1, stl, el, eln, ef, efp, efn, y, yp, yn, nl, n1, gs, g, mk,
    dl, dfw, dln, dfp, dfn, gbl, gb1,
):
    lat = nl.shape[1]
    count = widen(mk[m.slow[0] : m.slow[0] + 1, :], lat)
    one, two = totals(stl, atl, lat)
    gbl[0:1, :] = one
    gbl[1:2, :] = two
    mean, rstd = nl[0:1, :], nl[1:2, :]
    scale = gs[n : n + 1, 0:lat] * rstd
    one = one / count
    two = two / count * rstd

    def lat_grad(grad, value, span):
        mask = widen(mk[span[0] : span[1], :], lat)
        return (scale * mask * (grad - (one + (value - mean) * two))).astype(BF16)

    for t in range(frames):
        dl[t] = lat_grad(el[t], y[t, :, 0:lat], m.main)
    dln[...] = lat_grad(eln[...], yn[:, 0:lat], m.next)
    fcount = mk[m.fast[0] : m.fast[0] + 1, :]
    fone, ftwo = totals(st1, at1, LANES, True)
    gb1[0:1, :] = fone
    gb1[1:2, :] = ftwo
    fmean, frstd = n1[0:1, :], n1[1:2, :]
    fscale = g[n : n + 1, lo1 : lo1 + LANES] * frstd
    fone = fone / fcount
    ftwo = ftwo / fcount * frstd

    def first_grad(grad, value, span):
        mask = mk[span[0] : span[1], :]
        return (fscale * mask * (grad - (fone + (value - fmean) * ftwo))).astype(BF16)

    for t in range(frames):
        dfw[t] = first_grad(ef[t], y[t, :, lat:], m.main)
    dfp[...] = first_grad(efp[...], yp[:, lat:], m.prev)
    dfn[...] = first_grad(efn[...], yn[:, lat:], m.next)


def fast_input_back(m, n, frames, group, lo3, last, dl, dfw, dln, dfp, dfn, w7, pre, *rest):
    if last:
        mk, gx, buf = rest
    else:
        fw0, ft, n3, g, b, mk, pre0, s, buf = rest
    spots, lat = dl.shape[1], dl.shape[2]
    both = jnp.concatenate([flat(dl[...]), flat(dfw[...])], axis=1)
    buf[...] = jnp.zeros(buf.shape, F32)
    out = dot_nt(both, w7[...])
    for t in range(frames):
        for f in range(7):
            k = group * t + f
            buf[k] = buf[k] + out[t * spots : (t + 1) * spots, f * LANES : (f + 1) * LANES]
    buf[2] = buf[2] + dot_nt(dfp[...], w7[6 * LANES : 7 * LANES, lat:])
    after = dot_nt(jnp.concatenate([dln[...], dfn[...]], axis=1), w7[0 : 2 * LANES, :])
    total = frames * group
    for f in range(2):
        buf[total + f] = buf[total + f] + after[:, f * LANES : (f + 1) * LANES]
    mask = mk[m.main[0] : m.main[1], :]
    if last:
        for k in range(total):
            gx[k] = (pre[k] + buf[2 + k]) * mask
        return
    mean, rstd = n3[0:1, :], n3[1:2, :]
    gain = g[n - 1 : n, lo3 : lo3 + LANES]
    bias = b[n - 1 : n, lo3 : lo3 + LANES]
    one = jnp.zeros((8, LANES), F32)
    two = jnp.zeros((8, LANES), F32)
    for k in range(total):
        t, f = k // group, k % group
        hat = (ft[t, :, f * LANES : (f + 1) * LANES] - mean) * rstd
        z0 = fw0[2 + k].astype(F32) + hat * gain + bias
        grad = (pre[k] + buf[2 + k]) * mask * silu_slope(z0)
        pre0[k] = grad
        one = one + sublane_sums(grad)
        two = two + sublane_sums(grad * hat)
    s[...] = jnp.concatenate([row_sum(one), row_sum(two)], axis=1)


def point_weights(a2, d3, out):
    acts = flat(a2[...])
    for k in range(out.shape[0]):
        out[k] = dot_tn(acts, flat(d3[:, :, k * 256 : (k + 1) * 256])).astype(BF16)


def space_weights(cols, aw, d2, out, vw):
    frames, spots, width = d2.shape
    for t in range(frames):
        store_shifts(vw, t, aw[t].astype(F32), cols)
    grads = flat(d2[...])
    for i in range(3):
        out[i] = dot_tn(flat(vw[:, i * cols : i * cols + spots, :]), grads).astype(BF16)


def time_weights(skip, slow, jl, dw, out):
    frames, spots, width = jl.shape
    wide = slow.shape[2]
    grads = jnp.concatenate([flat(dw[2 - j : 2 - j + frames]) for j in range(3)], axis=1)
    for c in range(0, wide + jl.shape[2], 256):
        if c < wide:
            acts = flat(slow[skip : skip + frames, :, c : c + 256])
        else:
            acts = flat(jl[:, :, c - wide : c - wide + 256])
        got = dot_tn(acts, grads)
        for j in range(3):
            out[j, c : c + 256, :] = got[:, j * width : (j + 1) * width].astype(BF16)


def group_blocks(value, group):
    size = LANES // group
    rows = lax.broadcasted_iota(jnp.int32, (LANES, LANES), 0) >> (size.bit_length() - 1)
    lanes = lax.broadcasted_iota(jnp.int32, (LANES, LANES), 1) >> (size.bit_length() - 1)
    kept = jnp.where(rows == lanes, value, 0.0)
    kept = kept + pltpu.roll(kept, 64, 1)
    kept = kept + pltpu.roll(kept, 32, 1)
    total = kept[0:size]
    for k in range(1, group):
        total = total + kept[k * size : (k + 1) * size]
    return total


def at_lanes(blocks):
    lanes = lax.broadcasted_iota(jnp.int32, blocks[0].shape, 1) >> 5
    out = jnp.zeros(blocks[0].shape, F32)
    for k, block in enumerate(blocks):
        out = jnp.where(lanes == k, block, out)
    return out


def fast_weights(group, cols, lat, fw, dl, df, fa1, d2, fa2, d3, out, vw):
    frames, spots, _ = dl.shape
    size = LANES // group
    both = jnp.concatenate([flat(dl[...]), flat(df[...])], axis=1)
    taps = [[None] * group for _ in range(3)]
    for f in range(7):
        acts = jnp.concatenate([fw[group * t + f] for t in range(frames)], axis=0)
        got = dot_tn(acts, both)
        if f < 5:
            out[f * LANES : (f + 1) * LANES, :] = got[:, :lat].astype(BF16)
        for k in range(group):
            if 0 <= f - k - 1 < 3:
                taps[f - k - 1][k] = got[:, lat:]
    lanes = lax.broadcasted_iota(jnp.int32, (LANES, LANES), 1) >> (size.bit_length() - 1)
    tap_sums = []
    for j in range(3):
        kept = jnp.zeros((LANES, LANES), F32)
        for k in range(group):
            kept = jnp.where(lanes == k, taps[j][k], kept)
        kept = kept + pltpu.roll(kept, 64, 1)
        tap_sums.append(kept + pltpu.roll(kept, 32, 1))
    low = 5 * LANES
    out[low : low + LANES, 0:LANES] = at_lanes(tap_sums).T.astype(BF16)
    for t in range(frames):
        store_shifts(vw, t, fa1[t].astype(F32), cols)
    grads = flat(d2[...])
    for i in range(3):
        got = dot_tn(flat(vw[:, i * cols : i * cols + spots, :]), grads)
        blocks = [group_blocks(got[j * LANES : (j + 1) * LANES], group) for j in range(3)]
        out[low + size * i : low + size * (i + 1), LANES : 2 * LANES] = at_lanes(blocks).astype(BF16)
    acts = flat(fa2[...])
    total = jnp.zeros((size, LANES), F32)
    for k in range(group):
        got = dot_tn(acts, flat(d3[:, :, k * LANES : (k + 1) * LANES]))
        total = total + got[k * size : (k + 1) * size]
    out[low + 3 * size : low + 4 * size, LANES : 2 * LANES] = total.astype(BF16)


def unpack_fast(n, inner, load, outs):
    glat, gft, gfs, gfp = outs
    low = glat.shape[1]
    for at in range(0, low, inner):
        glat[n, at : at + inner, :] = load(at, inner)
    for i in range(4):
        got = load(low + inner * i, inner)
        if i < 3:
            gft[n, i] = got[:, 0:LANES]
            for j in range(3):
                moved = got[:, LANES:] if j == 0 else pltpu.roll(got[:, LANES:], LANES - inner * j, 1)
                gfs[n, 3 * i + j] = moved[:, 0:inner]
        else:
            gfp[n] = got[:, LANES:]


def rows_of(one, two=None):
    def load(at, count):
        ref = one
        size = one.shape[1]
        if two is not None:
            core, rest = at // (8 * size), at % (8 * size)
            if rest >= 4 * size:
                ref, rest = two, rest - 4 * size
            at = core * 4 * size + rest
        block, row = at // size, at % size
        assert row + count <= size
        return ref[block, row : row + count, :].astype(F32)

    return load


def copy_rows(start, one, out):
    for at in range(0, out.shape[0], 256):
        out[at : at + 256, :] = one[start + at : start + at + 256, :].astype(F32)


def copy_columns(start, one, out):
    for at in range(0, out.shape[1], 256):
        out[:, at : at + 256] = one[start + at : start + at + 256, :].astype(F32)


def place_rows(start, step, one, two, out):
    load = rows_of(one, two)
    for at in range(0, out.shape[0], step):
        out[at : at + step, :] = load(start + at, step)


def place_columns(start, one, two, out):
    load = rows_of(one, two)
    for at in range(0, out.shape[1], 256):
        out[:, at : at + 256] = load(start + at, 256)


def place_fast(inner, one_one, one_two, zero, *outs):
    unpack_fast(1, inner, rows_of(one_one, one_two), outs)
    unpack_fast(0, inner, rows_of(zero), outs)


def assemble_norms(inner, *refs):
    sums, (gs, bs, gf, bf) = refs[:-4], refs[-4:]
    lanes = lax.broadcasted_iota(jnp.int32, (8, LANES), 1) >> (inner.bit_length() - 1)
    for n in range(2):
        slow, fast = sums[7 * n : 7 * n + 4], sums[7 * n + 4 : 7 * n + 7]
        for row, gslow, gfast in ((1, gs, gf), (0, bs, bf)):
            at = 0
            for part in slow:
                gslow[n : n + 1, at : at + part.shape[1]] = part[row : row + 1, :]
                at += part.shape[1]
            one, two, three = [jnp.broadcast_to(part[row : row + 1, :], (8, LANES)) for part in fast]
            three = pltpu.roll(three, 2 * inner, 1)
            head = jnp.where(lanes == 0, one, jnp.where(lanes == 1, two, three))
            gfast[n : n + 1, 0:LANES] = head[0:1]
            gfast[n : n + 1, LANES : LANES + 2 * inner] = three[0:1, 0 : 2 * inner]


def on_device(
    x_slow,
    x_fast,
    w_lateral,
    w_slow_time,
    w_slow_space,
    w_slow_point,
    w_fast_time,
    w_fast_space,
    w_fast_point,
    gain_slow,
    bias_slow,
    gain_fast,
    bias_fast,
    clip_size,
    cot_slow,
    cot_fast,
):
    frames, fast_frames = x_slow.shape[0], x_fast.shape[0]
    group = fast_frames // frames
    rows, cols = x_slow.shape[3], x_slow.shape[4]
    spots = rows * cols
    wide, fwide = x_slow.shape[5], x_fast.shape[5]
    lat = w_lateral.shape[3]
    width = w_slow_space.shape[3]
    inner = w_fast_space.shape[3]
    packs = group * fwide
    both = lat + LANES
    m = Masks(spots, cols)
    devices = lax.axis_size("path") * lax.axis_size("rows")
    path = lax.axis_index("path")
    ext = spots + 2 * cols
    lo1, lo2, lo3 = lat, lat + width, lat + 2 * width
    every = slice(None)

    def part(fn, *static):
        return functools.partial(fn, *static)

    xs = x_slow.reshape(frames, spots, wide)
    xf = x_fast.reshape(fast_frames, spots, fwide)
    cs = cot_slow.reshape(frames, spots, wide)
    cf = cot_fast.reshape(fast_frames, spots, fwide)
    wft = jnp.swapaxes(w_fast_time, 2, 3)
    wfs_raw = w_fast_space.reshape(2, 9, inner, inner)
    wsp = w_slow_space.reshape(2, 3, 3 * width, width)

    def packed(value):
        return jnp.concatenate(
            [value[:, 0:inner]] * group + [value[:, inner : 2 * inner]] * group + [value[:, 2 * inner :]],
            axis=1,
        )

    xf_edge = swap_path(jnp.where(path > 0, xf[:2], xf[-2:]))
    xs_edge = swap_path(jnp.where(path > 0, xs[0], xs[-1]))

    def payload(k, *sums):
        size = sum(k.temps[s[1]].shape[1] for s in sums)
        out = k.give((devices, 1, size))
        k.step(spread_sums, *sums, out)
        return out

    def row_out(k, z, mk, col0, size):
        out = k.give((frames, cols, size))
        k.step(part(own_row, m, spots, cols, col0, size), z, mk, out)
        return out

    def edge_out(k, z, mk, size, tail=0):
        out = k.give((spots, size), BF16)
        k.step(part(own_edge, m, 0, tail), z, mk, out)
        return out

    def finish(k, **handles):
        got = k.run()
        return {name: got[handle[1]] for name, handle in handles.items()}

    def other_row(value):
        return swap(value, "rows", 1)

    first_flops = 2 * frames * spots * 7 * fwide * both
    k = Stage("entry")
    mk_out = k.give((m.rows, LANES))
    place = jnp.stack([lax.axis_index("rows"), path]).astype(jnp.int32)
    k.step(
        part(make_masks, m, rows, cols, lax.axis_size("path") - 1), k.scalar(place), k.scalar(clip_size), mk_out
    )
    w7_out = k.give((7 * fwide, both), BF16)
    k.step(part(make_w7, lat, group), k.take(w_lateral, 0), k.take(wft, 0), w7_out)
    fw = k.give((fast_frames + 4, spots, fwide), BF16)
    y = k.give((frames, spots, both))
    sy = k.temp((1, 2 * both))
    edge = k.take(xf_edge)
    k.step(
        part(fast_entry, m, frames, group), k.take(xf), edge, edge, mk_out, w7_out, fw, y, sy, flops=first_flops
    )
    pay = payload(k, sy)
    got = finish(
        k, mk=mk_out, w7=w7_out, fw=fw, y=y, pay=pay, ff_row=row_out(k, y, mk_out, lat, LANES),
        edge=edge_out(k, y, mk_out, both),
    )
    mk = got["mk"]
    saved = [{"fw": got["fw"], "y": got["y"], "w7": got["w7"]}, {}]
    st = gather_sums(got["pay"])
    saved[0]["ff_row"] = other_row(got["ff_row"])
    saved[0]["y_edge"] = swap_path(got["edge"])
    mk, wft, gain_fast, bias_fast = lax.optimization_barrier((mk, wft, gain_fast, bias_fast))
    gf, bf = packed(gain_fast), packed(bias_fast)
    k = Stage("prepare")
    w7_out = k.give((7 * fwide, both), BF16)
    k.step(part(make_w7, lat, group), k.take(w_lateral, 1), k.take(wft, 1), w7_out)
    blocks = []
    for n in range(2):
        blocks += [k.give((3, 3 * LANES, LANES), BF16), k.give((LANES, packs), BF16)]
        k.step(part(make_blocks, group), k.take(wfs_raw, n), k.take(w_fast_point, n), *blocks[-2:])
    got = finish(k, w7=w7_out, wfs0=blocks[0], wfp0=blocks[1], wfs1=blocks[2], wfp1=blocks[3])
    saved[1]["w7"] = got["w7"]
    wfs, wfp = [got["wfs0"], got["wfs1"]], [got["wfp0"], got["wfp1"]]
    k = Stage("slow_partial")
    xm = k.give((frames + 2, spots, wide), BF16)
    fpart = k.give((frames, spots, width))
    edge = k.take(xs_edge)
    k.step(
        part(slow_partial, m, frames),
        k.take(xs), edge, edge, k.take(mk), k.take(w_slow_time, 0, every, slice(0, wide)), xm, fpart,
        flops=2 * frames * spots * 3 * wide * width,
    )
    got = finish(k, sw=xm, fpart=fpart)
    saved[0]["sw"] = got["sw"]
    fpart_in = got["fpart"]

    for n in range(2):
        v = saved[n]
        k = Stage("join")
        mk_in, gs, bs = k.take(mk), k.take(gain_slow), k.take(bias_slow)
        st_in = k.take(st)
        names = {}
        if n == 0:
            fpart = k.take(fpart_in)
        else:
            fpart = k.temp((frames, spots, width))
            names.update(
                slow1=k.give((frames, spots, wide)),
                sw=k.give((frames + 2, spots, wide), BF16),
            )
            n3 = k.give((2, wide))
            k.step(
                part(slow_next, m, 0, frames, lo3, 2 * both),
                st_in, k.take(saved[0]["third"]), k.take(saved[0]["sw"]),
                k.take(w_slow_time, 1, every, slice(0, wide)), gs, bs, mk_in,
                names["slow1"], names["sw"], fpart, n3,
                flops=2 * frames * spots * 3 * wide * width,
            )
            names["n3"] = n3
        y_in, edge = k.take(v["y"]), k.take(v["y_edge"])
        jl = k.give((frames, spots, lat), BF16)
        first = k.give((frames, spots, width))
        nl = k.give((2, lat))
        s_first, s_fs = k.temp((1, 2 * width)), k.temp((1, 2 * LANES))
        k.step(
            part(lat_join, m, n, frames, lat),
            st_in, y_in, edge, edge, fpart, k.take(w_slow_time, n, every, slice(wide, wide + lat)), gs, bs, mk_in,
            jl, first, s_first, nl, k.temp((frames + 2, spots, lat), BF16),
            flops=2 * frames * spots * 3 * lat * width,
        )
        fa1 = k.give((frames, ext, LANES), BF16)
        fs = k.give((frames, spots, LANES))
        nf1 = k.give((2, LANES))
        k.step(
            part(space_forward, m, n, frames, cols, 0, 2 * lat, LANES, lat, True, m.fast),
            st_in, y_in, k.take(v["ff_row"]), k.take(wfs[n]), k.take(gf), k.take(bf), mk_in,
            fa1, fs, s_fs, nf1, k.temp((frames, ext, 3 * LANES), BF16),
            flops=2 * frames * spots * 9 * LANES * LANES,
        )
        pay = payload(k, s_first, s_fs)
        got = finish(
            k, jl=jl, first=first, nl=nl, fa1=fa1, fs=fs, nf1=nf1, pay=pay,
            first_row=row_out(k, first, mk_in, 0, width), fs_row=row_out(k, fs, mk_in, 0, LANES),
            first_edge=edge_out(k, first, mk_in, width), **names,
        )
        st = gather_sums(got["pay"])
        for name in ("jl", "first", "nl", "fa1", "fs", "nf1"):
            v[name] = got[name]
        if n == 1:
            slow1, saved[1]["sw"], saved[0]["n3"] = got["slow1"], got["sw"], got["n3"]
        first_row = other_row(got["first_row"])
        v["fs_row"] = other_row(got["fs_row"])
        v["first_edge"] = swap_path(got["first_edge"])
        k = Stage("space")
        mk_in, st_in = k.take(mk), k.take(st)
        a1 = k.give((frames, ext, width), BF16)
        second = k.give((frames, spots, width))
        n1 = k.give((2, width))
        s_second, s_ft = k.temp((1, 2 * width)), k.temp((1, 2 * LANES))
        k.step(
            part(space_forward, m, n, frames, cols, lo1, 0, width, 0, False, m.slow),
            st_in, k.take(v["first"]), k.take(first_row), k.take(wsp, n), k.take(gain_slow), k.take(bias_slow), mk_in,
            a1, second, s_second, n1, k.temp((frames, ext, 3 * width), BF16),
            flops=2 * frames * spots * 9 * width * width,
        )
        fa2 = k.give((frames, spots, LANES), BF16)
        ft = k.give((frames, spots, packs))
        nf2 = k.give((2, LANES))
        k.step(
            part(fast_third, m, n, frames, LANES, 2 * width),
            st_in, k.take(v["fs"]), k.take(wfp[n]), k.take(gf), k.take(bf), mk_in, fa2, ft, s_ft, nf2,
            flops=2 * frames * spots * LANES * packs,
        )
        pay = payload(k, s_second, s_ft)
        names = {"second_row": row_out(k, second, mk_in, 0, width)}
        if n == 0:
            names["second_edge"] = edge_out(k, second, mk_in, width)
            names["ft_edge"] = edge_out(k, ft, mk_in, 2 * fwide, (group - 2) * fwide)
        got = finish(k, a1=a1, second=second, n1=n1, fa2=fa2, ft=ft, nf2=nf2, pay=pay, **names)
        st = gather_sums(got["pay"])
        for name in ("a1", "second", "n1", "fa2", "ft", "nf2"):
            v[name] = got[name]
        v["second_row"] = other_row(got["second_row"])
        halo = 1 - n
        edges = []
        k = Stage("third")
        if n == 0:
            ft_edge = k.take(swap_path(got["ft_edge"]))
            edges = [k.take(swap_path(got["second_edge"]))] * 2
        mk_in, st_in = k.take(mk), k.take(st)
        a2 = k.give((frames, spots, width), BF16)
        third = k.give((frames + 2 * halo, spots, wide))
        n2 = k.give((2, width))
        nf3 = k.give((2, LANES))
        s_third = k.temp((1, 2 * wide))
        names = {}
        if n == 0:
            names.update(
                f1=k.give((fast_frames, spots, fwide)),
                fw=k.give((fast_frames + 4, spots, fwide), BF16),
                y=k.give((frames, spots, both)),
            )
            s_fast = k.temp((1, 2 * both))
            k.step(
                part(fast_next, m, n, frames, group, 2 * LANES, 2 * width),
                st_in, k.take(v["ft"]), ft_edge, ft_edge, k.take(v["fw"]), k.take(saved[1]["w7"]),
                k.take(gf), k.take(bf), mk_in, names["f1"], names["fw"], names["y"], s_fast, nf3,
                flops=first_flops,
            )
        else:
            names.update(out_fast=k.give((fast_frames, spots, fwide)), pre_f=k.give((fast_frames, spots, fwide)))
            s_fast = k.temp((1, 2 * LANES))
            k.step(
                part(fast_last, m, n, frames, group, 2 * LANES, 2 * width),
                st_in, k.take(v["ft"]), k.take(fast1), k.take(cf), k.take(gf), k.take(bf), mk_in,
                names["out_fast"], names["pre_f"], s_fast, nf3,
            )
        k.step(
            part(slow_third, m, n, frames, lo2, halo),
            st_in, k.take(v["second"]), *edges, k.take(w_slow_point, n), k.take(gain_slow), k.take(bias_slow), mk_in,
            a2, third, s_third, n2, k.temp((frames + 2 * halo, spots, width), BF16),
            flops=2 * frames * spots * width * wide,
        )
        if n == 0:
            pay = payload(k, s_fast, s_third)
            names["ff_row"] = row_out(k, names["y"], mk_in, lat, LANES)
            names["y_edge"] = edge_out(k, names["y"], mk_in, both)
        else:
            pay = payload(k, s_third, s_fast)
        got = finish(k, a2=a2, third=third, n2=n2, nf3=nf3, pay=pay, **names)
        st = gather_sums(got["pay"])
        for name in ("a2", "third", "n2", "nf3"):
            v[name] = got[name]
        if n == 0:
            fast1 = got["f1"]
            saved[1].update(
                fw=got["fw"], y=got["y"], ff_row=other_row(got["ff_row"]), y_edge=swap_path(got["y_edge"])
            )
        else:
            out_fast, pre_f = got["out_fast"], got["pre_f"]

    def third_back(k, n, at, st_in, mk_in, pre):
        v = saved[n]
        d3, e2 = k.give((frames, spots, wide), BF16), k.give((frames, spots, width))
        s, gb = k.temp((1, 2 * width)), k.give((2, wide))
        k.step(
            part(slow_third_back, m, n, frames, lo3, lo2, at, 1 - n),
            st_in, k.take(pre), k.take(v["third"]), k.take(v["n3"]), k.take(v["second"]), k.take(v["n2"]),
            k.take(w_slow_point, n), k.take(gain_slow), k.take(bias_slow), mk_in, d3, e2, s, gb,
            flops=2 * frames * spots * width * wide,
        )
        return dict(d3=d3, e2=e2, gb3=gb), s

    def fast_back3(k, n, at, st_in, mk_in, pre):
        v = saved[n]
        d3, e2 = k.give((frames, spots, packs), BF16), k.give((frames, spots, LANES))
        s, gb = k.temp((1, 2 * LANES)), k.give((2, LANES))
        k.step(
            part(fast_third_back, m, n, frames, group, 2 * LANES, LANES, at),
            st_in, k.take(pre), k.take(v["ft"]), k.take(v["nf3"]), k.take(v["fs"]), k.take(v["nf2"]),
            k.take(wfp[n]), k.take(gf), k.take(bf), mk_in, d3, e2, s, gb,
            flops=2 * frames * spots * LANES * packs,
        )
        return dict(d3f=d3, ef2=e2, gbf3=gb), s

    def second_back(k, n, at, st_in, mk_in, e2, e2_row):
        v = saved[n]
        d2, e1 = k.give((frames, spots, width), BF16), k.give((frames, spots, width))
        s, gb = k.temp((1, 2 * width)), k.give((2, width))
        k.step(
            part(space_back, m, n, frames, cols, lo2, lo1, at, width, 0, False, m.slow),
            st_in, k.take(e2), k.take(e2_row), k.take(v["second"]), k.take(v["second_row"]), k.take(v["n2"]),
            k.take(v["first"]), k.take(v["n1"]), k.take(wsp, n), k.take(gain_slow), k.take(bias_slow), mk_in,
            d2, e1, s, gb, k.temp((frames, ext, 3 * width), BF16),
            flops=2 * frames * spots * 9 * width * width,
        )
        return dict(d2=d2, e1=e1, gb2=gb), s

    def fast_back2(k, n, at, st_in, mk_in, ef2, ef2_row):
        v = saved[n]
        d2, e1 = k.give((frames, spots, LANES), BF16), k.give((frames, spots, LANES))
        s, gb = k.temp((1, 2 * LANES)), k.give((2, LANES))
        k.step(
            part(space_back, m, n, frames, cols, LANES, 0, at, LANES, lat, True, m.fast),
            st_in, k.take(ef2), k.take(ef2_row), k.take(v["fs"]), k.take(v["fs_row"]), k.take(v["nf2"]),
            k.take(v["y"]), k.take(v["nf1"]), k.take(wfs[n]), k.take(gf), k.take(bf), mk_in,
            d2, e1, s, gb, k.temp((frames, ext, 3 * LANES), BF16),
            flops=2 * frames * spots * 9 * LANES * LANES,
        )
        return dict(d2f=d2, ef1=e1, gbf2=gb), s

    def first_back(k, n, st_in, mk_in, e1, e1_edge):
        v = saved[n]
        dw, el = k.give((frames + 2, spots, width), BF16), k.give((frames, spots, lat))
        s, gb = k.temp((1, 2 * lat)), k.give((2, width))
        edge, zedge = k.take(e1_edge), k.take(v["first_edge"])
        k.step(
            part(slow_first_back, m, n, frames, lo1, 0),
            st_in, k.take(e1), edge, edge, k.take(v["first"]), zedge, zedge, k.take(v["n1"]),
            k.take(w_slow_time, n), k.take(v["y"]), k.take(v["nl"]), k.take(gain_slow), k.take(bias_slow), mk_in,
            dw, el, s, gb, flops=2 * frames * spots * 3 * lat * width,
        )
        return dict(dw=dw, el=el, gb1=gb), s

    def fast_back1(k, n, st1, at1, stl, atl, mk_in, el, el_edge, ef1, ef1_edge):
        v = saved[n]
        dl, df = k.give((frames, spots, lat), BF16), k.give((frames, spots, LANES), BF16)
        beside = [k.give((spots, lat), BF16), k.give((spots, LANES), BF16), k.give((spots, LANES), BF16)]
        gbl, gb1 = k.give((2, lat)), k.give((2, LANES))
        edge, yedge = k.take(ef1_edge), k.take(v["y_edge"])
        k.step(
            part(fast_first_back, m, n, frames, 0, at1, atl),
            st1, stl, k.take(el), k.take(el_edge), k.take(ef1), edge, edge, k.take(v["y"]), yedge, yedge,
            k.take(v["nl"]), k.take(v["nf1"]), k.take(gain_slow), k.take(gf), mk_in, dl, df, *beside, gbl, gb1,
        )
        return dict(dl=dl, df=df, dln=beside[0], dfp=beside[1], dfn=beside[2], gbl=gbl, gbf1=gb1)

    def weights_point(n, d3):
        k = Stage("point_weights")
        out = k.give((wide // 256, width, 256), BF16)
        k.step(point_weights, k.take(saved[n]["a2"]), k.take(d3), out, flops=2 * frames * spots * width * wide)
        return k.run()[0].reshape(-1, 256)

    def weights_space(n, d2):
        k = Stage("space_weights")
        out = k.give((3, 3 * width, width), BF16)
        k.step(
            part(space_weights, cols), k.take(saved[n]["a1"]), k.take(d2), out,
            k.temp((frames, ext, 3 * width), BF16), flops=2 * frames * spots * 9 * width * width,
        )
        return k.run()[0].reshape(-1, 256)

    def weights_time(n, dw):
        k = Stage("time_weights")
        out = k.give((3, wide + lat, width), BF16)
        k.step(
            part(time_weights, 1), k.take(saved[n]["sw"]), k.take(saved[n]["jl"]), k.take(dw), out,
            flops=2 * frames * spots * 3 * (wide + lat) * width,
        )
        return k.run()[0].reshape(-1, 256)

    def weights_fast(n, dl, df, d2, d3):
        v = saved[n]
        k = Stage("fast_weights")
        out = k.give((7 * LANES - LANES, 2 * LANES), BF16)
        k.step(
            part(fast_weights, group, cols, lat),
            k.take(v["fw"]), k.take(dl), k.take(df), k.take(v["fa1"]), k.take(d2), k.take(v["fa2"]), k.take(d3),
            out, k.temp((frames, ext, 3 * LANES), BF16), flops=first_flops,
        )
        return k.run()[0]

    b1, b0 = {}, {}
    k = Stage("last")
    mk_in, st_in = k.take(mk), k.take(st)
    out_slow, pre = k.give((frames, spots, wide)), k.give((frames, spots, wide))
    n3 = k.give((2, wide))
    s_pre = k.temp((1, 2 * wide))
    k.step(
        part(slow_last, m, 1, frames, lo3),
        st_in, k.take(saved[1]["third"]), k.take(slow1), k.take(cs), k.take(gain_slow), k.take(bias_slow), mk_in,
        out_slow, pre, s_pre, n3,
    )
    names, s_ef2 = fast_back3(k, 1, 2 * wide, st_in, mk_in, pre_f)
    pay = payload(k, s_pre, s_ef2)
    ef2_row = row_out(k, names["ef2"], mk_in, 0, LANES)
    b1 = finish(k, out_slow=out_slow, pre=pre, n3=n3, pay=pay, ef2_row=ef2_row, **names)
    saved[1]["n3"] = b1["n3"]
    out_slow = b1["out_slow"]
    st = gather_sums(b1["pay"])

    k = Stage("back_third")
    ef2_row = other_row(b1["ef2_row"])
    mk_in, st_in = k.take(mk), k.take(st)
    names, s_e2 = third_back(k, 1, 0, st_in, mk_in, b1["pre"])
    more, s_ef1 = fast_back2(k, 1, 2 * wide, st_in, mk_in, b1["ef2"], ef2_row)
    pay = payload(k, s_e2, s_ef1)
    e2_row, ef1_edge = row_out(k, names["e2"], mk_in, 0, width), edge_out(k, more["ef1"], mk_in, LANES)
    b1.update(finish(k, pay=pay, e2_row=e2_row, ef1_edge=ef1_edge, **names, **more))
    st = st_ef1 = gather_sums(b1["pay"])
    e2_row, ef1_edge = other_row(b1["e2_row"]), swap_path(b1["ef1_edge"])
    point1 = weights_point(1, b1["d3"])

    k = Stage("back_space")
    mk_in, st_in = k.take(mk), k.take(st)
    names, s_e1 = second_back(k, 1, 0, st_in, mk_in, b1["e2"], e2_row)
    pay = payload(k, s_e1)
    e1_edge = edge_out(k, names["e1"], mk_in, width)
    b1.update(finish(k, pay=pay, e1_edge=e1_edge, **names))
    st = gather_sums(b1["pay"])
    e1_edge = swap_path(b1["e1_edge"])
    space1 = weights_space(1, b1["d2"])

    k = Stage("back_first")
    mk_in, st_in = k.take(mk), k.take(st)
    names, s_el = first_back(k, 1, st_in, mk_in, b1["e1"], e1_edge)
    names["down"], s_down = k.give((frames, spots, wide)), k.temp((1, 2 * wide))
    k.step(
        part(slow_input_back, m, 1, frames, lo3, 1),
        names["dw"], k.take(w_slow_time, 1), k.take(b1["pre"]), k.take(saved[0]["sw"]), k.take(saved[0]["third"]),
        k.take(saved[0]["n3"]), k.take(gain_slow), k.take(bias_slow), mk_in, names["down"], s_down,
        flops=2 * frames * spots * 3 * wide * width,
    )
    pay = payload(k, s_el, s_down)
    el_edge = edge_out(k, names["el"], mk_in, lat)
    b1.update(finish(k, pay=pay, el_edge=el_edge, **names))
    st = gather_sums(b1["pay"])
    el_edge = swap_path(b1["el_edge"])
    time1 = weights_time(1, b1["dw"])
    sizes1 = [point1.shape[0], space1.shape[0], time1.shape[0]]
    ones = jnp.concatenate([point1, space1, time1], axis=0)
    ones = lax.psum(ones, AXES)

    GRADS = ("dw", "dl", "df", "dln", "dfp", "dfn")
    SUMS = ("gbl", "gb1", "gb2", "gb3", "gbf1", "gbf2", "gbf3")
    steps = exchange_steps()
    core, across, down = steps[:3]
    seen = {}

    def block_zero(st=st, el_edge=el_edge, ef1_edge=ef1_edge, b1=b1, b0=b0):
        b1, b0 = dict(b1), dict(b0)
        k = Stage("back_third")
        mk_in, st_in = k.take(mk), k.take(st)
        names, s_e2 = third_back(k, 0, 2 * lat, st_in, mk_in, b1["down"])
        more = fast_back1(
            k, 1, k.take(st_ef1), 2 * width, st_in, 0, mk_in, b1["el"], el_edge, b1["ef1"], ef1_edge
        )
        inner_grads = [more[name] for name in ("dl", "df", "dln", "dfp", "dfn")]
        more["downf"], s_pf = k.give((fast_frames, spots, fwide)), k.temp((1, 2 * LANES))
        k.step(
            part(fast_input_back, m, 1, frames, group, 2 * LANES, False),
            *inner_grads, k.take(saved[1]["w7"]), k.take(pre_f), k.take(saved[0]["fw"]), k.take(saved[0]["ft"]),
            k.take(saved[0]["nf3"]), k.take(gf), k.take(bf), mk_in, more["downf"], s_pf,
            k.temp((fast_frames + 4, spots, fwide)), flops=first_flops,
        )
        pay = payload(k, s_e2, s_pf)
        e2_row = row_out(k, names["e2"], mk_in, 0, width)
        got = finish(k, pay=pay, e2_row=e2_row, **names, **more)
        for name in more:
            b1[name] = got[name]
        b0.update({name: got[name] for name in names})
        st = gather_sums(got["pay"])
        e2_row = other_row(got["e2_row"])
        point0 = weights_point(0, b0["d3"])
        fast_1 = weights_fast(1, b1["dl"], b1["df"], b1["d2f"], b1["d3f"])

        k = Stage("back_space")
        mk_in, st_in = k.take(mk), k.take(st)
        names, s_e1 = second_back(k, 0, 0, st_in, mk_in, b0["e2"], e2_row)
        more, s_ef2 = fast_back3(k, 0, 2 * width, st_in, mk_in, b1["downf"])
        pay = payload(k, s_e1, s_ef2)
        e1_edge, ef2_row = edge_out(k, names["e1"], mk_in, width), row_out(k, more["ef2"], mk_in, 0, LANES)
        b0.update(finish(k, pay=pay, e1_edge=e1_edge, ef2_row=ef2_row, **names, **more))
        st = gather_sums(b0["pay"])
        e1_edge, ef2_row = swap_path(b0["e1_edge"]), other_row(b0["ef2_row"])
        space0 = weights_space(0, b0["d2"])
        mid = halve(jnp.concatenate([fast_1, point0, space0], axis=0), *core)
        st, mid = lax.optimization_barrier((st, mid))
        mid = halve_both(*parted(mid), across, down)

        k = Stage("back_first")
        mk_in, st_in = k.take(mk), k.take(st)
        names, s_el = first_back(k, 0, st_in, mk_in, b0["e1"], e1_edge)
        more, s_ef1 = fast_back2(k, 0, 2 * width, st_in, mk_in, b0["ef2"], ef2_row)
        pay = payload(k, s_el, s_ef1)
        el_edge, ef1_edge = edge_out(k, names["el"], mk_in, lat), edge_out(k, more["ef1"], mk_in, LANES)
        b0.update(finish(k, pay=pay, el_edge=el_edge, ef1_edge=ef1_edge, **names, **more))
        st = gather_sums(b0["pay"])
        el_edge, ef1_edge = swap_path(b0["el_edge"]), swap_path(b0["ef1_edge"])
        time0 = weights_time(0, b0["dw"])
        late = halve(time0, *core)
        st, mid, late = lax.optimization_barrier((st, mid, late))
        late = halve_both(*parted(late), across, down)
        mid = halve_both(*mid, down, across)

        k = Stage("back_fast")
        mk_in, st_in = k.take(mk), k.take(st)
        more = fast_back1(k, 0, st_in, 2 * lat, st_in, 0, mk_in, b0["el"], el_edge, b0["ef1"], ef1_edge)
        v = saved[0]
        rest = k.give((6 * LANES, 2 * LANES), BF16)
        k.step(
            part(fast_weights, group, cols, lat),
            k.take(v["fw"]), more["dl"], more["df"], k.take(v["fa1"]), k.take(b0["d2f"]), k.take(v["fa2"]),
            k.take(b0["d3f"]), rest, k.temp((frames, ext, 3 * LANES), BF16), flops=first_flops,
        )
        got = finish(k, rest=rest, **more)
        b0.update(got)
        rest, mid, late = lax.optimization_barrier((got["rest"], mid, late))
        rest = halve(rest, *core)
        mid = jnp.concatenate(mid, axis=0)
        seen["fast"], seen["point"] = fast_1.shape[0], point0.shape[0]
        sums = [b0[name] for name in SUMS] + [b1[name] for name in ("gbl", "gbf1")]
        grads = [b0[name] for name in GRADS] + [b1["down"], b1["downf"]]
        return (mid, *late, rest, *grads, *sums)

    like = jax.eval_shape(block_zero)
    got = lax.cond(
        clip_size[0, 0] > 0, block_zero, lambda: tuple(jnp.zeros(o.shape, o.dtype) for o in like)
    )
    mid, late, rest = got[0], got[1:3], got[3]
    b0 = dict(zip(GRADS + ("down", "downf") + SUMS, got[4:19]))
    b1["gbl"], b1["gbf1"] = got[19:21]

    k = Stage("slow_input")
    gx_slow = k.give((frames, spots, wide))
    k.step(
        part(slow_input_last, m, frames),
        k.take(b0["dw"]), k.take(w_slow_time, 0, every, slice(0, wide)), k.take(b0["down"]), k.take(mk), gx_slow,
        flops=2 * frames * spots * 3 * wide * width,
    )
    (gx_slow,) = k.run()
    k = Stage("fast_input")
    gx_fast = k.give((fast_frames, spots, fwide))
    k.step(
        part(fast_input_back, m, 0, frames, group, 2 * LANES, True),
        *[k.take(b0[name]) for name in GRADS[1:]], k.take(saved[0]["w7"]), k.take(b0["downf"]), k.take(mk), gx_fast,
        k.temp((fast_frames + 4, spots, fwide)), flops=first_flops,
    )
    (gx_fast,) = k.run()
    time_rows, space_rows = 3 * (wide + lat), 9 * width
    k = Stage("assemble_one")
    ones_in = k.take(ones)
    gtime, gspace = k.give((2, time_rows, width), F32, 1), k.give((2, space_rows, width), F32, 1)
    gpoint = k.give((2, width, wide), F32, 1)
    k.step(part(copy_rows, sizes1[0] + sizes1[1]), ones_in, gtime)
    k.step(part(copy_rows, sizes1[0]), ones_in, gspace)
    k.step(part(copy_columns, 0), ones_in, gpoint)
    half_done = k.run()

    def spread_both(one, two, tied=()):
        one, two = [one, swap(one, *down)], [two, swap(two, *across)]
        one, two, tied = lax.optimization_barrier((one, two, tied))
        one, two = [jnp.stack(pair) for pair in (one, two)]
        one, two = [one, swap(one, *across)], [two, swap(two, *down)]
        return [pair + [swap(half, *core) for half in pair] for pair in (one, two)], tied

    for step in steps[3:]:
        mid = halve(mid, *step)
    mid = mid.astype(BF16)
    for step in reversed(steps[3:]):
        mid = double(mid, *step)
    (mid_one, mid_two), _ = spread_both(*parted(mid))
    late = halve_both(*late, down, across)
    rest = halve(halve(rest, *across), *down)
    parts = [late[0].shape[0], rest.shape[0], late[1].shape[0]]
    value = jnp.concatenate([late[0], rest, late[1]], axis=0)
    for step in steps[3:4]:
        value, gx_slow = lax.optimization_barrier((halve(value, *step), gx_slow))
    for step in steps[4:]:
        value, gx_fast = lax.optimization_barrier((halve(value, *step), gx_fast))
    value = value.astype(BF16)
    for step in reversed(steps[3:]):
        value = double(value, *step)
    cut = parts[0] + parts[1]
    (one, two), half_done = spread_both(value[:cut], value[cut:], half_done)

    core_bit = lax.axis_index("rows") % 2
    down_bit = (lax.axis_index("rows") // 2) % 2

    k = Stage("assemble")
    flip_one = k.scalar((core_bit * 4 + path * 2 + down_bit).astype(jnp.int32).reshape(1))
    flip_two = k.scalar((core_bit * 4 + down_bit * 2 + path).astype(jnp.int32).reshape(1))
    mid_one, mid_two = k.take_blocks(mid_one, flip_one, every), k.take_blocks(mid_two, flip_two, every)
    start = seen["fast"]
    gspace = k.give((2, space_rows, width), F32, 0, half_done[1])
    k.step(part(place_rows, start + seen["point"], 256), mid_one, mid_two, gspace)
    gpoint = k.give((2, width, wide), F32, 0, half_done[2])
    k.step(part(place_columns, start), mid_one, mid_two, gpoint)
    late_one = k.take_blocks(one, flip_one, slice(0, parts[0]))
    late_two = k.take_blocks(two, flip_two, every)
    gtime = k.give((2, time_rows, width), F32, 0, half_done[0])
    k.step(part(place_rows, 0, 80), late_one, late_two, gtime)
    rest = k.take_blocks(one, flip_one, slice(parts[0], cut))
    fast_outs = [
        k.give((2, 5 * fwide, lat)), k.give((2, 3, inner, fwide)), k.give((2, 9, inner, inner)),
        k.give((2, inner, fwide)),
    ]
    k.step(part(place_fast, inner), mid_one, mid_two, rest, *fast_outs)
    sums = [k.take(b[name]) for b in (b0, b1) for name in ("gbl", "gb1", "gb2", "gb3", "gbf1", "gbf2", "gbf3")]
    norm_outs = [k.give(like.shape) for like in (gain_slow, bias_slow, gain_fast, bias_fast)]
    k.step(part(assemble_norms, inner), *sums, *norm_outs)
    got = k.run()
    glat, gft, gfs, gfp = [got[h[1]] for h in fast_outs]

    return (
        out_slow.reshape(x_slow.shape),
        out_fast.reshape(x_fast.shape),
        gx_slow.reshape(x_slow.shape),
        gx_fast.reshape(x_fast.shape),
        glat.reshape(w_lateral.shape),
        got[gtime[1]].reshape(w_slow_time.shape),
        got[gspace[1]].reshape(w_slow_space.shape),
        got[gpoint[1]],
        jnp.swapaxes(gft, 2, 3),
        gfs.reshape(w_fast_space.shape),
        gfp,
        *[got[h[1]] for h in norm_outs],
    )


def solution(mesh):
    spread = P("path", None, "rows", None, None, None)
    return jax.shard_map(
        on_device,
        mesh=mesh,
        in_specs=(spread, spread) + (P(),) * 12 + (spread, spread),
        out_specs=(spread,) * 4 + (P(),) * 11,
        check_vma=False,
    )
```

```python
import functools

import jax
import jax.numpy as jnp
import numpy as np
from jax import lax
from jax.experimental import pallas as pl
from jax.experimental.pallas import tpu as pltpu
from jax.sharding import PartitionSpec as P

TS = 8
TF = 32
F32 = jnp.float32
BF16 = jnp.bfloat16
EPSILON = 1e-05
LANES = 128
AXES = ("path", "rows")
VMEM_LIMIT = 53 * 2**20


def swap(value, axis, stride):
    pairs = [(source, source ^ stride) for source in range(lax.axis_size(axis))]
    return lax.ppermute(value, axis, pairs)


def gather_sums(spread):
    return lax.all_to_all(spread, AXES, 0, 0, tiled=True)


def swap_path(value):
    assert lax.axis_size("path") == 2
    return lax.ppermute(value, "path", [(0, 1), (1, 0)])


def exchange_steps():
    steps = [("rows", 1), ("path", 1)]
    stride = 2
    while stride < lax.axis_size("rows"):
        steps.append(("rows", stride))
        stride *= 2
    return steps


def halve(value, axis, stride):
    size = value.shape[0] // 2
    upper = (lax.axis_index(axis) // stride) % 2
    keep = lax.dynamic_slice_in_dim(value, upper * size, size, 0)
    give = lax.dynamic_slice_in_dim(value, (1 - upper) * size, size, 0)
    return keep.astype(F32) + swap(give.astype(BF16), axis, stride).astype(F32)


def double(value, axis, stride):
    upper = (lax.axis_index(axis) // stride) % 2
    got = swap(value, axis, stride)
    return jnp.concatenate(
        [jnp.where(upper == 0, value, got), jnp.where(upper == 0, got, value)], axis=0
    )


def halve_both(one, two, first, second):
    return halve(one, *first), halve(two, *second)


def parted(value):
    size = value.shape[0] // 2
    return value[:size], value[size:]


class Stage:
    def __init__(self, name):
        self.name = name
        self.arrays, self.views, self.scalars, self.pairs = [], [], [], []
        self.outs, self.temps, self.steps = [], [], []
        self.entries, self.ontos = [], []
        self.flops = 0

    def take(self, array, *view):
        for at, known in enumerate(self.arrays):
            if known is array:
                break
        else:
            at = len(self.arrays)
            self.arrays.append(array)
        for k, (other, seen) in enumerate(self.views):
            if other == at and seen == view:
                return ("in", k)
        self.views.append((at, view))
        return ("in", len(self.views) - 1)

    def take_blocks(self, values, flip, rows):
        self.pairs.append(([self.take(value, slice(None), rows) for value in values], flip))
        return ("pair", len(self.pairs) - 1)

    def scalar(self, array):
        self.scalars.append(array)
        return ("scalar", len(self.scalars) - 1)

    def give(self, dims, dtype=F32, at=None, onto=None):
        self.outs.append(jax.ShapeDtypeStruct(tuple(dims), dtype))
        self.entries.append(at)
        self.ontos.append(onto)
        return ("out", len(self.outs) - 1)

    def piece(self, handle, *index):
        return ("piece", (handle[1], index))

    def peek(self, handle):
        return ("peek", handle[1])

    def temp(self, dims, dtype=F32):
        self.temps.append(pltpu.VMEM(tuple(dims), dtype))
        return ("temp", len(self.temps) - 1)

    def step(self, fn, *handles, flops=0):
        self.flops += flops
        self.steps.append((fn, handles))

    def sem(self, view, block):
        return 8 * view + block

    def view_shape(self, view):
        at, index = view
        return np.broadcast_to(np.zeros((), np.int8), self.arrays[at].shape)[index].shape

    def run(self):
        arrays, views, outs, steps, pairs = self.arrays, self.views, self.outs, self.steps, self.pairs
        order, home = [], {}
        for k, (members, flip) in enumerate(pairs):
            for j, member in enumerate(members):
                home[member[1]] = (k, j, flip)
        under = [onto for onto in self.ontos if onto is not None]

        def need(handle):
            if handle[0] == "in":
                return [handle[1]]
            return [part[1] for part in pairs[handle[1]][0]] if handle[0] == "pair" else []

        for _, handles in steps:
            for handle in handles:
                for k in need(handle):
                    if k not in order:
                        order.append(k)

        def body(*refs):
            refs = list(refs)

            def cut(count):
                taken = refs[:count]
                del refs[:count]
                return taken

            scalars, hbm_in = cut(len(self.scalars)), cut(len(arrays))
            cut(len(under))
            hbm_out = cut(len(outs))
            alone = [k for k in range(len(views)) if k not in home]
            held = dict(zip(alone, cut(len(alone))))
            joint, made, temps, (sems,) = cut(len(pairs)), cut(len(outs)), cut(len(self.temps)), refs
            copies = {}
            for k in order:
                at, index = views[k]
                src = hbm_in[at].at[index] if index else hbm_in[at]
                if k in home:
                    pair, second, flip = home[k]
                    count = self.view_shape(views[k])[0]
                    copies[k] = []
                    for block in range(count):
                        to = (second * count + block) ^ scalars[flip[1]][0]
                        copies[k].append(
                            pltpu.make_async_copy(src.at[block], joint[pair].at[to], sems.at[self.sem(k, block)])
                        )
                else:
                    copies[k] = [pltpu.make_async_copy(src, held[k], sems.at[self.sem(k, 0)])]
                for copy in copies[k]:
                    copy.start()
            waited, sent = set(), {}
            for fn, handles in steps:
                given = []
                for handle in handles:
                    for k in need(handle):
                        if k not in waited:
                            for copy in copies[k]:
                                copy.wait()
                            waited.add(k)
                    if handle[0] == "piece":
                        given.append(made[handle[1][0]].at[handle[1][1]])
                        continue
                    place = {"in": held, "pair": joint, "out": made, "peek": made, "temp": temps, "scalar": scalars}
                    given.append(place[handle[0]][handle[1]])
                fn(*given)
                for kind, k in handles:
                    if kind == "out" and k not in sent:
                        to = hbm_out[k] if self.entries[k] is None else hbm_out[k].at[self.entries[k]]
                        sent[k] = [pltpu.make_async_copy(made[k], to, sems.at[8 * (len(views) + k)])]
                        sent[k][0].start()
                    elif kind == "piece":
                        k, index = k
                        done = sent.setdefault(k, [])
                        sem = sems.at[8 * (len(views) + k) + len(done)]
                        done.append(pltpu.make_async_copy(made[k].at[index], hbm_out[k].at[index], sem))
                        done[-1].start()
            for done in sent.values():
                for copy in done:
                    copy.wait()

        moved = sum(a.size * a.dtype.itemsize for a in outs)
        for view in views:
            moved += int(np.prod(self.view_shape(view))) * arrays[view[0]].dtype.itemsize
        scratch = [
            pltpu.VMEM(self.view_shape(view), arrays[view[0]].dtype) for k, view in enumerate(views) if k not in home
        ]
        for members, _ in pairs:
            size = self.view_shape(views[members[0][1]])
            scratch.append(
                pltpu.VMEM((len(members) * size[0],) + size[1:], arrays[views[members[0][1]][0]].dtype)
            )
        scratch += [
            pltpu.VMEM(o.shape if at is None else o.shape[1:], o.dtype) for o, at in zip(outs, self.entries)
        ]
        aliases = {}
        for k, onto in enumerate(self.ontos):
            if onto is not None:
                aliases[len(self.scalars) + len(arrays) + len(aliases)] = k
        scratch += self.temps + [pltpu.SemaphoreType.DMA((8 * (len(views) + len(outs)),))]
        return pl.pallas_call(
            body,
            out_shape=tuple(outs),
            in_specs=[pl.BlockSpec(memory_space=pltpu.SMEM) for _ in self.scalars]
            + [pl.BlockSpec(memory_space=pl.ANY) for _ in arrays + under],
            out_specs=tuple(pl.BlockSpec(memory_space=pl.ANY) for _ in outs),
            scratch_shapes=scratch,
            input_output_aliases=aliases,
            compiler_params=pltpu.CompilerParams(vmem_limit_bytes=VMEM_LIMIT),
            cost_estimate=pl.CostEstimate(flops=self.flops, bytes_accessed=moved, transcendentals=0),
            name=self.name,
        )(*self.scalars, *arrays, *under)


class Masks:
    def __init__(self, spots, cols):
        self.main = (0, spots)
        self.ext = (spots, 2 * spots + 2 * cols)
        self.prev = (2 * spots + 2 * cols, 3 * spots + 2 * cols)
        self.next = (3 * spots + 2 * cols, 4 * spots + 2 * cols)
        self.slow = (4 * spots + 2 * cols, 4 * spots + 2 * cols + 8)
        self.fast = (4 * spots + 2 * cols + 8, 4 * spots + 2 * cols + 16)
        self.half = (4 * spots + 2 * cols + 16, 4 * spots + 2 * cols + 24)
        self.path = (4 * spots + 2 * cols + 24, 4 * spots + 2 * cols + 32)
        self.rows = 4 * spots + 2 * cols + 32


def make_masks(m, rows, cols, last, place, clips, mk):
    half = place[0] % 2
    path = place[1]
    side = clips[0, place[0] // 2]
    area = 0
    for k in range(clips.shape[1]):
        area = area + clips[0, k] * clips[0, k]
    shift = cols.bit_length() - 1

    def inside(first, count):
        at = lax.broadcasted_iota(jnp.int32, (count * cols, LANES), 0)
        line = half * rows + first + (at >> shift)
        spot = at & (cols - 1)
        good = (line >= 0) & (line < 2 * rows) & (line < side) & (spot < side)
        return jnp.where(good, 1.0, 0.0)

    main = inside(0, rows)
    mk[m.main[0] : m.main[1], :] = main
    mk[m.ext[0] : m.ext[1], :] = inside(-1, rows + 2)
    mk[m.prev[0] : m.prev[1], :] = main * jnp.where(path > 0, 1.0, 0.0)
    mk[m.next[0] : m.next[1], :] = main * jnp.where(path < last, 1.0, 0.0)

    def fill(span, value):
        mk[span[0] : span[1], :] = jnp.full((8, LANES), value, F32)

    fill(m.slow, TS * area.astype(F32))
    fill(m.fast, TF * area.astype(F32))
    fill(m.half, half.astype(F32))
    fill(m.path, path.astype(F32))


def own_row(m, spots, cols, col0, width, z, mk, row):
    for t in range(z.shape[0]):
        lower = mk[m.half[0] : m.half[0] + 1, :] > 0.5
        for lane in range(0, width, LANES):
            at = col0 + lane
            row[t, :, lane : lane + LANES] = jnp.where(
                lower, z[t, 0:cols, at : at + LANES], z[t, spots - cols : spots, at : at + LANES]
            )


def own_edge(m, lead, tail, z, mk, edge):
    frames = z.shape[0]
    second = mk[m.path[0] : m.path[0] + 1, :] > 0.5
    for lane in range(0, edge.shape[1], LANES):
        edge[:, lane : lane + LANES] = jnp.where(
            second,
            z[0, :, lead + lane : lead + lane + LANES],
            z[frames - 1, :, tail + lane : tail + lane + LANES],
        ).astype(edge.dtype)


def spread_sums(*refs):
    parts, out = refs[:-1], refs[-1]
    row = jnp.concatenate([part[...] for part in parts], axis=1)
    out[...] = jnp.broadcast_to(row[None], out.shape)


def make_w7(lat, group, wl, wf, w7):
    inner = wf.shape[1]
    w7[...] = jnp.zeros(w7.shape, BF16)
    for j in range(wl.shape[0]):
        w7[j * LANES : (j + 1) * LANES, 0:lat] = wl[j]
    at = lax.broadcasted_iota(jnp.int32, (inner, LANES), 0)
    lane = lax.broadcasted_iota(jnp.int32, (inner, LANES), 1)
    places = [jnp.where(lane == at + inner * k, 1.0, 0.0).astype(BF16) for k in range(group)]
    for f in range(1, group + 3):
        used = [k for k in range(group) if 0 <= f - 1 - k < 3]
        got = None
        for k in used:
            more = dot_tn(wf[f - 1 - k], places[k])
            got = more if got is None else got + more
        w7[f * LANES : (f + 1) * LANES, lat : lat + LANES] = got.astype(BF16)


def make_blocks(group, ws, wp, wfs, wfp):
    inner = wp.shape[0]
    at = lax.broadcasted_iota(jnp.int32, (inner, LANES), 0)
    lane = lax.broadcasted_iota(jnp.int32, (inner, LANES), 1)
    tile = jnp.where((lane & (inner - 1)) == at, 1.0, 0.0).astype(BF16)
    shift = inner.bit_length() - 1
    for tap in range(ws.shape[0]):
        got = dot(ws[tap], tile)
        for k in range(group):
            kept = jnp.where((lane >> shift) == k, got, 0.0).astype(BF16)
            row = (tap % 3) * LANES + k * inner
            wfs[tap // 3, row : row + inner, :] = kept
    wfp[...] = jnp.zeros(wfp.shape, BF16)
    for k in range(group):
        wfp[k * inner : (k + 1) * inner, k * LANES : (k + 1) * LANES] = wp[...]


def widen(rows, width):
    return jnp.concatenate([rows] * (width // LANES), axis=1)


def sublane_sums(value):
    return jnp.sum(value.reshape(value.shape[0] // 8, 8, value.shape[1]), axis=0)


def row_sum(value):
    return jnp.sum(value, axis=0, keepdims=True)


def fold_packed(row):
    full = jnp.broadcast_to(row, (8, LANES))
    full = full + pltpu.roll(full, 64, 1)
    full = full + pltpu.roll(full, 32, 1)
    return full[0:1]


def totals(st, lo, width, packed=False):
    first = jnp.sum(st[:, :, lo : lo + width], axis=0)
    second = jnp.sum(st[:, :, lo + width : lo + 2 * width], axis=0)
    if packed:
        return fold_packed(first), fold_packed(second)
    return first, second


def norm_rows(st, lo, width, count, packed=False):
    first, second = totals(st, lo, width, packed)
    mean = first / count
    return mean, lax.rsqrt(second / count - mean * mean + EPSILON)


def keep_norm(lo, width, span, st, mk, nz):
    mean, rstd = norm_rows(st, lo, width, widen(mk[span[0] : span[0] + 1, :], width))
    nz[0:1, :] = mean
    nz[1:2, :] = rstd


def keep_sums(lo, width, st, gb):
    one, two = totals(st, lo, width)
    gb[0:1, :] = one
    gb[1:2, :] = two


def clear(*refs):
    for ref in refs:
        ref[...] = jnp.zeros(ref.shape, F32)


def close_sums(one, two, s):
    s[...] = jnp.concatenate([row_sum(one[...]), row_sum(two[...])], axis=1)


def sigmoid(value):
    return 0.5 * jnp.tanh(0.5 * value) + 0.5


def silu(value):
    return value * sigmoid(value)


def silu_slope(value):
    sigma = sigmoid(value)
    return sigma * (1.0 + value * (1.0 - sigma))


def dot(a, b):
    return jnp.dot(a, b, preferred_element_type=F32)


def dot_nt(a, b):
    return lax.dot_general(a, b, (((1,), (1,)), ((), ())), preferred_element_type=F32)


def dot_tn(a, b):
    return lax.dot_general(a, b, (((0,), (0,)), ((), ())), preferred_element_type=F32)


def flat(value):
    return value.reshape(value.shape[0] * value.shape[1], value.shape[2])


def store_shifts(dst, t, value, cols):
    rows, width = value.shape
    spot = lax.broadcasted_iota(jnp.int32, (rows, width), 0) & (cols - 1)
    left = jnp.where(spot == 0, 0.0, pltpu.roll(value, 1, 0))
    right = jnp.where(spot == cols - 1, 0.0, pltpu.roll(value, rows - 1, 0))
    dst[t, :, 0:width] = left.astype(BF16)
    dst[t, :, width : 2 * width] = value.astype(BF16)
    dst[t, :, 2 * width : 3 * width] = right.astype(BF16)


def taps_of(frames_ref, frames, group):
    return jnp.concatenate(
        [
            jnp.concatenate([frames_ref[group * t + f] for f in range(7)], axis=1)
            for t in range(frames)
        ],
        axis=0,
    )


def entry_sums(y, lat, frames, spots):
    width = y.shape[1]
    one = jnp.zeros((8, width), F32)
    two = jnp.zeros((8, width), F32)
    for t in range(frames):
        part = y[t * spots : (t + 1) * spots]
        one = one + sublane_sums(part)
        two = two + sublane_sums(part * part)
    one = row_sum(one)
    two = row_sum(two)
    return jnp.concatenate([one[:, :lat], two[:, :lat], one[:, lat:], two[:, lat:]], axis=1)


def fast_entry(m, frames, group, x, before, after, mk, w7, fw, y, s):
    spots = x.shape[1]
    count = x.shape[0]

    def put(at, value, span):
        fw[at] = (value.astype(F32) * mk[span[0] : span[1], :]).astype(BF16)

    for k in range(2):
        put(k, before[k], m.prev)
        put(2 + count + k, after[k], m.next)
    for k in range(count):
        put(2 + k, x[k], m.main)
    out = dot(taps_of(fw, frames, group), w7[...])
    for t in range(frames):
        y[t] = out[t * spots : (t + 1) * spots]
    s[...] = entry_sums(out, w7.shape[1] - LANES, frames, spots)


def slow_partial(m, frames, x, before, after, mk, wt, xm, fpart):
    spots, wide = x.shape[1], x.shape[2]
    sources = [(before, m.prev)] + [(x.at[t], m.main) for t in range(frames)] + [(after, m.next)]
    for k, (src, span) in enumerate(sources):
        for lo in range(0, wide, 256):
            mask = widen(mk[span[0] : span[1], :], 256)
            xm[k, :, lo : lo + 256] = (src[:, lo : lo + 256].astype(F32) * mask).astype(BF16)
    out = dot(flat(xm[0:frames]), wt[0, :wide, :])
    for j in range(1, 3):
        out = out + dot(flat(xm[j : j + frames]), wt[j, :wide, :])
    for t in range(frames):
        fpart[t] = out[t * spots : (t + 1) * spots]


def lat_join(m, n, frames, lat, st, y, before, after, fpart, wt, gs, bs, mk, jl, first, s, nl, jw):
    spots = y.shape[1]
    wide = wt.shape[1] - lat
    count = widen(mk[m.slow[0] : m.slow[0] + 1, :], lat)
    mean, rstd = norm_rows(st, 0, lat, count)
    nl[0:1, :] = mean
    nl[1:2, :] = rstd
    scale = rstd * gs[n : n + 1, 0:lat]
    bias = bs[n : n + 1, 0:lat]
    sources = (
        [(before[:, 0:lat], m.prev)]
        + [(y[t, :, 0:lat], m.main) for t in range(frames)]
        + [(after[:, 0:lat], m.next)]
    )
    for k, (value, span) in enumerate(sources):
        mask = widen(mk[span[0] : span[1], :], lat)
        act = (silu((value - mean) * scale + bias) * mask).astype(BF16)
        jw[k] = act
        if 1 <= k <= frames:
            jl[k - 1] = act
    out = flat(fpart[...])
    for j in range(3):
        out = out + dot(flat(jw[j : j + frames]), wt[j, wide:, :])
    one = jnp.zeros((8, out.shape[1]), F32)
    two = jnp.zeros((8, out.shape[1]), F32)
    for t in range(frames):
        part = out[t * spots : (t + 1) * spots]
        first[t] = part
        one = one + sublane_sums(part)
        two = two + sublane_sums(part * part)
    s[...] = jnp.concatenate([row_sum(one), row_sum(two)], axis=1)


def space_forward(
    m, n, frames, cols, lo, at, width, col0, packed, span, st, z, row, w, g, b, mk, aw, out, s, nz, vw
):
    spots = z.shape[1]
    count = widen(mk[span[0] : span[0] + 1, :], width)
    mean, rstd = norm_rows(st, at, width, count, packed)
    nz[0:1, :] = mean
    nz[1:2, :] = rstd
    scale = rstd * g[n : n + 1, lo : lo + width]
    bias = b[n : n + 1, lo : lo + width]
    mask = widen(mk[m.ext[0] : m.ext[1], :], width)
    for t in range(frames):
        value = jnp.concatenate([row[t], z[t, :, col0 : col0 + width], row[t]], axis=0)
        act = silu((value - mean) * scale + bias) * mask
        aw[t] = act.astype(BF16)
        store_shifts(vw, t, act, cols)
    total = dot(flat(vw[:, 0:spots, :]), w[0])
    for i in range(1, 3):
        total = total + dot(flat(vw[:, i * cols : i * cols + spots, :]), w[i])
    mask = widen(mk[m.main[0] : m.main[1], :], width)
    one = jnp.zeros((8, width), F32)
    two = jnp.zeros((8, width), F32)
    for t in range(frames):
        part = total[t * spots : (t + 1) * spots]
        out[t] = part
        part = part * mask
        one = one + sublane_sums(part)
        two = two + sublane_sums(part * part)
    s[...] = jnp.concatenate([row_sum(one), row_sum(two)], axis=1)


def slow_acts(m, n, frames, lo, halo, st, z, *rest):
    if halo:
        before, after, g, b, mk, a2, nz, aw = rest
    else:
        g, b, mk, a2, nz, aw = rest
    width = z.shape[2]
    keep_norm(0, width, m.slow, st, mk, nz)
    mean = nz[0:1, :]
    scale = nz[1:2, :] * g[n : n + 1, lo : lo + width]
    bias = b[n : n + 1, lo : lo + width]
    sources = [(z[t], m.main, t + halo) for t in range(frames)]
    if halo:
        sources += [(before[...], m.prev, 0), (after[...], m.next, frames + 1)]
    for value, span, at in sources:
        mask = widen(mk[span[0] : span[1], :], width)
        act = (silu((value - mean) * scale + bias) * mask).astype(BF16)
        aw[at] = act
        if halo <= at < frames + halo:
            a2[at - halo] = act


def slow_third(frames, halo, at, aw, wp, third, s):
    spots = aw.shape[1]
    wide = s.shape[1] // 2
    out = dot(flat(aw[...]), wp[...])
    one = jnp.zeros((8, 256), F32)
    two = jnp.zeros((8, 256), F32)
    for t in range(frames + 2 * halo):
        part = out[t * spots : (t + 1) * spots]
        third[t] = part.astype(BF16)
        if halo <= t < frames + halo:
            one = one + sublane_sums(part)
            two = two + sublane_sums(part * part)
    s[:, at : at + 256] = row_sum(one)
    s[:, wide + at : wide + at + 256] = row_sum(two)


def fast_third(m, n, frames, lo, at, st, z, wp, g, b, mk, a2, ft, s, nz):
    spots = z.shape[1]
    count = mk[m.fast[0] : m.fast[0] + 1, :]
    mean, rstd = norm_rows(st, at, LANES, count, True)
    nz[0:1, :] = mean
    nz[1:2, :] = rstd
    scale = rstd * g[n : n + 1, lo : lo + LANES]
    bias = b[n : n + 1, lo : lo + LANES]
    mask = mk[m.main[0] : m.main[1], :]
    for t in range(frames):
        a2[t] = (silu((z[t] - mean) * scale + bias) * mask).astype(BF16)
    acts = flat(a2[...])
    one = jnp.zeros((8, LANES), F32)
    two = jnp.zeros((8, LANES), F32)
    out = dot(acts, wp[...])
    for t in range(frames):
        for lane in range(0, wp.shape[1], LANES):
            part = out[t * spots : (t + 1) * spots, lane : lane + LANES]
            ft[t, :, lane : lane + LANES] = part.astype(BF16)
            one = one + sublane_sums(part)
            two = two + sublane_sums(part * part)
    s[...] = jnp.concatenate([row_sum(one), row_sum(two)], axis=1)


def fast_next(m, n, frames, group, lo, at, st, ft, before, after, fw0, w7, g, b, mk, fw1, y, s, nz):
    spots = ft.shape[1]
    count = mk[m.fast[0] : m.fast[0] + 1, :]
    mean, rstd = norm_rows(st, at, LANES, count)
    nz[0:1, :] = mean
    nz[1:2, :] = rstd
    scale = rstd * g[n : n + 1, lo : lo + LANES]
    bias = b[n : n + 1, lo : lo + LANES]
    total = frames * group

    def out_of(k, value, span):
        z = fw0[k].astype(F32) + ((value - mean) * scale + bias)
        return silu(z) * mk[span[0] : span[1], :]

    for k in range(2):
        lane = k * LANES
        fw1[k] = out_of(k, before[:, lane : lane + LANES], m.prev).astype(BF16)
        fw1[2 + total + k] = out_of(2 + total + k, after[:, lane : lane + LANES], m.next).astype(BF16)
    for t in range(frames):
        for f in range(group):
            k = t * group + f
            fw1[2 + k] = out_of(2 + k, ft[t, :, f * LANES : (f + 1) * LANES], m.main).astype(BF16)
    out = dot(taps_of(fw1, frames, group), w7[...])
    for t in range(frames):
        y[t] = out[t * spots : (t + 1) * spots]
    s[...] = entry_sums(out, w7.shape[1] - LANES, frames, spots)


def fast_last(m, n, frames, group, lo, at, st, ft, f1, cot, g, b, mk, out, pre, s, nz):
    count = mk[m.fast[0] : m.fast[0] + 1, :]
    mean, rstd = norm_rows(st, at, LANES, count)
    nz[0:1, :] = mean
    nz[1:2, :] = rstd
    gain = g[n : n + 1, lo : lo + LANES]
    bias = b[n : n + 1, lo : lo + LANES]
    mask = mk[m.main[0] : m.main[1], :]
    one = jnp.zeros((8, LANES), F32)
    two = jnp.zeros((8, LANES), F32)
    for t in range(frames):
        for f in range(group):
            k = t * group + f
            hat = (ft[t, :, f * LANES : (f + 1) * LANES].astype(F32) - mean) * rstd
            z = f1[k].astype(F32) + hat * gain + bias
            sigma = sigmoid(z)
            out[k] = z * sigma * mask
            grad = cot[k].astype(F32) * mask * (sigma * (1.0 + z * (1.0 - sigma)))
            pre[k] = grad.astype(BF16)
            one = one + sublane_sums(grad)
            two = two + sublane_sums(grad * hat)
    s[...] = jnp.concatenate([row_sum(one), row_sum(two)], axis=1)


def chunked(total, step, body, init):
    def turn(i, carry):
        return body(pl.multiple_of(i * step, step), carry)

    return lax.fori_loop(0, total // step, turn, init)


def slow_next(n, lo, span, third, xm, nz, g, b, mk, sw):
    spots, wide = third.shape
    mean = nz[0:1, :]
    scale = nz[1:2, :] * g[n : n + 1, lo : lo + wide]
    bias = b[n : n + 1, lo : lo + wide]

    def turn(at, carry):
        mask = widen(mk[pl.ds(span[0] + at, 16), :], 512)
        for c in range(0, wide, 512):
            z = third[pl.ds(at, 16), c : c + 512].astype(F32)
            z = (z - mean[:, c : c + 512]) * scale[:, c : c + 512] + bias[:, c : c + 512]
            z = xm[pl.ds(at, 16), c : c + 512].astype(F32) + z
            sw[pl.ds(at, 16), c : c + 512] = (silu(z) * mask).astype(BF16)
        return carry

    chunked(spots, 16, turn, 0)


def time_partial(frames, sw, wt, fpart):
    spots = sw.shape[1]
    out = dot(flat(sw[0:frames]), wt[0])
    for j in range(1, 3):
        out = out + dot(flat(sw[j : j + frames]), wt[j])
    for t in range(frames):
        fpart[t] = out[t * spots : (t + 1) * spots]


def slow_last(m, n, lo, third, slow, cot, nz, g, b, mk, out, pre, one, two):
    spots, wide = third.shape
    mean, rstd = nz[0:1, :], nz[1:2, :]
    gain = g[n : n + 1, lo : lo + wide]
    bias = b[n : n + 1, lo : lo + wide]

    def turn(at, sums):
        ones, twos = [], []
        mask = widen(mk[pl.ds(m.main[0] + at, 16), :], 512)
        for c in range(0, wide, 512):
            hat = third[pl.ds(at, 16), c : c + 512].astype(F32)
            hat = (hat - mean[:, c : c + 512]) * rstd[:, c : c + 512]
            z = slow[pl.ds(at, 16), c : c + 512].astype(F32) + hat * gain[:, c : c + 512] + bias[:, c : c + 512]
            sigma = sigmoid(z)
            out[pl.ds(at, 16), c : c + 512] = z * sigma * mask
            grad = cot[pl.ds(at, 16), c : c + 512].astype(F32) * mask
            grad = grad * (sigma * (1.0 + z * (1.0 - sigma)))
            pre[pl.ds(at, 16), c : c + 512] = grad.astype(BF16)
            ones.append(sublane_sums(grad))
            twos.append(sublane_sums(grad * hat))
        return sums[0] + jnp.concatenate(ones, axis=1), sums[1] + jnp.concatenate(twos, axis=1)

    one[...], two[...] = chunked(spots, 16, turn, (one[...], two[...]))


def slow_third_grad(m, n, lo, pre, third, n3, gb, g, mk, d3):
    spots, wide = pre.shape
    count = widen(mk[m.slow[0] : m.slow[0] + 1, :], wide)
    mean, rstd = n3[0:1, :], n3[1:2, :]
    scale = g[n : n + 1, lo : lo + wide] * rstd
    one = gb[0:1, :] / count
    two = gb[1:2, :] / count * rstd

    def turn(i, carry):
        mask = widen(mk[pl.ds(m.main[0] + i, 16), :], 512)
        for c in range(0, wide, 512):
            hat = (third[pl.ds(i, 16), c : c + 512].astype(F32) - mean[:, c : c + 512]) * two[:, c : c + 512]
            grad = pre[pl.ds(i, 16), c : c + 512].astype(F32) - mask * (one[:, c : c + 512] + hat)
            d3[pl.ds(i, 16), c : c + 512] = (scale[:, c : c + 512] * grad).astype(BF16)
        return carry

    chunked(spots, 16, turn, 0)


def slow_third_back(m, n, frames, lo, d3, z, n2, wp, g, b, mk, e2, s):
    spots, width = z.shape[1], z.shape[2]
    out = dot_nt(flat(d3[...]), wp[...])
    gain = g[n : n + 1, lo : lo + width]
    bias = b[n : n + 1, lo : lo + width]
    back_act(m, frames, spots, out, z, 0, n2[0:1, :], n2[1:2, :], gain, bias, mk, e2, s)


def back_act(m, frames, spots, out, z, col0, mean, rstd, gain, bias, mk, e, s):
    width = out.shape[1]
    mask = widen(mk[m.main[0] : m.main[1], :], width)
    one = jnp.zeros((8, width), F32)
    two = jnp.zeros((8, width), F32)
    for t in range(frames):
        hat = (z[t, :, col0 : col0 + width] - mean) * rstd
        grad = out[t * spots : (t + 1) * spots] * mask * silu_slope(hat * gain + bias)
        e[t] = grad
        one = one + sublane_sums(grad)
        two = two + sublane_sums(grad * hat)
    s[...] = jnp.concatenate([row_sum(one), row_sum(two)], axis=1)


def fast_third_back(m, n, frames, group, lo3, lo2, at, st, pre, ft, n3, z, n2, wp, g, b, mk, d3, e2, s, gb):
    spots = z.shape[1]
    count = mk[m.fast[0] : m.fast[0] + 1, :]
    one, two = totals(st, at, LANES)
    gb[0:1, :] = one
    gb[1:2, :] = two
    mean, rstd = n3[0:1, :], n3[1:2, :]
    scale = g[n : n + 1, lo3 : lo3 + LANES] * rstd
    one = one / count
    two = two / count * rstd
    mask = mk[m.main[0] : m.main[1], :]
    for t in range(frames):
        for f in range(group):
            hat = (ft[t, :, f * LANES : (f + 1) * LANES] - mean) * two
            grad = pre[t * group + f] - mask * (one + hat)
            d3[t, :, f * LANES : (f + 1) * LANES] = (scale * grad).astype(BF16)
    out = dot_nt(flat(d3[...]), wp[...])
    mean, rstd = n2[0:1, :], n2[1:2, :]
    gain = g[n : n + 1, lo2 : lo2 + LANES]
    bias = b[n : n + 1, lo2 : lo2 + LANES]
    back_act(m, frames, spots, out, z, 0, mean, rstd, gain, bias, mk, e2, s)


def space_back(
    m, n, frames, cols, lo2, lo1, at, width, col0, packed, span,
    st, e, erow, z, zrow, nz, z1, n1, w, g, b, mk, d2, e1, s, gb, vw,
):
    spots = z.shape[1]
    count = widen(mk[span[0] : span[0] + 1, :], width)
    one, two = totals(st, at, width, packed)
    gb[0:1, :] = one
    gb[1:2, :] = two
    mean, rstd = nz[0:1, :], nz[1:2, :]
    scale = g[n : n + 1, lo2 : lo2 + width] * rstd
    one = one / count
    two = two / count * rstd
    mask = widen(mk[m.ext[0] : m.ext[1], :], width)
    for t in range(frames):
        grad = jnp.concatenate([erow[t], e[t], erow[t]], axis=0)
        value = jnp.concatenate([zrow[t], z[t], zrow[t]], axis=0)
        grad = scale * mask * (grad - (one + (value - mean) * two))
        d2[t] = grad[cols : cols + spots].astype(BF16)
        store_shifts(vw, t, grad.astype(BF16).astype(F32), cols)
    total = None
    for i in range(3):
        rows = (2 - i) * cols
        for j in range(3):
            lane = (2 - j) * width
            part = dot_nt(flat(vw[:, rows : rows + spots, lane : lane + width]), w[i, j * width : (j + 1) * width, :])
            total = part if total is None else total + part
    mean, rstd = n1[0:1, :], n1[1:2, :]
    gain = g[n : n + 1, lo1 : lo1 + width]
    bias = b[n : n + 1, lo1 : lo1 + width]
    back_act(m, frames, spots, total, z1, col0, mean, rstd, gain, bias, mk, e1, s)


def first_taps(frames, dw):
    return [flat(dw[2 - j : 2 - j + frames]) for j in range(3)]


def time_back(taps, wt, lo, size):
    out = dot_nt(taps[0], wt[0, lo : lo + size, :])
    for j in range(1, 3):
        out = out + dot_nt(taps[j], wt[j, lo : lo + size, :])
    return out


def slow_first_back(m, n, frames, lo1, at, st, e, ep, en, z, zp, zn, n1, wt, y, nl, g, b, mk, dw, el, s, gb):
    spots, width = z.shape[1], z.shape[2]
    lat = nl.shape[1]
    wide = wt.shape[1] - lat
    count = widen(mk[m.slow[0] : m.slow[0] + 1, :], width)
    one, two = totals(st, at, width)
    gb[0:1, :] = one
    gb[1:2, :] = two
    mean, rstd = n1[0:1, :], n1[1:2, :]
    scale = g[n : n + 1, lo1 : lo1 + width] * rstd
    one = one / count
    two = two / count * rstd
    sources = (
        [(ep, zp, m.prev)] + [(e.at[t], z.at[t], m.main) for t in range(frames)] + [(en, zn, m.next)]
    )
    for k, (grad, value, span) in enumerate(sources):
        mask = widen(mk[span[0] : span[1], :], width)
        dw[k] = (scale * mask * (grad[...] - (one + (value[...] - mean) * two))).astype(BF16)
    out = time_back(first_taps(frames, dw), wt, wide, lat)
    back_act(
        m, frames, spots, out, y, 0, nl[0:1, :], nl[1:2, :], g[n : n + 1, 0:lat], b[n : n + 1, 0:lat], mk, el, s
    )


def slow_input_last(m, frames, dw, wt, pre, mk, gx):
    spots, wide = pre.shape[1], pre.shape[2]
    taps = first_taps(frames, dw)
    mask = widen(mk[m.main[0] : m.main[1], :], 256)
    for c in range(0, wide, 256):
        out = time_back(taps, wt, c, 256)
        for t in range(frames):
            gx[t, :, c : c + 256] = (out[t * spots : (t + 1) * spots] + pre[t, :, c : c + 256]) * mask


def slow_input_back(m, n, frames, lo, at, dw, wt, pre, xm, third, n3, g, b, mk, pre0, s):
    spots = pre.shape[1]
    wide = s.shape[1] // 2
    mask = widen(mk[m.main[0] : m.main[1], :], 256)
    out = time_back(first_taps(frames, dw), wt, 0, 256)
    mean, rstd = n3[0:1, at : at + 256], n3[1:2, at : at + 256]
    gain = g[n - 1 : n, lo + at : lo + at + 256]
    bias = b[n - 1 : n, lo + at : lo + at + 256]
    one = jnp.zeros((8, 256), F32)
    two = jnp.zeros((8, 256), F32)
    for t in range(frames):
        grad = (out[t * spots : (t + 1) * spots] + pre[t].astype(F32)) * mask
        hat = (third[t].astype(F32) - mean) * rstd
        z0 = xm[t].astype(F32) + hat * gain + bias
        grad = grad * silu_slope(z0)
        pre0[t] = grad.astype(BF16)
        one = one + sublane_sums(grad)
        two = two + sublane_sums(grad * hat)
    s[:, at : at + 256] = row_sum(one)
    s[:, wide + at : wide + at + 256] = row_sum(two)


def fast_first_back(
    m, n, frames, lo1, at1, atl, st1, stl, el, eln, ef, efp, efn, y, yp, yn, nl, n1, gs, g, mk,
    dl, dfw, dln, dfp, dfn, gbl, gb1,
):
    lat = nl.shape[1]
    count = widen(mk[m.slow[0] : m.slow[0] + 1, :], lat)
    one, two = totals(stl, atl, lat)
    gbl[0:1, :] = one
    gbl[1:2, :] = two
    mean, rstd = nl[0:1, :], nl[1:2, :]
    scale = gs[n : n + 1, 0:lat] * rstd
    one = one / count
    two = two / count * rstd

    def lat_grad(grad, value, span):
        mask = widen(mk[span[0] : span[1], :], lat)
        return (scale * mask * (grad - (one + (value - mean) * two))).astype(BF16)

    for t in range(frames):
        dl[t] = lat_grad(el[t], y[t, :, 0:lat], m.main)
    dln[...] = lat_grad(eln[...], yn[:, 0:lat], m.next)
    fcount = mk[m.fast[0] : m.fast[0] + 1, :]
    fone, ftwo = totals(st1, at1, LANES, True)
    gb1[0:1, :] = fone
    gb1[1:2, :] = ftwo
    fmean, frstd = n1[0:1, :], n1[1:2, :]
    fscale = g[n : n + 1, lo1 : lo1 + LANES] * frstd
    fone = fone / fcount
    ftwo = ftwo / fcount * frstd

    def first_grad(grad, value, span):
        mask = mk[span[0] : span[1], :]
        return (fscale * mask * (grad - (fone + (value - fmean) * ftwo))).astype(BF16)

    for t in range(frames):
        dfw[t] = first_grad(ef[t], y[t, :, lat:], m.main)
    dfp[...] = first_grad(efp[...], yp[:, lat:], m.prev)
    dfn[...] = first_grad(efn[...], yn[:, lat:], m.next)


def fast_input_back(m, n, frames, group, lo3, last, dl, dfw, dln, dfp, dfn, w7, pre, *rest):
    if last:
        mk, gx, buf = rest
    else:
        fw0, ft, n3, g, b, mk, pre0, s, buf = rest
    spots, lat = dl.shape[1], dl.shape[2]
    both = jnp.concatenate([flat(dl[...]), flat(dfw[...])], axis=1)
    buf[...] = jnp.zeros(buf.shape, F32)
    out = dot_nt(both, w7[...])
    for t in range(frames):
        for f in range(7):
            k = group * t + f
            buf[k] = buf[k] + out[t * spots : (t + 1) * spots, f * LANES : (f + 1) * LANES]
    buf[2] = buf[2] + dot_nt(dfp[...], w7[6 * LANES : 7 * LANES, lat:])
    after = dot_nt(jnp.concatenate([dln[...], dfn[...]], axis=1), w7[0 : 2 * LANES, :])
    total = frames * group
    for f in range(2):
        buf[total + f] = buf[total + f] + after[:, f * LANES : (f + 1) * LANES]
    mask = mk[m.main[0] : m.main[1], :]
    if last:
        for k in range(total):
            gx[k] = (pre[k] + buf[2 + k]) * mask
        return
    mean, rstd = n3[0:1, :], n3[1:2, :]
    gain = g[n - 1 : n, lo3 : lo3 + LANES]
    bias = b[n - 1 : n, lo3 : lo3 + LANES]
    one = jnp.zeros((8, LANES), F32)
    two = jnp.zeros((8, LANES), F32)
    for k in range(total):
        t, f = k // group, k % group
        hat = (ft[t, :, f * LANES : (f + 1) * LANES] - mean) * rstd
        z0 = fw0[2 + k].astype(F32) + hat * gain + bias
        grad = (pre[k] + buf[2 + k]) * mask * silu_slope(z0)
        pre0[k] = grad.astype(BF16)
        one = one + sublane_sums(grad)
        two = two + sublane_sums(grad * hat)
    s[...] = jnp.concatenate([row_sum(one), row_sum(two)], axis=1)


def point_weights(a2, d3, out):
    acts = flat(a2[...])
    for k in range(out.shape[0]):
        out[k] = dot_tn(acts, flat(d3[:, :, k * 256 : (k + 1) * 256])).astype(BF16)


def space_weights(cols, aw, d2, out, vw):
    frames, spots, width = d2.shape
    for t in range(frames):
        store_shifts(vw, t, aw[t].astype(F32), cols)
    grads = flat(d2[...])
    for i in range(3):
        out[i] = dot_tn(flat(vw[:, i * cols : i * cols + spots, :]), grads).astype(BF16)


def time_weights(skip, slow, jl, dw, out):
    frames, spots, width = jl.shape
    wide = slow.shape[2]
    grads = jnp.concatenate([flat(dw[2 - j : 2 - j + frames]) for j in range(3)], axis=1)
    for c in range(0, wide + jl.shape[2], 256):
        if c < wide:
            acts = flat(slow[skip : skip + frames, :, c : c + 256])
        else:
            acts = flat(jl[:, :, c - wide : c - wide + 256])
        got = dot_tn(acts, grads)
        for j in range(3):
            out[j, c : c + 256, :] = got[:, j * width : (j + 1) * width].astype(BF16)


def group_blocks(value, group):
    size = LANES // group
    rows = lax.broadcasted_iota(jnp.int32, (LANES, LANES), 0) >> (size.bit_length() - 1)
    lanes = lax.broadcasted_iota(jnp.int32, (LANES, LANES), 1) >> (size.bit_length() - 1)
    kept = jnp.where(rows == lanes, value, 0.0)
    kept = kept + pltpu.roll(kept, 64, 1)
    kept = kept + pltpu.roll(kept, 32, 1)
    total = kept[0:size]
    for k in range(1, group):
        total = total + kept[k * size : (k + 1) * size]
    return total


def at_lanes(blocks):
    lanes = lax.broadcasted_iota(jnp.int32, blocks[0].shape, 1) >> 5
    out = jnp.zeros(blocks[0].shape, F32)
    for k, block in enumerate(blocks):
        out = jnp.where(lanes == k, block, out)
    return out


def fast_weights(group, cols, lat, fw, dl, df, fa1, d2, fa2, d3, out, vw):
    frames, spots, _ = dl.shape
    size = LANES // group
    both = jnp.concatenate([flat(dl[...]), flat(df[...])], axis=1)
    taps = [[None] * group for _ in range(3)]
    for f in range(7):
        acts = jnp.concatenate([fw[group * t + f] for t in range(frames)], axis=0)
        got = dot_tn(acts, both)
        if f < 5:
            out[f * LANES : (f + 1) * LANES, :] = got[:, :lat].astype(BF16)
        for k in range(group):
            if 0 <= f - k - 1 < 3:
                taps[f - k - 1][k] = got[:, lat:]
    lanes = lax.broadcasted_iota(jnp.int32, (LANES, LANES), 1) >> (size.bit_length() - 1)
    tap_sums = []
    for j in range(3):
        kept = jnp.zeros((LANES, LANES), F32)
        for k in range(group):
            kept = jnp.where(lanes == k, taps[j][k], kept)
        kept = kept + pltpu.roll(kept, 64, 1)
        tap_sums.append(kept + pltpu.roll(kept, 32, 1))
    low = 5 * LANES
    out[low : low + LANES, 0:LANES] = at_lanes(tap_sums).T.astype(BF16)
    for t in range(frames):
        store_shifts(vw, t, fa1[t].astype(F32), cols)
    grads = flat(d2[...])
    for i in range(3):
        got = dot_tn(flat(vw[:, i * cols : i * cols + spots, :]), grads)
        blocks = [group_blocks(got[j * LANES : (j + 1) * LANES], group) for j in range(3)]
        out[low + size * i : low + size * (i + 1), LANES : 2 * LANES] = at_lanes(blocks).astype(BF16)
    acts = flat(fa2[...])
    total = jnp.zeros((size, LANES), F32)
    for k in range(group):
        got = dot_tn(acts, flat(d3[:, :, k * LANES : (k + 1) * LANES]))
        total = total + got[k * size : (k + 1) * size]
    out[low + 3 * size : low + 4 * size, LANES : 2 * LANES] = total.astype(BF16)


def unpack_fast(n, inner, load, outs):
    glat, gft, gfs, gfp = outs
    low = glat.shape[1]
    for at in range(0, low, inner):
        glat[n, at : at + inner, :] = load(at, inner)
    for i in range(4):
        got = load(low + inner * i, inner)
        if i < 3:
            gft[n, i] = got[:, 0:LANES]
            for j in range(3):
                moved = got[:, LANES:] if j == 0 else pltpu.roll(got[:, LANES:], LANES - inner * j, 1)
                gfs[n, 3 * i + j] = moved[:, 0:inner]
        else:
            gfp[n] = got[:, LANES:]


def rows_of(one, two=None):
    def load(at, count):
        ref = one
        size = one.shape[1]
        if two is not None:
            core, rest = at // (8 * size), at % (8 * size)
            if rest >= 4 * size:
                ref, rest = two, rest - 4 * size
            at = core * 4 * size + rest
        block, row = at // size, at % size
        assert row + count <= size
        return ref[block, row : row + count, :].astype(F32)

    return load


def copy_rows(start, one, out):
    for at in range(0, out.shape[0], 256):
        out[at : at + 256, :] = one[start + at : start + at + 256, :].astype(F32)


def copy_columns(start, one, out):
    for at in range(0, out.shape[1], 256):
        out[:, at : at + 256] = one[start + at : start + at + 256, :].astype(F32)


def place_rows(start, step, one, two, out):
    load = rows_of(one, two)
    for at in range(0, out.shape[0], step):
        out[at : at + step, :] = load(start + at, step)


def place_columns(start, one, two, out):
    load = rows_of(one, two)
    for at in range(0, out.shape[1], 256):
        out[:, at : at + 256] = load(start + at, 256)


def place_fast(inner, one_one, one_two, zero, *outs):
    unpack_fast(1, inner, rows_of(one_one, one_two), outs)
    unpack_fast(0, inner, rows_of(zero), outs)


def assemble_norms(inner, *refs):
    sums, (gs, bs, gf, bf) = refs[:-4], refs[-4:]
    lanes = lax.broadcasted_iota(jnp.int32, (8, LANES), 1) >> (inner.bit_length() - 1)
    for n in range(2):
        slow, fast = sums[7 * n : 7 * n + 4], sums[7 * n + 4 : 7 * n + 7]
        for row, gslow, gfast in ((1, gs, gf), (0, bs, bf)):
            at = 0
            for part in slow:
                gslow[n : n + 1, at : at + part.shape[1]] = part[row : row + 1, :]
                at += part.shape[1]
            one, two, three = [jnp.broadcast_to(part[row : row + 1, :], (8, LANES)) for part in fast]
            three = pltpu.roll(three, 2 * inner, 1)
            head = jnp.where(lanes == 0, one, jnp.where(lanes == 1, two, three))
            gfast[n : n + 1, 0:LANES] = head[0:1]
            gfast[n : n + 1, LANES : LANES + 2 * inner] = three[0:1, 0 : 2 * inner]


def on_device(
    x_slow,
    x_fast,
    w_lateral,
    w_slow_time,
    w_slow_space,
    w_slow_point,
    w_fast_time,
    w_fast_space,
    w_fast_point,
    gain_slow,
    bias_slow,
    gain_fast,
    bias_fast,
    clip_size,
    cot_slow,
    cot_fast,
):
    frames, fast_frames = x_slow.shape[0], x_fast.shape[0]
    group = fast_frames // frames
    rows, cols = x_slow.shape[3], x_slow.shape[4]
    spots = rows * cols
    wide, fwide = x_slow.shape[5], x_fast.shape[5]
    lat = w_lateral.shape[3]
    width = w_slow_space.shape[3]
    inner = w_fast_space.shape[3]
    packs = group * fwide
    both = lat + LANES
    m = Masks(spots, cols)
    devices = lax.axis_size("path") * lax.axis_size("rows")
    path = lax.axis_index("path")
    ext = spots + 2 * cols
    lo1, lo2, lo3 = lat, lat + width, lat + 2 * width
    every = slice(None)

    def part(fn, *static):
        return functools.partial(fn, *static)

    xs = x_slow.reshape(frames, spots, wide)
    xf = x_fast.reshape(fast_frames, spots, fwide)
    cs = cot_slow.reshape(frames, spots, wide)
    cf = cot_fast.reshape(fast_frames, spots, fwide)
    wft = jnp.swapaxes(w_fast_time, 2, 3)
    wfs_raw = w_fast_space.reshape(2, 9, inner, inner)
    wsp = w_slow_space.reshape(2, 3, 3 * width, width)

    def packed(value):
        return jnp.concatenate(
            [value[:, 0:inner]] * group + [value[:, inner : 2 * inner]] * group + [value[:, 2 * inner :]],
            axis=1,
        )

    xf_edge = swap_path(jnp.where(path > 0, xf[:2], xf[-2:]))
    xs_edge = swap_path(jnp.where(path > 0, xs[0], xs[-1]))

    def payload(k, *sums):
        size = sum(k.temps[s[1]].shape[1] for s in sums)
        out = k.give((devices, 1, size))
        k.step(spread_sums, *sums, out)
        return out

    def row_out(k, z, mk, col0, size):
        out = k.give((frames, cols, size))
        k.step(part(own_row, m, spots, cols, col0, size), z, mk, out)
        return out

    def edge_out(k, z, mk, size, tail=0):
        out = k.give((spots, size), BF16)
        k.step(part(own_edge, m, 0, tail), z, mk, out)
        return out

    def finish(k, **handles):
        got = k.run()
        return {name: got[handle[1]] for name, handle in handles.items()}

    def other_row(value):
        return swap(value, "rows", 1)

    first_flops = 2 * frames * spots * 7 * fwide * both
    k = Stage("entry")
    mk_out = k.give((m.rows, LANES))
    place = jnp.stack([lax.axis_index("rows"), path]).astype(jnp.int32)
    k.step(
        part(make_masks, m, rows, cols, lax.axis_size("path") - 1), k.scalar(place), k.scalar(clip_size), mk_out
    )
    w7_out = k.give((7 * fwide, both), BF16)
    k.step(part(make_w7, lat, group), k.take(w_lateral, 0), k.take(wft, 0), w7_out)
    fw = k.give((fast_frames + 4, spots, fwide), BF16)
    y = k.give((frames, spots, both))
    sy = k.temp((1, 2 * both))
    edge = k.take(xf_edge)
    k.step(
        part(fast_entry, m, frames, group), k.take(xf), edge, edge, mk_out, w7_out, fw, y, sy, flops=first_flops
    )
    pay = payload(k, sy)
    got = finish(
        k, mk=mk_out, w7=w7_out, fw=fw, y=y, pay=pay, ff_row=row_out(k, y, mk_out, lat, LANES),
        edge=edge_out(k, y, mk_out, both),
    )
    mk = got["mk"]
    saved = [{"fw": got["fw"], "y": got["y"], "w7": got["w7"]}, {}]
    st = gather_sums(got["pay"])
    saved[0]["ff_row"] = other_row(got["ff_row"])
    saved[0]["y_edge"] = swap_path(got["edge"])
    mk, wft, gain_fast, bias_fast = lax.optimization_barrier((mk, wft, gain_fast, bias_fast))
    gf, bf = packed(gain_fast), packed(bias_fast)
    k = Stage("prepare")
    w7_out = k.give((7 * fwide, both), BF16)
    k.step(part(make_w7, lat, group), k.take(w_lateral, 1), k.take(wft, 1), w7_out)
    blocks = []
    for n in range(2):
        blocks += [k.give((3, 3 * LANES, LANES), BF16), k.give((LANES, packs), BF16)]
        k.step(part(make_blocks, group), k.take(wfs_raw, n), k.take(w_fast_point, n), *blocks[-2:])
    got = finish(k, w7=w7_out, wfs0=blocks[0], wfp0=blocks[1], wfs1=blocks[2], wfp1=blocks[3])
    saved[1]["w7"] = got["w7"]
    wfs, wfp = [got["wfs0"], got["wfs1"]], [got["wfp0"], got["wfp1"]]
    k = Stage("slow_partial")
    xm = k.give((frames + 2, spots, wide), BF16)
    fpart = k.give((frames, spots, width))
    edge = k.take(xs_edge)
    k.step(
        part(slow_partial, m, frames),
        k.take(xs), edge, edge, k.take(mk), k.take(w_slow_time, 0, every, slice(0, wide)), xm, fpart,
        flops=2 * frames * spots * 3 * wide * width,
    )
    got = finish(k, sw=xm, fpart=fpart)
    saved[0]["sw"] = got["sw"]
    fpart_in = got["fpart"]

    for n in range(2):
        v = saved[n]
        k = Stage("join")
        mk_in, gs, bs = k.take(mk), k.take(gain_slow), k.take(bias_slow)
        st_in = k.take(st)
        names = {}
        if n == 0:
            fpart = k.take(fpart_in)
        else:
            fpart = k.temp((frames, spots, width))
            n3, next_sw = k.give((2, wide)), k.give((frames + 2, spots, wide), BF16)
            names.update(sw=next_sw, n3=n3)
            k.step(part(keep_norm, 2 * both, wide, m.slow), st_in, mk_in, n3)
            spans = [m.prev] + [m.main] * frames + [m.next]
            for f in range(frames + 2):
                k.step(
                    part(slow_next, 0, lo3, spans[f]),
                    k.take(saved[0]["third"], f), k.take(saved[0]["sw"], f), k.peek(n3), gs, bs, mk_in,
                    k.piece(next_sw, f),
                )
            k.step(
                part(time_partial, frames),
                k.peek(next_sw), k.take(w_slow_time, 1, every, slice(0, wide)), fpart,
                flops=2 * frames * spots * 3 * wide * width,
            )
        y_in, edge = k.take(v["y"]), k.take(v["y_edge"])
        jl = k.give((frames, spots, lat), BF16)
        first = k.give((frames, spots, width))
        nl = k.give((2, lat))
        s_first, s_fs = k.temp((1, 2 * width)), k.temp((1, 2 * LANES))
        k.step(
            part(lat_join, m, n, frames, lat),
            st_in, y_in, edge, edge, fpart, k.take(w_slow_time, n, every, slice(wide, wide + lat)), gs, bs, mk_in,
            jl, first, s_first, nl, k.temp((frames + 2, spots, lat), BF16),
            flops=2 * frames * spots * 3 * lat * width,
        )
        fa1 = k.give((frames, ext, LANES), BF16)
        fs = k.give((frames, spots, LANES))
        nf1 = k.give((2, LANES))
        k.step(
            part(space_forward, m, n, frames, cols, 0, 2 * lat, LANES, lat, True, m.fast),
            st_in, y_in, k.take(v["ff_row"]), k.take(wfs[n]), k.take(gf), k.take(bf), mk_in,
            fa1, fs, s_fs, nf1, k.temp((frames, ext, 3 * LANES), BF16),
            flops=2 * frames * spots * 9 * LANES * LANES,
        )
        pay = payload(k, s_first, s_fs)
        got = finish(
            k, jl=jl, first=first, nl=nl, fa1=fa1, fs=fs, nf1=nf1, pay=pay,
            first_row=row_out(k, first, mk_in, 0, width), fs_row=row_out(k, fs, mk_in, 0, LANES),
            first_edge=edge_out(k, first, mk_in, width), **names,
        )
        st = gather_sums(got["pay"])
        for name in ("jl", "first", "nl", "fa1", "fs", "nf1"):
            v[name] = got[name]
        if n == 1:
            saved[1]["sw"], saved[0]["n3"] = got["sw"], got["n3"]
        first_row = other_row(got["first_row"])
        v["fs_row"] = other_row(got["fs_row"])
        v["first_edge"] = swap_path(got["first_edge"])
        k = Stage("space")
        mk_in, st_in = k.take(mk), k.take(st)
        a1 = k.give((frames, ext, width), BF16)
        second = k.give((frames, spots, width))
        n1 = k.give((2, width))
        s_second, s_ft = k.temp((1, 2 * width)), k.temp((1, 2 * LANES))
        k.step(
            part(space_forward, m, n, frames, cols, lo1, 0, width, 0, False, m.slow),
            st_in, k.take(v["first"]), k.take(first_row), k.take(wsp, n), k.take(gain_slow), k.take(bias_slow), mk_in,
            a1, second, s_second, n1, k.temp((frames, ext, 3 * width), BF16),
            flops=2 * frames * spots * 9 * width * width,
        )
        fa2 = k.give((frames, spots, LANES), BF16)
        ft = k.give((frames, spots, packs), BF16)
        nf2 = k.give((2, LANES))
        k.step(
            part(fast_third, m, n, frames, LANES, 2 * width),
            st_in, k.take(v["fs"]), k.take(wfp[n]), k.take(gf), k.take(bf), mk_in, fa2, ft, s_ft, nf2,
            flops=2 * frames * spots * LANES * packs,
        )
        pay = payload(k, s_second, s_ft)
        names = {"second_row": row_out(k, second, mk_in, 0, width)}
        if n == 0:
            names["second_edge"] = edge_out(k, second, mk_in, width)
            names["ft_edge"] = edge_out(k, ft, mk_in, 2 * fwide, (group - 2) * fwide)
        got = finish(k, a1=a1, second=second, n1=n1, fa2=fa2, ft=ft, nf2=nf2, pay=pay, **names)
        st = gather_sums(got["pay"])
        for name in ("a1", "second", "n1", "fa2", "ft", "nf2"):
            v[name] = got[name]
        v["second_row"] = other_row(got["second_row"])
        halo = 1 - n
        edges = []
        k = Stage("third")
        if n == 0:
            ft_edge = k.take(swap_path(got["ft_edge"]))
            edges = [k.take(swap_path(got["second_edge"]))] * 2
        mk_in, st_in = k.take(mk), k.take(st)
        a2 = k.give((frames, spots, width), BF16)
        third = k.give((frames + 2 * halo, spots, wide), BF16)
        n2 = k.give((2, width))
        nf3 = k.give((2, LANES))
        s_third = k.temp((1, 2 * wide))
        names = {}
        if n == 0:
            names.update(
                fw=k.give((fast_frames + 4, spots, fwide), BF16),
                y=k.give((frames, spots, both)),
            )
            s_fast = k.temp((1, 2 * both))
            k.step(
                part(fast_next, m, n, frames, group, 2 * LANES, 2 * width),
                st_in, k.take(v["ft"]), ft_edge, ft_edge, k.take(v["fw"]), k.take(saved[1]["w7"]),
                k.take(gf), k.take(bf), mk_in, names["fw"], names["y"], s_fast, nf3,
                flops=first_flops,
            )
        else:
            names.update(out_fast=k.give((fast_frames, spots, fwide)), pre_f=k.give((fast_frames, spots, fwide), BF16))
            s_fast = k.temp((1, 2 * LANES))
            k.step(
                part(fast_last, m, n, frames, group, 2 * LANES, 2 * width),
                st_in, k.take(v["ft"]), k.take(v["fw"], slice(2, 2 + fast_frames)), k.take(cf), k.take(gf), k.take(bf), mk_in,
                names["out_fast"], names["pre_f"], s_fast, nf3,
            )
        aw = k.temp((frames + 2 * halo, spots, width), BF16)
        k.step(
            part(slow_acts, m, n, frames, lo2, halo),
            st_in, k.take(v["second"]), *edges, k.take(gain_slow), k.take(bias_slow), mk_in, a2, n2, aw,
        )
        for at in range(0, wide, 256):
            lanes = slice(at, at + 256)
            k.step(
                part(slow_third, frames, halo, at),
                aw, k.take(w_slow_point, n, every, lanes), k.piece(third, every, every, lanes), s_third,
                flops=2 * frames * spots * width * 256,
            )
        if n == 0:
            pay = payload(k, s_fast, s_third)
            names["ff_row"] = row_out(k, names["y"], mk_in, lat, LANES)
            names["y_edge"] = edge_out(k, names["y"], mk_in, both)
        else:
            pay = payload(k, s_third, s_fast)
        got = finish(k, a2=a2, third=third, n2=n2, nf3=nf3, pay=pay, **names)
        st = gather_sums(got["pay"])
        for name in ("a2", "third", "n2", "nf3"):
            v[name] = got[name]
        if n == 0:
            saved[1].update(
                fw=got["fw"], y=got["y"], ff_row=other_row(got["ff_row"]), y_edge=swap_path(got["y_edge"])
            )
        else:
            out_fast, pre_f = got["out_fast"], got["pre_f"]

    def third_back(k, n, at, st_in, mk_in, pre):
        v = saved[n]
        d3, e2 = k.give((frames, spots, wide), BF16), k.give((frames, spots, width))
        s, gb = k.temp((1, 2 * width)), k.give((2, wide))
        gs = k.take(gain_slow)
        k.step(part(keep_sums, at, wide), st_in, gb)
        for t in range(frames):
            k.step(
                part(slow_third_grad, m, n, lo3),
                k.take(pre, t), k.take(v["third"], t + 1 - n), k.take(v["n3"]), k.peek(gb), gs, mk_in,
                k.piece(d3, t),
            )
        k.step(
            part(slow_third_back, m, n, frames, lo2),
            k.peek(d3), k.take(v["second"]), k.take(v["n2"]), k.take(w_slow_point, n), gs, k.take(bias_slow), mk_in,
            e2, s, flops=2 * frames * spots * width * wide,
        )
        return dict(d3=d3, e2=e2, gb3=gb), s

    def fast_back3(k, n, at, st_in, mk_in, pre):
        v = saved[n]
        d3, e2 = k.give((frames, spots, packs), BF16), k.give((frames, spots, LANES))
        s, gb = k.temp((1, 2 * LANES)), k.give((2, LANES))
        k.step(
            part(fast_third_back, m, n, frames, group, 2 * LANES, LANES, at),
            st_in, k.take(pre), k.take(v["ft"]), k.take(v["nf3"]), k.take(v["fs"]), k.take(v["nf2"]),
            k.take(wfp[n]), k.take(gf), k.take(bf), mk_in, d3, e2, s, gb,
            flops=2 * frames * spots * LANES * packs,
        )
        return dict(d3f=d3, ef2=e2, gbf3=gb), s

    def second_back(k, n, at, st_in, mk_in, e2, e2_row):
        v = saved[n]
        d2, e1 = k.give((frames, spots, width), BF16), k.give((frames, spots, width))
        s, gb = k.temp((1, 2 * width)), k.give((2, width))
        k.step(
            part(space_back, m, n, frames, cols, lo2, lo1, at, width, 0, False, m.slow),
            st_in, k.take(e2), k.take(e2_row), k.take(v["second"]), k.take(v["second_row"]), k.take(v["n2"]),
            k.take(v["first"]), k.take(v["n1"]), k.take(wsp, n), k.take(gain_slow), k.take(bias_slow), mk_in,
            d2, e1, s, gb, k.temp((frames, ext, 3 * width), BF16),
            flops=2 * frames * spots * 9 * width * width,
        )
        return dict(d2=d2, e1=e1, gb2=gb), s

    def fast_back2(k, n, at, st_in, mk_in, ef2, ef2_row):
        v = saved[n]
        d2, e1 = k.give((frames, spots, LANES), BF16), k.give((frames, spots, LANES))
        s, gb = k.temp((1, 2 * LANES)), k.give((2, LANES))
        k.step(
            part(space_back, m, n, frames, cols, LANES, 0, at, LANES, lat, True, m.fast),
            st_in, k.take(ef2), k.take(ef2_row), k.take(v["fs"]), k.take(v["fs_row"]), k.take(v["nf2"]),
            k.take(v["y"]), k.take(v["nf1"]), k.take(wfs[n]), k.take(gf), k.take(bf), mk_in,
            d2, e1, s, gb, k.temp((frames, ext, 3 * LANES), BF16),
            flops=2 * frames * spots * 9 * LANES * LANES,
        )
        return dict(d2f=d2, ef1=e1, gbf2=gb), s

    def first_back(k, n, st_in, mk_in, e1, e1_edge):
        v = saved[n]
        dw, el = k.give((frames + 2, spots, width), BF16), k.give((frames, spots, lat))
        s, gb = k.temp((1, 2 * lat)), k.give((2, width))
        edge, zedge = k.take(e1_edge), k.take(v["first_edge"])
        k.step(
            part(slow_first_back, m, n, frames, lo1, 0),
            st_in, k.take(e1), edge, edge, k.take(v["first"]), zedge, zedge, k.take(v["n1"]),
            k.take(w_slow_time, n, every, slice(wide, wide + lat)), k.take(v["y"]), k.take(v["nl"]),
            k.take(gain_slow), k.take(bias_slow), mk_in, dw, el, s, gb, flops=2 * frames * spots * 3 * lat * width,
        )
        return dict(dw=dw, el=el, gb1=gb), s

    def fast_back1(k, n, st1, at1, stl, atl, mk_in, el, el_edge, ef1, ef1_edge):
        v = saved[n]
        dl, df = k.give((frames, spots, lat), BF16), k.give((frames, spots, LANES), BF16)
        beside = [k.give((spots, lat), BF16), k.give((spots, LANES), BF16), k.give((spots, LANES), BF16)]
        gbl, gb1 = k.give((2, lat)), k.give((2, LANES))
        edge, yedge = k.take(ef1_edge), k.take(v["y_edge"])
        k.step(
            part(fast_first_back, m, n, frames, 0, at1, atl),
            st1, stl, k.take(el), k.take(el_edge), k.take(ef1), edge, edge, k.take(v["y"]), yedge, yedge,
            k.take(v["nl"]), k.take(v["nf1"]), k.take(gain_slow), k.take(gf), mk_in, dl, df, *beside, gbl, gb1,
        )
        return dict(dl=dl, df=df, dln=beside[0], dfp=beside[1], dfn=beside[2], gbl=gbl, gbf1=gb1)

    def weights_point(n, d3):
        k = Stage("point_weights")
        out = k.give((wide // 256, width, 256), BF16)
        k.step(point_weights, k.take(saved[n]["a2"]), k.take(d3), out, flops=2 * frames * spots * width * wide)
        return k.run()[0].reshape(-1, 256)

    def weights_space(n, d2):
        k = Stage("space_weights")
        out = k.give((3, 3 * width, width), BF16)
        k.step(
            part(space_weights, cols), k.take(saved[n]["a1"]), k.take(d2), out,
            k.temp((frames, ext, 3 * width), BF16), flops=2 * frames * spots * 9 * width * width,
        )
        return k.run()[0].reshape(-1, 256)

    def weights_time(n, dw):
        k = Stage("time_weights")
        out = k.give((3, wide + lat, width), BF16)
        k.step(
            part(time_weights, 1), k.take(saved[n]["sw"]), k.take(saved[n]["jl"]), k.take(dw), out,
            flops=2 * frames * spots * 3 * (wide + lat) * width,
        )
        return k.run()[0].reshape(-1, 256)

    def weights_fast(n, dl, df, d2, d3):
        v = saved[n]
        k = Stage("fast_weights")
        out = k.give((7 * LANES - LANES, 2 * LANES), BF16)
        k.step(
            part(fast_weights, group, cols, lat),
            k.take(v["fw"]), k.take(dl), k.take(df), k.take(v["fa1"]), k.take(d2), k.take(v["fa2"]), k.take(d3),
            out, k.temp((frames, ext, 3 * LANES), BF16), flops=first_flops,
        )
        return k.run()[0]

    b1, b0 = {}, {}
    k = Stage("last")
    mk_in, st_in = k.take(mk), k.take(st)
    out_slow, pre = k.give((frames, spots, wide)), k.give((frames, spots, wide), BF16)
    n3 = k.give((2, wide))
    s_pre, one, two = k.temp((1, 2 * wide)), k.temp((8, wide)), k.temp((8, wide))
    k.step(part(keep_norm, 0, wide, m.slow), st_in, mk_in, n3)
    k.step(clear, one, two)
    for t in range(frames):
        k.step(
            part(slow_last, m, 1, lo3),
            k.take(saved[1]["third"], t), k.take(saved[1]["sw"], t + 1), k.take(cs, t), k.peek(n3),
            k.take(gain_slow), k.take(bias_slow), mk_in, k.piece(out_slow, t), k.piece(pre, t), one, two,
        )
    k.step(close_sums, one, two, s_pre)
    names, s_ef2 = fast_back3(k, 1, 2 * wide, st_in, mk_in, pre_f)
    pay = payload(k, s_pre, s_ef2)
    ef2_row = row_out(k, names["ef2"], mk_in, 0, LANES)
    b1 = finish(k, out_slow=out_slow, pre=pre, n3=n3, pay=pay, ef2_row=ef2_row, **names)
    saved[1]["n3"] = b1["n3"]
    out_slow = b1["out_slow"]
    st = gather_sums(b1["pay"])

    k = Stage("back_third")
    ef2_row = other_row(b1["ef2_row"])
    mk_in, st_in = k.take(mk), k.take(st)
    names, s_e2 = third_back(k, 1, 0, st_in, mk_in, b1["pre"])
    more, s_ef1 = fast_back2(k, 1, 2 * wide, st_in, mk_in, b1["ef2"], ef2_row)
    pay = payload(k, s_e2, s_ef1)
    e2_row, ef1_edge = row_out(k, names["e2"], mk_in, 0, width), edge_out(k, more["ef1"], mk_in, LANES)
    b1.update(finish(k, pay=pay, e2_row=e2_row, ef1_edge=ef1_edge, **names, **more))
    st = st_ef1 = gather_sums(b1["pay"])
    e2_row, ef1_edge = other_row(b1["e2_row"]), swap_path(b1["ef1_edge"])
    point1 = weights_point(1, b1["d3"])

    k = Stage("back_space")
    mk_in, st_in = k.take(mk), k.take(st)
    names, s_e1 = second_back(k, 1, 0, st_in, mk_in, b1["e2"], e2_row)
    pay = payload(k, s_e1)
    e1_edge = edge_out(k, names["e1"], mk_in, width)
    b1.update(finish(k, pay=pay, e1_edge=e1_edge, **names))
    st = gather_sums(b1["pay"])
    e1_edge = swap_path(b1["e1_edge"])
    space1 = weights_space(1, b1["d2"])

    k = Stage("back_first")
    mk_in, st_in = k.take(mk), k.take(st)
    names, s_el = first_back(k, 1, st_in, mk_in, b1["e1"], e1_edge)
    names["down"], s_down = k.give((frames, spots, wide), BF16), k.temp((1, 2 * wide))
    for at in range(0, wide, 256):
        lanes = slice(at, at + 256)
        k.step(
            part(slow_input_back, m, 1, frames, lo3, at),
            k.peek(names["dw"]), k.take(w_slow_time, 1, every, lanes), k.take(b1["pre"], every, every, lanes),
            k.take(saved[0]["sw"], slice(1, 1 + frames), every, lanes),
            k.take(saved[0]["third"], slice(1, 1 + frames), every, lanes),
            k.take(saved[0]["n3"]), k.take(gain_slow), k.take(bias_slow), mk_in,
            k.piece(names["down"], every, every, lanes), s_down,
            flops=2 * frames * spots * 3 * 256 * width,
        )
    pay = payload(k, s_el, s_down)
    el_edge = edge_out(k, names["el"], mk_in, lat)
    b1.update(finish(k, pay=pay, el_edge=el_edge, **names))
    st = gather_sums(b1["pay"])
    el_edge = swap_path(b1["el_edge"])
    time1 = weights_time(1, b1["dw"])
    sizes1 = [point1.shape[0], space1.shape[0], time1.shape[0]]
    ones = jnp.concatenate([point1, space1, time1], axis=0)
    ones = lax.psum(ones, AXES)

    GRADS = ("dw", "dl", "df", "dln", "dfp", "dfn")
    SUMS = ("gbl", "gb1", "gb2", "gb3", "gbf1", "gbf2", "gbf3")
    steps = exchange_steps()
    core, across, down = steps[:3]
    seen = {}

    def block_zero(st=st, el_edge=el_edge, ef1_edge=ef1_edge, b1=b1, b0=b0):
        b1, b0 = dict(b1), dict(b0)
        k = Stage("back_third")
        mk_in, st_in = k.take(mk), k.take(st)
        names, s_e2 = third_back(k, 0, 2 * lat, st_in, mk_in, b1["down"])
        more = fast_back1(
            k, 1, k.take(st_ef1), 2 * width, st_in, 0, mk_in, b1["el"], el_edge, b1["ef1"], ef1_edge
        )
        inner_grads = [more[name] for name in ("dl", "df", "dln", "dfp", "dfn")]
        more["downf"], s_pf = k.give((fast_frames, spots, fwide), BF16), k.temp((1, 2 * LANES))
        k.step(
            part(fast_input_back, m, 1, frames, group, 2 * LANES, False),
            *inner_grads, k.take(saved[1]["w7"]), k.take(pre_f), k.take(saved[0]["fw"]), k.take(saved[0]["ft"]),
            k.take(saved[0]["nf3"]), k.take(gf), k.take(bf), mk_in, more["downf"], s_pf,
            k.temp((fast_frames + 4, spots, fwide)), flops=first_flops,
        )
        pay = payload(k, s_e2, s_pf)
        e2_row = row_out(k, names["e2"], mk_in, 0, width)
        got = finish(k, pay=pay, e2_row=e2_row, **names, **more)
        for name in more:
            b1[name] = got[name]
        b0.update({name: got[name] for name in names})
        st = gather_sums(got["pay"])
        e2_row = other_row(got["e2_row"])
        point0 = weights_point(0, b0["d3"])
        fast_1 = weights_fast(1, b1["dl"], b1["df"], b1["d2f"], b1["d3f"])

        k = Stage("back_space")
        mk_in, st_in = k.take(mk), k.take(st)
        names, s_e1 = second_back(k, 0, 0, st_in, mk_in, b0["e2"], e2_row)
        more, s_ef2 = fast_back3(k, 0, 2 * width, st_in, mk_in, b1["downf"])
        pay = payload(k, s_e1, s_ef2)
        e1_edge, ef2_row = edge_out(k, names["e1"], mk_in, width), row_out(k, more["ef2"], mk_in, 0, LANES)
        b0.update(finish(k, pay=pay, e1_edge=e1_edge, ef2_row=ef2_row, **names, **more))
        st = gather_sums(b0["pay"])
        e1_edge, ef2_row = swap_path(b0["e1_edge"]), other_row(b0["ef2_row"])
        space0 = weights_space(0, b0["d2"])
        mid = halve(jnp.concatenate([fast_1, point0, space0], axis=0), *core)
        st, mid = lax.optimization_barrier((st, mid))
        mid = halve_both(*parted(mid), across, down)

        k = Stage("back_first")
        mk_in, st_in = k.take(mk), k.take(st)
        names, s_el = first_back(k, 0, st_in, mk_in, b0["e1"], e1_edge)
        more, s_ef1 = fast_back2(k, 0, 2 * width, st_in, mk_in, b0["ef2"], ef2_row)
        pay = payload(k, s_el, s_ef1)
        el_edge, ef1_edge = edge_out(k, names["el"], mk_in, lat), edge_out(k, more["ef1"], mk_in, LANES)
        b0.update(finish(k, pay=pay, el_edge=el_edge, ef1_edge=ef1_edge, **names, **more))
        st = gather_sums(b0["pay"])
        el_edge, ef1_edge = swap_path(b0["el_edge"]), swap_path(b0["ef1_edge"])
        time0 = weights_time(0, b0["dw"])
        late = halve(time0, *core)
        st, mid, late = lax.optimization_barrier((st, mid, late))
        late = halve_both(*parted(late), across, down)
        mid = halve_both(*mid, down, across)

        k = Stage("back_fast")
        mk_in, st_in = k.take(mk), k.take(st)
        more = fast_back1(k, 0, st_in, 2 * lat, st_in, 0, mk_in, b0["el"], el_edge, b0["ef1"], ef1_edge)
        v = saved[0]
        rest = k.give((6 * LANES, 2 * LANES), BF16)
        k.step(
            part(fast_weights, group, cols, lat),
            k.take(v["fw"]), more["dl"], more["df"], k.take(v["fa1"]), k.take(b0["d2f"]), k.take(v["fa2"]),
            k.take(b0["d3f"]), rest, k.temp((frames, ext, 3 * LANES), BF16), flops=first_flops,
        )
        got = finish(k, rest=rest, **more)
        b0.update(got)
        rest, mid, late = lax.optimization_barrier((got["rest"], mid, late))
        rest = halve(rest, *core)
        mid = jnp.concatenate(mid, axis=0)
        seen["fast"], seen["point"] = fast_1.shape[0], point0.shape[0]
        sums = [b0[name] for name in SUMS] + [b1[name] for name in ("gbl", "gbf1")]
        grads = [b0[name] for name in GRADS] + [b1["down"], b1["downf"]]
        return (mid, *late, rest, *grads, *sums)

    like = jax.eval_shape(block_zero)
    got = lax.cond(
        clip_size[0, 0] > 0, block_zero, lambda: tuple(jnp.zeros(o.shape, o.dtype) for o in like)
    )
    mid, late, rest = got[0], got[1:3], got[3]
    b0 = dict(zip(GRADS + ("down", "downf") + SUMS, got[4:19]))
    b1["gbl"], b1["gbf1"] = got[19:21]

    k = Stage("slow_input")
    gx_slow = k.give((frames, spots, wide))
    k.step(
        part(slow_input_last, m, frames),
        k.take(b0["dw"]), k.take(w_slow_time, 0, every, slice(0, wide)), k.take(b0["down"]), k.take(mk), gx_slow,
        flops=2 * frames * spots * 3 * wide * width,
    )
    (gx_slow,) = k.run()
    k = Stage("fast_input")
    gx_fast = k.give((fast_frames, spots, fwide))
    k.step(
        part(fast_input_back, m, 0, frames, group, 2 * LANES, True),
        *[k.take(b0[name]) for name in GRADS[1:]], k.take(saved[0]["w7"]), k.take(b0["downf"]), k.take(mk), gx_fast,
        k.temp((fast_frames + 4, spots, fwide)), flops=first_flops,
    )
    (gx_fast,) = k.run()
    time_rows, space_rows = 3 * (wide + lat), 9 * width
    k = Stage("assemble_one")
    ones_in = k.take(ones)
    gtime, gspace = k.give((2, time_rows, width), F32, 1), k.give((2, space_rows, width), F32, 1)
    gpoint = k.give((2, width, wide), F32, 1)
    k.step(part(copy_rows, sizes1[0] + sizes1[1]), ones_in, gtime)
    k.step(part(copy_rows, sizes1[0]), ones_in, gspace)
    k.step(part(copy_columns, 0), ones_in, gpoint)
    half_done = k.run()

    def spread_both(one, two, tied=()):
        one, two = [one, swap(one, *down)], [two, swap(two, *across)]
        one, two, tied = lax.optimization_barrier((one, two, tied))
        one, two = [jnp.stack(pair) for pair in (one, two)]
        one, two = [one, swap(one, *across)], [two, swap(two, *down)]
        return [pair + [swap(half, *core) for half in pair] for pair in (one, two)], tied

    for step in steps[3:]:
        mid = halve(mid, *step)
    mid = mid.astype(BF16)
    for step in reversed(steps[3:]):
        mid = double(mid, *step)
    (mid_one, mid_two), _ = spread_both(*parted(mid))
    late = halve_both(*late, down, across)
    rest = halve(halve(rest, *across), *down)
    parts = [late[0].shape[0], rest.shape[0], late[1].shape[0]]
    value = jnp.concatenate([late[0], rest, late[1]], axis=0)
    for step in steps[3:4]:
        value, gx_slow = lax.optimization_barrier((halve(value, *step), gx_slow))
    for step in steps[4:]:
        value, gx_fast = lax.optimization_barrier((halve(value, *step), gx_fast))
    value = value.astype(BF16)
    for step in reversed(steps[3:]):
        value = double(value, *step)
    cut = parts[0] + parts[1]
    (one, two), half_done = spread_both(value[:cut], value[cut:], half_done)

    core_bit = lax.axis_index("rows") % 2
    down_bit = (lax.axis_index("rows") // 2) % 2

    k = Stage("assemble")
    flip_one = k.scalar((core_bit * 4 + path * 2 + down_bit).astype(jnp.int32).reshape(1))
    flip_two = k.scalar((core_bit * 4 + down_bit * 2 + path).astype(jnp.int32).reshape(1))
    mid_one, mid_two = k.take_blocks(mid_one, flip_one, every), k.take_blocks(mid_two, flip_two, every)
    start = seen["fast"]
    gspace = k.give((2, space_rows, width), F32, 0, half_done[1])
    k.step(part(place_rows, start + seen["point"], 256), mid_one, mid_two, gspace)
    gpoint = k.give((2, width, wide), F32, 0, half_done[2])
    k.step(part(place_columns, start), mid_one, mid_two, gpoint)
    late_one = k.take_blocks(one, flip_one, slice(0, parts[0]))
    late_two = k.take_blocks(two, flip_two, every)
    gtime = k.give((2, time_rows, width), F32, 0, half_done[0])
    k.step(part(place_rows, 0, 80), late_one, late_two, gtime)
    rest = k.take_blocks(one, flip_one, slice(parts[0], cut))
    fast_outs = [
        k.give((2, 5 * fwide, lat)), k.give((2, 3, inner, fwide)), k.give((2, 9, inner, inner)),
        k.give((2, inner, fwide)),
    ]
    k.step(part(place_fast, inner), mid_one, mid_two, rest, *fast_outs)
    sums = [k.take(b[name]) for b in (b0, b1) for name in ("gbl", "gb1", "gb2", "gb3", "gbf1", "gbf2", "gbf3")]
    norm_outs = [k.give(like.shape) for like in (gain_slow, bias_slow, gain_fast, bias_fast)]
    k.step(part(assemble_norms, inner), *sums, *norm_outs)
    got = k.run()
    glat, gft, gfs, gfp = [got[h[1]] for h in fast_outs]

    return (
        out_slow.reshape(x_slow.shape),
        out_fast.reshape(x_fast.shape),
        gx_slow.reshape(x_slow.shape),
        gx_fast.reshape(x_fast.shape),
        glat.reshape(w_lateral.shape),
        got[gtime[1]].reshape(w_slow_time.shape),
        got[gspace[1]].reshape(w_slow_space.shape),
        got[gpoint[1]],
        jnp.swapaxes(gft, 2, 3),
        gfs.reshape(w_fast_space.shape),
        gfp,
        *[got[h[1]] for h in norm_outs],
    )


def solution(mesh):
    spread = P("path", None, "rows", None, None, None)
    return jax.shard_map(
        on_device,
        mesh=mesh,
        in_specs=(spread, spread) + (P(),) * 12 + (spread, spread),
        out_specs=(spread,) * 4 + (P(),) * 11,
        check_vma=False,
    )
```

```python
import functools

import jax
import jax.numpy as jnp
import numpy as np
from jax import lax
from jax.experimental import pallas as pl
from jax.experimental.pallas import tpu as pltpu
from jax.sharding import PartitionSpec as P

TS = 8
TF = 32
F32 = jnp.float32
BF16 = jnp.bfloat16
EPSILON = 1e-05
LANES = 128
AXES = ("path", "rows")
VMEM_LIMIT = 56 * 2**20


def swap(value, axis, stride):
    pairs = [(source, source ^ stride) for source in range(lax.axis_size(axis))]
    return lax.ppermute(value, axis, pairs)


def gather_sums(spread):
    return lax.all_to_all(spread, AXES, 0, 0, tiled=True)


def swap_path(value):
    assert lax.axis_size("path") == 2
    return lax.ppermute(value, "path", [(0, 1), (1, 0)])


def exchange_steps():
    steps = [("rows", 1), ("path", 1)]
    stride = 2
    while stride < lax.axis_size("rows"):
        steps.append(("rows", stride))
        stride *= 2
    return steps


def halve(value, axis, stride):
    size = value.shape[0] // 2
    upper = (lax.axis_index(axis) // stride) % 2
    keep = lax.dynamic_slice_in_dim(value, upper * size, size, 0)
    give = lax.dynamic_slice_in_dim(value, (1 - upper) * size, size, 0)
    return keep.astype(F32) + swap(give.astype(BF16), axis, stride).astype(F32)


def double(value, axis, stride):
    upper = (lax.axis_index(axis) // stride) % 2
    got = swap(value, axis, stride)
    return jnp.concatenate(
        [jnp.where(upper == 0, value, got), jnp.where(upper == 0, got, value)], axis=0
    )


def halve_both(one, two, first, second):
    return halve(one, *first), halve(two, *second)


def parted(value):
    size = value.shape[0] // 2
    return value[:size], value[size:]


class Stage:
    def __init__(self, name):
        self.name = name
        self.arrays, self.views, self.scalars, self.pairs = [], [], [], []
        self.outs, self.temps, self.steps = [], [], []
        self.entries, self.ontos = [], []
        self.flops = 0

    def take(self, array, *view):
        for at, known in enumerate(self.arrays):
            if known is array:
                break
        else:
            at = len(self.arrays)
            self.arrays.append(array)
        for k, (other, seen) in enumerate(self.views):
            if other == at and seen == view:
                return ("in", k)
        self.views.append((at, view))
        return ("in", len(self.views) - 1)

    def take_blocks(self, values, flip, rows):
        self.pairs.append(([self.take(value, slice(None), rows) for value in values], flip))
        return ("pair", len(self.pairs) - 1)

    def scalar(self, array):
        self.scalars.append(array)
        return ("scalar", len(self.scalars) - 1)

    def give(self, dims, dtype=F32, at=None, onto=None):
        self.outs.append(jax.ShapeDtypeStruct(tuple(dims), dtype))
        self.entries.append(at)
        self.ontos.append(onto)
        return ("out", len(self.outs) - 1)

    def piece(self, handle, *index):
        return ("piece", (handle[1], index))

    def peek(self, handle):
        return ("peek", handle[1])

    def temp(self, dims, dtype=F32):
        self.temps.append(pltpu.VMEM(tuple(dims), dtype))
        return ("temp", len(self.temps) - 1)

    def step(self, fn, *handles, flops=0):
        self.flops += flops
        self.steps.append((fn, handles))

    def sem(self, view, block):
        return 8 * view + block

    def view_shape(self, view):
        at, index = view
        return np.broadcast_to(np.zeros((), np.int8), self.arrays[at].shape)[index].shape

    def run(self):
        arrays, views, outs, steps, pairs = self.arrays, self.views, self.outs, self.steps, self.pairs
        order, home = [], {}
        for k, (members, flip) in enumerate(pairs):
            for j, member in enumerate(members):
                home[member[1]] = (k, j, flip)
        under = [onto for onto in self.ontos if onto is not None]

        def need(handle):
            if handle[0] == "in":
                return [handle[1]]
            return [part[1] for part in pairs[handle[1]][0]] if handle[0] == "pair" else []

        for _, handles in steps:
            for handle in handles:
                for k in need(handle):
                    if k not in order:
                        order.append(k)

        def body(*refs):
            refs = list(refs)

            def cut(count):
                taken = refs[:count]
                del refs[:count]
                return taken

            scalars, hbm_in = cut(len(self.scalars)), cut(len(arrays))
            cut(len(under))
            hbm_out = cut(len(outs))
            alone = [k for k in range(len(views)) if k not in home]
            held = dict(zip(alone, cut(len(alone))))
            joint, made, temps, (sems,) = cut(len(pairs)), cut(len(outs)), cut(len(self.temps)), refs
            copies = {}
            for k in order:
                at, index = views[k]
                src = hbm_in[at].at[index] if index else hbm_in[at]
                if k in home:
                    pair, second, flip = home[k]
                    count = self.view_shape(views[k])[0]
                    copies[k] = []
                    for block in range(count):
                        to = (second * count + block) ^ scalars[flip[1]][0]
                        copies[k].append(
                            pltpu.make_async_copy(src.at[block], joint[pair].at[to], sems.at[self.sem(k, block)])
                        )
                else:
                    copies[k] = [pltpu.make_async_copy(src, held[k], sems.at[self.sem(k, 0)])]
                for copy in copies[k]:
                    copy.start()
            waited, sent = set(), {}
            for fn, handles in steps:
                given = []
                for handle in handles:
                    for k in need(handle):
                        if k not in waited:
                            for copy in copies[k]:
                                copy.wait()
                            waited.add(k)
                    if handle[0] == "piece":
                        given.append(made[handle[1][0]].at[handle[1][1]])
                        continue
                    place = {"in": held, "pair": joint, "out": made, "peek": made, "temp": temps, "scalar": scalars}
                    given.append(place[handle[0]][handle[1]])
                fn(*given)
                for kind, k in handles:
                    if kind == "out" and k not in sent:
                        to = hbm_out[k] if self.entries[k] is None else hbm_out[k].at[self.entries[k]]
                        sent[k] = [pltpu.make_async_copy(made[k], to, sems.at[8 * (len(views) + k)])]
                        sent[k][0].start()
                    elif kind == "piece":
                        k, index = k
                        done = sent.setdefault(k, [])
                        sem = sems.at[8 * (len(views) + k) + len(done)]
                        done.append(pltpu.make_async_copy(made[k].at[index], hbm_out[k].at[index], sem))
                        done[-1].start()
            for done in sent.values():
                for copy in done:
                    copy.wait()

        moved = sum(a.size * a.dtype.itemsize for a in outs)
        for view in views:
            moved += int(np.prod(self.view_shape(view))) * arrays[view[0]].dtype.itemsize
        scratch = [
            pltpu.VMEM(self.view_shape(view), arrays[view[0]].dtype) for k, view in enumerate(views) if k not in home
        ]
        for members, _ in pairs:
            size = self.view_shape(views[members[0][1]])
            scratch.append(
                pltpu.VMEM((len(members) * size[0],) + size[1:], arrays[views[members[0][1]][0]].dtype)
            )
        scratch += [
            pltpu.VMEM(o.shape if at is None else o.shape[1:], o.dtype) for o, at in zip(outs, self.entries)
        ]
        aliases = {}
        for k, onto in enumerate(self.ontos):
            if onto is not None:
                aliases[len(self.scalars) + len(arrays) + len(aliases)] = k
        scratch += self.temps + [pltpu.SemaphoreType.DMA((8 * (len(views) + len(outs)),))]
        return pl.pallas_call(
            body,
            out_shape=tuple(outs),
            in_specs=[pl.BlockSpec(memory_space=pltpu.SMEM) for _ in self.scalars]
            + [pl.BlockSpec(memory_space=pl.ANY) for _ in arrays + under],
            out_specs=tuple(pl.BlockSpec(memory_space=pl.ANY) for _ in outs),
            scratch_shapes=scratch,
            input_output_aliases=aliases,
            compiler_params=pltpu.CompilerParams(vmem_limit_bytes=VMEM_LIMIT),
            cost_estimate=pl.CostEstimate(flops=self.flops, bytes_accessed=moved, transcendentals=0),
            name=self.name,
        )(*self.scalars, *arrays, *under)


class Masks:
    def __init__(self, spots, cols):
        self.main = (0, spots)
        self.ext = (spots, 2 * spots + 2 * cols)
        self.prev = (2 * spots + 2 * cols, 3 * spots + 2 * cols)
        self.next = (3 * spots + 2 * cols, 4 * spots + 2 * cols)
        self.slow = (4 * spots + 2 * cols, 4 * spots + 2 * cols + 8)
        self.fast = (4 * spots + 2 * cols + 8, 4 * spots + 2 * cols + 16)
        self.half = (4 * spots + 2 * cols + 16, 4 * spots + 2 * cols + 24)
        self.path = (4 * spots + 2 * cols + 24, 4 * spots + 2 * cols + 32)
        self.rows = 4 * spots + 2 * cols + 32


def make_masks(m, rows, cols, last, place, clips, mk):
    half = place[0] % 2
    path = place[1]
    side = clips[0, place[0] // 2]
    area = 0
    for k in range(clips.shape[1]):
        area = area + clips[0, k] * clips[0, k]
    shift = cols.bit_length() - 1

    def inside(first, count):
        at = lax.broadcasted_iota(jnp.int32, (count * cols, LANES), 0)
        line = half * rows + first + (at >> shift)
        spot = at & (cols - 1)
        good = (line >= 0) & (line < 2 * rows) & (line < side) & (spot < side)
        return jnp.where(good, 1.0, 0.0)

    main = inside(0, rows)
    mk[m.main[0] : m.main[1], :] = main
    mk[m.ext[0] : m.ext[1], :] = inside(-1, rows + 2)
    mk[m.prev[0] : m.prev[1], :] = main * jnp.where(path > 0, 1.0, 0.0)
    mk[m.next[0] : m.next[1], :] = main * jnp.where(path < last, 1.0, 0.0)

    def fill(span, value):
        mk[span[0] : span[1], :] = jnp.full((8, LANES), value, F32)

    fill(m.slow, TS * area.astype(F32))
    fill(m.fast, TF * area.astype(F32))
    fill(m.half, half.astype(F32))
    fill(m.path, path.astype(F32))


def own_row(m, spots, cols, col0, width, z, mk, row):
    for t in range(z.shape[0]):
        lower = mk[m.half[0] : m.half[0] + 1, :] > 0.5
        for lane in range(0, width, LANES):
            at = col0 + lane
            row[t, :, lane : lane + LANES] = jnp.where(
                lower, z[t, 0:cols, at : at + LANES], z[t, spots - cols : spots, at : at + LANES]
            )


def own_edge(m, lead, tail, z, mk, edge):
    frames = z.shape[0]
    second = mk[m.path[0] : m.path[0] + 1, :] > 0.5
    for lane in range(0, edge.shape[1], LANES):
        edge[:, lane : lane + LANES] = jnp.where(
            second,
            z[0, :, lead + lane : lead + lane + LANES],
            z[frames - 1, :, tail + lane : tail + lane + LANES],
        ).astype(edge.dtype)


def spread_sums(*refs):
    parts, out = refs[:-1], refs[-1]
    row = jnp.concatenate([part[...] for part in parts], axis=1)
    out[...] = jnp.broadcast_to(row[None], out.shape)


def make_w7(lat, group, wl, wf, w7):
    inner = wf.shape[1]
    w7[...] = jnp.zeros(w7.shape, BF16)
    for j in range(wl.shape[0]):
        w7[j * LANES : (j + 1) * LANES, 0:lat] = wl[j]
    at = lax.broadcasted_iota(jnp.int32, (inner, LANES), 0)
    lane = lax.broadcasted_iota(jnp.int32, (inner, LANES), 1)
    places = [jnp.where(lane == at + inner * k, 1.0, 0.0).astype(BF16) for k in range(group)]
    for f in range(1, group + 3):
        used = [k for k in range(group) if 0 <= f - 1 - k < 3]
        got = None
        for k in used:
            more = dot_tn(wf[f - 1 - k], places[k])
            got = more if got is None else got + more
        w7[f * LANES : (f + 1) * LANES, lat : lat + LANES] = got.astype(BF16)


def make_blocks(group, ws, wp, wfs, wfp):
    inner = wp.shape[0]
    at = lax.broadcasted_iota(jnp.int32, (inner, LANES), 0)
    lane = lax.broadcasted_iota(jnp.int32, (inner, LANES), 1)
    tile = jnp.where((lane & (inner - 1)) == at, 1.0, 0.0).astype(BF16)
    shift = inner.bit_length() - 1
    for tap in range(ws.shape[0]):
        got = dot(ws[tap], tile)
        for k in range(group):
            kept = jnp.where((lane >> shift) == k, got, 0.0).astype(BF16)
            row = (tap % 3) * LANES + k * inner
            wfs[tap // 3, row : row + inner, :] = kept
    wfp[...] = jnp.zeros(wfp.shape, BF16)
    for k in range(group):
        wfp[k * inner : (k + 1) * inner, k * LANES : (k + 1) * LANES] = wp[...]


def widen(rows, width):
    return jnp.concatenate([rows] * (width // LANES), axis=1)


def sublane_sums(value):
    return jnp.sum(value.reshape(value.shape[0] // 8, 8, value.shape[1]), axis=0)


def row_sum(value):
    return jnp.sum(value, axis=0, keepdims=True)


def fold_packed(row):
    full = jnp.broadcast_to(row, (8, LANES))
    full = full + pltpu.roll(full, 64, 1)
    full = full + pltpu.roll(full, 32, 1)
    return full[0:1]


def totals(st, lo, width, packed=False):
    first = jnp.sum(st[:, :, lo : lo + width], axis=0)
    second = jnp.sum(st[:, :, lo + width : lo + 2 * width], axis=0)
    if packed:
        return fold_packed(first), fold_packed(second)
    return first, second


def norm_rows(st, lo, width, count, packed=False):
    first, second = totals(st, lo, width, packed)
    mean = first / count
    return mean, lax.rsqrt(second / count - mean * mean + EPSILON)


def keep_norm(lo, width, span, st, mk, nz):
    mean, rstd = norm_rows(st, lo, width, widen(mk[span[0] : span[0] + 1, :], width))
    nz[0:1, :] = mean
    nz[1:2, :] = rstd


def keep_sums(lo, width, st, gb):
    one, two = totals(st, lo, width)
    gb[0:1, :] = one
    gb[1:2, :] = two


def clear(*refs):
    for ref in refs:
        ref[...] = jnp.zeros(ref.shape, F32)


def close_sums(one, two, s):
    s[...] = jnp.concatenate([row_sum(one[...]), row_sum(two[...])], axis=1)


def sigmoid(value):
    return 0.5 * jnp.tanh(0.5 * value) + 0.5


def silu(value):
    return value * sigmoid(value)


def silu_slope(value):
    sigma = sigmoid(value)
    return sigma * (1.0 + value * (1.0 - sigma))


def dot(a, b):
    return jnp.dot(a, b, preferred_element_type=F32)


def dot_nt(a, b):
    return lax.dot_general(a, b, (((1,), (1,)), ((), ())), preferred_element_type=F32)


def dot_tn(a, b):
    return lax.dot_general(a, b, (((0,), (0,)), ((), ())), preferred_element_type=F32)


def flat(value):
    return value.reshape(value.shape[0] * value.shape[1], value.shape[2])


def store_shifts(dst, t, value, cols):
    rows, width = value.shape
    spot = lax.broadcasted_iota(jnp.int32, (rows, width), 0) & (cols - 1)
    left = jnp.where(spot == 0, 0.0, pltpu.roll(value, 1, 0))
    right = jnp.where(spot == cols - 1, 0.0, pltpu.roll(value, rows - 1, 0))
    dst[t, :, 0:width] = left.astype(BF16)
    dst[t, :, width : 2 * width] = value.astype(BF16)
    dst[t, :, 2 * width : 3 * width] = right.astype(BF16)


def taps_of(frames_ref, frames, group):
    return jnp.concatenate(
        [
            jnp.concatenate([frames_ref[group * t + f] for f in range(7)], axis=1)
            for t in range(frames)
        ],
        axis=0,
    )


def entry_sums(y, lat, frames, spots):
    width = y.shape[1]
    one = jnp.zeros((8, width), F32)
    two = jnp.zeros((8, width), F32)
    for t in range(frames):
        part = y[t * spots : (t + 1) * spots]
        one = one + sublane_sums(part)
        two = two + sublane_sums(part * part)
    one = row_sum(one)
    two = row_sum(two)
    return jnp.concatenate([one[:, :lat], two[:, :lat], one[:, lat:], two[:, lat:]], axis=1)


def fast_entry(m, frames, group, x, before, after, mk, w7, fw, y, s):
    spots = x.shape[1]
    count = x.shape[0]

    def put(at, value, span):
        fw[at] = (value.astype(F32) * mk[span[0] : span[1], :]).astype(BF16)

    for k in range(2):
        put(k, before[k], m.prev)
        put(2 + count + k, after[k], m.next)
    for k in range(count):
        put(2 + k, x[k], m.main)
    out = dot(taps_of(fw, frames, group), w7[...])
    for t in range(frames):
        y[t] = out[t * spots : (t + 1) * spots]
    s[...] = entry_sums(out, w7.shape[1] - LANES, frames, spots)


def slow_partial(m, frames, x, before, after, mk, wt, xm, fpart):
    spots, wide = x.shape[1], x.shape[2]
    sources = [(before, m.prev)] + [(x.at[t], m.main) for t in range(frames)] + [(after, m.next)]
    for k, (src, span) in enumerate(sources):
        for lo in range(0, wide, 256):
            mask = widen(mk[span[0] : span[1], :], 256)
            xm[k, :, lo : lo + 256] = (src[:, lo : lo + 256].astype(F32) * mask).astype(BF16)
    out = dot(flat(xm[0:frames]), wt[0, :wide, :])
    for j in range(1, 3):
        out = out + dot(flat(xm[j : j + frames]), wt[j, :wide, :])
    for t in range(frames):
        fpart[t] = out[t * spots : (t + 1) * spots]


def lat_join(m, n, frames, lat, st, y, before, after, fpart, wt, gs, bs, mk, jl, first, s, nl, jw):
    spots = y.shape[1]
    wide = wt.shape[1] - lat
    count = widen(mk[m.slow[0] : m.slow[0] + 1, :], lat)
    mean, rstd = norm_rows(st, 0, lat, count)
    nl[0:1, :] = mean
    nl[1:2, :] = rstd
    scale = rstd * gs[n : n + 1, 0:lat]
    bias = bs[n : n + 1, 0:lat]
    sources = (
        [(before[:, 0:lat], m.prev)]
        + [(y[t, :, 0:lat], m.main) for t in range(frames)]
        + [(after[:, 0:lat], m.next)]
    )
    for k, (value, span) in enumerate(sources):
        mask = widen(mk[span[0] : span[1], :], lat)
        act = (silu((value - mean) * scale + bias) * mask).astype(BF16)
        jw[k] = act
        if 1 <= k <= frames:
            jl[k - 1] = act
    out = flat(fpart[...])
    for j in range(3):
        out = out + dot(flat(jw[j : j + frames]), wt[j, wide:, :])
    one = jnp.zeros((8, out.shape[1]), F32)
    two = jnp.zeros((8, out.shape[1]), F32)
    for t in range(frames):
        part = out[t * spots : (t + 1) * spots]
        first[t] = part
        one = one + sublane_sums(part)
        two = two + sublane_sums(part * part)
    s[...] = jnp.concatenate([row_sum(one), row_sum(two)], axis=1)


def space_forward(
    m, n, frames, cols, lo, at, width, col0, packed, span, st, z, row, w, g, b, mk, aw, out, s, nz, vw
):
    spots = z.shape[1]
    count = widen(mk[span[0] : span[0] + 1, :], width)
    mean, rstd = norm_rows(st, at, width, count, packed)
    nz[0:1, :] = mean
    nz[1:2, :] = rstd
    scale = rstd * g[n : n + 1, lo : lo + width]
    bias = b[n : n + 1, lo : lo + width]
    mask = widen(mk[m.ext[0] : m.ext[1], :], width)
    for t in range(frames):
        value = jnp.concatenate([row[t], z[t, :, col0 : col0 + width], row[t]], axis=0)
        act = silu((value - mean) * scale + bias) * mask
        aw[t] = act.astype(BF16)
        store_shifts(vw, t, act, cols)
    total = dot(flat(vw[:, 0:spots, :]), w[0])
    for i in range(1, 3):
        total = total + dot(flat(vw[:, i * cols : i * cols + spots, :]), w[i])
    mask = widen(mk[m.main[0] : m.main[1], :], width)
    one = jnp.zeros((8, width), F32)
    two = jnp.zeros((8, width), F32)
    for t in range(frames):
        part = total[t * spots : (t + 1) * spots]
        out[t] = part
        part = part * mask
        one = one + sublane_sums(part)
        two = two + sublane_sums(part * part)
    s[...] = jnp.concatenate([row_sum(one), row_sum(two)], axis=1)


def slow_acts(m, n, frames, lo, halo, st, z, *rest):
    if halo:
        before, after, g, b, mk, a2, nz, aw = rest
    else:
        g, b, mk, a2, nz, aw = rest
    width = z.shape[2]
    keep_norm(0, width, m.slow, st, mk, nz)
    mean = nz[0:1, :]
    scale = nz[1:2, :] * g[n : n + 1, lo : lo + width]
    bias = b[n : n + 1, lo : lo + width]
    sources = [(z[t], m.main, t + halo) for t in range(frames)]
    if halo:
        sources += [(before[...], m.prev, 0), (after[...], m.next, frames + 1)]
    for value, span, at in sources:
        mask = widen(mk[span[0] : span[1], :], width)
        act = (silu((value - mean) * scale + bias) * mask).astype(BF16)
        aw[at] = act
        if halo <= at < frames + halo:
            a2[at - halo] = act


def slow_third(frames, halo, at, aw, wp, third, s):
    spots = aw.shape[1]
    wide = s.shape[1] // 2
    out = dot(flat(aw[...]), wp[...])
    one = jnp.zeros((8, 256), F32)
    two = jnp.zeros((8, 256), F32)
    for t in range(frames + 2 * halo):
        part = out[t * spots : (t + 1) * spots]
        third[t] = part.astype(BF16)
        if halo <= t < frames + halo:
            one = one + sublane_sums(part)
            two = two + sublane_sums(part * part)
    s[:, at : at + 256] = row_sum(one)
    s[:, wide + at : wide + at + 256] = row_sum(two)


def fast_third(m, n, frames, lo, at, st, z, wp, g, b, mk, a2, ft, s, nz):
    spots = z.shape[1]
    count = mk[m.fast[0] : m.fast[0] + 1, :]
    mean, rstd = norm_rows(st, at, LANES, count, True)
    nz[0:1, :] = mean
    nz[1:2, :] = rstd
    scale = rstd * g[n : n + 1, lo : lo + LANES]
    bias = b[n : n + 1, lo : lo + LANES]
    mask = mk[m.main[0] : m.main[1], :]
    for t in range(frames):
        a2[t] = (silu((z[t] - mean) * scale + bias) * mask).astype(BF16)
    acts = flat(a2[...])
    one = jnp.zeros((8, LANES), F32)
    two = jnp.zeros((8, LANES), F32)
    out = dot(acts, wp[...])
    for t in range(frames):
        for lane in range(0, wp.shape[1], LANES):
            part = out[t * spots : (t + 1) * spots, lane : lane + LANES]
            ft[t, :, lane : lane + LANES] = part.astype(BF16)
            one = one + sublane_sums(part)
            two = two + sublane_sums(part * part)
    s[...] = jnp.concatenate([row_sum(one), row_sum(two)], axis=1)


def fast_next(m, n, frames, group, lo, at, st, ft, before, after, fw0, w7, g, b, mk, fw1, y, s, nz):
    spots = ft.shape[1]
    count = mk[m.fast[0] : m.fast[0] + 1, :]
    mean, rstd = norm_rows(st, at, LANES, count)
    nz[0:1, :] = mean
    nz[1:2, :] = rstd
    scale = rstd * g[n : n + 1, lo : lo + LANES]
    bias = b[n : n + 1, lo : lo + LANES]
    total = frames * group

    def out_of(k, value, span):
        z = fw0[k].astype(F32) + ((value - mean) * scale + bias)
        return silu(z) * mk[span[0] : span[1], :]

    for k in range(2):
        lane = k * LANES
        fw1[k] = out_of(k, before[:, lane : lane + LANES], m.prev).astype(BF16)
        fw1[2 + total + k] = out_of(2 + total + k, after[:, lane : lane + LANES], m.next).astype(BF16)
    for t in range(frames):
        for f in range(group):
            k = t * group + f
            fw1[2 + k] = out_of(2 + k, ft[t, :, f * LANES : (f + 1) * LANES], m.main).astype(BF16)
    out = dot(taps_of(fw1, frames, group), w7[...])
    for t in range(frames):
        y[t] = out[t * spots : (t + 1) * spots]
    s[...] = entry_sums(out, w7.shape[1] - LANES, frames, spots)


def fast_last(m, n, frames, group, lo, at, st, ft, f1, cot, g, b, mk, out, pre, s, nz):
    count = mk[m.fast[0] : m.fast[0] + 1, :]
    mean, rstd = norm_rows(st, at, LANES, count)
    nz[0:1, :] = mean
    nz[1:2, :] = rstd
    gain = g[n : n + 1, lo : lo + LANES]
    bias = b[n : n + 1, lo : lo + LANES]
    mask = mk[m.main[0] : m.main[1], :]
    one = jnp.zeros((8, LANES), F32)
    two = jnp.zeros((8, LANES), F32)
    for t in range(frames):
        for f in range(group):
            k = t * group + f
            hat = (ft[t, :, f * LANES : (f + 1) * LANES].astype(F32) - mean) * rstd
            z = f1[k].astype(F32) + hat * gain + bias
            sigma = sigmoid(z)
            out[k] = z * sigma * mask
            grad = cot[k].astype(F32) * mask * (sigma * (1.0 + z * (1.0 - sigma)))
            pre[k] = grad.astype(BF16)
            one = one + sublane_sums(grad)
            two = two + sublane_sums(grad * hat)
    s[...] = jnp.concatenate([row_sum(one), row_sum(two)], axis=1)


def chunked(total, step, body, init):
    def turn(i, carry):
        return body(pl.multiple_of(i * step, step), carry)

    return lax.fori_loop(0, total // step, turn, init)


def slow_next(n, lo, span, third, xm, nz, g, b, mk, sw):
    spots, wide = third.shape
    mean = nz[0:1, :]
    scale = nz[1:2, :] * g[n : n + 1, lo : lo + wide]
    bias = b[n : n + 1, lo : lo + wide]

    def turn(at, carry):
        mask = widen(mk[pl.ds(span[0] + at, 16), :], 512)
        for c in range(0, wide, 512):
            z = third[pl.ds(at, 16), c : c + 512].astype(F32)
            z = (z - mean[:, c : c + 512]) * scale[:, c : c + 512] + bias[:, c : c + 512]
            z = xm[pl.ds(at, 16), c : c + 512].astype(F32) + z
            sw[pl.ds(at, 16), c : c + 512] = (silu(z) * mask).astype(BF16)
        return carry

    chunked(spots, 16, turn, 0)


def time_partial(frames, sw, wt, fpart):
    spots = sw.shape[1]
    out = dot(flat(sw[0:frames]), wt[0])
    for j in range(1, 3):
        out = out + dot(flat(sw[j : j + frames]), wt[j])
    for t in range(frames):
        fpart[t] = out[t * spots : (t + 1) * spots]


def slow_last(m, n, lo, third, slow, cot, nz, g, b, mk, out, pre, one, two):
    spots, wide = third.shape
    mean, rstd = nz[0:1, :], nz[1:2, :]
    gain = g[n : n + 1, lo : lo + wide]
    bias = b[n : n + 1, lo : lo + wide]

    def turn(at, sums):
        ones, twos = [], []
        mask = widen(mk[pl.ds(m.main[0] + at, 16), :], 512)
        for c in range(0, wide, 512):
            hat = third[pl.ds(at, 16), c : c + 512].astype(F32)
            hat = (hat - mean[:, c : c + 512]) * rstd[:, c : c + 512]
            z = slow[pl.ds(at, 16), c : c + 512].astype(F32) + hat * gain[:, c : c + 512] + bias[:, c : c + 512]
            sigma = sigmoid(z)
            out[pl.ds(at, 16), c : c + 512] = z * sigma * mask
            grad = cot[pl.ds(at, 16), c : c + 512].astype(F32) * mask
            grad = grad * (sigma * (1.0 + z * (1.0 - sigma)))
            pre[pl.ds(at, 16), c : c + 512] = grad.astype(BF16)
            ones.append(sublane_sums(grad))
            twos.append(sublane_sums(grad * hat))
        return sums[0] + jnp.concatenate(ones, axis=1), sums[1] + jnp.concatenate(twos, axis=1)

    one[...], two[...] = chunked(spots, 16, turn, (one[...], two[...]))


def slow_third_grad(m, n, lo, pre, third, n3, gb, g, mk, d3):
    spots, wide = pre.shape
    count = widen(mk[m.slow[0] : m.slow[0] + 1, :], wide)
    mean, rstd = n3[0:1, :], n3[1:2, :]
    scale = g[n : n + 1, lo : lo + wide] * rstd
    one = gb[0:1, :] / count
    two = gb[1:2, :] / count * rstd

    def turn(i, carry):
        mask = widen(mk[pl.ds(m.main[0] + i, 16), :], 512)
        for c in range(0, wide, 512):
            hat = (third[pl.ds(i, 16), c : c + 512].astype(F32) - mean[:, c : c + 512]) * two[:, c : c + 512]
            grad = pre[pl.ds(i, 16), c : c + 512].astype(F32) - mask * (one[:, c : c + 512] + hat)
            d3[pl.ds(i, 16), c : c + 512] = (scale[:, c : c + 512] * grad).astype(BF16)
        return carry

    chunked(spots, 16, turn, 0)


def slow_third_back(m, n, frames, lo, d3, z, n2, wp, g, b, mk, e2, s):
    spots, width = z.shape[1], z.shape[2]
    out = dot_nt(flat(d3[...]), wp[...])
    gain = g[n : n + 1, lo : lo + width]
    bias = b[n : n + 1, lo : lo + width]
    back_act(m, frames, spots, out, z, 0, n2[0:1, :], n2[1:2, :], gain, bias, mk, e2, s)


def back_act(m, frames, spots, out, z, col0, mean, rstd, gain, bias, mk, e, s):
    width = out.shape[1]
    mask = widen(mk[m.main[0] : m.main[1], :], width)
    one = jnp.zeros((8, width), F32)
    two = jnp.zeros((8, width), F32)
    for t in range(frames):
        hat = (z[t, :, col0 : col0 + width] - mean) * rstd
        grad = out[t * spots : (t + 1) * spots] * mask * silu_slope(hat * gain + bias)
        e[t] = grad
        one = one + sublane_sums(grad)
        two = two + sublane_sums(grad * hat)
    s[...] = jnp.concatenate([row_sum(one), row_sum(two)], axis=1)


def fast_third_back(m, n, frames, group, lo3, lo2, at, st, pre, ft, n3, z, n2, wp, g, b, mk, d3, e2, s, gb):
    spots = z.shape[1]
    count = mk[m.fast[0] : m.fast[0] + 1, :]
    one, two = totals(st, at, LANES)
    gb[0:1, :] = one
    gb[1:2, :] = two
    mean, rstd = n3[0:1, :], n3[1:2, :]
    scale = g[n : n + 1, lo3 : lo3 + LANES] * rstd
    one = one / count
    two = two / count * rstd
    mask = mk[m.main[0] : m.main[1], :]
    for t in range(frames):
        for f in range(group):
            hat = (ft[t, :, f * LANES : (f + 1) * LANES] - mean) * two
            grad = pre[t * group + f] - mask * (one + hat)
            d3[t, :, f * LANES : (f + 1) * LANES] = (scale * grad).astype(BF16)
    out = dot_nt(flat(d3[...]), wp[...])
    mean, rstd = n2[0:1, :], n2[1:2, :]
    gain = g[n : n + 1, lo2 : lo2 + LANES]
    bias = b[n : n + 1, lo2 : lo2 + LANES]
    back_act(m, frames, spots, out, z, 0, mean, rstd, gain, bias, mk, e2, s)


def space_back(
    m, n, frames, cols, lo2, lo1, at, width, col0, packed, span,
    st, e, erow, z, zrow, nz, z1, n1, w, g, b, mk, d2, e1, s, gb, vw,
):
    spots = z.shape[1]
    count = widen(mk[span[0] : span[0] + 1, :], width)
    one, two = totals(st, at, width, packed)
    gb[0:1, :] = one
    gb[1:2, :] = two
    mean, rstd = nz[0:1, :], nz[1:2, :]
    scale = g[n : n + 1, lo2 : lo2 + width] * rstd
    one = one / count
    two = two / count * rstd
    mask = widen(mk[m.ext[0] : m.ext[1], :], width)
    for t in range(frames):
        grad = jnp.concatenate([erow[t], e[t], erow[t]], axis=0)
        value = jnp.concatenate([zrow[t], z[t], zrow[t]], axis=0)
        grad = scale * mask * (grad - (one + (value - mean) * two))
        d2[t] = grad[cols : cols + spots].astype(BF16)
        store_shifts(vw, t, grad.astype(BF16).astype(F32), cols)
    total = None
    for i in range(3):
        rows = (2 - i) * cols
        for j in range(3):
            lane = (2 - j) * width
            part = dot_nt(flat(vw[:, rows : rows + spots, lane : lane + width]), w[i, j * width : (j + 1) * width, :])
            total = part if total is None else total + part
    mean, rstd = n1[0:1, :], n1[1:2, :]
    gain = g[n : n + 1, lo1 : lo1 + width]
    bias = b[n : n + 1, lo1 : lo1 + width]
    back_act(m, frames, spots, total, z1, col0, mean, rstd, gain, bias, mk, e1, s)


def first_taps(frames, dw):
    return [flat(dw[2 - j : 2 - j + frames]) for j in range(3)]


def time_back(taps, wt, lo, size):
    out = dot_nt(taps[0], wt[0, lo : lo + size, :])
    for j in range(1, 3):
        out = out + dot_nt(taps[j], wt[j, lo : lo + size, :])
    return out


def slow_first_back(m, n, frames, lo1, at, st, e, ep, en, z, zp, zn, n1, wt, y, nl, g, b, mk, dw, el, s, gb):
    spots, width = z.shape[1], z.shape[2]
    lat = nl.shape[1]
    wide = wt.shape[1] - lat
    count = widen(mk[m.slow[0] : m.slow[0] + 1, :], width)
    one, two = totals(st, at, width)
    gb[0:1, :] = one
    gb[1:2, :] = two
    mean, rstd = n1[0:1, :], n1[1:2, :]
    scale = g[n : n + 1, lo1 : lo1 + width] * rstd
    one = one / count
    two = two / count * rstd
    sources = (
        [(ep, zp, m.prev)] + [(e.at[t], z.at[t], m.main) for t in range(frames)] + [(en, zn, m.next)]
    )
    for k, (grad, value, span) in enumerate(sources):
        mask = widen(mk[span[0] : span[1], :], width)
        dw[k] = (scale * mask * (grad[...] - (one + (value[...] - mean) * two))).astype(BF16)
    out = time_back(first_taps(frames, dw), wt, wide, lat)
    back_act(
        m, frames, spots, out, y, 0, nl[0:1, :], nl[1:2, :], g[n : n + 1, 0:lat], b[n : n + 1, 0:lat], mk, el, s
    )


def slow_input_last(m, frames, dw, wt, pre, mk, gx):
    spots, wide = pre.shape[1], pre.shape[2]
    taps = first_taps(frames, dw)
    mask = widen(mk[m.main[0] : m.main[1], :], 256)
    for c in range(0, wide, 256):
        out = time_back(taps, wt, c, 256)
        for t in range(frames):
            gx[t, :, c : c + 256] = (out[t * spots : (t + 1) * spots] + pre[t, :, c : c + 256]) * mask


def slow_input_back(m, n, frames, lo, at, dw, wt, pre, xm, third, n3, g, b, mk, pre0, s):
    spots = pre.shape[1]
    wide = s.shape[1] // 2
    mask = widen(mk[m.main[0] : m.main[1], :], 256)
    out = time_back(first_taps(frames, dw), wt, 0, 256)
    mean, rstd = n3[0:1, at : at + 256], n3[1:2, at : at + 256]
    gain = g[n - 1 : n, lo + at : lo + at + 256]
    bias = b[n - 1 : n, lo + at : lo + at + 256]
    one = jnp.zeros((8, 256), F32)
    two = jnp.zeros((8, 256), F32)
    for t in range(frames):
        grad = (out[t * spots : (t + 1) * spots] + pre[t].astype(F32)) * mask
        hat = (third[t].astype(F32) - mean) * rstd
        z0 = xm[t].astype(F32) + hat * gain + bias
        grad = grad * silu_slope(z0)
        pre0[t] = grad.astype(BF16)
        one = one + sublane_sums(grad)
        two = two + sublane_sums(grad * hat)
    s[:, at : at + 256] = row_sum(one)
    s[:, wide + at : wide + at + 256] = row_sum(two)


def fast_first_back(
    m, n, frames, lo1, at1, atl, st1, stl, el, eln, ef, efp, efn, y, yp, yn, nl, n1, gs, g, mk,
    dl, dfw, dln, dfp, dfn, gbl, gb1,
):
    lat = nl.shape[1]
    count = widen(mk[m.slow[0] : m.slow[0] + 1, :], lat)
    one, two = totals(stl, atl, lat)
    gbl[0:1, :] = one
    gbl[1:2, :] = two
    mean, rstd = nl[0:1, :], nl[1:2, :]
    scale = gs[n : n + 1, 0:lat] * rstd
    one = one / count
    two = two / count * rstd

    def lat_grad(grad, value, span):
        mask = widen(mk[span[0] : span[1], :], lat)
        return (scale * mask * (grad - (one + (value - mean) * two))).astype(BF16)

    for t in range(frames):
        dl[t] = lat_grad(el[t], y[t, :, 0:lat], m.main)
    dln[...] = lat_grad(eln[...], yn[:, 0:lat], m.next)
    fcount = mk[m.fast[0] : m.fast[0] + 1, :]
    fone, ftwo = totals(st1, at1, LANES, True)
    gb1[0:1, :] = fone
    gb1[1:2, :] = ftwo
    fmean, frstd = n1[0:1, :], n1[1:2, :]
    fscale = g[n : n + 1, lo1 : lo1 + LANES] * frstd
    fone = fone / fcount
    ftwo = ftwo / fcount * frstd

    def first_grad(grad, value, span):
        mask = mk[span[0] : span[1], :]
        return (fscale * mask * (grad - (fone + (value - fmean) * ftwo))).astype(BF16)

    for t in range(frames):
        dfw[t] = first_grad(ef[t], y[t, :, lat:], m.main)
    dfp[...] = first_grad(efp[...], yp[:, lat:], m.prev)
    dfn[...] = first_grad(efn[...], yn[:, lat:], m.next)


def fast_input_back(m, n, frames, group, lo3, last, dl, dfw, dln, dfp, dfn, w7, pre, *rest):
    if last:
        mk, gx, buf = rest
    else:
        fw0, ft, n3, g, b, mk, pre0, s, buf = rest
    spots, lat = dl.shape[1], dl.shape[2]
    both = jnp.concatenate([flat(dl[...]), flat(dfw[...])], axis=1)
    buf[...] = jnp.zeros(buf.shape, F32)
    out = dot_nt(both, w7[...])
    for t in range(frames):
        for f in range(7):
            k = group * t + f
            buf[k] = buf[k] + out[t * spots : (t + 1) * spots, f * LANES : (f + 1) * LANES]
    buf[2] = buf[2] + dot_nt(dfp[...], w7[6 * LANES : 7 * LANES, lat:])
    after = dot_nt(jnp.concatenate([dln[...], dfn[...]], axis=1), w7[0 : 2 * LANES, :])
    total = frames * group
    for f in range(2):
        buf[total + f] = buf[total + f] + after[:, f * LANES : (f + 1) * LANES]
    mask = mk[m.main[0] : m.main[1], :]
    if last:
        for k in range(total):
            gx[k] = (pre[k] + buf[2 + k]) * mask
        return
    mean, rstd = n3[0:1, :], n3[1:2, :]
    gain = g[n - 1 : n, lo3 : lo3 + LANES]
    bias = b[n - 1 : n, lo3 : lo3 + LANES]
    one = jnp.zeros((8, LANES), F32)
    two = jnp.zeros((8, LANES), F32)
    for k in range(total):
        t, f = k // group, k % group
        hat = (ft[t, :, f * LANES : (f + 1) * LANES] - mean) * rstd
        z0 = fw0[2 + k].astype(F32) + hat * gain + bias
        grad = (pre[k] + buf[2 + k]) * mask * silu_slope(z0)
        pre0[k] = grad.astype(BF16)
        one = one + sublane_sums(grad)
        two = two + sublane_sums(grad * hat)
    s[...] = jnp.concatenate([row_sum(one), row_sum(two)], axis=1)


def point_weights(a2, d3, out):
    acts = flat(a2[...])
    for k in range(out.shape[0]):
        out[k] = dot_tn(acts, flat(d3[:, :, k * 256 : (k + 1) * 256])).astype(BF16)


def space_weights(cols, aw, d2, out, vw):
    frames, spots, width = d2.shape
    for t in range(frames):
        store_shifts(vw, t, aw[t].astype(F32), cols)
    grads = flat(d2[...])
    for i in range(3):
        out[i] = dot_tn(flat(vw[:, i * cols : i * cols + spots, :]), grads).astype(BF16)


def time_weights(skip, slow, jl, dw, out):
    frames, spots, width = jl.shape
    wide = slow.shape[2]
    grads = jnp.concatenate([flat(dw[2 - j : 2 - j + frames]) for j in range(3)], axis=1)
    for c in range(0, wide + jl.shape[2], 256):
        if c < wide:
            acts = flat(slow[skip : skip + frames, :, c : c + 256])
        else:
            acts = flat(jl[:, :, c - wide : c - wide + 256])
        got = dot_tn(acts, grads)
        for j in range(3):
            out[j, c : c + 256, :] = got[:, j * width : (j + 1) * width].astype(BF16)


def group_blocks(value, group):
    size = LANES // group
    rows = lax.broadcasted_iota(jnp.int32, (LANES, LANES), 0) >> (size.bit_length() - 1)
    lanes = lax.broadcasted_iota(jnp.int32, (LANES, LANES), 1) >> (size.bit_length() - 1)
    kept = jnp.where(rows == lanes, value, 0.0)
    kept = kept + pltpu.roll(kept, 64, 1)
    kept = kept + pltpu.roll(kept, 32, 1)
    total = kept[0:size]
    for k in range(1, group):
        total = total + kept[k * size : (k + 1) * size]
    return total


def at_lanes(blocks):
    lanes = lax.broadcasted_iota(jnp.int32, blocks[0].shape, 1) >> 5
    out = jnp.zeros(blocks[0].shape, F32)
    for k, block in enumerate(blocks):
        out = jnp.where(lanes == k, block, out)
    return out


def fast_weights(group, cols, lat, fw, dl, df, fa1, d2, fa2, d3, out, vw):
    frames, spots, _ = dl.shape
    size = LANES // group
    both = jnp.concatenate([flat(dl[...]), flat(df[...])], axis=1)
    taps = [[None] * group for _ in range(3)]
    for f in range(7):
        acts = jnp.concatenate([fw[group * t + f] for t in range(frames)], axis=0)
        got = dot_tn(acts, both)
        if f < 5:
            out[f * LANES : (f + 1) * LANES, :] = got[:, :lat].astype(BF16)
        for k in range(group):
            if 0 <= f - k - 1 < 3:
                taps[f - k - 1][k] = got[:, lat:]
    lanes = lax.broadcasted_iota(jnp.int32, (LANES, LANES), 1) >> (size.bit_length() - 1)
    tap_sums = []
    for j in range(3):
        kept = jnp.zeros((LANES, LANES), F32)
        for k in range(group):
            kept = jnp.where(lanes == k, taps[j][k], kept)
        kept = kept + pltpu.roll(kept, 64, 1)
        tap_sums.append(kept + pltpu.roll(kept, 32, 1))
    low = 5 * LANES
    out[low : low + LANES, 0:LANES] = at_lanes(tap_sums).T.astype(BF16)
    for t in range(frames):
        store_shifts(vw, t, fa1[t].astype(F32), cols)
    grads = flat(d2[...])
    for i in range(3):
        got = dot_tn(flat(vw[:, i * cols : i * cols + spots, :]), grads)
        blocks = [group_blocks(got[j * LANES : (j + 1) * LANES], group) for j in range(3)]
        out[low + size * i : low + size * (i + 1), LANES : 2 * LANES] = at_lanes(blocks).astype(BF16)
    acts = flat(fa2[...])
    total = jnp.zeros((size, LANES), F32)
    for k in range(group):
        got = dot_tn(acts, flat(d3[:, :, k * LANES : (k + 1) * LANES]))
        total = total + got[k * size : (k + 1) * size]
    out[low + 3 * size : low + 4 * size, LANES : 2 * LANES] = total.astype(BF16)


def unpack_fast(n, inner, load, outs):
    glat, gft, gfs, gfp = outs
    low = glat.shape[1]
    for at in range(0, low, inner):
        glat[n, at : at + inner, :] = load(at, inner)
    for i in range(4):
        got = load(low + inner * i, inner)
        if i < 3:
            gft[n, i] = got[:, 0:LANES]
            for j in range(3):
                moved = got[:, LANES:] if j == 0 else pltpu.roll(got[:, LANES:], LANES - inner * j, 1)
                gfs[n, 3 * i + j] = moved[:, 0:inner]
        else:
            gfp[n] = got[:, LANES:]


def runs_of(at, count, base, half, one, two):
    found = []
    while count:
        core, row = at // half, base + at % half
        ref, size = one, one.shape[1]
        if row >= 4 * size:
            ref, row = two, row - 4 * size
            size = two.shape[1]
        block, row = core * 4 + row // size, row % size
        here = min(count, size - row, half - at % half)
        found.append((ref, block, row, here))
        at, count = at + here, count - here
    return found


def rows_of(base, half, one, two=None):
    def load(at, count):
        parts = [
            ref[block, row : row + here, :].astype(F32)
            for ref, block, row, here in runs_of(at, count, base, half, one, two)
        ]
        return parts[0] if len(parts) == 1 else jnp.concatenate(parts, axis=0)

    return load


def copy_rows(start, one, out):
    for at in range(0, out.shape[0], 256):
        out[at : at + 256, :] = one[start + at : start + at + 256, :].astype(F32)


def copy_columns(start, one, out):
    for at in range(0, out.shape[1], 256):
        out[:, at : at + 256] = one[start + at : start + at + 256, :].astype(F32)


def place_rows(start, base, half, one, two, out):
    at = 0
    for ref, block, row, here in runs_of(start, out.shape[0], base, half, one, two):
        out[at : at + here, :] = ref[block, row : row + here, :].astype(F32)
        at += here


def place_columns(start, base, half, one, two, out):
    for lane in range(0, out.shape[1], 256):
        at = 0
        for ref, block, row, here in runs_of(start + lane, 256, base, half, one, two):
            out[at : at + here, lane : lane + 256] = ref[block, row : row + here, :].astype(F32)
            at += here


def place_fast(inner, half, start, one, two, *outs):
    load = rows_of(0, half, one, two)
    unpack_fast(1, inner, load, outs)
    unpack_fast(0, inner, lambda at, count: load(start + at, count), outs)


def assemble_norms(inner, *refs):
    sums, (gs, bs, gf, bf) = refs[:-4], refs[-4:]
    lanes = lax.broadcasted_iota(jnp.int32, (8, LANES), 1) >> (inner.bit_length() - 1)
    for n in range(2):
        slow, fast = sums[7 * n : 7 * n + 4], sums[7 * n + 4 : 7 * n + 7]
        for row, gslow, gfast in ((1, gs, gf), (0, bs, bf)):
            at = 0
            for part in slow:
                gslow[n : n + 1, at : at + part.shape[1]] = part[row : row + 1, :]
                at += part.shape[1]
            one, two, three = [jnp.broadcast_to(part[row : row + 1, :], (8, LANES)) for part in fast]
            three = pltpu.roll(three, 2 * inner, 1)
            head = jnp.where(lanes == 0, one, jnp.where(lanes == 1, two, three))
            gfast[n : n + 1, 0:LANES] = head[0:1]
            gfast[n : n + 1, LANES : LANES + 2 * inner] = three[0:1, 0 : 2 * inner]


def on_device(
    x_slow,
    x_fast,
    w_lateral,
    w_slow_time,
    w_slow_space,
    w_slow_point,
    w_fast_time,
    w_fast_space,
    w_fast_point,
    gain_slow,
    bias_slow,
    gain_fast,
    bias_fast,
    clip_size,
    cot_slow,
    cot_fast,
):
    frames, fast_frames = x_slow.shape[0], x_fast.shape[0]
    group = fast_frames // frames
    rows, cols = x_slow.shape[3], x_slow.shape[4]
    spots = rows * cols
    wide, fwide = x_slow.shape[5], x_fast.shape[5]
    lat = w_lateral.shape[3]
    width = w_slow_space.shape[3]
    inner = w_fast_space.shape[3]
    packs = group * fwide
    both = lat + LANES
    m = Masks(spots, cols)
    devices = lax.axis_size("path") * lax.axis_size("rows")
    path = lax.axis_index("path")
    ext = spots + 2 * cols
    lo1, lo2, lo3 = lat, lat + width, lat + 2 * width
    every = slice(None)

    def part(fn, *static):
        return functools.partial(fn, *static)

    xs = x_slow.reshape(frames, spots, wide)
    xf = x_fast.reshape(fast_frames, spots, fwide)
    cs = cot_slow.reshape(frames, spots, wide)
    cf = cot_fast.reshape(fast_frames, spots, fwide)
    wft = jnp.swapaxes(w_fast_time, 2, 3)
    wfs_raw = w_fast_space.reshape(2, 9, inner, inner)
    wsp = w_slow_space.reshape(2, 3, 3 * width, width)

    def packed(value):
        return jnp.concatenate(
            [value[:, 0:inner]] * group + [value[:, inner : 2 * inner]] * group + [value[:, 2 * inner :]],
            axis=1,
        )

    xf_edge = swap_path(jnp.where(path > 0, xf[:2], xf[-2:]))
    xs_edge = swap_path(jnp.where(path > 0, xs[0], xs[-1]))

    def payload(k, *sums):
        size = sum(k.temps[s[1]].shape[1] for s in sums)
        out = k.give((devices, 1, size))
        k.step(spread_sums, *sums, out)
        return out

    def row_out(k, z, mk, col0, size):
        out = k.give((frames, cols, size))
        k.step(part(own_row, m, spots, cols, col0, size), z, mk, out)
        return out

    def edge_out(k, z, mk, size, tail=0):
        out = k.give((spots, size), BF16)
        k.step(part(own_edge, m, 0, tail), z, mk, out)
        return out

    def finish(k, **handles):
        got = k.run()
        return {name: got[handle[1]] for name, handle in handles.items()}

    def other_row(value):
        return swap(value, "rows", 1)

    first_flops = 2 * frames * spots * 7 * fwide * both
    k = Stage("entry")
    mk_out = k.give((m.rows, LANES))
    place = jnp.stack([lax.axis_index("rows"), path]).astype(jnp.int32)
    k.step(
        part(make_masks, m, rows, cols, lax.axis_size("path") - 1), k.scalar(place), k.scalar(clip_size), mk_out
    )
    w7_out = k.give((7 * fwide, both), BF16)
    k.step(part(make_w7, lat, group), k.take(w_lateral, 0), k.take(wft, 0), w7_out)
    fw = k.give((fast_frames + 4, spots, fwide), BF16)
    y = k.give((frames, spots, both))
    sy = k.temp((1, 2 * both))
    edge = k.take(xf_edge)
    k.step(
        part(fast_entry, m, frames, group), k.take(xf), edge, edge, mk_out, w7_out, fw, y, sy, flops=first_flops
    )
    pay = payload(k, sy)
    got = finish(
        k, mk=mk_out, w7=w7_out, fw=fw, y=y, pay=pay, ff_row=row_out(k, y, mk_out, lat, LANES),
        edge=edge_out(k, y, mk_out, both),
    )
    mk = got["mk"]
    saved = [{"fw": got["fw"], "y": got["y"], "w7": got["w7"]}, {}]
    st = gather_sums(got["pay"])
    saved[0]["ff_row"] = other_row(got["ff_row"])
    saved[0]["y_edge"] = swap_path(got["edge"])
    mk, wft, gain_fast, bias_fast = lax.optimization_barrier((mk, wft, gain_fast, bias_fast))
    gf, bf = packed(gain_fast), packed(bias_fast)
    k = Stage("prepare")
    w7_out = k.give((7 * fwide, both), BF16)
    k.step(part(make_w7, lat, group), k.take(w_lateral, 1), k.take(wft, 1), w7_out)
    blocks = []
    for n in range(2):
        blocks += [k.give((3, 3 * LANES, LANES), BF16), k.give((LANES, packs), BF16)]
        k.step(part(make_blocks, group), k.take(wfs_raw, n), k.take(w_fast_point, n), *blocks[-2:])
    got = finish(k, w7=w7_out, wfs0=blocks[0], wfp0=blocks[1], wfs1=blocks[2], wfp1=blocks[3])
    saved[1]["w7"] = got["w7"]
    wfs, wfp = [got["wfs0"], got["wfs1"]], [got["wfp0"], got["wfp1"]]
    k = Stage("slow_partial")
    xm = k.give((frames + 2, spots, wide), BF16)
    fpart = k.give((frames, spots, width))
    edge = k.take(xs_edge)
    k.step(
        part(slow_partial, m, frames),
        k.take(xs), edge, edge, k.take(mk), k.take(w_slow_time, 0, every, slice(0, wide)), xm, fpart,
        flops=2 * frames * spots * 3 * wide * width,
    )
    got = finish(k, sw=xm, fpart=fpart)
    saved[0]["sw"] = got["sw"]
    fpart_in = got["fpart"]

    for n in range(2):
        v = saved[n]
        k = Stage("join")
        mk_in, gs, bs = k.take(mk), k.take(gain_slow), k.take(bias_slow)
        st_in = k.take(st)
        names = {}
        if n == 0:
            fpart = k.take(fpart_in)
        else:
            fpart = k.temp((frames, spots, width))
            n3, next_sw = k.give((2, wide)), k.give((frames + 2, spots, wide), BF16)
            names.update(sw=next_sw, n3=n3)
            k.step(part(keep_norm, 2 * both, wide, m.slow), st_in, mk_in, n3)
            spans = [m.prev] + [m.main] * frames + [m.next]
            for f in range(frames + 2):
                k.step(
                    part(slow_next, 0, lo3, spans[f]),
                    k.take(saved[0]["third"], f), k.take(saved[0]["sw"], f), k.peek(n3), gs, bs, mk_in,
                    k.piece(next_sw, f),
                )
            k.step(
                part(time_partial, frames),
                k.peek(next_sw), k.take(w_slow_time, 1, every, slice(0, wide)), fpart,
                flops=2 * frames * spots * 3 * wide * width,
            )
        y_in, edge = k.take(v["y"]), k.take(v["y_edge"])
        jl = k.give((frames, spots, lat), BF16)
        first = k.give((frames, spots, width))
        nl = k.give((2, lat))
        s_first, s_fs = k.temp((1, 2 * width)), k.temp((1, 2 * LANES))
        k.step(
            part(lat_join, m, n, frames, lat),
            st_in, y_in, edge, edge, fpart, k.take(w_slow_time, n, every, slice(wide, wide + lat)), gs, bs, mk_in,
            jl, first, s_first, nl, k.temp((frames + 2, spots, lat), BF16),
            flops=2 * frames * spots * 3 * lat * width,
        )
        fa1 = k.give((frames, ext, LANES), BF16)
        fs = k.give((frames, spots, LANES))
        nf1 = k.give((2, LANES))
        k.step(
            part(space_forward, m, n, frames, cols, 0, 2 * lat, LANES, lat, True, m.fast),
            st_in, y_in, k.take(v["ff_row"]), k.take(wfs[n]), k.take(gf), k.take(bf), mk_in,
            fa1, fs, s_fs, nf1, k.temp((frames, ext, 3 * LANES), BF16),
            flops=2 * frames * spots * 9 * LANES * LANES,
        )
        pay = payload(k, s_first, s_fs)
        got = finish(
            k, jl=jl, first=first, nl=nl, fa1=fa1, fs=fs, nf1=nf1, pay=pay,
            first_row=row_out(k, first, mk_in, 0, width), fs_row=row_out(k, fs, mk_in, 0, LANES),
            first_edge=edge_out(k, first, mk_in, width), **names,
        )
        st = gather_sums(got["pay"])
        for name in ("jl", "first", "nl", "fa1", "fs", "nf1"):
            v[name] = got[name]
        if n == 1:
            saved[1]["sw"], saved[0]["n3"] = got["sw"], got["n3"]
        first_row = other_row(got["first_row"])
        st, v["fs_row"], v["first_edge"] = lax.optimization_barrier(
            (st, other_row(got["fs_row"]), swap_path(got["first_edge"]))
        )
        k = Stage("space")
        mk_in, st_in = k.take(mk), k.take(st)
        a1 = k.give((frames, ext, width), BF16)
        second = k.give((frames, spots, width))
        n1 = k.give((2, width))
        s_second, s_ft = k.temp((1, 2 * width)), k.temp((1, 2 * LANES))
        k.step(
            part(space_forward, m, n, frames, cols, lo1, 0, width, 0, False, m.slow),
            st_in, k.take(v["first"]), k.take(first_row), k.take(wsp, n), k.take(gain_slow), k.take(bias_slow), mk_in,
            a1, second, s_second, n1, k.temp((frames, ext, 3 * width), BF16),
            flops=2 * frames * spots * 9 * width * width,
        )
        fa2 = k.give((frames, spots, LANES), BF16)
        ft = k.give((frames, spots, packs), BF16)
        nf2 = k.give((2, LANES))
        k.step(
            part(fast_third, m, n, frames, LANES, 2 * width),
            st_in, k.take(v["fs"]), k.take(wfp[n]), k.take(gf), k.take(bf), mk_in, fa2, ft, s_ft, nf2,
            flops=2 * frames * spots * LANES * packs,
        )
        pay = payload(k, s_second, s_ft)
        names = {"second_row": row_out(k, second, mk_in, 0, width)}
        if n == 0:
            names["second_edge"] = edge_out(k, second, mk_in, width)
            names["ft_edge"] = edge_out(k, ft, mk_in, 2 * fwide, (group - 2) * fwide)
        got = finish(k, a1=a1, second=second, n1=n1, fa2=fa2, ft=ft, nf2=nf2, pay=pay, **names)
        st = gather_sums(got["pay"])
        for name in ("a1", "second", "n1", "fa2", "ft", "nf2"):
            v[name] = got[name]
        st, v["second_row"] = lax.optimization_barrier((st, other_row(got["second_row"])))
        halo = 1 - n
        edges = []
        k = Stage("third")
        if n == 0:
            ft_edge = k.take(swap_path(got["ft_edge"]))
            edges = [k.take(swap_path(got["second_edge"]))] * 2
        mk_in, st_in = k.take(mk), k.take(st)
        a2 = k.give((frames, spots, width), BF16)
        third = k.give((frames + 2 * halo, spots, wide), BF16)
        n2 = k.give((2, width))
        nf3 = k.give((2, LANES))
        s_third = k.temp((1, 2 * wide))
        names = {}
        if n == 0:
            names.update(
                fw=k.give((fast_frames + 4, spots, fwide), BF16),
                y=k.give((frames, spots, both)),
            )
            s_fast = k.temp((1, 2 * both))
            k.step(
                part(fast_next, m, n, frames, group, 2 * LANES, 2 * width),
                st_in, k.take(v["ft"]), ft_edge, ft_edge, k.take(v["fw"]), k.take(saved[1]["w7"]),
                k.take(gf), k.take(bf), mk_in, names["fw"], names["y"], s_fast, nf3,
                flops=first_flops,
            )
        else:
            names.update(out_fast=k.give((fast_frames, spots, fwide)), pre_f=k.give((fast_frames, spots, fwide), BF16))
            s_fast = k.temp((1, 2 * LANES))
            k.step(
                part(fast_last, m, n, frames, group, 2 * LANES, 2 * width),
                st_in, k.take(v["ft"]), k.take(v["fw"], slice(2, 2 + fast_frames)), k.take(cf), k.take(gf), k.take(bf), mk_in,
                names["out_fast"], names["pre_f"], s_fast, nf3,
            )
        aw = k.temp((frames + 2 * halo, spots, width), BF16)
        k.step(
            part(slow_acts, m, n, frames, lo2, halo),
            st_in, k.take(v["second"]), *edges, k.take(gain_slow), k.take(bias_slow), mk_in, a2, n2, aw,
        )
        for at in range(0, wide, 256):
            lanes = slice(at, at + 256)
            k.step(
                part(slow_third, frames, halo, at),
                aw, k.take(w_slow_point, n, every, lanes), k.piece(third, every, every, lanes), s_third,
                flops=2 * frames * spots * width * 256,
            )
        if n == 0:
            pay = payload(k, s_fast, s_third)
            names["ff_row"] = row_out(k, names["y"], mk_in, lat, LANES)
            names["y_edge"] = edge_out(k, names["y"], mk_in, both)
        else:
            pay = payload(k, s_third, s_fast)
        got = finish(k, a2=a2, third=third, n2=n2, nf3=nf3, pay=pay, **names)
        st = gather_sums(got["pay"])
        for name in ("a2", "third", "n2", "nf3"):
            v[name] = got[name]
        if n == 0:
            saved[1].update(
                fw=got["fw"], y=got["y"], ff_row=other_row(got["ff_row"]), y_edge=swap_path(got["y_edge"])
            )
        else:
            out_fast, pre_f = got["out_fast"], got["pre_f"]

    def third_back(k, n, at, st_in, mk_in, pre):
        v = saved[n]
        d3, e2 = k.give((frames, spots, wide), BF16), k.give((frames, spots, width))
        s, gb = k.temp((1, 2 * width)), k.give((2, wide))
        gs = k.take(gain_slow)
        k.step(part(keep_sums, at, wide), st_in, gb)
        for t in range(frames):
            k.step(
                part(slow_third_grad, m, n, lo3),
                k.take(pre, t), k.take(v["third"], t + 1 - n), k.take(v["n3"]), k.peek(gb), gs, mk_in,
                k.piece(d3, t),
            )
        k.step(
            part(slow_third_back, m, n, frames, lo2),
            k.peek(d3), k.take(v["second"]), k.take(v["n2"]), k.take(w_slow_point, n), gs, k.take(bias_slow), mk_in,
            e2, s, flops=2 * frames * spots * width * wide,
        )
        return dict(d3=d3, e2=e2, gb3=gb), s

    def fast_back3(k, n, at, st_in, mk_in, pre):
        v = saved[n]
        d3, e2 = k.give((frames, spots, packs), BF16), k.give((frames, spots, LANES))
        s, gb = k.temp((1, 2 * LANES)), k.give((2, LANES))
        k.step(
            part(fast_third_back, m, n, frames, group, 2 * LANES, LANES, at),
            st_in, k.take(pre), k.take(v["ft"]), k.take(v["nf3"]), k.take(v["fs"]), k.take(v["nf2"]),
            k.take(wfp[n]), k.take(gf), k.take(bf), mk_in, d3, e2, s, gb,
            flops=2 * frames * spots * LANES * packs,
        )
        return dict(d3f=d3, ef2=e2, gbf3=gb), s

    def second_back(k, n, at, st_in, mk_in, e2, e2_row):
        v = saved[n]
        d2, e1 = k.give((frames, spots, width), BF16), k.give((frames, spots, width))
        s, gb = k.temp((1, 2 * width)), k.give((2, width))
        k.step(
            part(space_back, m, n, frames, cols, lo2, lo1, at, width, 0, False, m.slow),
            st_in, k.take(e2), k.take(e2_row), k.take(v["second"]), k.take(v["second_row"]), k.take(v["n2"]),
            k.take(v["first"]), k.take(v["n1"]), k.take(wsp, n), k.take(gain_slow), k.take(bias_slow), mk_in,
            d2, e1, s, gb, k.temp((frames, ext, 3 * width), BF16),
            flops=2 * frames * spots * 9 * width * width,
        )
        return dict(d2=d2, e1=e1, gb2=gb), s

    def fast_back2(k, n, at, st_in, mk_in, ef2, ef2_row):
        v = saved[n]
        d2, e1 = k.give((frames, spots, LANES), BF16), k.give((frames, spots, LANES))
        s, gb = k.temp((1, 2 * LANES)), k.give((2, LANES))
        k.step(
            part(space_back, m, n, frames, cols, LANES, 0, at, LANES, lat, True, m.fast),
            st_in, k.take(ef2), k.take(ef2_row), k.take(v["fs"]), k.take(v["fs_row"]), k.take(v["nf2"]),
            k.take(v["y"]), k.take(v["nf1"]), k.take(wfs[n]), k.take(gf), k.take(bf), mk_in,
            d2, e1, s, gb, k.temp((frames, ext, 3 * LANES), BF16),
            flops=2 * frames * spots * 9 * LANES * LANES,
        )
        return dict(d2f=d2, ef1=e1, gbf2=gb), s

    def first_back(k, n, st_in, mk_in, e1, e1_edge):
        v = saved[n]
        dw, el = k.give((frames + 2, spots, width), BF16), k.give((frames, spots, lat))
        s, gb = k.temp((1, 2 * lat)), k.give((2, width))
        edge, zedge = k.take(e1_edge), k.take(v["first_edge"])
        k.step(
            part(slow_first_back, m, n, frames, lo1, 0),
            st_in, k.take(e1), edge, edge, k.take(v["first"]), zedge, zedge, k.take(v["n1"]),
            k.take(w_slow_time, n, every, slice(wide, wide + lat)), k.take(v["y"]), k.take(v["nl"]),
            k.take(gain_slow), k.take(bias_slow), mk_in, dw, el, s, gb, flops=2 * frames * spots * 3 * lat * width,
        )
        return dict(dw=dw, el=el, gb1=gb), s

    def fast_back1(k, n, st1, at1, stl, atl, mk_in, el, el_edge, ef1, ef1_edge):
        v = saved[n]
        dl, df = k.give((frames, spots, lat), BF16), k.give((frames, spots, LANES), BF16)
        beside = [k.give((spots, lat), BF16), k.give((spots, LANES), BF16), k.give((spots, LANES), BF16)]
        gbl, gb1 = k.give((2, lat)), k.give((2, LANES))
        edge, yedge = k.take(ef1_edge), k.take(v["y_edge"])
        k.step(
            part(fast_first_back, m, n, frames, 0, at1, atl),
            st1, stl, k.take(el), k.take(el_edge), k.take(ef1), edge, edge, k.take(v["y"]), yedge, yedge,
            k.take(v["nl"]), k.take(v["nf1"]), k.take(gain_slow), k.take(gf), mk_in, dl, df, *beside, gbl, gb1,
        )
        return dict(dl=dl, df=df, dln=beside[0], dfp=beside[1], dfn=beside[2], gbl=gbl, gbf1=gb1)

    def weights_point(n, d3):
        k = Stage("point_weights")
        out = k.give((wide // 256, width, 256), BF16)
        k.step(point_weights, k.take(saved[n]["a2"]), k.take(d3), out, flops=2 * frames * spots * width * wide)
        return k.run()[0].reshape(-1, 256)

    def weights_space(n, d2):
        k = Stage("space_weights")
        out = k.give((3, 3 * width, width), BF16)
        k.step(
            part(space_weights, cols), k.take(saved[n]["a1"]), k.take(d2), out,
            k.temp((frames, ext, 3 * width), BF16), flops=2 * frames * spots * 9 * width * width,
        )
        return k.run()[0].reshape(-1, 256)

    def weights_time(n, dw):
        k = Stage("time_weights")
        out = k.give((3, wide + lat, width), BF16)
        k.step(
            part(time_weights, 1), k.take(saved[n]["sw"]), k.take(saved[n]["jl"]), k.take(dw), out,
            flops=2 * frames * spots * 3 * (wide + lat) * width,
        )
        return k.run()[0].reshape(-1, 256)

    def weights_fast(n, dl, df, d2, d3):
        v = saved[n]
        k = Stage("fast_weights")
        out = k.give((7 * LANES - LANES, 2 * LANES), BF16)
        k.step(
            part(fast_weights, group, cols, lat),
            k.take(v["fw"]), k.take(dl), k.take(df), k.take(v["fa1"]), k.take(d2), k.take(v["fa2"]), k.take(d3),
            out, k.temp((frames, ext, 3 * LANES), BF16), flops=first_flops,
        )
        return k.run()[0]

    b1, b0 = {}, {}
    k = Stage("last")
    mk_in, st_in = k.take(mk), k.take(st)
    out_slow, pre = k.give((frames, spots, wide)), k.give((frames, spots, wide), BF16)
    n3 = k.give((2, wide))
    s_pre, one, two = k.temp((1, 2 * wide)), k.temp((8, wide)), k.temp((8, wide))
    k.step(part(keep_norm, 0, wide, m.slow), st_in, mk_in, n3)
    k.step(clear, one, two)
    for t in range(frames):
        k.step(
            part(slow_last, m, 1, lo3),
            k.take(saved[1]["third"], t), k.take(saved[1]["sw"], t + 1), k.take(cs, t), k.peek(n3),
            k.take(gain_slow), k.take(bias_slow), mk_in, k.piece(out_slow, t), k.piece(pre, t), one, two,
        )
    k.step(close_sums, one, two, s_pre)
    names, s_ef2 = fast_back3(k, 1, 2 * wide, st_in, mk_in, pre_f)
    pay = payload(k, s_pre, s_ef2)
    ef2_row = row_out(k, names["ef2"], mk_in, 0, LANES)
    b1 = finish(k, out_slow=out_slow, pre=pre, n3=n3, pay=pay, ef2_row=ef2_row, **names)
    saved[1]["n3"] = b1["n3"]
    out_slow = b1["out_slow"]
    st = gather_sums(b1["pay"])

    k = Stage("back_third")
    ef2_row = other_row(b1["ef2_row"])
    mk_in, st_in = k.take(mk), k.take(st)
    names, s_e2 = third_back(k, 1, 0, st_in, mk_in, b1["pre"])
    more, s_ef1 = fast_back2(k, 1, 2 * wide, st_in, mk_in, b1["ef2"], ef2_row)
    pay = payload(k, s_e2, s_ef1)
    e2_row, ef1_edge = row_out(k, names["e2"], mk_in, 0, width), edge_out(k, more["ef1"], mk_in, LANES)
    b1.update(finish(k, pay=pay, e2_row=e2_row, ef1_edge=ef1_edge, **names, **more))
    st = st_ef1 = gather_sums(b1["pay"])
    e2_row = other_row(b1["e2_row"])
    st, ef1_edge = lax.optimization_barrier((st, swap_path(b1["ef1_edge"])))
    point1 = weights_point(1, b1["d3"])

    k = Stage("back_space")
    mk_in, st_in = k.take(mk), k.take(st)
    names, s_e1 = second_back(k, 1, 0, st_in, mk_in, b1["e2"], e2_row)
    pay = payload(k, s_e1)
    e1_edge = edge_out(k, names["e1"], mk_in, width)
    b1.update(finish(k, pay=pay, e1_edge=e1_edge, **names))
    st = gather_sums(b1["pay"])
    e1_edge = swap_path(b1["e1_edge"])
    space1 = weights_space(1, b1["d2"])

    k = Stage("back_first")
    mk_in, st_in = k.take(mk), k.take(st)
    names, s_el = first_back(k, 1, st_in, mk_in, b1["e1"], e1_edge)
    names["down"], s_down = k.give((frames, spots, wide), BF16), k.temp((1, 2 * wide))
    for at in range(0, wide, 256):
        lanes = slice(at, at + 256)
        k.step(
            part(slow_input_back, m, 1, frames, lo3, at),
            k.peek(names["dw"]), k.take(w_slow_time, 1, every, lanes), k.take(b1["pre"], every, every, lanes),
            k.take(saved[0]["sw"], slice(1, 1 + frames), every, lanes),
            k.take(saved[0]["third"], slice(1, 1 + frames), every, lanes),
            k.take(saved[0]["n3"]), k.take(gain_slow), k.take(bias_slow), mk_in,
            k.piece(names["down"], every, every, lanes), s_down,
            flops=2 * frames * spots * 3 * 256 * width,
        )
    pay = payload(k, s_el, s_down)
    el_edge = edge_out(k, names["el"], mk_in, lat)
    b1.update(finish(k, pay=pay, el_edge=el_edge, **names))
    st = gather_sums(b1["pay"])
    el_edge = swap_path(b1["el_edge"])
    time1 = weights_time(1, b1["dw"])
    sizes1 = [point1.shape[0], space1.shape[0], time1.shape[0]]
    ones = jnp.concatenate([point1, space1, time1], axis=0)
    st, ones, el_edge = lax.optimization_barrier((st, ones, el_edge))
    ones = lax.psum(ones, AXES)

    GRADS = ("dl", "df", "dln", "dfp", "dfn")
    SUMS = ("gbl", "gb1", "gb2", "gb3", "gbf1", "gbf2", "gbf3")
    steps = exchange_steps()
    core, across, down = steps[:3]
    seen = {}

    def block_zero(st=st, el_edge=el_edge, ef1_edge=ef1_edge, b1=b1, b0=b0):
        b1, b0 = dict(b1), dict(b0)
        k = Stage("back_third")
        mk_in, st_in = k.take(mk), k.take(st)
        names, s_e2 = third_back(k, 0, 2 * lat, st_in, mk_in, b1["down"])
        more = fast_back1(
            k, 1, k.take(st_ef1), 2 * width, st_in, 0, mk_in, b1["el"], el_edge, b1["ef1"], ef1_edge
        )
        inner_grads = [more[name] for name in ("dl", "df", "dln", "dfp", "dfn")]
        more["downf"], s_pf = k.give((fast_frames, spots, fwide), BF16), k.temp((1, 2 * LANES))
        k.step(
            part(fast_input_back, m, 1, frames, group, 2 * LANES, False),
            *inner_grads, k.take(saved[1]["w7"]), k.take(pre_f), k.take(saved[0]["fw"]), k.take(saved[0]["ft"]),
            k.take(saved[0]["nf3"]), k.take(gf), k.take(bf), mk_in, more["downf"], s_pf,
            k.temp((fast_frames + 4, spots, fwide)), flops=first_flops,
        )
        pay = payload(k, s_e2, s_pf)
        e2_row = row_out(k, names["e2"], mk_in, 0, width)
        got = finish(k, pay=pay, e2_row=e2_row, **names, **more)
        for name in more:
            b1[name] = got[name]
        b0.update({name: got[name] for name in names})
        st = gather_sums(got["pay"])
        e2_row = other_row(got["e2_row"])
        point0 = weights_point(0, b0["d3"])
        fast_1 = weights_fast(1, b1["dl"], b1["df"], b1["d2f"], b1["d3f"])

        k = Stage("back_space")
        mk_in, st_in = k.take(mk), k.take(st)
        names, s_e1 = second_back(k, 0, 0, st_in, mk_in, b0["e2"], e2_row)
        more, s_ef2 = fast_back3(k, 0, 2 * width, st_in, mk_in, b1["downf"])
        pay = payload(k, s_e1, s_ef2)
        e1_edge, ef2_row = edge_out(k, names["e1"], mk_in, width), row_out(k, more["ef2"], mk_in, 0, LANES)
        b0.update(finish(k, pay=pay, e1_edge=e1_edge, ef2_row=ef2_row, **names, **more))
        st = gather_sums(b0["pay"])
        e1_edge, ef2_row = swap_path(b0["e1_edge"]), other_row(b0["ef2_row"])
        space0 = weights_space(0, b0["d2"])

        k = Stage("back_first")
        mk_in, st_in = k.take(mk), k.take(st)
        names, s_el = first_back(k, 0, st_in, mk_in, b0["e1"], e1_edge)
        more, s_ef1 = fast_back2(k, 0, 2 * width, st_in, mk_in, b0["ef2"], ef2_row)
        pay = payload(k, s_el, s_ef1)
        el_edge, ef1_edge = edge_out(k, names["el"], mk_in, lat), edge_out(k, more["ef1"], mk_in, LANES)
        b0.update(finish(k, pay=pay, el_edge=el_edge, ef1_edge=ef1_edge, **names, **more))
        st = gather_sums(b0["pay"])
        el_edge, ef1_edge = swap_path(b0["el_edge"]), swap_path(b0["ef1_edge"])
        time0 = weights_time(0, b0["dw"])
        k = Stage("back_fast")
        mk_in, st_in = k.take(mk), k.take(st)
        more = fast_back1(k, 0, st_in, 2 * lat, st_in, 0, mk_in, b0["el"], el_edge, b0["ef1"], ef1_edge)
        v = saved[0]
        rest = k.give((6 * LANES, 2 * LANES), BF16)
        k.step(
            part(fast_weights, group, cols, lat),
            k.take(v["fw"]), more["dl"], more["df"], k.take(v["fa1"]), k.take(b0["d2f"]), k.take(v["fa2"]),
            k.take(b0["d3f"]), rest, k.temp((frames, ext, 3 * LANES), BF16), flops=first_flops,
        )
        got = finish(k, rest=rest, **more)
        b0.update(got)
        pieces = [fast_1, point0, space0, time0, got["rest"]]
        seen["rows"] = [sum(piece.shape[0] for piece in pieces[:at]) for at in range(6)]
        value = halve(jnp.concatenate(pieces, axis=0), *core)
        k = Stage("slow_input")
        gx_slow = k.give((frames, spots, wide))
        k.step(
            part(slow_input_last, m, frames),
            k.take(b0["dw"]), k.take(w_slow_time, 0, every, slice(0, wide)), k.take(b1["down"]), k.take(mk), gx_slow,
            flops=2 * frames * spots * 3 * wide * width,
        )
        (gx_slow,) = k.run()
        k = Stage("fast_input")
        gx_fast = k.give((fast_frames, spots, fwide))
        k.step(
            part(fast_input_back, m, 0, frames, group, 2 * LANES, True),
            *[k.take(b0[name]) for name in GRADS], k.take(saved[0]["w7"]), k.take(b1["downf"]), k.take(mk), gx_fast,
            k.temp((fast_frames + 4, spots, fwide)), flops=first_flops,
        )
        (gx_fast,) = k.run()
        pair, gx_slow = lax.optimization_barrier((halve_both(*parted(value), across, down), gx_slow))
        pair, gx_fast = lax.optimization_barrier((halve_both(*pair, down, across), gx_fast))
        value = jnp.concatenate(pair, axis=0)
        for step in steps[3:]:
            value = halve(value, *step)
        value = value.astype(BF16)
        for step in reversed(steps[3:]):
            value = double(value, *step)
        sums = [b0[name] for name in SUMS] + [b1[name] for name in ("gbl", "gbf1")]
        return (value, gx_slow, gx_fast, *sums)

    like = jax.eval_shape(block_zero)
    got = lax.cond(
        clip_size[0, 0] > 0, block_zero, lambda: tuple(jnp.zeros(o.shape, o.dtype) for o in like)
    )
    value, gx_slow, gx_fast = got[:3]
    b0 = dict(zip(SUMS, got[3:10]))
    b1["gbl"], b1["gbf1"] = got[10:12]

    time_rows, space_rows = 3 * (wide + lat), 9 * width
    k = Stage("assemble_one")
    ones_in = k.take(ones)
    gtime, gspace = k.give((2, time_rows, width), F32, 1), k.give((2, space_rows, width), F32, 1)
    gpoint = k.give((2, width, wide), F32, 1)
    k.step(part(copy_rows, sizes1[0] + sizes1[1]), ones_in, gtime)
    k.step(part(copy_rows, sizes1[0]), ones_in, gspace)
    k.step(part(copy_columns, 0), ones_in, gpoint)
    half_done = k.run()

    def spread_both(one, two, tied=()):
        one, two = [one, swap(one, *down)], [two, swap(two, *across)]
        one, two, tied = lax.optimization_barrier((one, two, tied))
        one, two = [jnp.stack(pair) for pair in (one, two)]
        one, two = [one, swap(one, *across)], [two, swap(two, *down)]
        return [pair + [swap(half, *core) for half in pair] for pair in (one, two)], tied

    (one, two), half_done = spread_both(*parted(value), half_done)

    core_bit = lax.axis_index("rows") % 2
    down_bit = (lax.axis_index("rows") // 2) % 2

    k = Stage("assemble")
    flip_one = k.scalar((core_bit * 4 + path * 2 + down_bit).astype(jnp.int32).reshape(1))
    flip_two = k.scalar((core_bit * 4 + down_bit * 2 + path).astype(jnp.int32).reshape(1))
    one_in = k.take_blocks(one, flip_one, every)
    two_in = k.take_blocks(two, flip_two, every)
    starts = seen["rows"]
    half_rows = starts[5] // 2
    gtime = k.give((2, time_rows, width), F32, 0, half_done[0])
    k.step(part(place_rows, starts[3], 0, half_rows), one_in, two_in, gtime)
    gspace = k.give((2, space_rows, width), F32, 0, half_done[1])
    k.step(part(place_rows, starts[2], 0, half_rows), one_in, two_in, gspace)
    gpoint = k.give((2, width, wide), F32, 0, half_done[2])
    k.step(part(place_columns, starts[1], 0, half_rows), one_in, two_in, gpoint)
    fast_outs = [
        k.give((2, 5 * fwide, lat)), k.give((2, 3, inner, fwide)), k.give((2, 9, inner, inner)),
        k.give((2, inner, fwide)),
    ]
    k.step(part(place_fast, inner, half_rows, starts[4]), one_in, two_in, *fast_outs)
    sums = [k.take(b[name]) for b in (b0, b1) for name in ("gbl", "gb1", "gb2", "gb3", "gbf1", "gbf2", "gbf3")]
    norm_outs = [k.give(like.shape) for like in (gain_slow, bias_slow, gain_fast, bias_fast)]
    k.step(part(assemble_norms, inner), *sums, *norm_outs)
    got = k.run()
    glat, gft, gfs, gfp = [got[h[1]] for h in fast_outs]

    return (
        out_slow.reshape(x_slow.shape),
        out_fast.reshape(x_fast.shape),
        gx_slow.reshape(x_slow.shape),
        gx_fast.reshape(x_fast.shape),
        glat.reshape(w_lateral.shape),
        got[gtime[1]].reshape(w_slow_time.shape),
        got[gspace[1]].reshape(w_slow_space.shape),
        got[gpoint[1]],
        jnp.swapaxes(gft, 2, 3),
        gfs.reshape(w_fast_space.shape),
        gfp,
        *[got[h[1]] for h in norm_outs],
    )


def solution(mesh):
    spread = P("path", None, "rows", None, None, None)
    return jax.shard_map(
        on_device,
        mesh=mesh,
        in_specs=(spread, spread) + (P(),) * 12 + (spread, spread),
        out_specs=(spread,) * 4 + (P(),) * 11,
        check_vma=False,
    )
```

```python
import functools

import jax
import jax.numpy as jnp
import numpy as np
from jax import lax
from jax.experimental import pallas as pl
from jax.experimental.pallas import tpu as pltpu
from jax.sharding import PartitionSpec as P

TS = 8
TF = 32
F32 = jnp.float32
BF16 = jnp.bfloat16
EPSILON = 1e-05
LANES = 128
AXES = ("path", "rows")
VMEM_LIMIT = 56 * 2**20


def swap(value, axis, stride):
    pairs = [(source, source ^ stride) for source in range(lax.axis_size(axis))]
    return lax.ppermute(value, axis, pairs)


def gather_sums(spread):
    return lax.all_to_all(spread, AXES, 0, 0, tiled=True)


def swap_path(value):
    assert lax.axis_size("path") == 2
    return lax.ppermute(value, "path", [(0, 1), (1, 0)])


def exchange_steps():
    steps = [("rows", 1), ("path", 1)]
    stride = 2
    while stride < lax.axis_size("rows"):
        steps.append(("rows", stride))
        stride *= 2
    return steps


def halve(value, axis, stride):
    size = value.shape[0] // 2
    upper = (lax.axis_index(axis) // stride) % 2
    keep = lax.dynamic_slice_in_dim(value, upper * size, size, 0)
    give = lax.dynamic_slice_in_dim(value, (1 - upper) * size, size, 0)
    return keep.astype(F32) + swap(give.astype(BF16), axis, stride).astype(F32)


def double(value, axis, stride):
    upper = (lax.axis_index(axis) // stride) % 2
    got = swap(value, axis, stride)
    return jnp.concatenate(
        [jnp.where(upper == 0, value, got), jnp.where(upper == 0, got, value)], axis=0
    )


def halve_both(one, two, first, second):
    return halve(one, *first), halve(two, *second)


def parted(value):
    size = value.shape[0] // 2
    return value[:size], value[size:]


class Stage:
    def __init__(self, name):
        self.name = name
        self.arrays, self.views, self.scalars, self.pairs = [], [], [], []
        self.outs, self.temps, self.steps = [], [], []
        self.entries, self.ontos = [], []
        self.flops = 0

    def take(self, array, *view):
        for at, known in enumerate(self.arrays):
            if known is array:
                break
        else:
            at = len(self.arrays)
            self.arrays.append(array)
        for k, (other, seen) in enumerate(self.views):
            if other == at and seen == view:
                return ("in", k)
        self.views.append((at, view))
        return ("in", len(self.views) - 1)

    def take_blocks(self, values, flip, rows):
        self.pairs.append(([self.take(value, slice(None), rows) for value in values], flip))
        return ("pair", len(self.pairs) - 1)

    def scalar(self, array):
        self.scalars.append(array)
        return ("scalar", len(self.scalars) - 1)

    def give(self, dims, dtype=F32, at=None, onto=None):
        self.outs.append(jax.ShapeDtypeStruct(tuple(dims), dtype))
        self.entries.append(at)
        self.ontos.append(onto)
        return ("out", len(self.outs) - 1)

    def piece(self, handle, *index):
        return ("piece", (handle[1], index))

    def peek(self, handle):
        return ("peek", handle[1])

    def temp(self, dims, dtype=F32):
        self.temps.append(pltpu.VMEM(tuple(dims), dtype))
        return ("temp", len(self.temps) - 1)

    def step(self, fn, *handles, flops=0):
        self.flops += flops
        self.steps.append((fn, handles))

    def sem(self, view, block):
        return 8 * view + block

    def view_shape(self, view):
        at, index = view
        return np.broadcast_to(np.zeros((), np.int8), self.arrays[at].shape)[index].shape

    def run(self):
        arrays, views, outs, steps, pairs = self.arrays, self.views, self.outs, self.steps, self.pairs
        order, home = [], {}
        for k, (members, flip) in enumerate(pairs):
            for j, member in enumerate(members):
                home[member[1]] = (k, j, flip)
        under = [onto for onto in self.ontos if onto is not None]

        def need(handle):
            if handle[0] == "in":
                return [handle[1]]
            return [part[1] for part in pairs[handle[1]][0]] if handle[0] == "pair" else []

        for _, handles in steps:
            for handle in handles:
                for k in need(handle):
                    if k not in order:
                        order.append(k)

        def body(*refs):
            refs = list(refs)

            def cut(count):
                taken = refs[:count]
                del refs[:count]
                return taken

            scalars, hbm_in = cut(len(self.scalars)), cut(len(arrays))
            cut(len(under))
            hbm_out = cut(len(outs))
            alone = [k for k in range(len(views)) if k not in home]
            held = dict(zip(alone, cut(len(alone))))
            joint, made, temps, (sems,) = cut(len(pairs)), cut(len(outs)), cut(len(self.temps)), refs
            copies = {}
            for k in order:
                at, index = views[k]
                src = hbm_in[at].at[index] if index else hbm_in[at]
                if k in home:
                    pair, second, flip = home[k]
                    count = self.view_shape(views[k])[0]
                    copies[k] = []
                    for block in range(count):
                        to = (second * count + block) ^ scalars[flip[1]][0]
                        copies[k].append(
                            pltpu.make_async_copy(src.at[block], joint[pair].at[to], sems.at[self.sem(k, block)])
                        )
                else:
                    copies[k] = [pltpu.make_async_copy(src, held[k], sems.at[self.sem(k, 0)])]
                for copy in copies[k]:
                    copy.start()
            waited, sent = set(), {}
            for fn, handles in steps:
                given = []
                for handle in handles:
                    for k in need(handle):
                        if k not in waited:
                            for copy in copies[k]:
                                copy.wait()
                            waited.add(k)
                    if handle[0] == "piece":
                        given.append(made[handle[1][0]].at[handle[1][1]])
                        continue
                    place = {"in": held, "pair": joint, "out": made, "peek": made, "temp": temps, "scalar": scalars}
                    given.append(place[handle[0]][handle[1]])
                fn(*given)
                for kind, k in handles:
                    if kind == "out" and k not in sent:
                        to = hbm_out[k] if self.entries[k] is None else hbm_out[k].at[self.entries[k]]
                        sent[k] = [pltpu.make_async_copy(made[k], to, sems.at[8 * (len(views) + k)])]
                        sent[k][0].start()
                    elif kind == "piece":
                        k, index = k
                        done = sent.setdefault(k, [])
                        sem = sems.at[8 * (len(views) + k) + len(done)]
                        done.append(pltpu.make_async_copy(made[k].at[index], hbm_out[k].at[index], sem))
                        done[-1].start()
            for done in sent.values():
                for copy in done:
                    copy.wait()

        moved = sum(a.size * a.dtype.itemsize for a in outs)
        for view in views:
            moved += int(np.prod(self.view_shape(view))) * arrays[view[0]].dtype.itemsize
        scratch = [
            pltpu.VMEM(self.view_shape(view), arrays[view[0]].dtype) for k, view in enumerate(views) if k not in home
        ]
        for members, _ in pairs:
            size = self.view_shape(views[members[0][1]])
            scratch.append(
                pltpu.VMEM((len(members) * size[0],) + size[1:], arrays[views[members[0][1]][0]].dtype)
            )
        scratch += [
            pltpu.VMEM(o.shape if at is None else o.shape[1:], o.dtype) for o, at in zip(outs, self.entries)
        ]
        aliases = {}
        for k, onto in enumerate(self.ontos):
            if onto is not None:
                aliases[len(self.scalars) + len(arrays) + len(aliases)] = k
        scratch += self.temps + [pltpu.SemaphoreType.DMA((8 * (len(views) + len(outs)),))]
        return pl.pallas_call(
            body,
            out_shape=tuple(outs),
            in_specs=[pl.BlockSpec(memory_space=pltpu.SMEM) for _ in self.scalars]
            + [pl.BlockSpec(memory_space=pl.ANY) for _ in arrays + under],
            out_specs=tuple(pl.BlockSpec(memory_space=pl.ANY) for _ in outs),
            scratch_shapes=scratch,
            input_output_aliases=aliases,
            compiler_params=pltpu.CompilerParams(vmem_limit_bytes=VMEM_LIMIT),
            cost_estimate=pl.CostEstimate(flops=self.flops, bytes_accessed=moved, transcendentals=0),
            name=self.name,
        )(*self.scalars, *arrays, *under)


class Masks:
    def __init__(self, spots, cols):
        self.main = (0, spots)
        self.ext = (spots, 2 * spots + 2 * cols)
        self.prev = (2 * spots + 2 * cols, 3 * spots + 2 * cols)
        self.next = (3 * spots + 2 * cols, 4 * spots + 2 * cols)
        self.slow = (4 * spots + 2 * cols, 4 * spots + 2 * cols + 8)
        self.fast = (4 * spots + 2 * cols + 8, 4 * spots + 2 * cols + 16)
        self.half = (4 * spots + 2 * cols + 16, 4 * spots + 2 * cols + 24)
        self.path = (4 * spots + 2 * cols + 24, 4 * spots + 2 * cols + 32)
        self.rows = 4 * spots + 2 * cols + 32


def make_masks(m, rows, cols, last, place, clips, mk):
    half = place[0] % 2
    path = place[1]
    side = clips[0, place[0] // 2]
    area = 0
    for k in range(clips.shape[1]):
        area = area + clips[0, k] * clips[0, k]
    shift = cols.bit_length() - 1

    def inside(first, count):
        at = lax.broadcasted_iota(jnp.int32, (count * cols, LANES), 0)
        line = half * rows + first + (at >> shift)
        spot = at & (cols - 1)
        good = (line >= 0) & (line < 2 * rows) & (line < side) & (spot < side)
        return jnp.where(good, 1.0, 0.0)

    main = inside(0, rows)
    mk[m.main[0] : m.main[1], :] = main
    mk[m.ext[0] : m.ext[1], :] = inside(-1, rows + 2)
    mk[m.prev[0] : m.prev[1], :] = main * jnp.where(path > 0, 1.0, 0.0)
    mk[m.next[0] : m.next[1], :] = main * jnp.where(path < last, 1.0, 0.0)

    def fill(span, value):
        mk[span[0] : span[1], :] = jnp.full((8, LANES), value, F32)

    fill(m.slow, TS * area.astype(F32))
    fill(m.fast, TF * area.astype(F32))
    fill(m.half, half.astype(F32))
    fill(m.path, path.astype(F32))


def own_row(m, spots, cols, col0, width, z, mk, row):
    for t in range(z.shape[0]):
        lower = mk[m.half[0] : m.half[0] + 1, :] > 0.5
        for lane in range(0, width, LANES):
            at = col0 + lane
            row[t, :, lane : lane + LANES] = jnp.where(
                lower, z[t, 0:cols, at : at + LANES], z[t, spots - cols : spots, at : at + LANES]
            )


def own_edge(m, lead, tail, z, mk, edge):
    frames = z.shape[0]
    second = mk[m.path[0] : m.path[0] + 1, :] > 0.5
    for lane in range(0, edge.shape[1], LANES):
        edge[:, lane : lane + LANES] = jnp.where(
            second,
            z[0, :, lead + lane : lead + lane + LANES],
            z[frames - 1, :, tail + lane : tail + lane + LANES],
        ).astype(edge.dtype)


def spread_sums(*refs):
    parts, out = refs[:-1], refs[-1]
    row = jnp.concatenate([part[...] for part in parts], axis=1)
    out[...] = jnp.broadcast_to(row[None], out.shape)


def make_w7(lat, group, wl, wf, w7):
    inner = wf.shape[1]
    w7[...] = jnp.zeros(w7.shape, BF16)
    for j in range(wl.shape[0]):
        w7[j * LANES : (j + 1) * LANES, 0:lat] = wl[j]
    at = lax.broadcasted_iota(jnp.int32, (inner, LANES), 0)
    lane = lax.broadcasted_iota(jnp.int32, (inner, LANES), 1)
    places = [jnp.where(lane == at + inner * k, 1.0, 0.0).astype(BF16) for k in range(group)]
    for f in range(1, group + 3):
        used = [k for k in range(group) if 0 <= f - 1 - k < 3]
        got = None
        for k in used:
            more = dot_tn(wf[f - 1 - k], places[k])
            got = more if got is None else got + more
        w7[f * LANES : (f + 1) * LANES, lat : lat + LANES] = got.astype(BF16)


def make_blocks(group, ws, wp, wfs, wfp):
    inner = wp.shape[0]
    at = lax.broadcasted_iota(jnp.int32, (inner, LANES), 0)
    lane = lax.broadcasted_iota(jnp.int32, (inner, LANES), 1)
    tile = jnp.where((lane & (inner - 1)) == at, 1.0, 0.0).astype(BF16)
    shift = inner.bit_length() - 1
    for tap in range(ws.shape[0]):
        got = dot(ws[tap], tile)
        for k in range(group):
            kept = jnp.where((lane >> shift) == k, got, 0.0).astype(BF16)
            row = (tap % 3) * LANES + k * inner
            wfs[tap // 3, row : row + inner, :] = kept
    wfp[...] = jnp.zeros(wfp.shape, BF16)
    for k in range(group):
        wfp[k * inner : (k + 1) * inner, k * LANES : (k + 1) * LANES] = wp[...]


def widen(rows, width):
    return jnp.concatenate([rows] * (width // LANES), axis=1)


def sublane_sums(value):
    return jnp.sum(value.reshape(value.shape[0] // 8, 8, value.shape[1]), axis=0)


def row_sum(value):
    return jnp.sum(value, axis=0, keepdims=True)


def fold_packed(row):
    full = jnp.broadcast_to(row, (8, LANES))
    full = full + pltpu.roll(full, 64, 1)
    full = full + pltpu.roll(full, 32, 1)
    return full[0:1]


def totals(st, lo, width, packed=False):
    first = jnp.sum(st[:, :, lo : lo + width], axis=0)
    second = jnp.sum(st[:, :, lo + width : lo + 2 * width], axis=0)
    if packed:
        return fold_packed(first), fold_packed(second)
    return first, second


def norm_rows(st, lo, width, count, packed=False):
    first, second = totals(st, lo, width, packed)
    mean = first / count
    return mean, lax.rsqrt(second / count - mean * mean + EPSILON)


def keep_norm(lo, width, span, st, mk, nz):
    mean, rstd = norm_rows(st, lo, width, widen(mk[span[0] : span[0] + 1, :], width))
    nz[0:1, :] = mean
    nz[1:2, :] = rstd


def keep_sums(lo, width, st, gb):
    one, two = totals(st, lo, width)
    gb[0:1, :] = one
    gb[1:2, :] = two


def clear(*refs):
    for ref in refs:
        ref[...] = jnp.zeros(ref.shape, F32)


def close_sums(one, two, s):
    s[...] = jnp.concatenate([row_sum(one[...]), row_sum(two[...])], axis=1)


def sigmoid(value):
    return 0.5 * jnp.tanh(0.5 * value) + 0.5


def silu(value):
    return value * sigmoid(value)


def silu_slope(value):
    sigma = sigmoid(value)
    return sigma * (1.0 + value * (1.0 - sigma))


def dot(a, b):
    return jnp.dot(a, b, preferred_element_type=F32)


def dot_nt(a, b):
    return lax.dot_general(a, b, (((1,), (1,)), ((), ())), preferred_element_type=F32)


def dot_tn(a, b):
    return lax.dot_general(a, b, (((0,), (0,)), ((), ())), preferred_element_type=F32)


def flat(value):
    return value.reshape(value.shape[0] * value.shape[1], value.shape[2])


def store_shifts(dst, t, value, cols):
    rows, width = value.shape
    spot = lax.broadcasted_iota(jnp.int32, (rows, width), 0) & (cols - 1)
    left = jnp.where(spot == 0, 0.0, pltpu.roll(value, 1, 0))
    right = jnp.where(spot == cols - 1, 0.0, pltpu.roll(value, rows - 1, 0))
    dst[t, :, 0:width] = left.astype(BF16)
    dst[t, :, width : 2 * width] = value.astype(BF16)
    dst[t, :, 2 * width : 3 * width] = right.astype(BF16)


def taps_of(frames_ref, frames, group):
    return jnp.concatenate(
        [
            jnp.concatenate([frames_ref[group * t + f] for f in range(7)], axis=1)
            for t in range(frames)
        ],
        axis=0,
    )


def entry_sums(y, lat, frames, spots):
    width = y.shape[1]
    one = jnp.zeros((8, width), F32)
    two = jnp.zeros((8, width), F32)
    for t in range(frames):
        part = y[t * spots : (t + 1) * spots]
        one = one + sublane_sums(part)
        two = two + sublane_sums(part * part)
    one = row_sum(one)
    two = row_sum(two)
    return jnp.concatenate([one[:, :lat], two[:, :lat], one[:, lat:], two[:, lat:]], axis=1)


def fast_entry(m, frames, group, x, before, after, mk, w7, fw, y, s):
    spots = x.shape[1]
    count = x.shape[0]

    def put(at, value, span):
        fw[at] = (value.astype(F32) * mk[span[0] : span[1], :]).astype(BF16)

    for k in range(2):
        put(k, before[k], m.prev)
        put(2 + count + k, after[k], m.next)
    for k in range(count):
        put(2 + k, x[k], m.main)
    out = dot(taps_of(fw, frames, group), w7[...])
    for t in range(frames):
        y[t] = out[t * spots : (t + 1) * spots]
    s[...] = entry_sums(out, w7.shape[1] - LANES, frames, spots)


def slow_partial(m, frames, x, before, after, mk, wt, xm, fpart):
    spots, wide = x.shape[1], x.shape[2]
    sources = [(before, m.prev)] + [(x.at[t], m.main) for t in range(frames)] + [(after, m.next)]
    for k, (src, span) in enumerate(sources):
        for lo in range(0, wide, 256):
            mask = widen(mk[span[0] : span[1], :], 256)
            xm[k, :, lo : lo + 256] = (src[:, lo : lo + 256].astype(F32) * mask).astype(BF16)
    out = dot(flat(xm[0:frames]), wt[0, :wide, :])
    for j in range(1, 3):
        out = out + dot(flat(xm[j : j + frames]), wt[j, :wide, :])
    for t in range(frames):
        fpart[t] = out[t * spots : (t + 1) * spots]


def lat_join(m, n, frames, lat, st, y, before, after, fpart, wt, gs, bs, mk, jl, first, s, nl, jw):
    spots = y.shape[1]
    wide = wt.shape[1] - lat
    count = widen(mk[m.slow[0] : m.slow[0] + 1, :], lat)
    mean, rstd = norm_rows(st, 0, lat, count)
    nl[0:1, :] = mean
    nl[1:2, :] = rstd
    scale = rstd * gs[n : n + 1, 0:lat]
    bias = bs[n : n + 1, 0:lat]
    sources = (
        [(before[:, 0:lat], m.prev)]
        + [(y[t, :, 0:lat], m.main) for t in range(frames)]
        + [(after[:, 0:lat], m.next)]
    )
    for k, (value, span) in enumerate(sources):
        mask = widen(mk[span[0] : span[1], :], lat)
        act = (silu((value - mean) * scale + bias) * mask).astype(BF16)
        jw[k] = act
        if 1 <= k <= frames:
            jl[k - 1] = act
    out = flat(fpart[...])
    for j in range(3):
        out = out + dot(flat(jw[j : j + frames]), wt[j, wide:, :])
    one = jnp.zeros((8, out.shape[1]), F32)
    two = jnp.zeros((8, out.shape[1]), F32)
    for t in range(frames):
        part = out[t * spots : (t + 1) * spots]
        first[t] = part
        one = one + sublane_sums(part)
        two = two + sublane_sums(part * part)
    s[...] = jnp.concatenate([row_sum(one), row_sum(two)], axis=1)


def space_forward(
    m, n, frames, cols, lo, at, width, col0, packed, span, st, z, row, w, g, b, mk, aw, out, s, nz, vw
):
    spots = z.shape[1]
    count = widen(mk[span[0] : span[0] + 1, :], width)
    mean, rstd = norm_rows(st, at, width, count, packed)
    nz[0:1, :] = mean
    nz[1:2, :] = rstd
    scale = rstd * g[n : n + 1, lo : lo + width]
    bias = b[n : n + 1, lo : lo + width]
    mask = widen(mk[m.ext[0] : m.ext[1], :], width)
    for t in range(frames):
        value = jnp.concatenate([row[t], z[t, :, col0 : col0 + width], row[t]], axis=0)
        act = silu((value - mean) * scale + bias) * mask
        aw[t] = act.astype(BF16)
        store_shifts(vw, t, act, cols)
    total = dot(flat(vw[:, 0:spots, :]), w[0])
    for i in range(1, 3):
        total = total + dot(flat(vw[:, i * cols : i * cols + spots, :]), w[i])
    mask = widen(mk[m.main[0] : m.main[1], :], width)
    one = jnp.zeros((8, width), F32)
    two = jnp.zeros((8, width), F32)
    for t in range(frames):
        part = total[t * spots : (t + 1) * spots]
        out[t] = part
        part = part * mask
        one = one + sublane_sums(part)
        two = two + sublane_sums(part * part)
    s[...] = jnp.concatenate([row_sum(one), row_sum(two)], axis=1)


def slow_acts(m, n, frames, lo, halo, st, z, *rest):
    if halo:
        before, after, g, b, mk, a2, nz, aw = rest
    else:
        g, b, mk, a2, nz, aw = rest
    width = z.shape[2]
    keep_norm(0, width, m.slow, st, mk, nz)
    mean = nz[0:1, :]
    scale = nz[1:2, :] * g[n : n + 1, lo : lo + width]
    bias = b[n : n + 1, lo : lo + width]
    sources = [(z[t], m.main, t + halo) for t in range(frames)]
    if halo:
        sources += [(before[...], m.prev, 0), (after[...], m.next, frames + 1)]
    for value, span, at in sources:
        mask = widen(mk[span[0] : span[1], :], width)
        act = (silu((value - mean) * scale + bias) * mask).astype(BF16)
        aw[at] = act
        if halo <= at < frames + halo:
            a2[at - halo] = act


def slow_third(frames, halo, at, aw, wp, third, s):
    spots = aw.shape[1]
    wide = s.shape[1] // 2
    out = dot(flat(aw[...]), wp[...])
    one = jnp.zeros((8, 256), F32)
    two = jnp.zeros((8, 256), F32)
    for t in range(frames + 2 * halo):
        part = out[t * spots : (t + 1) * spots]
        third[t] = part.astype(BF16)
        if halo <= t < frames + halo:
            one = one + sublane_sums(part)
            two = two + sublane_sums(part * part)
    s[:, at : at + 256] = row_sum(one)
    s[:, wide + at : wide + at + 256] = row_sum(two)


def fast_third(m, n, frames, lo, at, st, z, wp, g, b, mk, a2, ft, s, nz):
    spots = z.shape[1]
    count = mk[m.fast[0] : m.fast[0] + 1, :]
    mean, rstd = norm_rows(st, at, LANES, count, True)
    nz[0:1, :] = mean
    nz[1:2, :] = rstd
    scale = rstd * g[n : n + 1, lo : lo + LANES]
    bias = b[n : n + 1, lo : lo + LANES]
    mask = mk[m.main[0] : m.main[1], :]
    for t in range(frames):
        a2[t] = (silu((z[t] - mean) * scale + bias) * mask).astype(BF16)
    acts = flat(a2[...])
    one = jnp.zeros((8, LANES), F32)
    two = jnp.zeros((8, LANES), F32)
    out = dot(acts, wp[...])
    for t in range(frames):
        for lane in range(0, wp.shape[1], LANES):
            part = out[t * spots : (t + 1) * spots, lane : lane + LANES]
            ft[t, :, lane : lane + LANES] = part.astype(BF16)
            one = one + sublane_sums(part)
            two = two + sublane_sums(part * part)
    s[...] = jnp.concatenate([row_sum(one), row_sum(two)], axis=1)


def fast_next(m, n, frames, group, lo, at, st, ft, before, after, fw0, w7, g, b, mk, fw1, y, s, nz):
    spots = ft.shape[1]
    count = mk[m.fast[0] : m.fast[0] + 1, :]
    mean, rstd = norm_rows(st, at, LANES, count)
    nz[0:1, :] = mean
    nz[1:2, :] = rstd
    scale = rstd * g[n : n + 1, lo : lo + LANES]
    bias = b[n : n + 1, lo : lo + LANES]
    total = frames * group

    def out_of(k, value, span):
        z = fw0[k].astype(F32) + ((value - mean) * scale + bias)
        return silu(z) * mk[span[0] : span[1], :]

    for k in range(2):
        lane = k * LANES
        fw1[k] = out_of(k, before[:, lane : lane + LANES], m.prev).astype(BF16)
        fw1[2 + total + k] = out_of(2 + total + k, after[:, lane : lane + LANES], m.next).astype(BF16)
    for t in range(frames):
        for f in range(group):
            k = t * group + f
            fw1[2 + k] = out_of(2 + k, ft[t, :, f * LANES : (f + 1) * LANES], m.main).astype(BF16)
    out = dot(taps_of(fw1, frames, group), w7[...])
    for t in range(frames):
        y[t] = out[t * spots : (t + 1) * spots]
    s[...] = entry_sums(out, w7.shape[1] - LANES, frames, spots)


def fast_last(m, n, frames, group, lo, at, st, ft, f1, cot, g, b, mk, out, pre, s, nz):
    count = mk[m.fast[0] : m.fast[0] + 1, :]
    mean, rstd = norm_rows(st, at, LANES, count)
    nz[0:1, :] = mean
    nz[1:2, :] = rstd
    gain = g[n : n + 1, lo : lo + LANES]
    bias = b[n : n + 1, lo : lo + LANES]
    mask = mk[m.main[0] : m.main[1], :]
    one = jnp.zeros((8, LANES), F32)
    two = jnp.zeros((8, LANES), F32)
    for t in range(frames):
        for f in range(group):
            k = t * group + f
            hat = (ft[t, :, f * LANES : (f + 1) * LANES].astype(F32) - mean) * rstd
            z = f1[k].astype(F32) + hat * gain + bias
            sigma = sigmoid(z)
            out[k] = z * sigma * mask
            grad = cot[k].astype(F32) * mask * (sigma * (1.0 + z * (1.0 - sigma)))
            pre[k] = grad.astype(BF16)
            one = one + sublane_sums(grad)
            two = two + sublane_sums(grad * hat)
    s[...] = jnp.concatenate([row_sum(one), row_sum(two)], axis=1)


def chunked(total, step, body, init):
    def turn(i, carry):
        return body(pl.multiple_of(i * step, step), carry)

    return lax.fori_loop(0, total // step, turn, init)


def slow_next(n, lo, span, third, xm, nz, g, b, mk, sw):
    spots, wide = third.shape
    mean = nz[0:1, :]
    scale = nz[1:2, :] * g[n : n + 1, lo : lo + wide]
    bias = b[n : n + 1, lo : lo + wide]

    def turn(at, carry):
        mask = widen(mk[pl.ds(span[0] + at, 16), :], 512)
        for c in range(0, wide, 512):
            z = third[pl.ds(at, 16), c : c + 512].astype(F32)
            z = (z - mean[:, c : c + 512]) * scale[:, c : c + 512] + bias[:, c : c + 512]
            z = xm[pl.ds(at, 16), c : c + 512].astype(F32) + z
            sw[pl.ds(at, 16), c : c + 512] = (silu(z) * mask).astype(BF16)
        return carry

    chunked(spots, 16, turn, 0)


def time_partial(frames, sw, wt, fpart):
    spots = sw.shape[1]
    out = dot(flat(sw[0:frames]), wt[0])
    for j in range(1, 3):
        out = out + dot(flat(sw[j : j + frames]), wt[j])
    for t in range(frames):
        fpart[t] = out[t * spots : (t + 1) * spots]


def slow_last(m, n, lo, third, slow, cot, nz, g, b, mk, out, pre, one, two):
    spots, wide = third.shape
    mean, rstd = nz[0:1, :], nz[1:2, :]
    gain = g[n : n + 1, lo : lo + wide]
    bias = b[n : n + 1, lo : lo + wide]

    def turn(at, sums):
        ones, twos = [], []
        mask = widen(mk[pl.ds(m.main[0] + at, 16), :], 512)
        for c in range(0, wide, 512):
            hat = third[pl.ds(at, 16), c : c + 512].astype(F32)
            hat = (hat - mean[:, c : c + 512]) * rstd[:, c : c + 512]
            z = slow[pl.ds(at, 16), c : c + 512].astype(F32) + hat * gain[:, c : c + 512] + bias[:, c : c + 512]
            sigma = sigmoid(z)
            out[pl.ds(at, 16), c : c + 512] = z * sigma * mask
            grad = cot[pl.ds(at, 16), c : c + 512].astype(F32) * mask
            grad = grad * (sigma * (1.0 + z * (1.0 - sigma)))
            pre[pl.ds(at, 16), c : c + 512] = grad.astype(BF16)
            ones.append(sublane_sums(grad))
            twos.append(sublane_sums(grad * hat))
        return sums[0] + jnp.concatenate(ones, axis=1), sums[1] + jnp.concatenate(twos, axis=1)

    one[...], two[...] = chunked(spots, 16, turn, (one[...], two[...]))


def slow_third_grad(m, n, lo, pre, third, n3, gb, g, mk, d3):
    spots, wide = pre.shape
    count = widen(mk[m.slow[0] : m.slow[0] + 1, :], wide)
    mean, rstd = n3[0:1, :], n3[1:2, :]
    scale = g[n : n + 1, lo : lo + wide] * rstd
    one = gb[0:1, :] / count
    two = gb[1:2, :] / count * rstd

    def turn(i, carry):
        mask = widen(mk[pl.ds(m.main[0] + i, 16), :], 512)
        for c in range(0, wide, 512):
            hat = (third[pl.ds(i, 16), c : c + 512].astype(F32) - mean[:, c : c + 512]) * two[:, c : c + 512]
            grad = pre[pl.ds(i, 16), c : c + 512].astype(F32) - mask * (one[:, c : c + 512] + hat)
            d3[pl.ds(i, 16), c : c + 512] = (scale[:, c : c + 512] * grad).astype(BF16)
        return carry

    chunked(spots, 16, turn, 0)


def slow_third_back(m, n, frames, lo, d3, z, n2, wp, g, b, mk, e2, s):
    spots, width = z.shape[1], z.shape[2]
    out = dot_nt(flat(d3[...]), wp[...])
    gain = g[n : n + 1, lo : lo + width]
    bias = b[n : n + 1, lo : lo + width]
    back_act(m, frames, spots, out, z, 0, n2[0:1, :], n2[1:2, :], gain, bias, mk, e2, s)


def back_act(m, frames, spots, out, z, col0, mean, rstd, gain, bias, mk, e, s):
    width = out.shape[1]
    mask = widen(mk[m.main[0] : m.main[1], :], width)
    one = jnp.zeros((8, width), F32)
    two = jnp.zeros((8, width), F32)
    for t in range(frames):
        hat = (z[t, :, col0 : col0 + width] - mean) * rstd
        grad = out[t * spots : (t + 1) * spots] * mask * silu_slope(hat * gain + bias)
        e[t] = grad
        one = one + sublane_sums(grad)
        two = two + sublane_sums(grad * hat)
    s[...] = jnp.concatenate([row_sum(one), row_sum(two)], axis=1)


def fast_third_back(m, n, frames, group, lo3, lo2, at, st, pre, ft, n3, z, n2, wp, g, b, mk, d3, e2, s, gb):
    spots = z.shape[1]
    count = mk[m.fast[0] : m.fast[0] + 1, :]
    one, two = totals(st, at, LANES)
    gb[0:1, :] = one
    gb[1:2, :] = two
    mean, rstd = n3[0:1, :], n3[1:2, :]
    scale = g[n : n + 1, lo3 : lo3 + LANES] * rstd
    one = one / count
    two = two / count * rstd
    mask = mk[m.main[0] : m.main[1], :]
    for t in range(frames):
        for f in range(group):
            hat = (ft[t, :, f * LANES : (f + 1) * LANES] - mean) * two
            grad = pre[t * group + f] - mask * (one + hat)
            d3[t, :, f * LANES : (f + 1) * LANES] = (scale * grad).astype(BF16)
    out = dot_nt(flat(d3[...]), wp[...])
    mean, rstd = n2[0:1, :], n2[1:2, :]
    gain = g[n : n + 1, lo2 : lo2 + LANES]
    bias = b[n : n + 1, lo2 : lo2 + LANES]
    back_act(m, frames, spots, out, z, 0, mean, rstd, gain, bias, mk, e2, s)


def space_back(
    m, n, frames, cols, lo2, lo1, at, width, col0, packed, span,
    st, e, erow, z, zrow, nz, z1, n1, w, g, b, mk, d2, e1, s, gb, vw,
):
    spots = z.shape[1]
    count = widen(mk[span[0] : span[0] + 1, :], width)
    one, two = totals(st, at, width, packed)
    gb[0:1, :] = one
    gb[1:2, :] = two
    mean, rstd = nz[0:1, :], nz[1:2, :]
    scale = g[n : n + 1, lo2 : lo2 + width] * rstd
    one = one / count
    two = two / count * rstd
    mask = widen(mk[m.ext[0] : m.ext[1], :], width)
    for t in range(frames):
        grad = jnp.concatenate([erow[t], e[t], erow[t]], axis=0)
        value = jnp.concatenate([zrow[t], z[t], zrow[t]], axis=0)
        grad = scale * mask * (grad - (one + (value - mean) * two))
        d2[t] = grad[cols : cols + spots].astype(BF16)
        store_shifts(vw, t, grad.astype(BF16).astype(F32), cols)
    total = None
    for i in range(3):
        rows = (2 - i) * cols
        for j in range(3):
            lane = (2 - j) * width
            part = dot_nt(flat(vw[:, rows : rows + spots, lane : lane + width]), w[i, j * width : (j + 1) * width, :])
            total = part if total is None else total + part
    mean, rstd = n1[0:1, :], n1[1:2, :]
    gain = g[n : n + 1, lo1 : lo1 + width]
    bias = b[n : n + 1, lo1 : lo1 + width]
    back_act(m, frames, spots, total, z1, col0, mean, rstd, gain, bias, mk, e1, s)


def first_taps(frames, dw):
    return [flat(dw[2 - j : 2 - j + frames]) for j in range(3)]


def time_back(taps, wt, lo, size):
    out = dot_nt(taps[0], wt[0, lo : lo + size, :])
    for j in range(1, 3):
        out = out + dot_nt(taps[j], wt[j, lo : lo + size, :])
    return out


def slow_first_back(m, n, frames, lo1, at, st, e, ep, en, z, zp, zn, n1, wt, y, nl, g, b, mk, dw, el, s, gb):
    spots, width = z.shape[1], z.shape[2]
    lat = nl.shape[1]
    wide = wt.shape[1] - lat
    count = widen(mk[m.slow[0] : m.slow[0] + 1, :], width)
    one, two = totals(st, at, width)
    gb[0:1, :] = one
    gb[1:2, :] = two
    mean, rstd = n1[0:1, :], n1[1:2, :]
    scale = g[n : n + 1, lo1 : lo1 + width] * rstd
    one = one / count
    two = two / count * rstd
    sources = (
        [(ep, zp, m.prev)] + [(e.at[t], z.at[t], m.main) for t in range(frames)] + [(en, zn, m.next)]
    )
    for k, (grad, value, span) in enumerate(sources):
        mask = widen(mk[span[0] : span[1], :], width)
        dw[k] = (scale * mask * (grad[...] - (one + (value[...] - mean) * two))).astype(BF16)
    out = time_back(first_taps(frames, dw), wt, wide, lat)
    back_act(
        m, frames, spots, out, y, 0, nl[0:1, :], nl[1:2, :], g[n : n + 1, 0:lat], b[n : n + 1, 0:lat], mk, el, s
    )


def slow_input_last(m, frames, dw, wt, pre, mk, gx):
    spots, wide = pre.shape[1], pre.shape[2]
    taps = first_taps(frames, dw)
    mask = widen(mk[m.main[0] : m.main[1], :], 256)
    for c in range(0, wide, 256):
        out = time_back(taps, wt, c, 256)
        for t in range(frames):
            gx[t, :, c : c + 256] = (out[t * spots : (t + 1) * spots] + pre[t, :, c : c + 256]) * mask


def slow_input_back(m, n, frames, lo, at, dw, wt, pre, xm, third, n3, g, b, mk, pre0, s):
    spots = pre.shape[1]
    wide = s.shape[1] // 2
    mask = widen(mk[m.main[0] : m.main[1], :], 256)
    out = time_back(first_taps(frames, dw), wt, 0, 256)
    mean, rstd = n3[0:1, at : at + 256], n3[1:2, at : at + 256]
    gain = g[n - 1 : n, lo + at : lo + at + 256]
    bias = b[n - 1 : n, lo + at : lo + at + 256]
    one = jnp.zeros((8, 256), F32)
    two = jnp.zeros((8, 256), F32)
    for t in range(frames):
        grad = (out[t * spots : (t + 1) * spots] + pre[t].astype(F32)) * mask
        hat = (third[t].astype(F32) - mean) * rstd
        z0 = xm[t].astype(F32) + hat * gain + bias
        grad = grad * silu_slope(z0)
        pre0[t] = grad.astype(BF16)
        one = one + sublane_sums(grad)
        two = two + sublane_sums(grad * hat)
    s[:, at : at + 256] = row_sum(one)
    s[:, wide + at : wide + at + 256] = row_sum(two)


def fast_first_back(
    m, n, frames, lo1, at1, atl, st1, stl, el, eln, ef, efp, efn, y, yp, yn, nl, n1, gs, g, mk,
    dl, dfw, dln, dfp, dfn, gbl, gb1,
):
    lat = nl.shape[1]
    count = widen(mk[m.slow[0] : m.slow[0] + 1, :], lat)
    one, two = totals(stl, atl, lat)
    gbl[0:1, :] = one
    gbl[1:2, :] = two
    mean, rstd = nl[0:1, :], nl[1:2, :]
    scale = gs[n : n + 1, 0:lat] * rstd
    one = one / count
    two = two / count * rstd

    def lat_grad(grad, value, span):
        mask = widen(mk[span[0] : span[1], :], lat)
        return (scale * mask * (grad - (one + (value - mean) * two))).astype(BF16)

    for t in range(frames):
        dl[t] = lat_grad(el[t], y[t, :, 0:lat], m.main)
    dln[...] = lat_grad(eln[...], yn[:, 0:lat], m.next)
    fcount = mk[m.fast[0] : m.fast[0] + 1, :]
    fone, ftwo = totals(st1, at1, LANES, True)
    gb1[0:1, :] = fone
    gb1[1:2, :] = ftwo
    fmean, frstd = n1[0:1, :], n1[1:2, :]
    fscale = g[n : n + 1, lo1 : lo1 + LANES] * frstd
    fone = fone / fcount
    ftwo = ftwo / fcount * frstd

    def first_grad(grad, value, span):
        mask = mk[span[0] : span[1], :]
        return (fscale * mask * (grad - (fone + (value - fmean) * ftwo))).astype(BF16)

    for t in range(frames):
        dfw[t] = first_grad(ef[t], y[t, :, lat:], m.main)
    dfp[...] = first_grad(efp[...], yp[:, lat:], m.prev)
    dfn[...] = first_grad(efn[...], yn[:, lat:], m.next)


def fast_input_back(m, n, frames, group, lo3, last, dl, dfw, dln, dfp, dfn, w7, pre, *rest):
    if last:
        mk, gx, buf = rest
    else:
        fw0, ft, n3, g, b, mk, pre0, s, buf = rest
    spots, lat = dl.shape[1], dl.shape[2]
    both = jnp.concatenate([flat(dl[...]), flat(dfw[...])], axis=1)
    buf[...] = jnp.zeros(buf.shape, F32)
    out = dot_nt(both, w7[...])
    for t in range(frames):
        for f in range(7):
            k = group * t + f
            buf[k] = buf[k] + out[t * spots : (t + 1) * spots, f * LANES : (f + 1) * LANES]
    buf[2] = buf[2] + dot_nt(dfp[...], w7[6 * LANES : 7 * LANES, lat:])
    after = dot_nt(jnp.concatenate([dln[...], dfn[...]], axis=1), w7[0 : 2 * LANES, :])
    total = frames * group
    for f in range(2):
        buf[total + f] = buf[total + f] + after[:, f * LANES : (f + 1) * LANES]
    mask = mk[m.main[0] : m.main[1], :]
    if last:
        for k in range(total):
            gx[k] = (pre[k] + buf[2 + k]) * mask
        return
    mean, rstd = n3[0:1, :], n3[1:2, :]
    gain = g[n - 1 : n, lo3 : lo3 + LANES]
    bias = b[n - 1 : n, lo3 : lo3 + LANES]
    one = jnp.zeros((8, LANES), F32)
    two = jnp.zeros((8, LANES), F32)
    for k in range(total):
        t, f = k // group, k % group
        hat = (ft[t, :, f * LANES : (f + 1) * LANES] - mean) * rstd
        z0 = fw0[2 + k].astype(F32) + hat * gain + bias
        grad = (pre[k] + buf[2 + k]) * mask * silu_slope(z0)
        pre0[k] = grad.astype(BF16)
        one = one + sublane_sums(grad)
        two = two + sublane_sums(grad * hat)
    s[...] = jnp.concatenate([row_sum(one), row_sum(two)], axis=1)


def point_weights(a2, d3, out):
    acts = flat(a2[...])
    for k in range(out.shape[0]):
        out[k] = dot_tn(acts, flat(d3[:, :, k * 256 : (k + 1) * 256])).astype(BF16)


def space_weights(cols, aw, d2, out, vw):
    frames, spots, width = d2.shape
    for t in range(frames):
        store_shifts(vw, t, aw[t].astype(F32), cols)
    grads = flat(d2[...])
    for i in range(3):
        out[i] = dot_tn(flat(vw[:, i * cols : i * cols + spots, :]), grads).astype(BF16)


def time_weights(skip, slow, jl, dw, out):
    frames, spots, width = jl.shape
    wide = slow.shape[2]
    grads = jnp.concatenate([flat(dw[2 - j : 2 - j + frames]) for j in range(3)], axis=1)
    for c in range(0, wide + jl.shape[2], 256):
        if c < wide:
            acts = flat(slow[skip : skip + frames, :, c : c + 256])
        else:
            acts = flat(jl[:, :, c - wide : c - wide + 256])
        got = dot_tn(acts, grads)
        for j in range(3):
            out[j, c : c + 256, :] = got[:, j * width : (j + 1) * width].astype(BF16)


def group_blocks(value, group):
    size = LANES // group
    rows = lax.broadcasted_iota(jnp.int32, (LANES, LANES), 0) >> (size.bit_length() - 1)
    lanes = lax.broadcasted_iota(jnp.int32, (LANES, LANES), 1) >> (size.bit_length() - 1)
    kept = jnp.where(rows == lanes, value, 0.0)
    kept = kept + pltpu.roll(kept, 64, 1)
    kept = kept + pltpu.roll(kept, 32, 1)
    total = kept[0:size]
    for k in range(1, group):
        total = total + kept[k * size : (k + 1) * size]
    return total


def at_lanes(blocks):
    lanes = lax.broadcasted_iota(jnp.int32, blocks[0].shape, 1) >> 5
    out = jnp.zeros(blocks[0].shape, F32)
    for k, block in enumerate(blocks):
        out = jnp.where(lanes == k, block, out)
    return out


def fast_weights(group, cols, lat, fw, dl, df, fa1, d2, fa2, d3, out, vw):
    frames, spots, _ = dl.shape
    size = LANES // group
    both = jnp.concatenate([flat(dl[...]), flat(df[...])], axis=1)
    taps = [[None] * group for _ in range(3)]
    for f in range(7):
        acts = jnp.concatenate([fw[group * t + f] for t in range(frames)], axis=0)
        got = dot_tn(acts, both)
        if f < 5:
            out[f * LANES : (f + 1) * LANES, :] = got[:, :lat].astype(BF16)
        for k in range(group):
            if 0 <= f - k - 1 < 3:
                taps[f - k - 1][k] = got[:, lat:]
    lanes = lax.broadcasted_iota(jnp.int32, (LANES, LANES), 1) >> (size.bit_length() - 1)
    tap_sums = []
    for j in range(3):
        kept = jnp.zeros((LANES, LANES), F32)
        for k in range(group):
            kept = jnp.where(lanes == k, taps[j][k], kept)
        kept = kept + pltpu.roll(kept, 64, 1)
        tap_sums.append(kept + pltpu.roll(kept, 32, 1))
    low = 5 * LANES
    out[low : low + LANES, 0:LANES] = at_lanes(tap_sums).T.astype(BF16)
    for t in range(frames):
        store_shifts(vw, t, fa1[t].astype(F32), cols)
    grads = flat(d2[...])
    for i in range(3):
        got = dot_tn(flat(vw[:, i * cols : i * cols + spots, :]), grads)
        blocks = [group_blocks(got[j * LANES : (j + 1) * LANES], group) for j in range(3)]
        out[low + size * i : low + size * (i + 1), LANES : 2 * LANES] = at_lanes(blocks).astype(BF16)
    acts = flat(fa2[...])
    total = jnp.zeros((size, LANES), F32)
    for k in range(group):
        got = dot_tn(acts, flat(d3[:, :, k * LANES : (k + 1) * LANES]))
        total = total + got[k * size : (k + 1) * size]
    out[low + 3 * size : low + 4 * size, LANES : 2 * LANES] = total.astype(BF16)


def unpack_fast(n, inner, load, outs):
    glat, gft, gfs, gfp = outs
    low = glat.shape[1]
    for at in range(0, low, inner):
        glat[n, at : at + inner, :] = load(at, inner)
    for i in range(4):
        got = load(low + inner * i, inner)
        if i < 3:
            gft[n, i] = got[:, 0:LANES]
            for j in range(3):
                moved = got[:, LANES:] if j == 0 else pltpu.roll(got[:, LANES:], LANES - inner * j, 1)
                gfs[n, 3 * i + j] = moved[:, 0:inner]
        else:
            gfp[n] = got[:, LANES:]


def runs_of(at, count, base, half, one, two):
    found = []
    while count:
        core, row = at // half, base + at % half
        ref, size = one, one.shape[1]
        if row >= 4 * size:
            ref, row = two, row - 4 * size
            size = two.shape[1]
        block, row = core * 4 + row // size, row % size
        here = min(count, size - row, half - at % half)
        found.append((ref, block, row, here))
        at, count = at + here, count - here
    return found


def rows_of(base, half, one, two=None):
    def load(at, count):
        parts = [
            ref[block, row : row + here, :].astype(F32)
            for ref, block, row, here in runs_of(at, count, base, half, one, two)
        ]
        return parts[0] if len(parts) == 1 else jnp.concatenate(parts, axis=0)

    return load


def copy_rows(start, one, out):
    for at in range(0, out.shape[0], 256):
        out[at : at + 256, :] = one[start + at : start + at + 256, :].astype(F32)


def copy_columns(start, one, out):
    for at in range(0, out.shape[1], 256):
        out[:, at : at + 256] = one[start + at : start + at + 256, :].astype(F32)


def place_rows(start, base, half, one, two, out):
    at = 0
    for ref, block, row, here in runs_of(start, out.shape[0], base, half, one, two):
        out[at : at + here, :] = ref[block, row : row + here, :].astype(F32)
        at += here


def place_columns(start, base, half, one, two, out):
    for lane in range(0, out.shape[1], 256):
        at = 0
        for ref, block, row, here in runs_of(start + lane, 256, base, half, one, two):
            out[at : at + here, lane : lane + 256] = ref[block, row : row + here, :].astype(F32)
            at += here


def place_fast(inner, half_mid, half_late, start, mid_one, mid_two, one, two, *outs):
    unpack_fast(1, inner, rows_of(0, half_mid, mid_one, mid_two), outs)
    load = rows_of(0, half_late, one, two)
    unpack_fast(0, inner, lambda at, count: load(start + at, count), outs)


def assemble_norms(inner, *refs):
    sums, (gs, bs, gf, bf) = refs[:-4], refs[-4:]
    lanes = lax.broadcasted_iota(jnp.int32, (8, LANES), 1) >> (inner.bit_length() - 1)
    for n in range(2):
        slow, fast = sums[7 * n : 7 * n + 4], sums[7 * n + 4 : 7 * n + 7]
        for row, gslow, gfast in ((1, gs, gf), (0, bs, bf)):
            at = 0
            for part in slow:
                gslow[n : n + 1, at : at + part.shape[1]] = part[row : row + 1, :]
                at += part.shape[1]
            one, two, three = [jnp.broadcast_to(part[row : row + 1, :], (8, LANES)) for part in fast]
            three = pltpu.roll(three, 2 * inner, 1)
            head = jnp.where(lanes == 0, one, jnp.where(lanes == 1, two, three))
            gfast[n : n + 1, 0:LANES] = head[0:1]
            gfast[n : n + 1, LANES : LANES + 2 * inner] = three[0:1, 0 : 2 * inner]


def on_device(
    x_slow,
    x_fast,
    w_lateral,
    w_slow_time,
    w_slow_space,
    w_slow_point,
    w_fast_time,
    w_fast_space,
    w_fast_point,
    gain_slow,
    bias_slow,
    gain_fast,
    bias_fast,
    clip_size,
    cot_slow,
    cot_fast,
):
    frames, fast_frames = x_slow.shape[0], x_fast.shape[0]
    group = fast_frames // frames
    rows, cols = x_slow.shape[3], x_slow.shape[4]
    spots = rows * cols
    wide, fwide = x_slow.shape[5], x_fast.shape[5]
    lat = w_lateral.shape[3]
    width = w_slow_space.shape[3]
    inner = w_fast_space.shape[3]
    packs = group * fwide
    both = lat + LANES
    m = Masks(spots, cols)
    devices = lax.axis_size("path") * lax.axis_size("rows")
    path = lax.axis_index("path")
    ext = spots + 2 * cols
    lo1, lo2, lo3 = lat, lat + width, lat + 2 * width
    every = slice(None)

    def part(fn, *static):
        return functools.partial(fn, *static)

    xs = x_slow.reshape(frames, spots, wide)
    xf = x_fast.reshape(fast_frames, spots, fwide)
    cs = cot_slow.reshape(frames, spots, wide)
    cf = cot_fast.reshape(fast_frames, spots, fwide)
    wft = jnp.swapaxes(w_fast_time, 2, 3)
    wfs_raw = w_fast_space.reshape(2, 9, inner, inner)
    wsp = w_slow_space.reshape(2, 3, 3 * width, width)

    def packed(value):
        return jnp.concatenate(
            [value[:, 0:inner]] * group + [value[:, inner : 2 * inner]] * group + [value[:, 2 * inner :]],
            axis=1,
        )

    xf_edge = swap_path(jnp.where(path > 0, xf[:2], xf[-2:]))
    xs_edge = swap_path(jnp.where(path > 0, xs[0], xs[-1]))

    def payload(k, *sums):
        size = sum(k.temps[s[1]].shape[1] for s in sums)
        out = k.give((devices, 1, size))
        k.step(spread_sums, *sums, out)
        return out

    def row_out(k, z, mk, col0, size):
        out = k.give((frames, cols, size))
        k.step(part(own_row, m, spots, cols, col0, size), z, mk, out)
        return out

    def edge_out(k, z, mk, size, tail=0):
        out = k.give((spots, size), BF16)
        k.step(part(own_edge, m, 0, tail), z, mk, out)
        return out

    def finish(k, **handles):
        got = k.run()
        return {name: got[handle[1]] for name, handle in handles.items()}

    def other_row(value):
        return swap(value, "rows", 1)

    first_flops = 2 * frames * spots * 7 * fwide * both
    k = Stage("entry")
    mk_out = k.give((m.rows, LANES))
    place = jnp.stack([lax.axis_index("rows"), path]).astype(jnp.int32)
    k.step(
        part(make_masks, m, rows, cols, lax.axis_size("path") - 1), k.scalar(place), k.scalar(clip_size), mk_out
    )
    w7_out = k.give((7 * fwide, both), BF16)
    k.step(part(make_w7, lat, group), k.take(w_lateral, 0), k.take(wft, 0), w7_out)
    fw = k.give((fast_frames + 4, spots, fwide), BF16)
    y = k.give((frames, spots, both))
    sy = k.temp((1, 2 * both))
    edge = k.take(xf_edge)
    k.step(
        part(fast_entry, m, frames, group), k.take(xf), edge, edge, mk_out, w7_out, fw, y, sy, flops=first_flops
    )
    pay = payload(k, sy)
    got = finish(
        k, mk=mk_out, w7=w7_out, fw=fw, y=y, pay=pay, ff_row=row_out(k, y, mk_out, lat, LANES),
        edge=edge_out(k, y, mk_out, both),
    )
    mk = got["mk"]
    saved = [{"fw": got["fw"], "y": got["y"], "w7": got["w7"]}, {}]
    st = gather_sums(got["pay"])
    saved[0]["ff_row"] = other_row(got["ff_row"])
    saved[0]["y_edge"] = swap_path(got["edge"])
    mk, wft, gain_fast, bias_fast = lax.optimization_barrier((mk, wft, gain_fast, bias_fast))
    gf, bf = packed(gain_fast), packed(bias_fast)
    k = Stage("prepare")
    w7_out = k.give((7 * fwide, both), BF16)
    k.step(part(make_w7, lat, group), k.take(w_lateral, 1), k.take(wft, 1), w7_out)
    blocks = []
    for n in range(2):
        blocks += [k.give((3, 3 * LANES, LANES), BF16), k.give((LANES, packs), BF16)]
        k.step(part(make_blocks, group), k.take(wfs_raw, n), k.take(w_fast_point, n), *blocks[-2:])
    got = finish(k, w7=w7_out, wfs0=blocks[0], wfp0=blocks[1], wfs1=blocks[2], wfp1=blocks[3])
    saved[1]["w7"] = got["w7"]
    wfs, wfp = [got["wfs0"], got["wfs1"]], [got["wfp0"], got["wfp1"]]
    k = Stage("slow_partial")
    xm = k.give((frames + 2, spots, wide), BF16)
    fpart = k.give((frames, spots, width))
    edge = k.take(xs_edge)
    k.step(
        part(slow_partial, m, frames),
        k.take(xs), edge, edge, k.take(mk), k.take(w_slow_time, 0, every, slice(0, wide)), xm, fpart,
        flops=2 * frames * spots * 3 * wide * width,
    )
    got = finish(k, sw=xm, fpart=fpart)
    saved[0]["sw"] = got["sw"]
    fpart_in = got["fpart"]

    for n in range(2):
        v = saved[n]
        k = Stage("join")
        mk_in, gs, bs = k.take(mk), k.take(gain_slow), k.take(bias_slow)
        st_in = k.take(st)
        names = {}
        if n == 0:
            fpart = k.take(fpart_in)
        else:
            fpart = k.temp((frames, spots, width))
            n3, next_sw = k.give((2, wide)), k.give((frames + 2, spots, wide), BF16)
            names.update(sw=next_sw, n3=n3)
            k.step(part(keep_norm, 2 * both, wide, m.slow), st_in, mk_in, n3)
            spans = [m.prev] + [m.main] * frames + [m.next]
            for f in range(frames + 2):
                k.step(
                    part(slow_next, 0, lo3, spans[f]),
                    k.take(saved[0]["third"], f), k.take(saved[0]["sw"], f), k.peek(n3), gs, bs, mk_in,
                    k.piece(next_sw, f),
                )
            k.step(
                part(time_partial, frames),
                k.peek(next_sw), k.take(w_slow_time, 1, every, slice(0, wide)), fpart,
                flops=2 * frames * spots * 3 * wide * width,
            )
        y_in, edge = k.take(v["y"]), k.take(v["y_edge"])
        jl = k.give((frames, spots, lat), BF16)
        first = k.give((frames, spots, width))
        nl = k.give((2, lat))
        s_first, s_fs = k.temp((1, 2 * width)), k.temp((1, 2 * LANES))
        k.step(
            part(lat_join, m, n, frames, lat),
            st_in, y_in, edge, edge, fpart, k.take(w_slow_time, n, every, slice(wide, wide + lat)), gs, bs, mk_in,
            jl, first, s_first, nl, k.temp((frames + 2, spots, lat), BF16),
            flops=2 * frames * spots * 3 * lat * width,
        )
        fa1 = k.give((frames, ext, LANES), BF16)
        fs = k.give((frames, spots, LANES))
        nf1 = k.give((2, LANES))
        k.step(
            part(space_forward, m, n, frames, cols, 0, 2 * lat, LANES, lat, True, m.fast),
            st_in, y_in, k.take(v["ff_row"]), k.take(wfs[n]), k.take(gf), k.take(bf), mk_in,
            fa1, fs, s_fs, nf1, k.temp((frames, ext, 3 * LANES), BF16),
            flops=2 * frames * spots * 9 * LANES * LANES,
        )
        pay = payload(k, s_first, s_fs)
        got = finish(
            k, jl=jl, first=first, nl=nl, fa1=fa1, fs=fs, nf1=nf1, pay=pay,
            first_row=row_out(k, first, mk_in, 0, width), fs_row=row_out(k, fs, mk_in, 0, LANES),
            first_edge=edge_out(k, first, mk_in, width), **names,
        )
        st = gather_sums(got["pay"])
        for name in ("jl", "first", "nl", "fa1", "fs", "nf1"):
            v[name] = got[name]
        if n == 1:
            saved[1]["sw"], saved[0]["n3"] = got["sw"], got["n3"]
        first_row = other_row(got["first_row"])
        st, v["fs_row"], v["first_edge"] = lax.optimization_barrier(
            (st, other_row(got["fs_row"]), swap_path(got["first_edge"]))
        )
        k = Stage("space")
        mk_in, st_in = k.take(mk), k.take(st)
        a1 = k.give((frames, ext, width), BF16)
        second = k.give((frames, spots, width))
        n1 = k.give((2, width))
        s_second, s_ft = k.temp((1, 2 * width)), k.temp((1, 2 * LANES))
        k.step(
            part(space_forward, m, n, frames, cols, lo1, 0, width, 0, False, m.slow),
            st_in, k.take(v["first"]), k.take(first_row), k.take(wsp, n), k.take(gain_slow), k.take(bias_slow), mk_in,
            a1, second, s_second, n1, k.temp((frames, ext, 3 * width), BF16),
            flops=2 * frames * spots * 9 * width * width,
        )
        fa2 = k.give((frames, spots, LANES), BF16)
        ft = k.give((frames, spots, packs), BF16)
        nf2 = k.give((2, LANES))
        k.step(
            part(fast_third, m, n, frames, LANES, 2 * width),
            st_in, k.take(v["fs"]), k.take(wfp[n]), k.take(gf), k.take(bf), mk_in, fa2, ft, s_ft, nf2,
            flops=2 * frames * spots * LANES * packs,
        )
        pay = payload(k, s_second, s_ft)
        names = {"second_row": row_out(k, second, mk_in, 0, width)}
        if n == 0:
            names["second_edge"] = edge_out(k, second, mk_in, width)
            names["ft_edge"] = edge_out(k, ft, mk_in, 2 * fwide, (group - 2) * fwide)
        got = finish(k, a1=a1, second=second, n1=n1, fa2=fa2, ft=ft, nf2=nf2, pay=pay, **names)
        st = gather_sums(got["pay"])
        for name in ("a1", "second", "n1", "fa2", "ft", "nf2"):
            v[name] = got[name]
        st, v["second_row"] = lax.optimization_barrier((st, other_row(got["second_row"])))
        halo = 1 - n
        edges = []
        k = Stage("third")
        if n == 0:
            ft_edge = k.take(swap_path(got["ft_edge"]))
            edges = [k.take(swap_path(got["second_edge"]))] * 2
        mk_in, st_in = k.take(mk), k.take(st)
        a2 = k.give((frames, spots, width), BF16)
        third = k.give((frames + 2 * halo, spots, wide), BF16)
        n2 = k.give((2, width))
        nf3 = k.give((2, LANES))
        s_third = k.temp((1, 2 * wide))
        names = {}
        if n == 0:
            names.update(
                fw=k.give((fast_frames + 4, spots, fwide), BF16),
                y=k.give((frames, spots, both)),
            )
            s_fast = k.temp((1, 2 * both))
            k.step(
                part(fast_next, m, n, frames, group, 2 * LANES, 2 * width),
                st_in, k.take(v["ft"]), ft_edge, ft_edge, k.take(v["fw"]), k.take(saved[1]["w7"]),
                k.take(gf), k.take(bf), mk_in, names["fw"], names["y"], s_fast, nf3,
                flops=first_flops,
            )
        else:
            names.update(out_fast=k.give((fast_frames, spots, fwide)), pre_f=k.give((fast_frames, spots, fwide), BF16))
            s_fast = k.temp((1, 2 * LANES))
            k.step(
                part(fast_last, m, n, frames, group, 2 * LANES, 2 * width),
                st_in, k.take(v["ft"]), k.take(v["fw"], slice(2, 2 + fast_frames)), k.take(cf), k.take(gf), k.take(bf), mk_in,
                names["out_fast"], names["pre_f"], s_fast, nf3,
            )
        aw = k.temp((frames + 2 * halo, spots, width), BF16)
        k.step(
            part(slow_acts, m, n, frames, lo2, halo),
            st_in, k.take(v["second"]), *edges, k.take(gain_slow), k.take(bias_slow), mk_in, a2, n2, aw,
        )
        for at in range(0, wide, 256):
            lanes = slice(at, at + 256)
            k.step(
                part(slow_third, frames, halo, at),
                aw, k.take(w_slow_point, n, every, lanes), k.piece(third, every, every, lanes), s_third,
                flops=2 * frames * spots * width * 256,
            )
        if n == 0:
            pay = payload(k, s_fast, s_third)
            names["ff_row"] = row_out(k, names["y"], mk_in, lat, LANES)
            names["y_edge"] = edge_out(k, names["y"], mk_in, both)
        else:
            pay = payload(k, s_third, s_fast)
        got = finish(k, a2=a2, third=third, n2=n2, nf3=nf3, pay=pay, **names)
        st = gather_sums(got["pay"])
        for name in ("a2", "third", "n2", "nf3"):
            v[name] = got[name]
        if n == 0:
            saved[1].update(
                fw=got["fw"], y=got["y"], ff_row=other_row(got["ff_row"]), y_edge=swap_path(got["y_edge"])
            )
        else:
            out_fast, pre_f = got["out_fast"], got["pre_f"]

    def third_back(k, n, at, st_in, mk_in, pre):
        v = saved[n]
        d3, e2 = k.give((frames, spots, wide), BF16), k.give((frames, spots, width))
        s, gb = k.temp((1, 2 * width)), k.give((2, wide))
        gs = k.take(gain_slow)
        k.step(part(keep_sums, at, wide), st_in, gb)
        for t in range(frames):
            k.step(
                part(slow_third_grad, m, n, lo3),
                k.take(pre, t), k.take(v["third"], t + 1 - n), k.take(v["n3"]), k.peek(gb), gs, mk_in,
                k.piece(d3, t),
            )
        k.step(
            part(slow_third_back, m, n, frames, lo2),
            k.peek(d3), k.take(v["second"]), k.take(v["n2"]), k.take(w_slow_point, n), gs, k.take(bias_slow), mk_in,
            e2, s, flops=2 * frames * spots * width * wide,
        )
        return dict(d3=d3, e2=e2, gb3=gb), s

    def fast_back3(k, n, at, st_in, mk_in, pre):
        v = saved[n]
        d3, e2 = k.give((frames, spots, packs), BF16), k.give((frames, spots, LANES))
        s, gb = k.temp((1, 2 * LANES)), k.give((2, LANES))
        k.step(
            part(fast_third_back, m, n, frames, group, 2 * LANES, LANES, at),
            st_in, k.take(pre), k.take(v["ft"]), k.take(v["nf3"]), k.take(v["fs"]), k.take(v["nf2"]),
            k.take(wfp[n]), k.take(gf), k.take(bf), mk_in, d3, e2, s, gb,
            flops=2 * frames * spots * LANES * packs,
        )
        return dict(d3f=d3, ef2=e2, gbf3=gb), s

    def second_back(k, n, at, st_in, mk_in, e2, e2_row):
        v = saved[n]
        d2, e1 = k.give((frames, spots, width), BF16), k.give((frames, spots, width))
        s, gb = k.temp((1, 2 * width)), k.give((2, width))
        k.step(
            part(space_back, m, n, frames, cols, lo2, lo1, at, width, 0, False, m.slow),
            st_in, k.take(e2), k.take(e2_row), k.take(v["second"]), k.take(v["second_row"]), k.take(v["n2"]),
            k.take(v["first"]), k.take(v["n1"]), k.take(wsp, n), k.take(gain_slow), k.take(bias_slow), mk_in,
            d2, e1, s, gb, k.temp((frames, ext, 3 * width), BF16),
            flops=2 * frames * spots * 9 * width * width,
        )
        return dict(d2=d2, e1=e1, gb2=gb), s

    def fast_back2(k, n, at, st_in, mk_in, ef2, ef2_row):
        v = saved[n]
        d2, e1 = k.give((frames, spots, LANES), BF16), k.give((frames, spots, LANES))
        s, gb = k.temp((1, 2 * LANES)), k.give((2, LANES))
        k.step(
            part(space_back, m, n, frames, cols, LANES, 0, at, LANES, lat, True, m.fast),
            st_in, k.take(ef2), k.take(ef2_row), k.take(v["fs"]), k.take(v["fs_row"]), k.take(v["nf2"]),
            k.take(v["y"]), k.take(v["nf1"]), k.take(wfs[n]), k.take(gf), k.take(bf), mk_in,
            d2, e1, s, gb, k.temp((frames, ext, 3 * LANES), BF16),
            flops=2 * frames * spots * 9 * LANES * LANES,
        )
        return dict(d2f=d2, ef1=e1, gbf2=gb), s

    def first_back(k, n, st_in, mk_in, e1, e1_edge):
        v = saved[n]
        dw, el = k.give((frames + 2, spots, width), BF16), k.give((frames, spots, lat))
        s, gb = k.temp((1, 2 * lat)), k.give((2, width))
        edge, zedge = k.take(e1_edge), k.take(v["first_edge"])
        k.step(
            part(slow_first_back, m, n, frames, lo1, 0),
            st_in, k.take(e1), edge, edge, k.take(v["first"]), zedge, zedge, k.take(v["n1"]),
            k.take(w_slow_time, n, every, slice(wide, wide + lat)), k.take(v["y"]), k.take(v["nl"]),
            k.take(gain_slow), k.take(bias_slow), mk_in, dw, el, s, gb, flops=2 * frames * spots * 3 * lat * width,
        )
        return dict(dw=dw, el=el, gb1=gb), s

    def fast_back1(k, n, st1, at1, stl, atl, mk_in, el, el_edge, ef1, ef1_edge):
        v = saved[n]
        dl, df = k.give((frames, spots, lat), BF16), k.give((frames, spots, LANES), BF16)
        beside = [k.give((spots, lat), BF16), k.give((spots, LANES), BF16), k.give((spots, LANES), BF16)]
        gbl, gb1 = k.give((2, lat)), k.give((2, LANES))
        edge, yedge = k.take(ef1_edge), k.take(v["y_edge"])
        k.step(
            part(fast_first_back, m, n, frames, 0, at1, atl),
            st1, stl, k.take(el), k.take(el_edge), k.take(ef1), edge, edge, k.take(v["y"]), yedge, yedge,
            k.take(v["nl"]), k.take(v["nf1"]), k.take(gain_slow), k.take(gf), mk_in, dl, df, *beside, gbl, gb1,
        )
        return dict(dl=dl, df=df, dln=beside[0], dfp=beside[1], dfn=beside[2], gbl=gbl, gbf1=gb1)

    def weights_point(n, d3):
        k = Stage("point_weights")
        out = k.give((wide // 256, width, 256), BF16)
        k.step(point_weights, k.take(saved[n]["a2"]), k.take(d3), out, flops=2 * frames * spots * width * wide)
        return k.run()[0].reshape(-1, 256)

    def weights_space(n, d2):
        k = Stage("space_weights")
        out = k.give((3, 3 * width, width), BF16)
        k.step(
            part(space_weights, cols), k.take(saved[n]["a1"]), k.take(d2), out,
            k.temp((frames, ext, 3 * width), BF16), flops=2 * frames * spots * 9 * width * width,
        )
        return k.run()[0].reshape(-1, 256)

    def weights_time(n, dw):
        k = Stage("time_weights")
        out = k.give((3, wide + lat, width), BF16)
        k.step(
            part(time_weights, 1), k.take(saved[n]["sw"]), k.take(saved[n]["jl"]), k.take(dw), out,
            flops=2 * frames * spots * 3 * (wide + lat) * width,
        )
        return k.run()[0].reshape(-1, 256)

    def weights_fast(n, dl, df, d2, d3):
        v = saved[n]
        k = Stage("fast_weights")
        out = k.give((7 * LANES - LANES, 2 * LANES), BF16)
        k.step(
            part(fast_weights, group, cols, lat),
            k.take(v["fw"]), k.take(dl), k.take(df), k.take(v["fa1"]), k.take(d2), k.take(v["fa2"]), k.take(d3),
            out, k.temp((frames, ext, 3 * LANES), BF16), flops=first_flops,
        )
        return k.run()[0]

    b1, b0 = {}, {}
    k = Stage("last")
    mk_in, st_in = k.take(mk), k.take(st)
    out_slow, pre = k.give((frames, spots, wide)), k.give((frames, spots, wide), BF16)
    n3 = k.give((2, wide))
    s_pre, one, two = k.temp((1, 2 * wide)), k.temp((8, wide)), k.temp((8, wide))
    k.step(part(keep_norm, 0, wide, m.slow), st_in, mk_in, n3)
    k.step(clear, one, two)
    for t in range(frames):
        k.step(
            part(slow_last, m, 1, lo3),
            k.take(saved[1]["third"], t), k.take(saved[1]["sw"], t + 1), k.take(cs, t), k.peek(n3),
            k.take(gain_slow), k.take(bias_slow), mk_in, k.piece(out_slow, t), k.piece(pre, t), one, two,
        )
    k.step(close_sums, one, two, s_pre)
    names, s_ef2 = fast_back3(k, 1, 2 * wide, st_in, mk_in, pre_f)
    pay = payload(k, s_pre, s_ef2)
    ef2_row = row_out(k, names["ef2"], mk_in, 0, LANES)
    b1 = finish(k, out_slow=out_slow, pre=pre, n3=n3, pay=pay, ef2_row=ef2_row, **names)
    saved[1]["n3"] = b1["n3"]
    out_slow = b1["out_slow"]
    st = gather_sums(b1["pay"])

    k = Stage("back_third")
    ef2_row = other_row(b1["ef2_row"])
    mk_in, st_in = k.take(mk), k.take(st)
    names, s_e2 = third_back(k, 1, 0, st_in, mk_in, b1["pre"])
    more, s_ef1 = fast_back2(k, 1, 2 * wide, st_in, mk_in, b1["ef2"], ef2_row)
    pay = payload(k, s_e2, s_ef1)
    e2_row, ef1_edge = row_out(k, names["e2"], mk_in, 0, width), edge_out(k, more["ef1"], mk_in, LANES)
    b1.update(finish(k, pay=pay, e2_row=e2_row, ef1_edge=ef1_edge, **names, **more))
    st = st_ef1 = gather_sums(b1["pay"])
    e2_row = other_row(b1["e2_row"])
    st, ef1_edge = lax.optimization_barrier((st, swap_path(b1["ef1_edge"])))
    point1 = weights_point(1, b1["d3"])

    k = Stage("back_space")
    mk_in, st_in = k.take(mk), k.take(st)
    names, s_e1 = second_back(k, 1, 0, st_in, mk_in, b1["e2"], e2_row)
    pay = payload(k, s_e1)
    e1_edge = edge_out(k, names["e1"], mk_in, width)
    b1.update(finish(k, pay=pay, e1_edge=e1_edge, **names))
    st = gather_sums(b1["pay"])
    e1_edge = swap_path(b1["e1_edge"])
    space1 = weights_space(1, b1["d2"])

    k = Stage("back_first")
    mk_in, st_in = k.take(mk), k.take(st)
    names, s_el = first_back(k, 1, st_in, mk_in, b1["e1"], e1_edge)
    names["down"], s_down = k.give((frames, spots, wide), BF16), k.temp((1, 2 * wide))
    for at in range(0, wide, 256):
        lanes = slice(at, at + 256)
        k.step(
            part(slow_input_back, m, 1, frames, lo3, at),
            k.peek(names["dw"]), k.take(w_slow_time, 1, every, lanes), k.take(b1["pre"], every, every, lanes),
            k.take(saved[0]["sw"], slice(1, 1 + frames), every, lanes),
            k.take(saved[0]["third"], slice(1, 1 + frames), every, lanes),
            k.take(saved[0]["n3"]), k.take(gain_slow), k.take(bias_slow), mk_in,
            k.piece(names["down"], every, every, lanes), s_down,
            flops=2 * frames * spots * 3 * 256 * width,
        )
    pay = payload(k, s_el, s_down)
    el_edge = edge_out(k, names["el"], mk_in, lat)
    b1.update(finish(k, pay=pay, el_edge=el_edge, **names))
    st = gather_sums(b1["pay"])
    el_edge = swap_path(b1["el_edge"])
    time1 = weights_time(1, b1["dw"])
    sizes1 = [point1.shape[0], space1.shape[0], time1.shape[0]]
    ones = jnp.concatenate([point1, space1, time1], axis=0)
    st, ones, el_edge = lax.optimization_barrier((st, ones, el_edge))
    ones = lax.psum(ones, AXES)

    GRADS = ("df", "dln", "dfp", "dfn")
    SUMS = ("gbl", "gb1", "gb2", "gb3", "gbf1", "gbf2", "gbf3")
    steps = exchange_steps()
    core, across, down = steps[:3]
    seen = {}

    def block_zero(st=st, el_edge=el_edge, ef1_edge=ef1_edge, b1=b1, b0=b0):
        b1, b0 = dict(b1), dict(b0)
        k = Stage("back_third")
        mk_in, st_in = k.take(mk), k.take(st)
        names, s_e2 = third_back(k, 0, 2 * lat, st_in, mk_in, b1["down"])
        more = fast_back1(
            k, 1, k.take(st_ef1), 2 * width, st_in, 0, mk_in, b1["el"], el_edge, b1["ef1"], ef1_edge
        )
        inner_grads = [more[name] for name in ("dl", "df", "dln", "dfp", "dfn")]
        more["downf"], s_pf = k.give((fast_frames, spots, fwide), BF16), k.temp((1, 2 * LANES))
        k.step(
            part(fast_input_back, m, 1, frames, group, 2 * LANES, False),
            *inner_grads, k.take(saved[1]["w7"]), k.take(pre_f), k.take(saved[0]["fw"]), k.take(saved[0]["ft"]),
            k.take(saved[0]["nf3"]), k.take(gf), k.take(bf), mk_in, more["downf"], s_pf,
            k.temp((fast_frames + 4, spots, fwide)), flops=first_flops,
        )
        pay = payload(k, s_e2, s_pf)
        e2_row = row_out(k, names["e2"], mk_in, 0, width)
        got = finish(k, pay=pay, e2_row=e2_row, **names, **more)
        for name in more:
            b1[name] = got[name]
        b0.update({name: got[name] for name in names})
        st = gather_sums(got["pay"])
        e2_row = other_row(got["e2_row"])
        point0 = weights_point(0, b0["d3"])
        fast_1 = weights_fast(1, b1["dl"], b1["df"], b1["d2f"], b1["d3f"])

        k = Stage("back_space")
        mk_in, st_in = k.take(mk), k.take(st)
        names, s_e1 = second_back(k, 0, 0, st_in, mk_in, b0["e2"], e2_row)
        more, s_ef2 = fast_back3(k, 0, 2 * width, st_in, mk_in, b1["downf"])
        pay = payload(k, s_e1, s_ef2)
        e1_edge, ef2_row = edge_out(k, names["e1"], mk_in, width), row_out(k, more["ef2"], mk_in, 0, LANES)
        b0.update(finish(k, pay=pay, e1_edge=e1_edge, ef2_row=ef2_row, **names, **more))
        st = gather_sums(b0["pay"])
        e1_edge, ef2_row = swap_path(b0["e1_edge"]), other_row(b0["ef2_row"])
        space0 = weights_space(0, b0["d2"])
        mid = jnp.concatenate([fast_1, point0, space0], axis=0)
        st, mid = lax.optimization_barrier((st, mid))

        k = Stage("back_first")
        mk_in, st_in = k.take(mk), k.take(st)
        names, s_el = first_back(k, 0, st_in, mk_in, b0["e1"], e1_edge)
        more, s_ef1 = fast_back2(k, 0, 2 * width, st_in, mk_in, b0["ef2"], ef2_row)
        pay = payload(k, s_el, s_ef1)
        el_edge, ef1_edge = edge_out(k, names["el"], mk_in, lat), edge_out(k, more["ef1"], mk_in, LANES)
        b0.update(finish(k, pay=pay, el_edge=el_edge, ef1_edge=ef1_edge, **names, **more))
        b0["dw"], mid = lax.optimization_barrier((b0["dw"], mid))
        mid = halve(mid, *core)
        st = gather_sums(b0["pay"])
        el_edge, ef1_edge = swap_path(b0["el_edge"]), swap_path(b0["ef1_edge"])
        time0 = weights_time(0, b0["dw"])
        st, mid = lax.optimization_barrier((st, mid))
        mid = halve_both(*parted(mid), across, down)
        k = Stage("back_fast")
        mk_in, st_in = k.take(mk), k.take(st)
        more = fast_back1(k, 0, st_in, 2 * lat, st_in, 0, mk_in, b0["el"], el_edge, b0["ef1"], ef1_edge)
        v = saved[0]
        rest = k.give((6 * LANES, 2 * LANES), BF16)
        k.step(
            part(fast_weights, group, cols, lat),
            k.take(v["fw"]), more["dl"], more["df"], k.take(v["fa1"]), k.take(b0["d2f"]), k.take(v["fa2"]),
            k.take(b0["d3f"]), rest, k.temp((frames, ext, 3 * LANES), BF16), flops=first_flops,
        )
        got = finish(k, rest=rest, **more)
        b0.update(got)
        seen["rows"] = [piece.shape[0] for piece in (fast_1, point0, space0, time0, got["rest"])]
        late = halve(jnp.concatenate([time0, got["rest"]], axis=0), *core)
        late, dw0 = lax.optimization_barrier((late, b0["dw"]))
        late = halve_both(*parted(late), across, down)
        late, dl0 = lax.optimization_barrier((late, b0["dl"]))
        k = Stage("slow_input")
        gx_slow = k.give((frames, spots, wide))
        k.step(
            part(slow_input_last, m, frames),
            k.take(dw0), k.take(w_slow_time, 0, every, slice(0, wide)), k.take(b1["down"]), k.take(mk), gx_slow,
            flops=2 * frames * spots * 3 * wide * width,
        )
        (gx_slow,) = k.run()
        k = Stage("fast_input")
        gx_fast = k.give((fast_frames, spots, fwide))
        k.step(
            part(fast_input_back, m, 0, frames, group, 2 * LANES, True),
            k.take(dl0), *[k.take(b0[name]) for name in GRADS], k.take(saved[0]["w7"]), k.take(b1["downf"]), k.take(mk), gx_fast,
            k.temp((fast_frames + 4, spots, fwide)), flops=first_flops,
        )
        (gx_fast,) = k.run()
        def along(value, ahead=steps[3:]):
            for step in ahead:
                value = halve(value, *step)
            value = value.astype(BF16)
            for step in reversed(steps[3:]):
                value = double(value, *step)
            return value

        mid = along(jnp.concatenate(halve_both(*mid, down, across), axis=0))
        late, gx_slow = lax.optimization_barrier((halve_both(*late, down, across), gx_slow))
        late = jnp.concatenate(late, axis=0)
        for step in steps[3:4]:
            late, gx_fast = lax.optimization_barrier((halve(late, *step), gx_fast))
        late = along(late, steps[4:])
        sums = [b0[name] for name in SUMS] + [b1[name] for name in ("gbl", "gbf1")]
        return (mid, late, gx_slow, gx_fast, *sums)

    like = jax.eval_shape(block_zero)
    got = lax.cond(
        clip_size[0, 0] > 0, block_zero, lambda: tuple(jnp.zeros(o.shape, o.dtype) for o in like)
    )
    mid, late, gx_slow, gx_fast = got[:4]
    b0 = dict(zip(SUMS, got[4:11]))
    b1["gbl"], b1["gbf1"] = got[11:13]

    time_rows, space_rows = 3 * (wide + lat), 9 * width
    k = Stage("assemble_one")
    ones_in = k.take(ones)
    gtime, gspace = k.give((2, time_rows, width), F32, 1), k.give((2, space_rows, width), F32, 1)
    gpoint = k.give((2, width, wide), F32, 1)
    k.step(part(copy_rows, sizes1[0] + sizes1[1]), ones_in, gtime)
    k.step(part(copy_rows, sizes1[0]), ones_in, gspace)
    k.step(part(copy_columns, 0), ones_in, gpoint)
    half_done = k.run()

    def spread_both(one, two, tied=()):
        one, two = [one, swap(one, *down)], [two, swap(two, *across)]
        one, two, tied = lax.optimization_barrier((one, two, tied))
        one, two = [jnp.stack(pair) for pair in (one, two)]
        one, two = [one, swap(one, *across)], [two, swap(two, *down)]
        return [pair + [swap(half, *core) for half in pair] for pair in (one, two)], tied

    (mid_one, mid_two), _ = spread_both(*parted(mid))
    (one, two), half_done = spread_both(*parted(late), half_done)

    core_bit = lax.axis_index("rows") % 2
    down_bit = (lax.axis_index("rows") // 2) % 2

    k = Stage("assemble")
    flip_one = k.scalar((core_bit * 4 + path * 2 + down_bit).astype(jnp.int32).reshape(1))
    flip_two = k.scalar((core_bit * 4 + down_bit * 2 + path).astype(jnp.int32).reshape(1))
    one_in = k.take_blocks(one, flip_one, every)
    two_in = k.take_blocks(two, flip_two, every)
    mid_one, mid_two = k.take_blocks(mid_one, flip_one, every), k.take_blocks(mid_two, flip_two, every)
    sizes = seen["rows"]
    half_mid, half_late = sum(sizes[:3]) // 2, sum(sizes[3:]) // 2
    gspace = k.give((2, space_rows, width), F32, 0, half_done[1])
    k.step(part(place_rows, sizes[0] + sizes[1], 0, half_mid), mid_one, mid_two, gspace)
    gpoint = k.give((2, width, wide), F32, 0, half_done[2])
    k.step(part(place_columns, sizes[0], 0, half_mid), mid_one, mid_two, gpoint)
    gtime = k.give((2, time_rows, width), F32, 0, half_done[0])
    k.step(part(place_rows, 0, 0, half_late), one_in, two_in, gtime)
    fast_outs = [
        k.give((2, 5 * fwide, lat)), k.give((2, 3, inner, fwide)), k.give((2, 9, inner, inner)),
        k.give((2, inner, fwide)),
    ]
    k.step(part(place_fast, inner, half_mid, half_late, sizes[3]), mid_one, mid_two, one_in, two_in, *fast_outs)
    sums = [k.take(b[name]) for b in (b0, b1) for name in ("gbl", "gb1", "gb2", "gb3", "gbf1", "gbf2", "gbf3")]
    norm_outs = [k.give(like.shape) for like in (gain_slow, bias_slow, gain_fast, bias_fast)]
    k.step(part(assemble_norms, inner), *sums, *norm_outs)
    got = k.run()
    glat, gft, gfs, gfp = [got[h[1]] for h in fast_outs]

    return (
        out_slow.reshape(x_slow.shape),
        out_fast.reshape(x_fast.shape),
        gx_slow.reshape(x_slow.shape),
        gx_fast.reshape(x_fast.shape),
        glat.reshape(w_lateral.shape),
        got[gtime[1]].reshape(w_slow_time.shape),
        got[gspace[1]].reshape(w_slow_space.shape),
        got[gpoint[1]],
        jnp.swapaxes(gft, 2, 3),
        gfs.reshape(w_fast_space.shape),
        gfp,
        *[got[h[1]] for h in norm_outs],
    )


def solution(mesh):
    spread = P("path", None, "rows", None, None, None)
    return jax.shard_map(
        on_device,
        mesh=mesh,
        in_specs=(spread, spread) + (P(),) * 12 + (spread, spread),
        out_specs=(spread,) * 4 + (P(),) * 11,
        check_vma=False,
    )
```

```python
import functools

import jax
import jax.numpy as jnp
import numpy as np
from jax import lax
from jax.experimental import pallas as pl
from jax.experimental.pallas import tpu as pltpu
from jax.sharding import PartitionSpec as P

TS = 8
TF = 32
F32 = jnp.float32
BF16 = jnp.bfloat16
EPSILON = 1e-05
LANES = 128
AXES = ("path", "rows")
VMEM_LIMIT = 56 * 2**20


def swap(value, axis, stride):
    pairs = [(source, source ^ stride) for source in range(lax.axis_size(axis))]
    return lax.ppermute(value, axis, pairs)


def gather_sums(spread):
    return lax.all_to_all(spread, AXES, 0, 0, tiled=True)


def swap_path(value):
    assert lax.axis_size("path") == 2
    return lax.ppermute(value, "path", [(0, 1), (1, 0)])


def exchange_steps():
    steps = [("rows", 1), ("path", 1)]
    stride = 2
    while stride < lax.axis_size("rows"):
        steps.append(("rows", stride))
        stride *= 2
    return steps


def halve(value, axis, stride):
    size = value.shape[0] // 2
    upper = (lax.axis_index(axis) // stride) % 2
    keep = lax.dynamic_slice_in_dim(value, upper * size, size, 0)
    give = lax.dynamic_slice_in_dim(value, (1 - upper) * size, size, 0)
    return keep.astype(F32) + swap(give.astype(BF16), axis, stride).astype(F32)


def double(value, axis, stride):
    upper = (lax.axis_index(axis) // stride) % 2
    got = swap(value, axis, stride)
    return jnp.concatenate(
        [jnp.where(upper == 0, value, got), jnp.where(upper == 0, got, value)], axis=0
    )


def halve_both(one, two, first, second):
    return halve(one, *first), halve(two, *second)


def parted(value):
    size = value.shape[0] // 2
    return value[:size], value[size:]


class Stage:
    def __init__(self, name):
        self.name = name
        self.arrays, self.views, self.scalars, self.pairs = [], [], [], []
        self.outs, self.temps, self.steps = [], [], []
        self.entries, self.ontos = [], []
        self.flops = 0

    def take(self, array, *view):
        for at, known in enumerate(self.arrays):
            if known is array:
                break
        else:
            at = len(self.arrays)
            self.arrays.append(array)
        for k, (other, seen) in enumerate(self.views):
            if other == at and seen == view:
                return ("in", k)
        self.views.append((at, view))
        return ("in", len(self.views) - 1)

    def take_blocks(self, values, flip, rows):
        self.pairs.append(([self.take(value, slice(None), rows) for value in values], flip))
        return ("pair", len(self.pairs) - 1)

    def scalar(self, array):
        self.scalars.append(array)
        return ("scalar", len(self.scalars) - 1)

    def give(self, dims, dtype=F32, at=None, onto=None):
        self.outs.append(jax.ShapeDtypeStruct(tuple(dims), dtype))
        self.entries.append(at)
        self.ontos.append(onto)
        return ("out", len(self.outs) - 1)

    def piece(self, handle, *index):
        return ("piece", (handle[1], index))

    def peek(self, handle):
        return ("peek", handle[1])

    def temp(self, dims, dtype=F32):
        self.temps.append(pltpu.VMEM(tuple(dims), dtype))
        return ("temp", len(self.temps) - 1)

    def step(self, fn, *handles, flops=0):
        self.flops += flops
        self.steps.append((fn, handles))

    def sem(self, view, block):
        return 8 * view + block

    def view_shape(self, view):
        at, index = view
        return np.broadcast_to(np.zeros((), np.int8), self.arrays[at].shape)[index].shape

    def run(self):
        arrays, views, outs, steps, pairs = self.arrays, self.views, self.outs, self.steps, self.pairs
        order, home = [], {}
        for k, (members, flip) in enumerate(pairs):
            for j, member in enumerate(members):
                home[member[1]] = (k, j, flip)
        under = [onto for onto in self.ontos if onto is not None]

        def need(handle):
            if handle[0] == "in":
                return [handle[1]]
            return [part[1] for part in pairs[handle[1]][0]] if handle[0] == "pair" else []

        for _, handles in steps:
            for handle in handles:
                for k in need(handle):
                    if k not in order:
                        order.append(k)

        def body(*refs):
            refs = list(refs)

            def cut(count):
                taken = refs[:count]
                del refs[:count]
                return taken

            scalars, hbm_in = cut(len(self.scalars)), cut(len(arrays))
            cut(len(under))
            hbm_out = cut(len(outs))
            alone = [k for k in range(len(views)) if k not in home]
            held = dict(zip(alone, cut(len(alone))))
            joint, made, temps, (sems,) = cut(len(pairs)), cut(len(outs)), cut(len(self.temps)), refs
            copies = {}
            for k in order:
                at, index = views[k]
                src = hbm_in[at].at[index] if index else hbm_in[at]
                if k in home:
                    pair, second, flip = home[k]
                    count = self.view_shape(views[k])[0]
                    copies[k] = []
                    for block in range(count):
                        to = (second * count + block) ^ scalars[flip[1]][0]
                        copies[k].append(
                            pltpu.make_async_copy(src.at[block], joint[pair].at[to], sems.at[self.sem(k, block)])
                        )
                else:
                    copies[k] = [pltpu.make_async_copy(src, held[k], sems.at[self.sem(k, 0)])]
                for copy in copies[k]:
                    copy.start()
            waited, sent = set(), {}
            for fn, handles in steps:
                given = []
                for handle in handles:
                    for k in need(handle):
                        if k not in waited:
                            for copy in copies[k]:
                                copy.wait()
                            waited.add(k)
                    if handle[0] == "piece":
                        given.append(made[handle[1][0]].at[handle[1][1]])
                        continue
                    place = {"in": held, "pair": joint, "out": made, "peek": made, "temp": temps, "scalar": scalars}
                    given.append(place[handle[0]][handle[1]])
                fn(*given)
                for kind, k in handles:
                    if kind == "out" and k not in sent:
                        to = hbm_out[k] if self.entries[k] is None else hbm_out[k].at[self.entries[k]]
                        sent[k] = [pltpu.make_async_copy(made[k], to, sems.at[8 * (len(views) + k)])]
                        sent[k][0].start()
                    elif kind == "piece":
                        k, index = k
                        done = sent.setdefault(k, [])
                        sem = sems.at[8 * (len(views) + k) + len(done)]
                        done.append(pltpu.make_async_copy(made[k].at[index], hbm_out[k].at[index], sem))
                        done[-1].start()
            for done in sent.values():
                for copy in done:
                    copy.wait()

        moved = sum(a.size * a.dtype.itemsize for a in outs)
        for view in views:
            moved += int(np.prod(self.view_shape(view))) * arrays[view[0]].dtype.itemsize
        scratch = [
            pltpu.VMEM(self.view_shape(view), arrays[view[0]].dtype) for k, view in enumerate(views) if k not in home
        ]
        for members, _ in pairs:
            size = self.view_shape(views[members[0][1]])
            scratch.append(
                pltpu.VMEM((len(members) * size[0],) + size[1:], arrays[views[members[0][1]][0]].dtype)
            )
        scratch += [
            pltpu.VMEM(o.shape if at is None else o.shape[1:], o.dtype) for o, at in zip(outs, self.entries)
        ]
        aliases = {}
        for k, onto in enumerate(self.ontos):
            if onto is not None:
                aliases[len(self.scalars) + len(arrays) + len(aliases)] = k
        scratch += self.temps + [pltpu.SemaphoreType.DMA((8 * (len(views) + len(outs)),))]
        return pl.pallas_call(
            body,
            out_shape=tuple(outs),
            in_specs=[pl.BlockSpec(memory_space=pltpu.SMEM) for _ in self.scalars]
            + [pl.BlockSpec(memory_space=pl.ANY) for _ in arrays + under],
            out_specs=tuple(pl.BlockSpec(memory_space=pl.ANY) for _ in outs),
            scratch_shapes=scratch,
            input_output_aliases=aliases,
            compiler_params=pltpu.CompilerParams(vmem_limit_bytes=VMEM_LIMIT),
            cost_estimate=pl.CostEstimate(flops=self.flops, bytes_accessed=moved, transcendentals=0),
            name=self.name,
        )(*self.scalars, *arrays, *under)


class Masks:
    def __init__(self, spots, cols):
        self.main = (0, spots)
        self.ext = (spots, 2 * spots + 2 * cols)
        self.prev = (2 * spots + 2 * cols, 3 * spots + 2 * cols)
        self.next = (3 * spots + 2 * cols, 4 * spots + 2 * cols)
        self.slow = (4 * spots + 2 * cols, 4 * spots + 2 * cols + 8)
        self.fast = (4 * spots + 2 * cols + 8, 4 * spots + 2 * cols + 16)
        self.half = (4 * spots + 2 * cols + 16, 4 * spots + 2 * cols + 24)
        self.path = (4 * spots + 2 * cols + 24, 4 * spots + 2 * cols + 32)
        self.rows = 4 * spots + 2 * cols + 32


def make_masks(m, rows, cols, last, place, clips, mk):
    half = place[0] % 2
    path = place[1]
    side = clips[0, place[0] // 2]
    area = 0
    for k in range(clips.shape[1]):
        area = area + clips[0, k] * clips[0, k]
    shift = cols.bit_length() - 1

    def inside(first, count):
        at = lax.broadcasted_iota(jnp.int32, (count * cols, LANES), 0)
        line = half * rows + first + (at >> shift)
        spot = at & (cols - 1)
        good = (line >= 0) & (line < 2 * rows) & (line < side) & (spot < side)
        return jnp.where(good, 1.0, 0.0)

    main = inside(0, rows)
    mk[m.main[0] : m.main[1], :] = main
    mk[m.ext[0] : m.ext[1], :] = inside(-1, rows + 2)
    mk[m.prev[0] : m.prev[1], :] = main * jnp.where(path > 0, 1.0, 0.0)
    mk[m.next[0] : m.next[1], :] = main * jnp.where(path < last, 1.0, 0.0)

    def fill(span, value):
        mk[span[0] : span[1], :] = jnp.full((8, LANES), value, F32)

    fill(m.slow, TS * area.astype(F32))
    fill(m.fast, TF * area.astype(F32))
    fill(m.half, half.astype(F32))
    fill(m.path, path.astype(F32))


def own_row(m, spots, cols, col0, width, z, mk, row):
    for t in range(z.shape[0]):
        lower = mk[m.half[0] : m.half[0] + 1, :] > 0.5
        for lane in range(0, width, LANES):
            at = col0 + lane
            row[t, :, lane : lane + LANES] = jnp.where(
                lower, z[t, 0:cols, at : at + LANES], z[t, spots - cols : spots, at : at + LANES]
            )


def own_edge(m, lead, tail, z, mk, edge):
    frames = z.shape[0]
    second = mk[m.path[0] : m.path[0] + 1, :] > 0.5
    for lane in range(0, edge.shape[1], LANES):
        edge[:, lane : lane + LANES] = jnp.where(
            second,
            z[0, :, lead + lane : lead + lane + LANES],
            z[frames - 1, :, tail + lane : tail + lane + LANES],
        ).astype(edge.dtype)


def spread_sums(*refs):
    parts, out = refs[:-1], refs[-1]
    row = jnp.concatenate([part[...] for part in parts], axis=1)
    out[...] = jnp.broadcast_to(row[None], out.shape)


def make_w7(lat, group, wl, wf, w7):
    inner = wf.shape[1]
    w7[...] = jnp.zeros(w7.shape, BF16)
    for j in range(wl.shape[0]):
        w7[j * LANES : (j + 1) * LANES, 0:lat] = wl[j]
    at = lax.broadcasted_iota(jnp.int32, (inner, LANES), 0)
    lane = lax.broadcasted_iota(jnp.int32, (inner, LANES), 1)
    places = [jnp.where(lane == at + inner * k, 1.0, 0.0).astype(BF16) for k in range(group)]
    for f in range(1, group + 3):
        used = [k for k in range(group) if 0 <= f - 1 - k < 3]
        got = None
        for k in used:
            more = dot_tn(wf[f - 1 - k], places[k])
            got = more if got is None else got + more
        w7[f * LANES : (f + 1) * LANES, lat : lat + LANES] = got.astype(BF16)


def make_blocks(group, ws, wp, wfs, wfp):
    inner = wp.shape[0]
    at = lax.broadcasted_iota(jnp.int32, (inner, LANES), 0)
    lane = lax.broadcasted_iota(jnp.int32, (inner, LANES), 1)
    tile = jnp.where((lane & (inner - 1)) == at, 1.0, 0.0).astype(BF16)
    shift = inner.bit_length() - 1
    for tap in range(ws.shape[0]):
        got = dot(ws[tap], tile)
        for k in range(group):
            kept = jnp.where((lane >> shift) == k, got, 0.0).astype(BF16)
            row = (tap % 3) * LANES + k * inner
            wfs[tap // 3, row : row + inner, :] = kept
    wfp[...] = jnp.zeros(wfp.shape, BF16)
    for k in range(group):
        wfp[k * inner : (k + 1) * inner, k * LANES : (k + 1) * LANES] = wp[...]


def widen(rows, width):
    return jnp.concatenate([rows] * (width // LANES), axis=1)


def sublane_sums(value):
    return jnp.sum(value.reshape(value.shape[0] // 8, 8, value.shape[1]), axis=0)


def row_sum(value):
    return jnp.sum(value, axis=0, keepdims=True)


def fold_packed(row):
    full = jnp.broadcast_to(row, (8, LANES))
    full = full + pltpu.roll(full, 64, 1)
    full = full + pltpu.roll(full, 32, 1)
    return full[0:1]


def totals(st, lo, width, packed=False):
    first = jnp.sum(st[:, :, lo : lo + width], axis=0)
    second = jnp.sum(st[:, :, lo + width : lo + 2 * width], axis=0)
    if packed:
        return fold_packed(first), fold_packed(second)
    return first, second


def norm_rows(st, lo, width, count, packed=False):
    first, second = totals(st, lo, width, packed)
    mean = first / count
    return mean, lax.rsqrt(second / count - mean * mean + EPSILON)


def keep_norm(lo, width, span, st, mk, nz):
    mean, rstd = norm_rows(st, lo, width, widen(mk[span[0] : span[0] + 1, :], width))
    nz[0:1, :] = mean
    nz[1:2, :] = rstd


def keep_sums(lo, width, st, gb):
    one, two = totals(st, lo, width)
    gb[0:1, :] = one
    gb[1:2, :] = two


def clear(*refs):
    for ref in refs:
        ref[...] = jnp.zeros(ref.shape, F32)


def close_sums(one, two, s):
    s[...] = jnp.concatenate([row_sum(one[...]), row_sum(two[...])], axis=1)


def sigmoid(value):
    return 0.5 * jnp.tanh(0.5 * value) + 0.5


def silu(value):
    return value * sigmoid(value)


def silu_slope(value):
    sigma = sigmoid(value)
    return sigma * (1.0 + value * (1.0 - sigma))


def dot(a, b):
    return jnp.dot(a, b, preferred_element_type=F32)


def dot_nt(a, b):
    return lax.dot_general(a, b, (((1,), (1,)), ((), ())), preferred_element_type=F32)


def dot_tn(a, b):
    return lax.dot_general(a, b, (((0,), (0,)), ((), ())), preferred_element_type=F32)


def flat(value):
    return value.reshape(value.shape[0] * value.shape[1], value.shape[2])


def store_shifts(dst, t, value, cols):
    rows, width = value.shape
    spot = lax.broadcasted_iota(jnp.int32, (rows, width), 0) & (cols - 1)
    left = jnp.where(spot == 0, 0.0, pltpu.roll(value, 1, 0))
    right = jnp.where(spot == cols - 1, 0.0, pltpu.roll(value, rows - 1, 0))
    dst[t, :, 0:width] = left.astype(BF16)
    dst[t, :, width : 2 * width] = value.astype(BF16)
    dst[t, :, 2 * width : 3 * width] = right.astype(BF16)


def taps_of(frames_ref, frames, group):
    return jnp.concatenate(
        [
            jnp.concatenate([frames_ref[group * t + f] for f in range(7)], axis=1)
            for t in range(frames)
        ],
        axis=0,
    )


def entry_sums(y, lat, frames, spots):
    width = y.shape[1]
    one = jnp.zeros((8, width), F32)
    two = jnp.zeros((8, width), F32)
    for t in range(frames):
        part = y[t * spots : (t + 1) * spots]
        one = one + sublane_sums(part)
        two = two + sublane_sums(part * part)
    one = row_sum(one)
    two = row_sum(two)
    return jnp.concatenate([one[:, :lat], two[:, :lat], one[:, lat:], two[:, lat:]], axis=1)


def fast_entry(m, frames, group, x, before, after, mk, w7, fw, y, s):
    spots = x.shape[1]
    count = x.shape[0]

    def put(at, value, span):
        fw[at] = (value.astype(F32) * mk[span[0] : span[1], :]).astype(BF16)

    for k in range(2):
        put(k, before[k], m.prev)
        put(2 + count + k, after[k], m.next)
    for k in range(count):
        put(2 + k, x[k], m.main)
    out = dot(taps_of(fw, frames, group), w7[...])
    for t in range(frames):
        y[t] = out[t * spots : (t + 1) * spots]
    s[...] = entry_sums(out, w7.shape[1] - LANES, frames, spots)


def slow_partial(m, frames, x, before, after, mk, wt, xm, fpart):
    spots, wide = x.shape[1], x.shape[2]
    sources = [(before, m.prev)] + [(x.at[t], m.main) for t in range(frames)] + [(after, m.next)]
    for k, (src, span) in enumerate(sources):
        for lo in range(0, wide, 256):
            mask = widen(mk[span[0] : span[1], :], 256)
            xm[k, :, lo : lo + 256] = (src[:, lo : lo + 256].astype(F32) * mask).astype(BF16)
    out = dot(flat(xm[0:frames]), wt[0, :wide, :])
    for j in range(1, 3):
        out = out + dot(flat(xm[j : j + frames]), wt[j, :wide, :])
    for t in range(frames):
        fpart[t] = out[t * spots : (t + 1) * spots]


def lat_join(m, n, frames, lat, st, y, before, after, fpart, wt, gs, bs, mk, jl, first, s, nl, jw):
    spots = y.shape[1]
    wide = wt.shape[1] - lat
    count = widen(mk[m.slow[0] : m.slow[0] + 1, :], lat)
    mean, rstd = norm_rows(st, 0, lat, count)
    nl[0:1, :] = mean
    nl[1:2, :] = rstd
    scale = rstd * gs[n : n + 1, 0:lat]
    bias = bs[n : n + 1, 0:lat]
    sources = (
        [(before[:, 0:lat], m.prev)]
        + [(y[t, :, 0:lat], m.main) for t in range(frames)]
        + [(after[:, 0:lat], m.next)]
    )
    for k, (value, span) in enumerate(sources):
        mask = widen(mk[span[0] : span[1], :], lat)
        act = (silu((value - mean) * scale + bias) * mask).astype(BF16)
        jw[k] = act
        if 1 <= k <= frames:
            jl[k - 1] = act
    out = flat(fpart[...])
    for j in range(3):
        out = out + dot(flat(jw[j : j + frames]), wt[j, wide:, :])
    one = jnp.zeros((8, out.shape[1]), F32)
    two = jnp.zeros((8, out.shape[1]), F32)
    for t in range(frames):
        part = out[t * spots : (t + 1) * spots]
        first[t] = part
        one = one + sublane_sums(part)
        two = two + sublane_sums(part * part)
    s[...] = jnp.concatenate([row_sum(one), row_sum(two)], axis=1)


def space_forward(
    m, n, frames, cols, lo, at, width, col0, packed, span, st, z, row, w, g, b, mk, aw, out, s, nz, vw
):
    spots = z.shape[1]
    count = widen(mk[span[0] : span[0] + 1, :], width)
    mean, rstd = norm_rows(st, at, width, count, packed)
    nz[0:1, :] = mean
    nz[1:2, :] = rstd
    scale = rstd * g[n : n + 1, lo : lo + width]
    bias = b[n : n + 1, lo : lo + width]
    mask = widen(mk[m.ext[0] : m.ext[1], :], width)
    for t in range(frames):
        value = jnp.concatenate([row[t], z[t, :, col0 : col0 + width], row[t]], axis=0)
        act = silu((value - mean) * scale + bias) * mask
        aw[t] = act.astype(BF16)
        store_shifts(vw, t, act, cols)
    total = dot(flat(vw[:, 0:spots, :]), w[0])
    for i in range(1, 3):
        total = total + dot(flat(vw[:, i * cols : i * cols + spots, :]), w[i])
    mask = widen(mk[m.main[0] : m.main[1], :], width)
    one = jnp.zeros((8, width), F32)
    two = jnp.zeros((8, width), F32)
    for t in range(frames):
        part = total[t * spots : (t + 1) * spots]
        out[t] = part
        part = part * mask
        one = one + sublane_sums(part)
        two = two + sublane_sums(part * part)
    s[...] = jnp.concatenate([row_sum(one), row_sum(two)], axis=1)


def slow_acts(m, n, frames, lo, halo, st, z, *rest):
    if halo:
        before, after, g, b, mk, a2, nz, aw = rest
    else:
        g, b, mk, a2, nz, aw = rest
    width = z.shape[2]
    keep_norm(0, width, m.slow, st, mk, nz)
    mean = nz[0:1, :]
    scale = nz[1:2, :] * g[n : n + 1, lo : lo + width]
    bias = b[n : n + 1, lo : lo + width]
    sources = [(z[t], m.main, t + halo) for t in range(frames)]
    if halo:
        sources += [(before[...], m.prev, 0), (after[...], m.next, frames + 1)]
    for value, span, at in sources:
        mask = widen(mk[span[0] : span[1], :], width)
        act = (silu((value - mean) * scale + bias) * mask).astype(BF16)
        aw[at] = act
        if halo <= at < frames + halo:
            a2[at - halo] = act


def slow_third(frames, halo, at, aw, wp, third, s):
    spots = aw.shape[1]
    wide = s.shape[1] // 2
    out = dot(flat(aw[...]), wp[...])
    one = jnp.zeros((8, 256), F32)
    two = jnp.zeros((8, 256), F32)
    for t in range(frames + 2 * halo):
        part = out[t * spots : (t + 1) * spots]
        third[t] = part.astype(BF16)
        if halo <= t < frames + halo:
            one = one + sublane_sums(part)
            two = two + sublane_sums(part * part)
    s[:, at : at + 256] = row_sum(one)
    s[:, wide + at : wide + at + 256] = row_sum(two)


def fast_third(m, n, frames, lo, at, st, z, wp, g, b, mk, a2, ft, s, nz):
    spots = z.shape[1]
    count = mk[m.fast[0] : m.fast[0] + 1, :]
    mean, rstd = norm_rows(st, at, LANES, count, True)
    nz[0:1, :] = mean
    nz[1:2, :] = rstd
    scale = rstd * g[n : n + 1, lo : lo + LANES]
    bias = b[n : n + 1, lo : lo + LANES]
    mask = mk[m.main[0] : m.main[1], :]
    for t in range(frames):
        a2[t] = (silu((z[t] - mean) * scale + bias) * mask).astype(BF16)
    acts = flat(a2[...])
    one = jnp.zeros((8, LANES), F32)
    two = jnp.zeros((8, LANES), F32)
    out = dot(acts, wp[...])
    for t in range(frames):
        for lane in range(0, wp.shape[1], LANES):
            part = out[t * spots : (t + 1) * spots, lane : lane + LANES]
            ft[t, :, lane : lane + LANES] = part.astype(BF16)
            one = one + sublane_sums(part)
            two = two + sublane_sums(part * part)
    s[...] = jnp.concatenate([row_sum(one), row_sum(two)], axis=1)


def fast_next(m, n, frames, group, lo, at, st, ft, before, after, fw0, w7, g, b, mk, fw1, y, s, nz):
    spots = ft.shape[1]
    count = mk[m.fast[0] : m.fast[0] + 1, :]
    mean, rstd = norm_rows(st, at, LANES, count)
    nz[0:1, :] = mean
    nz[1:2, :] = rstd
    scale = rstd * g[n : n + 1, lo : lo + LANES]
    bias = b[n : n + 1, lo : lo + LANES]
    total = frames * group

    def out_of(k, value, span):
        z = fw0[k].astype(F32) + ((value - mean) * scale + bias)
        return silu(z) * mk[span[0] : span[1], :]

    for k in range(2):
        lane = k * LANES
        fw1[k] = out_of(k, before[:, lane : lane + LANES], m.prev).astype(BF16)
        fw1[2 + total + k] = out_of(2 + total + k, after[:, lane : lane + LANES], m.next).astype(BF16)
    for t in range(frames):
        for f in range(group):
            k = t * group + f
            fw1[2 + k] = out_of(2 + k, ft[t, :, f * LANES : (f + 1) * LANES], m.main).astype(BF16)
    out = dot(taps_of(fw1, frames, group), w7[...])
    for t in range(frames):
        y[t] = out[t * spots : (t + 1) * spots]
    s[...] = entry_sums(out, w7.shape[1] - LANES, frames, spots)


def fast_last(m, n, frames, group, lo, at, st, ft, f1, cot, g, b, mk, out, pre, s, nz):
    count = mk[m.fast[0] : m.fast[0] + 1, :]
    mean, rstd = norm_rows(st, at, LANES, count)
    nz[0:1, :] = mean
    nz[1:2, :] = rstd
    gain = g[n : n + 1, lo : lo + LANES]
    bias = b[n : n + 1, lo : lo + LANES]
    mask = mk[m.main[0] : m.main[1], :]
    one = jnp.zeros((8, LANES), F32)
    two = jnp.zeros((8, LANES), F32)
    for t in range(frames):
        for f in range(group):
            k = t * group + f
            hat = (ft[t, :, f * LANES : (f + 1) * LANES].astype(F32) - mean) * rstd
            z = f1[k].astype(F32) + hat * gain + bias
            sigma = sigmoid(z)
            out[k] = z * sigma * mask
            grad = cot[k].astype(F32) * mask * (sigma * (1.0 + z * (1.0 - sigma)))
            pre[k] = grad.astype(BF16)
            one = one + sublane_sums(grad)
            two = two + sublane_sums(grad * hat)
    s[...] = jnp.concatenate([row_sum(one), row_sum(two)], axis=1)


def chunked(total, step, body, init):
    def turn(i, carry):
        return body(pl.multiple_of(i * step, step), carry)

    return lax.fori_loop(0, total // step, turn, init)


def slow_next(n, lo, span, third, xm, nz, g, b, mk, sw):
    spots, wide = third.shape
    mean = nz[0:1, :]
    scale = nz[1:2, :] * g[n : n + 1, lo : lo + wide]
    bias = b[n : n + 1, lo : lo + wide]

    def turn(at, carry):
        mask = widen(mk[pl.ds(span[0] + at, 16), :], 512)
        for c in range(0, wide, 512):
            z = third[pl.ds(at, 16), c : c + 512].astype(F32)
            z = (z - mean[:, c : c + 512]) * scale[:, c : c + 512] + bias[:, c : c + 512]
            z = xm[pl.ds(at, 16), c : c + 512].astype(F32) + z
            sw[pl.ds(at, 16), c : c + 512] = (silu(z) * mask).astype(BF16)
        return carry

    chunked(spots, 16, turn, 0)


def time_partial(frames, sw, wt, fpart):
    spots = sw.shape[1]
    out = dot(flat(sw[0:frames]), wt[0])
    for j in range(1, 3):
        out = out + dot(flat(sw[j : j + frames]), wt[j])
    for t in range(frames):
        fpart[t] = out[t * spots : (t + 1) * spots]


def slow_last(m, n, lo, third, slow, cot, nz, g, b, mk, out, pre, one, two):
    spots, wide = third.shape
    mean, rstd = nz[0:1, :], nz[1:2, :]
    gain = g[n : n + 1, lo : lo + wide]
    bias = b[n : n + 1, lo : lo + wide]

    def turn(at, sums):
        ones, twos = [], []
        mask = widen(mk[pl.ds(m.main[0] + at, 16), :], 512)
        for c in range(0, wide, 512):
            hat = third[pl.ds(at, 16), c : c + 512].astype(F32)
            hat = (hat - mean[:, c : c + 512]) * rstd[:, c : c + 512]
            z = slow[pl.ds(at, 16), c : c + 512].astype(F32) + hat * gain[:, c : c + 512] + bias[:, c : c + 512]
            sigma = sigmoid(z)
            out[pl.ds(at, 16), c : c + 512] = z * sigma * mask
            grad = cot[pl.ds(at, 16), c : c + 512].astype(F32) * mask
            grad = grad * (sigma * (1.0 + z * (1.0 - sigma)))
            pre[pl.ds(at, 16), c : c + 512] = grad.astype(BF16)
            ones.append(sublane_sums(grad))
            twos.append(sublane_sums(grad * hat))
        return sums[0] + jnp.concatenate(ones, axis=1), sums[1] + jnp.concatenate(twos, axis=1)

    one[...], two[...] = chunked(spots, 16, turn, (one[...], two[...]))


def slow_third_grad(m, n, lo, pre, third, n3, gb, g, mk, d3):
    spots, wide = pre.shape
    count = widen(mk[m.slow[0] : m.slow[0] + 1, :], wide)
    mean, rstd = n3[0:1, :], n3[1:2, :]
    scale = g[n : n + 1, lo : lo + wide] * rstd
    one = gb[0:1, :] / count
    two = gb[1:2, :] / count * rstd

    def turn(i, carry):
        mask = widen(mk[pl.ds(m.main[0] + i, 16), :], 512)
        for c in range(0, wide, 512):
            hat = (third[pl.ds(i, 16), c : c + 512].astype(F32) - mean[:, c : c + 512]) * two[:, c : c + 512]
            grad = pre[pl.ds(i, 16), c : c + 512].astype(F32) - mask * (one[:, c : c + 512] + hat)
            d3[pl.ds(i, 16), c : c + 512] = (scale[:, c : c + 512] * grad).astype(BF16)
        return carry

    chunked(spots, 16, turn, 0)


def slow_third_back(m, n, frames, lo, d3, z, n2, wp, g, b, mk, e2, s):
    spots, width = z.shape[1], z.shape[2]
    out = dot_nt(flat(d3[...]), wp[...])
    gain = g[n : n + 1, lo : lo + width]
    bias = b[n : n + 1, lo : lo + width]
    back_act(m, frames, spots, out, z, 0, n2[0:1, :], n2[1:2, :], gain, bias, mk, e2, s)


def back_act(m, frames, spots, out, z, col0, mean, rstd, gain, bias, mk, e, s):
    width = out.shape[1]
    mask = widen(mk[m.main[0] : m.main[1], :], width)
    one = jnp.zeros((8, width), F32)
    two = jnp.zeros((8, width), F32)
    for t in range(frames):
        hat = (z[t, :, col0 : col0 + width] - mean) * rstd
        grad = out[t * spots : (t + 1) * spots] * mask * silu_slope(hat * gain + bias)
        e[t] = grad
        one = one + sublane_sums(grad)
        two = two + sublane_sums(grad * hat)
    s[...] = jnp.concatenate([row_sum(one), row_sum(two)], axis=1)


def fast_third_back(m, n, frames, group, lo3, lo2, at, st, pre, ft, n3, z, n2, wp, g, b, mk, d3, e2, s, gb):
    spots = z.shape[1]
    count = mk[m.fast[0] : m.fast[0] + 1, :]
    one, two = totals(st, at, LANES)
    gb[0:1, :] = one
    gb[1:2, :] = two
    mean, rstd = n3[0:1, :], n3[1:2, :]
    scale = g[n : n + 1, lo3 : lo3 + LANES] * rstd
    one = one / count
    two = two / count * rstd
    mask = mk[m.main[0] : m.main[1], :]
    for t in range(frames):
        for f in range(group):
            hat = (ft[t, :, f * LANES : (f + 1) * LANES] - mean) * two
            grad = pre[t * group + f] - mask * (one + hat)
            d3[t, :, f * LANES : (f + 1) * LANES] = (scale * grad).astype(BF16)
    out = dot_nt(flat(d3[...]), wp[...])
    mean, rstd = n2[0:1, :], n2[1:2, :]
    gain = g[n : n + 1, lo2 : lo2 + LANES]
    bias = b[n : n + 1, lo2 : lo2 + LANES]
    back_act(m, frames, spots, out, z, 0, mean, rstd, gain, bias, mk, e2, s)


def space_back(
    m, n, frames, cols, lo2, lo1, at, width, col0, packed, span,
    st, e, erow, z, zrow, nz, z1, n1, w, g, b, mk, d2, e1, s, gb, vw,
):
    spots = z.shape[1]
    count = widen(mk[span[0] : span[0] + 1, :], width)
    one, two = totals(st, at, width, packed)
    gb[0:1, :] = one
    gb[1:2, :] = two
    mean, rstd = nz[0:1, :], nz[1:2, :]
    scale = g[n : n + 1, lo2 : lo2 + width] * rstd
    one = one / count
    two = two / count * rstd
    mask = widen(mk[m.ext[0] : m.ext[1], :], width)
    for t in range(frames):
        grad = jnp.concatenate([erow[t], e[t], erow[t]], axis=0)
        value = jnp.concatenate([zrow[t], z[t], zrow[t]], axis=0)
        grad = scale * mask * (grad - (one + (value - mean) * two))
        d2[t] = grad[cols : cols + spots].astype(BF16)
        store_shifts(vw, t, grad.astype(BF16).astype(F32), cols)
    total = None
    for i in range(3):
        rows = (2 - i) * cols
        for j in range(3):
            lane = (2 - j) * width
            part = dot_nt(flat(vw[:, rows : rows + spots, lane : lane + width]), w[i, j * width : (j + 1) * width, :])
            total = part if total is None else total + part
    mean, rstd = n1[0:1, :], n1[1:2, :]
    gain = g[n : n + 1, lo1 : lo1 + width]
    bias = b[n : n + 1, lo1 : lo1 + width]
    back_act(m, frames, spots, total, z1, col0, mean, rstd, gain, bias, mk, e1, s)


def first_taps(frames, dw):
    return [flat(dw[2 - j : 2 - j + frames]) for j in range(3)]


def time_back(taps, wt, lo, size):
    out = dot_nt(taps[0], wt[0, lo : lo + size, :])
    for j in range(1, 3):
        out = out + dot_nt(taps[j], wt[j, lo : lo + size, :])
    return out


def slow_first_back(m, n, frames, lo1, at, st, e, ep, en, z, zp, zn, n1, wt, y, nl, g, b, mk, dw, el, s, gb):
    spots, width = z.shape[1], z.shape[2]
    lat = nl.shape[1]
    wide = wt.shape[1] - lat
    count = widen(mk[m.slow[0] : m.slow[0] + 1, :], width)
    one, two = totals(st, at, width)
    gb[0:1, :] = one
    gb[1:2, :] = two
    mean, rstd = n1[0:1, :], n1[1:2, :]
    scale = g[n : n + 1, lo1 : lo1 + width] * rstd
    one = one / count
    two = two / count * rstd
    sources = (
        [(ep, zp, m.prev)] + [(e.at[t], z.at[t], m.main) for t in range(frames)] + [(en, zn, m.next)]
    )
    for k, (grad, value, span) in enumerate(sources):
        mask = widen(mk[span[0] : span[1], :], width)
        dw[k] = (scale * mask * (grad[...] - (one + (value[...] - mean) * two))).astype(BF16)
    out = time_back(first_taps(frames, dw), wt, wide, lat)
    back_act(
        m, frames, spots, out, y, 0, nl[0:1, :], nl[1:2, :], g[n : n + 1, 0:lat], b[n : n + 1, 0:lat], mk, el, s
    )


def slow_input_last(m, frames, dw, wt, pre, mk, gx):
    spots, wide = pre.shape[1], pre.shape[2]
    taps = first_taps(frames, dw)
    mask = widen(mk[m.main[0] : m.main[1], :], 256)
    for c in range(0, wide, 256):
        out = time_back(taps, wt, c, 256)
        for t in range(frames):
            gx[t, :, c : c + 256] = (out[t * spots : (t + 1) * spots] + pre[t, :, c : c + 256]) * mask


def slow_input_back(m, n, frames, lo, at, dw, wt, pre, xm, third, n3, g, b, mk, pre0, s):
    spots = pre.shape[1]
    wide = s.shape[1] // 2
    mask = widen(mk[m.main[0] : m.main[1], :], 256)
    out = time_back(first_taps(frames, dw), wt, 0, 256)
    mean, rstd = n3[0:1, at : at + 256], n3[1:2, at : at + 256]
    gain = g[n - 1 : n, lo + at : lo + at + 256]
    bias = b[n - 1 : n, lo + at : lo + at + 256]
    one = jnp.zeros((8, 256), F32)
    two = jnp.zeros((8, 256), F32)
    for t in range(frames):
        grad = (out[t * spots : (t + 1) * spots] + pre[t].astype(F32)) * mask
        hat = (third[t].astype(F32) - mean) * rstd
        z0 = xm[t].astype(F32) + hat * gain + bias
        grad = grad * silu_slope(z0)
        pre0[t] = grad.astype(BF16)
        one = one + sublane_sums(grad)
        two = two + sublane_sums(grad * hat)
    s[:, at : at + 256] = row_sum(one)
    s[:, wide + at : wide + at + 256] = row_sum(two)


def fast_first_back(
    m, n, frames, lo1, at1, atl, st1, stl, el, eln, ef, efp, efn, y, yp, yn, nl, n1, gs, g, mk,
    dl, dfw, dln, dfp, dfn, gbl, gb1,
):
    lat = nl.shape[1]
    count = widen(mk[m.slow[0] : m.slow[0] + 1, :], lat)
    one, two = totals(stl, atl, lat)
    gbl[0:1, :] = one
    gbl[1:2, :] = two
    mean, rstd = nl[0:1, :], nl[1:2, :]
    scale = gs[n : n + 1, 0:lat] * rstd
    one = one / count
    two = two / count * rstd

    def lat_grad(grad, value, span):
        mask = widen(mk[span[0] : span[1], :], lat)
        return (scale * mask * (grad - (one + (value - mean) * two))).astype(BF16)

    for t in range(frames):
        dl[t] = lat_grad(el[t], y[t, :, 0:lat], m.main)
    dln[...] = lat_grad(eln[...], yn[:, 0:lat], m.next)
    fcount = mk[m.fast[0] : m.fast[0] + 1, :]
    fone, ftwo = totals(st1, at1, LANES, True)
    gb1[0:1, :] = fone
    gb1[1:2, :] = ftwo
    fmean, frstd = n1[0:1, :], n1[1:2, :]
    fscale = g[n : n + 1, lo1 : lo1 + LANES] * frstd
    fone = fone / fcount
    ftwo = ftwo / fcount * frstd

    def first_grad(grad, value, span):
        mask = mk[span[0] : span[1], :]
        return (fscale * mask * (grad - (fone + (value - fmean) * ftwo))).astype(BF16)

    for t in range(frames):
        dfw[t] = first_grad(ef[t], y[t, :, lat:], m.main)
    dfp[...] = first_grad(efp[...], yp[:, lat:], m.prev)
    dfn[...] = first_grad(efn[...], yn[:, lat:], m.next)


def fast_input_back(m, n, frames, group, lo3, last, dl, dfw, dln, dfp, dfn, w7, pre, *rest):
    if last:
        mk, gx, buf = rest
    else:
        fw0, ft, n3, g, b, mk, pre0, s, buf = rest
    spots, lat = dl.shape[1], dl.shape[2]
    both = jnp.concatenate([flat(dl[...]), flat(dfw[...])], axis=1)
    buf[...] = jnp.zeros(buf.shape, F32)
    out = dot_nt(both, w7[...])
    for t in range(frames):
        for f in range(7):
            k = group * t + f
            buf[k] = buf[k] + out[t * spots : (t + 1) * spots, f * LANES : (f + 1) * LANES]
    buf[2] = buf[2] + dot_nt(dfp[...], w7[6 * LANES : 7 * LANES, lat:])
    after = dot_nt(jnp.concatenate([dln[...], dfn[...]], axis=1), w7[0 : 2 * LANES, :])
    total = frames * group
    for f in range(2):
        buf[total + f] = buf[total + f] + after[:, f * LANES : (f + 1) * LANES]
    mask = mk[m.main[0] : m.main[1], :]
    if last:
        for k in range(total):
            gx[k] = (pre[k] + buf[2 + k]) * mask
        return
    mean, rstd = n3[0:1, :], n3[1:2, :]
    gain = g[n - 1 : n, lo3 : lo3 + LANES]
    bias = b[n - 1 : n, lo3 : lo3 + LANES]
    one = jnp.zeros((8, LANES), F32)
    two = jnp.zeros((8, LANES), F32)
    for k in range(total):
        t, f = k // group, k % group
        hat = (ft[t, :, f * LANES : (f + 1) * LANES] - mean) * rstd
        z0 = fw0[2 + k].astype(F32) + hat * gain + bias
        grad = (pre[k] + buf[2 + k]) * mask * silu_slope(z0)
        pre0[k] = grad.astype(BF16)
        one = one + sublane_sums(grad)
        two = two + sublane_sums(grad * hat)
    s[...] = jnp.concatenate([row_sum(one), row_sum(two)], axis=1)


def point_weights(a2, d3, out):
    acts = flat(a2[...])
    for k in range(out.shape[0]):
        out[k] = dot_tn(acts, flat(d3[:, :, k * 256 : (k + 1) * 256])).astype(BF16)


def space_weights(cols, aw, d2, out, vw):
    frames, spots, width = d2.shape
    for t in range(frames):
        store_shifts(vw, t, aw[t].astype(F32), cols)
    grads = flat(d2[...])
    for i in range(3):
        out[i] = dot_tn(flat(vw[:, i * cols : i * cols + spots, :]), grads).astype(BF16)


def time_weights(skip, slow, jl, dw, out):
    frames, spots, width = jl.shape
    wide = slow.shape[2]
    grads = jnp.concatenate([flat(dw[2 - j : 2 - j + frames]) for j in range(3)], axis=1)
    for c in range(0, wide + jl.shape[2], 256):
        if c < wide:
            acts = flat(slow[skip : skip + frames, :, c : c + 256])
        else:
            acts = flat(jl[:, :, c - wide : c - wide + 256])
        got = dot_tn(acts, grads)
        for j in range(3):
            out[j, c : c + 256, :] = got[:, j * width : (j + 1) * width].astype(BF16)


def group_blocks(value, group):
    size = LANES // group
    rows = lax.broadcasted_iota(jnp.int32, (LANES, LANES), 0) >> (size.bit_length() - 1)
    lanes = lax.broadcasted_iota(jnp.int32, (LANES, LANES), 1) >> (size.bit_length() - 1)
    kept = jnp.where(rows == lanes, value, 0.0)
    kept = kept + pltpu.roll(kept, 64, 1)
    kept = kept + pltpu.roll(kept, 32, 1)
    total = kept[0:size]
    for k in range(1, group):
        total = total + kept[k * size : (k + 1) * size]
    return total


def at_lanes(blocks):
    lanes = lax.broadcasted_iota(jnp.int32, blocks[0].shape, 1) >> 5
    out = jnp.zeros(blocks[0].shape, F32)
    for k, block in enumerate(blocks):
        out = jnp.where(lanes == k, block, out)
    return out


def fast_weights(group, cols, lat, fw, dl, df, fa1, d2, fa2, d3, out, vw):
    frames, spots, _ = dl.shape
    size = LANES // group
    both = jnp.concatenate([flat(dl[...]), flat(df[...])], axis=1)
    taps = [[None] * group for _ in range(3)]
    for f in range(7):
        acts = jnp.concatenate([fw[group * t + f] for t in range(frames)], axis=0)
        got = dot_tn(acts, both)
        if f < 5:
            out[f * LANES : (f + 1) * LANES, :] = got[:, :lat].astype(BF16)
        for k in range(group):
            if 0 <= f - k - 1 < 3:
                taps[f - k - 1][k] = got[:, lat:]
    lanes = lax.broadcasted_iota(jnp.int32, (LANES, LANES), 1) >> (size.bit_length() - 1)
    tap_sums = []
    for j in range(3):
        kept = jnp.zeros((LANES, LANES), F32)
        for k in range(group):
            kept = jnp.where(lanes == k, taps[j][k], kept)
        kept = kept + pltpu.roll(kept, 64, 1)
        tap_sums.append(kept + pltpu.roll(kept, 32, 1))
    low = 5 * LANES
    out[low : low + LANES, 0:LANES] = at_lanes(tap_sums).T.astype(BF16)
    for t in range(frames):
        store_shifts(vw, t, fa1[t].astype(F32), cols)
    grads = flat(d2[...])
    for i in range(3):
        got = dot_tn(flat(vw[:, i * cols : i * cols + spots, :]), grads)
        blocks = [group_blocks(got[j * LANES : (j + 1) * LANES], group) for j in range(3)]
        out[low + size * i : low + size * (i + 1), LANES : 2 * LANES] = at_lanes(blocks).astype(BF16)
    acts = flat(fa2[...])
    total = jnp.zeros((size, LANES), F32)
    for k in range(group):
        got = dot_tn(acts, flat(d3[:, :, k * LANES : (k + 1) * LANES]))
        total = total + got[k * size : (k + 1) * size]
    out[low + 3 * size : low + 4 * size, LANES : 2 * LANES] = total.astype(BF16)


def unpack_fast(n, inner, load, outs):
    glat, gft, gfs, gfp = outs
    low = glat.shape[1]
    for at in range(0, low, inner):
        glat[n, at : at + inner, :] = load(at, inner)
    for i in range(4):
        got = load(low + inner * i, inner)
        if i < 3:
            gft[n, i] = got[:, 0:LANES]
            for j in range(3):
                moved = got[:, LANES:] if j == 0 else pltpu.roll(got[:, LANES:], LANES - inner * j, 1)
                gfs[n, 3 * i + j] = moved[:, 0:inner]
        else:
            gfp[n] = got[:, LANES:]


def runs_of(at, count, base, half, one, two):
    found = []
    while count:
        core, row = at // half, base + at % half
        ref, size = one, one.shape[1]
        if row >= 4 * size:
            ref, row = two, row - 4 * size
            size = two.shape[1]
        block, row = core * 4 + row // size, row % size
        here = min(count, size - row, half - at % half)
        found.append((ref, block, row, here))
        at, count = at + here, count - here
    return found


def rows_of(base, half, one, two=None):
    def load(at, count):
        parts = [
            ref[block, row : row + here, :].astype(F32)
            for ref, block, row, here in runs_of(at, count, base, half, one, two)
        ]
        return parts[0] if len(parts) == 1 else jnp.concatenate(parts, axis=0)

    return load


def copy_rows(start, one, out):
    for at in range(0, out.shape[0], 256):
        out[at : at + 256, :] = one[start + at : start + at + 256, :].astype(F32)


def copy_columns(start, one, out):
    for at in range(0, out.shape[1], 256):
        out[:, at : at + 256] = one[start + at : start + at + 256, :].astype(F32)


def place_rows(start, base, half, one, two, out):
    at = 0
    for ref, block, row, here in runs_of(start, out.shape[0], base, half, one, two):
        out[at : at + here, :] = ref[block, row : row + here, :].astype(F32)
        at += here


def place_columns(start, base, half, one, two, out):
    for lane in range(0, out.shape[1], 256):
        at = 0
        for ref, block, row, here in runs_of(start + lane, 256, base, half, one, two):
            out[at : at + here, lane : lane + 256] = ref[block, row : row + here, :].astype(F32)
            at += here


def place_fast(inner, half_mid, half_late, start, mid_one, mid_two, one, two, *outs):
    unpack_fast(1, inner, rows_of(0, half_mid, mid_one, mid_two), outs)
    load = rows_of(0, half_late, one, two)
    unpack_fast(0, inner, lambda at, count: load(start + at, count), outs)


def assemble_norms(inner, *refs):
    sums, (gs, bs, gf, bf) = refs[:-4], refs[-4:]
    lanes = lax.broadcasted_iota(jnp.int32, (8, LANES), 1) >> (inner.bit_length() - 1)
    for n in range(2):
        slow, fast = sums[7 * n : 7 * n + 4], sums[7 * n + 4 : 7 * n + 7]
        for row, gslow, gfast in ((1, gs, gf), (0, bs, bf)):
            at = 0
            for part in slow:
                gslow[n : n + 1, at : at + part.shape[1]] = part[row : row + 1, :]
                at += part.shape[1]
            one, two, three = [jnp.broadcast_to(part[row : row + 1, :], (8, LANES)) for part in fast]
            three = pltpu.roll(three, 2 * inner, 1)
            head = jnp.where(lanes == 0, one, jnp.where(lanes == 1, two, three))
            gfast[n : n + 1, 0:LANES] = head[0:1]
            gfast[n : n + 1, LANES : LANES + 2 * inner] = three[0:1, 0 : 2 * inner]


def on_device(
    x_slow,
    x_fast,
    w_lateral,
    w_slow_time,
    w_slow_space,
    w_slow_point,
    w_fast_time,
    w_fast_space,
    w_fast_point,
    gain_slow,
    bias_slow,
    gain_fast,
    bias_fast,
    clip_size,
    cot_slow,
    cot_fast,
):
    frames, fast_frames = x_slow.shape[0], x_fast.shape[0]
    group = fast_frames // frames
    rows, cols = x_slow.shape[3], x_slow.shape[4]
    spots = rows * cols
    wide, fwide = x_slow.shape[5], x_fast.shape[5]
    lat = w_lateral.shape[3]
    width = w_slow_space.shape[3]
    inner = w_fast_space.shape[3]
    packs = group * fwide
    both = lat + LANES
    m = Masks(spots, cols)
    devices = lax.axis_size("path") * lax.axis_size("rows")
    path = lax.axis_index("path")
    ext = spots + 2 * cols
    lo1, lo2, lo3 = lat, lat + width, lat + 2 * width
    every = slice(None)

    def part(fn, *static):
        return functools.partial(fn, *static)

    xs = x_slow.reshape(frames, spots, wide)
    xf = x_fast.reshape(fast_frames, spots, fwide)
    cs = cot_slow.reshape(frames, spots, wide)
    cf = cot_fast.reshape(fast_frames, spots, fwide)
    wft = jnp.swapaxes(w_fast_time, 2, 3)
    wfs_raw = w_fast_space.reshape(2, 9, inner, inner)
    wsp = w_slow_space.reshape(2, 3, 3 * width, width)

    def packed(value):
        return jnp.concatenate(
            [value[:, 0:inner]] * group + [value[:, inner : 2 * inner]] * group + [value[:, 2 * inner :]],
            axis=1,
        )

    xf_edge = swap_path(jnp.where(path > 0, xf[:2], xf[-2:]))
    xs_edge = swap_path(jnp.where(path > 0, xs[0], xs[-1]))

    def payload(k, *sums):
        size = sum(k.temps[s[1]].shape[1] for s in sums)
        out = k.give((devices, 1, size))
        k.step(spread_sums, *sums, out)
        return out

    def row_out(k, z, mk, col0, size):
        out = k.give((frames, cols, size))
        k.step(part(own_row, m, spots, cols, col0, size), z, mk, out)
        return out

    def edge_out(k, z, mk, size, tail=0):
        out = k.give((spots, size), BF16)
        k.step(part(own_edge, m, 0, tail), z, mk, out)
        return out

    def finish(k, **handles):
        got = k.run()
        return {name: got[handle[1]] for name, handle in handles.items()}

    def other_row(value):
        return swap(value, "rows", 1)

    first_flops = 2 * frames * spots * 7 * fwide * both
    k = Stage("entry")
    mk_out = k.give((m.rows, LANES))
    place = jnp.stack([lax.axis_index("rows"), path]).astype(jnp.int32)
    k.step(
        part(make_masks, m, rows, cols, lax.axis_size("path") - 1), k.scalar(place), k.scalar(clip_size), mk_out
    )
    w7_out = k.give((7 * fwide, both), BF16)
    k.step(part(make_w7, lat, group), k.take(w_lateral, 0), k.take(wft, 0), w7_out)
    fw = k.give((fast_frames + 4, spots, fwide), BF16)
    y = k.give((frames, spots, both))
    sy = k.temp((1, 2 * both))
    edge = k.take(xf_edge)
    k.step(
        part(fast_entry, m, frames, group), k.take(xf), edge, edge, mk_out, w7_out, fw, y, sy, flops=first_flops
    )
    pay = payload(k, sy)
    got = finish(
        k, mk=mk_out, w7=w7_out, fw=fw, y=y, pay=pay, ff_row=row_out(k, y, mk_out, lat, LANES),
        edge=edge_out(k, y, mk_out, both),
    )
    mk = got["mk"]
    saved = [{"fw": got["fw"], "y": got["y"], "w7": got["w7"]}, {}]
    st = gather_sums(got["pay"])
    saved[0]["ff_row"] = other_row(got["ff_row"])
    saved[0]["y_edge"] = swap_path(got["edge"])
    mk, wft, gain_fast, bias_fast = lax.optimization_barrier((mk, wft, gain_fast, bias_fast))
    gf, bf = packed(gain_fast), packed(bias_fast)
    k = Stage("prepare")
    w7_out = k.give((7 * fwide, both), BF16)
    k.step(part(make_w7, lat, group), k.take(w_lateral, 1), k.take(wft, 1), w7_out)
    blocks = []
    for n in range(2):
        blocks += [k.give((3, 3 * LANES, LANES), BF16), k.give((LANES, packs), BF16)]
        k.step(part(make_blocks, group), k.take(wfs_raw, n), k.take(w_fast_point, n), *blocks[-2:])
    got = finish(k, w7=w7_out, wfs0=blocks[0], wfp0=blocks[1], wfs1=blocks[2], wfp1=blocks[3])
    saved[1]["w7"] = got["w7"]
    wfs, wfp = [got["wfs0"], got["wfs1"]], [got["wfp0"], got["wfp1"]]
    k = Stage("slow_partial")
    xm = k.give((frames + 2, spots, wide), BF16)
    fpart = k.give((frames, spots, width))
    edge = k.take(xs_edge)
    k.step(
        part(slow_partial, m, frames),
        k.take(xs), edge, edge, k.take(mk), k.take(w_slow_time, 0, every, slice(0, wide)), xm, fpart,
        flops=2 * frames * spots * 3 * wide * width,
    )
    got = finish(k, sw=xm, fpart=fpart)
    saved[0]["sw"] = got["sw"]
    fpart_in = got["fpart"]

    for n in range(2):
        v = saved[n]
        k = Stage("join")
        mk_in, gs, bs = k.take(mk), k.take(gain_slow), k.take(bias_slow)
        st_in = k.take(st)
        names = {}
        if n == 0:
            fpart = k.take(fpart_in)
        else:
            fpart = k.temp((frames, spots, width))
            n3, next_sw = k.give((2, wide)), k.give((frames + 2, spots, wide), BF16)
            names.update(sw=next_sw, n3=n3)
            k.step(part(keep_norm, 2 * both, wide, m.slow), st_in, mk_in, n3)
            spans = [m.prev] + [m.main] * frames + [m.next]
            for f in range(frames + 2):
                k.step(
                    part(slow_next, 0, lo3, spans[f]),
                    k.take(saved[0]["third"], f), k.take(saved[0]["sw"], f), k.peek(n3), gs, bs, mk_in,
                    k.piece(next_sw, f),
                )
            k.step(
                part(time_partial, frames),
                k.peek(next_sw), k.take(w_slow_time, 1, every, slice(0, wide)), fpart,
                flops=2 * frames * spots * 3 * wide * width,
            )
        y_in, edge = k.take(v["y"]), k.take(v["y_edge"])
        jl = k.give((frames, spots, lat), BF16)
        first = k.give((frames, spots, width))
        nl = k.give((2, lat))
        s_first, s_fs = k.temp((1, 2 * width)), k.temp((1, 2 * LANES))
        k.step(
            part(lat_join, m, n, frames, lat),
            st_in, y_in, edge, edge, fpart, k.take(w_slow_time, n, every, slice(wide, wide + lat)), gs, bs, mk_in,
            jl, first, s_first, nl, k.temp((frames + 2, spots, lat), BF16),
            flops=2 * frames * spots * 3 * lat * width,
        )
        fa1 = k.give((frames, ext, LANES), BF16)
        fs = k.give((frames, spots, LANES))
        nf1 = k.give((2, LANES))
        k.step(
            part(space_forward, m, n, frames, cols, 0, 2 * lat, LANES, lat, True, m.fast),
            st_in, y_in, k.take(v["ff_row"]), k.take(wfs[n]), k.take(gf), k.take(bf), mk_in,
            fa1, fs, s_fs, nf1, k.temp((frames, ext, 3 * LANES), BF16),
            flops=2 * frames * spots * 9 * LANES * LANES,
        )
        pay = payload(k, s_first, s_fs)
        got = finish(
            k, jl=jl, first=first, nl=nl, fa1=fa1, fs=fs, nf1=nf1, pay=pay,
            first_row=row_out(k, first, mk_in, 0, width), fs_row=row_out(k, fs, mk_in, 0, LANES),
            first_edge=edge_out(k, first, mk_in, width), **names,
        )
        st = gather_sums(got["pay"])
        for name in ("jl", "first", "nl", "fa1", "fs", "nf1"):
            v[name] = got[name]
        if n == 1:
            saved[1]["sw"], saved[0]["n3"] = got["sw"], got["n3"]
        first_row = other_row(got["first_row"])
        st, v["fs_row"], v["first_edge"] = lax.optimization_barrier(
            (st, other_row(got["fs_row"]), swap_path(got["first_edge"]))
        )
        k = Stage("space")
        mk_in, st_in = k.take(mk), k.take(st)
        a1 = k.give((frames, ext, width), BF16)
        second = k.give((frames, spots, width))
        n1 = k.give((2, width))
        s_second, s_ft = k.temp((1, 2 * width)), k.temp((1, 2 * LANES))
        k.step(
            part(space_forward, m, n, frames, cols, lo1, 0, width, 0, False, m.slow),
            st_in, k.take(v["first"]), k.take(first_row), k.take(wsp, n), k.take(gain_slow), k.take(bias_slow), mk_in,
            a1, second, s_second, n1, k.temp((frames, ext, 3 * width), BF16),
            flops=2 * frames * spots * 9 * width * width,
        )
        fa2 = k.give((frames, spots, LANES), BF16)
        ft = k.give((frames, spots, packs), BF16)
        nf2 = k.give((2, LANES))
        k.step(
            part(fast_third, m, n, frames, LANES, 2 * width),
            st_in, k.take(v["fs"]), k.take(wfp[n]), k.take(gf), k.take(bf), mk_in, fa2, ft, s_ft, nf2,
            flops=2 * frames * spots * LANES * packs,
        )
        pay = payload(k, s_second, s_ft)
        names = {"second_row": row_out(k, second, mk_in, 0, width)}
        if n == 0:
            names["second_edge"] = edge_out(k, second, mk_in, width)
            names["ft_edge"] = edge_out(k, ft, mk_in, 2 * fwide, (group - 2) * fwide)
        got = finish(k, a1=a1, second=second, n1=n1, fa2=fa2, ft=ft, nf2=nf2, pay=pay, **names)
        st = gather_sums(got["pay"])
        for name in ("a1", "second", "n1", "fa2", "ft", "nf2"):
            v[name] = got[name]
        st, v["second_row"] = lax.optimization_barrier((st, other_row(got["second_row"])))
        halo = 1 - n
        edges = []
        k = Stage("third")
        if n == 0:
            ft_edge = k.take(swap_path(got["ft_edge"]))
            edges = [k.take(swap_path(got["second_edge"]))] * 2
        mk_in, st_in = k.take(mk), k.take(st)
        a2 = k.give((frames, spots, width), BF16)
        third = k.give((frames + 2 * halo, spots, wide), BF16)
        n2 = k.give((2, width))
        nf3 = k.give((2, LANES))
        s_third = k.temp((1, 2 * wide))
        names = {}
        if n == 0:
            names.update(
                fw=k.give((fast_frames + 4, spots, fwide), BF16),
                y=k.give((frames, spots, both)),
            )
            s_fast = k.temp((1, 2 * both))
            k.step(
                part(fast_next, m, n, frames, group, 2 * LANES, 2 * width),
                st_in, k.take(v["ft"]), ft_edge, ft_edge, k.take(v["fw"]), k.take(saved[1]["w7"]),
                k.take(gf), k.take(bf), mk_in, names["fw"], names["y"], s_fast, nf3,
                flops=first_flops,
            )
        else:
            names.update(out_fast=k.give((fast_frames, spots, fwide)), pre_f=k.give((fast_frames, spots, fwide), BF16))
            s_fast = k.temp((1, 2 * LANES))
            k.step(
                part(fast_last, m, n, frames, group, 2 * LANES, 2 * width),
                st_in, k.take(v["ft"]), k.take(v["fw"], slice(2, 2 + fast_frames)), k.take(cf), k.take(gf), k.take(bf), mk_in,
                names["out_fast"], names["pre_f"], s_fast, nf3,
            )
        aw = k.temp((frames + 2 * halo, spots, width), BF16)
        k.step(
            part(slow_acts, m, n, frames, lo2, halo),
            st_in, k.take(v["second"]), *edges, k.take(gain_slow), k.take(bias_slow), mk_in, a2, n2, aw,
        )
        for at in range(0, wide, 256):
            lanes = slice(at, at + 256)
            k.step(
                part(slow_third, frames, halo, at),
                aw, k.take(w_slow_point, n, every, lanes), k.piece(third, every, every, lanes), s_third,
                flops=2 * frames * spots * width * 256,
            )
        if n == 0:
            pay = payload(k, s_fast, s_third)
            names["ff_row"] = row_out(k, names["y"], mk_in, lat, LANES)
            names["y_edge"] = edge_out(k, names["y"], mk_in, both)
        else:
            pay = payload(k, s_third, s_fast)
        got = finish(k, a2=a2, third=third, n2=n2, nf3=nf3, pay=pay, **names)
        st = gather_sums(got["pay"])
        for name in ("a2", "third", "n2", "nf3"):
            v[name] = got[name]
        if n == 0:
            saved[1].update(
                fw=got["fw"], y=got["y"], ff_row=other_row(got["ff_row"]), y_edge=swap_path(got["y_edge"])
            )
        else:
            out_fast, pre_f = got["out_fast"], got["pre_f"]

    def third_back(k, n, at, st_in, mk_in, pre):
        v = saved[n]
        d3, e2 = k.give((frames, spots, wide), BF16), k.give((frames, spots, width))
        s, gb = k.temp((1, 2 * width)), k.give((2, wide))
        gs = k.take(gain_slow)
        k.step(part(keep_sums, at, wide), st_in, gb)
        for t in range(frames):
            k.step(
                part(slow_third_grad, m, n, lo3),
                k.take(pre, t), k.take(v["third"], t + 1 - n), k.take(v["n3"]), k.peek(gb), gs, mk_in,
                k.piece(d3, t),
            )
        k.step(
            part(slow_third_back, m, n, frames, lo2),
            k.peek(d3), k.take(v["second"]), k.take(v["n2"]), k.take(w_slow_point, n), gs, k.take(bias_slow), mk_in,
            e2, s, flops=2 * frames * spots * width * wide,
        )
        return dict(d3=d3, e2=e2, gb3=gb), s

    def fast_back3(k, n, at, st_in, mk_in, pre):
        v = saved[n]
        d3, e2 = k.give((frames, spots, packs), BF16), k.give((frames, spots, LANES))
        s, gb = k.temp((1, 2 * LANES)), k.give((2, LANES))
        k.step(
            part(fast_third_back, m, n, frames, group, 2 * LANES, LANES, at),
            st_in, k.take(pre), k.take(v["ft"]), k.take(v["nf3"]), k.take(v["fs"]), k.take(v["nf2"]),
            k.take(wfp[n]), k.take(gf), k.take(bf), mk_in, d3, e2, s, gb,
            flops=2 * frames * spots * LANES * packs,
        )
        return dict(d3f=d3, ef2=e2, gbf3=gb), s

    def second_back(k, n, at, st_in, mk_in, e2, e2_row):
        v = saved[n]
        d2, e1 = k.give((frames, spots, width), BF16), k.give((frames, spots, width))
        s, gb = k.temp((1, 2 * width)), k.give((2, width))
        k.step(
            part(space_back, m, n, frames, cols, lo2, lo1, at, width, 0, False, m.slow),
            st_in, k.take(e2), k.take(e2_row), k.take(v["second"]), k.take(v["second_row"]), k.take(v["n2"]),
            k.take(v["first"]), k.take(v["n1"]), k.take(wsp, n), k.take(gain_slow), k.take(bias_slow), mk_in,
            d2, e1, s, gb, k.temp((frames, ext, 3 * width), BF16),
            flops=2 * frames * spots * 9 * width * width,
        )
        return dict(d2=d2, e1=e1, gb2=gb), s

    def fast_back2(k, n, at, st_in, mk_in, ef2, ef2_row):
        v = saved[n]
        d2, e1 = k.give((frames, spots, LANES), BF16), k.give((frames, spots, LANES))
        s, gb = k.temp((1, 2 * LANES)), k.give((2, LANES))
        k.step(
            part(space_back, m, n, frames, cols, LANES, 0, at, LANES, lat, True, m.fast),
            st_in, k.take(ef2), k.take(ef2_row), k.take(v["fs"]), k.take(v["fs_row"]), k.take(v["nf2"]),
            k.take(v["y"]), k.take(v["nf1"]), k.take(wfs[n]), k.take(gf), k.take(bf), mk_in,
            d2, e1, s, gb, k.temp((frames, ext, 3 * LANES), BF16),
            flops=2 * frames * spots * 9 * LANES * LANES,
        )
        return dict(d2f=d2, ef1=e1, gbf2=gb), s

    def first_back(k, n, st_in, mk_in, e1, e1_edge):
        v = saved[n]
        dw, el = k.give((frames + 2, spots, width), BF16), k.give((frames, spots, lat))
        s, gb = k.temp((1, 2 * lat)), k.give((2, width))
        edge, zedge = k.take(e1_edge), k.take(v["first_edge"])
        k.step(
            part(slow_first_back, m, n, frames, lo1, 0),
            st_in, k.take(e1), edge, edge, k.take(v["first"]), zedge, zedge, k.take(v["n1"]),
            k.take(w_slow_time, n, every, slice(wide, wide + lat)), k.take(v["y"]), k.take(v["nl"]),
            k.take(gain_slow), k.take(bias_slow), mk_in, dw, el, s, gb, flops=2 * frames * spots * 3 * lat * width,
        )
        return dict(dw=dw, el=el, gb1=gb), s

    def fast_back1(k, n, st1, at1, stl, atl, mk_in, el, el_edge, ef1, ef1_edge):
        v = saved[n]
        dl, df = k.give((frames, spots, lat), BF16), k.give((frames, spots, LANES), BF16)
        beside = [k.give((spots, lat), BF16), k.give((spots, LANES), BF16), k.give((spots, LANES), BF16)]
        gbl, gb1 = k.give((2, lat)), k.give((2, LANES))
        edge, yedge = k.take(ef1_edge), k.take(v["y_edge"])
        k.step(
            part(fast_first_back, m, n, frames, 0, at1, atl),
            st1, stl, k.take(el), k.take(el_edge), k.take(ef1), edge, edge, k.take(v["y"]), yedge, yedge,
            k.take(v["nl"]), k.take(v["nf1"]), k.take(gain_slow), k.take(gf), mk_in, dl, df, *beside, gbl, gb1,
        )
        return dict(dl=dl, df=df, dln=beside[0], dfp=beside[1], dfn=beside[2], gbl=gbl, gbf1=gb1)

    def weights_point(n, d3):
        k = Stage("point_weights")
        out = k.give((wide // 256, width, 256), BF16)
        k.step(point_weights, k.take(saved[n]["a2"]), k.take(d3), out, flops=2 * frames * spots * width * wide)
        return k.run()[0].reshape(-1, 256)

    def weights_space(n, d2):
        k = Stage("space_weights")
        out = k.give((3, 3 * width, width), BF16)
        k.step(
            part(space_weights, cols), k.take(saved[n]["a1"]), k.take(d2), out,
            k.temp((frames, ext, 3 * width), BF16), flops=2 * frames * spots * 9 * width * width,
        )
        return k.run()[0].reshape(-1, 256)

    def weights_time(n, dw):
        k = Stage("time_weights")
        out = k.give((3, wide + lat, width), BF16)
        k.step(
            part(time_weights, 1), k.take(saved[n]["sw"]), k.take(saved[n]["jl"]), k.take(dw), out,
            flops=2 * frames * spots * 3 * (wide + lat) * width,
        )
        return k.run()[0].reshape(-1, 256)

    def weights_fast(n, dl, df, d2, d3):
        v = saved[n]
        k = Stage("fast_weights")
        out = k.give((7 * LANES - LANES, 2 * LANES), BF16)
        k.step(
            part(fast_weights, group, cols, lat),
            k.take(v["fw"]), k.take(dl), k.take(df), k.take(v["fa1"]), k.take(d2), k.take(v["fa2"]), k.take(d3),
            out, k.temp((frames, ext, 3 * LANES), BF16), flops=first_flops,
        )
        return k.run()[0]

    b1, b0 = {}, {}
    k = Stage("last")
    mk_in, st_in = k.take(mk), k.take(st)
    out_slow, pre = k.give((frames, spots, wide)), k.give((frames, spots, wide), BF16)
    n3 = k.give((2, wide))
    s_pre, one, two = k.temp((1, 2 * wide)), k.temp((8, wide)), k.temp((8, wide))
    k.step(part(keep_norm, 0, wide, m.slow), st_in, mk_in, n3)
    k.step(clear, one, two)
    for t in range(frames):
        k.step(
            part(slow_last, m, 1, lo3),
            k.take(saved[1]["third"], t), k.take(saved[1]["sw"], t + 1), k.take(cs, t), k.peek(n3),
            k.take(gain_slow), k.take(bias_slow), mk_in, k.piece(out_slow, t), k.piece(pre, t), one, two,
        )
    k.step(close_sums, one, two, s_pre)
    names, s_ef2 = fast_back3(k, 1, 2 * wide, st_in, mk_in, pre_f)
    pay = payload(k, s_pre, s_ef2)
    ef2_row = row_out(k, names["ef2"], mk_in, 0, LANES)
    b1 = finish(k, out_slow=out_slow, pre=pre, n3=n3, pay=pay, ef2_row=ef2_row, **names)
    saved[1]["n3"] = b1["n3"]
    out_slow = b1["out_slow"]
    st = gather_sums(b1["pay"])

    k = Stage("back_third")
    ef2_row = other_row(b1["ef2_row"])
    mk_in, st_in = k.take(mk), k.take(st)
    names, s_e2 = third_back(k, 1, 0, st_in, mk_in, b1["pre"])
    more, s_ef1 = fast_back2(k, 1, 2 * wide, st_in, mk_in, b1["ef2"], ef2_row)
    pay = payload(k, s_e2, s_ef1)
    e2_row, ef1_edge = row_out(k, names["e2"], mk_in, 0, width), edge_out(k, more["ef1"], mk_in, LANES)
    b1.update(finish(k, pay=pay, e2_row=e2_row, ef1_edge=ef1_edge, **names, **more))
    st = st_ef1 = gather_sums(b1["pay"])
    e2_row = other_row(b1["e2_row"])
    st, ef1_edge = lax.optimization_barrier((st, swap_path(b1["ef1_edge"])))
    point1 = weights_point(1, b1["d3"])

    k = Stage("back_space")
    mk_in, st_in = k.take(mk), k.take(st)
    names, s_e1 = second_back(k, 1, 0, st_in, mk_in, b1["e2"], e2_row)
    pay = payload(k, s_e1)
    e1_edge = edge_out(k, names["e1"], mk_in, width)
    b1.update(finish(k, pay=pay, e1_edge=e1_edge, **names))
    st = gather_sums(b1["pay"])
    e1_edge = swap_path(b1["e1_edge"])
    space1 = weights_space(1, b1["d2"])

    k = Stage("back_first")
    mk_in, st_in = k.take(mk), k.take(st)
    names, s_el = first_back(k, 1, st_in, mk_in, b1["e1"], e1_edge)
    names["down"], s_down = k.give((frames, spots, wide), BF16), k.temp((1, 2 * wide))
    for at in range(0, wide, 256):
        lanes = slice(at, at + 256)
        k.step(
            part(slow_input_back, m, 1, frames, lo3, at),
            k.peek(names["dw"]), k.take(w_slow_time, 1, every, lanes), k.take(b1["pre"], every, every, lanes),
            k.take(saved[0]["sw"], slice(1, 1 + frames), every, lanes),
            k.take(saved[0]["third"], slice(1, 1 + frames), every, lanes),
            k.take(saved[0]["n3"]), k.take(gain_slow), k.take(bias_slow), mk_in,
            k.piece(names["down"], every, every, lanes), s_down,
            flops=2 * frames * spots * 3 * 256 * width,
        )
    pay = payload(k, s_el, s_down)
    el_edge = edge_out(k, names["el"], mk_in, lat)
    b1.update(finish(k, pay=pay, el_edge=el_edge, **names))
    st = gather_sums(b1["pay"])
    el_edge = swap_path(b1["el_edge"])
    time1 = weights_time(1, b1["dw"])
    sizes1 = [point1.shape[0], space1.shape[0], time1.shape[0]]
    ones = jnp.concatenate([point1, space1, time1], axis=0)
    st, ones, el_edge = lax.optimization_barrier((st, ones, el_edge))
    ones = lax.psum(ones, AXES)

    GRADS = ("df", "dln", "dfp", "dfn")
    SUMS = ("gbl", "gb1", "gb2", "gb3", "gbf1", "gbf2", "gbf3")
    steps = exchange_steps()
    core, across, down = steps[:3]
    seen = {}

    def spread_both(one, two, tied=()):
        one, two = [one, swap(one, *down)], [two, swap(two, *across)]
        one, two = [jnp.stack(pair) for pair in (one, two)]
        one, two = [one, swap(one, *across)], [two, swap(two, *down)]
        one, two, tied = lax.optimization_barrier((one, two, tied))
        return [pair + [swap(half, *core) for half in pair] for pair in (one, two)], tied

    def block_zero(st=st, el_edge=el_edge, ef1_edge=ef1_edge, b1=b1, b0=b0):
        b1, b0 = dict(b1), dict(b0)
        k = Stage("back_third")
        mk_in, st_in = k.take(mk), k.take(st)
        names, s_e2 = third_back(k, 0, 2 * lat, st_in, mk_in, b1["down"])
        more = fast_back1(
            k, 1, k.take(st_ef1), 2 * width, st_in, 0, mk_in, b1["el"], el_edge, b1["ef1"], ef1_edge
        )
        inner_grads = [more[name] for name in ("dl", "df", "dln", "dfp", "dfn")]
        more["downf"], s_pf = k.give((fast_frames, spots, fwide), BF16), k.temp((1, 2 * LANES))
        k.step(
            part(fast_input_back, m, 1, frames, group, 2 * LANES, False),
            *inner_grads, k.take(saved[1]["w7"]), k.take(pre_f), k.take(saved[0]["fw"]), k.take(saved[0]["ft"]),
            k.take(saved[0]["nf3"]), k.take(gf), k.take(bf), mk_in, more["downf"], s_pf,
            k.temp((fast_frames + 4, spots, fwide)), flops=first_flops,
        )
        pay = payload(k, s_e2, s_pf)
        e2_row = row_out(k, names["e2"], mk_in, 0, width)
        got = finish(k, pay=pay, e2_row=e2_row, **names, **more)
        for name in more:
            b1[name] = got[name]
        b0.update({name: got[name] for name in names})
        st = gather_sums(got["pay"])
        e2_row = other_row(got["e2_row"])
        point0 = weights_point(0, b0["d3"])
        fast_1 = weights_fast(1, b1["dl"], b1["df"], b1["d2f"], b1["d3f"])

        k = Stage("back_space")
        mk_in, st_in = k.take(mk), k.take(st)
        names, s_e1 = second_back(k, 0, 0, st_in, mk_in, b0["e2"], e2_row)
        more, s_ef2 = fast_back3(k, 0, 2 * width, st_in, mk_in, b1["downf"])
        pay = payload(k, s_e1, s_ef2)
        e1_edge, ef2_row = edge_out(k, names["e1"], mk_in, width), row_out(k, more["ef2"], mk_in, 0, LANES)
        b0.update(finish(k, pay=pay, e1_edge=e1_edge, ef2_row=ef2_row, **names, **more))
        st = gather_sums(b0["pay"])
        e1_edge, ef2_row = swap_path(b0["e1_edge"]), other_row(b0["ef2_row"])
        space0 = weights_space(0, b0["d2"])
        mid = jnp.concatenate([fast_1, point0, space0], axis=0)
        st, mid = lax.optimization_barrier((st, mid))

        k = Stage("back_first")
        mk_in, st_in = k.take(mk), k.take(st)
        names, s_el = first_back(k, 0, st_in, mk_in, b0["e1"], e1_edge)
        more, s_ef1 = fast_back2(k, 0, 2 * width, st_in, mk_in, b0["ef2"], ef2_row)
        pay = payload(k, s_el, s_ef1)
        el_edge, ef1_edge = edge_out(k, names["el"], mk_in, lat), edge_out(k, more["ef1"], mk_in, LANES)
        b0.update(finish(k, pay=pay, el_edge=el_edge, ef1_edge=ef1_edge, **names, **more))
        b0["dw"], mid = lax.optimization_barrier((b0["dw"], mid))
        mid = halve(mid, *core)
        st = gather_sums(b0["pay"])
        el_edge, ef1_edge = swap_path(b0["el_edge"]), swap_path(b0["ef1_edge"])
        time0 = weights_time(0, b0["dw"])
        st, mid = lax.optimization_barrier((st, mid))
        mid = halve_both(*parted(mid), across, down)
        k = Stage("back_fast")
        mk_in, st_in = k.take(mk), k.take(st)
        more = fast_back1(k, 0, st_in, 2 * lat, st_in, 0, mk_in, b0["el"], el_edge, b0["ef1"], ef1_edge)
        v = saved[0]
        rest = k.give((6 * LANES, 2 * LANES), BF16)
        k.step(
            part(fast_weights, group, cols, lat),
            k.take(v["fw"]), more["dl"], more["df"], k.take(v["fa1"]), k.take(b0["d2f"]), k.take(v["fa2"]),
            k.take(b0["d3f"]), rest, k.temp((frames, ext, 3 * LANES), BF16), flops=first_flops,
        )
        got = finish(k, rest=rest, **more)
        b0.update(got)
        seen["rows"] = [piece.shape[0] for piece in (fast_1, point0, space0, time0, got["rest"])]
        late = halve(jnp.concatenate([time0, got["rest"]], axis=0), *core)
        late, dw0 = lax.optimization_barrier((late, b0["dw"]))
        late = halve_both(*parted(late), across, down)
        late, dl0 = lax.optimization_barrier((late, b0["dl"]))
        k = Stage("slow_input")
        gx_slow = k.give((frames, spots, wide))
        k.step(
            part(slow_input_last, m, frames),
            k.take(dw0), k.take(w_slow_time, 0, every, slice(0, wide)), k.take(b1["down"]), k.take(mk), gx_slow,
            flops=2 * frames * spots * 3 * wide * width,
        )
        (gx_slow,) = k.run()
        k = Stage("fast_input")
        gx_fast = k.give((fast_frames, spots, fwide))
        k.step(
            part(fast_input_back, m, 0, frames, group, 2 * LANES, True),
            k.take(dl0), *[k.take(b0[name]) for name in GRADS], k.take(saved[0]["w7"]), k.take(b1["downf"]), k.take(mk), gx_fast,
            k.temp((fast_frames + 4, spots, fwide)), flops=first_flops,
        )
        (gx_fast,) = k.run()
        def along(value, ahead=steps[3:]):
            for step in ahead:
                value = halve(value, *step)
            value = value.astype(BF16)
            for step in reversed(steps[3:]):
                value = double(value, *step)
            return value

        mid = along(jnp.concatenate(halve_both(*mid, down, across), axis=0))
        late, gx_slow = lax.optimization_barrier((halve_both(*late, down, across), gx_slow))
        late = jnp.concatenate(late, axis=0)
        for step in steps[3:4]:
            late, gx_fast = lax.optimization_barrier((halve(late, *step), gx_fast))
        late = along(late, steps[4:])
        (mid_one, mid_two), _ = spread_both(*parted(mid))
        sums = [b0[name] for name in SUMS] + [b1[name] for name in ("gbl", "gbf1")]
        return (*mid_one, *mid_two, late, gx_slow, gx_fast, *sums)

    like = jax.eval_shape(block_zero)
    got = lax.cond(
        clip_size[0, 0] > 0, block_zero, lambda: tuple(jnp.zeros(o.shape, o.dtype) for o in like)
    )
    mid_one, mid_two = list(got[:4]), list(got[4:8])
    late, gx_slow, gx_fast = got[8:11]
    b0 = dict(zip(SUMS, got[11:18]))
    b1["gbl"], b1["gbf1"] = got[18:20]

    time_rows, space_rows = 3 * (wide + lat), 9 * width
    k = Stage("assemble_one")
    ones_in = k.take(ones)
    gtime, gspace = k.give((2, time_rows, width), F32, 1), k.give((2, space_rows, width), F32, 1)
    gpoint = k.give((2, width, wide), F32, 1)
    k.step(part(copy_rows, sizes1[0] + sizes1[1]), ones_in, gtime)
    k.step(part(copy_rows, sizes1[0]), ones_in, gspace)
    k.step(part(copy_columns, 0), ones_in, gpoint)
    half_done = k.run()

    (one, two), half_done = spread_both(*parted(late), half_done)

    core_bit = lax.axis_index("rows") % 2
    down_bit = (lax.axis_index("rows") // 2) % 2

    k = Stage("assemble")
    flip_one = k.scalar((core_bit * 4 + path * 2 + down_bit).astype(jnp.int32).reshape(1))
    flip_two = k.scalar((core_bit * 4 + down_bit * 2 + path).astype(jnp.int32).reshape(1))
    one_in = k.take_blocks(one, flip_one, every)
    two_in = k.take_blocks(two, flip_two, every)
    mid_one, mid_two = k.take_blocks(mid_one, flip_one, every), k.take_blocks(mid_two, flip_two, every)
    sizes = seen["rows"]
    half_mid, half_late = sum(sizes[:3]) // 2, sum(sizes[3:]) // 2
    gspace = k.give((2, space_rows, width), F32, 0, half_done[1])
    k.step(part(place_rows, sizes[0] + sizes[1], 0, half_mid), mid_one, mid_two, gspace)
    gpoint = k.give((2, width, wide), F32, 0, half_done[2])
    k.step(part(place_columns, sizes[0], 0, half_mid), mid_one, mid_two, gpoint)
    gtime = k.give((2, time_rows, width), F32, 0, half_done[0])
    k.step(part(place_rows, 0, 0, half_late), one_in, two_in, gtime)
    fast_outs = [
        k.give((2, 5 * fwide, lat)), k.give((2, 3, inner, fwide)), k.give((2, 9, inner, inner)),
        k.give((2, inner, fwide)),
    ]
    k.step(part(place_fast, inner, half_mid, half_late, sizes[3]), mid_one, mid_two, one_in, two_in, *fast_outs)
    sums = [k.take(b[name]) for b in (b0, b1) for name in ("gbl", "gb1", "gb2", "gb3", "gbf1", "gbf2", "gbf3")]
    norm_outs = [k.give(like.shape) for like in (gain_slow, bias_slow, gain_fast, bias_fast)]
    k.step(part(assemble_norms, inner), *sums, *norm_outs)
    got = k.run()
    glat, gft, gfs, gfp = [got[h[1]] for h in fast_outs]

    return (
        out_slow.reshape(x_slow.shape),
        out_fast.reshape(x_fast.shape),
        gx_slow.reshape(x_slow.shape),
        gx_fast.reshape(x_fast.shape),
        glat.reshape(w_lateral.shape),
        got[gtime[1]].reshape(w_slow_time.shape),
        got[gspace[1]].reshape(w_slow_space.shape),
        got[gpoint[1]],
        jnp.swapaxes(gft, 2, 3),
        gfs.reshape(w_fast_space.shape),
        gfp,
        *[got[h[1]] for h in norm_outs],
    )


def solution(mesh):
    spread = P("path", None, "rows", None, None, None)
    return jax.shard_map(
        on_device,
        mesh=mesh,
        in_specs=(spread, spread) + (P(),) * 12 + (spread, spread),
        out_specs=(spread,) * 4 + (P(),) * 11,
        check_vma=False,
    )
```

```python
import functools

import jax
import jax.numpy as jnp
import numpy as np
from jax import lax
from jax.experimental import pallas as pl
from jax.experimental.pallas import tpu as pltpu
from jax.sharding import PartitionSpec as P

TS = 8
TF = 32
F32 = jnp.float32
BF16 = jnp.bfloat16
EPSILON = 1e-05
LANES = 128
AXES = ("path", "rows")
VMEM_LIMIT = 56 * 2**20


def swap(value, axis, stride):
    pairs = [(source, source ^ stride) for source in range(lax.axis_size(axis))]
    return lax.ppermute(value, axis, pairs)


def gather_sums(spread):
    return lax.all_to_all(spread, AXES, 0, 0, tiled=True)


def swap_path(value):
    assert lax.axis_size("path") == 2
    return lax.ppermute(value, "path", [(0, 1), (1, 0)])


def exchange_steps():
    steps = [("rows", 1), ("path", 1)]
    stride = 2
    while stride < lax.axis_size("rows"):
        steps.append(("rows", stride))
        stride *= 2
    return steps


def halve(value, axis, stride):
    size = value.shape[0] // 2
    upper = (lax.axis_index(axis) // stride) % 2
    keep = lax.dynamic_slice_in_dim(value, upper * size, size, 0)
    give = lax.dynamic_slice_in_dim(value, (1 - upper) * size, size, 0)
    return keep.astype(F32) + swap(give.astype(BF16), axis, stride).astype(F32)


def double(value, axis, stride):
    upper = (lax.axis_index(axis) // stride) % 2
    got = swap(value, axis, stride)
    return jnp.concatenate(
        [jnp.where(upper == 0, value, got), jnp.where(upper == 0, got, value)], axis=0
    )


def halve_both(one, two, first, second):
    return halve(one, *first), halve(two, *second)


def parted(value):
    size = value.shape[0] // 2
    return value[:size], value[size:]


class Stage:
    def __init__(self, name):
        self.name = name
        self.arrays, self.views, self.scalars, self.pairs = [], [], [], []
        self.outs, self.temps, self.steps = [], [], []
        self.entries, self.ontos = [], []
        self.flops = 0

    def take(self, array, *view):
        for at, known in enumerate(self.arrays):
            if known is array:
                break
        else:
            at = len(self.arrays)
            self.arrays.append(array)
        for k, (other, seen) in enumerate(self.views):
            if other == at and seen == view:
                return ("in", k)
        self.views.append((at, view))
        return ("in", len(self.views) - 1)

    def take_blocks(self, values, flip, rows):
        self.pairs.append(([self.take(value, slice(None), rows) for value in values], flip))
        return ("pair", len(self.pairs) - 1)

    def scalar(self, array):
        self.scalars.append(array)
        return ("scalar", len(self.scalars) - 1)

    def give(self, dims, dtype=F32, at=None, onto=None):
        self.outs.append(jax.ShapeDtypeStruct(tuple(dims), dtype))
        self.entries.append(at)
        self.ontos.append(onto)
        return ("out", len(self.outs) - 1)

    def piece(self, handle, *index):
        return ("piece", (handle[1], index))

    def peek(self, handle):
        return ("peek", handle[1])

    def temp(self, dims, dtype=F32):
        self.temps.append(pltpu.VMEM(tuple(dims), dtype))
        return ("temp", len(self.temps) - 1)

    def step(self, fn, *handles, flops=0):
        self.flops += flops
        self.steps.append((fn, handles))

    def sem(self, view, block):
        return 8 * view + block

    def view_shape(self, view):
        at, index = view
        return np.broadcast_to(np.zeros((), np.int8), self.arrays[at].shape)[index].shape

    def run(self):
        arrays, views, outs, steps, pairs = self.arrays, self.views, self.outs, self.steps, self.pairs
        order, home = [], {}
        for k, (members, flip) in enumerate(pairs):
            for j, member in enumerate(members):
                home[member[1]] = (k, j, flip)
        under = [onto for onto in self.ontos if onto is not None]

        def need(handle):
            if handle[0] == "in":
                return [handle[1]]
            return [part[1] for part in pairs[handle[1]][0]] if handle[0] == "pair" else []

        for _, handles in steps:
            for handle in handles:
                for k in need(handle):
                    if k not in order:
                        order.append(k)

        def body(*refs):
            refs = list(refs)

            def cut(count):
                taken = refs[:count]
                del refs[:count]
                return taken

            scalars, hbm_in = cut(len(self.scalars)), cut(len(arrays))
            cut(len(under))
            hbm_out = cut(len(outs))
            alone = [k for k in range(len(views)) if k not in home]
            held = dict(zip(alone, cut(len(alone))))
            joint, made, temps, (sems,) = cut(len(pairs)), cut(len(outs)), cut(len(self.temps)), refs
            copies = {}
            for k in order:
                at, index = views[k]
                src = hbm_in[at].at[index] if index else hbm_in[at]
                if k in home:
                    pair, second, flip = home[k]
                    count = self.view_shape(views[k])[0]
                    copies[k] = []
                    for block in range(count):
                        to = (second * count + block) ^ scalars[flip[1]][0]
                        copies[k].append(
                            pltpu.make_async_copy(src.at[block], joint[pair].at[to], sems.at[self.sem(k, block)])
                        )
                else:
                    copies[k] = [pltpu.make_async_copy(src, held[k], sems.at[self.sem(k, 0)])]
                for copy in copies[k]:
                    copy.start()
            waited, sent = set(), {}
            for fn, handles in steps:
                given = []
                for handle in handles:
                    for k in need(handle):
                        if k not in waited:
                            for copy in copies[k]:
                                copy.wait()
                            waited.add(k)
                    if handle[0] == "piece":
                        given.append(made[handle[1][0]].at[handle[1][1]])
                        continue
                    place = {"in": held, "pair": joint, "out": made, "peek": made, "temp": temps, "scalar": scalars}
                    given.append(place[handle[0]][handle[1]])
                fn(*given)
                for kind, k in handles:
                    if kind == "out" and k not in sent:
                        to = hbm_out[k] if self.entries[k] is None else hbm_out[k].at[self.entries[k]]
                        sent[k] = [pltpu.make_async_copy(made[k], to, sems.at[8 * (len(views) + k)])]
                        sent[k][0].start()
                    elif kind == "piece":
                        k, index = k
                        done = sent.setdefault(k, [])
                        sem = sems.at[8 * (len(views) + k) + len(done)]
                        done.append(pltpu.make_async_copy(made[k].at[index], hbm_out[k].at[index], sem))
                        done[-1].start()
            for done in sent.values():
                for copy in done:
                    copy.wait()

        moved = sum(a.size * a.dtype.itemsize for a in outs)
        for view in views:
            moved += int(np.prod(self.view_shape(view))) * arrays[view[0]].dtype.itemsize
        scratch = [
            pltpu.VMEM(self.view_shape(view), arrays[view[0]].dtype) for k, view in enumerate(views) if k not in home
        ]
        for members, _ in pairs:
            size = self.view_shape(views[members[0][1]])
            scratch.append(
                pltpu.VMEM((len(members) * size[0],) + size[1:], arrays[views[members[0][1]][0]].dtype)
            )
        scratch += [
            pltpu.VMEM(o.shape if at is None else o.shape[1:], o.dtype) for o, at in zip(outs, self.entries)
        ]
        aliases = {}
        for k, onto in enumerate(self.ontos):
            if onto is not None:
                aliases[len(self.scalars) + len(arrays) + len(aliases)] = k
        scratch += self.temps + [pltpu.SemaphoreType.DMA((8 * (len(views) + len(outs)),))]
        return pl.pallas_call(
            body,
            out_shape=tuple(outs),
            in_specs=[pl.BlockSpec(memory_space=pltpu.SMEM) for _ in self.scalars]
            + [pl.BlockSpec(memory_space=pl.ANY) for _ in arrays + under],
            out_specs=tuple(pl.BlockSpec(memory_space=pl.ANY) for _ in outs),
            scratch_shapes=scratch,
            input_output_aliases=aliases,
            compiler_params=pltpu.CompilerParams(vmem_limit_bytes=VMEM_LIMIT),
            cost_estimate=pl.CostEstimate(flops=self.flops, bytes_accessed=moved, transcendentals=0),
            name=self.name,
        )(*self.scalars, *arrays, *under)


class Masks:
    def __init__(self, spots, cols):
        self.main = (0, spots)
        self.ext = (spots, 2 * spots + 2 * cols)
        self.prev = (2 * spots + 2 * cols, 3 * spots + 2 * cols)
        self.next = (3 * spots + 2 * cols, 4 * spots + 2 * cols)
        self.slow = (4 * spots + 2 * cols, 4 * spots + 2 * cols + 8)
        self.fast = (4 * spots + 2 * cols + 8, 4 * spots + 2 * cols + 16)
        self.half = (4 * spots + 2 * cols + 16, 4 * spots + 2 * cols + 24)
        self.path = (4 * spots + 2 * cols + 24, 4 * spots + 2 * cols + 32)
        self.rows = 4 * spots + 2 * cols + 32


def make_masks(m, rows, cols, last, place, clips, mk):
    half = place[0] % 2
    path = place[1]
    side = clips[0, place[0] // 2]
    area = 0
    for k in range(clips.shape[1]):
        area = area + clips[0, k] * clips[0, k]
    shift = cols.bit_length() - 1

    def inside(first, count):
        at = lax.broadcasted_iota(jnp.int32, (count * cols, LANES), 0)
        line = half * rows + first + (at >> shift)
        spot = at & (cols - 1)
        good = (line >= 0) & (line < 2 * rows) & (line < side) & (spot < side)
        return jnp.where(good, 1.0, 0.0)

    main = inside(0, rows)
    mk[m.main[0] : m.main[1], :] = main
    mk[m.ext[0] : m.ext[1], :] = inside(-1, rows + 2)
    mk[m.prev[0] : m.prev[1], :] = main * jnp.where(path > 0, 1.0, 0.0)
    mk[m.next[0] : m.next[1], :] = main * jnp.where(path < last, 1.0, 0.0)

    def fill(span, value):
        mk[span[0] : span[1], :] = jnp.full((8, LANES), value, F32)

    fill(m.slow, TS * area.astype(F32))
    fill(m.fast, TF * area.astype(F32))
    fill(m.half, half.astype(F32))
    fill(m.path, path.astype(F32))


def own_row(m, spots, cols, col0, width, z, mk, row):
    for t in range(z.shape[0]):
        lower = mk[m.half[0] : m.half[0] + 1, :] > 0.5
        for lane in range(0, width, LANES):
            at = col0 + lane
            row[t, :, lane : lane + LANES] = jnp.where(
                lower, z[t, 0:cols, at : at + LANES], z[t, spots - cols : spots, at : at + LANES]
            )


def own_edge(m, lead, tail, z, mk, edge):
    frames = z.shape[0]
    second = mk[m.path[0] : m.path[0] + 1, :] > 0.5
    for lane in range(0, edge.shape[1], LANES):
        edge[:, lane : lane + LANES] = jnp.where(
            second,
            z[0, :, lead + lane : lead + lane + LANES],
            z[frames - 1, :, tail + lane : tail + lane + LANES],
        ).astype(edge.dtype)


def spread_sums(*refs):
    parts, out = refs[:-1], refs[-1]
    row = jnp.concatenate([part[...] for part in parts], axis=1)
    out[...] = jnp.broadcast_to(row[None], out.shape)


def make_w7(lat, group, wl, wf, w7):
    inner = wf.shape[1]
    w7[...] = jnp.zeros(w7.shape, BF16)
    for j in range(wl.shape[0]):
        w7[j * LANES : (j + 1) * LANES, 0:lat] = wl[j]
    at = lax.broadcasted_iota(jnp.int32, (inner, LANES), 0)
    lane = lax.broadcasted_iota(jnp.int32, (inner, LANES), 1)
    places = [jnp.where(lane == at + inner * k, 1.0, 0.0).astype(BF16) for k in range(group)]
    for f in range(1, group + 3):
        used = [k for k in range(group) if 0 <= f - 1 - k < 3]
        got = None
        for k in used:
            more = dot_tn(wf[f - 1 - k], places[k])
            got = more if got is None else got + more
        w7[f * LANES : (f + 1) * LANES, lat : lat + LANES] = got.astype(BF16)


def make_blocks(group, ws, wp, wfs, wfp):
    inner = wp.shape[0]
    at = lax.broadcasted_iota(jnp.int32, (inner, LANES), 0)
    lane = lax.broadcasted_iota(jnp.int32, (inner, LANES), 1)
    tile = jnp.where((lane & (inner - 1)) == at, 1.0, 0.0).astype(BF16)
    shift = inner.bit_length() - 1
    for tap in range(ws.shape[0]):
        got = dot(ws[tap], tile)
        for k in range(group):
            kept = jnp.where((lane >> shift) == k, got, 0.0).astype(BF16)
            row = (tap % 3) * LANES + k * inner
            wfs[tap // 3, row : row + inner, :] = kept
    wfp[...] = jnp.zeros(wfp.shape, BF16)
    for k in range(group):
        wfp[k * inner : (k + 1) * inner, k * LANES : (k + 1) * LANES] = wp[...]


def widen(rows, width):
    return jnp.concatenate([rows] * (width // LANES), axis=1)


def sublane_sums(value):
    return jnp.sum(value.reshape(value.shape[0] // 8, 8, value.shape[1]), axis=0)


def row_sum(value):
    return jnp.sum(value, axis=0, keepdims=True)


def fold_packed(row):
    full = jnp.broadcast_to(row, (8, LANES))
    full = full + pltpu.roll(full, 64, 1)
    full = full + pltpu.roll(full, 32, 1)
    return full[0:1]


def totals(st, lo, width, packed=False):
    first = jnp.sum(st[:, :, lo : lo + width], axis=0)
    second = jnp.sum(st[:, :, lo + width : lo + 2 * width], axis=0)
    if packed:
        return fold_packed(first), fold_packed(second)
    return first, second


def norm_rows(st, lo, width, count, packed=False):
    first, second = totals(st, lo, width, packed)
    mean = first / count
    return mean, lax.rsqrt(second / count - mean * mean + EPSILON)


def keep_norm(lo, width, span, st, mk, nz):
    mean, rstd = norm_rows(st, lo, width, widen(mk[span[0] : span[0] + 1, :], width))
    nz[0:1, :] = mean
    nz[1:2, :] = rstd


def keep_sums(lo, width, st, gb):
    one, two = totals(st, lo, width)
    gb[0:1, :] = one
    gb[1:2, :] = two


def clear(*refs):
    for ref in refs:
        ref[...] = jnp.zeros(ref.shape, F32)


def close_sums(one, two, s):
    s[...] = jnp.concatenate([row_sum(one[...]), row_sum(two[...])], axis=1)


def sigmoid(value):
    return 0.5 * jnp.tanh(0.5 * value) + 0.5


def silu(value):
    return value * sigmoid(value)


def silu_slope(value):
    sigma = sigmoid(value)
    return sigma * (1.0 + value * (1.0 - sigma))


def dot(a, b):
    return jnp.dot(a, b, preferred_element_type=F32)


def dot_nt(a, b):
    return lax.dot_general(a, b, (((1,), (1,)), ((), ())), preferred_element_type=F32)


def dot_tn(a, b):
    return lax.dot_general(a, b, (((0,), (0,)), ((), ())), preferred_element_type=F32)


def flat(value):
    return value.reshape(value.shape[0] * value.shape[1], value.shape[2])


def store_shifts(dst, t, value, cols):
    rows, width = value.shape
    spot = lax.broadcasted_iota(jnp.int32, (rows, width), 0) & (cols - 1)
    left = jnp.where(spot == 0, 0.0, pltpu.roll(value, 1, 0))
    right = jnp.where(spot == cols - 1, 0.0, pltpu.roll(value, rows - 1, 0))
    dst[t, :, 0:width] = left.astype(BF16)
    dst[t, :, width : 2 * width] = value.astype(BF16)
    dst[t, :, 2 * width : 3 * width] = right.astype(BF16)


def taps_of(frames_ref, frames, group):
    return jnp.concatenate(
        [
            jnp.concatenate([frames_ref[group * t + f] for f in range(7)], axis=1)
            for t in range(frames)
        ],
        axis=0,
    )


def entry_sums(y, lat, frames, spots):
    width = y.shape[1]
    one = jnp.zeros((8, width), F32)
    two = jnp.zeros((8, width), F32)
    for t in range(frames):
        part = y[t * spots : (t + 1) * spots]
        one = one + sublane_sums(part)
        two = two + sublane_sums(part * part)
    one = row_sum(one)
    two = row_sum(two)
    return jnp.concatenate([one[:, :lat], two[:, :lat], one[:, lat:], two[:, lat:]], axis=1)


def fast_entry(m, frames, group, x, before, after, mk, w7, fw, y, s):
    spots = x.shape[1]
    count = x.shape[0]

    def put(at, value, span):
        fw[at] = (value.astype(F32) * mk[span[0] : span[1], :]).astype(BF16)

    for k in range(2):
        put(k, before[k], m.prev)
        put(2 + count + k, after[k], m.next)
    for k in range(count):
        put(2 + k, x[k], m.main)
    out = dot(taps_of(fw, frames, group), w7[...])
    for t in range(frames):
        y[t] = out[t * spots : (t + 1) * spots]
    s[...] = entry_sums(out, w7.shape[1] - LANES, frames, spots)


def slow_partial(m, frames, x, before, after, mk, wt, xm, fpart):
    spots, wide = x.shape[1], x.shape[2]
    sources = [(before, m.prev)] + [(x.at[t], m.main) for t in range(frames)] + [(after, m.next)]
    for k, (src, span) in enumerate(sources):
        for lo in range(0, wide, 256):
            mask = widen(mk[span[0] : span[1], :], 256)
            xm[k, :, lo : lo + 256] = (src[:, lo : lo + 256].astype(F32) * mask).astype(BF16)
    out = dot(flat(xm[0:frames]), wt[0, :wide, :])
    for j in range(1, 3):
        out = out + dot(flat(xm[j : j + frames]), wt[j, :wide, :])
    for t in range(frames):
        fpart[t] = out[t * spots : (t + 1) * spots]


def lat_join(m, n, frames, lat, st, y, before, after, fpart, wt, gs, bs, mk, jl, first, s, nl, jw):
    spots = y.shape[1]
    wide = wt.shape[1] - lat
    count = widen(mk[m.slow[0] : m.slow[0] + 1, :], lat)
    mean, rstd = norm_rows(st, 0, lat, count)
    nl[0:1, :] = mean
    nl[1:2, :] = rstd
    scale = rstd * gs[n : n + 1, 0:lat]
    bias = bs[n : n + 1, 0:lat]
    sources = (
        [(before[:, 0:lat], m.prev)]
        + [(y[t, :, 0:lat], m.main) for t in range(frames)]
        + [(after[:, 0:lat], m.next)]
    )
    for k, (value, span) in enumerate(sources):
        mask = widen(mk[span[0] : span[1], :], lat)
        act = (silu((value - mean) * scale + bias) * mask).astype(BF16)
        jw[k] = act
        if 1 <= k <= frames:
            jl[k - 1] = act
    out = flat(fpart[...])
    for j in range(3):
        out = out + dot(flat(jw[j : j + frames]), wt[j, wide:, :])
    one = jnp.zeros((8, out.shape[1]), F32)
    two = jnp.zeros((8, out.shape[1]), F32)
    for t in range(frames):
        part = out[t * spots : (t + 1) * spots]
        first[t] = part
        one = one + sublane_sums(part)
        two = two + sublane_sums(part * part)
    s[...] = jnp.concatenate([row_sum(one), row_sum(two)], axis=1)


def space_forward(
    m, n, frames, cols, lo, at, width, col0, packed, span, st, z, row, w, g, b, mk, aw, out, s, nz, vw
):
    spots = z.shape[1]
    count = widen(mk[span[0] : span[0] + 1, :], width)
    mean, rstd = norm_rows(st, at, width, count, packed)
    nz[0:1, :] = mean
    nz[1:2, :] = rstd
    scale = rstd * g[n : n + 1, lo : lo + width]
    bias = b[n : n + 1, lo : lo + width]
    mask = widen(mk[m.ext[0] : m.ext[1], :], width)
    for t in range(frames):
        value = jnp.concatenate([row[t], z[t, :, col0 : col0 + width], row[t]], axis=0)
        act = silu((value - mean) * scale + bias) * mask
        aw[t] = act.astype(BF16)
        store_shifts(vw, t, act, cols)
    total = dot(flat(vw[:, 0:spots, :]), w[0])
    for i in range(1, 3):
        total = total + dot(flat(vw[:, i * cols : i * cols + spots, :]), w[i])
    mask = widen(mk[m.main[0] : m.main[1], :], width)
    one = jnp.zeros((8, width), F32)
    two = jnp.zeros((8, width), F32)
    for t in range(frames):
        part = total[t * spots : (t + 1) * spots]
        out[t] = part
        part = part * mask
        one = one + sublane_sums(part)
        two = two + sublane_sums(part * part)
    s[...] = jnp.concatenate([row_sum(one), row_sum(two)], axis=1)


def slow_acts(m, n, frames, lo, halo, st, z, *rest):
    if halo:
        before, after, g, b, mk, a2, nz, aw = rest
    else:
        g, b, mk, a2, nz, aw = rest
    width = z.shape[2]
    keep_norm(0, width, m.slow, st, mk, nz)
    mean = nz[0:1, :]
    scale = nz[1:2, :] * g[n : n + 1, lo : lo + width]
    bias = b[n : n + 1, lo : lo + width]
    sources = [(z[t], m.main, t + halo) for t in range(frames)]
    if halo:
        sources += [(before[...], m.prev, 0), (after[...], m.next, frames + 1)]
    for value, span, at in sources:
        mask = widen(mk[span[0] : span[1], :], width)
        act = (silu((value - mean) * scale + bias) * mask).astype(BF16)
        aw[at] = act
        if halo <= at < frames + halo:
            a2[at - halo] = act


def slow_third(frames, halo, at, aw, wp, third, s):
    spots = aw.shape[1]
    wide = s.shape[1] // 2
    out = dot(flat(aw[...]), wp[...])
    one = jnp.zeros((8, 256), F32)
    two = jnp.zeros((8, 256), F32)
    for t in range(frames + 2 * halo):
        part = out[t * spots : (t + 1) * spots]
        third[t] = part.astype(BF16)
        if halo <= t < frames + halo:
            one = one + sublane_sums(part)
            two = two + sublane_sums(part * part)
    s[:, at : at + 256] = row_sum(one)
    s[:, wide + at : wide + at + 256] = row_sum(two)


def fast_third(m, n, frames, lo, at, st, z, wp, g, b, mk, a2, ft, s, nz):
    spots = z.shape[1]
    count = mk[m.fast[0] : m.fast[0] + 1, :]
    mean, rstd = norm_rows(st, at, LANES, count, True)
    nz[0:1, :] = mean
    nz[1:2, :] = rstd
    scale = rstd * g[n : n + 1, lo : lo + LANES]
    bias = b[n : n + 1, lo : lo + LANES]
    mask = mk[m.main[0] : m.main[1], :]
    for t in range(frames):
        a2[t] = (silu((z[t] - mean) * scale + bias) * mask).astype(BF16)
    acts = flat(a2[...])
    one = jnp.zeros((8, LANES), F32)
    two = jnp.zeros((8, LANES), F32)
    out = dot(acts, wp[...])
    for t in range(frames):
        for lane in range(0, wp.shape[1], LANES):
            part = out[t * spots : (t + 1) * spots, lane : lane + LANES]
            ft[t, :, lane : lane + LANES] = part.astype(BF16)
            one = one + sublane_sums(part)
            two = two + sublane_sums(part * part)
    s[...] = jnp.concatenate([row_sum(one), row_sum(two)], axis=1)


def fast_next(m, n, frames, group, lo, at, st, ft, before, after, fw0, w7, g, b, mk, fw1, y, s, nz):
    spots = ft.shape[1]
    count = mk[m.fast[0] : m.fast[0] + 1, :]
    mean, rstd = norm_rows(st, at, LANES, count)
    nz[0:1, :] = mean
    nz[1:2, :] = rstd
    scale = rstd * g[n : n + 1, lo : lo + LANES]
    bias = b[n : n + 1, lo : lo + LANES]
    total = frames * group

    def out_of(k, value, span):
        z = fw0[k].astype(F32) + ((value - mean) * scale + bias)
        return silu(z) * mk[span[0] : span[1], :]

    for k in range(2):
        lane = k * LANES
        fw1[k] = out_of(k, before[:, lane : lane + LANES], m.prev).astype(BF16)
        fw1[2 + total + k] = out_of(2 + total + k, after[:, lane : lane + LANES], m.next).astype(BF16)
    for t in range(frames):
        for f in range(group):
            k = t * group + f
            fw1[2 + k] = out_of(2 + k, ft[t, :, f * LANES : (f + 1) * LANES], m.main).astype(BF16)
    out = dot(taps_of(fw1, frames, group), w7[...])
    for t in range(frames):
        y[t] = out[t * spots : (t + 1) * spots]
    s[...] = entry_sums(out, w7.shape[1] - LANES, frames, spots)


def fast_last(m, n, frames, group, lo, at, st, ft, f1, cot, g, b, mk, out, pre, s, nz):
    count = mk[m.fast[0] : m.fast[0] + 1, :]
    mean, rstd = norm_rows(st, at, LANES, count)
    nz[0:1, :] = mean
    nz[1:2, :] = rstd
    gain = g[n : n + 1, lo : lo + LANES]
    bias = b[n : n + 1, lo : lo + LANES]
    mask = mk[m.main[0] : m.main[1], :]
    one = jnp.zeros((8, LANES), F32)
    two = jnp.zeros((8, LANES), F32)
    for t in range(frames):
        for f in range(group):
            k = t * group + f
            hat = (ft[t, :, f * LANES : (f + 1) * LANES].astype(F32) - mean) * rstd
            z = f1[k].astype(F32) + hat * gain + bias
            sigma = sigmoid(z)
            out[k] = z * sigma * mask
            grad = cot[k].astype(F32) * mask * (sigma * (1.0 + z * (1.0 - sigma)))
            pre[k] = grad.astype(BF16)
            one = one + sublane_sums(grad)
            two = two + sublane_sums(grad * hat)
    s[...] = jnp.concatenate([row_sum(one), row_sum(two)], axis=1)


def chunked(total, step, body, init):
    def turn(i, carry):
        return body(pl.multiple_of(i * step, step), carry)

    return lax.fori_loop(0, total // step, turn, init)


def slow_next(n, lo, span, third, xm, nz, g, b, mk, sw):
    spots, wide = third.shape
    mean = nz[0:1, :]
    scale = nz[1:2, :] * g[n : n + 1, lo : lo + wide]
    bias = b[n : n + 1, lo : lo + wide]

    def turn(at, carry):
        mask = widen(mk[pl.ds(span[0] + at, 16), :], 512)
        for c in range(0, wide, 512):
            z = third[pl.ds(at, 16), c : c + 512].astype(F32)
            z = (z - mean[:, c : c + 512]) * scale[:, c : c + 512] + bias[:, c : c + 512]
            z = xm[pl.ds(at, 16), c : c + 512].astype(F32) + z
            sw[pl.ds(at, 16), c : c + 512] = (silu(z) * mask).astype(BF16)
        return carry

    chunked(spots, 16, turn, 0)


def time_partial(frames, sw, wt, fpart):
    spots = sw.shape[1]
    out = dot(flat(sw[0:frames]), wt[0])
    for j in range(1, 3):
        out = out + dot(flat(sw[j : j + frames]), wt[j])
    for t in range(frames):
        fpart[t] = out[t * spots : (t + 1) * spots]


def slow_last(m, n, lo, third, slow, cot, nz, g, b, mk, out, pre, one, two):
    spots, wide = third.shape
    mean, rstd = nz[0:1, :], nz[1:2, :]
    gain = g[n : n + 1, lo : lo + wide]
    bias = b[n : n + 1, lo : lo + wide]

    def turn(at, sums):
        ones, twos = [], []
        mask = widen(mk[pl.ds(m.main[0] + at, 16), :], 512)
        for c in range(0, wide, 512):
            hat = third[pl.ds(at, 16), c : c + 512].astype(F32)
            hat = (hat - mean[:, c : c + 512]) * rstd[:, c : c + 512]
            z = slow[pl.ds(at, 16), c : c + 512].astype(F32) + hat * gain[:, c : c + 512] + bias[:, c : c + 512]
            sigma = sigmoid(z)
            out[pl.ds(at, 16), c : c + 512] = z * sigma * mask
            grad = cot[pl.ds(at, 16), c : c + 512].astype(F32) * mask
            grad = grad * (sigma * (1.0 + z * (1.0 - sigma)))
            pre[pl.ds(at, 16), c : c + 512] = grad.astype(BF16)
            ones.append(sublane_sums(grad))
            twos.append(sublane_sums(grad * hat))
        return sums[0] + jnp.concatenate(ones, axis=1), sums[1] + jnp.concatenate(twos, axis=1)

    one[...], two[...] = chunked(spots, 16, turn, (one[...], two[...]))


def slow_third_grad(m, n, lo, pre, third, n3, gb, g, mk, d3):
    spots, wide = pre.shape
    count = widen(mk[m.slow[0] : m.slow[0] + 1, :], wide)
    mean, rstd = n3[0:1, :], n3[1:2, :]
    scale = g[n : n + 1, lo : lo + wide] * rstd
    one = gb[0:1, :] / count
    two = gb[1:2, :] / count * rstd

    def turn(i, carry):
        mask = widen(mk[pl.ds(m.main[0] + i, 16), :], 512)
        for c in range(0, wide, 512):
            hat = (third[pl.ds(i, 16), c : c + 512].astype(F32) - mean[:, c : c + 512]) * two[:, c : c + 512]
            grad = pre[pl.ds(i, 16), c : c + 512].astype(F32) - mask * (one[:, c : c + 512] + hat)
            d3[pl.ds(i, 16), c : c + 512] = (scale[:, c : c + 512] * grad).astype(BF16)
        return carry

    chunked(spots, 16, turn, 0)


def slow_third_back(m, n, frames, lo, d3, z, n2, wp, g, b, mk, e2, s):
    spots, width = z.shape[1], z.shape[2]
    out = dot_nt(flat(d3[...]), wp[...])
    gain = g[n : n + 1, lo : lo + width]
    bias = b[n : n + 1, lo : lo + width]
    back_act(m, frames, spots, out, z, 0, n2[0:1, :], n2[1:2, :], gain, bias, mk, e2, s)


def back_act(m, frames, spots, out, z, col0, mean, rstd, gain, bias, mk, e, s):
    width = out.shape[1]
    mask = widen(mk[m.main[0] : m.main[1], :], width)
    one = jnp.zeros((8, width), F32)
    two = jnp.zeros((8, width), F32)
    for t in range(frames):
        hat = (z[t, :, col0 : col0 + width] - mean) * rstd
        grad = out[t * spots : (t + 1) * spots] * mask * silu_slope(hat * gain + bias)
        e[t] = grad
        one = one + sublane_sums(grad)
        two = two + sublane_sums(grad * hat)
    s[...] = jnp.concatenate([row_sum(one), row_sum(two)], axis=1)


def fast_third_back(m, n, frames, group, lo3, lo2, at, st, pre, ft, n3, z, n2, wp, g, b, mk, d3, e2, s, gb):
    spots = z.shape[1]
    count = mk[m.fast[0] : m.fast[0] + 1, :]
    one, two = totals(st, at, LANES)
    gb[0:1, :] = one
    gb[1:2, :] = two
    mean, rstd = n3[0:1, :], n3[1:2, :]
    scale = g[n : n + 1, lo3 : lo3 + LANES] * rstd
    one = one / count
    two = two / count * rstd
    mask = mk[m.main[0] : m.main[1], :]
    for t in range(frames):
        for f in range(group):
            hat = (ft[t, :, f * LANES : (f + 1) * LANES] - mean) * two
            grad = pre[t * group + f] - mask * (one + hat)
            d3[t, :, f * LANES : (f + 1) * LANES] = (scale * grad).astype(BF16)
    out = dot_nt(flat(d3[...]), wp[...])
    mean, rstd = n2[0:1, :], n2[1:2, :]
    gain = g[n : n + 1, lo2 : lo2 + LANES]
    bias = b[n : n + 1, lo2 : lo2 + LANES]
    back_act(m, frames, spots, out, z, 0, mean, rstd, gain, bias, mk, e2, s)


def space_back(
    m, n, frames, cols, lo2, lo1, at, width, col0, packed, span,
    st, e, erow, z, zrow, nz, z1, n1, w, g, b, mk, d2, e1, s, gb, vw,
):
    spots = z.shape[1]
    count = widen(mk[span[0] : span[0] + 1, :], width)
    one, two = totals(st, at, width, packed)
    gb[0:1, :] = one
    gb[1:2, :] = two
    mean, rstd = nz[0:1, :], nz[1:2, :]
    scale = g[n : n + 1, lo2 : lo2 + width] * rstd
    one = one / count
    two = two / count * rstd
    mask = widen(mk[m.ext[0] : m.ext[1], :], width)
    for t in range(frames):
        grad = jnp.concatenate([erow[t], e[t], erow[t]], axis=0)
        value = jnp.concatenate([zrow[t], z[t], zrow[t]], axis=0)
        grad = scale * mask * (grad - (one + (value - mean) * two))
        d2[t] = grad[cols : cols + spots].astype(BF16)
        store_shifts(vw, t, grad.astype(BF16).astype(F32), cols)
    total = None
    for i in range(3):
        rows = (2 - i) * cols
        for j in range(3):
            lane = (2 - j) * width
            part = dot_nt(flat(vw[:, rows : rows + spots, lane : lane + width]), w[i, j * width : (j + 1) * width, :])
            total = part if total is None else total + part
    mean, rstd = n1[0:1, :], n1[1:2, :]
    gain = g[n : n + 1, lo1 : lo1 + width]
    bias = b[n : n + 1, lo1 : lo1 + width]
    back_act(m, frames, spots, total, z1, col0, mean, rstd, gain, bias, mk, e1, s)


def first_taps(frames, dw):
    return [flat(dw[2 - j : 2 - j + frames]) for j in range(3)]


def time_back(taps, wt, lo, size):
    out = dot_nt(taps[0], wt[0, lo : lo + size, :])
    for j in range(1, 3):
        out = out + dot_nt(taps[j], wt[j, lo : lo + size, :])
    return out


def slow_first_back(m, n, frames, lo1, at, st, e, ep, en, z, zp, zn, n1, wt, y, nl, g, b, mk, dw, el, s, gb):
    spots, width = z.shape[1], z.shape[2]
    lat = nl.shape[1]
    wide = wt.shape[1] - lat
    count = widen(mk[m.slow[0] : m.slow[0] + 1, :], width)
    one, two = totals(st, at, width)
    gb[0:1, :] = one
    gb[1:2, :] = two
    mean, rstd = n1[0:1, :], n1[1:2, :]
    scale = g[n : n + 1, lo1 : lo1 + width] * rstd
    one = one / count
    two = two / count * rstd
    sources = (
        [(ep, zp, m.prev)] + [(e.at[t], z.at[t], m.main) for t in range(frames)] + [(en, zn, m.next)]
    )
    for k, (grad, value, span) in enumerate(sources):
        mask = widen(mk[span[0] : span[1], :], width)
        dw[k] = (scale * mask * (grad[...] - (one + (value[...] - mean) * two))).astype(BF16)
    out = time_back(first_taps(frames, dw), wt, wide, lat)
    back_act(
        m, frames, spots, out, y, 0, nl[0:1, :], nl[1:2, :], g[n : n + 1, 0:lat], b[n : n + 1, 0:lat], mk, el, s
    )


def slow_input_last(m, frames, dw, wt, pre, mk, gx):
    spots, wide = pre.shape[1], pre.shape[2]
    taps = first_taps(frames, dw)
    mask = widen(mk[m.main[0] : m.main[1], :], 256)
    for c in range(0, wide, 256):
        out = time_back(taps, wt, c, 256)
        for t in range(frames):
            gx[t, :, c : c + 256] = (out[t * spots : (t + 1) * spots] + pre[t, :, c : c + 256]) * mask


def slow_input_back(m, n, frames, lo, at, dw, wt, pre, xm, third, n3, g, b, mk, pre0, s):
    spots = pre.shape[1]
    wide = s.shape[1] // 2
    mask = widen(mk[m.main[0] : m.main[1], :], 256)
    out = time_back(first_taps(frames, dw), wt, 0, 256)
    mean, rstd = n3[0:1, at : at + 256], n3[1:2, at : at + 256]
    gain = g[n - 1 : n, lo + at : lo + at + 256]
    bias = b[n - 1 : n, lo + at : lo + at + 256]
    one = jnp.zeros((8, 256), F32)
    two = jnp.zeros((8, 256), F32)
    for t in range(frames):
        grad = (out[t * spots : (t + 1) * spots] + pre[t].astype(F32)) * mask
        hat = (third[t].astype(F32) - mean) * rstd
        z0 = xm[t].astype(F32) + hat * gain + bias
        grad = grad * silu_slope(z0)
        pre0[t] = grad.astype(BF16)
        one = one + sublane_sums(grad)
        two = two + sublane_sums(grad * hat)
    s[:, at : at + 256] = row_sum(one)
    s[:, wide + at : wide + at + 256] = row_sum(two)


def fast_first_back(
    m, n, frames, lo1, at1, atl, st1, stl, el, eln, ef, efp, efn, y, yp, yn, nl, n1, gs, g, mk,
    dl, dfw, dln, dfp, dfn, gbl, gb1,
):
    lat = nl.shape[1]
    count = widen(mk[m.slow[0] : m.slow[0] + 1, :], lat)
    one, two = totals(stl, atl, lat)
    gbl[0:1, :] = one
    gbl[1:2, :] = two
    mean, rstd = nl[0:1, :], nl[1:2, :]
    scale = gs[n : n + 1, 0:lat] * rstd
    one = one / count
    two = two / count * rstd

    def lat_grad(grad, value, span):
        mask = widen(mk[span[0] : span[1], :], lat)
        return (scale * mask * (grad - (one + (value - mean) * two))).astype(BF16)

    for t in range(frames):
        dl[t] = lat_grad(el[t], y[t, :, 0:lat], m.main)
    dln[...] = lat_grad(eln[...], yn[:, 0:lat], m.next)
    fcount = mk[m.fast[0] : m.fast[0] + 1, :]
    fone, ftwo = totals(st1, at1, LANES, True)
    gb1[0:1, :] = fone
    gb1[1:2, :] = ftwo
    fmean, frstd = n1[0:1, :], n1[1:2, :]
    fscale = g[n : n + 1, lo1 : lo1 + LANES] * frstd
    fone = fone / fcount
    ftwo = ftwo / fcount * frstd

    def first_grad(grad, value, span):
        mask = mk[span[0] : span[1], :]
        return (fscale * mask * (grad - (fone + (value - fmean) * ftwo))).astype(BF16)

    for t in range(frames):
        dfw[t] = first_grad(ef[t], y[t, :, lat:], m.main)
    dfp[...] = first_grad(efp[...], yp[:, lat:], m.prev)
    dfn[...] = first_grad(efn[...], yn[:, lat:], m.next)


def fast_input_back(m, n, frames, group, lo3, last, dl, dfw, dln, dfp, dfn, w7, pre, *rest):
    if last:
        mk, gx, buf = rest
    else:
        fw0, ft, n3, g, b, mk, pre0, s, buf = rest
    spots, lat = dl.shape[1], dl.shape[2]
    both = jnp.concatenate([flat(dl[...]), flat(dfw[...])], axis=1)
    buf[...] = jnp.zeros(buf.shape, F32)
    out = dot_nt(both, w7[...])
    for t in range(frames):
        for f in range(7):
            k = group * t + f
            buf[k] = buf[k] + out[t * spots : (t + 1) * spots, f * LANES : (f + 1) * LANES]
    buf[2] = buf[2] + dot_nt(dfp[...], w7[6 * LANES : 7 * LANES, lat:])
    after = dot_nt(jnp.concatenate([dln[...], dfn[...]], axis=1), w7[0 : 2 * LANES, :])
    total = frames * group
    for f in range(2):
        buf[total + f] = buf[total + f] + after[:, f * LANES : (f + 1) * LANES]
    mask = mk[m.main[0] : m.main[1], :]
    if last:
        for k in range(total):
            gx[k] = (pre[k] + buf[2 + k]) * mask
        return
    mean, rstd = n3[0:1, :], n3[1:2, :]
    gain = g[n - 1 : n, lo3 : lo3 + LANES]
    bias = b[n - 1 : n, lo3 : lo3 + LANES]
    one = jnp.zeros((8, LANES), F32)
    two = jnp.zeros((8, LANES), F32)
    for k in range(total):
        t, f = k // group, k % group
        hat = (ft[t, :, f * LANES : (f + 1) * LANES] - mean) * rstd
        z0 = fw0[2 + k].astype(F32) + hat * gain + bias
        grad = (pre[k] + buf[2 + k]) * mask * silu_slope(z0)
        pre0[k] = grad.astype(BF16)
        one = one + sublane_sums(grad)
        two = two + sublane_sums(grad * hat)
    s[...] = jnp.concatenate([row_sum(one), row_sum(two)], axis=1)


def point_weights(a2, d3, out):
    acts = flat(a2[...])
    for k in range(out.shape[0]):
        out[k] = dot_tn(acts, flat(d3[:, :, k * 256 : (k + 1) * 256])).astype(BF16)


def space_weights(cols, aw, d2, out, vw):
    frames, spots, width = d2.shape
    for t in range(frames):
        store_shifts(vw, t, aw[t].astype(F32), cols)
    grads = flat(d2[...])
    for i in range(3):
        out[i] = dot_tn(flat(vw[:, i * cols : i * cols + spots, :]), grads).astype(BF16)


def time_weights(skip, slow, jl, dw, out):
    frames, spots, width = jl.shape
    wide = slow.shape[2]
    grads = jnp.concatenate([flat(dw[2 - j : 2 - j + frames]) for j in range(3)], axis=1)
    for c in range(0, wide + jl.shape[2], 256):
        if c < wide:
            acts = flat(slow[skip : skip + frames, :, c : c + 256])
        else:
            acts = flat(jl[:, :, c - wide : c - wide + 256])
        got = dot_tn(acts, grads)
        for j in range(3):
            out[j, c : c + 256, :] = got[:, j * width : (j + 1) * width].astype(BF16)


def group_blocks(value, group):
    size = LANES // group
    rows = lax.broadcasted_iota(jnp.int32, (LANES, LANES), 0) >> (size.bit_length() - 1)
    lanes = lax.broadcasted_iota(jnp.int32, (LANES, LANES), 1) >> (size.bit_length() - 1)
    kept = jnp.where(rows == lanes, value, 0.0)
    kept = kept + pltpu.roll(kept, 64, 1)
    kept = kept + pltpu.roll(kept, 32, 1)
    total = kept[0:size]
    for k in range(1, group):
        total = total + kept[k * size : (k + 1) * size]
    return total


def at_lanes(blocks):
    lanes = lax.broadcasted_iota(jnp.int32, blocks[0].shape, 1) >> 5
    out = jnp.zeros(blocks[0].shape, F32)
    for k, block in enumerate(blocks):
        out = jnp.where(lanes == k, block, out)
    return out


def fast_weights(group, cols, lat, fw, dl, df, fa1, d2, fa2, d3, out, vw):
    frames, spots, _ = dl.shape
    size = LANES // group
    both = jnp.concatenate([flat(dl[...]), flat(df[...])], axis=1)
    taps = [[None] * group for _ in range(3)]
    for f in range(7):
        acts = jnp.concatenate([fw[group * t + f] for t in range(frames)], axis=0)
        got = dot_tn(acts, both)
        if f < 5:
            out[f * LANES : (f + 1) * LANES, :] = got[:, :lat].astype(BF16)
        for k in range(group):
            if 0 <= f - k - 1 < 3:
                taps[f - k - 1][k] = got[:, lat:]
    lanes = lax.broadcasted_iota(jnp.int32, (LANES, LANES), 1) >> (size.bit_length() - 1)
    tap_sums = []
    for j in range(3):
        kept = jnp.zeros((LANES, LANES), F32)
        for k in range(group):
            kept = jnp.where(lanes == k, taps[j][k], kept)
        kept = kept + pltpu.roll(kept, 64, 1)
        tap_sums.append(kept + pltpu.roll(kept, 32, 1))
    low = 5 * LANES
    out[low : low + LANES, 0:LANES] = at_lanes(tap_sums).T.astype(BF16)
    for t in range(frames):
        store_shifts(vw, t, fa1[t].astype(F32), cols)
    grads = flat(d2[...])
    for i in range(3):
        got = dot_tn(flat(vw[:, i * cols : i * cols + spots, :]), grads)
        blocks = [group_blocks(got[j * LANES : (j + 1) * LANES], group) for j in range(3)]
        out[low + size * i : low + size * (i + 1), LANES : 2 * LANES] = at_lanes(blocks).astype(BF16)
    acts = flat(fa2[...])
    total = jnp.zeros((size, LANES), F32)
    for k in range(group):
        got = dot_tn(acts, flat(d3[:, :, k * LANES : (k + 1) * LANES]))
        total = total + got[k * size : (k + 1) * size]
    out[low + 3 * size : low + 4 * size, LANES : 2 * LANES] = total.astype(BF16)


def unpack_fast(n, inner, load, outs):
    glat, gft, gfs, gfp = outs
    low = glat.shape[1]
    for at in range(0, low, inner):
        glat[n, at : at + inner, :] = load(at, inner)
    for i in range(4):
        got = load(low + inner * i, inner)
        if i < 3:
            gft[n, i] = got[:, 0:LANES]
            for j in range(3):
                moved = got[:, LANES:] if j == 0 else pltpu.roll(got[:, LANES:], LANES - inner * j, 1)
                gfs[n, 3 * i + j] = moved[:, 0:inner]
        else:
            gfp[n] = got[:, LANES:]


def runs_of(at, count, base, half, one, two):
    found = []
    while count:
        core, row = at // half, base + at % half
        ref, size = one, one.shape[1]
        if row >= 4 * size:
            ref, row = two, row - 4 * size
            size = two.shape[1]
        block, row = core * 4 + row // size, row % size
        here = min(count, size - row, half - at % half)
        found.append((ref, block, row, here))
        at, count = at + here, count - here
    return found


def rows_of(base, half, one, two=None):
    def load(at, count):
        parts = [
            ref[block, row : row + here, :].astype(F32)
            for ref, block, row, here in runs_of(at, count, base, half, one, two)
        ]
        return parts[0] if len(parts) == 1 else jnp.concatenate(parts, axis=0)

    return load


def copy_rows(start, one, out):
    for at in range(0, out.shape[0], 256):
        out[at : at + 256, :] = one[start + at : start + at + 256, :].astype(F32)


def copy_columns(start, one, out):
    for at in range(0, out.shape[1], 256):
        out[:, at : at + 256] = one[start + at : start + at + 256, :].astype(F32)


def place_rows(start, base, half, one, two, out):
    at = 0
    for ref, block, row, here in runs_of(start, out.shape[0], base, half, one, two):
        out[at : at + here, :] = ref[block, row : row + here, :].astype(F32)
        at += here


def place_columns(start, base, half, one, two, out):
    for lane in range(0, out.shape[1], 256):
        at = 0
        for ref, block, row, here in runs_of(start + lane, 256, base, half, one, two):
            out[at : at + here, lane : lane + 256] = ref[block, row : row + here, :].astype(F32)
            at += here


def place_fast(inner, half_mid, half_late, start, mid_one, mid_two, one, two, *outs):
    unpack_fast(1, inner, rows_of(0, half_mid, mid_one, mid_two), outs)
    load = rows_of(0, half_late, one, two)
    unpack_fast(0, inner, lambda at, count: load(start + at, count), outs)


def assemble_norms(inner, *refs):
    sums, (gs, bs, gf, bf) = refs[:-4], refs[-4:]
    lanes = lax.broadcasted_iota(jnp.int32, (8, LANES), 1) >> (inner.bit_length() - 1)
    for n in range(2):
        slow, fast = sums[7 * n : 7 * n + 4], sums[7 * n + 4 : 7 * n + 7]
        for row, gslow, gfast in ((1, gs, gf), (0, bs, bf)):
            at = 0
            for part in slow:
                gslow[n : n + 1, at : at + part.shape[1]] = part[row : row + 1, :]
                at += part.shape[1]
            one, two, three = [jnp.broadcast_to(part[row : row + 1, :], (8, LANES)) for part in fast]
            three = pltpu.roll(three, 2 * inner, 1)
            head = jnp.where(lanes == 0, one, jnp.where(lanes == 1, two, three))
            gfast[n : n + 1, 0:LANES] = head[0:1]
            gfast[n : n + 1, LANES : LANES + 2 * inner] = three[0:1, 0 : 2 * inner]


def on_device(
    x_slow,
    x_fast,
    w_lateral,
    w_slow_time,
    w_slow_space,
    w_slow_point,
    w_fast_time,
    w_fast_space,
    w_fast_point,
    gain_slow,
    bias_slow,
    gain_fast,
    bias_fast,
    clip_size,
    cot_slow,
    cot_fast,
):
    frames, fast_frames = x_slow.shape[0], x_fast.shape[0]
    group = fast_frames // frames
    rows, cols = x_slow.shape[3], x_slow.shape[4]
    spots = rows * cols
    wide, fwide = x_slow.shape[5], x_fast.shape[5]
    lat = w_lateral.shape[3]
    width = w_slow_space.shape[3]
    inner = w_fast_space.shape[3]
    packs = group * fwide
    both = lat + LANES
    m = Masks(spots, cols)
    devices = lax.axis_size("path") * lax.axis_size("rows")
    path = lax.axis_index("path")
    ext = spots + 2 * cols
    lo1, lo2, lo3 = lat, lat + width, lat + 2 * width
    every = slice(None)

    def part(fn, *static):
        return functools.partial(fn, *static)

    xs = x_slow.reshape(frames, spots, wide)
    xf = x_fast.reshape(fast_frames, spots, fwide)
    cs = cot_slow.reshape(frames, spots, wide)
    cf = cot_fast.reshape(fast_frames, spots, fwide)
    wft = jnp.swapaxes(w_fast_time, 2, 3)
    wfs_raw = w_fast_space.reshape(2, 9, inner, inner)
    wsp = w_slow_space.reshape(2, 3, 3 * width, width)

    def packed(value):
        return jnp.concatenate(
            [value[:, 0:inner]] * group + [value[:, inner : 2 * inner]] * group + [value[:, 2 * inner :]],
            axis=1,
        )

    xf_edge = swap_path(jnp.where(path > 0, xf[:2], xf[-2:]))
    xs_edge = swap_path(jnp.where(path > 0, xs[0], xs[-1]))

    def payload(k, *sums):
        size = sum(k.temps[s[1]].shape[1] for s in sums)
        out = k.give((devices, 1, size))
        k.step(spread_sums, *sums, out)
        return out

    def row_out(k, z, mk, col0, size):
        out = k.give((frames, cols, size))
        k.step(part(own_row, m, spots, cols, col0, size), z, mk, out)
        return out

    def edge_out(k, z, mk, size, tail=0):
        out = k.give((spots, size), BF16)
        k.step(part(own_edge, m, 0, tail), z, mk, out)
        return out

    def finish(k, **handles):
        got = k.run()
        return {name: got[handle[1]] for name, handle in handles.items()}

    def other_row(value):
        return swap(value, "rows", 1)

    first_flops = 2 * frames * spots * 7 * fwide * both
    k = Stage("entry")
    mk_out = k.give((m.rows, LANES))
    place = jnp.stack([lax.axis_index("rows"), path]).astype(jnp.int32)
    k.step(
        part(make_masks, m, rows, cols, lax.axis_size("path") - 1), k.scalar(place), k.scalar(clip_size), mk_out
    )
    w7_out = k.give((7 * fwide, both), BF16)
    k.step(part(make_w7, lat, group), k.take(w_lateral, 0), k.take(wft, 0), w7_out)
    fw = k.give((fast_frames + 4, spots, fwide), BF16)
    y = k.give((frames, spots, both))
    sy = k.temp((1, 2 * both))
    edge = k.take(xf_edge)
    k.step(
        part(fast_entry, m, frames, group), k.take(xf), edge, edge, mk_out, w7_out, fw, y, sy, flops=first_flops
    )
    pay = payload(k, sy)
    got = finish(
        k, mk=mk_out, w7=w7_out, fw=fw, y=y, pay=pay, ff_row=row_out(k, y, mk_out, lat, LANES),
        edge=edge_out(k, y, mk_out, both),
    )
    mk = got["mk"]
    saved = [{"fw": got["fw"], "y": got["y"], "w7": got["w7"]}, {}]
    st = gather_sums(got["pay"])
    saved[0]["ff_row"] = other_row(got["ff_row"])
    saved[0]["y_edge"] = swap_path(got["edge"])
    mk, wft, gain_fast, bias_fast = lax.optimization_barrier((mk, wft, gain_fast, bias_fast))
    gf, bf = packed(gain_fast), packed(bias_fast)
    k = Stage("prepare")
    w7_out = k.give((7 * fwide, both), BF16)
    k.step(part(make_w7, lat, group), k.take(w_lateral, 1), k.take(wft, 1), w7_out)
    blocks = []
    for n in range(2):
        blocks += [k.give((3, 3 * LANES, LANES), BF16), k.give((LANES, packs), BF16)]
        k.step(part(make_blocks, group), k.take(wfs_raw, n), k.take(w_fast_point, n), *blocks[-2:])
    got = finish(k, w7=w7_out, wfs0=blocks[0], wfp0=blocks[1], wfs1=blocks[2], wfp1=blocks[3])
    saved[1]["w7"] = got["w7"]
    wfs, wfp = [got["wfs0"], got["wfs1"]], [got["wfp0"], got["wfp1"]]
    k = Stage("slow_partial")
    xm = k.give((frames + 2, spots, wide), BF16)
    fpart = k.give((frames, spots, width))
    edge = k.take(xs_edge)
    k.step(
        part(slow_partial, m, frames),
        k.take(xs), edge, edge, k.take(mk), k.take(w_slow_time, 0, every, slice(0, wide)), xm, fpart,
        flops=2 * frames * spots * 3 * wide * width,
    )
    got = finish(k, sw=xm, fpart=fpart)
    saved[0]["sw"] = got["sw"]
    fpart_in = got["fpart"]

    for n in range(2):
        v = saved[n]
        k = Stage("join")
        mk_in, gs, bs = k.take(mk), k.take(gain_slow), k.take(bias_slow)
        st_in = k.take(st)
        names = {}
        if n == 0:
            fpart = k.take(fpart_in)
        else:
            fpart = k.temp((frames, spots, width))
            n3, next_sw = k.give((2, wide)), k.give((frames + 2, spots, wide), BF16)
            names.update(sw=next_sw, n3=n3)
            k.step(part(keep_norm, 2 * both, wide, m.slow), st_in, mk_in, n3)
            spans = [m.prev] + [m.main] * frames + [m.next]
            for f in range(frames + 2):
                k.step(
                    part(slow_next, 0, lo3, spans[f]),
                    k.take(saved[0]["third"], f), k.take(saved[0]["sw"], f), k.peek(n3), gs, bs, mk_in,
                    k.piece(next_sw, f),
                )
            k.step(
                part(time_partial, frames),
                k.peek(next_sw), k.take(w_slow_time, 1, every, slice(0, wide)), fpart,
                flops=2 * frames * spots * 3 * wide * width,
            )
        y_in, edge = k.take(v["y"]), k.take(v["y_edge"])
        jl = k.give((frames, spots, lat), BF16)
        first = k.give((frames, spots, width))
        nl = k.give((2, lat))
        s_first, s_fs = k.temp((1, 2 * width)), k.temp((1, 2 * LANES))
        k.step(
            part(lat_join, m, n, frames, lat),
            st_in, y_in, edge, edge, fpart, k.take(w_slow_time, n, every, slice(wide, wide + lat)), gs, bs, mk_in,
            jl, first, s_first, nl, k.temp((frames + 2, spots, lat), BF16),
            flops=2 * frames * spots * 3 * lat * width,
        )
        fa1 = k.give((frames, ext, LANES), BF16)
        fs = k.give((frames, spots, LANES))
        nf1 = k.give((2, LANES))
        k.step(
            part(space_forward, m, n, frames, cols, 0, 2 * lat, LANES, lat, True, m.fast),
            st_in, y_in, k.take(v["ff_row"]), k.take(wfs[n]), k.take(gf), k.take(bf), mk_in,
            fa1, fs, s_fs, nf1, k.temp((frames, ext, 3 * LANES), BF16),
            flops=2 * frames * spots * 9 * LANES * LANES,
        )
        pay = payload(k, s_first, s_fs)
        got = finish(
            k, jl=jl, first=first, nl=nl, fa1=fa1, fs=fs, nf1=nf1, pay=pay,
            first_row=row_out(k, first, mk_in, 0, width), fs_row=row_out(k, fs, mk_in, 0, LANES),
            first_edge=edge_out(k, first, mk_in, width), **names,
        )
        st = gather_sums(got["pay"])
        for name in ("jl", "first", "nl", "fa1", "fs", "nf1"):
            v[name] = got[name]
        if n == 1:
            saved[1]["sw"], saved[0]["n3"] = got["sw"], got["n3"]
        first_row = other_row(got["first_row"])
        st, v["fs_row"], v["first_edge"] = lax.optimization_barrier(
            (st, other_row(got["fs_row"]), swap_path(got["first_edge"]))
        )
        k = Stage("space")
        mk_in, st_in = k.take(mk), k.take(st)
        a1 = k.give((frames, ext, width), BF16)
        second = k.give((frames, spots, width))
        n1 = k.give((2, width))
        s_second, s_ft = k.temp((1, 2 * width)), k.temp((1, 2 * LANES))
        k.step(
            part(space_forward, m, n, frames, cols, lo1, 0, width, 0, False, m.slow),
            st_in, k.take(v["first"]), k.take(first_row), k.take(wsp, n), k.take(gain_slow), k.take(bias_slow), mk_in,
            a1, second, s_second, n1, k.temp((frames, ext, 3 * width), BF16),
            flops=2 * frames * spots * 9 * width * width,
        )
        fa2 = k.give((frames, spots, LANES), BF16)
        ft = k.give((frames, spots, packs), BF16)
        nf2 = k.give((2, LANES))
        k.step(
            part(fast_third, m, n, frames, LANES, 2 * width),
            st_in, k.take(v["fs"]), k.take(wfp[n]), k.take(gf), k.take(bf), mk_in, fa2, ft, s_ft, nf2,
            flops=2 * frames * spots * LANES * packs,
        )
        pay = payload(k, s_second, s_ft)
        names = {"second_row": row_out(k, second, mk_in, 0, width)}
        if n == 0:
            names["second_edge"] = edge_out(k, second, mk_in, width)
            names["ft_edge"] = edge_out(k, ft, mk_in, 2 * fwide, (group - 2) * fwide)
        got = finish(k, a1=a1, second=second, n1=n1, fa2=fa2, ft=ft, nf2=nf2, pay=pay, **names)
        st = gather_sums(got["pay"])
        for name in ("a1", "second", "n1", "fa2", "ft", "nf2"):
            v[name] = got[name]
        st, v["second_row"] = lax.optimization_barrier((st, other_row(got["second_row"])))
        halo = 1 - n
        edges = []
        k = Stage("third")
        if n == 0:
            ft_edge = k.take(swap_path(got["ft_edge"]))
            edges = [k.take(swap_path(got["second_edge"]))] * 2
        mk_in, st_in = k.take(mk), k.take(st)
        a2 = k.give((frames, spots, width), BF16)
        third = k.give((frames + 2 * halo, spots, wide), BF16)
        n2 = k.give((2, width))
        nf3 = k.give((2, LANES))
        s_third = k.temp((1, 2 * wide))
        names = {}
        if n == 0:
            names.update(
                fw=k.give((fast_frames + 4, spots, fwide), BF16),
                y=k.give((frames, spots, both)),
            )
            s_fast = k.temp((1, 2 * both))
            k.step(
                part(fast_next, m, n, frames, group, 2 * LANES, 2 * width),
                st_in, k.take(v["ft"]), ft_edge, ft_edge, k.take(v["fw"]), k.take(saved[1]["w7"]),
                k.take(gf), k.take(bf), mk_in, names["fw"], names["y"], s_fast, nf3,
                flops=first_flops,
            )
        else:
            names.update(out_fast=k.give((fast_frames, spots, fwide)), pre_f=k.give((fast_frames, spots, fwide), BF16))
            s_fast = k.temp((1, 2 * LANES))
            k.step(
                part(fast_last, m, n, frames, group, 2 * LANES, 2 * width),
                st_in, k.take(v["ft"]), k.take(v["fw"], slice(2, 2 + fast_frames)), k.take(cf), k.take(gf), k.take(bf), mk_in,
                names["out_fast"], names["pre_f"], s_fast, nf3,
            )
        aw = k.temp((frames + 2 * halo, spots, width), BF16)
        k.step(
            part(slow_acts, m, n, frames, lo2, halo),
            st_in, k.take(v["second"]), *edges, k.take(gain_slow), k.take(bias_slow), mk_in, a2, n2, aw,
        )
        for at in range(0, wide, 256):
            lanes = slice(at, at + 256)
            k.step(
                part(slow_third, frames, halo, at),
                aw, k.take(w_slow_point, n, every, lanes), k.piece(third, every, every, lanes), s_third,
                flops=2 * frames * spots * width * 256,
            )
        if n == 0:
            pay = payload(k, s_fast, s_third)
            names["ff_row"] = row_out(k, names["y"], mk_in, lat, LANES)
            names["y_edge"] = edge_out(k, names["y"], mk_in, both)
        else:
            pay = payload(k, s_third, s_fast)
        got = finish(k, a2=a2, third=third, n2=n2, nf3=nf3, pay=pay, **names)
        st = gather_sums(got["pay"])
        for name in ("a2", "third", "n2", "nf3"):
            v[name] = got[name]
        if n == 0:
            saved[1].update(
                fw=got["fw"], y=got["y"], ff_row=other_row(got["ff_row"]), y_edge=swap_path(got["y_edge"])
            )
        else:
            out_fast, pre_f = got["out_fast"], got["pre_f"]

    def third_back(k, n, at, st_in, mk_in, pre):
        v = saved[n]
        d3, e2 = k.give((frames, spots, wide), BF16), k.give((frames, spots, width))
        s, gb = k.temp((1, 2 * width)), k.give((2, wide))
        gs = k.take(gain_slow)
        k.step(part(keep_sums, at, wide), st_in, gb)
        for t in range(frames):
            k.step(
                part(slow_third_grad, m, n, lo3),
                k.take(pre, t), k.take(v["third"], t + 1 - n), k.take(v["n3"]), k.peek(gb), gs, mk_in,
                k.piece(d3, t),
            )
        k.step(
            part(slow_third_back, m, n, frames, lo2),
            k.peek(d3), k.take(v["second"]), k.take(v["n2"]), k.take(w_slow_point, n), gs, k.take(bias_slow), mk_in,
            e2, s, flops=2 * frames * spots * width * wide,
        )
        return dict(d3=d3, e2=e2, gb3=gb), s

    def fast_back3(k, n, at, st_in, mk_in, pre):
        v = saved[n]
        d3, e2 = k.give((frames, spots, packs), BF16), k.give((frames, spots, LANES))
        s, gb = k.temp((1, 2 * LANES)), k.give((2, LANES))
        k.step(
            part(fast_third_back, m, n, frames, group, 2 * LANES, LANES, at),
            st_in, k.take(pre), k.take(v["ft"]), k.take(v["nf3"]), k.take(v["fs"]), k.take(v["nf2"]),
            k.take(wfp[n]), k.take(gf), k.take(bf), mk_in, d3, e2, s, gb,
            flops=2 * frames * spots * LANES * packs,
        )
        return dict(d3f=d3, ef2=e2, gbf3=gb), s

    def second_back(k, n, at, st_in, mk_in, e2, e2_row):
        v = saved[n]
        d2, e1 = k.give((frames, spots, width), BF16), k.give((frames, spots, width))
        s, gb = k.temp((1, 2 * width)), k.give((2, width))
        k.step(
            part(space_back, m, n, frames, cols, lo2, lo1, at, width, 0, False, m.slow),
            st_in, k.take(e2), k.take(e2_row), k.take(v["second"]), k.take(v["second_row"]), k.take(v["n2"]),
            k.take(v["first"]), k.take(v["n1"]), k.take(wsp, n), k.take(gain_slow), k.take(bias_slow), mk_in,
            d2, e1, s, gb, k.temp((frames, ext, 3 * width), BF16),
            flops=2 * frames * spots * 9 * width * width,
        )
        return dict(d2=d2, e1=e1, gb2=gb), s

    def fast_back2(k, n, at, st_in, mk_in, ef2, ef2_row):
        v = saved[n]
        d2, e1 = k.give((frames, spots, LANES), BF16), k.give((frames, spots, LANES))
        s, gb = k.temp((1, 2 * LANES)), k.give((2, LANES))
        k.step(
            part(space_back, m, n, frames, cols, LANES, 0, at, LANES, lat, True, m.fast),
            st_in, k.take(ef2), k.take(ef2_row), k.take(v["fs"]), k.take(v["fs_row"]), k.take(v["nf2"]),
            k.take(v["y"]), k.take(v["nf1"]), k.take(wfs[n]), k.take(gf), k.take(bf), mk_in,
            d2, e1, s, gb, k.temp((frames, ext, 3 * LANES), BF16),
            flops=2 * frames * spots * 9 * LANES * LANES,
        )
        return dict(d2f=d2, ef1=e1, gbf2=gb), s

    def first_back(k, n, st_in, mk_in, e1, e1_edge):
        v = saved[n]
        dw, el = k.give((frames + 2, spots, width), BF16), k.give((frames, spots, lat))
        s, gb = k.temp((1, 2 * lat)), k.give((2, width))
        edge, zedge = k.take(e1_edge), k.take(v["first_edge"])
        k.step(
            part(slow_first_back, m, n, frames, lo1, 0),
            st_in, k.take(e1), edge, edge, k.take(v["first"]), zedge, zedge, k.take(v["n1"]),
            k.take(w_slow_time, n, every, slice(wide, wide + lat)), k.take(v["y"]), k.take(v["nl"]),
            k.take(gain_slow), k.take(bias_slow), mk_in, dw, el, s, gb, flops=2 * frames * spots * 3 * lat * width,
        )
        return dict(dw=dw, el=el, gb1=gb), s

    def fast_back1(k, n, st1, at1, stl, atl, mk_in, el, el_edge, ef1, ef1_edge):
        v = saved[n]
        dl, df = k.give((frames, spots, lat), BF16), k.give((frames, spots, LANES), BF16)
        beside = [k.give((spots, lat), BF16), k.give((spots, LANES), BF16), k.give((spots, LANES), BF16)]
        gbl, gb1 = k.give((2, lat)), k.give((2, LANES))
        edge, yedge = k.take(ef1_edge), k.take(v["y_edge"])
        k.step(
            part(fast_first_back, m, n, frames, 0, at1, atl),
            st1, stl, k.take(el), k.take(el_edge), k.take(ef1), edge, edge, k.take(v["y"]), yedge, yedge,
            k.take(v["nl"]), k.take(v["nf1"]), k.take(gain_slow), k.take(gf), mk_in, dl, df, *beside, gbl, gb1,
        )
        return dict(dl=dl, df=df, dln=beside[0], dfp=beside[1], dfn=beside[2], gbl=gbl, gbf1=gb1)

    def weights_point(n, d3):
        k = Stage("point_weights")
        out = k.give((wide // 256, width, 256), BF16)
        k.step(point_weights, k.take(saved[n]["a2"]), k.take(d3), out, flops=2 * frames * spots * width * wide)
        return k.run()[0].reshape(-1, 256)

    def weights_space(n, d2):
        k = Stage("space_weights")
        out = k.give((3, 3 * width, width), BF16)
        k.step(
            part(space_weights, cols), k.take(saved[n]["a1"]), k.take(d2), out,
            k.temp((frames, ext, 3 * width), BF16), flops=2 * frames * spots * 9 * width * width,
        )
        return k.run()[0].reshape(-1, 256)

    def weights_time(n, dw):
        k = Stage("time_weights")
        out = k.give((3, wide + lat, width), BF16)
        k.step(
            part(time_weights, 1), k.take(saved[n]["sw"]), k.take(saved[n]["jl"]), k.take(dw), out,
            flops=2 * frames * spots * 3 * (wide + lat) * width,
        )
        return k.run()[0].reshape(-1, 256)

    def weights_fast(n, dl, df, d2, d3):
        v = saved[n]
        k = Stage("fast_weights")
        out = k.give((7 * LANES - LANES, 2 * LANES), BF16)
        k.step(
            part(fast_weights, group, cols, lat),
            k.take(v["fw"]), k.take(dl), k.take(df), k.take(v["fa1"]), k.take(d2), k.take(v["fa2"]), k.take(d3),
            out, k.temp((frames, ext, 3 * LANES), BF16), flops=first_flops,
        )
        return k.run()[0]

    b1, b0 = {}, {}
    k = Stage("last")
    mk_in, st_in = k.take(mk), k.take(st)
    out_slow, pre = k.give((frames, spots, wide)), k.give((frames, spots, wide), BF16)
    n3 = k.give((2, wide))
    s_pre, one, two = k.temp((1, 2 * wide)), k.temp((8, wide)), k.temp((8, wide))
    k.step(part(keep_norm, 0, wide, m.slow), st_in, mk_in, n3)
    k.step(clear, one, two)
    for t in range(frames):
        k.step(
            part(slow_last, m, 1, lo3),
            k.take(saved[1]["third"], t), k.take(saved[1]["sw"], t + 1), k.take(cs, t), k.peek(n3),
            k.take(gain_slow), k.take(bias_slow), mk_in, k.piece(out_slow, t), k.piece(pre, t), one, two,
        )
    k.step(close_sums, one, two, s_pre)
    names, s_ef2 = fast_back3(k, 1, 2 * wide, st_in, mk_in, pre_f)
    pay = payload(k, s_pre, s_ef2)
    ef2_row = row_out(k, names["ef2"], mk_in, 0, LANES)
    b1 = finish(k, out_slow=out_slow, pre=pre, n3=n3, pay=pay, ef2_row=ef2_row, **names)
    saved[1]["n3"] = b1["n3"]
    out_slow = b1["out_slow"]
    st = gather_sums(b1["pay"])

    k = Stage("back_third")
    ef2_row = other_row(b1["ef2_row"])
    mk_in, st_in = k.take(mk), k.take(st)
    names, s_e2 = third_back(k, 1, 0, st_in, mk_in, b1["pre"])
    more, s_ef1 = fast_back2(k, 1, 2 * wide, st_in, mk_in, b1["ef2"], ef2_row)
    pay = payload(k, s_e2, s_ef1)
    e2_row, ef1_edge = row_out(k, names["e2"], mk_in, 0, width), edge_out(k, more["ef1"], mk_in, LANES)
    b1.update(finish(k, pay=pay, e2_row=e2_row, ef1_edge=ef1_edge, **names, **more))
    st = st_ef1 = gather_sums(b1["pay"])
    e2_row = other_row(b1["e2_row"])
    st, ef1_edge = lax.optimization_barrier((st, swap_path(b1["ef1_edge"])))
    point1 = weights_point(1, b1["d3"])

    k = Stage("back_space")
    mk_in, st_in = k.take(mk), k.take(st)
    names, s_e1 = second_back(k, 1, 0, st_in, mk_in, b1["e2"], e2_row)
    pay = payload(k, s_e1)
    e1_edge = edge_out(k, names["e1"], mk_in, width)
    b1.update(finish(k, pay=pay, e1_edge=e1_edge, **names))
    st = gather_sums(b1["pay"])
    e1_edge = swap_path(b1["e1_edge"])
    space1 = weights_space(1, b1["d2"])

    k = Stage("back_first")
    mk_in, st_in = k.take(mk), k.take(st)
    names, s_el = first_back(k, 1, st_in, mk_in, b1["e1"], e1_edge)
    names["down"], s_down = k.give((frames, spots, wide), BF16), k.temp((1, 2 * wide))
    for at in range(0, wide, 256):
        lanes = slice(at, at + 256)
        k.step(
            part(slow_input_back, m, 1, frames, lo3, at),
            k.peek(names["dw"]), k.take(w_slow_time, 1, every, lanes), k.take(b1["pre"], every, every, lanes),
            k.take(saved[0]["sw"], slice(1, 1 + frames), every, lanes),
            k.take(saved[0]["third"], slice(1, 1 + frames), every, lanes),
            k.take(saved[0]["n3"]), k.take(gain_slow), k.take(bias_slow), mk_in,
            k.piece(names["down"], every, every, lanes), s_down,
            flops=2 * frames * spots * 3 * 256 * width,
        )
    pay = payload(k, s_el, s_down)
    el_edge = edge_out(k, names["el"], mk_in, lat)
    b1.update(finish(k, pay=pay, el_edge=el_edge, **names))
    st = gather_sums(b1["pay"])
    el_edge = swap_path(b1["el_edge"])
    time1 = weights_time(1, b1["dw"])
    sizes1 = [point1.shape[0], space1.shape[0], time1.shape[0]]
    ones = jnp.concatenate([point1, space1, time1], axis=0)
    st, ones, el_edge = lax.optimization_barrier((st, ones, el_edge))
    ones = lax.psum(ones, AXES)

    GRADS = ("df", "dln", "dfp", "dfn")
    SUMS = ("gbl", "gb1", "gb2", "gb3", "gbf1", "gbf2", "gbf3")
    steps = exchange_steps()
    core, across, down = steps[:3]
    seen = {}

    def spread_both(one, two, tied=()):
        one, two = [one, swap(one, *down)], [two, swap(two, *across)]
        one, two = [jnp.stack(pair) for pair in (one, two)]
        one, two = [one, swap(one, *across)], [two, swap(two, *down)]
        one, two, tied = lax.optimization_barrier((one, two, tied))
        return [pair + [swap(half, *core) for half in pair] for pair in (one, two)], tied

    def block_zero(st=st, el_edge=el_edge, ef1_edge=ef1_edge, b1=b1, b0=b0):
        b1, b0 = dict(b1), dict(b0)
        k = Stage("back_third")
        mk_in, st_in = k.take(mk), k.take(st)
        names, s_e2 = third_back(k, 0, 2 * lat, st_in, mk_in, b1["down"])
        more = fast_back1(
            k, 1, k.take(st_ef1), 2 * width, st_in, 0, mk_in, b1["el"], el_edge, b1["ef1"], ef1_edge
        )
        inner_grads = [more[name] for name in ("dl", "df", "dln", "dfp", "dfn")]
        more["downf"], s_pf = k.give((fast_frames, spots, fwide), BF16), k.temp((1, 2 * LANES))
        k.step(
            part(fast_input_back, m, 1, frames, group, 2 * LANES, False),
            *inner_grads, k.take(saved[1]["w7"]), k.take(pre_f), k.take(saved[0]["fw"]), k.take(saved[0]["ft"]),
            k.take(saved[0]["nf3"]), k.take(gf), k.take(bf), mk_in, more["downf"], s_pf,
            k.temp((fast_frames + 4, spots, fwide)), flops=first_flops,
        )
        pay = payload(k, s_e2, s_pf)
        e2_row = row_out(k, names["e2"], mk_in, 0, width)
        got = finish(k, pay=pay, e2_row=e2_row, **names, **more)
        for name in more:
            b1[name] = got[name]
        b0.update({name: got[name] for name in names})
        st = gather_sums(got["pay"])
        e2_row = other_row(got["e2_row"])
        point0 = weights_point(0, b0["d3"])
        fast_1 = weights_fast(1, b1["dl"], b1["df"], b1["d2f"], b1["d3f"])

        k = Stage("back_space")
        mk_in, st_in = k.take(mk), k.take(st)
        names, s_e1 = second_back(k, 0, 0, st_in, mk_in, b0["e2"], e2_row)
        more, s_ef2 = fast_back3(k, 0, 2 * width, st_in, mk_in, b1["downf"])
        pay = payload(k, s_e1, s_ef2)
        e1_edge, ef2_row = edge_out(k, names["e1"], mk_in, width), row_out(k, more["ef2"], mk_in, 0, LANES)
        b0.update(finish(k, pay=pay, e1_edge=e1_edge, ef2_row=ef2_row, **names, **more))
        st = gather_sums(b0["pay"])
        e1_edge, ef2_row = swap_path(b0["e1_edge"]), other_row(b0["ef2_row"])
        space0 = weights_space(0, b0["d2"])
        mid = jnp.concatenate([fast_1, point0, space0], axis=0)
        st, mid = lax.optimization_barrier((st, mid))

        k = Stage("back_first")
        mk_in, st_in = k.take(mk), k.take(st)
        names, s_el = first_back(k, 0, st_in, mk_in, b0["e1"], e1_edge)
        more, s_ef1 = fast_back2(k, 0, 2 * width, st_in, mk_in, b0["ef2"], ef2_row)
        pay = payload(k, s_el, s_ef1)
        el_edge, ef1_edge = edge_out(k, names["el"], mk_in, lat), edge_out(k, more["ef1"], mk_in, LANES)
        b0.update(finish(k, pay=pay, el_edge=el_edge, ef1_edge=ef1_edge, **names, **more))
        b0["dw"], mid = lax.optimization_barrier((b0["dw"], mid))
        mid = halve(mid, *core)
        st = gather_sums(b0["pay"])
        el_edge, ef1_edge = swap_path(b0["el_edge"]), swap_path(b0["ef1_edge"])
        time0 = weights_time(0, b0["dw"])
        st, mid = lax.optimization_barrier((st, mid))
        mid = halve_both(*parted(mid), across, down)
        k = Stage("back_fast")
        mk_in, st_in = k.take(mk), k.take(st)
        more = fast_back1(k, 0, st_in, 2 * lat, st_in, 0, mk_in, b0["el"], el_edge, b0["ef1"], ef1_edge)
        v = saved[0]
        rest = k.give((6 * LANES, 2 * LANES), BF16)
        k.step(
            part(fast_weights, group, cols, lat),
            k.take(v["fw"]), more["dl"], more["df"], k.take(v["fa1"]), k.take(b0["d2f"]), k.take(v["fa2"]),
            k.take(b0["d3f"]), rest, k.temp((frames, ext, 3 * LANES), BF16), flops=first_flops,
        )
        got = finish(k, rest=rest, **more)
        b0.update(got)
        seen["rows"] = [piece.shape[0] for piece in (fast_1, point0, space0, time0, got["rest"])]
        late = halve(jnp.concatenate([time0, got["rest"]], axis=0), *core)
        mid, late, dw0 = lax.optimization_barrier((mid, late, b0["dw"]))
        mid, late = halve_both(*mid, down, across), halve_both(*parted(late), across, down)
        mid, late, dl0 = lax.optimization_barrier((mid, late, b0["dl"]))
        k = Stage("slow_input")
        gx_slow = k.give((frames, spots, wide))
        k.step(
            part(slow_input_last, m, frames),
            k.take(dw0), k.take(w_slow_time, 0, every, slice(0, wide)), k.take(b1["down"]), k.take(mk), gx_slow,
            flops=2 * frames * spots * 3 * wide * width,
        )
        (gx_slow,) = k.run()
        k = Stage("fast_input")
        gx_fast = k.give((fast_frames, spots, fwide))
        k.step(
            part(fast_input_back, m, 0, frames, group, 2 * LANES, True),
            k.take(dl0), *[k.take(b0[name]) for name in GRADS], k.take(saved[0]["w7"]), k.take(b1["downf"]), k.take(mk), gx_fast,
            k.temp((fast_frames + 4, spots, fwide)), flops=first_flops,
        )
        (gx_fast,) = k.run()
        def along(value, ahead=steps[3:]):
            for step in ahead:
                value = halve(value, *step)
            value = value.astype(BF16)
            for step in reversed(steps[3:]):
                value = double(value, *step)
            return value

        mid, late = jnp.concatenate(mid, axis=0), halve_both(*late, down, across)
        for step in steps[3:4]:
            mid = halve(mid, *step)
        mid, late, gx_slow = lax.optimization_barrier((mid, late, gx_slow))
        late = jnp.concatenate(late, axis=0)
        for step in steps[3:4]:
            late = halve(late, *step)
        for step in steps[4:5]:
            mid = halve(mid, *step)
        mid, late, gx_fast = lax.optimization_barrier((mid, late, gx_fast))
        mid, late = along(mid, steps[5:]), along(late, steps[4:])
        (mid_one, mid_two), _ = spread_both(*parted(mid))
        sums = [b0[name] for name in SUMS] + [b1[name] for name in ("gbl", "gbf1")]
        return (*mid_one, *mid_two, late, gx_slow, gx_fast, *sums)

    like = jax.eval_shape(block_zero)
    got = lax.cond(
        clip_size[0, 0] > 0, block_zero, lambda: tuple(jnp.zeros(o.shape, o.dtype) for o in like)
    )
    mid_one, mid_two = list(got[:4]), list(got[4:8])
    late, gx_slow, gx_fast = got[8:11]
    b0 = dict(zip(SUMS, got[11:18]))
    b1["gbl"], b1["gbf1"] = got[18:20]

    time_rows, space_rows = 3 * (wide + lat), 9 * width
    k = Stage("assemble_one")
    ones_in = k.take(ones)
    gtime, gspace = k.give((2, time_rows, width), F32, 1), k.give((2, space_rows, width), F32, 1)
    gpoint = k.give((2, width, wide), F32, 1)
    k.step(part(copy_rows, sizes1[0] + sizes1[1]), ones_in, gtime)
    k.step(part(copy_rows, sizes1[0]), ones_in, gspace)
    k.step(part(copy_columns, 0), ones_in, gpoint)
    half_done = k.run()

    (one, two), half_done = spread_both(*parted(late), half_done)

    core_bit = lax.axis_index("rows") % 2
    down_bit = (lax.axis_index("rows") // 2) % 2

    k = Stage("assemble")
    flip_one = k.scalar((core_bit * 4 + path * 2 + down_bit).astype(jnp.int32).reshape(1))
    flip_two = k.scalar((core_bit * 4 + down_bit * 2 + path).astype(jnp.int32).reshape(1))
    one_in = k.take_blocks(one, flip_one, every)
    two_in = k.take_blocks(two, flip_two, every)
    mid_one, mid_two = k.take_blocks(mid_one, flip_one, every), k.take_blocks(mid_two, flip_two, every)
    sizes = seen["rows"]
    half_mid, half_late = sum(sizes[:3]) // 2, sum(sizes[3:]) // 2
    gspace = k.give((2, space_rows, width), F32, 0, half_done[1])
    k.step(part(place_rows, sizes[0] + sizes[1], 0, half_mid), mid_one, mid_two, gspace)
    gpoint = k.give((2, width, wide), F32, 0, half_done[2])
    k.step(part(place_columns, sizes[0], 0, half_mid), mid_one, mid_two, gpoint)
    gtime = k.give((2, time_rows, width), F32, 0, half_done[0])
    k.step(part(place_rows, 0, 0, half_late), one_in, two_in, gtime)
    fast_outs = [
        k.give((2, 5 * fwide, lat)), k.give((2, 3, inner, fwide)), k.give((2, 9, inner, inner)),
        k.give((2, inner, fwide)),
    ]
    k.step(part(place_fast, inner, half_mid, half_late, sizes[3]), mid_one, mid_two, one_in, two_in, *fast_outs)
    sums = [k.take(b[name]) for b in (b0, b1) for name in ("gbl", "gb1", "gb2", "gb3", "gbf1", "gbf2", "gbf3")]
    norm_outs = [k.give(like.shape) for like in (gain_slow, bias_slow, gain_fast, bias_fast)]
    k.step(part(assemble_norms, inner), *sums, *norm_outs)
    got = k.run()
    glat, gft, gfs, gfp = [got[h[1]] for h in fast_outs]

    return (
        out_slow.reshape(x_slow.shape),
        out_fast.reshape(x_fast.shape),
        gx_slow.reshape(x_slow.shape),
        gx_fast.reshape(x_fast.shape),
        glat.reshape(w_lateral.shape),
        got[gtime[1]].reshape(w_slow_time.shape),
        got[gspace[1]].reshape(w_slow_space.shape),
        got[gpoint[1]],
        jnp.swapaxes(gft, 2, 3),
        gfs.reshape(w_fast_space.shape),
        gfp,
        *[got[h[1]] for h in norm_outs],
    )


def solution(mesh):
    spread = P("path", None, "rows", None, None, None)
    return jax.shard_map(
        on_device,
        mesh=mesh,
        in_specs=(spread, spread) + (P(),) * 12 + (spread, spread),
        out_specs=(spread,) * 4 + (P(),) * 11,
        check_vma=False,
    )
```

```python
import functools

import jax
import jax.numpy as jnp
import numpy as np
from jax import lax
from jax.experimental import pallas as pl
from jax.experimental.pallas import tpu as pltpu
from jax.sharding import PartitionSpec as P

TS = 8
TF = 32
F32 = jnp.float32
BF16 = jnp.bfloat16
EPSILON = 1e-05
LANES = 128
AXES = ("path", "rows")
VMEM_LIMIT = 56 * 2**20


def swap(value, axis, stride):
    pairs = [(source, source ^ stride) for source in range(lax.axis_size(axis))]
    return lax.ppermute(value, axis, pairs)


def gather_sums(spread):
    return lax.all_to_all(spread, AXES, 0, 0, tiled=True)


def swap_path(value):
    assert lax.axis_size("path") == 2
    return lax.ppermute(value, "path", [(0, 1), (1, 0)])


def exchange_steps():
    steps = [("rows", 1), ("path", 1)]
    stride = 2
    while stride < lax.axis_size("rows"):
        steps.append(("rows", stride))
        stride *= 2
    return steps


def halve(value, axis, stride):
    size = value.shape[0] // 2
    upper = (lax.axis_index(axis) // stride) % 2
    keep = lax.dynamic_slice_in_dim(value, upper * size, size, 0)
    give = lax.dynamic_slice_in_dim(value, (1 - upper) * size, size, 0)
    return keep.astype(F32) + swap(give.astype(BF16), axis, stride).astype(F32)


def double(value, axis, stride):
    upper = (lax.axis_index(axis) // stride) % 2
    got = swap(value, axis, stride)
    return jnp.concatenate(
        [jnp.where(upper == 0, value, got), jnp.where(upper == 0, got, value)], axis=0
    )


def halve_both(one, two, first, second):
    return halve(one, *first), halve(two, *second)


def parted(value):
    size = value.shape[0] // 2
    return value[:size], value[size:]


class Stage:
    def __init__(self, name):
        self.name = name
        self.arrays, self.views, self.scalars, self.pairs = [], [], [], []
        self.outs, self.temps, self.steps = [], [], []
        self.entries, self.ontos = [], []
        self.flops = 0

    def take(self, array, *view):
        for at, known in enumerate(self.arrays):
            if known is array:
                break
        else:
            at = len(self.arrays)
            self.arrays.append(array)
        for k, (other, seen) in enumerate(self.views):
            if other == at and seen == view:
                return ("in", k)
        self.views.append((at, view))
        return ("in", len(self.views) - 1)

    def take_blocks(self, values, flip, rows):
        self.pairs.append(([self.take(value, slice(None), rows) for value in values], flip))
        return ("pair", len(self.pairs) - 1)

    def scalar(self, array):
        self.scalars.append(array)
        return ("scalar", len(self.scalars) - 1)

    def give(self, dims, dtype=F32, at=None, onto=None):
        self.outs.append(jax.ShapeDtypeStruct(tuple(dims), dtype))
        self.entries.append(at)
        self.ontos.append(onto)
        return ("out", len(self.outs) - 1)

    def piece(self, handle, *index):
        return ("piece", (handle[1], index))

    def peek(self, handle):
        return ("peek", handle[1])

    def temp(self, dims, dtype=F32):
        self.temps.append(pltpu.VMEM(tuple(dims), dtype))
        return ("temp", len(self.temps) - 1)

    def step(self, fn, *handles, flops=0):
        self.flops += flops
        self.steps.append((fn, handles))

    def sem(self, view, block):
        return 8 * view + block

    def view_shape(self, view):
        at, index = view
        return np.broadcast_to(np.zeros((), np.int8), self.arrays[at].shape)[index].shape

    def run(self):
        arrays, views, outs, steps, pairs = self.arrays, self.views, self.outs, self.steps, self.pairs
        order, home = [], {}
        for k, (members, flip) in enumerate(pairs):
            for j, member in enumerate(members):
                home[member[1]] = (k, j, flip)
        under = [onto for onto in self.ontos if onto is not None]

        def need(handle):
            if handle[0] == "in":
                return [handle[1]]
            return [part[1] for part in pairs[handle[1]][0]] if handle[0] == "pair" else []

        for _, handles in steps:
            for handle in handles:
                for k in need(handle):
                    if k not in order:
                        order.append(k)

        def body(*refs):
            refs = list(refs)

            def cut(count):
                taken = refs[:count]
                del refs[:count]
                return taken

            scalars, hbm_in = cut(len(self.scalars)), cut(len(arrays))
            cut(len(under))
            hbm_out = cut(len(outs))
            alone = [k for k in range(len(views)) if k not in home]
            held = dict(zip(alone, cut(len(alone))))
            joint, made, temps, (sems,) = cut(len(pairs)), cut(len(outs)), cut(len(self.temps)), refs
            copies = {}
            for k in order:
                at, index = views[k]
                src = hbm_in[at].at[index] if index else hbm_in[at]
                if k in home:
                    pair, second, flip = home[k]
                    count = self.view_shape(views[k])[0]
                    copies[k] = []
                    for block in range(count):
                        to = (second * count + block) ^ scalars[flip[1]][0]
                        copies[k].append(
                            pltpu.make_async_copy(src.at[block], joint[pair].at[to], sems.at[self.sem(k, block)])
                        )
                else:
                    copies[k] = [pltpu.make_async_copy(src, held[k], sems.at[self.sem(k, 0)])]
                for copy in copies[k]:
                    copy.start()
            waited, sent = set(), {}
            for fn, handles in steps:
                given = []
                for handle in handles:
                    for k in need(handle):
                        if k not in waited:
                            for copy in copies[k]:
                                copy.wait()
                            waited.add(k)
                    if handle[0] == "piece":
                        given.append(made[handle[1][0]].at[handle[1][1]])
                        continue
                    place = {"in": held, "pair": joint, "out": made, "peek": made, "temp": temps, "scalar": scalars}
                    given.append(place[handle[0]][handle[1]])
                fn(*given)
                for kind, k in handles:
                    if kind == "out" and k not in sent:
                        to = hbm_out[k] if self.entries[k] is None else hbm_out[k].at[self.entries[k]]
                        sent[k] = [pltpu.make_async_copy(made[k], to, sems.at[8 * (len(views) + k)])]
                        sent[k][0].start()
                    elif kind == "piece":
                        k, index = k
                        done = sent.setdefault(k, [])
                        sem = sems.at[8 * (len(views) + k) + len(done)]
                        done.append(pltpu.make_async_copy(made[k].at[index], hbm_out[k].at[index], sem))
                        done[-1].start()
            for done in sent.values():
                for copy in done:
                    copy.wait()

        moved = sum(a.size * a.dtype.itemsize for a in outs)
        for view in views:
            moved += int(np.prod(self.view_shape(view))) * arrays[view[0]].dtype.itemsize
        scratch = [
            pltpu.VMEM(self.view_shape(view), arrays[view[0]].dtype) for k, view in enumerate(views) if k not in home
        ]
        for members, _ in pairs:
            size = self.view_shape(views[members[0][1]])
            scratch.append(
                pltpu.VMEM((len(members) * size[0],) + size[1:], arrays[views[members[0][1]][0]].dtype)
            )
        scratch += [
            pltpu.VMEM(o.shape if at is None else o.shape[1:], o.dtype) for o, at in zip(outs, self.entries)
        ]
        aliases = {}
        for k, onto in enumerate(self.ontos):
            if onto is not None:
                aliases[len(self.scalars) + len(arrays) + len(aliases)] = k
        scratch += self.temps + [pltpu.SemaphoreType.DMA((8 * (len(views) + len(outs)),))]
        return pl.pallas_call(
            body,
            out_shape=tuple(outs),
            in_specs=[pl.BlockSpec(memory_space=pltpu.SMEM) for _ in self.scalars]
            + [pl.BlockSpec(memory_space=pl.ANY) for _ in arrays + under],
            out_specs=tuple(pl.BlockSpec(memory_space=pl.ANY) for _ in outs),
            scratch_shapes=scratch,
            input_output_aliases=aliases,
            compiler_params=pltpu.CompilerParams(vmem_limit_bytes=VMEM_LIMIT),
            cost_estimate=pl.CostEstimate(flops=self.flops, bytes_accessed=moved, transcendentals=0),
            name=self.name,
        )(*self.scalars, *arrays, *under)


class Masks:
    def __init__(self, spots, cols):
        self.main = (0, spots)
        self.ext = (spots, 2 * spots + 2 * cols)
        self.prev = (2 * spots + 2 * cols, 3 * spots + 2 * cols)
        self.next = (3 * spots + 2 * cols, 4 * spots + 2 * cols)
        self.slow = (4 * spots + 2 * cols, 4 * spots + 2 * cols + 8)
        self.fast = (4 * spots + 2 * cols + 8, 4 * spots + 2 * cols + 16)
        self.half = (4 * spots + 2 * cols + 16, 4 * spots + 2 * cols + 24)
        self.path = (4 * spots + 2 * cols + 24, 4 * spots + 2 * cols + 32)
        self.rows = 4 * spots + 2 * cols + 32


def make_masks(m, rows, cols, last, place, clips, mk):
    half = place[0] % 2
    path = place[1]
    side = clips[0, place[0] // 2]
    area = 0
    for k in range(clips.shape[1]):
        area = area + clips[0, k] * clips[0, k]
    shift = cols.bit_length() - 1

    def inside(first, count):
        at = lax.broadcasted_iota(jnp.int32, (count * cols, LANES), 0)
        line = half * rows + first + (at >> shift)
        spot = at & (cols - 1)
        good = (line >= 0) & (line < 2 * rows) & (line < side) & (spot < side)
        return jnp.where(good, 1.0, 0.0)

    main = inside(0, rows)
    mk[m.main[0] : m.main[1], :] = main
    mk[m.ext[0] : m.ext[1], :] = inside(-1, rows + 2)
    mk[m.prev[0] : m.prev[1], :] = main * jnp.where(path > 0, 1.0, 0.0)
    mk[m.next[0] : m.next[1], :] = main * jnp.where(path < last, 1.0, 0.0)

    def fill(span, value):
        mk[span[0] : span[1], :] = jnp.full((8, LANES), value, F32)

    fill(m.slow, TS * area.astype(F32))
    fill(m.fast, TF * area.astype(F32))
    fill(m.half, half.astype(F32))
    fill(m.path, path.astype(F32))


def own_row(m, spots, cols, col0, width, z, mk, row):
    for t in range(z.shape[0]):
        lower = mk[m.half[0] : m.half[0] + 1, :] > 0.5
        for lane in range(0, width, LANES):
            at = col0 + lane
            row[t, :, lane : lane + LANES] = jnp.where(
                lower, z[t, 0:cols, at : at + LANES], z[t, spots - cols : spots, at : at + LANES]
            )


def own_edge(m, lead, tail, z, mk, edge):
    frames = z.shape[0]
    second = mk[m.path[0] : m.path[0] + 1, :] > 0.5
    for lane in range(0, edge.shape[1], LANES):
        edge[:, lane : lane + LANES] = jnp.where(
            second,
            z[0, :, lead + lane : lead + lane + LANES],
            z[frames - 1, :, tail + lane : tail + lane + LANES],
        ).astype(edge.dtype)


def spread_sums(*refs):
    parts, out = refs[:-1], refs[-1]
    row = jnp.concatenate([part[...] for part in parts], axis=1)
    out[...] = jnp.broadcast_to(row[None], out.shape)


def make_w7(lat, group, wl, wf, w7):
    inner = wf.shape[1]
    w7[...] = jnp.zeros(w7.shape, BF16)
    for j in range(wl.shape[0]):
        w7[j * LANES : (j + 1) * LANES, 0:lat] = wl[j]
    at = lax.broadcasted_iota(jnp.int32, (inner, LANES), 0)
    lane = lax.broadcasted_iota(jnp.int32, (inner, LANES), 1)
    places = [jnp.where(lane == at + inner * k, 1.0, 0.0).astype(BF16) for k in range(group)]
    for f in range(1, group + 3):
        used = [k for k in range(group) if 0 <= f - 1 - k < 3]
        got = None
        for k in used:
            more = dot_tn(wf[f - 1 - k], places[k])
            got = more if got is None else got + more
        w7[f * LANES : (f + 1) * LANES, lat : lat + LANES] = got.astype(BF16)


def make_blocks(group, ws, wp, wfs, wfp):
    inner = wp.shape[0]
    at = lax.broadcasted_iota(jnp.int32, (inner, LANES), 0)
    lane = lax.broadcasted_iota(jnp.int32, (inner, LANES), 1)
    tile = jnp.where((lane & (inner - 1)) == at, 1.0, 0.0).astype(BF16)
    shift = inner.bit_length() - 1
    for tap in range(ws.shape[0]):
        got = dot(ws[tap], tile)
        for k in range(group):
            kept = jnp.where((lane >> shift) == k, got, 0.0).astype(BF16)
            row = (tap % 3) * LANES + k * inner
            wfs[tap // 3, row : row + inner, :] = kept
    wfp[...] = jnp.zeros(wfp.shape, BF16)
    for k in range(group):
        wfp[k * inner : (k + 1) * inner, k * LANES : (k + 1) * LANES] = wp[...]


def widen(rows, width):
    return jnp.concatenate([rows] * (width // LANES), axis=1)


def sublane_sums(value):
    return jnp.sum(value.reshape(value.shape[0] // 8, 8, value.shape[1]), axis=0)


def row_sum(value):
    return jnp.sum(value, axis=0, keepdims=True)


def fold_packed(row):
    full = jnp.broadcast_to(row, (8, LANES))
    full = full + pltpu.roll(full, 64, 1)
    full = full + pltpu.roll(full, 32, 1)
    return full[0:1]


def totals(st, lo, width, packed=False):
    first = jnp.sum(st[:, :, lo : lo + width], axis=0)
    second = jnp.sum(st[:, :, lo + width : lo + 2 * width], axis=0)
    if packed:
        return fold_packed(first), fold_packed(second)
    return first, second


def norm_rows(st, lo, width, count, packed=False):
    first, second = totals(st, lo, width, packed)
    mean = first / count
    return mean, lax.rsqrt(second / count - mean * mean + EPSILON)


def keep_norm(lo, width, span, st, mk, nz):
    mean, rstd = norm_rows(st, lo, width, widen(mk[span[0] : span[0] + 1, :], width))
    nz[0:1, :] = mean
    nz[1:2, :] = rstd


def keep_sums(lo, width, st, gb):
    one, two = totals(st, lo, width)
    gb[0:1, :] = one
    gb[1:2, :] = two


def clear(*refs):
    for ref in refs:
        ref[...] = jnp.zeros(ref.shape, F32)


def close_sums(one, two, s):
    s[...] = jnp.concatenate([row_sum(one[...]), row_sum(two[...])], axis=1)


def sigmoid(value):
    return 0.5 * jnp.tanh(0.5 * value) + 0.5


def silu(value):
    return value * sigmoid(value)


def silu_slope(value):
    sigma = sigmoid(value)
    return sigma * (1.0 + value * (1.0 - sigma))


def dot(a, b):
    return jnp.dot(a, b, preferred_element_type=F32)


def dot_nt(a, b):
    return lax.dot_general(a, b, (((1,), (1,)), ((), ())), preferred_element_type=F32)


def dot_tn(a, b):
    return lax.dot_general(a, b, (((0,), (0,)), ((), ())), preferred_element_type=F32)


def flat(value):
    return value.reshape(value.shape[0] * value.shape[1], value.shape[2])


def store_shifts(dst, t, value, cols):
    rows, width = value.shape
    spot = lax.broadcasted_iota(jnp.int32, (rows, width), 0) & (cols - 1)
    left = jnp.where(spot == 0, 0.0, pltpu.roll(value, 1, 0))
    right = jnp.where(spot == cols - 1, 0.0, pltpu.roll(value, rows - 1, 0))
    dst[t, :, 0:width] = left.astype(BF16)
    dst[t, :, width : 2 * width] = value.astype(BF16)
    dst[t, :, 2 * width : 3 * width] = right.astype(BF16)


def taps_of(frames_ref, frames, group):
    return jnp.concatenate(
        [
            jnp.concatenate([frames_ref[group * t + f] for f in range(7)], axis=1)
            for t in range(frames)
        ],
        axis=0,
    )


def entry_sums(y, lat, frames, spots):
    width = y.shape[1]
    one = jnp.zeros((8, width), F32)
    two = jnp.zeros((8, width), F32)
    for t in range(frames):
        part = y[t * spots : (t + 1) * spots]
        one = one + sublane_sums(part)
        two = two + sublane_sums(part * part)
    one = row_sum(one)
    two = row_sum(two)
    return jnp.concatenate([one[:, :lat], two[:, :lat], one[:, lat:], two[:, lat:]], axis=1)


def fast_entry(m, frames, group, x, before, after, mk, w7, fw, y, s):
    spots = x.shape[1]
    count = x.shape[0]

    def put(at, value, span):
        fw[at] = (value.astype(F32) * mk[span[0] : span[1], :]).astype(BF16)

    for k in range(2):
        put(k, before[k], m.prev)
        put(2 + count + k, after[k], m.next)
    for k in range(count):
        put(2 + k, x[k], m.main)
    out = dot(taps_of(fw, frames, group), w7[...])
    for t in range(frames):
        y[t] = out[t * spots : (t + 1) * spots]
    s[...] = entry_sums(out, w7.shape[1] - LANES, frames, spots)


def slow_partial(m, frames, x, before, after, mk, wt, xm, fpart):
    spots, wide = x.shape[1], x.shape[2]
    sources = [(before, m.prev)] + [(x.at[t], m.main) for t in range(frames)] + [(after, m.next)]
    for k, (src, span) in enumerate(sources):
        for lo in range(0, wide, 256):
            mask = widen(mk[span[0] : span[1], :], 256)
            xm[k, :, lo : lo + 256] = (src[:, lo : lo + 256].astype(F32) * mask).astype(BF16)
    out = dot(flat(xm[0:frames]), wt[0, :wide, :])
    for j in range(1, 3):
        out = out + dot(flat(xm[j : j + frames]), wt[j, :wide, :])
    for t in range(frames):
        fpart[t] = out[t * spots : (t + 1) * spots]


def lat_join(m, n, frames, lat, st, y, before, after, fpart, wt, gs, bs, mk, jl, first, s, nl, jw):
    spots = y.shape[1]
    wide = wt.shape[1] - lat
    count = widen(mk[m.slow[0] : m.slow[0] + 1, :], lat)
    mean, rstd = norm_rows(st, 0, lat, count)
    nl[0:1, :] = mean
    nl[1:2, :] = rstd
    scale = rstd * gs[n : n + 1, 0:lat]
    bias = bs[n : n + 1, 0:lat]
    sources = (
        [(before[:, 0:lat], m.prev)]
        + [(y[t, :, 0:lat], m.main) for t in range(frames)]
        + [(after[:, 0:lat], m.next)]
    )
    for k, (value, span) in enumerate(sources):
        mask = widen(mk[span[0] : span[1], :], lat)
        act = (silu((value - mean) * scale + bias) * mask).astype(BF16)
        jw[k] = act
        if 1 <= k <= frames:
            jl[k - 1] = act
    out = flat(fpart[...])
    for j in range(3):
        out = out + dot(flat(jw[j : j + frames]), wt[j, wide:, :])
    one = jnp.zeros((8, out.shape[1]), F32)
    two = jnp.zeros((8, out.shape[1]), F32)
    for t in range(frames):
        part = out[t * spots : (t + 1) * spots]
        first[t] = part
        one = one + sublane_sums(part)
        two = two + sublane_sums(part * part)
    s[...] = jnp.concatenate([row_sum(one), row_sum(two)], axis=1)


def space_forward(
    m, n, frames, cols, lo, at, width, col0, packed, span, st, z, row, w, g, b, mk, aw, out, s, nz, vw
):
    spots = z.shape[1]
    count = widen(mk[span[0] : span[0] + 1, :], width)
    mean, rstd = norm_rows(st, at, width, count, packed)
    nz[0:1, :] = mean
    nz[1:2, :] = rstd
    scale = rstd * g[n : n + 1, lo : lo + width]
    bias = b[n : n + 1, lo : lo + width]
    mask = widen(mk[m.ext[0] : m.ext[1], :], width)
    for t in range(frames):
        value = jnp.concatenate([row[t], z[t, :, col0 : col0 + width], row[t]], axis=0)
        act = silu((value - mean) * scale + bias) * mask
        aw[t] = act.astype(BF16)
        store_shifts(vw, t, act, cols)
    total = dot(flat(vw[:, 0:spots, :]), w[0])
    for i in range(1, 3):
        total = total + dot(flat(vw[:, i * cols : i * cols + spots, :]), w[i])
    mask = widen(mk[m.main[0] : m.main[1], :], width)
    one = jnp.zeros((8, width), F32)
    two = jnp.zeros((8, width), F32)
    for t in range(frames):
        part = total[t * spots : (t + 1) * spots]
        out[t] = part
        part = part * mask
        one = one + sublane_sums(part)
        two = two + sublane_sums(part * part)
    s[...] = jnp.concatenate([row_sum(one), row_sum(two)], axis=1)


def slow_acts(m, n, frames, lo, halo, st, z, *rest):
    if halo:
        before, after, g, b, mk, a2, nz, aw = rest
    else:
        g, b, mk, a2, nz, aw = rest
    width = z.shape[2]
    keep_norm(0, width, m.slow, st, mk, nz)
    mean = nz[0:1, :]
    scale = nz[1:2, :] * g[n : n + 1, lo : lo + width]
    bias = b[n : n + 1, lo : lo + width]
    sources = [(z[t], m.main, t + halo) for t in range(frames)]
    if halo:
        sources += [(before[...], m.prev, 0), (after[...], m.next, frames + 1)]
    for value, span, at in sources:
        mask = widen(mk[span[0] : span[1], :], width)
        act = (silu((value - mean) * scale + bias) * mask).astype(BF16)
        aw[at] = act
        if halo <= at < frames + halo:
            a2[at - halo] = act


def slow_third(frames, halo, at, aw, wp, third, s):
    spots = aw.shape[1]
    wide = s.shape[1] // 2
    out = dot(flat(aw[...]), wp[...])
    one = jnp.zeros((8, 256), F32)
    two = jnp.zeros((8, 256), F32)
    for t in range(frames + 2 * halo):
        part = out[t * spots : (t + 1) * spots]
        third[t] = part.astype(BF16)
        if halo <= t < frames + halo:
            one = one + sublane_sums(part)
            two = two + sublane_sums(part * part)
    s[:, at : at + 256] = row_sum(one)
    s[:, wide + at : wide + at + 256] = row_sum(two)


def fast_third(m, n, frames, lo, at, st, z, wp, g, b, mk, a2, ft, s, nz):
    spots = z.shape[1]
    count = mk[m.fast[0] : m.fast[0] + 1, :]
    mean, rstd = norm_rows(st, at, LANES, count, True)
    nz[0:1, :] = mean
    nz[1:2, :] = rstd
    scale = rstd * g[n : n + 1, lo : lo + LANES]
    bias = b[n : n + 1, lo : lo + LANES]
    mask = mk[m.main[0] : m.main[1], :]
    for t in range(frames):
        a2[t] = (silu((z[t] - mean) * scale + bias) * mask).astype(BF16)
    acts = flat(a2[...])
    one = jnp.zeros((8, LANES), F32)
    two = jnp.zeros((8, LANES), F32)
    out = dot(acts, wp[...])
    for t in range(frames):
        for lane in range(0, wp.shape[1], LANES):
            part = out[t * spots : (t + 1) * spots, lane : lane + LANES]
            ft[t, :, lane : lane + LANES] = part.astype(BF16)
            one = one + sublane_sums(part)
            two = two + sublane_sums(part * part)
    s[...] = jnp.concatenate([row_sum(one), row_sum(two)], axis=1)


def fast_next(m, n, frames, group, lo, at, st, ft, before, after, fw0, w7, g, b, mk, fw1, y, s, nz):
    spots = ft.shape[1]
    count = mk[m.fast[0] : m.fast[0] + 1, :]
    mean, rstd = norm_rows(st, at, LANES, count)
    nz[0:1, :] = mean
    nz[1:2, :] = rstd
    scale = rstd * g[n : n + 1, lo : lo + LANES]
    bias = b[n : n + 1, lo : lo + LANES]
    total = frames * group

    def out_of(k, value, span):
        z = fw0[k].astype(F32) + ((value - mean) * scale + bias)
        return silu(z) * mk[span[0] : span[1], :]

    for k in range(2):
        lane = k * LANES
        fw1[k] = out_of(k, before[:, lane : lane + LANES], m.prev).astype(BF16)
        fw1[2 + total + k] = out_of(2 + total + k, after[:, lane : lane + LANES], m.next).astype(BF16)
    for t in range(frames):
        for f in range(group):
            k = t * group + f
            fw1[2 + k] = out_of(2 + k, ft[t, :, f * LANES : (f + 1) * LANES], m.main).astype(BF16)
    out = dot(taps_of(fw1, frames, group), w7[...])
    for t in range(frames):
        y[t] = out[t * spots : (t + 1) * spots]
    s[...] = entry_sums(out, w7.shape[1] - LANES, frames, spots)


def fast_last(m, n, frames, group, lo, at, st, ft, f1, cot, g, b, mk, out, pre, s, nz):
    count = mk[m.fast[0] : m.fast[0] + 1, :]
    mean, rstd = norm_rows(st, at, LANES, count)
    nz[0:1, :] = mean
    nz[1:2, :] = rstd
    gain = g[n : n + 1, lo : lo + LANES]
    bias = b[n : n + 1, lo : lo + LANES]
    mask = mk[m.main[0] : m.main[1], :]
    one = jnp.zeros((8, LANES), F32)
    two = jnp.zeros((8, LANES), F32)
    for t in range(frames):
        for f in range(group):
            k = t * group + f
            hat = (ft[t, :, f * LANES : (f + 1) * LANES].astype(F32) - mean) * rstd
            z = f1[k].astype(F32) + hat * gain + bias
            sigma = sigmoid(z)
            out[k] = z * sigma * mask
            grad = cot[k].astype(F32) * mask * (sigma * (1.0 + z * (1.0 - sigma)))
            pre[k] = grad.astype(BF16)
            one = one + sublane_sums(grad)
            two = two + sublane_sums(grad * hat)
    s[...] = jnp.concatenate([row_sum(one), row_sum(two)], axis=1)


def chunked(total, step, body, init):
    def turn(i, carry):
        return body(pl.multiple_of(i * step, step), carry)

    return lax.fori_loop(0, total // step, turn, init)


def slow_next(n, lo, span, third, xm, nz, g, b, mk, sw):
    spots, wide = third.shape
    mean = nz[0:1, :]
    scale = nz[1:2, :] * g[n : n + 1, lo : lo + wide]
    bias = b[n : n + 1, lo : lo + wide]

    def turn(at, carry):
        mask = widen(mk[pl.ds(span[0] + at, 16), :], 512)
        for c in range(0, wide, 512):
            z = third[pl.ds(at, 16), c : c + 512].astype(F32)
            z = (z - mean[:, c : c + 512]) * scale[:, c : c + 512] + bias[:, c : c + 512]
            z = xm[pl.ds(at, 16), c : c + 512].astype(F32) + z
            sw[pl.ds(at, 16), c : c + 512] = (silu(z) * mask).astype(BF16)
        return carry

    chunked(spots, 16, turn, 0)


def time_partial(frames, sw, wt, fpart):
    spots = sw.shape[1]
    out = dot(flat(sw[0:frames]), wt[0])
    for j in range(1, 3):
        out = out + dot(flat(sw[j : j + frames]), wt[j])
    for t in range(frames):
        fpart[t] = out[t * spots : (t + 1) * spots]


def slow_last(m, n, lo, third, slow, cot, nz, g, b, mk, out, pre, one, two):
    spots, wide = third.shape
    mean, rstd = nz[0:1, :], nz[1:2, :]
    gain = g[n : n + 1, lo : lo + wide]
    bias = b[n : n + 1, lo : lo + wide]

    def turn(at, sums):
        ones, twos = [], []
        mask = widen(mk[pl.ds(m.main[0] + at, 16), :], 512)
        for c in range(0, wide, 512):
            hat = third[pl.ds(at, 16), c : c + 512].astype(F32)
            hat = (hat - mean[:, c : c + 512]) * rstd[:, c : c + 512]
            z = slow[pl.ds(at, 16), c : c + 512].astype(F32) + hat * gain[:, c : c + 512] + bias[:, c : c + 512]
            sigma = sigmoid(z)
            out[pl.ds(at, 16), c : c + 512] = z * sigma * mask
            grad = cot[pl.ds(at, 16), c : c + 512].astype(F32) * mask
            grad = grad * (sigma * (1.0 + z * (1.0 - sigma)))
            pre[pl.ds(at, 16), c : c + 512] = grad.astype(BF16)
            ones.append(sublane_sums(grad))
            twos.append(sublane_sums(grad * hat))
        return sums[0] + jnp.concatenate(ones, axis=1), sums[1] + jnp.concatenate(twos, axis=1)

    one[...], two[...] = chunked(spots, 16, turn, (one[...], two[...]))


def slow_third_grad(m, n, lo, pre, third, n3, gb, g, mk, d3):
    spots, wide = pre.shape
    count = widen(mk[m.slow[0] : m.slow[0] + 1, :], wide)
    mean, rstd = n3[0:1, :], n3[1:2, :]
    scale = g[n : n + 1, lo : lo + wide] * rstd
    one = gb[0:1, :] / count
    two = gb[1:2, :] / count * rstd

    def turn(i, carry):
        mask = widen(mk[pl.ds(m.main[0] + i, 16), :], 512)
        for c in range(0, wide, 512):
            hat = (third[pl.ds(i, 16), c : c + 512].astype(F32) - mean[:, c : c + 512]) * two[:, c : c + 512]
            grad = pre[pl.ds(i, 16), c : c + 512].astype(F32) - mask * (one[:, c : c + 512] + hat)
            d3[pl.ds(i, 16), c : c + 512] = (scale[:, c : c + 512] * grad).astype(BF16)
        return carry

    chunked(spots, 16, turn, 0)


def slow_third_back(m, n, frames, lo, d3, z, n2, wp, g, b, mk, e2, s):
    spots, width = z.shape[1], z.shape[2]
    out = dot_nt(flat(d3[...]), wp[...])
    gain = g[n : n + 1, lo : lo + width]
    bias = b[n : n + 1, lo : lo + width]
    back_act(m, frames, spots, out, z, 0, n2[0:1, :], n2[1:2, :], gain, bias, mk, e2, s)


def back_act(m, frames, spots, out, z, col0, mean, rstd, gain, bias, mk, e, s):
    width = out.shape[1]
    mask = widen(mk[m.main[0] : m.main[1], :], width)
    one = jnp.zeros((8, width), F32)
    two = jnp.zeros((8, width), F32)
    for t in range(frames):
        hat = (z[t, :, col0 : col0 + width] - mean) * rstd
        grad = out[t * spots : (t + 1) * spots] * mask * silu_slope(hat * gain + bias)
        e[t] = grad
        one = one + sublane_sums(grad)
        two = two + sublane_sums(grad * hat)
    s[...] = jnp.concatenate([row_sum(one), row_sum(two)], axis=1)


def fast_third_back(m, n, frames, group, lo3, lo2, at, st, pre, ft, n3, z, n2, wp, g, b, mk, d3, e2, s, gb):
    spots = z.shape[1]
    count = mk[m.fast[0] : m.fast[0] + 1, :]
    one, two = totals(st, at, LANES)
    gb[0:1, :] = one
    gb[1:2, :] = two
    mean, rstd = n3[0:1, :], n3[1:2, :]
    scale = g[n : n + 1, lo3 : lo3 + LANES] * rstd
    one = one / count
    two = two / count * rstd
    mask = mk[m.main[0] : m.main[1], :]
    for t in range(frames):
        for f in range(group):
            hat = (ft[t, :, f * LANES : (f + 1) * LANES] - mean) * two
            grad = pre[t * group + f] - mask * (one + hat)
            d3[t, :, f * LANES : (f + 1) * LANES] = (scale * grad).astype(BF16)
    out = dot_nt(flat(d3[...]), wp[...])
    mean, rstd = n2[0:1, :], n2[1:2, :]
    gain = g[n : n + 1, lo2 : lo2 + LANES]
    bias = b[n : n + 1, lo2 : lo2 + LANES]
    back_act(m, frames, spots, out, z, 0, mean, rstd, gain, bias, mk, e2, s)


def space_back(
    m, n, frames, cols, lo2, lo1, at, width, col0, packed, span,
    st, e, erow, z, zrow, nz, z1, n1, w, g, b, mk, d2, e1, s, gb, vw,
):
    spots = z.shape[1]
    count = widen(mk[span[0] : span[0] + 1, :], width)
    one, two = totals(st, at, width, packed)
    gb[0:1, :] = one
    gb[1:2, :] = two
    mean, rstd = nz[0:1, :], nz[1:2, :]
    scale = g[n : n + 1, lo2 : lo2 + width] * rstd
    one = one / count
    two = two / count * rstd
    mask = widen(mk[m.ext[0] : m.ext[1], :], width)
    for t in range(frames):
        grad = jnp.concatenate([erow[t], e[t], erow[t]], axis=0)
        value = jnp.concatenate([zrow[t], z[t], zrow[t]], axis=0)
        grad = scale * mask * (grad - (one + (value - mean) * two))
        d2[t] = grad[cols : cols + spots].astype(BF16)
        store_shifts(vw, t, grad.astype(BF16).astype(F32), cols)
    total = None
    for i in range(3):
        rows = (2 - i) * cols
        for j in range(3):
            lane = (2 - j) * width
            part = dot_nt(flat(vw[:, rows : rows + spots, lane : lane + width]), w[i, j * width : (j + 1) * width, :])
            total = part if total is None else total + part
    mean, rstd = n1[0:1, :], n1[1:2, :]
    gain = g[n : n + 1, lo1 : lo1 + width]
    bias = b[n : n + 1, lo1 : lo1 + width]
    back_act(m, frames, spots, total, z1, col0, mean, rstd, gain, bias, mk, e1, s)


def first_taps(frames, dw):
    return [flat(dw[2 - j : 2 - j + frames]) for j in range(3)]


def time_back(taps, wt, lo, size):
    out = dot_nt(taps[0], wt[0, lo : lo + size, :])
    for j in range(1, 3):
        out = out + dot_nt(taps[j], wt[j, lo : lo + size, :])
    return out


def slow_first_back(m, n, frames, lo1, at, st, e, ep, en, z, zp, zn, n1, wt, y, nl, g, b, mk, dw, el, s, gb):
    spots, width = z.shape[1], z.shape[2]
    lat = nl.shape[1]
    wide = wt.shape[1] - lat
    count = widen(mk[m.slow[0] : m.slow[0] + 1, :], width)
    one, two = totals(st, at, width)
    gb[0:1, :] = one
    gb[1:2, :] = two
    mean, rstd = n1[0:1, :], n1[1:2, :]
    scale = g[n : n + 1, lo1 : lo1 + width] * rstd
    one = one / count
    two = two / count * rstd
    sources = (
        [(ep, zp, m.prev)] + [(e.at[t], z.at[t], m.main) for t in range(frames)] + [(en, zn, m.next)]
    )
    for k, (grad, value, span) in enumerate(sources):
        mask = widen(mk[span[0] : span[1], :], width)
        dw[k] = (scale * mask * (grad[...] - (one + (value[...] - mean) * two))).astype(BF16)
    out = time_back(first_taps(frames, dw), wt, wide, lat)
    back_act(
        m, frames, spots, out, y, 0, nl[0:1, :], nl[1:2, :], g[n : n + 1, 0:lat], b[n : n + 1, 0:lat], mk, el, s
    )


def slow_input_last(m, frames, dw, wt, pre, mk, gx):
    spots, wide = pre.shape[1], pre.shape[2]
    taps = first_taps(frames, dw)
    mask = widen(mk[m.main[0] : m.main[1], :], 256)
    for c in range(0, wide, 256):
        out = time_back(taps, wt, c, 256)
        for t in range(frames):
            gx[t, :, c : c + 256] = (out[t * spots : (t + 1) * spots] + pre[t, :, c : c + 256]) * mask


def slow_input_back(m, n, frames, lo, at, dw, wt, pre, xm, third, n3, g, b, mk, pre0, s):
    spots = pre.shape[1]
    wide = s.shape[1] // 2
    mask = widen(mk[m.main[0] : m.main[1], :], 256)
    out = time_back(first_taps(frames, dw), wt, 0, 256)
    mean, rstd = n3[0:1, at : at + 256], n3[1:2, at : at + 256]
    gain = g[n - 1 : n, lo + at : lo + at + 256]
    bias = b[n - 1 : n, lo + at : lo + at + 256]
    one = jnp.zeros((8, 256), F32)
    two = jnp.zeros((8, 256), F32)
    for t in range(frames):
        grad = (out[t * spots : (t + 1) * spots] + pre[t].astype(F32)) * mask
        hat = (third[t].astype(F32) - mean) * rstd
        z0 = xm[t].astype(F32) + hat * gain + bias
        grad = grad * silu_slope(z0)
        pre0[t] = grad.astype(BF16)
        one = one + sublane_sums(grad)
        two = two + sublane_sums(grad * hat)
    s[:, at : at + 256] = row_sum(one)
    s[:, wide + at : wide + at + 256] = row_sum(two)


def fast_first_back(
    m, n, frames, lo1, at1, atl, st1, stl, el, eln, ef, efp, efn, y, yp, yn, nl, n1, gs, g, mk,
    dl, dfw, dln, dfp, dfn, gbl, gb1,
):
    lat = nl.shape[1]
    count = widen(mk[m.slow[0] : m.slow[0] + 1, :], lat)
    one, two = totals(stl, atl, lat)
    gbl[0:1, :] = one
    gbl[1:2, :] = two
    mean, rstd = nl[0:1, :], nl[1:2, :]
    scale = gs[n : n + 1, 0:lat] * rstd
    one = one / count
    two = two / count * rstd

    def lat_grad(grad, value, span):
        mask = widen(mk[span[0] : span[1], :], lat)
        return (scale * mask * (grad - (one + (value - mean) * two))).astype(BF16)

    for t in range(frames):
        dl[t] = lat_grad(el[t], y[t, :, 0:lat], m.main)
    dln[...] = lat_grad(eln[...], yn[:, 0:lat], m.next)
    fcount = mk[m.fast[0] : m.fast[0] + 1, :]
    fone, ftwo = totals(st1, at1, LANES, True)
    gb1[0:1, :] = fone
    gb1[1:2, :] = ftwo
    fmean, frstd = n1[0:1, :], n1[1:2, :]
    fscale = g[n : n + 1, lo1 : lo1 + LANES] * frstd
    fone = fone / fcount
    ftwo = ftwo / fcount * frstd

    def first_grad(grad, value, span):
        mask = mk[span[0] : span[1], :]
        return (fscale * mask * (grad - (fone + (value - fmean) * ftwo))).astype(BF16)

    for t in range(frames):
        dfw[t] = first_grad(ef[t], y[t, :, lat:], m.main)
    dfp[...] = first_grad(efp[...], yp[:, lat:], m.prev)
    dfn[...] = first_grad(efn[...], yn[:, lat:], m.next)


def fast_input_back(m, n, frames, group, lo3, last, dl, dfw, dln, dfp, dfn, w7, pre, *rest):
    if last:
        mk, gx, buf = rest
    else:
        fw0, ft, n3, g, b, mk, pre0, s, buf = rest
    spots, lat = dl.shape[1], dl.shape[2]
    both = jnp.concatenate([flat(dl[...]), flat(dfw[...])], axis=1)
    buf[...] = jnp.zeros(buf.shape, F32)
    out = dot_nt(both, w7[...])
    for t in range(frames):
        for f in range(7):
            k = group * t + f
            buf[k] = buf[k] + out[t * spots : (t + 1) * spots, f * LANES : (f + 1) * LANES]
    buf[2] = buf[2] + dot_nt(dfp[...], w7[6 * LANES : 7 * LANES, lat:])
    after = dot_nt(jnp.concatenate([dln[...], dfn[...]], axis=1), w7[0 : 2 * LANES, :])
    total = frames * group
    for f in range(2):
        buf[total + f] = buf[total + f] + after[:, f * LANES : (f + 1) * LANES]
    mask = mk[m.main[0] : m.main[1], :]
    if last:
        for k in range(total):
            gx[k] = (pre[k] + buf[2 + k]) * mask
        return
    mean, rstd = n3[0:1, :], n3[1:2, :]
    gain = g[n - 1 : n, lo3 : lo3 + LANES]
    bias = b[n - 1 : n, lo3 : lo3 + LANES]
    one = jnp.zeros((8, LANES), F32)
    two = jnp.zeros((8, LANES), F32)
    for k in range(total):
        t, f = k // group, k % group
        hat = (ft[t, :, f * LANES : (f + 1) * LANES] - mean) * rstd
        z0 = fw0[2 + k].astype(F32) + hat * gain + bias
        grad = (pre[k] + buf[2 + k]) * mask * silu_slope(z0)
        pre0[k] = grad.astype(BF16)
        one = one + sublane_sums(grad)
        two = two + sublane_sums(grad * hat)
    s[...] = jnp.concatenate([row_sum(one), row_sum(two)], axis=1)


def point_weights(a2, d3, out):
    acts = flat(a2[...])
    for k in range(out.shape[0]):
        out[k] = dot_tn(acts, flat(d3[:, :, k * 256 : (k + 1) * 256])).astype(BF16)


def space_weights(cols, aw, d2, out, vw):
    frames, spots, width = d2.shape
    for t in range(frames):
        store_shifts(vw, t, aw[t].astype(F32), cols)
    grads = flat(d2[...])
    for i in range(3):
        out[i] = dot_tn(flat(vw[:, i * cols : i * cols + spots, :]), grads).astype(BF16)


def time_weights(skip, slow, jl, dw, out):
    frames, spots, width = jl.shape
    wide = slow.shape[2]
    grads = jnp.concatenate([flat(dw[2 - j : 2 - j + frames]) for j in range(3)], axis=1)
    for c in range(0, wide + jl.shape[2], 256):
        if c < wide:
            acts = flat(slow[skip : skip + frames, :, c : c + 256])
        else:
            acts = flat(jl[:, :, c - wide : c - wide + 256])
        got = dot_tn(acts, grads)
        for j in range(3):
            out[j, c : c + 256, :] = got[:, j * width : (j + 1) * width].astype(BF16)


def group_blocks(value, group):
    size = LANES // group
    rows = lax.broadcasted_iota(jnp.int32, (LANES, LANES), 0) >> (size.bit_length() - 1)
    lanes = lax.broadcasted_iota(jnp.int32, (LANES, LANES), 1) >> (size.bit_length() - 1)
    kept = jnp.where(rows == lanes, value, 0.0)
    kept = kept + pltpu.roll(kept, 64, 1)
    kept = kept + pltpu.roll(kept, 32, 1)
    total = kept[0:size]
    for k in range(1, group):
        total = total + kept[k * size : (k + 1) * size]
    return total


def at_lanes(blocks):
    lanes = lax.broadcasted_iota(jnp.int32, blocks[0].shape, 1) >> 5
    out = jnp.zeros(blocks[0].shape, F32)
    for k, block in enumerate(blocks):
        out = jnp.where(lanes == k, block, out)
    return out


def fast_weights(group, cols, lat, fw, dl, df, fa1, d2, fa2, d3, out, vw):
    frames, spots, _ = dl.shape
    size = LANES // group
    both = jnp.concatenate([flat(dl[...]), flat(df[...])], axis=1)
    taps = [[None] * group for _ in range(3)]
    for f in range(7):
        acts = jnp.concatenate([fw[group * t + f] for t in range(frames)], axis=0)
        got = dot_tn(acts, both)
        if f < 5:
            out[f * LANES : (f + 1) * LANES, :] = got[:, :lat].astype(BF16)
        for k in range(group):
            if 0 <= f - k - 1 < 3:
                taps[f - k - 1][k] = got[:, lat:]
    lanes = lax.broadcasted_iota(jnp.int32, (LANES, LANES), 1) >> (size.bit_length() - 1)
    tap_sums = []
    for j in range(3):
        kept = jnp.zeros((LANES, LANES), F32)
        for k in range(group):
            kept = jnp.where(lanes == k, taps[j][k], kept)
        kept = kept + pltpu.roll(kept, 64, 1)
        tap_sums.append(kept + pltpu.roll(kept, 32, 1))
    low = 5 * LANES
    out[low : low + LANES, 0:LANES] = at_lanes(tap_sums).T.astype(BF16)
    for t in range(frames):
        store_shifts(vw, t, fa1[t].astype(F32), cols)
    grads = flat(d2[...])
    for i in range(3):
        got = dot_tn(flat(vw[:, i * cols : i * cols + spots, :]), grads)
        blocks = [group_blocks(got[j * LANES : (j + 1) * LANES], group) for j in range(3)]
        out[low + size * i : low + size * (i + 1), LANES : 2 * LANES] = at_lanes(blocks).astype(BF16)
    acts = flat(fa2[...])
    total = jnp.zeros((size, LANES), F32)
    for k in range(group):
        got = dot_tn(acts, flat(d3[:, :, k * LANES : (k + 1) * LANES]))
        total = total + got[k * size : (k + 1) * size]
    out[low + 3 * size : low + 4 * size, LANES : 2 * LANES] = total.astype(BF16)


def unpack_fast(n, inner, load, outs):
    glat, gft, gfs, gfp = outs
    low = glat.shape[1]
    for at in range(0, low, inner):
        glat[n, at : at + inner, :] = load(at, inner)
    for i in range(4):
        got = load(low + inner * i, inner)
        if i < 3:
            gft[n, i] = got[:, 0:LANES]
            for j in range(3):
                moved = got[:, LANES:] if j == 0 else pltpu.roll(got[:, LANES:], LANES - inner * j, 1)
                gfs[n, 3 * i + j] = moved[:, 0:inner]
        else:
            gfp[n] = got[:, LANES:]


def runs_of(at, count, base, half, one, two):
    found = []
    while count:
        core, row = at // half, base + at % half
        ref, size = one, one.shape[1]
        if row >= 4 * size:
            ref, row = two, row - 4 * size
            size = two.shape[1]
        block, row = core * 4 + row // size, row % size
        here = min(count, size - row, half - at % half)
        found.append((ref, block, row, here))
        at, count = at + here, count - here
    return found


def rows_of(base, half, one, two=None):
    def load(at, count):
        parts = [
            ref[block, row : row + here, :].astype(F32)
            for ref, block, row, here in runs_of(at, count, base, half, one, two)
        ]
        return parts[0] if len(parts) == 1 else jnp.concatenate(parts, axis=0)

    return load


def copy_rows(start, one, out):
    for at in range(0, out.shape[0], 256):
        out[at : at + 256, :] = one[start + at : start + at + 256, :].astype(F32)


def copy_columns(start, one, out):
    for at in range(0, out.shape[1], 256):
        out[:, at : at + 256] = one[start + at : start + at + 256, :].astype(F32)


def place_rows(start, base, half, one, two, out):
    at = 0
    for ref, block, row, here in runs_of(start, out.shape[0], base, half, one, two):
        out[at : at + here, :] = ref[block, row : row + here, :].astype(F32)
        at += here


def place_columns(start, base, half, one, two, out):
    for lane in range(0, out.shape[1], 256):
        at = 0
        for ref, block, row, here in runs_of(start + lane, 256, base, half, one, two):
            out[at : at + here, lane : lane + 256] = ref[block, row : row + here, :].astype(F32)
            at += here


def place_fast(inner, half_mid, half_late, start, mid_one, mid_two, one, two, *outs):
    unpack_fast(1, inner, rows_of(0, half_mid, mid_one, mid_two), outs)
    load = rows_of(0, half_late, one, two)
    unpack_fast(0, inner, lambda at, count: load(start + at, count), outs)


def assemble_norms(inner, *refs):
    sums, (gs, bs, gf, bf) = refs[:-4], refs[-4:]
    lanes = lax.broadcasted_iota(jnp.int32, (8, LANES), 1) >> (inner.bit_length() - 1)
    for n in range(2):
        slow, fast = sums[7 * n : 7 * n + 4], sums[7 * n + 4 : 7 * n + 7]
        for row, gslow, gfast in ((1, gs, gf), (0, bs, bf)):
            at = 0
            for part in slow:
                gslow[n : n + 1, at : at + part.shape[1]] = part[row : row + 1, :]
                at += part.shape[1]
            one, two, three = [jnp.broadcast_to(part[row : row + 1, :], (8, LANES)) for part in fast]
            three = pltpu.roll(three, 2 * inner, 1)
            head = jnp.where(lanes == 0, one, jnp.where(lanes == 1, two, three))
            gfast[n : n + 1, 0:LANES] = head[0:1]
            gfast[n : n + 1, LANES : LANES + 2 * inner] = three[0:1, 0 : 2 * inner]


def on_device(
    x_slow,
    x_fast,
    w_lateral,
    w_slow_time,
    w_slow_space,
    w_slow_point,
    w_fast_time,
    w_fast_space,
    w_fast_point,
    gain_slow,
    bias_slow,
    gain_fast,
    bias_fast,
    clip_size,
    cot_slow,
    cot_fast,
):
    frames, fast_frames = x_slow.shape[0], x_fast.shape[0]
    group = fast_frames // frames
    rows, cols = x_slow.shape[3], x_slow.shape[4]
    spots = rows * cols
    wide, fwide = x_slow.shape[5], x_fast.shape[5]
    lat = w_lateral.shape[3]
    width = w_slow_space.shape[3]
    inner = w_fast_space.shape[3]
    packs = group * fwide
    both = lat + LANES
    m = Masks(spots, cols)
    devices = lax.axis_size("path") * lax.axis_size("rows")
    path = lax.axis_index("path")
    ext = spots + 2 * cols
    lo1, lo2, lo3 = lat, lat + width, lat + 2 * width
    every = slice(None)

    def part(fn, *static):
        return functools.partial(fn, *static)

    xs = x_slow.reshape(frames, spots, wide)
    xf = x_fast.reshape(fast_frames, spots, fwide)
    cs = cot_slow.reshape(frames, spots, wide)
    cf = cot_fast.reshape(fast_frames, spots, fwide)
    wft = jnp.swapaxes(w_fast_time, 2, 3)
    wfs_raw = w_fast_space.reshape(2, 9, inner, inner)
    wsp = w_slow_space.reshape(2, 3, 3 * width, width)

    def packed(value):
        return jnp.concatenate(
            [value[:, 0:inner]] * group + [value[:, inner : 2 * inner]] * group + [value[:, 2 * inner :]],
            axis=1,
        )

    xf_edge = swap_path(jnp.where(path > 0, xf[:2], xf[-2:]))
    xs_edge = swap_path(jnp.where(path > 0, xs[0], xs[-1]))

    def payload(k, *sums):
        size = sum(k.temps[s[1]].shape[1] for s in sums)
        out = k.give((devices, 1, size))
        k.step(spread_sums, *sums, out)
        return out

    def row_out(k, z, mk, col0, size):
        out = k.give((frames, cols, size))
        k.step(part(own_row, m, spots, cols, col0, size), z, mk, out)
        return out

    def edge_out(k, z, mk, size, tail=0):
        out = k.give((spots, size), BF16)
        k.step(part(own_edge, m, 0, tail), z, mk, out)
        return out

    def finish(k, **handles):
        got = k.run()
        return {name: got[handle[1]] for name, handle in handles.items()}

    def other_row(value):
        return swap(value, "rows", 1)

    first_flops = 2 * frames * spots * 7 * fwide * both
    k = Stage("entry")
    mk_out = k.give((m.rows, LANES))
    place = jnp.stack([lax.axis_index("rows"), path]).astype(jnp.int32)
    k.step(
        part(make_masks, m, rows, cols, lax.axis_size("path") - 1), k.scalar(place), k.scalar(clip_size), mk_out
    )
    w7_out = k.give((7 * fwide, both), BF16)
    k.step(part(make_w7, lat, group), k.take(w_lateral, 0), k.take(wft, 0), w7_out)
    fw = k.give((fast_frames + 4, spots, fwide), BF16)
    y = k.give((frames, spots, both))
    sy = k.temp((1, 2 * both))
    edge = k.take(xf_edge)
    k.step(
        part(fast_entry, m, frames, group), k.take(xf), edge, edge, mk_out, w7_out, fw, y, sy, flops=first_flops
    )
    pay = payload(k, sy)
    got = finish(
        k, mk=mk_out, w7=w7_out, fw=fw, y=y, pay=pay, ff_row=row_out(k, y, mk_out, lat, LANES),
        edge=edge_out(k, y, mk_out, both),
    )
    mk = got["mk"]
    saved = [{"fw": got["fw"], "y": got["y"], "w7": got["w7"]}, {}]
    st = gather_sums(got["pay"])
    saved[0]["ff_row"] = other_row(got["ff_row"])
    saved[0]["y_edge"] = swap_path(got["edge"])
    mk, wft, gain_fast, bias_fast = lax.optimization_barrier((mk, wft, gain_fast, bias_fast))
    gf, bf = packed(gain_fast), packed(bias_fast)
    k = Stage("prepare")
    w7_out = k.give((7 * fwide, both), BF16)
    k.step(part(make_w7, lat, group), k.take(w_lateral, 1), k.take(wft, 1), w7_out)
    blocks = []
    for n in range(2):
        blocks += [k.give((3, 3 * LANES, LANES), BF16), k.give((LANES, packs), BF16)]
        k.step(part(make_blocks, group), k.take(wfs_raw, n), k.take(w_fast_point, n), *blocks[-2:])
    got = finish(k, w7=w7_out, wfs0=blocks[0], wfp0=blocks[1], wfs1=blocks[2], wfp1=blocks[3])
    saved[1]["w7"] = got["w7"]
    wfs, wfp = [got["wfs0"], got["wfs1"]], [got["wfp0"], got["wfp1"]]
    k = Stage("slow_partial")
    xm = k.give((frames + 2, spots, wide), BF16)
    fpart = k.give((frames, spots, width))
    edge = k.take(xs_edge)
    k.step(
        part(slow_partial, m, frames),
        k.take(xs), edge, edge, k.take(mk), k.take(w_slow_time, 0, every, slice(0, wide)), xm, fpart,
        flops=2 * frames * spots * 3 * wide * width,
    )
    got = finish(k, sw=xm, fpart=fpart)
    saved[0]["sw"] = got["sw"]
    fpart_in = got["fpart"]

    for n in range(2):
        v = saved[n]
        k = Stage("join")
        mk_in, gs, bs = k.take(mk), k.take(gain_slow), k.take(bias_slow)
        st_in = k.take(st)
        names = {}
        if n == 0:
            fpart = k.take(fpart_in)
        else:
            fpart = k.temp((frames, spots, width))
            n3, next_sw = k.give((2, wide)), k.give((frames + 2, spots, wide), BF16)
            names.update(sw=next_sw, n3=n3)
            k.step(part(keep_norm, 2 * both, wide, m.slow), st_in, mk_in, n3)
            spans = [m.prev] + [m.main] * frames + [m.next]
            for f in range(frames + 2):
                k.step(
                    part(slow_next, 0, lo3, spans[f]),
                    k.take(saved[0]["third"], f), k.take(saved[0]["sw"], f), k.peek(n3), gs, bs, mk_in,
                    k.piece(next_sw, f),
                )
            k.step(
                part(time_partial, frames),
                k.peek(next_sw), k.take(w_slow_time, 1, every, slice(0, wide)), fpart,
                flops=2 * frames * spots * 3 * wide * width,
            )
        y_in, edge = k.take(v["y"]), k.take(v["y_edge"])
        jl = k.give((frames, spots, lat), BF16)
        first = k.give((frames, spots, width))
        nl = k.give((2, lat))
        s_first, s_fs = k.temp((1, 2 * width)), k.temp((1, 2 * LANES))
        k.step(
            part(lat_join, m, n, frames, lat),
            st_in, y_in, edge, edge, fpart, k.take(w_slow_time, n, every, slice(wide, wide + lat)), gs, bs, mk_in,
            jl, first, s_first, nl, k.temp((frames + 2, spots, lat), BF16),
            flops=2 * frames * spots * 3 * lat * width,
        )
        fa1 = k.give((frames, ext, LANES), BF16)
        fs = k.give((frames, spots, LANES))
        nf1 = k.give((2, LANES))
        k.step(
            part(space_forward, m, n, frames, cols, 0, 2 * lat, LANES, lat, True, m.fast),
            st_in, y_in, k.take(v["ff_row"]), k.take(wfs[n]), k.take(gf), k.take(bf), mk_in,
            fa1, fs, s_fs, nf1, k.temp((frames, ext, 3 * LANES), BF16),
            flops=2 * frames * spots * 9 * LANES * LANES,
        )
        pay = payload(k, s_first, s_fs)
        got = finish(
            k, jl=jl, first=first, nl=nl, fa1=fa1, fs=fs, nf1=nf1, pay=pay,
            first_row=row_out(k, first, mk_in, 0, width), fs_row=row_out(k, fs, mk_in, 0, LANES),
            first_edge=edge_out(k, first, mk_in, width), **names,
        )
        st = gather_sums(got["pay"])
        for name in ("jl", "first", "nl", "fa1", "fs", "nf1"):
            v[name] = got[name]
        if n == 1:
            saved[1]["sw"], saved[0]["n3"] = got["sw"], got["n3"]
        first_row = other_row(got["first_row"])
        st, v["fs_row"], v["first_edge"] = lax.optimization_barrier(
            (st, other_row(got["fs_row"]), swap_path(got["first_edge"]))
        )
        k = Stage("space")
        mk_in, st_in = k.take(mk), k.take(st)
        a1 = k.give((frames, ext, width), BF16)
        second = k.give((frames, spots, width))
        n1 = k.give((2, width))
        s_second, s_ft = k.temp((1, 2 * width)), k.temp((1, 2 * LANES))
        k.step(
            part(space_forward, m, n, frames, cols, lo1, 0, width, 0, False, m.slow),
            st_in, k.take(v["first"]), k.take(first_row), k.take(wsp, n), k.take(gain_slow), k.take(bias_slow), mk_in,
            a1, second, s_second, n1, k.temp((frames, ext, 3 * width), BF16),
            flops=2 * frames * spots * 9 * width * width,
        )
        fa2 = k.give((frames, spots, LANES), BF16)
        ft = k.give((frames, spots, packs), BF16)
        nf2 = k.give((2, LANES))
        k.step(
            part(fast_third, m, n, frames, LANES, 2 * width),
            st_in, k.take(v["fs"]), k.take(wfp[n]), k.take(gf), k.take(bf), mk_in, fa2, ft, s_ft, nf2,
            flops=2 * frames * spots * LANES * packs,
        )
        pay = payload(k, s_second, s_ft)
        names = {"second_row": row_out(k, second, mk_in, 0, width)}
        if n == 0:
            names["second_edge"] = edge_out(k, second, mk_in, width)
            names["ft_edge"] = edge_out(k, ft, mk_in, 2 * fwide, (group - 2) * fwide)
        got = finish(k, a1=a1, second=second, n1=n1, fa2=fa2, ft=ft, nf2=nf2, pay=pay, **names)
        st = gather_sums(got["pay"])
        for name in ("a1", "second", "n1", "fa2", "ft", "nf2"):
            v[name] = got[name]
        st, v["second_row"] = lax.optimization_barrier((st, other_row(got["second_row"])))
        halo = 1 - n
        edges = []
        k = Stage("third")
        if n == 0:
            ft_edge = k.take(swap_path(got["ft_edge"]))
            edges = [k.take(swap_path(got["second_edge"]))] * 2
        mk_in, st_in = k.take(mk), k.take(st)
        a2 = k.give((frames, spots, width), BF16)
        third = k.give((frames + 2 * halo, spots, wide), BF16)
        n2 = k.give((2, width))
        nf3 = k.give((2, LANES))
        s_third = k.temp((1, 2 * wide))
        names = {}
        if n == 0:
            names.update(
                fw=k.give((fast_frames + 4, spots, fwide), BF16),
                y=k.give((frames, spots, both)),
            )
            s_fast = k.temp((1, 2 * both))
            k.step(
                part(fast_next, m, n, frames, group, 2 * LANES, 2 * width),
                st_in, k.take(v["ft"]), ft_edge, ft_edge, k.take(v["fw"]), k.take(saved[1]["w7"]),
                k.take(gf), k.take(bf), mk_in, names["fw"], names["y"], s_fast, nf3,
                flops=first_flops,
            )
        else:
            names.update(out_fast=k.give((fast_frames, spots, fwide)), pre_f=k.give((fast_frames, spots, fwide), BF16))
            s_fast = k.temp((1, 2 * LANES))
            k.step(
                part(fast_last, m, n, frames, group, 2 * LANES, 2 * width),
                st_in, k.take(v["ft"]), k.take(v["fw"], slice(2, 2 + fast_frames)), k.take(cf), k.take(gf), k.take(bf), mk_in,
                names["out_fast"], names["pre_f"], s_fast, nf3,
            )
        aw = k.temp((frames + 2 * halo, spots, width), BF16)
        k.step(
            part(slow_acts, m, n, frames, lo2, halo),
            st_in, k.take(v["second"]), *edges, k.take(gain_slow), k.take(bias_slow), mk_in, a2, n2, aw,
        )
        for at in range(0, wide, 256):
            lanes = slice(at, at + 256)
            k.step(
                part(slow_third, frames, halo, at),
                aw, k.take(w_slow_point, n, every, lanes), k.piece(third, every, every, lanes), s_third,
                flops=2 * frames * spots * width * 256,
            )
        if n == 0:
            pay = payload(k, s_fast, s_third)
            names["ff_row"] = row_out(k, names["y"], mk_in, lat, LANES)
            names["y_edge"] = edge_out(k, names["y"], mk_in, both)
        else:
            pay = payload(k, s_third, s_fast)
        got = finish(k, a2=a2, third=third, n2=n2, nf3=nf3, pay=pay, **names)
        st = gather_sums(got["pay"])
        for name in ("a2", "third", "n2", "nf3"):
            v[name] = got[name]
        if n == 0:
            saved[1].update(
                fw=got["fw"], y=got["y"], ff_row=other_row(got["ff_row"]), y_edge=swap_path(got["y_edge"])
            )
        else:
            out_fast, pre_f = got["out_fast"], got["pre_f"]

    def third_back(k, n, at, st_in, mk_in, pre):
        v = saved[n]
        d3, e2 = k.give((frames, spots, wide), BF16), k.give((frames, spots, width))
        s, gb = k.temp((1, 2 * width)), k.give((2, wide))
        gs = k.take(gain_slow)
        k.step(part(keep_sums, at, wide), st_in, gb)
        for t in range(frames):
            k.step(
                part(slow_third_grad, m, n, lo3),
                k.take(pre, t), k.take(v["third"], t + 1 - n), k.take(v["n3"]), k.peek(gb), gs, mk_in,
                k.piece(d3, t),
            )
        k.step(
            part(slow_third_back, m, n, frames, lo2),
            k.peek(d3), k.take(v["second"]), k.take(v["n2"]), k.take(w_slow_point, n), gs, k.take(bias_slow), mk_in,
            e2, s, flops=2 * frames * spots * width * wide,
        )
        return dict(d3=d3, e2=e2, gb3=gb), s

    def fast_back3(k, n, at, st_in, mk_in, pre):
        v = saved[n]
        d3, e2 = k.give((frames, spots, packs), BF16), k.give((frames, spots, LANES))
        s, gb = k.temp((1, 2 * LANES)), k.give((2, LANES))
        k.step(
            part(fast_third_back, m, n, frames, group, 2 * LANES, LANES, at),
            st_in, k.take(pre), k.take(v["ft"]), k.take(v["nf3"]), k.take(v["fs"]), k.take(v["nf2"]),
            k.take(wfp[n]), k.take(gf), k.take(bf), mk_in, d3, e2, s, gb,
            flops=2 * frames * spots * LANES * packs,
        )
        return dict(d3f=d3, ef2=e2, gbf3=gb), s

    def second_back(k, n, at, st_in, mk_in, e2, e2_row):
        v = saved[n]
        d2, e1 = k.give((frames, spots, width), BF16), k.give((frames, spots, width))
        s, gb = k.temp((1, 2 * width)), k.give((2, width))
        k.step(
            part(space_back, m, n, frames, cols, lo2, lo1, at, width, 0, False, m.slow),
            st_in, k.take(e2), k.take(e2_row), k.take(v["second"]), k.take(v["second_row"]), k.take(v["n2"]),
            k.take(v["first"]), k.take(v["n1"]), k.take(wsp, n), k.take(gain_slow), k.take(bias_slow), mk_in,
            d2, e1, s, gb, k.temp((frames, ext, 3 * width), BF16),
            flops=2 * frames * spots * 9 * width * width,
        )
        return dict(d2=d2, e1=e1, gb2=gb), s

    def fast_back2(k, n, at, st_in, mk_in, ef2, ef2_row):
        v = saved[n]
        d2, e1 = k.give((frames, spots, LANES), BF16), k.give((frames, spots, LANES))
        s, gb = k.temp((1, 2 * LANES)), k.give((2, LANES))
        k.step(
            part(space_back, m, n, frames, cols, LANES, 0, at, LANES, lat, True, m.fast),
            st_in, k.take(ef2), k.take(ef2_row), k.take(v["fs"]), k.take(v["fs_row"]), k.take(v["nf2"]),
            k.take(v["y"]), k.take(v["nf1"]), k.take(wfs[n]), k.take(gf), k.take(bf), mk_in,
            d2, e1, s, gb, k.temp((frames, ext, 3 * LANES), BF16),
            flops=2 * frames * spots * 9 * LANES * LANES,
        )
        return dict(d2f=d2, ef1=e1, gbf2=gb), s

    def first_back(k, n, st_in, mk_in, e1, e1_edge):
        v = saved[n]
        dw, el = k.give((frames + 2, spots, width), BF16), k.give((frames, spots, lat))
        s, gb = k.temp((1, 2 * lat)), k.give((2, width))
        edge, zedge = k.take(e1_edge), k.take(v["first_edge"])
        k.step(
            part(slow_first_back, m, n, frames, lo1, 0),
            st_in, k.take(e1), edge, edge, k.take(v["first"]), zedge, zedge, k.take(v["n1"]),
            k.take(w_slow_time, n, every, slice(wide, wide + lat)), k.take(v["y"]), k.take(v["nl"]),
            k.take(gain_slow), k.take(bias_slow), mk_in, dw, el, s, gb, flops=2 * frames * spots * 3 * lat * width,
        )
        return dict(dw=dw, el=el, gb1=gb), s

    def fast_back1(k, n, st1, at1, stl, atl, mk_in, el, el_edge, ef1, ef1_edge):
        v = saved[n]
        dl, df = k.give((frames, spots, lat), BF16), k.give((frames, spots, LANES), BF16)
        beside = [k.give((spots, lat), BF16), k.give((spots, LANES), BF16), k.give((spots, LANES), BF16)]
        gbl, gb1 = k.give((2, lat)), k.give((2, LANES))
        edge, yedge = k.take(ef1_edge), k.take(v["y_edge"])
        k.step(
            part(fast_first_back, m, n, frames, 0, at1, atl),
            st1, stl, k.take(el), k.take(el_edge), k.take(ef1), edge, edge, k.take(v["y"]), yedge, yedge,
            k.take(v["nl"]), k.take(v["nf1"]), k.take(gain_slow), k.take(gf), mk_in, dl, df, *beside, gbl, gb1,
        )
        return dict(dl=dl, df=df, dln=beside[0], dfp=beside[1], dfn=beside[2], gbl=gbl, gbf1=gb1)

    def weights_point(n, d3):
        k = Stage("point_weights")
        out = k.give((wide // 256, width, 256), BF16)
        k.step(point_weights, k.take(saved[n]["a2"]), k.take(d3), out, flops=2 * frames * spots * width * wide)
        return k.run()[0].reshape(-1, 256)

    def weights_space(n, d2):
        k = Stage("space_weights")
        out = k.give((3, 3 * width, width), BF16)
        k.step(
            part(space_weights, cols), k.take(saved[n]["a1"]), k.take(d2), out,
            k.temp((frames, ext, 3 * width), BF16), flops=2 * frames * spots * 9 * width * width,
        )
        return k.run()[0].reshape(-1, 256)

    def weights_time(n, dw):
        k = Stage("time_weights")
        out = k.give((3, wide + lat, width), BF16)
        k.step(
            part(time_weights, 1), k.take(saved[n]["sw"]), k.take(saved[n]["jl"]), k.take(dw), out,
            flops=2 * frames * spots * 3 * (wide + lat) * width,
        )
        return k.run()[0].reshape(-1, 256)

    def weights_fast(n, dl, df, d2, d3):
        v = saved[n]
        k = Stage("fast_weights")
        out = k.give((7 * LANES - LANES, 2 * LANES), BF16)
        k.step(
            part(fast_weights, group, cols, lat),
            k.take(v["fw"]), k.take(dl), k.take(df), k.take(v["fa1"]), k.take(d2), k.take(v["fa2"]), k.take(d3),
            out, k.temp((frames, ext, 3 * LANES), BF16), flops=first_flops,
        )
        return k.run()[0]

    b1, b0 = {}, {}
    k = Stage("last")
    mk_in, st_in = k.take(mk), k.take(st)
    out_slow, pre = k.give((frames, spots, wide)), k.give((frames, spots, wide), BF16)
    n3 = k.give((2, wide))
    s_pre, one, two = k.temp((1, 2 * wide)), k.temp((8, wide)), k.temp((8, wide))
    k.step(part(keep_norm, 0, wide, m.slow), st_in, mk_in, n3)
    k.step(clear, one, two)
    for t in range(frames):
        k.step(
            part(slow_last, m, 1, lo3),
            k.take(saved[1]["third"], t), k.take(saved[1]["sw"], t + 1), k.take(cs, t), k.peek(n3),
            k.take(gain_slow), k.take(bias_slow), mk_in, k.piece(out_slow, t), k.piece(pre, t), one, two,
        )
    k.step(close_sums, one, two, s_pre)
    names, s_ef2 = fast_back3(k, 1, 2 * wide, st_in, mk_in, pre_f)
    pay = payload(k, s_pre, s_ef2)
    ef2_row = row_out(k, names["ef2"], mk_in, 0, LANES)
    b1 = finish(k, out_slow=out_slow, pre=pre, n3=n3, pay=pay, ef2_row=ef2_row, **names)
    saved[1]["n3"] = b1["n3"]
    out_slow = b1["out_slow"]
    st = gather_sums(b1["pay"])

    k = Stage("back_third")
    ef2_row = other_row(b1["ef2_row"])
    mk_in, st_in = k.take(mk), k.take(st)
    names, s_e2 = third_back(k, 1, 0, st_in, mk_in, b1["pre"])
    more, s_ef1 = fast_back2(k, 1, 2 * wide, st_in, mk_in, b1["ef2"], ef2_row)
    pay = payload(k, s_e2, s_ef1)
    e2_row, ef1_edge = row_out(k, names["e2"], mk_in, 0, width), edge_out(k, more["ef1"], mk_in, LANES)
    b1.update(finish(k, pay=pay, e2_row=e2_row, ef1_edge=ef1_edge, **names, **more))
    st = st_ef1 = gather_sums(b1["pay"])
    e2_row = other_row(b1["e2_row"])
    st, ef1_edge = lax.optimization_barrier((st, swap_path(b1["ef1_edge"])))
    point1 = weights_point(1, b1["d3"])

    k = Stage("back_space")
    mk_in, st_in = k.take(mk), k.take(st)
    names, s_e1 = second_back(k, 1, 0, st_in, mk_in, b1["e2"], e2_row)
    pay = payload(k, s_e1)
    e1_edge = edge_out(k, names["e1"], mk_in, width)
    b1.update(finish(k, pay=pay, e1_edge=e1_edge, **names))
    st = gather_sums(b1["pay"])
    e1_edge = swap_path(b1["e1_edge"])
    space1 = weights_space(1, b1["d2"])

    k = Stage("back_first")
    mk_in, st_in = k.take(mk), k.take(st)
    names, s_el = first_back(k, 1, st_in, mk_in, b1["e1"], e1_edge)
    names["down"], s_down = k.give((frames, spots, wide), BF16), k.temp((1, 2 * wide))
    for at in range(0, wide, 256):
        lanes = slice(at, at + 256)
        k.step(
            part(slow_input_back, m, 1, frames, lo3, at),
            k.peek(names["dw"]), k.take(w_slow_time, 1, every, lanes), k.take(b1["pre"], every, every, lanes),
            k.take(saved[0]["sw"], slice(1, 1 + frames), every, lanes),
            k.take(saved[0]["third"], slice(1, 1 + frames), every, lanes),
            k.take(saved[0]["n3"]), k.take(gain_slow), k.take(bias_slow), mk_in,
            k.piece(names["down"], every, every, lanes), s_down,
            flops=2 * frames * spots * 3 * 256 * width,
        )
    pay = payload(k, s_el, s_down)
    el_edge = edge_out(k, names["el"], mk_in, lat)
    b1.update(finish(k, pay=pay, el_edge=el_edge, **names))
    st = gather_sums(b1["pay"])
    el_edge = swap_path(b1["el_edge"])
    time1 = weights_time(1, b1["dw"])
    sizes1 = [point1.shape[0], space1.shape[0], time1.shape[0]]
    ones = jnp.concatenate([point1, space1, time1], axis=0)
    st, ones, el_edge = lax.optimization_barrier((st, ones, el_edge))
    ones = lax.psum(ones, AXES)

    GRADS = ("df", "dln", "dfp", "dfn")
    SUMS = ("gbl", "gb1", "gb2", "gb3", "gbf1", "gbf2", "gbf3")
    steps = exchange_steps()
    core, across, down = steps[:3]
    seen = {}

    def spread_both(one, two, tied=()):
        one, two = [one, swap(one, *down)], [two, swap(two, *across)]
        one, two = [jnp.stack(pair) for pair in (one, two)]
        one, two = [one, swap(one, *across)], [two, swap(two, *down)]
        one, two, tied = lax.optimization_barrier((one, two, tied))
        return [pair + [swap(half, *core) for half in pair] for pair in (one, two)], tied

    def block_zero(st=st, el_edge=el_edge, ef1_edge=ef1_edge, b1=b1, b0=b0):
        b1, b0 = dict(b1), dict(b0)
        k = Stage("back_third")
        mk_in, st_in = k.take(mk), k.take(st)
        names, s_e2 = third_back(k, 0, 2 * lat, st_in, mk_in, b1["down"])
        more = fast_back1(
            k, 1, k.take(st_ef1), 2 * width, st_in, 0, mk_in, b1["el"], el_edge, b1["ef1"], ef1_edge
        )
        inner_grads = [more[name] for name in ("dl", "df", "dln", "dfp", "dfn")]
        more["downf"], s_pf = k.give((fast_frames, spots, fwide), BF16), k.temp((1, 2 * LANES))
        k.step(
            part(fast_input_back, m, 1, frames, group, 2 * LANES, False),
            *inner_grads, k.take(saved[1]["w7"]), k.take(pre_f), k.take(saved[0]["fw"]), k.take(saved[0]["ft"]),
            k.take(saved[0]["nf3"]), k.take(gf), k.take(bf), mk_in, more["downf"], s_pf,
            k.temp((fast_frames + 4, spots, fwide)), flops=first_flops,
        )
        pay = payload(k, s_e2, s_pf)
        e2_row = row_out(k, names["e2"], mk_in, 0, width)
        got = finish(k, pay=pay, e2_row=e2_row, **names, **more)
        for name in more:
            b1[name] = got[name]
        b0.update({name: got[name] for name in names})
        st = gather_sums(got["pay"])
        e2_row = other_row(got["e2_row"])
        point0 = weights_point(0, b0["d3"])
        fast_1 = weights_fast(1, b1["dl"], b1["df"], b1["d2f"], b1["d3f"])

        k = Stage("back_space")
        mk_in, st_in = k.take(mk), k.take(st)
        names, s_e1 = second_back(k, 0, 0, st_in, mk_in, b0["e2"], e2_row)
        more, s_ef2 = fast_back3(k, 0, 2 * width, st_in, mk_in, b1["downf"])
        pay = payload(k, s_e1, s_ef2)
        e1_edge, ef2_row = edge_out(k, names["e1"], mk_in, width), row_out(k, more["ef2"], mk_in, 0, LANES)
        b0.update(finish(k, pay=pay, e1_edge=e1_edge, ef2_row=ef2_row, **names, **more))
        st = gather_sums(b0["pay"])
        e1_edge, ef2_row = swap_path(b0["e1_edge"]), other_row(b0["ef2_row"])
        space0 = weights_space(0, b0["d2"])
        mid = jnp.concatenate([fast_1, point0, space0], axis=0)
        st, mid = lax.optimization_barrier((st, mid))

        k = Stage("back_first")
        mk_in, st_in = k.take(mk), k.take(st)
        names, s_el = first_back(k, 0, st_in, mk_in, b0["e1"], e1_edge)
        more, s_ef1 = fast_back2(k, 0, 2 * width, st_in, mk_in, b0["ef2"], ef2_row)
        pay = payload(k, s_el, s_ef1)
        el_edge, ef1_edge = edge_out(k, names["el"], mk_in, lat), edge_out(k, more["ef1"], mk_in, LANES)
        b0.update(finish(k, pay=pay, el_edge=el_edge, ef1_edge=ef1_edge, **names, **more))
        b0["dw"], mid = lax.optimization_barrier((b0["dw"], mid))
        mid = halve(mid, *core)
        st = gather_sums(b0["pay"])
        el_edge, ef1_edge = swap_path(b0["el_edge"]), swap_path(b0["ef1_edge"])
        time0 = weights_time(0, b0["dw"])
        st, mid = lax.optimization_barrier((st, mid))
        mid = halve_both(*parted(mid), across, down)
        k = Stage("back_fast")
        mk_in, st_in = k.take(mk), k.take(st)
        more = fast_back1(k, 0, st_in, 2 * lat, st_in, 0, mk_in, b0["el"], el_edge, b0["ef1"], ef1_edge)
        v = saved[0]
        rest = k.give((6 * LANES, 2 * LANES), BF16)
        k.step(
            part(fast_weights, group, cols, lat),
            k.take(v["fw"]), more["dl"], more["df"], k.take(v["fa1"]), k.take(b0["d2f"]), k.take(v["fa2"]),
            k.take(b0["d3f"]), rest, k.temp((frames, ext, 3 * LANES), BF16), flops=first_flops,
        )
        got = finish(k, rest=rest, **more)
        b0.update(got)
        seen["rows"] = [piece.shape[0] for piece in (fast_1, point0, space0, time0, got["rest"])]
        late = halve(jnp.concatenate([time0, got["rest"]], axis=0), *core)
        mid = halve_both(*mid, down, across)
        late, mid, dw0 = lax.optimization_barrier((late, mid, b0["dw"]))
        late = halve_both(*parted(late), across, down)
        late, dl0 = lax.optimization_barrier((late, b0["dl"]))
        k = Stage("slow_input")
        gx_slow = k.give((frames, spots, wide))
        k.step(
            part(slow_input_last, m, frames),
            k.take(dw0), k.take(w_slow_time, 0, every, slice(0, wide)), k.take(b1["down"]), k.take(mk), gx_slow,
            flops=2 * frames * spots * 3 * wide * width,
        )
        (gx_slow,) = k.run()
        k = Stage("fast_input")
        gx_fast = k.give((fast_frames, spots, fwide))
        k.step(
            part(fast_input_back, m, 0, frames, group, 2 * LANES, True),
            k.take(dl0), *[k.take(b0[name]) for name in GRADS], k.take(saved[0]["w7"]), k.take(b1["downf"]), k.take(mk), gx_fast,
            k.temp((fast_frames + 4, spots, fwide)), flops=first_flops,
        )
        (gx_fast,) = k.run()
        def along(value, ahead=steps[3:]):
            for step in ahead:
                value = halve(value, *step)
            value = value.astype(BF16)
            for step in reversed(steps[3:]):
                value = double(value, *step)
            return value

        mid = along(jnp.concatenate(mid, axis=0))
        late, gx_slow = lax.optimization_barrier((halve_both(*late, down, across), gx_slow))
        late = jnp.concatenate(late, axis=0)
        for step in steps[3:4]:
            late, gx_fast = lax.optimization_barrier((halve(late, *step), gx_fast))
        late = along(late, steps[4:])
        (mid_one, mid_two), _ = spread_both(*parted(mid))
        sums = [b0[name] for name in SUMS] + [b1[name] for name in ("gbl", "gbf1")]
        return (*mid_one, *mid_two, late, gx_slow, gx_fast, *sums)

    like = jax.eval_shape(block_zero)
    got = lax.cond(
        clip_size[0, 0] > 0, block_zero, lambda: tuple(jnp.zeros(o.shape, o.dtype) for o in like)
    )
    mid_one, mid_two = list(got[:4]), list(got[4:8])
    late, gx_slow, gx_fast = got[8:11]
    b0 = dict(zip(SUMS, got[11:18]))
    b1["gbl"], b1["gbf1"] = got[18:20]

    time_rows, space_rows = 3 * (wide + lat), 9 * width
    k = Stage("assemble_one")
    ones_in = k.take(ones)
    gtime, gspace = k.give((2, time_rows, width), F32, 1), k.give((2, space_rows, width), F32, 1)
    gpoint = k.give((2, width, wide), F32, 1)
    k.step(part(copy_rows, sizes1[0] + sizes1[1]), ones_in, gtime)
    k.step(part(copy_rows, sizes1[0]), ones_in, gspace)
    k.step(part(copy_columns, 0), ones_in, gpoint)
    half_done = k.run()

    (one, two), half_done = spread_both(*parted(late), half_done)

    core_bit = lax.axis_index("rows") % 2
    down_bit = (lax.axis_index("rows") // 2) % 2

    k = Stage("assemble")
    flip_one = k.scalar((core_bit * 4 + path * 2 + down_bit).astype(jnp.int32).reshape(1))
    flip_two = k.scalar((core_bit * 4 + down_bit * 2 + path).astype(jnp.int32).reshape(1))
    one_in = k.take_blocks(one, flip_one, every)
    two_in = k.take_blocks(two, flip_two, every)
    mid_one, mid_two = k.take_blocks(mid_one, flip_one, every), k.take_blocks(mid_two, flip_two, every)
    sizes = seen["rows"]
    half_mid, half_late = sum(sizes[:3]) // 2, sum(sizes[3:]) // 2
    gspace = k.give((2, space_rows, width), F32, 0, half_done[1])
    k.step(part(place_rows, sizes[0] + sizes[1], 0, half_mid), mid_one, mid_two, gspace)
    gpoint = k.give((2, width, wide), F32, 0, half_done[2])
    k.step(part(place_columns, sizes[0], 0, half_mid), mid_one, mid_two, gpoint)
    gtime = k.give((2, time_rows, width), F32, 0, half_done[0])
    k.step(part(place_rows, 0, 0, half_late), one_in, two_in, gtime)
    fast_outs = [
        k.give((2, 5 * fwide, lat)), k.give((2, 3, inner, fwide)), k.give((2, 9, inner, inner)),
        k.give((2, inner, fwide)),
    ]
    k.step(part(place_fast, inner, half_mid, half_late, sizes[3]), mid_one, mid_two, one_in, two_in, *fast_outs)
    sums = [k.take(b[name]) for b in (b0, b1) for name in ("gbl", "gb1", "gb2", "gb3", "gbf1", "gbf2", "gbf3")]
    norm_outs = [k.give(like.shape) for like in (gain_slow, bias_slow, gain_fast, bias_fast)]
    k.step(part(assemble_norms, inner), *sums, *norm_outs)
    got = k.run()
    glat, gft, gfs, gfp = [got[h[1]] for h in fast_outs]

    return (
        out_slow.reshape(x_slow.shape),
        out_fast.reshape(x_fast.shape),
        gx_slow.reshape(x_slow.shape),
        gx_fast.reshape(x_fast.shape),
        glat.reshape(w_lateral.shape),
        got[gtime[1]].reshape(w_slow_time.shape),
        got[gspace[1]].reshape(w_slow_space.shape),
        got[gpoint[1]],
        jnp.swapaxes(gft, 2, 3),
        gfs.reshape(w_fast_space.shape),
        gfp,
        *[got[h[1]] for h in norm_outs],
    )


def solution(mesh):
    spread = P("path", None, "rows", None, None, None)
    return jax.shard_map(
        on_device,
        mesh=mesh,
        in_specs=(spread, spread) + (P(),) * 12 + (spread, spread),
        out_specs=(spread,) * 4 + (P(),) * 11,
        check_vma=False,
    )
```
